32 devices in a mesh: rows: 4 (over y, x), seq: 8 (over z, core).
Axes of the slice: x: 2, y: 2, z: 4, core: 2. Of those that a mesh axis runs over, the one named last changes fastest.
Arguments:
- layer_input: bfloat16 [8, 512, 2048], P('rows', 'seq')
- output_gradient: bfloat16 [8, 512, 2048], P('rows', 'seq')
- norm_gain_vectors: float32 [2, 2048], replicated, may hold values from 0.1 to 1.9
- query_output_frozen: bfloat16 [2, 2048, 2048], P(None, 'seq'), may hold values from -0.125 to 0.125
- key_value_frozen: bfloat16 [2, 2048, 512], P(None, 'seq'), may hold values from -0.125 to 0.125
- gate_up_frozen: bfloat16 [2, 2048, 8192], P(None, 'seq'), may hold values from -0.125 to 0.125
- down_frozen_weight: bfloat16 [8192, 2048], P('seq'), may hold values from -0.0625 to 0.0625
- attention_adapter_a: float32 [4, 16, 2048], replicated, may hold values from -0.125 to 0.125
- query_output_adapter_b: float32 [2, 16, 2048], replicated, may hold values from -0.3125 to 0.3125
- key_value_adapter_b: float32 [2, 16, 512], replicated, may hold values from -0.3125 to 0.3125
- query_magnitude: float32 [2048], replicated, may hold values from 0.8 to 1.6
- key_value_magnitude: float32 [2, 512], replicated, may hold values from 0.8 to 1.6
- output_magnitude: float32 [2048], replicated, may hold values from 3 to 12
- gate_up_adapter_a: float32 [2, 16, 2048], replicated, may hold values from -0.125 to 0.125
- gate_up_adapter_b: float32 [2, 16, 8192], replicated, may hold values from -0.3125 to 0.3125
- gate_up_magnitude: float32 [2, 8192], replicated, may hold values from 0.6 to 1.8
- down_adapter_a: float32 [16, 8192], replicated, may hold values from -0.0625 to 0.0625
- down_adapter_b: float32 [16, 2048], replicated, may hold values from -0.3125 to 0.3125
- down_magnitude: float32 [2048], replicated, may hold values from 0.7 to 2.5
- prompt_length_list: int32 [4], P('rows'), may hold values from 64 to 256, as said below
- response_length_list: int32 [8], P('rows'), may hold values from 1 to 448
Outputs:
- out: bfloat16 [8, 512, 2048], P('rows', 'seq')
- grad_x: float32 [8, 512, 2048], P('rows', 'seq')
- grad_attn_lora_a: float32 [4, 16, 2048], replicated
- grad_query_out_lora_b: float32 [2, 16, 2048], replicated
- grad_key_value_lora_b: float32 [2, 16, 512], replicated
- grad_query_mag: float32 [2048], replicated
- grad_key_value_mag: float32 [2, 512], replicated
- grad_out_mag: float32 [2048], replicated
- grad_gate_up_lora_a: float32 [2, 16, 2048], replicated
- grad_gate_up_lora_b: float32 [2, 16, 8192], replicated
- grad_gate_up_mag: float32 [2, 8192], replicated
- grad_down_lora_a: float32 [16, 8192], replicated
- grad_down_lora_b: float32 [16, 2048], replicated
- grad_down_mag: float32 [2048], replicated
- stats: float32 [7, 2], replicated
The draws below stay inside these ranges and needn't reach their ends.
Inputs may be any that keep to these rules, and one draw needn't show every extreme that they name: prompt_length_list[p] + response_length_list[r] <= 512 for both rows r = 2 p and 2 p + 1 of pair p, and row 0 fills all 512 positions.
All inputs are finite; a program needn't handle non-finite values.
Results may differ from the reference program's by a relative error of at most 0.023.
Values may be sent and summed in bfloat16 or wider, within the bound.
A program may use at most 384 MiB of HBM per device.

```python
import math
import jax
import jax.numpy as jnp
from jax import lax

MODEL_DIM = 2048
FEEDFWD_UNITS = 8192
HEADS = 32
KV_HEADS = 8
HEAD_DIM = 64
ADAPTER_RANK = 16
ALPHA = 32
PAIR = 2
KEY_VALUE_WIDTH = 512
LENGTH = 512
PAIRS = 4
ROWS = 8


def draw_layer_input(key, part):
    key = jax.random.fold_in(key, 3)
    row_key, column_key, normal_key = jax.random.split(key, 3)
    row_scale = jnp.exp(jax.random.uniform(row_key, (ROWS, LENGTH, 1), jnp.float32, math.log(0.3), math.log(3.0)))
    column_scale = jnp.exp(jax.random.uniform(column_key, (1, 1, MODEL_DIM), jnp.float32, math.log(0.3), math.log(3.0)))
    normal_part = jax.random.normal(normal_key, (ROWS, LENGTH, MODEL_DIM), jnp.float32)
    return (normal_part * row_scale * column_scale).astype(jnp.bfloat16)


def draw_output_gradient(key, part):
    key = jax.random.fold_in(key, 5)
    normal_key = jax.random.fold_in(key, 0)
    position = jnp.arange(LENGTH, dtype=jnp.float32)[None, :, None] / LENGTH
    row_place = jnp.arange(ROWS, dtype=jnp.float32)[:, None, None] / ROWS
    normal_part = jax.random.normal(normal_key, (ROWS, LENGTH, MODEL_DIM), jnp.float32)
    rising = 3.0 ** (position + row_place)
    return (normal_part * rising).astype(jnp.bfloat16)


def length_tables(key):
    base_key = jax.random.fold_in(key, 7)
    prompt_key, reply_key = jax.random.split(base_key)
    prompts = jax.random.randint(prompt_key, (PAIRS,), LENGTH // 8, LENGTH // 2 + 1, dtype=jnp.int32)
    prompts = prompts.at[0].set(LENGTH // 2).at[1].set(LENGTH // 8)
    room_left = jnp.repeat(LENGTH - prompts, 2)
    replies = 1 + jax.random.randint(reply_key, (ROWS,), 0, LENGTH, dtype=jnp.int32) % room_left
    replies = replies.at[0].set(room_left[0]).at[2].set(room_left[2])
    return (prompts, replies)


def draw_prompt_length_list(key, part):
    return length_tables(key)[0]


def draw_response_length_list(key, part):
    return length_tables(key)[1]


def block_levels(stream_key, dims, cuts, least, high):
    level = 1.0
    for dim, parts in cuts:
        heights = jax.random.uniform(jax.random.fold_in(jax.random.fold_in(stream_key, 6), dim), (parts,), jnp.float32, least / len(cuts), high / len(cuts))
        level = level * jnp.repeat(jnp.exp(heights), dims[dim] // parts).reshape((-1,) + (1,) * (len(dims) - 1 - dim))
    return level


def centred(rng, dims, deviation, most, shards=(), kind=jnp.bfloat16):
    drawn = deviation * jax.random.normal(rng, dims, jnp.float32)
    if shards:
        drawn = drawn * block_levels(rng, dims, shards, -0.22, 0.18)
    return jnp.clip(drawn, -most, most).astype(kind)


def setup_inputs(seed: int = 0) -> dict:
    streams_of = jax.random.split(jax.random.key(seed), 22)
    layer_input = draw_layer_input(jax.random.fold_in(streams_of[21], 71), 0)
    output_gradient = draw_output_gradient(jax.random.fold_in(streams_of[21], 71), 0)
    norm_gain_vectors = jnp.clip(1.0 + 0.18 * jax.random.normal(streams_of[2], (2, MODEL_DIM), jnp.float32), 0.1, 1.9)
    query_output_frozen = centred(streams_of[3], (2, MODEL_DIM, MODEL_DIM), MODEL_DIM ** -0.5, 0.125, ((1, 8),))
    key_value_frozen = centred(streams_of[4], (2, MODEL_DIM, KEY_VALUE_WIDTH), MODEL_DIM ** -0.5, 0.125, ((1, 8),))
    gate_up_frozen = centred(streams_of[5], (2, MODEL_DIM, FEEDFWD_UNITS), MODEL_DIM ** -0.5, 0.125, ((1, 8),))
    down_frozen_weight = centred(streams_of[6], (FEEDFWD_UNITS, MODEL_DIM), FEEDFWD_UNITS ** -0.5, 0.0625, ((0, 8),))
    attention_adapter_a = centred(streams_of[7], (4, ADAPTER_RANK, MODEL_DIM), MODEL_DIM ** -0.5, 0.125, (), jnp.float32)
    query_output_adapter_b = centred(streams_of[8], (2, ADAPTER_RANK, MODEL_DIM), 0.05, 0.3125, (), jnp.float32)
    key_value_adapter_b = centred(streams_of[9], (2, ADAPTER_RANK, KEY_VALUE_WIDTH), 0.05, 0.3125, (), jnp.float32)
    query_magnitude = jnp.clip(jnp.exp(jax.random.uniform(streams_of[10], (MODEL_DIM,), jnp.float32, math.log(0.8), math.log(1.6))), 0.8, 1.6)
    key_value_magnitude = jnp.clip(jnp.exp(jax.random.uniform(streams_of[11], (2, KEY_VALUE_WIDTH), jnp.float32, math.log(0.8), math.log(1.6))), 0.8, 1.6)
    output_magnitude = jnp.clip(jnp.exp(jax.random.uniform(streams_of[12], (MODEL_DIM,), jnp.float32, math.log(3.0), math.log(12.0))), 3.0, 12.0)
    gate_up_adapter_a = centred(streams_of[13], (2, ADAPTER_RANK, MODEL_DIM), MODEL_DIM ** -0.5, 0.125, (), jnp.float32)
    gate_up_adapter_b = centred(streams_of[14], (2, ADAPTER_RANK, FEEDFWD_UNITS), 0.05, 0.3125, (), jnp.float32)
    gate_up_magnitude = jnp.clip(jnp.exp(jax.random.uniform(streams_of[15], (2, FEEDFWD_UNITS), jnp.float32, math.log(0.6), math.log(1.8))), 0.6, 1.8)
    down_adapter_a = centred(streams_of[16], (ADAPTER_RANK, FEEDFWD_UNITS), FEEDFWD_UNITS ** -0.5, 0.0625, (), jnp.float32)
    down_adapter_b = centred(streams_of[17], (ADAPTER_RANK, MODEL_DIM), 0.05, 0.3125, (), jnp.float32)
    down_magnitude = jnp.clip(jnp.exp(jax.random.uniform(streams_of[18], (MODEL_DIM,), jnp.float32, math.log(0.7), math.log(2.5))), 0.7, 2.5)
    prompt_length_list = draw_prompt_length_list(jax.random.fold_in(streams_of[21], 71), 0)
    response_length_list = draw_response_length_list(jax.random.fold_in(streams_of[21], 71), 0)
    return dict(layer_input=layer_input, output_gradient=output_gradient, norm_gain_vectors=norm_gain_vectors, query_output_frozen=query_output_frozen, key_value_frozen=key_value_frozen, gate_up_frozen=gate_up_frozen, down_frozen_weight=down_frozen_weight, attention_adapter_a=attention_adapter_a, query_output_adapter_b=query_output_adapter_b, key_value_adapter_b=key_value_adapter_b, query_magnitude=query_magnitude, key_value_magnitude=key_value_magnitude, output_magnitude=output_magnitude, gate_up_adapter_a=gate_up_adapter_a, gate_up_adapter_b=gate_up_adapter_b, gate_up_magnitude=gate_up_magnitude, down_adapter_a=down_adapter_a, down_adapter_b=down_adapter_b, down_magnitude=down_magnitude, prompt_length_list=prompt_length_list, response_length_list=response_length_list)


highest = lax.Precision.HIGHEST

@jax.custom_vjp
def low_rank_update(v):
    return lax.optimization_barrier(v.astype(jnp.bfloat16)).astype(jnp.float32)

@jax.custom_vjp
def low_back(v):
    return v

def low_keep(v):
    return (low_rank_update(v), None)

def low_pass(kept, grad):
    return (grad,)

def back_keep(v):
    return (v, None)

def back_low(kept, grad):
    return (low_rank_update(grad),)
low_rank_update.defvjp(low_keep, low_pass)
low_back.defvjp(back_keep, back_low)

def rms_scale(values, gain):
    return values * lax.rsqrt(lax.optimization_barrier(jnp.mean(values * values, axis=-1, keepdims=True)) + 1e-05) * gain

def rotate(values, positions, direction_sign):
    half_dim = values.shape[-1] // 2
    frequency = 500000.0 ** (-(jnp.arange(half_dim, dtype=jnp.float32) * 2.0) / values.shape[-1])
    angles = positions.astype(jnp.float32)[:, None] * frequency[None, :]
    cosine = jnp.cos(angles)[:, None, :]
    sine_part = direction_sign * jnp.sin(angles)[:, None, :]
    first_half = values[..., :half_dim]
    second_half = values[..., half_dim:]
    return jnp.concatenate([first_half * cosine - second_half * sine_part, second_half * cosine + first_half * sine_part], axis=-1)

def column_norms(merged_weight, down_factor_a, down_factor_b):
    merged = merged_weight + ALPHA / ADAPTER_RANK * jnp.dot(down_factor_a.T, down_factor_b, precision=highest)
    return jnp.sqrt(lax.optimization_barrier(jnp.sum(merged * merged, axis=0)) + 1e-06)

def decomposed_adapter(input_rows, merged_weight, adapter_factor_a, adapter_factor_b, magnitude_vector):
    down_factor_a = low_rank_update(adapter_factor_a)
    down_factor_b = low_rank_update(adapter_factor_b)
    norms = column_norms(merged_weight, down_factor_a, down_factor_b)
    base_out = jnp.dot(input_rows, merged_weight, precision=highest)
    inner_low = low_rank_update(low_back(jnp.dot(input_rows, down_factor_a.T, precision=highest)))
    before = low_back(base_out + ALPHA / ADAPTER_RANK * jnp.dot(inner_low, down_factor_b, precision=highest))
    return before * (magnitude_vector / norms)

def attention(queries, keys, values, valid_len):
    block_rows = min(512, LENGTH)
    block_count = LENGTH // block_rows
    key_pos = jnp.arange(LENGTH, dtype=jnp.int32)
    blocks = queries.reshape(PAIR, block_count, block_rows, KV_HEADS, HEADS // KV_HEADS, HEAD_DIM).transpose(1, 0, 2, 3, 4, 5)
    starts = jnp.arange(block_count, dtype=jnp.int32) * block_rows

    def one_block(operands):
        q_blk, block_start = operands
        q_pos = block_start + jnp.arange(block_rows, dtype=jnp.int32)
        scores = jnp.einsum('rqhgd,rkhd->rhgqk', q_blk, keys, precision=highest) * HEAD_DIM ** (-0.5)
        scores = low_back(scores)
        allowed = (key_pos[None, None, :] <= q_pos[None, :, None]) & (key_pos[None, None, :] < valid_len[:, None, None])
        masked = jnp.where(allowed[:, None, None], scores, -1e+30)
        row_max = lax.optimization_barrier(jnp.max(masked, axis=-1, keepdims=True))
        unscaled = jnp.exp(masked - row_max)
        shares = unscaled / lax.optimization_barrier(jnp.sum(unscaled, axis=-1, keepdims=True))
        return jnp.einsum('rhgqk,rkhd->rqhgd', low_rank_update(shares), values, precision=highest)
    mixed_out = lax.map(jax.checkpoint(one_block), (blocks, starts))
    return mixed_out.transpose(1, 0, 2, 3, 4, 5).reshape(PAIR * LENGTH, MODEL_DIM)

def layer(input_rows, adapter_set, frozen_weights, valid_len):
    attention_adapter_a, query_output_adapter_b, key_value_adapter_b, query_magnitude, key_value_magnitude, output_magnitude, gate_up_adapter_a, gate_up_adapter_b, gate_up_magnitude, down_adapter_a, down_adapter_b, down_magnitude = adapter_set
    norm_gain_vectors, query_output_frozen, key_value_frozen, gate_up_frozen, down_frozen_weight = frozen_weights
    token_rows = input_rows.reshape(PAIR * LENGTH, MODEL_DIM)
    positions = jnp.tile(jnp.arange(LENGTH, dtype=jnp.int32), PAIR)
    first_input = low_rank_update(rms_scale(token_rows, norm_gain_vectors[0]))
    query_unnormed = decomposed_adapter(first_input, query_output_frozen[0], attention_adapter_a[0], query_output_adapter_b[0], query_magnitude)
    key_unnormed = decomposed_adapter(first_input, key_value_frozen[0], attention_adapter_a[1], key_value_adapter_b[0], key_value_magnitude[0])
    value_unnormed = decomposed_adapter(first_input, key_value_frozen[1], attention_adapter_a[2], key_value_adapter_b[1], key_value_magnitude[1])
    queries = low_rank_update(low_back(rotate(query_unnormed.reshape(-1, HEADS, HEAD_DIM), positions, 1.0)))
    keys = low_rank_update(low_back(rotate(key_unnormed.reshape(-1, KV_HEADS, HEAD_DIM), positions, 1.0)))
    values = low_rank_update(low_back(value_unnormed))
    attention_result = attention(queries.reshape(PAIR, LENGTH, KV_HEADS, HEADS // KV_HEADS, HEAD_DIM), keys.reshape(PAIR, LENGTH, KV_HEADS, HEAD_DIM), values.reshape(PAIR, LENGTH, KV_HEADS, HEAD_DIM), valid_len)
    attention_result = low_rank_update(low_back(attention_result))
    residual_stream = token_rows + decomposed_adapter(attention_result, query_output_frozen[1], attention_adapter_a[3], query_output_adapter_b[1], output_magnitude)
    second_input = low_rank_update(rms_scale(residual_stream, norm_gain_vectors[1]))
    gate_output = decomposed_adapter(second_input, gate_up_frozen[0], gate_up_adapter_a[0], gate_up_adapter_b[0], gate_up_magnitude[0])
    lift_output = decomposed_adapter(second_input, gate_up_frozen[1], gate_up_adapter_a[1], gate_up_adapter_b[1], gate_up_magnitude[1])
    hidden_rows = low_rank_update(jax.nn.sigmoid(gate_output) * gate_output * lift_output)
    layer_result = residual_stream + decomposed_adapter(hidden_rows, down_frozen_weight, down_adapter_a, down_adapter_b, down_magnitude)
    return layer_result.reshape(PAIR, LENGTH, MODEL_DIM)

def drift_stats(magnitude_vector, norms):
    drift = jnp.sqrt(jnp.mean(jnp.square(magnitude_vector - norms))) / jnp.sqrt(jnp.mean(jnp.square(magnitude_vector)) + 1e-06)
    return jnp.stack([drift, jnp.mean(norms)])

def reference(layer_input, output_gradient, norm_gain_vectors, query_output_frozen, key_value_frozen, gate_up_frozen, down_frozen_weight, attention_adapter_a, query_output_adapter_b, key_value_adapter_b, query_magnitude, key_value_magnitude, output_magnitude, gate_up_adapter_a, gate_up_adapter_b, gate_up_magnitude, down_adapter_a, down_adapter_b, down_magnitude, prompt_length_list, response_length_list):
    frozen_weights = (norm_gain_vectors, query_output_frozen.astype(jnp.float32), key_value_frozen.astype(jnp.float32), gate_up_frozen.astype(jnp.float32), down_frozen_weight.astype(jnp.float32))
    adapter_set = (attention_adapter_a, query_output_adapter_b, key_value_adapter_b, query_magnitude, key_value_magnitude, output_magnitude, gate_up_adapter_a, gate_up_adapter_b, gate_up_magnitude, down_adapter_a, down_adapter_b, down_magnitude)
    valid_all = (jnp.repeat(prompt_length_list, PAIR) + response_length_list).astype(jnp.int32)
    input_rows = layer_input.astype(jnp.float32).reshape(PAIRS, PAIR, LENGTH, MODEL_DIM)
    cotangents = output_gradient.astype(jnp.float32).reshape(PAIRS, PAIR, LENGTH, MODEL_DIM)
    valid_pairs = valid_all.reshape(PAIRS, PAIR)
    zero_grads = jax.tree.map(jnp.zeros_like, adapter_set)

    def pair_step(totals, pair_slab):
        pair_inputs, pair_cotangent, pair_valid = pair_slab

        def forward_pair(values, params):
            return layer(values, params, frozen_weights, pair_valid)
        pair_out, pullback = jax.vjp(forward_pair, pair_inputs, adapter_set)
        pair_grad_x, pair_grads = pullback(pair_cotangent)
        return (jax.tree.map(jnp.add, totals, pair_grads), (pair_out.astype(jnp.bfloat16), pair_grad_x))
    totals, (outs_all, grads_all) = lax.scan(pair_step, zero_grads, (input_rows, cotangents, valid_pairs))
    piece_list = [(frozen_weights[1][0], attention_adapter_a[0], query_output_adapter_b[0], query_magnitude), (frozen_weights[2][0], attention_adapter_a[1], key_value_adapter_b[0], key_value_magnitude[0]), (frozen_weights[2][1], attention_adapter_a[2], key_value_adapter_b[1], key_value_magnitude[1]), (frozen_weights[1][1], attention_adapter_a[3], query_output_adapter_b[1], output_magnitude), (frozen_weights[3][0], gate_up_adapter_a[0], gate_up_adapter_b[0], gate_up_magnitude[0]), (frozen_weights[3][1], gate_up_adapter_a[1], gate_up_adapter_b[1], gate_up_magnitude[1]), (frozen_weights[4], down_adapter_a, down_adapter_b, down_magnitude)]
    stats = jnp.stack([drift_stats(piece[3], column_norms(piece[0], low_rank_update(piece[1]), low_rank_update(piece[2]))) for piece in piece_list])
    return (outs_all.reshape(ROWS, LENGTH, MODEL_DIM), grads_all.reshape(ROWS, LENGTH, MODEL_DIM), totals[0], totals[1], totals[2], totals[3], totals[4], totals[5], totals[6], totals[7], totals[8], totals[9], totals[10], totals[11], stats)
```

```python
import jax
import jax.numpy as jnp
from jax import lax
from jax.sharding import PartitionSpec as P

HEADS = 32
KV_HEADS = 8
HEAD_DIM = 64
ADAPTER_RANK = 16
ALPHA = 32


highest = lax.Precision.HIGHEST
last_last = (((1,), (1,)), ((), ()))
first_first = (((0,), (0,)), ((), ()))


def rms_scale(values, gain):
    inverse = lax.rsqrt(jnp.mean(values * values, axis=-1, keepdims=True) + 1e-05)
    return values * inverse * gain


def rotate(values, positions, direction_sign):
    half_dim = values.shape[-1] // 2
    frequency = 500000.0 ** (-(jnp.arange(half_dim, dtype=jnp.float32) * 2.0) / values.shape[-1])
    angles = positions.astype(jnp.float32)[:, None] * frequency[None, :]
    cosine = jnp.cos(angles)[:, None, :]
    sine_part = direction_sign * jnp.sin(angles)[:, None, :]
    first_half = values[..., :half_dim]
    second_half = values[..., half_dim:]
    return jnp.concatenate(
        [
            first_half * cosine - second_half * sine_part,
            second_half * cosine + first_half * sine_part,
        ],
        axis=-1,
    )


SCALE = ALPHA / ADAPTER_RANK


def dot_f32(a, b):
    return jnp.dot(a, b, preferred_element_type=jnp.float32)


def dot_nt(a, b):
    return lax.dot_general(a, b, last_last, preferred_element_type=jnp.float32)


def dot_tn(a, b):
    return lax.dot_general(a, b, first_first, preferred_element_type=jnp.float32)


def block_rows(blocks):
    total = sum(b.shape[1] for b in blocks)
    rows, start = [], 0
    for b in blocks:
        rows.append(jnp.pad(b, ((0, 0), (start, total - start - b.shape[1]))))
        start += b.shape[1]
    return jnp.concatenate(rows, axis=0)


def square_terms(weight, a_low, b_low):
    cross = dot_f32(a_low, weight)
    squares = jnp.sum(jnp.square(weight.astype(jnp.float32)), axis=0)
    return squares + 2.0 * SCALE * jnp.sum(b_low.astype(jnp.float32) * cross, axis=0), cross


def gram_times_b(a_low, b_low):
    a_wide = a_low.astype(jnp.float32)
    return jnp.dot(
        jnp.dot(a_wide, a_wide.T, precision=highest), b_low.astype(jnp.float32), precision=highest
    )


def project(rows, weight, a_low, b_low):
    base = dot_f32(rows, weight)
    inner = dot_nt(rows, a_low).astype(jnp.bfloat16)
    return base + SCALE * dot_f32(inner, b_low), inner


def back_low(grad_before, a_low, b_low):
    return (SCALE * dot_nt(grad_before, b_low)).astype(jnp.bfloat16)


def spread_term(weight, a_low, b_low, column):
    b_wide = b_low.astype(jnp.float32)
    weighted = b_wide * column
    upper = weighted.astype(jnp.bfloat16)
    lower = (weighted - upper.astype(jnp.float32)).astype(jnp.bfloat16)
    rank = b_low.shape[0]
    both = dot_nt(jnp.concatenate([upper, lower], axis=0), weight)
    inner = jnp.dot(weighted, b_wide.T, precision=highest)
    return (
        both[:rank]
        + both[rank:]
        + SCALE * jnp.dot(inner, a_low.astype(jnp.float32), precision=highest)
    )

def to_heads(flat, pair_rows, span_len, group_count, ratio, head_dim):
    shaped = flat.reshape(pair_rows, span_len, group_count, ratio, head_dim)
    return shaped.transpose(2, 0, 3, 1, 4).reshape(
        group_count, pair_rows, ratio * span_len, head_dim
    )


def from_heads(stacked, pair_rows, span_len, group_count, ratio, head_dim):
    shaped = stacked.reshape(group_count, pair_rows, ratio, span_len, head_dim)
    return shaped.transpose(1, 3, 0, 2, 4).reshape(
        pair_rows * span_len, group_count * ratio * head_dim
    )


def keys_to_heads(whole, group_count, head_dim):
    pair_rows, length_all, _ = whole.shape
    return whole.reshape(pair_rows, length_all, group_count, head_dim).transpose(2, 0, 1, 3)


def keys_from_heads(stacked):
    group_count, pair_rows, length_all, head_dim = stacked.shape
    return stacked.transpose(1, 2, 0, 3).reshape(pair_rows, length_all, group_count * head_dim)


def score_block(head_q, head_k, row_pos, key_pos, valid_len):
    scores = jnp.einsum(
        "rqd,rkd->rqk", head_q, head_k, preferred_element_type=jnp.float32
    ) * head_q.shape[-1] ** (-0.5)
    allowed = (key_pos[None, None, :] <= row_pos[None, :, None]) & (
        key_pos[None, None, :] < valid_len[:, None, None]
    )
    return (scores, allowed)


def drift_stats(magnitude_vector, norms):
    drift = jnp.sqrt(jnp.mean(jnp.square(magnitude_vector - norms))) / jnp.sqrt(
        jnp.mean(jnp.square(magnitude_vector)) + 1e-06
    )
    return jnp.stack([drift, jnp.mean(norms)])


def local(
    layer_input,
    output_gradient,
    norm_gain_vectors,
    query_output_frozen,
    key_value_frozen,
    gate_up_frozen,
    down_frozen_weight,
    attention_adapter_a,
    query_output_adapter_b,
    key_value_adapter_b,
    query_magnitude,
    key_value_magnitude,
    output_magnitude,
    gate_up_adapter_a,
    gate_up_adapter_b,
    gate_up_magnitude,
    down_adapter_a,
    down_adapter_b,
    down_magnitude,
    prompt_length_list,
    response_length_list,
):
    pair_rows, span_len, model_width = layer_input.shape
    token_count = pair_rows * span_len
    head_count, group_count, head_dim = HEADS, KV_HEADS, HEAD_DIM
    ratio = head_count // group_count
    kv_width = group_count * head_dim
    seq_size = lax.axis_size("seq")
    seq_index = lax.axis_index("seq")
    first_member = (seq_index == 0).astype(jnp.float32)
    low = jnp.bfloat16
    rank = ADAPTER_RANK

    qkv_local = jnp.concatenate(
        [query_output_frozen[0], key_value_frozen[0], key_value_frozen[1]], axis=1
    )
    weight_qkv = lax.all_gather(qkv_local, "seq", axis=0, tiled=True)
    weight_o = lax.all_gather(query_output_frozen[1], "seq", axis=0, tiled=True)
    weight_gu = lax.all_to_all(gate_up_frozen, "seq", split_axis=2, concat_axis=1, tiled=True)
    weight_d = down_frozen_weight
    slice_units = weight_d.shape[0]

    a_qkv = attention_adapter_a[:3].reshape(3 * rank, model_width).astype(low)
    b_qkv = block_rows(
        [query_output_adapter_b[0], key_value_adapter_b[0], key_value_adapter_b[1]]
    ).astype(low)
    m_qkv = jnp.concatenate([query_magnitude, key_value_magnitude[0], key_value_magnitude[1]])
    a_o = attention_adapter_a[3].astype(low)
    b_o = query_output_adapter_b[1].astype(low)
    a_gu = gate_up_adapter_a.astype(low)
    start = seq_index * slice_units
    b_gu = lax.dynamic_slice_in_dim(gate_up_adapter_b, start, slice_units, 2).astype(low)
    m_gu = lax.dynamic_slice_in_dim(gate_up_magnitude, start, slice_units, 1)
    a_d = down_adapter_a.astype(low)
    a_d_local = lax.dynamic_slice_in_dim(a_d, start, slice_units, 1)
    b_d = down_adapter_b.astype(low)

    def norms_of(squares, a_low, b_low):
        b_wide = b_low.astype(jnp.float32)
        gram_b = gram_times_b(a_low, b_low)
        return jnp.sqrt(squares + SCALE * SCALE * jnp.sum(b_wide * gram_b, axis=0) + 1e-06), gram_b

    sq_d, cross_d = square_terms(weight_d, a_d_local, b_d)
    sq_d = lax.psum(sq_d, "seq")
    n_d, gram_d = norms_of(sq_d, a_d, b_d)
    ratio_d = down_magnitude / n_d

    sq_qkv, cross_qkv = square_terms(weight_qkv, a_qkv, b_qkv)
    n_qkv, gram_qkv = norms_of(sq_qkv, a_qkv, b_qkv)
    ratio_qkv = m_qkv / n_qkv
    sq_o, cross_o = square_terms(weight_o, a_o, b_o)
    n_o, gram_o = norms_of(sq_o, a_o, b_o)
    ratio_o = output_magnitude / n_o

    query_pos = seq_index * span_len + jnp.arange(span_len, dtype=jnp.int32)
    positions = jnp.tile(query_pos, pair_rows)
    row_pos = jnp.tile(query_pos, ratio)
    key_pos = jnp.arange(span_len * seq_size, dtype=jnp.int32)
    valid_len = prompt_length_list[0] + response_length_list

    token_rows = layer_input.reshape(token_count, model_width).astype(jnp.float32)
    first_input = rms_scale(token_rows, norm_gain_vectors[0]).astype(low)
    before_qkv, inner_qkv = project(first_input, weight_qkv, a_qkv, b_qkv)
    qkv = before_qkv * ratio_qkv
    q_flat = qkv[:, :model_width]
    k_flat = qkv[:, model_width : model_width + kv_width]
    v_flat = qkv[:, model_width + kv_width :]
    queries = rotate(q_flat.reshape(token_count, head_count, head_dim), positions, 1.0).astype(low)
    key_rows = rotate(k_flat.reshape(token_count, group_count, head_dim), positions, 1.0).astype(
        low
    )
    keys_values = jnp.concatenate(
        [key_rows.reshape(token_count, kv_width), v_flat.astype(low)], axis=1
    ).reshape(pair_rows, span_len, 2 * kv_width)
    kv_all = lax.all_gather(keys_values, "seq", axis=1, tiled=True)
    query_heads = to_heads(
        queries.reshape(token_count, model_width), pair_rows, span_len, group_count, ratio, head_dim
    )
    key_heads = keys_to_heads(kv_all[..., :kv_width], group_count, head_dim)
    value_heads = keys_to_heads(kv_all[..., kv_width:], group_count, head_dim)

    def forward_head(operands):
        head_q, head_k, head_v = operands
        scores, allowed = score_block(head_q, head_k, row_pos, key_pos, valid_len)
        masked = jnp.where(allowed, scores, -1e30)
        row_max = jnp.max(masked, axis=-1, keepdims=True)
        unscaled = jnp.exp(masked - row_max)
        row_total = jnp.sum(unscaled, axis=-1, keepdims=True)
        shares = unscaled / row_total
        mixed_out = jnp.einsum(
            "rqk,rkd->rqd", shares.astype(jnp.bfloat16), head_v, preferred_element_type=jnp.float32
        )
        return (mixed_out, (row_max + jnp.log(row_total))[..., 0])

    mixed_heads, log_totals = lax.map(forward_head, (query_heads, key_heads, value_heads))
    attended = from_heads(
        mixed_heads, pair_rows, span_len, group_count, ratio, head_dim
    ).astype(low)
    before_o, inner_o = project(attended, weight_o, a_o, b_o)
    residual = token_rows + before_o * ratio_o
    second_input = rms_scale(residual, norm_gain_vectors[1]).astype(low)

    u2 = lax.all_gather(second_input, "seq", axis=0, tiled=True)
    grad_out_rows = output_gradient.reshape(token_count, model_width)
    gy_all = lax.all_gather(grad_out_rows, "seq", axis=0, tiled=True)
    gb_d = (gy_all.astype(jnp.float32) * ratio_d).astype(low)
    gi_d = back_low(gb_d, a_d, b_d)
    grad_hidden = dot_nt(gb_d, weight_d) + dot_f32(gi_d, a_d_local)

    branch = []
    for i in range(2):
        sq, cross = square_terms(weight_gu[i], a_gu[i], b_gu[i])
        norm, gram_b = norms_of(sq, a_gu[i], b_gu[i])
        before, inner = project(u2, weight_gu[i], a_gu[i], b_gu[i])
        branch.append((norm, gram_b, cross, m_gu[i] / norm, before, inner))
    gate = branch[0][4] * branch[0][3]
    lift = branch[1][4] * branch[1][3]
    sig = jax.nn.sigmoid(gate)
    silu = sig * gate
    hidden = (silu * lift).astype(low)
    down_partial = dot_f32(hidden, weight_d)
    inner_d_partial = dot_nt(hidden, a_d_local)
    down_sum = lax.psum_scatter(down_partial.astype(low), "seq", scatter_dimension=0, tiled=True)
    inner_d = lax.psum_scatter(inner_d_partial, "seq", scatter_dimension=0, tiled=True).astype(low)
    before_d = down_sum.astype(jnp.float32) + SCALE * dot_f32(inner_d, b_d)
    layer_result = (residual + before_d * ratio_d).astype(low)

    grad_rows = grad_out_rows.astype(jnp.float32)
    gm_d = jnp.sum(grad_rows * before_d, axis=0) / n_d
    gm_d_line = lax.psum(gm_d, "seq")
    c_d = -gm_d_line * down_magnitude / (n_d * n_d)
    gb_d_own = (grad_rows * ratio_d).astype(low)
    spread_d = spread_term(weight_d, jnp.zeros_like(a_d_local), b_d, c_d)
    weighted_d = b_d.astype(jnp.float32) * c_d
    spread_d = spread_d + SCALE * jnp.dot(
        jnp.dot(weighted_d, b_d.astype(jnp.float32).T, precision=highest),
        a_d_local.astype(jnp.float32),
        precision=highest,
    )
    ga_d = dot_tn(gi_d, hidden) + SCALE * spread_d
    gB_d = SCALE * dot_tn(inner_d, gb_d_own) + SCALE * c_d * (
        cross_d + first_member * SCALE * gram_d
    )

    ggate = grad_hidden * lift * sig * (1.0 + gate * (1.0 - sig))
    glift = grad_hidden * silu
    grad_in = None
    ga_gu, gB_gu, gm_gu = [], [], []
    for i, g in enumerate((ggate, glift)):
        norm, gram_b, cross, rat, before, inner = branch[i]
        gb = (g * rat).astype(low)
        gi = back_low(gb, a_gu[i], b_gu[i])
        term = dot_nt(gb, weight_gu[i])
        gm = jnp.sum(g * before, axis=0) / norm
        c = -gm * m_gu[i] / (norm * norm)
        grad_in = term if grad_in is None else grad_in + term
        low_term = dot_f32(gi, a_gu[i])
        grad_in = grad_in + low_term
        ga_gu.append(dot_tn(gi, u2) + SCALE * spread_term(weight_gu[i], a_gu[i], b_gu[i], c))
        gB_gu.append(SCALE * dot_tn(inner, gb) + SCALE * c * (cross + SCALE * gram_b))
        gm_gu.append(gm)
    in_grad = lax.psum_scatter(grad_in.astype(low), "seq", scatter_dimension=0, tiled=True)
    _, second_pull = jax.vjp(lambda v: rms_scale(v, norm_gain_vectors[1]), residual)
    grad_residual = grad_rows + second_pull(in_grad.astype(jnp.float32))[0]

    def back_full(upstream, rows, weight, a_low, b_low, ratio_p, norm, magnitude, before, inner, cross, gram_b):
        gb = (upstream * ratio_p).astype(low)
        gi = back_low(gb, a_low, b_low)
        grad_rows_in = dot_nt(gb, weight) + dot_f32(gi, a_low)
        gm = jnp.sum(upstream * before, axis=0) / norm
        c = -gm * magnitude / (norm * norm)
        ga = dot_tn(gi, rows) + SCALE * spread_term(weight, a_low, b_low, c)
        gB = SCALE * dot_tn(inner, gb) + SCALE * c * (cross + SCALE * gram_b)
        return grad_rows_in, ga, gB, gm

    grad_att, ga_o, gB_o, gm_o = back_full(
        grad_residual, attended, weight_o, a_o, b_o, ratio_o, n_o, output_magnitude,
        before_o, inner_o, cross_o, gram_o,
    )
    grad_att_heads = to_heads(
        grad_att.astype(low), pair_rows, span_len, group_count, ratio, head_dim
    )
    scale_factor = head_dim ** (-0.5)

    def backward_head(operands):
        head_q, head_k, head_v, head_lse, head_grad = operands
        scores, allowed = score_block(head_q, head_k, row_pos, key_pos, valid_len)
        shares = jnp.where(allowed, jnp.exp(scores - head_lse[..., None]), 0.0)
        grad_shares = jnp.einsum(
            "rqd,rkd->rqk", head_grad, head_v, preferred_element_type=jnp.float32
        )
        centre = jnp.sum(shares * grad_shares, axis=-1, keepdims=True)
        grad_scores = (shares * (grad_shares - centre)).astype(jnp.bfloat16)
        grad_q = (
            jnp.einsum("rqk,rkd->rqd", grad_scores, head_k, preferred_element_type=jnp.float32)
            * scale_factor
        )
        grad_k = (
            jnp.einsum("rqk,rqd->rkd", grad_scores, head_q, preferred_element_type=jnp.float32)
            * scale_factor
        )
        grad_v = jnp.einsum(
            "rqk,rqd->rkd",
            shares.astype(jnp.bfloat16),
            head_grad,
            preferred_element_type=jnp.float32,
        )
        return (grad_q, grad_k, grad_v)

    grad_q_heads, grad_k_heads, grad_v_heads = lax.map(
        backward_head, (query_heads, key_heads, value_heads, log_totals, grad_att_heads)
    )
    kv_grads = jnp.concatenate(
        [keys_from_heads(grad_k_heads).astype(low), keys_from_heads(grad_v_heads).astype(low)],
        axis=2,
    )
    kv_grads = lax.psum_scatter(kv_grads, "seq", scatter_dimension=1, tiled=True)
    kv_grads = kv_grads.reshape(token_count, 2 * kv_width).astype(jnp.float32)
    grad_query = from_heads(grad_q_heads, pair_rows, span_len, group_count, ratio, head_dim)
    grad_query = (
        grad_query.astype(low).astype(jnp.float32).reshape(token_count, head_count, head_dim)
    )
    grad_query = rotate(grad_query, positions, -1.0).reshape(token_count, model_width)
    grad_key = kv_grads[:, :kv_width].reshape(token_count, group_count, head_dim)
    grad_key = rotate(grad_key, positions, -1.0).reshape(token_count, kv_width)
    grad_qkv = jnp.concatenate([grad_query, grad_key, kv_grads[:, kv_width:]], axis=1)
    first_grad, ga_qkv, gB_qkv, gm_qkv = back_full(
        grad_qkv, first_input, weight_qkv, a_qkv, b_qkv, ratio_qkv, n_qkv, m_qkv,
        before_qkv, inner_qkv, cross_qkv, gram_qkv,
    )
    _, first_pull = jax.vjp(lambda v: rms_scale(v, norm_gain_vectors[0]), token_rows)
    grad_inputs = grad_residual + first_pull(first_grad)[0]

    k_end = model_width + kv_width
    full_units = gate_up_magnitude.shape[1]

    def place(piece, axis):
        shape = list(piece.shape)
        shape[axis] = full_units
        return lax.dynamic_update_slice_in_dim(
            jnp.zeros(shape, piece.dtype), piece, start, axis
        )

    summed = lax.psum(
        (
            jnp.concatenate([ga_qkv, ga_o], axis=0).reshape(4, rank, model_width),
            jnp.stack([gB_qkv[:rank, :model_width], gB_o]),
            jnp.stack(
                [gB_qkv[rank : 2 * rank, model_width:k_end], gB_qkv[2 * rank :, k_end:]]
            ),
            gm_qkv[:model_width],
            gm_qkv[model_width:].reshape(2, kv_width),
            gm_o,
            jnp.stack(ga_gu),
            place(jnp.stack(gB_gu), 2),
            place(jnp.stack(gm_gu), 1),
            place(ga_d, 1),
            gB_d,
            gm_d,
        ),
        ("rows", "seq"),
    )
    norms_gu = lax.all_gather(
        jnp.stack([branch[0][0], branch[1][0]]), "seq", axis=1, tiled=True
    )
    stats = jnp.stack(
        [
            drift_stats(query_magnitude, n_qkv[:model_width]),
            drift_stats(key_value_magnitude[0], n_qkv[model_width:k_end]),
            drift_stats(key_value_magnitude[1], n_qkv[k_end:]),
            drift_stats(output_magnitude, n_o),
            drift_stats(gate_up_magnitude[0], norms_gu[0]),
            drift_stats(gate_up_magnitude[1], norms_gu[1]),
            drift_stats(down_magnitude, n_d),
        ]
    )
    shape = (pair_rows, span_len, model_width)
    return (layer_result.reshape(shape), grad_inputs.reshape(shape), *summed, stats)


def solution(mesh):
    return jax.shard_map(
        local,
        mesh=mesh,
        in_specs=(
            P("rows", "seq", None),
            P("rows", "seq", None),
            P(),
            P(None, "seq", None),
            P(None, "seq", None),
            P(None, "seq", None),
            P("seq", None),
            P(),
            P(),
            P(),
            P(),
            P(),
            P(),
            P(),
            P(),
            P(),
            P(),
            P(),
            P(),
            P("rows"),
            P("rows"),
        ),
        out_specs=(
            P("rows", "seq", None),
            P("rows", "seq", None),
            P(),
            P(),
            P(),
            P(),
            P(),
            P(),
            P(),
            P(),
            P(),
            P(),
            P(),
            P(),
            P(),
        ),
        check_vma=False,
    )
```

```python
import functools

import jax
import jax.numpy as jnp
from jax import lax
from jax.experimental import pallas as pl
from jax.experimental.pallas import tpu as pltpu
from jax.sharding import PartitionSpec as P

HEADS = 32
KV_HEADS = 8
HEAD_DIM = 64
ADAPTER_RANK = 16
ALPHA = 32


highest = lax.Precision.HIGHEST
last_last = (((1,), (1,)), ((), ()))
first_first = (((0,), (0,)), ((), ()))


def rms_scale(values, gain):
    inverse = lax.rsqrt(jnp.mean(values * values, axis=-1, keepdims=True) + 1e-05)
    return values * inverse * gain


def rotate(values, positions, direction_sign):
    half_dim = values.shape[-1] // 2
    frequency = 500000.0 ** (-(jnp.arange(half_dim, dtype=jnp.float32) * 2.0) / values.shape[-1])
    angles = positions.astype(jnp.float32)[:, None] * frequency[None, :]
    cosine = jnp.cos(angles)[:, None, :]
    sine_part = direction_sign * jnp.sin(angles)[:, None, :]
    first_half = values[..., :half_dim]
    second_half = values[..., half_dim:]
    return jnp.concatenate(
        [
            first_half * cosine - second_half * sine_part,
            second_half * cosine + first_half * sine_part,
        ],
        axis=-1,
    )


MESH = pl.DeviceIdType.MESH


def place_in_seq():
    s = lax.axis_index("seq")
    return s, s // 2, lax.rem(s, 2)


def greet(nc, q, s):
    barrier = pltpu.get_barrier_semaphore()

    def signal(target):
        pl.semaphore_signal(barrier, inc=1, device_id={"seq": target}, device_id_type=MESH)

    sibling = s + 1 - 2 * lax.rem(s, 2)
    signal(sibling)
    pl.when(q > 0)(lambda: signal(s - 2))
    pl.when(q < nc - 1)(lambda: signal(s + 2))
    pl.semaphore_wait(barrier, 1 + jnp.where(q > 0, 1, 0) + jnp.where(q < nc - 1, 1, 0))
    return sibling


def gather_kernel(n, count, *refs):
    nc = n // 2
    xs, outs = refs[:count], refs[count : 2 * count]
    local_sem, to_sib, to_left, to_right, recv = refs[2 * count :]
    s, q, c = place_in_seq()
    sibling = greet(nc, q, s)
    locals_ = [
        pltpu.make_async_copy(xs[k], outs[k].at[s], local_sem.at[k]) for k in range(count)
    ]
    for cp in locals_:
        cp.start()

    def copy(k, src, slot, sems, target):
        return pltpu.make_async_remote_copy(
            src_ref=src,
            dst_ref=outs[k].at[slot],
            send_sem=sems.at[k, slot],
            recv_sem=recv.at[k, slot],
            device_id={"seq": target},
            device_id_type=MESH,
        )

    for k in range(count):
        pl.when(q > 0)(lambda k=k: copy(k, xs[k], s, to_left, s - 2).start())
        pl.when(q < nc - 1)(lambda k=k: copy(k, xs[k], s, to_right, s + 2).start())
        copy(k, xs[k], s, to_sib, sibling).start()
    for t in range(1, nc):

        @pl.when(q - t >= 0)
        def _(t=t):
            slot = s - 2 * t
            for k in range(count):
                src = outs[k].at[slot]
                copy(k, src, slot, to_right, s).wait_recv()
                pl.when(q < nc - 1)(
                    lambda k=k: copy(k, src, slot, to_right, s + 2).start()
                )
                copy(k, src, slot, to_sib, sibling).start()

        @pl.when(q + t < nc)
        def _(t=t):
            slot = s + 2 * t
            for k in range(count):
                src = outs[k].at[slot]
                copy(k, src, slot, to_left, s).wait_recv()
                pl.when(q > 0)(lambda k=k: copy(k, src, slot, to_left, s - 2).start())
                copy(k, src, slot, to_sib, sibling).start()

    for cp in locals_:
        cp.wait()
    other = 1 - 2 * c
    for p in range(nc):
        mine, theirs = 2 * p + c, 2 * p + c + other
        for k in range(count):
            copy(k, outs[k].at[theirs], theirs, to_sib, sibling).wait_recv()
            copy(k, outs[k].at[mine], mine, to_sib, sibling).wait_send()
            pl.when((q < nc - 1) & (p <= q))(
                lambda k=k: copy(k, outs[k].at[mine], mine, to_right, sibling).wait_send()
            )
            pl.when((q > 0) & (p >= q))(
                lambda k=k: copy(k, outs[k].at[mine], mine, to_left, sibling).wait_send()
            )


def gather_seq(n, arrays, collective_id):
    count = len(arrays)
    nbytes = sum(a.size * a.dtype.itemsize for a in arrays)
    dma = pltpu.SemaphoreType.DMA
    return pl.pallas_call(
        functools.partial(gather_kernel, n, count),
        out_shape=tuple(jax.ShapeDtypeStruct((n, *a.shape), a.dtype) for a in arrays),
        in_specs=[pl.BlockSpec(memory_space=pl.ANY)] * count,
        out_specs=tuple([pl.BlockSpec(memory_space=pl.ANY)] * count),
        scratch_shapes=[dma((count,))] + [dma((count, n))] * 4,
        compiler_params=pltpu.CompilerParams(collective_id=collective_id, has_side_effects=True),
        cost_estimate=pl.CostEstimate(flops=0, transcendentals=0, bytes_accessed=nbytes * n * 20),
        name="gather_seq",
    )(*arrays)


def scatter_kernel(n, x_ref, o_ref, own, sib, from_left, from_right, load_sem, to_sib, sib_in, to_right, right_in, to_left, left_in):
    nc = n // 2
    s, q, c = place_in_seq()
    sibling = greet(nc, q, s)
    theirs = 1 - c

    def load(p):
        return pltpu.make_async_copy(x_ref.at[2 * p + c], own.at[p], load_sem.at[p])

    def to_sibling(p):
        return pltpu.make_async_remote_copy(
            src_ref=x_ref.at[2 * p + theirs],
            dst_ref=sib.at[p],
            send_sem=to_sib.at[p],
            recv_sem=sib_in.at[p],
            device_id={"seq": sibling},
            device_id_type=MESH,
        )

    def rightward(p, target):
        return pltpu.make_async_remote_copy(
            src_ref=own.at[p],
            dst_ref=from_left.at[p],
            send_sem=to_right.at[p],
            recv_sem=right_in.at[p],
            device_id={"seq": target},
            device_id_type=MESH,
        )

    def leftward(p, target):
        return pltpu.make_async_remote_copy(
            src_ref=own.at[p],
            dst_ref=from_right.at[p],
            send_sem=to_left.at[p],
            recv_sem=left_in.at[p],
            device_id={"seq": target},
            device_id_type=MESH,
        )

    order = []
    for t in range(nc):
        for p in (nc - 1 - t, t):
            if p not in order:
                order.append(p)
    for p in order:
        to_sibling(p).start()
        load(p).start()

    f32 = jnp.float32
    for p in order:
        load(p).wait()
        to_sibling(p).wait_recv()

        @pl.when(p > q)
        def _(p=p):
            @pl.when(q > 0)
            def _():
                rightward(p, s).wait_recv()
                total = own[p].astype(f32) + sib[p].astype(f32) + from_left[p].astype(f32)
                own[p] = total.astype(own.dtype)

            @pl.when(q == 0)
            def _():
                own[p] = (own[p].astype(f32) + sib[p].astype(f32)).astype(own.dtype)

            rightward(p, s + 2).start()

        @pl.when(p < q)
        def _(p=p):
            @pl.when(q < nc - 1)
            def _():
                leftward(p, s).wait_recv()
                total = own[p].astype(f32) + sib[p].astype(f32) + from_right[p].astype(f32)
                own[p] = total.astype(own.dtype)

            @pl.when(q == nc - 1)
            def _():
                own[p] = (own[p].astype(f32) + sib[p].astype(f32)).astype(own.dtype)

            leftward(p, s - 2).start()

    o_ref[...] = own[q].astype(f32) + sib[q].astype(f32)

    @pl.when(q > 0)
    def _():
        rightward(q, s).wait_recv()
        o_ref[...] += from_left[q].astype(f32)

    @pl.when(q < nc - 1)
    def _():
        leftward(q, s).wait_recv()
        o_ref[...] += from_right[q].astype(f32)

    for p in range(nc):
        to_sibling(p).wait_send()
        pl.when(p > q)(lambda p=p: rightward(p, s).wait_send())
        pl.when(p < q)(lambda p=p: leftward(p, s).wait_send())


def scatter_seq(n, x, collective_id):
    nc = n // 2
    _, rows, cols = x.shape
    dma = pltpu.SemaphoreType.DMA
    buf = pltpu.VMEM((nc, rows, cols), x.dtype)
    return pl.pallas_call(
        functools.partial(scatter_kernel, n),
        out_shape=jax.ShapeDtypeStruct((rows, cols), jnp.float32),
        in_specs=[pl.BlockSpec(memory_space=pl.ANY)],
        out_specs=pl.BlockSpec(memory_space=pltpu.VMEM),
        scratch_shapes=[buf] * 4 + [dma((nc,))] * 7,
        compiler_params=pltpu.CompilerParams(
            collective_id=collective_id, has_side_effects=True, vmem_limit_bytes=32 << 20
        ),
        cost_estimate=pl.CostEstimate(flops=0, transcendentals=0, bytes_accessed=x.size * 2 * 20),
        name="scatter_seq",
    )(x)


def near_first(i, q, nc):
    short = jnp.where(q <= nc - 1 - q, q, nc - 1 - q)
    far = jnp.where(q <= nc - 1 - q, i, nc - 1 - i)
    step = (i + 1) // 2
    near = q - step if i % 2 else q + step
    return jnp.where(i <= 2 * short, near, far)


def weights_kernel(n, rows, xa, wa, local, edge, a_in, a_sib_in, a_out, a_sib_out):
    nc, half = n // 2, rows // 2
    others = half - 1
    s, q, c = place_in_seq()
    sibling = s + 1 - 2 * c
    r = lax.axis_index("rows")
    a, b = r // 2, lax.rem(r, 2)
    b_row = r + 1 - 2 * b

    def a_row(k):
        return lax.rem(a + k + half, half) * 2 + b

    def diagonal(k):
        return lax.rem(a + k + half, half) * 2 + 1 - b

    barrier = pltpu.get_barrier_semaphore()
    for t in range(1, n):
        pl.semaphore_signal(
            barrier, inc=1, device_id=(r, lax.rem(s + t, n)), device_id_type=MESH
        )
    pl.semaphore_signal(barrier, inc=1, device_id=(b_row, s), device_id_type=MESH)
    for k in range(1, half):
        pl.semaphore_signal(barrier, inc=1, device_id=(a_row(k), s), device_id_type=MESH)
    pl.semaphore_wait(barrier, n - 1 + half)

    def remote(src, dst, send, recv, row, seq):
        return pltpu.make_async_remote_copy(
            src_ref=src, dst_ref=dst, send_sem=send, recv_sem=recv,
            device_id=(row, seq), device_id_type=MESH,
        )

    both, first, second = pl.ds(0, 2), pl.ds(0, 1), pl.ds(1, 1)
    LINE, FROM_B = 0, 1

    def from_a(k):
        return 1 + k

    def relay_b(k):
        return 1 + others + k

    def relay_a(k):
        return 1 + 2 * others + k

    def a_view(p, core, parts, row):
        return wa.at[parts, 2 * p + core, row]

    def content(kind):
        if kind == LINE:
            return both, r
        if kind == FROM_B:
            return both, b_row
        for k in range(1, half):
            if kind == from_a(k):
                return both, a_row(-k)
            if kind == relay_b(k):
                return second, diagonal(-k)
            if kind == relay_a(k):
                return first, diagonal(-k)

    kinds = 2 + 3 * others

    def a_send(p, parts, row, kind, target_row):
        return remote(
            a_view(p, c, parts, row), a_view(p, c, parts, row),
            a_out.at[p, kind], a_in.at[p, kind], target_row, s,
        )

    def a_arrival(p, kind):
        parts, row = content(kind)
        return a_send(p, parts, row, kind, r)

    def a_to_sibling(p, kind, core):
        parts, row = content(kind)
        return remote(
            a_view(p, core, parts, row), a_view(p, core, parts, row),
            a_sib_out.at[p, kind], a_sib_in.at[p, kind], r, sibling,
        )

    def line_send(p, src, sem, target):
        return remote(src, a_view(p, c, both, r), sem, a_in.at[p, LINE], r, target)

    own = xa.at[both, r]
    to_left = lambda: line_send(q, own, edge.at[0], s - 2)
    to_right = lambda: line_send(q, own, edge.at[1], s + 2)
    pl.when(q > 0)(lambda: to_left().start())
    pl.when(q < nc - 1)(lambda: to_right().start())
    order = [near_first(i, q, nc) for i in range(nc)]
    sib_a = lambda: remote(xa, wa.at[:, s], edge.at[2], edge.at[3], r, sibling)
    keep_a = pltpu.make_async_copy(xa, wa.at[:, s], local.at[0])
    sib_a().start()
    keep_a.start()

    def spread_a(p):
        a_send(p, both, r, FROM_B, b_row).start()
        for k in range(1, half):
            a_send(p, both, r, from_a(k), a_row(k)).start()

    for p in order[1:]:
        a_arrival(p, LINE).wait_recv()
        pl.when((p < q) & (q < nc - 1))(
            lambda p=p: line_send(p, a_view(p, c, both, r), a_out.at[p, LINE], s + 2).start()
        )
        pl.when((p > q) & (q > 0))(
            lambda p=p: line_send(p, a_view(p, c, both, r), a_out.at[p, LINE], s - 2).start()
        )
        spread_a(p)
        a_to_sibling(p, LINE, c).start()
    for p in order[1:]:
        a_arrival(p, FROM_B).wait_recv()
        for k in range(1, half):
            a_send(p, first, b_row, relay_a(k), a_row(k)).start()
        a_to_sibling(p, FROM_B, c).start()
        for k in range(1, half):
            a_arrival(p, from_a(k)).wait_recv()
            a_send(p, second, a_row(-k), relay_b(k), b_row).start()
            a_to_sibling(p, from_a(k), c).start()
    for p in order[1:]:
        for k in range(1, half):
            for kind in (relay_b(k), relay_a(k)):
                a_arrival(p, kind).wait_recv()
                a_to_sibling(p, kind, c).start()
    keep_a.wait()
    sib_a().wait()
    pl.when(q > 0)(lambda: to_left().wait_send())
    pl.when(q < nc - 1)(lambda: to_right().wait_send())
    for p in order[1:]:
        pl.when(((p < q) & (q < nc - 1)) | ((p > q) & (q > 0)))(
            lambda p=p: line_send(p, a_view(p, c, both, r), a_out.at[p, LINE], s).wait_send()
        )
        for kind in range(kinds):
            a_to_sibling(p, kind, c).wait_send()
            a_to_sibling(p, kind, 1 - c).wait_recv()
        a_send(p, both, r, FROM_B, b_row).wait_send()
        for k in range(1, half):
            a_send(p, both, r, from_a(k), r).wait_send()
            a_send(p, first, b_row, relay_a(k), r).wait_send()
            a_send(p, second, a_row(-k), relay_b(k), r).wait_send()


def gather_weights(n, rows, xa, collective_id):
    nc = n // 2
    block = xa.shape[1]
    part = block // rows
    xa = xa.reshape(2, rows, part, xa.shape[2])
    kinds = 2 + 3 * (rows // 2 - 1)
    dma = pltpu.SemaphoreType.DMA
    anywhere = pl.BlockSpec(memory_space=pl.ANY)
    wa = pl.pallas_call(
        functools.partial(weights_kernel, n, rows),
        out_shape=jax.ShapeDtypeStruct((2, n, rows, part, xa.shape[3]), xa.dtype),
        in_specs=[anywhere],
        out_specs=anywhere,
        scratch_shapes=[dma((1,)), dma((4,))] + [dma((nc, kinds))] * 4,
        compiler_params=pltpu.CompilerParams(collective_id=collective_id, has_side_effects=True),
        cost_estimate=pl.CostEstimate(
            flops=0, transcendentals=0, bytes_accessed=250 * 1024 * 1024
        ),
        name="gather_weights",
    )(xa)
    return wa.reshape(2, n * block, -1)

def reshard_units(gate_up, n, rows):
    half = rows // 2
    _, block, units_all = gate_up.shape
    part, units = block // rows, units_all // n
    r = lax.axis_index("rows")
    a, b = r // 2, lax.rem(r, 2)
    mine = lax.dynamic_slice_in_dim(gate_up, r * part, part, 1)
    mine = mine.reshape(2, part, n, units).transpose(2, 0, 1, 3)
    mine = lax.all_to_all(mine, "seq", split_axis=0, concat_axis=0, tiled=True)
    swap = [(i, i ^ 1) for i in range(rows)]
    turns = [[(i, (i + 2 * k) % rows) for i in range(rows)] for k in range(1, half)]
    from_b = lax.ppermute(mine, "rows", swap)
    from_a = [lax.ppermute(mine, "rows", turn) for turn in turns]
    pieces, holds = [mine, from_b], [r, 2 * a + 1 - b]
    for k in range(1, half):
        a_from = lax.rem(a - k + half, half)
        pieces.append(from_a[k - 1])
        holds.append(2 * a_from + b)
        gate = lax.ppermute(from_b[:, 0], "rows", turns[k - 1])
        lift = lax.ppermute(from_a[k - 1][:, 1], "rows", swap)
        pieces.append(jnp.stack([gate, lift], axis=1))
        holds.append(2 * a_from + 1 - b)
    return pieces, holds


def join_units(pieces, holds):
    rows = len(pieces)
    n, _, part, units = pieces[0].shape
    joined = jnp.zeros((2, n, rows, part, units), pieces[0].dtype)
    for piece, hold in zip(pieces, holds):
        joined = lax.dynamic_update_slice_in_dim(
            joined, piece.transpose(1, 0, 2, 3)[:, :, None], hold, 2
        )
    return joined.reshape(2, n * rows * part, units)


SCALE = ALPHA / ADAPTER_RANK


def dot_f32(a, b):
    return jnp.dot(a, b, preferred_element_type=jnp.float32)


def dot_nt(a, b):
    return lax.dot_general(a, b, last_last, preferred_element_type=jnp.float32)


def dot_tn(a, b):
    return lax.dot_general(a, b, first_first, preferred_element_type=jnp.float32)


def block_rows(blocks):
    total = sum(b.shape[1] for b in blocks)
    rows, start = [], 0
    for b in blocks:
        rows.append(jnp.pad(b, ((0, 0), (start, total - start - b.shape[1]))))
        start += b.shape[1]
    return jnp.concatenate(rows, axis=0)


def square_terms(weight, a_low, b_low):
    cross = dot_f32(a_low, weight)
    squares = jnp.sum(jnp.square(weight.astype(jnp.float32)), axis=0)
    return squares + 2.0 * SCALE * jnp.sum(b_low.astype(jnp.float32) * cross, axis=0), cross


def gram_times_b(a_low, b_low):
    a_wide = a_low.astype(jnp.float32)
    return jnp.dot(
        jnp.dot(a_wide, a_wide.T, precision=highest), b_low.astype(jnp.float32), precision=highest
    )


def project(rows, weight, a_low, b_low):
    base = dot_f32(rows, weight)
    inner = dot_nt(rows, a_low).astype(jnp.bfloat16)
    return base + SCALE * dot_f32(inner, b_low), inner


def back_low(grad_before, a_low, b_low):
    return (SCALE * dot_nt(grad_before, b_low)).astype(jnp.bfloat16)


def spread_term(weight, a_low, b_low, column):
    b_wide = b_low.astype(jnp.float32)
    weighted = b_wide * column
    upper = weighted.astype(jnp.bfloat16)
    lower = (weighted - upper.astype(jnp.float32)).astype(jnp.bfloat16)
    rank = b_low.shape[0]
    both = dot_nt(jnp.concatenate([upper, lower], axis=0), weight)
    inner = jnp.dot(weighted, b_wide.T, precision=highest)
    return (
        both[:rank]
        + both[rank:]
        + SCALE * jnp.dot(inner, a_low.astype(jnp.float32), precision=highest)
    )

def to_heads(flat, pair_rows, span_len, group_count, ratio, head_dim):
    shaped = flat.reshape(pair_rows, span_len, group_count, ratio, head_dim)
    return shaped.transpose(2, 0, 3, 1, 4).reshape(
        group_count, pair_rows, ratio * span_len, head_dim
    )


def from_heads(stacked, pair_rows, span_len, group_count, ratio, head_dim):
    shaped = stacked.reshape(group_count, pair_rows, ratio, span_len, head_dim)
    return shaped.transpose(1, 3, 0, 2, 4).reshape(
        pair_rows * span_len, group_count * ratio * head_dim
    )


def keys_to_heads(whole, group_count, head_dim):
    pair_rows, length_all, _ = whole.shape
    return whole.reshape(pair_rows, length_all, group_count, head_dim).transpose(2, 0, 1, 3)


def keys_from_heads(stacked):
    group_count, pair_rows, length_all, head_dim = stacked.shape
    return stacked.transpose(1, 2, 0, 3).reshape(pair_rows, length_all, group_count * head_dim)


def score_block(head_q, head_k, row_pos, key_pos, valid_len):
    scores = jnp.einsum(
        "rqd,rkd->rqk", head_q, head_k, preferred_element_type=jnp.float32
    ) * head_q.shape[-1] ** (-0.5)
    allowed = (key_pos[None, None, :] <= row_pos[None, :, None]) & (
        key_pos[None, None, :] < valid_len[:, None, None]
    )
    return (scores, allowed)


def drift_stats(magnitude_vector, norms):
    drift = jnp.sqrt(jnp.mean(jnp.square(magnitude_vector - norms))) / jnp.sqrt(
        jnp.mean(jnp.square(magnitude_vector)) + 1e-06
    )
    return jnp.stack([drift, jnp.mean(norms)])


def local(
    layer_input,
    output_gradient,
    norm_gain_vectors,
    query_output_frozen,
    key_value_frozen,
    gate_up_frozen,
    down_frozen_weight,
    attention_adapter_a,
    query_output_adapter_b,
    key_value_adapter_b,
    query_magnitude,
    key_value_magnitude,
    output_magnitude,
    gate_up_adapter_a,
    gate_up_adapter_b,
    gate_up_magnitude,
    down_adapter_a,
    down_adapter_b,
    down_magnitude,
    prompt_length_list,
    response_length_list,
):
    pair_rows, span_len, model_width = layer_input.shape
    token_count = pair_rows * span_len
    head_count, group_count, head_dim = HEADS, KV_HEADS, HEAD_DIM
    ratio = head_count // group_count
    kv_width = group_count * head_dim
    seq_size = lax.axis_size("seq")
    seq_index = lax.axis_index("seq")
    first_member = (seq_index == 0).astype(jnp.float32)
    low = jnp.bfloat16
    rank = ADAPTER_RANK

    rows_size = lax.axis_size("rows")
    packed = jnp.stack(
        [
            jnp.concatenate([query_output_frozen[0], key_value_frozen[0]], axis=1),
            jnp.concatenate([key_value_frozen[1], query_output_frozen[1]], axis=1),
        ]
    )
    weight_parts = gather_weights(seq_size, rows_size, packed, 1)
    weight_qk, weight_v = weight_parts[0], weight_parts[1, :, :kv_width]
    weight_o = weight_parts[1, :, kv_width:]
    weight_qkv = jnp.concatenate([weight_qk, weight_v], axis=1)
    weight_gu = join_units(*reshard_units(gate_up_frozen, seq_size, rows_size))
    weight_d = down_frozen_weight
    slice_units = weight_d.shape[0]

    a_qkv = attention_adapter_a[:3].reshape(3 * rank, model_width).astype(low)
    b_qkv = block_rows(
        [query_output_adapter_b[0], key_value_adapter_b[0], key_value_adapter_b[1]]
    ).astype(low)
    m_qkv = jnp.concatenate([query_magnitude, key_value_magnitude[0], key_value_magnitude[1]])
    a_o = attention_adapter_a[3].astype(low)
    b_o = query_output_adapter_b[1].astype(low)
    a_gu = gate_up_adapter_a.astype(low)
    start = seq_index * slice_units
    b_gu = lax.dynamic_slice_in_dim(gate_up_adapter_b, start, slice_units, 2).astype(low)
    m_gu = lax.dynamic_slice_in_dim(gate_up_magnitude, start, slice_units, 1)
    a_d = down_adapter_a.astype(low)
    a_d_local = lax.dynamic_slice_in_dim(a_d, start, slice_units, 1)
    b_d = down_adapter_b.astype(low)

    def norms_of(squares, a_low, b_low):
        b_wide = b_low.astype(jnp.float32)
        gram_b = gram_times_b(a_low, b_low)
        return jnp.sqrt(squares + SCALE * SCALE * jnp.sum(b_wide * gram_b, axis=0) + 1e-06), gram_b

    sq_d, cross_d = square_terms(weight_d, a_d_local, b_d)
    sq_d = lax.psum(sq_d, "seq")
    n_d, gram_d = norms_of(sq_d, a_d, b_d)
    ratio_d = down_magnitude / n_d

    sq_qkv, cross_qkv = square_terms(weight_qkv, a_qkv, b_qkv)
    n_qkv, gram_qkv = norms_of(sq_qkv, a_qkv, b_qkv)
    ratio_qkv = m_qkv / n_qkv
    sq_o, cross_o = square_terms(weight_o, a_o, b_o)
    n_o, gram_o = norms_of(sq_o, a_o, b_o)
    ratio_o = output_magnitude / n_o

    query_pos = seq_index * span_len + jnp.arange(span_len, dtype=jnp.int32)
    positions = jnp.tile(query_pos, pair_rows)
    row_pos = jnp.tile(query_pos, ratio)
    key_pos = jnp.arange(span_len * seq_size, dtype=jnp.int32)
    valid_len = prompt_length_list[0] + response_length_list

    token_rows = layer_input.reshape(token_count, model_width).astype(jnp.float32)
    first_input = rms_scale(token_rows, norm_gain_vectors[0]).astype(low)
    before_qkv, inner_qkv = project(first_input, weight_qkv, a_qkv, b_qkv)
    qkv = before_qkv * ratio_qkv
    q_flat = qkv[:, :model_width]
    k_flat = qkv[:, model_width : model_width + kv_width]
    v_flat = qkv[:, model_width + kv_width :]
    queries = rotate(q_flat.reshape(token_count, head_count, head_dim), positions, 1.0).astype(low)
    key_rows = rotate(k_flat.reshape(token_count, group_count, head_dim), positions, 1.0).astype(
        low
    )
    keys_values = jnp.concatenate(
        [key_rows.reshape(token_count, kv_width), v_flat.astype(low)], axis=1
    )
    (kv_all,) = gather_seq(seq_size, [keys_values], 2)
    kv_all = kv_all.reshape(seq_size, pair_rows, span_len, 2 * kv_width)
    kv_all = kv_all.transpose(1, 0, 2, 3).reshape(pair_rows, seq_size * span_len, 2 * kv_width)
    query_heads = to_heads(
        queries.reshape(token_count, model_width), pair_rows, span_len, group_count, ratio, head_dim
    )
    key_heads = keys_to_heads(kv_all[..., :kv_width], group_count, head_dim)
    value_heads = keys_to_heads(kv_all[..., kv_width:], group_count, head_dim)

    def forward_head(operands):
        head_q, head_k, head_v = operands
        scores, allowed = score_block(head_q, head_k, row_pos, key_pos, valid_len)
        masked = jnp.where(allowed, scores, -1e30)
        row_max = jnp.max(masked, axis=-1, keepdims=True)
        unscaled = jnp.exp(masked - row_max)
        row_total = jnp.sum(unscaled, axis=-1, keepdims=True)
        shares = unscaled / row_total
        mixed_out = jnp.einsum(
            "rqk,rkd->rqd", shares.astype(jnp.bfloat16), head_v, preferred_element_type=jnp.float32
        )
        return (mixed_out, (row_max + jnp.log(row_total))[..., 0])

    mixed_heads, log_totals = lax.map(forward_head, (query_heads, key_heads, value_heads))
    attended = from_heads(
        mixed_heads, pair_rows, span_len, group_count, ratio, head_dim
    ).astype(low)
    before_o, inner_o = project(attended, weight_o, a_o, b_o)
    residual = token_rows + before_o * ratio_o
    second_input = rms_scale(residual, norm_gain_vectors[1]).astype(low)

    (u2,) = gather_seq(seq_size, [second_input], 3)
    u2 = u2.reshape(seq_size * token_count, model_width)
    grad_out_rows = output_gradient.reshape(token_count, model_width)
    gy_all = lax.all_gather(grad_out_rows, "seq", axis=0, tiled=True)
    gb_d = (gy_all.astype(jnp.float32) * ratio_d).astype(low)
    gi_d = back_low(gb_d, a_d, b_d)
    grad_hidden = dot_nt(gb_d, weight_d) + dot_f32(gi_d, a_d_local)

    branch = []
    for i in range(2):
        sq, cross = square_terms(weight_gu[i], a_gu[i], b_gu[i])
        norm, gram_b = norms_of(sq, a_gu[i], b_gu[i])
        before, inner = project(u2, weight_gu[i], a_gu[i], b_gu[i])
        branch.append((norm, gram_b, cross, m_gu[i] / norm, before, inner))
    gate = branch[0][4] * branch[0][3]
    lift = branch[1][4] * branch[1][3]
    sig = jax.nn.sigmoid(gate)
    silu = sig * gate
    hidden = (silu * lift).astype(low)
    down_partial = dot_f32(hidden, weight_d)
    inner_d_partial = dot_nt(hidden, a_d_local)
    down_sum = lax.psum_scatter(down_partial.astype(low), "seq", scatter_dimension=0, tiled=True)
    inner_d = lax.psum_scatter(inner_d_partial, "seq", scatter_dimension=0, tiled=True).astype(low)
    before_d = down_sum.astype(jnp.float32) + SCALE * dot_f32(inner_d, b_d)
    layer_result = (residual + before_d * ratio_d).astype(low)

    grad_rows = grad_out_rows.astype(jnp.float32)
    gm_d = jnp.sum(grad_rows * before_d, axis=0) / n_d
    gm_d_line = lax.psum(gm_d, "seq")
    c_d = -gm_d_line * down_magnitude / (n_d * n_d)
    gb_d_own = (grad_rows * ratio_d).astype(low)
    spread_d = spread_term(weight_d, jnp.zeros_like(a_d_local), b_d, c_d)
    weighted_d = b_d.astype(jnp.float32) * c_d
    spread_d = spread_d + SCALE * jnp.dot(
        jnp.dot(weighted_d, b_d.astype(jnp.float32).T, precision=highest),
        a_d_local.astype(jnp.float32),
        precision=highest,
    )
    ga_d = dot_tn(gi_d, hidden) + SCALE * spread_d
    gB_d = SCALE * dot_tn(inner_d, gb_d_own) + SCALE * c_d * (
        cross_d + first_member * SCALE * gram_d
    )

    ggate = grad_hidden * lift * sig * (1.0 + gate * (1.0 - sig))
    glift = grad_hidden * silu
    grad_in = None
    ga_gu, gB_gu, gm_gu = [], [], []
    for i, g in enumerate((ggate, glift)):
        norm, gram_b, cross, rat, before, inner = branch[i]
        gb = (g * rat).astype(low)
        gi = back_low(gb, a_gu[i], b_gu[i])
        term = dot_nt(gb, weight_gu[i])
        gm = jnp.sum(g * before, axis=0) / norm
        c = -gm * m_gu[i] / (norm * norm)
        grad_in = term if grad_in is None else grad_in + term
        low_term = dot_f32(gi, a_gu[i])
        grad_in = grad_in + low_term
        ga_gu.append(dot_tn(gi, u2) + SCALE * spread_term(weight_gu[i], a_gu[i], b_gu[i], c))
        gB_gu.append(SCALE * dot_tn(inner, gb) + SCALE * c * (cross + SCALE * gram_b))
        gm_gu.append(gm)
    in_grad = scatter_seq(
        seq_size, grad_in.astype(low).reshape(seq_size, token_count, model_width), 4
    )
    _, second_pull = jax.vjp(lambda v: rms_scale(v, norm_gain_vectors[1]), residual)
    grad_residual = grad_rows + second_pull(in_grad)[0]

    def back_full(upstream, rows, weight, a_low, b_low, ratio_p, norm, magnitude, before, inner, cross, gram_b):
        gb = (upstream * ratio_p).astype(low)
        gi = back_low(gb, a_low, b_low)
        grad_rows_in = dot_nt(gb, weight) + dot_f32(gi, a_low)
        gm = jnp.sum(upstream * before, axis=0) / norm
        c = -gm * magnitude / (norm * norm)
        ga = dot_tn(gi, rows) + SCALE * spread_term(weight, a_low, b_low, c)
        gB = SCALE * dot_tn(inner, gb) + SCALE * c * (cross + SCALE * gram_b)
        return grad_rows_in, ga, gB, gm

    grad_att, ga_o, gB_o, gm_o = back_full(
        grad_residual, attended, weight_o, a_o, b_o, ratio_o, n_o, output_magnitude,
        before_o, inner_o, cross_o, gram_o,
    )
    grad_att_heads = to_heads(
        grad_att.astype(low), pair_rows, span_len, group_count, ratio, head_dim
    )
    scale_factor = head_dim ** (-0.5)

    def backward_head(operands):
        head_q, head_k, head_v, head_lse, head_grad = operands
        scores, allowed = score_block(head_q, head_k, row_pos, key_pos, valid_len)
        shares = jnp.where(allowed, jnp.exp(scores - head_lse[..., None]), 0.0)
        grad_shares = jnp.einsum(
            "rqd,rkd->rqk", head_grad, head_v, preferred_element_type=jnp.float32
        )
        centre = jnp.sum(shares * grad_shares, axis=-1, keepdims=True)
        grad_scores = (shares * (grad_shares - centre)).astype(jnp.bfloat16)
        grad_q = (
            jnp.einsum("rqk,rkd->rqd", grad_scores, head_k, preferred_element_type=jnp.float32)
            * scale_factor
        )
        grad_k = (
            jnp.einsum("rqk,rqd->rkd", grad_scores, head_q, preferred_element_type=jnp.float32)
            * scale_factor
        )
        grad_v = jnp.einsum(
            "rqk,rqd->rkd",
            shares.astype(jnp.bfloat16),
            head_grad,
            preferred_element_type=jnp.float32,
        )
        return (grad_q, grad_k, grad_v)

    grad_q_heads, grad_k_heads, grad_v_heads = lax.map(
        backward_head, (query_heads, key_heads, value_heads, log_totals, grad_att_heads)
    )
    kv_grads = jnp.concatenate(
        [keys_from_heads(grad_k_heads).astype(low), keys_from_heads(grad_v_heads).astype(low)],
        axis=2,
    )
    kv_grads = kv_grads.reshape(pair_rows, seq_size, span_len, 2 * kv_width)
    kv_grads = scatter_seq(
        seq_size,
        kv_grads.transpose(1, 0, 2, 3).reshape(seq_size, token_count, 2 * kv_width),
        5,
    )
    kv_grads = kv_grads.astype(low).astype(jnp.float32)
    grad_query = from_heads(grad_q_heads, pair_rows, span_len, group_count, ratio, head_dim)
    grad_query = (
        grad_query.astype(low).astype(jnp.float32).reshape(token_count, head_count, head_dim)
    )
    grad_query = rotate(grad_query, positions, -1.0).reshape(token_count, model_width)
    grad_key = kv_grads[:, :kv_width].reshape(token_count, group_count, head_dim)
    grad_key = rotate(grad_key, positions, -1.0).reshape(token_count, kv_width)
    grad_qkv = jnp.concatenate([grad_query, grad_key, kv_grads[:, kv_width:]], axis=1)
    first_grad, ga_qkv, gB_qkv, gm_qkv = back_full(
        grad_qkv, first_input, weight_qkv, a_qkv, b_qkv, ratio_qkv, n_qkv, m_qkv,
        before_qkv, inner_qkv, cross_qkv, gram_qkv,
    )
    _, first_pull = jax.vjp(lambda v: rms_scale(v, norm_gain_vectors[0]), token_rows)
    grad_inputs = grad_residual + first_pull(first_grad)[0]

    k_end = model_width + kv_width
    full_units = gate_up_magnitude.shape[1]

    def place(piece, axis):
        shape = list(piece.shape)
        shape[axis] = full_units
        return lax.dynamic_update_slice_in_dim(
            jnp.zeros(shape, piece.dtype), piece, start, axis
        )

    summed = lax.psum(
        (
            jnp.concatenate([ga_qkv, ga_o], axis=0).reshape(4, rank, model_width),
            jnp.stack([gB_qkv[:rank, :model_width], gB_o]),
            jnp.stack(
                [gB_qkv[rank : 2 * rank, model_width:k_end], gB_qkv[2 * rank :, k_end:]]
            ),
            gm_qkv[:model_width],
            gm_qkv[model_width:].reshape(2, kv_width),
            gm_o,
            jnp.stack(ga_gu),
            place(jnp.stack(gB_gu), 2),
            place(jnp.stack(gm_gu), 1),
            place(ga_d, 1),
            gB_d,
            gm_d,
        ),
        ("rows", "seq"),
    )
    norms_gu = lax.all_gather(
        jnp.stack([branch[0][0], branch[1][0]]), "seq", axis=1, tiled=True
    )
    stats = jnp.stack(
        [
            drift_stats(query_magnitude, n_qkv[:model_width]),
            drift_stats(key_value_magnitude[0], n_qkv[model_width:k_end]),
            drift_stats(key_value_magnitude[1], n_qkv[k_end:]),
            drift_stats(output_magnitude, n_o),
            drift_stats(gate_up_magnitude[0], norms_gu[0]),
            drift_stats(gate_up_magnitude[1], norms_gu[1]),
            drift_stats(down_magnitude, n_d),
        ]
    )
    shape = (pair_rows, span_len, model_width)
    return (layer_result.reshape(shape), grad_inputs.reshape(shape), *summed, stats)


def solution(mesh):
    return jax.shard_map(
        local,
        mesh=mesh,
        in_specs=(
            P("rows", "seq", None),
            P("rows", "seq", None),
            P(),
            P(None, "seq", None),
            P(None, "seq", None),
            P(None, "seq", None),
            P("seq", None),
            P(),
            P(),
            P(),
            P(),
            P(),
            P(),
            P(),
            P(),
            P(),
            P(),
            P(),
            P(),
            P("rows"),
            P("rows"),
        ),
        out_specs=(
            P("rows", "seq", None),
            P("rows", "seq", None),
            P(),
            P(),
            P(),
            P(),
            P(),
            P(),
            P(),
            P(),
            P(),
            P(),
            P(),
            P(),
            P(),
        ),
        check_vma=False,
    )
```

```python
import functools

import jax
import jax.numpy as jnp
from jax import lax
from jax.experimental import pallas as pl
from jax.experimental.pallas import tpu as pltpu
from jax.sharding import PartitionSpec as P

HEADS = 32
KV_HEADS = 8
HEAD_DIM = 64
ADAPTER_RANK = 16
ALPHA = 32
SCALE = ALPHA / ADAPTER_RANK
TILE = 512

highest = lax.Precision.HIGHEST
last_last = (((1,), (1,)), ((), ()))
first_first = (((0,), (0,)), ((), ()))

def dot_f32(a, b):
    return jnp.dot(a, b, preferred_element_type=jnp.float32)


def dot_nt(a, b):
    return lax.dot_general(a, b, last_last, preferred_element_type=jnp.float32)


def dot_tn(a, b):
    return lax.dot_general(a, b, first_first, preferred_element_type=jnp.float32)


def unit_rms(v):
    return lax.rsqrt(jnp.mean(v * v, axis=-1, keepdims=True) + 1e-05)


def rms_back(v, gain, upstream):
    r = unit_rms(v)
    scaled = gain * upstream
    return r * scaled - v * (r * r * r) * jnp.mean(scaled * v, axis=-1, keepdims=True)


def turn(z, cosine, sine):
    width = z.shape[1]
    lane = lax.broadcasted_iota(jnp.int32, z.shape, 1)
    half = HEAD_DIM // 2
    other = jnp.where(
        lax.rem(lane, HEAD_DIM) < half, -pltpu.roll(z, width - half, 1), pltpu.roll(z, half, 1)
    )
    copies = width // cosine.shape[1]
    return z * jnp.tile(cosine, (1, copies)) + other * jnp.tile(sine, (1, copies))


def column_norms(w, a, b_wide, cross):
    ones = jnp.ones((16, w.shape[0]), jnp.bfloat16)
    squares = dot_f32(ones, w * w)[:1]
    gram_b = jnp.dot(dot_nt(a, a), b_wide, precision=highest, preferred_element_type=jnp.float32)
    squares = squares + 2.0 * SCALE * jnp.sum(b_wide * cross, axis=0, keepdims=True)
    squares = squares + SCALE * SCALE * jnp.sum(b_wide * gram_b, axis=0, keepdims=True)
    return jnp.sqrt(squares + 1e-06), cross + SCALE * gram_b


def project_kernel(kv_tiles, x_ref, gain_ref, a_ref, w_ref, b_ref, m_ref, cos_ref, sin_ref,
                   u_ref, before_ref, q_ref, kv_ref, n_ref, cross_ref):
    j = pl.program_id(0)
    q_tiles = kv_tiles[0]

    @pl.when(j == 0)
    def _():
        v = x_ref[...].astype(jnp.float32)
        u_ref[...] = (v * unit_rms(v) * gain_ref[...]).astype(jnp.bfloat16)

    a = a_ref[0].astype(jnp.bfloat16)
    b = b_ref[...].astype(jnp.bfloat16)
    b_wide = b.astype(jnp.float32)
    w = w_ref[0]
    rows = u_ref.shape[0]

    @pl.when(j < kv_tiles[1])
    def _():
        both = dot_f32(jnp.concatenate([u_ref[...], a], axis=0), w)
        norm, cross = column_norms(w, a, b_wide, both[rows:])
        n_ref[...] = norm
        cross_ref[...] = cross
        inner = dot_nt(u_ref[...], a).astype(jnp.bfloat16)
        before = both[:rows] + SCALE * dot_f32(inner, b)
        before_ref[...] = before
        y = before * (m_ref[...] / norm)

        @pl.when(j < q_tiles)
        def _():
            q_ref[...] = turn(y, cos_ref[...], sin_ref[...]).astype(jnp.bfloat16)

        @pl.when(j == q_tiles)
        def _():
            kv_ref[...] = turn(y, cos_ref[...], sin_ref[...]).astype(jnp.bfloat16)

        @pl.when(j > q_tiles)
        def _():
            kv_ref[...] = y.astype(jnp.bfloat16)

    @pl.when(j >= kv_tiles[1])
    def _():
        norm, cross = column_norms(w, a, b_wide, dot_f32(a, w))
        n_ref[...] = norm
        cross_ref[...] = cross


def project_qkv(x, gain, a, weights, b, m, cosine, sine):
    rows, width = x.shape
    cols = b.shape[1]
    per_half = weights.shape[2] // TILE
    q_tiles = width // TILE
    k_cols = weights.shape[2] - width
    kv_tiles = (q_tiles, q_tiles + 2 * k_cols // TILE)
    last = kv_tiles[1] - 1
    full = lambda shape: pl.BlockSpec(shape, lambda j: (0,) * len(shape))
    col = lambda height: pl.BlockSpec((height, TILE), lambda j: (0, j))
    which = lambda j: jnp.where(j < q_tiles, 0, jnp.where(j > last, 3, 1 + j - q_tiles))
    f32, low = jnp.float32, jnp.bfloat16
    return pl.pallas_call(
        functools.partial(project_kernel, kv_tiles),
        out_shape=(
            jax.ShapeDtypeStruct((rows, width), low),
            jax.ShapeDtypeStruct((rows, width + 2 * k_cols), f32),
            jax.ShapeDtypeStruct((rows, width), low),
            jax.ShapeDtypeStruct((rows, 2 * k_cols), low),
            jax.ShapeDtypeStruct((1, cols), f32),
            jax.ShapeDtypeStruct((16, cols), f32),
        ),
        grid=(cols // TILE,),
        in_specs=[
            full((rows, width)),
            full((1, width)),
            pl.BlockSpec((1, 16, width), lambda j: (which(j), 0, 0)),
            pl.BlockSpec((1, width, TILE), lambda j: (j // per_half, 0, j % per_half)),
            col(16),
            col(1),
            full(cosine.shape),
            full(sine.shape),
        ],
        out_specs=(
            full((rows, width)),
            pl.BlockSpec((rows, TILE), lambda j: (0, jnp.minimum(j, last))),
            pl.BlockSpec((rows, TILE), lambda j: (0, jnp.minimum(j, q_tiles - 1))),
            pl.BlockSpec((rows, TILE), lambda j: (0, jnp.clip(j - q_tiles, 0, last - q_tiles))),
            col(1),
            col(16),
        ),
        compiler_params=pltpu.CompilerParams(vmem_limit_bytes=40 << 20),
        cost_estimate=pl.CostEstimate(
            flops=2 * rows * width * cols, transcendentals=0, bytes_accessed=2 * width * cols
        ),
        name="project_qkv",
    )(x, gain, a, weights, b, m, cosine, sine)


def out_kernel(att_ref, a_ref, w_ref, b_ref, m_ref, n_ref, x_ref, gain_ref, before_ref, x1_ref, u2_ref):
    t = pl.program_id(0)
    a = a_ref[...].astype(jnp.bfloat16)
    b = b_ref[...].astype(jnp.bfloat16)
    inner = dot_nt(att_ref[...], a).astype(jnp.bfloat16)
    before = dot_f32(att_ref[...], w_ref[0]) + SCALE * dot_f32(inner, b)
    before_ref[...] = before
    x1_ref[:, pl.ds(pl.multiple_of(t * TILE, TILE), TILE)] = (
        x_ref[...].astype(jnp.float32) + before * (m_ref[...] / n_ref[...])
    )

    @pl.when(t == pl.num_programs(0) - 1)
    def _():
        v = x1_ref[...]
        u2_ref[...] = (v * unit_rms(v) * gain_ref[...]).astype(jnp.bfloat16)


def project_out(att, a, weights, b, m, norms, x, gain):
    rows, width = att.shape
    tiles = width // TILE
    skip = (weights.shape[2] - width) // TILE
    full = lambda shape: pl.BlockSpec(shape, lambda t: (0,) * len(shape))
    col = lambda height: pl.BlockSpec((height, TILE), lambda t: (0, t))
    f32 = jnp.float32
    return pl.pallas_call(
        out_kernel,
        out_shape=(
            jax.ShapeDtypeStruct((rows, width), f32),
            jax.ShapeDtypeStruct((rows, width), f32),
            jax.ShapeDtypeStruct((rows, width), jnp.bfloat16),
        ),
        grid=(tiles,),
        in_specs=[
            full((rows, width)),
            full((16, width)),
            pl.BlockSpec((1, width, TILE), lambda t: (1, 0, skip + t)),
            col(16),
            col(1),
            col(1),
            col(rows),
            full((1, width)),
        ],
        out_specs=(col(rows), full((rows, width)), full((rows, width))),
        compiler_params=pltpu.CompilerParams(vmem_limit_bytes=40 << 20),
        cost_estimate=pl.CostEstimate(
            flops=2 * rows * width * width, transcendentals=0, bytes_accessed=2 * width * width
        ),
        name="project_out",
    )(att, a, weights, b, m, norms, x, gain)


def out_back_kernel(in_ref, x1_ref, gain_ref, gy_ref, before_ref, att_ref, a_ref, b_ref, m_ref, n_ref, cross_ref,
                    w_ref, gx_ref, gatt_ref, ga_ref, gb_ref, gm_ref, lhs, gi, tail):
    t = pl.program_id(0)
    rows, width = gx_ref.shape
    low = jnp.bfloat16
    a = a_ref[...].astype(low)

    @pl.when(t == 0)
    def _():
        gx = gy_ref[...].astype(jnp.float32) + rms_back(x1_ref[...], gain_ref[...], in_ref[...])
        gx_ref[...] = gx
        norm = n_ref[...]
        gb = (gx * (m_ref[...] / norm)).astype(low)
        lhs[:rows] = gb
        b = b_ref[...].astype(low)
        b_wide = b.astype(jnp.float32)
        gi[...] = (SCALE * dot_nt(gb, b)).astype(low)
        gm = jnp.sum(gx * before_ref[...], axis=0, keepdims=True) / norm
        gm_ref[...] = gm
        c = -gm * m_ref[...] / (norm * norm)
        weighted = b_wide * c
        lhs[rows:] = weighted.astype(low)
        tail[...] = lax.dot_general(
            weighted, b_wide, last_last, precision=highest, preferred_element_type=jnp.float32
        )
        inner = dot_nt(att_ref[...], a).astype(low)
        gb_ref[...] = SCALE * dot_tn(inner, gb) + SCALE * c * cross_ref[...]

    span = pl.ds(pl.multiple_of(t * TILE, TILE), TILE)
    a_tile = a_ref[:, span].astype(low)
    gi_low = gi[...]
    back = dot_nt(lhs[...], w_ref[0, :, w_ref.shape[2] - width :])
    gatt_ref[...] = (back[:rows] + dot_f32(gi_low, a_tile)).astype(low)
    spread = back[rows:] + SCALE * jnp.dot(
        tail[...], a_tile.astype(jnp.float32), precision=highest, preferred_element_type=jnp.float32
    )
    ga_ref[...] = dot_tn(gi_low, att_ref[:, span]) + SCALE * spread


def out_back(in_grad, x1, gain, gy, before, att, a, b, m, norms, cross, weights):
    rows, width = x1.shape
    tiles = width // TILE
    full = lambda shape: pl.BlockSpec(shape, lambda t: (0,) * len(shape))
    col = lambda height: pl.BlockSpec((height, TILE), lambda t: (0, t))
    f32, low = jnp.float32, jnp.bfloat16
    wide = full((rows, width))
    return pl.pallas_call(
        out_back_kernel,
        out_shape=(
            jax.ShapeDtypeStruct((rows, width), f32),
            jax.ShapeDtypeStruct((rows, width), low),
            jax.ShapeDtypeStruct((16, width), f32),
            jax.ShapeDtypeStruct((16, width), f32),
            jax.ShapeDtypeStruct((1, width), f32),
        ),
        grid=(tiles,),
        in_specs=[wide, wide, full((1, width)), wide, wide, wide, full((16, width)), full((16, width)),
                  full((1, width)), full((1, width)), full((16, width)),
                  pl.BlockSpec((1, TILE, weights.shape[2]), lambda t: (1, t, 0))],
        out_specs=(wide, col(rows), col(16), full((16, width)), full((1, width))),
        scratch_shapes=[
            pltpu.VMEM((rows + 16, width), low),
            pltpu.VMEM((rows, 16), low),
            pltpu.VMEM((16, 16), f32),
        ],
        compiler_params=pltpu.CompilerParams(vmem_limit_bytes=48 << 20),
        cost_estimate=pl.CostEstimate(
            flops=2 * rows * width * width, transcendentals=0, bytes_accessed=2 * width * width
        ),
        name="out_back",
    )(in_grad, x1, gain, gy, before, att, a, b, m, norms, cross, weights)


def qkv_back_kernel(gq_ref, gkv_ref, cos_ref, sin_ref, before_ref, u_ref, a_ref, b_ref, m_ref, n_ref, cross_ref,
                    x_ref, gain_ref, gx_ref, w0_ref, w1_ref,
                    out_ref, ga_ref, gb_ref, gm_ref, lhs0, lhs1, gi, tail):
    t = pl.program_id(0)
    rows, width = gx_ref.shape
    low = jnp.bfloat16
    k_cols = w1_ref.shape[2]
    bounds = [(0, width), (width, width + k_cols), (width + k_cols, width + 2 * k_cols)]

    @pl.when(t == 0)
    def _():
        cosine, sine = cos_ref[...], -sin_ref[...]
        k_parts = [gkv_ref[:, 256 * j : 256 * j + 128] for j in range(k_cols // 128)]
        v_parts = [gkv_ref[:, 256 * j + 128 : 256 * j + 256] for j in range(k_cols // 128)]
        rounded = lambda z: z.astype(low).astype(jnp.float32)
        ups = [
            turn(gq_ref[...].astype(jnp.float32), cosine, sine),
            turn(rounded(jnp.concatenate(k_parts, axis=1)), cosine, sine),
            rounded(jnp.concatenate(v_parts, axis=1)),
        ]
        lhs0[rows:] = jnp.zeros_like(lhs0[rows:])
        lhs1[rows:] = jnp.zeros_like(lhs1[rows:])
        for p, (start, stop) in enumerate(bounds):
            g, norm, m = ups[p], n_ref[:, start:stop], m_ref[:, start:stop]
            a = a_ref[p].astype(low)
            b = b_ref[:, start:stop].astype(low)
            b_wide = b.astype(jnp.float32)
            gb = (g * (m / norm)).astype(low)
            gm = jnp.sum(g * before_ref[:, start:stop], axis=0, keepdims=True) / norm
            gm_ref[:, start:stop] = gm
            c = -gm * m / (norm * norm)
            weighted = b_wide * c
            gi[:, 16 * p : 16 * p + 16] = (SCALE * dot_nt(gb, b)).astype(low)
            tail[16 * p : 16 * p + 16] = lax.dot_general(
                weighted, b_wide, last_last, precision=highest, preferred_element_type=jnp.float32
            )
            inner = dot_nt(u_ref[...], a).astype(low)
            gb_ref[:, start:stop] = SCALE * dot_tn(inner, gb) + SCALE * c * cross_ref[:, start:stop]
            lhs, at = (lhs1, 0) if p == 2 else (lhs0, start)
            lhs[:rows, at : at + stop - start] = gb
            lhs[rows + 16 * p : rows + 16 * p + 16, at : at + stop - start] = weighted.astype(low)

    span = pl.ds(pl.multiple_of(t * TILE, TILE), TILE)
    back = dot_nt(lhs0[...], w0_ref[0]) + dot_nt(lhs1[...], w1_ref[0])
    grad_in = back[:rows]
    for p in range(3):
        a_tile = a_ref[p, :, span].astype(low)
        gi_p = gi[:, 16 * p : 16 * p + 16]
        grad_in = grad_in + dot_f32(gi_p, a_tile)
        spread = back[rows + 16 * p : rows + 16 * p + 16] + SCALE * jnp.dot(
            tail[16 * p : 16 * p + 16], a_tile.astype(jnp.float32), precision=highest,
            preferred_element_type=jnp.float32,
        )
        ga_ref[p] = dot_tn(gi_p, u_ref[:, span]) + SCALE * spread
    out_ref[:, span] = grad_in

    @pl.when(t == pl.num_programs(0) - 1)
    def _():
        v = x_ref[...].astype(jnp.float32)
        out_ref[...] = gx_ref[...] + rms_back(v, gain_ref[...], out_ref[...])


def qkv_back(gq, gkv, cosine, sine, before, u, a, b, m, norms, cross, x, gain, gx, weights):
    rows, width = gx.shape
    cols = before.shape[1]
    k_cols = (cols - width) // 2
    tiles = width // TILE
    full = lambda shape: pl.BlockSpec(shape, lambda t: (0,) * len(shape))
    f32, low = jnp.float32, jnp.bfloat16
    wide = full((rows, width))
    return pl.pallas_call(
        qkv_back_kernel,
        out_shape=(
            jax.ShapeDtypeStruct((rows, width), f32),
            jax.ShapeDtypeStruct((3, 16, width), f32),
            jax.ShapeDtypeStruct((16, cols), f32),
            jax.ShapeDtypeStruct((1, cols), f32),
        ),
        grid=(tiles,),
        in_specs=[wide, full(gkv.shape), full(cosine.shape), full(sine.shape), full((rows, cols)), wide,
                  full((3, 16, width)), full((16, cols)), full((1, cols)), full((1, cols)), full((16, cols)),
                  wide, full((1, width)), wide,
                  pl.BlockSpec((1, TILE, width + k_cols), lambda t: (0, t, 0)),
                  pl.BlockSpec((1, TILE, k_cols), lambda t: (1, t, 0))],
        out_specs=(wide, pl.BlockSpec((3, 16, TILE), lambda t: (0, 0, t)), full((16, cols)), full((1, cols))),
        scratch_shapes=[
            pltpu.VMEM((rows + 48, width + k_cols), low),
            pltpu.VMEM((rows + 48, k_cols), low),
            pltpu.VMEM((rows, 48), low),
            pltpu.VMEM((48, 16), f32),
        ],
        compiler_params=pltpu.CompilerParams(vmem_limit_bytes=48 << 20),
        cost_estimate=pl.CostEstimate(
            flops=2 * rows * width * cols, transcendentals=0, bytes_accessed=2 * width * cols
        ),
        name="qkv_back",
    )(gq, gkv, cosine, sine, before, u, a, b, m, norms, cross, x, gain, gx, weights, weights)

MESH = pl.DeviceIdType.MESH


def place_in_seq():
    s = lax.axis_index("seq")
    return s, s // 2, lax.rem(s, 2)


def greet(nc, q, s):
    barrier = pltpu.get_barrier_semaphore()

    def signal(target):
        pl.semaphore_signal(barrier, inc=1, device_id={"seq": target}, device_id_type=MESH)

    sibling = s + 1 - 2 * lax.rem(s, 2)
    signal(sibling)
    pl.when(q > 0)(lambda: signal(s - 2))
    pl.when(q < nc - 1)(lambda: signal(s + 2))
    pl.semaphore_wait(barrier, 1 + jnp.where(q > 0, 1, 0) + jnp.where(q < nc - 1, 1, 0))
    return sibling


def gather_kernel(n, count, *refs):
    nc = n // 2
    xs, outs = refs[:count], refs[count : 2 * count]
    local_sem, to_sib, to_left, to_right, recv = refs[2 * count :]
    s, q, c = place_in_seq()
    sibling = greet(nc, q, s)
    locals_ = [
        pltpu.make_async_copy(xs[k], outs[k].at[s], local_sem.at[k]) for k in range(count)
    ]
    for cp in locals_:
        cp.start()

    def copy(k, src, slot, sems, target):
        return pltpu.make_async_remote_copy(
            src_ref=src,
            dst_ref=outs[k].at[slot],
            send_sem=sems.at[k, slot],
            recv_sem=recv.at[k, slot],
            device_id={"seq": target},
            device_id_type=MESH,
        )

    for k in range(count):
        pl.when(q > 0)(lambda k=k: copy(k, xs[k], s, to_left, s - 2).start())
        pl.when(q < nc - 1)(lambda k=k: copy(k, xs[k], s, to_right, s + 2).start())
        copy(k, xs[k], s, to_sib, sibling).start()
    for t in range(1, nc):

        @pl.when(q - t >= 0)
        def _(t=t):
            slot = s - 2 * t
            for k in range(count):
                src = outs[k].at[slot]
                copy(k, src, slot, to_right, s).wait_recv()
                pl.when(q < nc - 1)(
                    lambda k=k: copy(k, src, slot, to_right, s + 2).start()
                )
                copy(k, src, slot, to_sib, sibling).start()

        @pl.when(q + t < nc)
        def _(t=t):
            slot = s + 2 * t
            for k in range(count):
                src = outs[k].at[slot]
                copy(k, src, slot, to_left, s).wait_recv()
                pl.when(q > 0)(lambda k=k: copy(k, src, slot, to_left, s - 2).start())
                copy(k, src, slot, to_sib, sibling).start()

    for cp in locals_:
        cp.wait()
    other = 1 - 2 * c
    for p in range(nc):
        mine, theirs = 2 * p + c, 2 * p + c + other
        for k in range(count):
            copy(k, outs[k].at[theirs], theirs, to_sib, sibling).wait_recv()
            copy(k, outs[k].at[mine], mine, to_sib, sibling).wait_send()
            pl.when((q < nc - 1) & (p <= q))(
                lambda k=k: copy(k, outs[k].at[mine], mine, to_right, sibling).wait_send()
            )
            pl.when((q > 0) & (p >= q))(
                lambda k=k: copy(k, outs[k].at[mine], mine, to_left, sibling).wait_send()
            )


def gather_seq(n, arrays, collective_id):
    count = len(arrays)
    nbytes = sum(a.size * a.dtype.itemsize for a in arrays)
    dma = pltpu.SemaphoreType.DMA
    return pl.pallas_call(
        functools.partial(gather_kernel, n, count),
        out_shape=tuple(jax.ShapeDtypeStruct((n, *a.shape), a.dtype) for a in arrays),
        in_specs=[pl.BlockSpec(memory_space=pl.ANY)] * count,
        out_specs=tuple([pl.BlockSpec(memory_space=pl.ANY)] * count),
        scratch_shapes=[dma((count,))] + [dma((count, n))] * 4,
        compiler_params=pltpu.CompilerParams(collective_id=collective_id, has_side_effects=True),
        cost_estimate=pl.CostEstimate(flops=0, transcendentals=0, bytes_accessed=nbytes * n * 20),
        name="gather_seq",
    )(*arrays)


def scatter_kernel(n, x_ref, e_ref, o_ref, all_ref, own, sib, from_left, from_right,
                   load_sem, to_sib, sib_in, to_right, right_in, to_left, left_in, e_out, e_in):
    nc = n // 2
    s, q, c = place_in_seq()
    sibling = s + 1 - 2 * c
    theirs = 1 - c
    barrier = pltpu.get_barrier_semaphore()
    for t in range(1, n):
        pl.semaphore_signal(
            barrier, inc=1, device_id={"seq": lax.rem(s + t, n)}, device_id_type=MESH
        )
    pl.semaphore_wait(barrier, n - 1)

    def small(t, slot):
        return pltpu.make_async_remote_copy(
            src_ref=e_ref,
            dst_ref=all_ref.at[slot],
            send_sem=e_out.at[t],
            recv_sem=e_in.at[t],
            device_id={"seq": lax.rem(s + t, n)},
            device_id_type=MESH,
        )

    for t in range(1, n):
        small(t, s).start()
    all_ref[s] = e_ref[...]

    def load(p):
        return pltpu.make_async_copy(x_ref.at[2 * p + c], own.at[p], load_sem.at[p])

    def to_sibling(p):
        return pltpu.make_async_remote_copy(
            src_ref=x_ref.at[2 * p + theirs],
            dst_ref=sib.at[p],
            send_sem=to_sib.at[p],
            recv_sem=sib_in.at[p],
            device_id={"seq": sibling},
            device_id_type=MESH,
        )

    def rightward(p, target):
        return pltpu.make_async_remote_copy(
            src_ref=own.at[p],
            dst_ref=from_left.at[p],
            send_sem=to_right.at[p],
            recv_sem=right_in.at[p],
            device_id={"seq": target},
            device_id_type=MESH,
        )

    def leftward(p, target):
        return pltpu.make_async_remote_copy(
            src_ref=own.at[p],
            dst_ref=from_right.at[p],
            send_sem=to_left.at[p],
            recv_sem=left_in.at[p],
            device_id={"seq": target},
            device_id_type=MESH,
        )

    order = []
    for t in range(nc):
        for p in (nc - 1 - t, t):
            if p not in order:
                order.append(p)
    for p in order:
        to_sibling(p).start()
        load(p).start()

    f32 = jnp.float32
    for p in order:
        load(p).wait()
        to_sibling(p).wait_recv()

        @pl.when(p > q)
        def _(p=p):
            @pl.when(q > 0)
            def _():
                rightward(p, s).wait_recv()
                total = own[p].astype(f32) + sib[p].astype(f32) + from_left[p].astype(f32)
                own[p] = total.astype(own.dtype)

            @pl.when(q == 0)
            def _():
                own[p] = (own[p].astype(f32) + sib[p].astype(f32)).astype(own.dtype)

            rightward(p, s + 2).start()

        @pl.when(p < q)
        def _(p=p):
            @pl.when(q < nc - 1)
            def _():
                leftward(p, s).wait_recv()
                total = own[p].astype(f32) + sib[p].astype(f32) + from_right[p].astype(f32)
                own[p] = total.astype(own.dtype)

            @pl.when(q == nc - 1)
            def _():
                own[p] = (own[p].astype(f32) + sib[p].astype(f32)).astype(own.dtype)

            leftward(p, s - 2).start()

    o_ref[...] = own[q].astype(f32) + sib[q].astype(f32)

    @pl.when(q > 0)
    def _():
        rightward(q, s).wait_recv()
        o_ref[...] += from_left[q].astype(f32)

    @pl.when(q < nc - 1)
    def _():
        leftward(q, s).wait_recv()
        o_ref[...] += from_right[q].astype(f32)

    for t in range(1, n):
        small(t, lax.rem(s - t + n, n)).wait_recv()
        small(t, s).wait_send()
    for p in range(nc):
        to_sibling(p).wait_send()
        pl.when(p > q)(lambda p=p: rightward(p, s).wait_send())
        pl.when(p < q)(lambda p=p: leftward(p, s).wait_send())


def scatter_seq(n, x, extra, collective_id):
    nc = n // 2
    _, rows, cols = x.shape
    dma = pltpu.SemaphoreType.DMA
    buf = pltpu.VMEM((nc, rows, cols), x.dtype)
    return pl.pallas_call(
        functools.partial(scatter_kernel, n),
        out_shape=(
            jax.ShapeDtypeStruct((rows, cols), jnp.float32),
            jax.ShapeDtypeStruct((n, *extra.shape), extra.dtype),
        ),
        in_specs=[pl.BlockSpec(memory_space=pl.ANY), pl.BlockSpec(memory_space=pltpu.VMEM)],
        out_specs=(pl.BlockSpec(memory_space=pltpu.VMEM),) * 2,
        scratch_shapes=[buf] * 4 + [dma((nc,))] * 7 + [dma((n,))] * 2,
        compiler_params=pltpu.CompilerParams(
            collective_id=collective_id, has_side_effects=True, vmem_limit_bytes=32 << 20
        ),
        cost_estimate=pl.CostEstimate(flops=0, transcendentals=0, bytes_accessed=x.size * 2 * 20),
        name="scatter_seq",
    )(x, extra)

def near_first(i, q, nc):
    short = jnp.where(q <= nc - 1 - q, q, nc - 1 - q)
    far = jnp.where(q <= nc - 1 - q, i, nc - 1 - i)
    step = (i + 1) // 2
    near = q - step if i % 2 else q + step
    return jnp.where(i <= 2 * short, near, far)


def weights_kernel(n, rows, xa, wa, local, edge, a_in, a_sib_in, a_out, a_sib_out):
    nc, half = n // 2, rows // 2
    others = half - 1
    s, q, c = place_in_seq()
    sibling = s + 1 - 2 * c
    r = lax.axis_index("rows")
    a, b = r // 2, lax.rem(r, 2)
    b_row = r + 1 - 2 * b

    def a_row(k):
        return lax.rem(a + k + half, half) * 2 + b

    def diagonal(k):
        return lax.rem(a + k + half, half) * 2 + 1 - b

    barrier = pltpu.get_barrier_semaphore()
    for t in range(1, n):
        pl.semaphore_signal(
            barrier, inc=1, device_id=(r, lax.rem(s + t, n)), device_id_type=MESH
        )
    pl.semaphore_signal(barrier, inc=1, device_id=(b_row, s), device_id_type=MESH)
    for k in range(1, half):
        pl.semaphore_signal(barrier, inc=1, device_id=(a_row(k), s), device_id_type=MESH)
    pl.semaphore_wait(barrier, n - 1 + half)

    def remote(src, dst, send, recv, row, seq):
        return pltpu.make_async_remote_copy(
            src_ref=src, dst_ref=dst, send_sem=send, recv_sem=recv,
            device_id=(row, seq), device_id_type=MESH,
        )

    both, first, second = pl.ds(0, 2), pl.ds(0, 1), pl.ds(1, 1)
    LINE, FROM_B = 0, 1

    def from_a(k):
        return 1 + k

    def relay_b(k):
        return 1 + others + k

    def relay_a(k):
        return 1 + 2 * others + k

    def a_view(p, core, parts, row):
        return wa.at[parts, 2 * p + core, row]

    def content(kind):
        if kind == LINE:
            return both, r
        if kind == FROM_B:
            return both, b_row
        for k in range(1, half):
            if kind == from_a(k):
                return both, a_row(-k)
            if kind == relay_b(k):
                return second, diagonal(-k)
            if kind == relay_a(k):
                return first, diagonal(-k)

    kinds = 2 + 3 * others

    def a_send(p, parts, row, kind, target_row):
        return remote(
            a_view(p, c, parts, row), a_view(p, c, parts, row),
            a_out.at[p, kind], a_in.at[p, kind], target_row, s,
        )

    def a_arrival(p, kind):
        parts, row = content(kind)
        return a_send(p, parts, row, kind, r)

    def a_to_sibling(p, kind, core):
        parts, row = content(kind)
        return remote(
            a_view(p, core, parts, row), a_view(p, core, parts, row),
            a_sib_out.at[p, kind], a_sib_in.at[p, kind], r, sibling,
        )

    def line_send(p, src, sem, target):
        return remote(src, a_view(p, c, both, r), sem, a_in.at[p, LINE], r, target)

    own = xa.at[both, r]
    to_left = lambda: line_send(q, own, edge.at[0], s - 2)
    to_right = lambda: line_send(q, own, edge.at[1], s + 2)
    pl.when(q > 0)(lambda: to_left().start())
    pl.when(q < nc - 1)(lambda: to_right().start())
    order = [near_first(i, q, nc) for i in range(nc)]
    sib_a = lambda: remote(xa, wa.at[:, s], edge.at[2], edge.at[3], r, sibling)
    keep_a = pltpu.make_async_copy(xa, wa.at[:, s], local.at[0])
    sib_a().start()
    keep_a.start()

    def spread_a(p):
        a_send(p, both, r, FROM_B, b_row).start()
        for k in range(1, half):
            a_send(p, both, r, from_a(k), a_row(k)).start()

    for p in order[1:]:
        a_arrival(p, LINE).wait_recv()
        pl.when((p < q) & (q < nc - 1))(
            lambda p=p: line_send(p, a_view(p, c, both, r), a_out.at[p, LINE], s + 2).start()
        )
        pl.when((p > q) & (q > 0))(
            lambda p=p: line_send(p, a_view(p, c, both, r), a_out.at[p, LINE], s - 2).start()
        )
        spread_a(p)
        a_to_sibling(p, LINE, c).start()
    for p in order[1:]:
        a_arrival(p, FROM_B).wait_recv()
        for k in range(1, half):
            a_send(p, first, b_row, relay_a(k), a_row(k)).start()
        a_to_sibling(p, FROM_B, c).start()
        for k in range(1, half):
            a_arrival(p, from_a(k)).wait_recv()
            a_send(p, second, a_row(-k), relay_b(k), b_row).start()
            a_to_sibling(p, from_a(k), c).start()
    for p in order[1:]:
        for k in range(1, half):
            for kind in (relay_b(k), relay_a(k)):
                a_arrival(p, kind).wait_recv()
                a_to_sibling(p, kind, c).start()
    keep_a.wait()
    sib_a().wait()
    pl.when(q > 0)(lambda: to_left().wait_send())
    pl.when(q < nc - 1)(lambda: to_right().wait_send())
    for p in order[1:]:
        pl.when(((p < q) & (q < nc - 1)) | ((p > q) & (q > 0)))(
            lambda p=p: line_send(p, a_view(p, c, both, r), a_out.at[p, LINE], s).wait_send()
        )
        for kind in range(kinds):
            a_to_sibling(p, kind, c).wait_send()
            a_to_sibling(p, kind, 1 - c).wait_recv()
        a_send(p, both, r, FROM_B, b_row).wait_send()
        for k in range(1, half):
            a_send(p, both, r, from_a(k), r).wait_send()
            a_send(p, first, b_row, relay_a(k), r).wait_send()
            a_send(p, second, a_row(-k), relay_b(k), r).wait_send()


def gather_weights(n, rows, xa, collective_id):
    nc = n // 2
    block = xa.shape[1]
    part = block // rows
    xa = xa.reshape(2, rows, part, xa.shape[2])
    kinds = 2 + 3 * (rows // 2 - 1)
    dma = pltpu.SemaphoreType.DMA
    anywhere = pl.BlockSpec(memory_space=pl.ANY)
    wa = pl.pallas_call(
        functools.partial(weights_kernel, n, rows),
        out_shape=jax.ShapeDtypeStruct((2, n, rows, part, xa.shape[3]), xa.dtype),
        in_specs=[anywhere],
        out_specs=anywhere,
        scratch_shapes=[dma((1,)), dma((4,))] + [dma((nc, kinds))] * 4,
        compiler_params=pltpu.CompilerParams(collective_id=collective_id, has_side_effects=True),
        cost_estimate=pl.CostEstimate(
            flops=0, transcendentals=0, bytes_accessed=250 * 1024 * 1024
        ),
        name="gather_weights",
    )(xa)
    return wa.reshape(2, n * block, -1)

def swap_halves(x):
    return pltpu.roll(x.astype(jnp.float32), HEAD_DIM, 1)


def stack_heads(block):
    lane = lax.broadcasted_iota(jnp.int32, (block.shape[0], 128), 1)
    rows = []
    for h in range(8):
        pair = block[:, (h // 2) * 128 : (h // 2 + 1) * 128].astype(jnp.float32)
        if h % 2 != h // 4:
            pair = swap_halves(pair)
        keep = lane < HEAD_DIM if h // 4 == 0 else lane >= HEAD_DIM
        rows.append(jnp.where(keep, pair, 0.0).astype(jnp.bfloat16))
    return jnp.concatenate(rows, axis=0)


def unstack_heads(stacked, span):
    lane = lax.broadcasted_iota(jnp.int32, (span, 128), 1)
    pairs = []
    for t in range(4):
        first = stacked[2 * t * span : (2 * t + 1) * span]
        second = stacked[(2 * t + 1) * span : (2 * t + 2) * span]
        if t < 2:
            second = swap_halves(second)
        else:
            first = swap_halves(first)
        pairs.append(jnp.where(lane < HEAD_DIM, first, second))
    return jnp.concatenate(pairs, axis=1)


def attend_kernel(valid_ref, q_ref, k_ref, v_ref, o_ref, p_ref):
    span = q_ref.shape[1]
    keys = k_ref.shape[0] * span
    q8 = stack_heads(q_ref[0])
    k2 = k_ref[:, 0].reshape(keys, 128)
    v2 = v_ref[:, 0].reshape(keys, 128)
    scores = lax.dot_general(q8, k2, last_last, preferred_element_type=jnp.float32)
    scores = scores * HEAD_DIM**-0.5
    first_pos = lax.axis_index("seq") * span
    q_pos = first_pos + lax.broadcasted_iota(jnp.int32, (8, span, keys), 1).reshape(8 * span, keys)
    k_pos = lax.broadcasted_iota(jnp.int32, (8 * span, keys), 1)
    allowed = (k_pos <= q_pos) & (k_pos < valid_ref[pl.program_id(0)])
    scores = jnp.where(allowed, scores, -1e30)
    unscaled = jnp.exp(scores - jnp.max(scores, axis=1, keepdims=True))
    shares = unscaled * (1.0 / jnp.sum(unscaled, axis=1, keepdims=True))
    shares = shares.astype(jnp.bfloat16)
    p_ref[0, 0] = shares
    mixed = jnp.dot(shares, v2, preferred_element_type=jnp.float32)
    o_ref[0] = unstack_heads(mixed, span).astype(jnp.bfloat16)


def attend(q, kv, valid):
    pair, span, width = q.shape
    n, kv_width = kv.shape[0], kv.shape[3] // 2
    groups = kv_width // 128
    keys = n * span
    q_spec = pl.BlockSpec((1, span, 512), lambda p, j, *_: (p, 0, j))
    flops = 4 * pair * groups * 8 * span * keys * 128
    return pl.pallas_call(
        attend_kernel,
        out_shape=(
            jax.ShapeDtypeStruct(q.shape, jnp.bfloat16),
            jax.ShapeDtypeStruct((pair, groups, 8 * span, keys), jnp.bfloat16),
        ),
        grid_spec=pltpu.PrefetchScalarGridSpec(
            num_scalar_prefetch=1,
            grid=(pair, groups),
            in_specs=[
                q_spec,
                pl.BlockSpec((n, 1, span, 128), lambda p, j, *_: (0, p, 0, j)),
                pl.BlockSpec((n, 1, span, 128), lambda p, j, *_: (0, p, 0, groups + j)),
            ],
            out_specs=(
                q_spec,
                pl.BlockSpec((1, 1, 8 * span, keys), lambda p, j, *_: (p, j, 0, 0)),
            ),
        ),
        compiler_params=pltpu.CompilerParams(vmem_limit_bytes=40 << 20),
        cost_estimate=pl.CostEstimate(
            flops=flops, transcendentals=flops // 512, bytes_accessed=8 << 20
        ),
        name="attend",
    )(valid, q, kv, kv)


def attend_back_kernel(q_ref, k_ref, v_ref, p_ref, g_ref, gq_ref, gkv_ref):
    span = q_ref.shape[1]
    keys = k_ref.shape[0] * span
    q8 = stack_heads(q_ref[0])
    g8 = stack_heads(g_ref[0])
    k2 = k_ref[:, 0].reshape(keys, 128)
    v2 = v_ref[:, 0].reshape(keys, 128)
    low = p_ref[0, 0]
    shares = low.astype(jnp.float32)
    grad_shares = lax.dot_general(g8, v2, last_last, preferred_element_type=jnp.float32)
    weighted = shares * grad_shares
    centre = jnp.sum(weighted, axis=1, keepdims=True)
    grad_scores = (weighted - shares * centre).astype(jnp.bfloat16)
    gq = jnp.dot(grad_scores, k2, preferred_element_type=jnp.float32) * HEAD_DIM**-0.5
    gq_ref[0] = unstack_heads(gq, span).astype(jnp.bfloat16)
    gk = lax.dot_general(grad_scores, q8, first_first, preferred_element_type=jnp.float32)
    gv = lax.dot_general(low, g8, first_first, preferred_element_type=jnp.float32)
    both = jnp.concatenate([gk * HEAD_DIM**-0.5, gv], axis=1).astype(jnp.bfloat16)
    gkv_ref[:, 0] = both.reshape(gkv_ref.shape[0], span, 256)


def attend_back(q, kv, shares, g):
    pair, span, _ = q.shape
    n, kv_width = kv.shape[0], kv.shape[3] // 2
    groups = kv_width // 128
    keys = n * span
    q_spec = pl.BlockSpec((1, span, 512), lambda p, j: (p, 0, j))
    flops = 10 * pair * groups * 8 * span * keys * 128
    return pl.pallas_call(
        attend_back_kernel,
        out_shape=(
            jax.ShapeDtypeStruct(q.shape, jnp.bfloat16),
            jax.ShapeDtypeStruct(kv.shape, jnp.bfloat16),
        ),
        grid=(pair, groups),
        in_specs=[
            q_spec,
            pl.BlockSpec((n, 1, span, 128), lambda p, j: (0, p, 0, j)),
            pl.BlockSpec((n, 1, span, 128), lambda p, j: (0, p, 0, groups + j)),
            pl.BlockSpec((1, 1, 8 * span, keys), lambda p, j: (p, j, 0, 0)),
            q_spec,
        ],
        out_specs=(
            q_spec,
            pl.BlockSpec((n, 1, span, 256), lambda p, j: (0, p, 0, j)),
        ),
        compiler_params=pltpu.CompilerParams(vmem_limit_bytes=40 << 20),
        cost_estimate=pl.CostEstimate(flops=flops, transcendentals=0, bytes_accessed=8 << 20),
        name="attend_back",
    )(q, kv, kv, shares, g)

def by_distance(i, q, nc):
    room = nc - 1 - q
    left_half = q <= room
    short = jnp.where(left_half, q, room)
    far = jnp.where(left_half, i, nc - 1 - i)
    step = (i + 1) // 2
    near = jnp.where(lax.rem(i, 2) == 1, q - step, q + step)
    return jnp.where(i <= 2 * short, near, far)


def ffn_kernel(n, rows, pieces, u_hbm, gy_hbm, wd_hbm, a_ref, b_ref, m_ref, ad_ref, bd_ref, md_ref, nd_ref,
               in_ref, down_hbm, ga_ref, gb_ref, gm_ref, norm_ref, gad_ref, gbd_ref, gmd_ref,
               w_parts, wd, u, gy, down, own, theirs, sib, from_left, from_right, ratio, cross,
               w_sem, load_sem, down_sem, to_sib, sib_in, to_right, right_in, to_left, left_in):
    nc = n // 2
    f32, low = jnp.float32, jnp.bfloat16
    s, q, c = place_in_seq()
    tokens = own.shape[1]

    weights = [pltpu.make_async_copy(wd_hbm, wd, w_sem.at[0])]
    for src, g, hold in place_pieces(rows, pieces):
        weights.append(
            pltpu.make_async_copy(src, w_parts.at[g, :, hold], w_sem.at[len(weights)])
        )
    for cp in weights:
        cp.start()

    def loads(i):
        p = by_distance(nc - 1 - i, q, nc)
        slot = lax.rem(i, 2)
        pair = pl.ds(2 * p, 2)
        return (
            pltpu.make_async_copy(u_hbm.at[pair], u.at[slot], load_sem.at[0, slot]),
            pltpu.make_async_copy(gy_hbm.at[pair], gy.at[slot], load_sem.at[1, slot]),
        )

    for cp in loads(0):
        cp.start()
    sibling = greet(nc, q, s)

    def to_sibling(p):
        return pltpu.make_async_remote_copy(
            src_ref=theirs.at[p], dst_ref=sib.at[p], send_sem=to_sib.at[p], recv_sem=sib_in.at[p],
            device_id={"seq": sibling}, device_id_type=MESH,
        )

    def rightward(p, target):
        return pltpu.make_async_remote_copy(
            src_ref=own.at[p], dst_ref=from_left.at[p], send_sem=to_right.at[p], recv_sem=right_in.at[p],
            device_id={"seq": target}, device_id_type=MESH,
        )

    def leftward(p, target):
        return pltpu.make_async_remote_copy(
            src_ref=own.at[p], dst_ref=from_right.at[p], send_sem=to_left.at[p], recv_sem=left_in.at[p],
            device_id={"seq": target}, device_id_type=MESH,
        )

    def down_out(p):
        return pltpu.make_async_copy(
            down.at[lax.rem(p, 2)], down_hbm.at[pl.ds(2 * p, 2)], down_sem.at[lax.rem(p, 2)]
        )

    def pass_on(p):
        to_sibling(p).wait_recv()

        @pl.when(p > q)
        def _():
            @pl.when(q > 0)
            def _():
                rightward(p, s).wait_recv()
                own[p] = (own[p].astype(f32) + sib[p].astype(f32) + from_left[p].astype(f32)).astype(low)

            @pl.when(q == 0)
            def _():
                own[p] = (own[p].astype(f32) + sib[p].astype(f32)).astype(low)

            rightward(p, s + 2).start()

        @pl.when(p < q)
        def _():
            @pl.when(q < nc - 1)
            def _():
                leftward(p, s).wait_recv()
                own[p] = (own[p].astype(f32) + sib[p].astype(f32) + from_right[p].astype(f32)).astype(low)

            @pl.when(q == nc - 1)
            def _():
                own[p] = (own[p].astype(f32) + sib[p].astype(f32)).astype(low)

            leftward(p, s - 2).start()

    def starts_flow(p):
        return ((p > q) & (q == 0)) | ((p < q) & (q == nc - 1))

    w = [w_parts.at[g] for g in range(2)]
    width = u_hbm.shape[2]
    weight = lambda g: w[g][...].reshape(width, -1)
    bd = bd_ref[...].astype(low)
    ad = ad_ref[...].astype(low)
    a = [a_ref[g].astype(low) for g in range(2)]
    b = [b_ref[g].astype(low) for g in range(2)]
    for cp in weights:
        cp.wait()
    for g in range(2):
        norm, cr = column_norms(weight(g), a[g], b[g].astype(f32), dot_f32(a[g], weight(g)))
        norm_ref[g] = norm
        cross[g] = cr
        ratio[g] = m_ref[g] / norm
    for ref in (ga_ref, gb_ref, gm_ref, gad_ref, gbd_ref, gmd_ref):
        ref[...] = jnp.zeros_like(ref)
    ratio_d = md_ref[...] / nd_ref[...]

    def step(i, carry):
        p = by_distance(nc - 1 - i, q, nc)
        slot = lax.rem(i, 2)
        for cp in loads(i):
            cp.wait()

        @pl.when(i + 1 < nc)
        def _():
            for cp in loads(i + 1):
                cp.start()

        x = u[slot].reshape(2 * tokens, -1)
        upstream = gy[slot].reshape(2 * tokens, -1).astype(f32)
        gb_d = (upstream * ratio_d).astype(low)
        gi_d = (SCALE * dot_nt(gb_d, bd)).astype(low)
        gh = dot_nt(gb_d, wd[...]) + dot_f32(gi_d, ad)
        inner = [dot_nt(x, a[g]).astype(low) for g in range(2)]
        before = [dot_f32(x, weight(g)) + SCALE * dot_f32(inner[g], b[g]) for g in range(2)]
        gate = before[0] * ratio[0]
        lift = before[1] * ratio[1]
        sig = 1.0 / (1.0 + jnp.exp(-gate))
        silu = gate * sig
        hidden = (silu * lift).astype(low)
        grads = [gh * lift * sig * (1.0 + gate * (1.0 - sig)), gh * silu]
        gb = [(grads[g] * ratio[g]).astype(low) for g in range(2)]
        gi = [(SCALE * dot_nt(gb[g], b[g])).astype(low) for g in range(2)]
        back = dot_nt(gb[0], weight(0)) + dot_nt(gb[1], weight(1)) + dot_f32(gi[0], a[0]) + dot_f32(gi[1], a[1])
        back = back.astype(low).reshape(2, tokens, -1)
        first, second = back[0], back[1]

        @pl.when(c == 0)
        def _():
            own[p] = first
            theirs[p] = second

        @pl.when(c == 1)
        def _():
            own[p] = second
            theirs[p] = first

        to_sibling(p).start()
        inner_d = dot_nt(hidden, ad).astype(low)
        part = dot_f32(hidden, wd[...]) + SCALE * dot_f32(inner_d, bd)

        @pl.when(i >= 2)
        def _():
            down_out(slot).wait()

        down[slot] = part.astype(low).reshape(2, tokens, -1)
        pltpu.make_async_copy(down.at[slot], down_hbm.at[pl.ds(2 * p, 2)], down_sem.at[slot]).start()
        gmd_ref[...] += jnp.sum(upstream * part, axis=0, keepdims=True)
        gad_ref[...] += dot_tn(gi_d, hidden)
        gbd_ref[...] += SCALE * dot_tn(inner_d, gb_d)
        for g in range(2):
            gm_ref[g] += jnp.sum(grads[g] * before[g], axis=0, keepdims=True)
            ga_ref[g] += dot_tn(gi[g], x)
            gb_ref[g] += SCALE * dot_tn(inner[g], gb[g])

        pl.when(starts_flow(p))(lambda: pass_on(p))
        last = by_distance(nc - i, q, nc)
        pl.when((i > 0) & jnp.logical_not(starts_flow(last)))(lambda: pass_on(last))
        return carry

    lax.fori_loop(0, nc, step, 0)

    gmd_ref[...] = gmd_ref[...] / nd_ref[...]
    for g in range(2):
        norm = norm_ref[g]
        gm = gm_ref[g] / norm
        gm_ref[g] = gm
        col = -gm * m_ref[g] / (norm * norm)
        b_wide = b[g].astype(f32)
        weighted = b_wide * col
        tail = lax.dot_general(
            weighted, b_wide, (((1,), (1,)), ((), ())), precision=highest, preferred_element_type=f32
        )
        spread = dot_nt(weighted.astype(low), weight(g)) + SCALE * jnp.dot(
            tail, a[g].astype(f32), precision=highest, preferred_element_type=f32
        )
        ga_ref[g] += SCALE * spread
        gb_ref[g] += SCALE * col * cross[g]

    to_sibling(q).wait_recv()
    in_ref[...] = own[q].astype(f32) + sib[q].astype(f32)

    @pl.when(q > 0)
    def _():
        rightward(q, s).wait_recv()
        in_ref[...] += from_left[q].astype(f32)

    @pl.when(q < nc - 1)
    def _():
        leftward(q, s).wait_recv()
        in_ref[...] += from_right[q].astype(f32)

    for i in range(min(2, nc)):
        pltpu.make_async_copy(down.at[i], down_hbm.at[pl.ds(0, 2)], down_sem.at[i]).wait()
    for p in range(nc):
        to_sibling(p).wait_send()
        pl.when(p > q)(lambda p=p: rightward(p, s).wait_send())
        pl.when(p < q)(lambda p=p: leftward(p, s).wait_send())


def reshard_units(gate_up, n, rows):
    half = rows // 2
    _, block, units_all = gate_up.shape
    part, units = block // rows, units_all // n
    r = lax.axis_index("rows")
    mine = lax.dynamic_slice_in_dim(gate_up, r * part, part, 1)
    mine = mine.reshape(2, part, n, units).transpose(2, 0, 1, 3)
    mine = lax.all_to_all(mine, "seq", split_axis=0, concat_axis=0, tiled=True)
    swap = [(i, i ^ 1) for i in range(rows)]
    turns = [[(i, (i + 2 * k) % rows) for i in range(rows)] for k in range(1, half)]
    from_b = lax.ppermute(mine, "rows", swap)
    from_a = [lax.ppermute(mine, "rows", turn) for turn in turns]
    pieces = [mine, from_b, *from_a]
    for k in range(1, half):
        pieces.append(lax.ppermute(from_b[:, 0], "rows", turns[k - 1]))
        pieces.append(lax.ppermute(from_a[k - 1][:, 1], "rows", swap))
    return pieces


def place_pieces(rows, pieces):
    half = rows // 2
    r = lax.axis_index("rows")
    a, b = r // 2, lax.rem(r, 2)
    turned = lambda k: 2 * lax.rem(a - k + half, half)
    holds = [r, 2 * a + 1 - b] + [turned(k) + b for k in range(1, half)]
    out = [(pieces[i].at[:, g], g, hold) for i, hold in enumerate(holds) for g in range(2)]
    for k in range(1, half):
        for g in range(2):
            out.append((pieces[half + 1 + 2 * (k - 1) + g], g, turned(k) + 1 - b))
    return out


def feed_forward(n, rows, pieces, u, gy, wd, a, b, m, ad, bd, md, nd, collective_id):
    nc = n // 2
    _, tokens, width = u.shape
    units = wd.shape[0]
    f32, low = jnp.float32, jnp.bfloat16
    shape = jax.ShapeDtypeStruct
    vmem = pl.BlockSpec(memory_space=pltpu.VMEM)
    hbm = pl.BlockSpec(memory_space=pl.ANY)
    dma = pltpu.SemaphoreType.DMA
    line = pltpu.VMEM((nc, tokens, width), low)
    pair = pltpu.VMEM((2, 2, tokens, width), low)
    part = pieces[0].shape[2]
    count = len(pieces)

    def kernel(*refs):
        ffn_kernel(n, rows, refs[:count], *refs[count:])

    return pl.pallas_call(
        kernel,
        out_shape=(
            shape((tokens, width), f32),
            shape((n, tokens, width), low),
            shape((2, 16, width), f32),
            shape((2, 16, units), f32),
            shape((2, 1, units), f32),
            shape((2, 1, units), f32),
            shape((16, units), f32),
            shape((16, width), f32),
            shape((1, width), f32),
        ),
        in_specs=[hbm] * (count + 3) + [vmem] * 7,
        out_specs=(vmem, hbm) + (vmem,) * 7,
        scratch_shapes=[
            pltpu.VMEM((2, n, rows, part, units), low),
            pltpu.VMEM((units, width), low),
            pair, pair, pair,
            line, line, line, line, line,
            pltpu.VMEM((2, 1, units), f32),
            pltpu.VMEM((2, 16, units), f32),
            dma((1 + 2 * rows,)), dma((2, 2)), dma((2,)),
        ] + [dma((nc,))] * 6,
        compiler_params=pltpu.CompilerParams(
            collective_id=collective_id, has_side_effects=True, vmem_limit_bytes=60 << 20
        ),
        cost_estimate=pl.CostEstimate(
            flops=12 * n * tokens * width * units, transcendentals=n * tokens * units,
            bytes_accessed=32 << 20,
        ),
        name="feed_forward",
    )(*pieces, u, gy, wd, a, b, m, ad, bd, md, nd)

def square_terms(weight, a_low, b_low):
    cross = dot_f32(a_low, weight)
    squares = jnp.sum(jnp.square(weight.astype(jnp.float32)), axis=0, keepdims=True)
    return squares + 2.0 * SCALE * jnp.sum(b_low.astype(jnp.float32) * cross, axis=0, keepdims=True), cross


def drift_stats(magnitude_vector, norms):
    drift = jnp.sqrt(jnp.mean(jnp.square(magnitude_vector - norms))) / jnp.sqrt(
        jnp.mean(jnp.square(magnitude_vector)) + 1e-06
    )
    return jnp.stack([drift, jnp.mean(norms)])


def local(
    layer_input,
    output_gradient,
    norm_gain_vectors,
    query_output_frozen,
    key_value_frozen,
    gate_up_frozen,
    down_frozen_weight,
    attention_adapter_a,
    query_output_adapter_b,
    key_value_adapter_b,
    query_magnitude,
    key_value_magnitude,
    output_magnitude,
    gate_up_adapter_a,
    gate_up_adapter_b,
    gate_up_magnitude,
    down_adapter_a,
    down_adapter_b,
    down_magnitude,
    prompt_length_list,
    response_length_list,
):
    pair_rows, span_len, model_width = layer_input.shape
    token_count = pair_rows * span_len
    kv_width = KV_HEADS * HEAD_DIM
    qkv_width = model_width + 2 * kv_width
    seq_size = lax.axis_size("seq")
    rows_size = lax.axis_size("rows")
    seq_index = lax.axis_index("seq")
    first_member = (seq_index == 0).astype(jnp.float32)
    low, f32 = jnp.bfloat16, jnp.float32
    rank = ADAPTER_RANK
    slice_units = down_frozen_weight.shape[0]
    start = seq_index * slice_units

    pieces = reshard_units(gate_up_frozen, seq_size, rows_size)
    packed = jnp.stack(
        [
            jnp.concatenate([query_output_frozen[0], key_value_frozen[0]], axis=1),
            jnp.concatenate([key_value_frozen[1], query_output_frozen[1]], axis=1),
        ]
    )
    weights = gather_weights(seq_size, rows_size, packed, 1)
    weights, grad_out_rows = lax.optimization_barrier(
        (weights, output_gradient.reshape(token_count, model_width))
    )
    gy_all = lax.all_gather(grad_out_rows, "seq", axis=0, tiled=False)

    b_attn = jnp.concatenate(
        [
            query_output_adapter_b[0],
            key_value_adapter_b[0],
            key_value_adapter_b[1],
            query_output_adapter_b[1],
        ],
        axis=1,
    )
    m_attn = jnp.concatenate(
        [query_magnitude, key_value_magnitude[0], key_value_magnitude[1], output_magnitude]
    )[None]
    b_gu = lax.dynamic_slice_in_dim(gate_up_adapter_b, start, slice_units, 2)
    m_gu = lax.dynamic_slice_in_dim(gate_up_magnitude, start, slice_units, 1)[:, None]
    a_d = lax.dynamic_slice_in_dim(down_adapter_a, start, slice_units, 1)
    b_d = down_adapter_b.astype(low)
    m_d = down_magnitude[None]
    sq_d, cross_d = square_terms(down_frozen_weight, a_d.astype(low), b_d)

    positions = seq_index * span_len + jnp.arange(span_len, dtype=jnp.int32)
    half_dim = HEAD_DIM // 2
    frequency = 500000.0 ** (-(jnp.arange(half_dim, dtype=f32) * 2.0) / HEAD_DIM)
    angles = positions.astype(f32)[:, None] * frequency[None, :]
    cosine = jnp.tile(jnp.cos(angles), (pair_rows, 4))
    sine = jnp.tile(jnp.sin(angles), (pair_rows, 4))
    valid_len = prompt_length_list[0] + response_length_list

    x = layer_input.reshape(token_count, model_width)
    gain_attn, gain_ffn = norm_gain_vectors[:1], norm_gain_vectors[1:]
    u1, before_qkv, q, kv, n_attn, cross_attn = project_qkv(
        x, gain_attn, attention_adapter_a, weights, b_attn, m_attn, cosine, sine
    )
    kv_all, sq_all = gather_seq(seq_size, [kv, sq_d], 2)
    kv_all = kv_all.reshape(seq_size, pair_rows, span_len, 2 * kv_width)
    q = q.reshape(pair_rows, span_len, model_width)
    att, shares = attend(q, kv_all, valid_len)
    att = att.reshape(token_count, model_width)
    b_o, m_o, n_o = b_attn[:, qkv_width:], m_attn[:, qkv_width:], n_attn[:, qkv_width:]
    a_o = attention_adapter_a[3]
    before_o, x1, u2 = project_out(att, a_o, weights, b_o, m_o, n_o, x, gain_ffn)

    (u2_all,) = gather_seq(seq_size, [u2], 3)
    a_d_wide, b_d_wide = down_adapter_a.astype(low).astype(f32), b_d.astype(f32)
    gram_d = jnp.dot(
        jnp.dot(a_d_wide, a_d_wide.T, precision=highest), b_d_wide, precision=highest
    )
    sq_d = jnp.sum(sq_all, axis=0) + SCALE * SCALE * jnp.sum(
        b_d_wide * gram_d, axis=0, keepdims=True
    )
    n_d = jnp.sqrt(sq_d + 1e-06)
    in_grad, down_parts, ga_gu, gb_gu, gm_gu, n_gu, ga_d, gb_d, gm_d = feed_forward(
        seq_size, rows_size, pieces, u2_all, gy_all, down_frozen_weight, gate_up_adapter_a, b_gu,
        m_gu, a_d, down_adapter_b, m_d, n_d, 4,
    )
    before_d = lax.psum_scatter(
        down_parts.reshape(seq_size * token_count, model_width), "seq", scatter_dimension=0,
        tiled=True,
    )
    layer_result = (x1 + before_d.astype(f32) * (m_d / n_d)).astype(low)

    gx1, grad_att, ga_o, gb_o, gm_o = out_back(
        in_grad, x1, gain_ffn, grad_out_rows, before_o, att, a_o, b_o, m_o, n_o,
        cross_attn[:, qkv_width:], weights,
    )
    gq, gkv = attend_back(q, kv_all, shares, grad_att.reshape(q.shape))
    gkv, gm_d_all = scatter_seq(
        seq_size, gkv.reshape(seq_size, token_count, 2 * kv_width), gm_d, 5
    )
    grad_inputs, ga_qkv, gb_qkv, gm_qkv = qkv_back(
        gq.reshape(token_count, model_width), gkv, cosine, sine, before_qkv, u1,
        attention_adapter_a[:3], b_attn[:, :qkv_width], m_attn[:, :qkv_width],
        n_attn[:, :qkv_width], cross_attn[:, :qkv_width], x, gain_attn, gx1, weights,
    )

    c_d = -jnp.sum(gm_d_all, axis=0) * m_d / (n_d * n_d)
    weighted = b_d_wide * c_d
    tail = lax.dot_general(weighted, b_d_wide, last_last, precision=highest)
    spread = dot_nt(weighted.astype(low), down_frozen_weight) + SCALE * jnp.dot(
        tail, a_d.astype(low).astype(f32), precision=highest
    )
    ga_d = ga_d + SCALE * spread
    gb_d = gb_d + SCALE * c_d * (cross_d + first_member * SCALE * gram_d)

    k_end = model_width + kv_width
    full_units = gate_up_magnitude.shape[1]

    def place(piece, axis):
        shape = list(piece.shape)
        shape[axis] = full_units
        return lax.dynamic_update_slice_in_dim(jnp.zeros(shape, piece.dtype), piece, start, axis)

    summed = lax.psum(
        (
            jnp.concatenate([ga_qkv, ga_o[None]], axis=0),
            jnp.stack([gb_qkv[:, :model_width], gb_o]),
            jnp.stack([gb_qkv[:, model_width:k_end], gb_qkv[:, k_end:]]),
            gm_qkv[0, :model_width],
            gm_qkv[0, model_width:].reshape(2, kv_width),
            gm_o[0],
            ga_gu,
            place(gb_gu, 2),
            place(gm_gu[:, 0], 1),
            place(ga_d, 1),
            gb_d,
            gm_d[0],
        ),
        ("rows", "seq"),
    )
    norms_gu = lax.all_gather(n_gu[:, 0], "seq", axis=1, tiled=True)
    stats = jnp.stack(
        [
            drift_stats(query_magnitude, n_attn[0, :model_width]),
            drift_stats(key_value_magnitude[0], n_attn[0, model_width:k_end]),
            drift_stats(key_value_magnitude[1], n_attn[0, k_end:qkv_width]),
            drift_stats(output_magnitude, n_o[0]),
            drift_stats(gate_up_magnitude[0], norms_gu[0]),
            drift_stats(gate_up_magnitude[1], norms_gu[1]),
            drift_stats(down_magnitude, n_d[0]),
        ]
    )
    shape = (pair_rows, span_len, model_width)
    return (layer_result.reshape(shape), grad_inputs.reshape(shape), *summed, stats)

def solution(mesh):
    return jax.shard_map(
        local,
        mesh=mesh,
        in_specs=(
            P("rows", "seq", None),
            P("rows", "seq", None),
            P(),
            P(None, "seq", None),
            P(None, "seq", None),
            P(None, "seq", None),
            P("seq", None),
            P(),
            P(),
            P(),
            P(),
            P(),
            P(),
            P(),
            P(),
            P(),
            P(),
            P(),
            P(),
            P("rows"),
            P("rows"),
        ),
        out_specs=(
            P("rows", "seq", None),
            P("rows", "seq", None),
            P(),
            P(),
            P(),
            P(),
            P(),
            P(),
            P(),
            P(),
            P(),
            P(),
            P(),
            P(),
            P(),
        ),
        check_vma=False,
    )
```

```python
import functools

import jax
import jax.numpy as jnp
from jax import lax
from jax.experimental import pallas as pl
from jax.experimental.pallas import tpu as pltpu
from jax.sharding import PartitionSpec as P

HEADS = 32
KV_HEADS = 8
HEAD_DIM = 64
ADAPTER_RANK = 16
ALPHA = 32
SCALE = ALPHA / ADAPTER_RANK
TILE = 512

highest = lax.Precision.HIGHEST
last_last = (((1,), (1,)), ((), ()))
first_first = (((0,), (0,)), ((), ()))

def dot_f32(a, b):
    return jnp.dot(a, b, preferred_element_type=jnp.float32)


def dot_nt(a, b):
    return lax.dot_general(a, b, last_last, preferred_element_type=jnp.float32)


def dot_tn(a, b):
    return lax.dot_general(a, b, first_first, preferred_element_type=jnp.float32)


def unit_rms(v):
    return lax.rsqrt(jnp.mean(v * v, axis=-1, keepdims=True) + 1e-05)


def rms_back(v, gain, upstream):
    r = unit_rms(v)
    scaled = gain * upstream
    return r * scaled - v * (r * r * r) * jnp.mean(scaled * v, axis=-1, keepdims=True)


def turn(z, cosine, sine):
    width = z.shape[1]
    lane = lax.broadcasted_iota(jnp.int32, z.shape, 1)
    half = HEAD_DIM // 2
    other = jnp.where(
        lax.rem(lane, HEAD_DIM) < half, -pltpu.roll(z, width - half, 1), pltpu.roll(z, half, 1)
    )
    copies = width // cosine.shape[1]
    return z * jnp.tile(cosine, (1, copies)) + other * jnp.tile(sine, (1, copies))


def column_norms(w, a, b_wide, cross):
    ones = jnp.ones((16, w.shape[0]), jnp.bfloat16)
    squares = dot_f32(ones, w * w)[:1]
    gram_b = jnp.dot(dot_nt(a, a), b_wide, precision=highest, preferred_element_type=jnp.float32)
    squares = squares + 2.0 * SCALE * jnp.sum(b_wide * cross, axis=0, keepdims=True)
    squares = squares + SCALE * SCALE * jnp.sum(b_wide * gram_b, axis=0, keepdims=True)
    return jnp.sqrt(squares + 1e-06), cross + SCALE * gram_b


def project_kernel(kv_tiles, x_ref, gain_ref, a_ref, w_ref, b_ref, m_ref, cos_ref, sin_ref,
                   u_ref, before_ref, q_ref, kv_ref, n_ref, cross_ref):
    j = pl.program_id(0)
    q_tiles = kv_tiles[0]

    @pl.when(j == 0)
    def _():
        v = x_ref[...].astype(jnp.float32)
        u_ref[...] = (v * unit_rms(v) * gain_ref[...]).astype(jnp.bfloat16)

    a = a_ref[0].astype(jnp.bfloat16)
    b = b_ref[...].astype(jnp.bfloat16)
    b_wide = b.astype(jnp.float32)
    w = w_ref[0]
    rows = u_ref.shape[0]

    @pl.when(j < kv_tiles[1])
    def _():
        both = dot_f32(jnp.concatenate([u_ref[...], a], axis=0), w)
        norm, cross = column_norms(w, a, b_wide, both[rows:])
        n_ref[...] = norm
        cross_ref[...] = cross
        inner = dot_nt(u_ref[...], a).astype(jnp.bfloat16)
        before = both[:rows] + SCALE * dot_f32(inner, b)
        before_ref[...] = before
        y = before * (m_ref[...] / norm)

        @pl.when(j < q_tiles)
        def _():
            q_ref[...] = turn(y, cos_ref[...], sin_ref[...]).astype(jnp.bfloat16)

        @pl.when(j == q_tiles)
        def _():
            kv_ref[...] = turn(y, cos_ref[...], sin_ref[...]).astype(jnp.bfloat16)

        @pl.when(j > q_tiles)
        def _():
            kv_ref[...] = y.astype(jnp.bfloat16)

    @pl.when(j >= kv_tiles[1])
    def _():
        norm, cross = column_norms(w, a, b_wide, dot_f32(a, w))
        n_ref[...] = norm
        cross_ref[...] = cross


def project_qkv(x, gain, a, weights, b, m, cosine, sine):
    rows, width = x.shape
    cols = b.shape[1]
    per_half = weights.shape[2] // TILE
    q_tiles = width // TILE
    k_cols = weights.shape[2] - width
    kv_tiles = (q_tiles, q_tiles + 2 * k_cols // TILE)
    last = kv_tiles[1] - 1
    full = lambda shape: pl.BlockSpec(shape, lambda j: (0,) * len(shape))
    col = lambda height: pl.BlockSpec((height, TILE), lambda j: (0, j))
    which = lambda j: jnp.where(j < q_tiles, 0, jnp.where(j > last, 3, 1 + j - q_tiles))
    f32, low = jnp.float32, jnp.bfloat16
    return pl.pallas_call(
        functools.partial(project_kernel, kv_tiles),
        out_shape=(
            jax.ShapeDtypeStruct((rows, width), low),
            jax.ShapeDtypeStruct((rows, width + 2 * k_cols), f32),
            jax.ShapeDtypeStruct((rows, width), low),
            jax.ShapeDtypeStruct((rows, 2 * k_cols), low),
            jax.ShapeDtypeStruct((1, cols), f32),
            jax.ShapeDtypeStruct((16, cols), f32),
        ),
        grid=(cols // TILE,),
        in_specs=[
            full((rows, width)),
            full((1, width)),
            pl.BlockSpec((1, 16, width), lambda j: (which(j), 0, 0)),
            pl.BlockSpec((1, width, TILE), lambda j: (j // per_half, 0, j % per_half)),
            col(16),
            col(1),
            full(cosine.shape),
            full(sine.shape),
        ],
        out_specs=(
            full((rows, width)),
            pl.BlockSpec((rows, TILE), lambda j: (0, jnp.minimum(j, last))),
            pl.BlockSpec((rows, TILE), lambda j: (0, jnp.minimum(j, q_tiles - 1))),
            pl.BlockSpec((rows, TILE), lambda j: (0, jnp.clip(j - q_tiles, 0, last - q_tiles))),
            col(1),
            col(16),
        ),
        compiler_params=pltpu.CompilerParams(vmem_limit_bytes=40 << 20),
        cost_estimate=pl.CostEstimate(
            flops=2 * rows * width * cols, transcendentals=0, bytes_accessed=2 * width * cols
        ),
        name="project_qkv",
    )(x, gain, a, weights, b, m, cosine, sine)


def out_kernel(att_ref, a_ref, w_ref, b_ref, m_ref, n_ref, x_ref, gain_ref, before_ref, x1_ref, u2_ref):
    t = pl.program_id(0)
    a = a_ref[...].astype(jnp.bfloat16)
    b = b_ref[...].astype(jnp.bfloat16)
    inner = dot_nt(att_ref[...], a).astype(jnp.bfloat16)
    before = dot_f32(att_ref[...], w_ref[0]) + SCALE * dot_f32(inner, b)
    before_ref[...] = before
    x1_ref[:, pl.ds(pl.multiple_of(t * TILE, TILE), TILE)] = (
        x_ref[...].astype(jnp.float32) + before * (m_ref[...] / n_ref[...])
    )

    @pl.when(t == pl.num_programs(0) - 1)
    def _():
        v = x1_ref[...]
        u2_ref[...] = (v * unit_rms(v) * gain_ref[...]).astype(jnp.bfloat16)


def project_out(att, a, weights, b, m, norms, x, gain):
    rows, width = att.shape
    tiles = width // TILE
    skip = (weights.shape[2] - width) // TILE
    full = lambda shape: pl.BlockSpec(shape, lambda t: (0,) * len(shape))
    col = lambda height: pl.BlockSpec((height, TILE), lambda t: (0, t))
    f32 = jnp.float32
    return pl.pallas_call(
        out_kernel,
        out_shape=(
            jax.ShapeDtypeStruct((rows, width), f32),
            jax.ShapeDtypeStruct((rows, width), f32),
            jax.ShapeDtypeStruct((rows, width), jnp.bfloat16),
        ),
        grid=(tiles,),
        in_specs=[
            full((rows, width)),
            full((16, width)),
            pl.BlockSpec((1, width, TILE), lambda t: (1, 0, skip + t)),
            col(16),
            col(1),
            col(1),
            col(rows),
            full((1, width)),
        ],
        out_specs=(col(rows), full((rows, width)), full((rows, width))),
        compiler_params=pltpu.CompilerParams(vmem_limit_bytes=40 << 20),
        cost_estimate=pl.CostEstimate(
            flops=2 * rows * width * width, transcendentals=0, bytes_accessed=2 * width * width
        ),
        name="project_out",
    )(att, a, weights, b, m, norms, x, gain)


def out_back_kernel(in_ref, x1_ref, gain_ref, gy_ref, before_ref, att_ref, a_ref, b_ref, m_ref, n_ref, cross_ref,
                    w_ref, gx_ref, gatt_ref, ga_ref, gb_ref, gm_ref, lhs, gi, tail):
    t = pl.program_id(0)
    rows, width = gx_ref.shape
    low = jnp.bfloat16
    a = a_ref[...].astype(low)

    @pl.when(t == 0)
    def _():
        gx = gy_ref[...].astype(jnp.float32) + rms_back(x1_ref[...], gain_ref[...], in_ref[...])
        gx_ref[...] = gx
        norm = n_ref[...]
        gb = (gx * (m_ref[...] / norm)).astype(low)
        lhs[:rows] = gb
        b = b_ref[...].astype(low)
        b_wide = b.astype(jnp.float32)
        gi[...] = (SCALE * dot_nt(gb, b)).astype(low)
        gm = jnp.sum(gx * before_ref[...], axis=0, keepdims=True) / norm
        gm_ref[...] = gm
        c = -gm * m_ref[...] / (norm * norm)
        weighted = b_wide * c
        lhs[rows:] = weighted.astype(low)
        tail[...] = lax.dot_general(
            weighted, b_wide, last_last, precision=highest, preferred_element_type=jnp.float32
        )
        inner = dot_nt(att_ref[...], a).astype(low)
        gb_ref[...] = SCALE * dot_tn(inner, gb) + SCALE * c * cross_ref[...]

    span = pl.ds(pl.multiple_of(t * TILE, TILE), TILE)
    a_tile = a_ref[:, span].astype(low)
    gi_low = gi[...]
    back = dot_nt(lhs[...], w_ref[0, :, w_ref.shape[2] - width :])
    gatt_ref[...] = (back[:rows] + dot_f32(gi_low, a_tile)).astype(low)
    spread = back[rows:] + SCALE * jnp.dot(
        tail[...], a_tile.astype(jnp.float32), precision=highest, preferred_element_type=jnp.float32
    )
    ga_ref[...] = dot_tn(gi_low, att_ref[:, span]) + SCALE * spread


def out_back(in_grad, x1, gain, gy, before, att, a, b, m, norms, cross, weights):
    rows, width = x1.shape
    tiles = width // TILE
    full = lambda shape: pl.BlockSpec(shape, lambda t: (0,) * len(shape))
    col = lambda height: pl.BlockSpec((height, TILE), lambda t: (0, t))
    f32, low = jnp.float32, jnp.bfloat16
    wide = full((rows, width))
    return pl.pallas_call(
        out_back_kernel,
        out_shape=(
            jax.ShapeDtypeStruct((rows, width), f32),
            jax.ShapeDtypeStruct((rows, width), low),
            jax.ShapeDtypeStruct((16, width), f32),
            jax.ShapeDtypeStruct((16, width), f32),
            jax.ShapeDtypeStruct((1, width), f32),
        ),
        grid=(tiles,),
        in_specs=[wide, wide, full((1, width)), wide, wide, wide, full((16, width)), full((16, width)),
                  full((1, width)), full((1, width)), full((16, width)),
                  pl.BlockSpec((1, TILE, weights.shape[2]), lambda t: (1, t, 0))],
        out_specs=(wide, col(rows), col(16), full((16, width)), full((1, width))),
        scratch_shapes=[
            pltpu.VMEM((rows + 16, width), low),
            pltpu.VMEM((rows, 16), low),
            pltpu.VMEM((16, 16), f32),
        ],
        compiler_params=pltpu.CompilerParams(vmem_limit_bytes=48 << 20),
        cost_estimate=pl.CostEstimate(
            flops=2 * rows * width * width, transcendentals=0, bytes_accessed=2 * width * width
        ),
        name="out_back",
    )(in_grad, x1, gain, gy, before, att, a, b, m, norms, cross, weights)


def qkv_back_kernel(gq_ref, gkv_ref, cos_ref, sin_ref, before_ref, u_ref, a_ref, b_ref, m_ref, n_ref, cross_ref,
                    x_ref, gain_ref, gx_ref, w0_ref, w1_ref,
                    out_ref, ga_ref, gb_ref, gm_ref, lhs0, lhs1, gi, tail):
    t = pl.program_id(0)
    rows, width = gx_ref.shape
    low = jnp.bfloat16
    k_cols = w1_ref.shape[2]
    bounds = [(0, width), (width, width + k_cols), (width + k_cols, width + 2 * k_cols)]

    @pl.when(t == 0)
    def _():
        cosine, sine = cos_ref[...], -sin_ref[...]
        k_parts = [gkv_ref[:, 256 * j : 256 * j + 128] for j in range(k_cols // 128)]
        v_parts = [gkv_ref[:, 256 * j + 128 : 256 * j + 256] for j in range(k_cols // 128)]
        rounded = lambda z: z.astype(low).astype(jnp.float32)
        ups = [
            turn(gq_ref[...].astype(jnp.float32), cosine, sine),
            turn(rounded(jnp.concatenate(k_parts, axis=1)), cosine, sine),
            rounded(jnp.concatenate(v_parts, axis=1)),
        ]
        lhs0[rows:] = jnp.zeros_like(lhs0[rows:])
        lhs1[rows:] = jnp.zeros_like(lhs1[rows:])
        for p, (start, stop) in enumerate(bounds):
            g, norm, m = ups[p], n_ref[:, start:stop], m_ref[:, start:stop]
            a = a_ref[p].astype(low)
            b = b_ref[:, start:stop].astype(low)
            b_wide = b.astype(jnp.float32)
            gb = (g * (m / norm)).astype(low)
            gm = jnp.sum(g * before_ref[:, start:stop], axis=0, keepdims=True) / norm
            gm_ref[:, start:stop] = gm
            c = -gm * m / (norm * norm)
            weighted = b_wide * c
            gi[:, 16 * p : 16 * p + 16] = (SCALE * dot_nt(gb, b)).astype(low)
            tail[16 * p : 16 * p + 16] = lax.dot_general(
                weighted, b_wide, last_last, precision=highest, preferred_element_type=jnp.float32
            )
            inner = dot_nt(u_ref[...], a).astype(low)
            gb_ref[:, start:stop] = SCALE * dot_tn(inner, gb) + SCALE * c * cross_ref[:, start:stop]
            lhs, at = (lhs1, 0) if p == 2 else (lhs0, start)
            lhs[:rows, at : at + stop - start] = gb
            lhs[rows + 16 * p : rows + 16 * p + 16, at : at + stop - start] = weighted.astype(low)

    span = pl.ds(pl.multiple_of(t * TILE, TILE), TILE)
    back = dot_nt(lhs0[...], w0_ref[0]) + dot_nt(lhs1[...], w1_ref[0])
    grad_in = back[:rows]
    for p in range(3):
        a_tile = a_ref[p, :, span].astype(low)
        gi_p = gi[:, 16 * p : 16 * p + 16]
        grad_in = grad_in + dot_f32(gi_p, a_tile)
        spread = back[rows + 16 * p : rows + 16 * p + 16] + SCALE * jnp.dot(
            tail[16 * p : 16 * p + 16], a_tile.astype(jnp.float32), precision=highest,
            preferred_element_type=jnp.float32,
        )
        ga_ref[p] = dot_tn(gi_p, u_ref[:, span]) + SCALE * spread
    out_ref[:, span] = grad_in

    @pl.when(t == pl.num_programs(0) - 1)
    def _():
        v = x_ref[...].astype(jnp.float32)
        out_ref[...] = gx_ref[...] + rms_back(v, gain_ref[...], out_ref[...])


def qkv_back(gq, gkv, cosine, sine, before, u, a, b, m, norms, cross, x, gain, gx, weights):
    rows, width = gx.shape
    cols = before.shape[1]
    k_cols = (cols - width) // 2
    tiles = width // TILE
    full = lambda shape: pl.BlockSpec(shape, lambda t: (0,) * len(shape))
    f32, low = jnp.float32, jnp.bfloat16
    wide = full((rows, width))
    return pl.pallas_call(
        qkv_back_kernel,
        out_shape=(
            jax.ShapeDtypeStruct((rows, width), f32),
            jax.ShapeDtypeStruct((3, 16, width), f32),
            jax.ShapeDtypeStruct((16, cols), f32),
            jax.ShapeDtypeStruct((1, cols), f32),
        ),
        grid=(tiles,),
        in_specs=[wide, full(gkv.shape), full(cosine.shape), full(sine.shape), full((rows, cols)), wide,
                  full((3, 16, width)), full((16, cols)), full((1, cols)), full((1, cols)), full((16, cols)),
                  wide, full((1, width)), wide,
                  pl.BlockSpec((1, TILE, width + k_cols), lambda t: (0, t, 0)),
                  pl.BlockSpec((1, TILE, k_cols), lambda t: (1, t, 0))],
        out_specs=(wide, pl.BlockSpec((3, 16, TILE), lambda t: (0, 0, t)), full((16, cols)), full((1, cols))),
        scratch_shapes=[
            pltpu.VMEM((rows + 48, width + k_cols), low),
            pltpu.VMEM((rows + 48, k_cols), low),
            pltpu.VMEM((rows, 48), low),
            pltpu.VMEM((48, 16), f32),
        ],
        compiler_params=pltpu.CompilerParams(vmem_limit_bytes=48 << 20),
        cost_estimate=pl.CostEstimate(
            flops=2 * rows * width * cols, transcendentals=0, bytes_accessed=2 * width * cols
        ),
        name="qkv_back",
    )(gq, gkv, cosine, sine, before, u, a, b, m, norms, cross, x, gain, gx, weights, weights)

MESH = pl.DeviceIdType.MESH


def place_in_seq():
    s = lax.axis_index("seq")
    return s, s // 2, lax.rem(s, 2)


def greet(nc, q, s):
    barrier = pltpu.get_barrier_semaphore()

    def signal(target):
        pl.semaphore_signal(barrier, inc=1, device_id={"seq": target}, device_id_type=MESH)

    sibling = s + 1 - 2 * lax.rem(s, 2)
    signal(sibling)
    pl.when(q > 0)(lambda: signal(s - 2))
    pl.when(q < nc - 1)(lambda: signal(s + 2))
    pl.semaphore_wait(barrier, 1 + jnp.where(q > 0, 1, 0) + jnp.where(q < nc - 1, 1, 0))
    return sibling

def near_first(i, q, nc):
    short = jnp.where(q <= nc - 1 - q, q, nc - 1 - q)
    far = jnp.where(q <= nc - 1 - q, i, nc - 1 - i)
    step = (i + 1) // 2
    near = q - step if i % 2 else q + step
    return jnp.where(i <= 2 * short, near, far)


def place_in_rows(rows):
    half = rows // 2
    r = lax.axis_index("rows")
    a, b = r // 2, lax.rem(r, 2)
    turned = lambda k: 2 * lax.rem(a + k + half, half)
    return r, 2 * a + 1 - b, lambda k: turned(k) + b, lambda k: turned(k) + 1 - b


def greet_all(n, rows):
    s = lax.axis_index("seq")
    r, b_row, a_row, _ = place_in_rows(rows)
    barrier = pltpu.get_barrier_semaphore()
    for t in range(1, n):
        pl.semaphore_signal(
            barrier, inc=1, device_id=(r, lax.rem(s + t, n)), device_id_type=MESH
        )
    pl.semaphore_signal(barrier, inc=1, device_id=(b_row, s), device_id_type=MESH)
    for k in range(1, rows // 2):
        pl.semaphore_signal(barrier, inc=1, device_id=(a_row(k), s), device_id_type=MESH)
    pl.semaphore_wait(barrier, n - 1 + rows // 2)


def remote(src, dst, send, recv, row, seq):
    return pltpu.make_async_remote_copy(
        src_ref=src, dst_ref=dst, send_sem=send, recv_sem=recv,
        device_id=(row, seq), device_id_type=MESH,
    )


def weights_kernel(n, rows, xa, xg, wa, gz, near, local, edge, a_in, a_sib_in, a_out, a_sib_out, z_in, z_out):
    nc, half = n // 2, rows // 2
    others = half - 1
    units = gz.shape[-1]
    s, q, c = place_in_seq()
    sibling = s + 1 - 2 * c
    r, b_row, a_row, diagonal = place_in_rows(rows)
    greet_all(n, rows)

    both, first, second = pl.ds(0, 2), pl.ds(0, 1), pl.ds(1, 1)
    LINE, FROM_B = 0, 1

    def from_a(k):
        return 1 + k

    def relay_b(k):
        return 1 + others + k

    def relay_a(k):
        return 1 + 2 * others + k

    def a_view(p, core, parts, row):
        return wa.at[parts, 2 * p + core, row]

    def content(kind):
        if kind == LINE:
            return both, r
        if kind == FROM_B:
            return both, b_row
        for k in range(1, half):
            if kind == from_a(k):
                return both, a_row(-k)
            if kind == relay_b(k):
                return second, diagonal(-k)
            if kind == relay_a(k):
                return first, diagonal(-k)

    kinds = 2 + 3 * others

    def a_send(p, parts, row, kind, target_row):
        return remote(
            a_view(p, c, parts, row), a_view(p, c, parts, row),
            a_out.at[p, kind], a_in.at[p, kind], target_row, s,
        )

    def a_arrival(p, kind):
        parts, row = content(kind)
        return a_send(p, parts, row, kind, r)

    def a_to_sibling(p, kind, core):
        parts, row = content(kind)
        return remote(
            a_view(p, core, parts, row), a_view(p, core, parts, row),
            a_sib_out.at[p, kind], a_sib_in.at[p, kind], r, sibling,
        )

    def columns(device):
        return pl.ds(pl.multiple_of(device * units, units), units)

    def z_send(p, core):
        return remote(
            xg.at[:, r, :, columns(2 * p + core)], gz.at[:, s],
            z_out.at[p, core], z_in.at[q, c], r, 2 * p + core,
        )

    def z_arrival(p, core):
        slot = gz.at[:, 2 * p + core]
        return remote(slot, slot, z_out.at[p, core], z_in.at[p, core], r, s)

    def line_send(p, src, sem, target):
        return remote(src, a_view(p, c, both, r), sem, a_in.at[p, LINE], r, target)

    own = xa.at[both, r]
    to_left = lambda: line_send(q, own, edge.at[0], s - 2)
    to_right = lambda: line_send(q, own, edge.at[1], s + 2)
    pl.when(q > 0)(lambda: to_left().start())
    pl.when(q < nc - 1)(lambda: to_right().start())
    order = [near_first(i, q, nc) for i in range(nc)]
    sib_a = lambda: remote(xa, wa.at[:, s], edge.at[2], edge.at[3], r, sibling)
    sib_g = lambda: remote(
        xg.at[:, :, :, columns(sibling)], near.at[:, c], edge.at[4], edge.at[5], r, sibling
    )
    keep_a = pltpu.make_async_copy(xa, wa.at[:, s], local.at[0])
    keep_g = pltpu.make_async_copy(xg.at[:, :, :, columns(s)], near.at[:, c], local.at[1])
    sib_a().start()
    keep_a.start()
    for p in order[1:]:
        a_arrival(p, LINE).wait_recv()
        pl.when((p < q) & (q < nc - 1))(
            lambda p=p: line_send(p, a_view(p, c, both, r), a_out.at[p, LINE], s + 2).start()
        )
        pl.when((p > q) & (q > 0))(
            lambda p=p: line_send(p, a_view(p, c, both, r), a_out.at[p, LINE], s - 2).start()
        )
        a_send(p, both, r, FROM_B, b_row).start()
        for k in range(1, half):
            a_send(p, both, r, from_a(k), a_row(k)).start()
        a_to_sibling(p, LINE, c).start()
        for core in range(2):
            z_send(p, core).start()
    sib_g().start()
    keep_g.start()
    for p in order[1:]:
        a_arrival(p, FROM_B).wait_recv()
        for k in range(1, half):
            a_send(p, first, b_row, relay_a(k), a_row(k)).start()
        a_to_sibling(p, FROM_B, c).start()
        for k in range(1, half):
            a_arrival(p, from_a(k)).wait_recv()
            a_send(p, second, a_row(-k), relay_b(k), b_row).start()
            a_to_sibling(p, from_a(k), c).start()
    for p in order[1:]:
        for k in range(1, half):
            for kind in (relay_b(k), relay_a(k)):
                a_arrival(p, kind).wait_recv()
                a_to_sibling(p, kind, c).start()
    keep_a.wait()
    keep_g.wait()
    sib_a().wait()
    sib_g().wait()
    pl.when(q > 0)(lambda: to_left().wait_send())
    pl.when(q < nc - 1)(lambda: to_right().wait_send())
    for p in order[1:]:
        pl.when(((p < q) & (q < nc - 1)) | ((p > q) & (q > 0)))(
            lambda p=p: line_send(p, a_view(p, c, both, r), a_out.at[p, LINE], s).wait_send()
        )
        for kind in range(kinds):
            a_to_sibling(p, kind, c).wait_send()
            a_to_sibling(p, kind, 1 - c).wait_recv()
        a_send(p, both, r, FROM_B, b_row).wait_send()
        for k in range(1, half):
            a_send(p, both, r, from_a(k), r).wait_send()
            a_send(p, first, b_row, relay_a(k), r).wait_send()
            a_send(p, second, a_row(-k), relay_b(k), r).wait_send()
        for core in range(2):
            z_send(p, core).wait_send()
            z_arrival(p, core).wait_recv()


def gather_weights(n, rows, xa, xg, collective_id):
    nc = n // 2
    block = xa.shape[1]
    part = block // rows
    xa = xa.reshape(2, rows, part, xa.shape[2])
    xg = xg.reshape(2, rows, part, xg.shape[2])
    units = xg.shape[3] // n
    kinds = 2 + 3 * (rows // 2 - 1)
    dma = pltpu.SemaphoreType.DMA
    anywhere = pl.BlockSpec(memory_space=pl.ANY)
    shape = jax.ShapeDtypeStruct
    wa, gz, near = pl.pallas_call(
        functools.partial(weights_kernel, n, rows),
        out_shape=(
            shape((2, n, rows, part, xa.shape[3]), xa.dtype),
            shape((2, n, part, units), xg.dtype),
            shape((2, 2, rows, part, units), xg.dtype),
        ),
        in_specs=[anywhere] * 2,
        out_specs=(anywhere,) * 3,
        scratch_shapes=[dma((2,)), dma((6,))] + [dma((nc, kinds))] * 4 + [dma((nc, 2))] * 2,
        compiler_params=pltpu.CompilerParams(collective_id=collective_id, has_side_effects=True),
        cost_estimate=pl.CostEstimate(
            flops=0, transcendentals=0, bytes_accessed=250 * 1024 * 1024
        ),
        name="gather_weights",
    )(xa, xg)
    return wa.reshape(2, n * block, -1), gz, near


def gather_kernel(n, rows, count, shared, *refs):
    nc = n // 2
    sources = refs[: count + len(shared[0])]
    outs = refs[len(sources) : 2 * len(sources) - len(shared[0]) + len(shared[1])]
    local_sem, to_sib, to_left, to_right, recv, share_out, share_in = refs[len(sources) + len(outs) :]
    xs, held, swapped = sources[:count], sources[count:], outs[count:]
    s, q, c = place_in_seq()
    sibling = s + 1 - 2 * c
    r, b_row, a_row, _ = place_in_rows(rows)
    greet_all(n, rows)
    locals_ = [
        pltpu.make_async_copy(xs[k], outs[k].at[s], local_sem.at[k]) for k in range(count)
    ]
    for cp in locals_:
        cp.start()

    def copy(k, src, slot, sems, target):
        return remote(src, outs[k].at[slot], sems.at[k, slot], recv.at[k, slot], r, target)

    def share(i, p):
        source, piece, turn, _ = shared[1][i]
        pair = pl.ds(2 * p, 2)
        src = held[source].at[pair] if piece is None else held[source].at[piece, pair]
        target = b_row if turn == 0 else a_row(turn)
        return remote(src, swapped[i].at[pair], share_out.at[i, p], share_in.at[i, p], target, s)

    for k in range(count):
        pl.when(q > 0)(lambda k=k: copy(k, xs[k], s, to_left, s - 2).start())
        pl.when(q < nc - 1)(lambda k=k: copy(k, xs[k], s, to_right, s + 2).start())
        copy(k, xs[k], s, to_sib, sibling).start()
    order = [near_first(i, q, nc) for i in range(nc)]
    for p in order[1:]:
        for i in range(len(shared[1])):
            share(i, p).start()
    for p in order[1:]:
        slot = 2 * p + c
        for k in range(count):
            src = outs[k].at[slot]
            copy(k, src, slot, to_right, s).wait_recv()
            pl.when((p < q) & (q < nc - 1))(
                lambda k=k, src=src, slot=slot: copy(k, src, slot, to_right, s + 2).start()
            )
            pl.when((p > q) & (q > 0))(
                lambda k=k, src=src, slot=slot: copy(k, src, slot, to_left, s - 2).start()
            )
            copy(k, src, slot, to_sib, sibling).start()
    for cp in locals_:
        cp.wait()
    for p in range(nc):
        mine, theirs = 2 * p + c, 2 * p + 1 - c
        for k in range(count):
            copy(k, outs[k].at[theirs], theirs, to_sib, sibling).wait_recv()
            copy(k, outs[k].at[mine], mine, to_sib, sibling).wait_send()
            pl.when((q < nc - 1) & (p <= q))(
                lambda k=k, mine=mine: copy(k, outs[k].at[mine], mine, to_right, s).wait_send()
            )
            pl.when((q > 0) & (p >= q))(
                lambda k=k, mine=mine: copy(k, outs[k].at[mine], mine, to_left, s).wait_send()
            )
    for p in order[1:]:
        for i in range(len(shared[1])):
            share(i, p).wait_send()
            share(i, p).wait_recv()


def gather_seq(n, rows, arrays, collective_id, held=(), shares=()):
    nc, count = n // 2, len(arrays)
    nbytes = sum(a.size * a.dtype.itemsize for a in arrays)
    dma = pltpu.SemaphoreType.DMA
    shape = jax.ShapeDtypeStruct
    outs = [shape((n, *a.shape), a.dtype) for a in arrays]
    outs += [shape(held[source].shape[-3:], held[source].dtype) for source, _, _ in shares]
    anywhere = pl.BlockSpec(memory_space=pl.ANY)
    listed = (tuple(held), [(source, piece, turn, None) for source, piece, turn in shares])
    sems = dma((max(1, len(shares)), nc))
    got = pl.pallas_call(
        functools.partial(gather_kernel, n, rows, count, (range(len(held)), listed[1])),
        out_shape=tuple(outs),
        in_specs=[anywhere] * (count + len(held)),
        out_specs=(anywhere,) * len(outs),
        scratch_shapes=[dma((count,))] + [dma((count, n))] * 4 + [sems] * 2,
        compiler_params=pltpu.CompilerParams(collective_id=collective_id, has_side_effects=True),
        cost_estimate=pl.CostEstimate(flops=0, transcendentals=0, bytes_accessed=nbytes * n * 20),
        name="gather_seq",
    )(*arrays, *held)
    return got[:count], got[count:]

def scatter_kernel(n, x_ref, o_ref, own, sib, from_left, from_right,
                   load_sem, to_sib, sib_in, to_right, right_in, to_left, left_in):
    nc = n // 2
    s, q, c = place_in_seq()
    sibling = greet(nc, q, s)
    theirs = 1 - c

    def load(p):
        return pltpu.make_async_copy(x_ref.at[2 * p + c], own.at[p], load_sem.at[p])

    def to_sibling(p):
        return pltpu.make_async_remote_copy(
            src_ref=x_ref.at[2 * p + theirs],
            dst_ref=sib.at[p],
            send_sem=to_sib.at[p],
            recv_sem=sib_in.at[p],
            device_id={"seq": sibling},
            device_id_type=MESH,
        )

    def rightward(p, target):
        return pltpu.make_async_remote_copy(
            src_ref=own.at[p],
            dst_ref=from_left.at[p],
            send_sem=to_right.at[p],
            recv_sem=right_in.at[p],
            device_id={"seq": target},
            device_id_type=MESH,
        )

    def leftward(p, target):
        return pltpu.make_async_remote_copy(
            src_ref=own.at[p],
            dst_ref=from_right.at[p],
            send_sem=to_left.at[p],
            recv_sem=left_in.at[p],
            device_id={"seq": target},
            device_id_type=MESH,
        )

    order = []
    for t in range(nc):
        for p in (nc - 1 - t, t):
            if p not in order:
                order.append(p)
    for p in order:
        to_sibling(p).start()
        load(p).start()

    f32 = jnp.float32
    for p in order:
        load(p).wait()
        to_sibling(p).wait_recv()

        @pl.when(p > q)
        def _(p=p):
            @pl.when(q > 0)
            def _():
                rightward(p, s).wait_recv()
                total = own[p].astype(f32) + sib[p].astype(f32) + from_left[p].astype(f32)
                own[p] = total.astype(own.dtype)

            @pl.when(q == 0)
            def _():
                own[p] = (own[p].astype(f32) + sib[p].astype(f32)).astype(own.dtype)

            rightward(p, s + 2).start()

        @pl.when(p < q)
        def _(p=p):
            @pl.when(q < nc - 1)
            def _():
                leftward(p, s).wait_recv()
                total = own[p].astype(f32) + sib[p].astype(f32) + from_right[p].astype(f32)
                own[p] = total.astype(own.dtype)

            @pl.when(q == nc - 1)
            def _():
                own[p] = (own[p].astype(f32) + sib[p].astype(f32)).astype(own.dtype)

            leftward(p, s - 2).start()

    o_ref[...] = own[q].astype(f32) + sib[q].astype(f32)

    @pl.when(q > 0)
    def _():
        rightward(q, s).wait_recv()
        o_ref[...] += from_left[q].astype(f32)

    @pl.when(q < nc - 1)
    def _():
        leftward(q, s).wait_recv()
        o_ref[...] += from_right[q].astype(f32)

    for p in range(nc):
        to_sibling(p).wait_send()
        pl.when(p > q)(lambda p=p: rightward(p, s).wait_send())
        pl.when(p < q)(lambda p=p: leftward(p, s).wait_send())


def scatter_seq(n, x, collective_id):
    nc = n // 2
    _, rows, cols = x.shape
    dma = pltpu.SemaphoreType.DMA
    buf = pltpu.VMEM((nc, rows, cols), x.dtype)
    return pl.pallas_call(
        functools.partial(scatter_kernel, n),
        out_shape=jax.ShapeDtypeStruct((rows, cols), jnp.float32),
        in_specs=[pl.BlockSpec(memory_space=pl.ANY)],
        out_specs=pl.BlockSpec(memory_space=pltpu.VMEM),
        scratch_shapes=[buf] * 4 + [dma((nc,))] * 7,
        compiler_params=pltpu.CompilerParams(
            collective_id=collective_id, has_side_effects=True, vmem_limit_bytes=32 << 20
        ),
        cost_estimate=pl.CostEstimate(flops=0, transcendentals=0, bytes_accessed=x.size * 2 * 20),
        name="scatter_seq",
    )(x)

def swap_halves(x):
    return pltpu.roll(x.astype(jnp.float32), HEAD_DIM, 1)


def stack_heads(block):
    lane = lax.broadcasted_iota(jnp.int32, (block.shape[0], 128), 1)
    rows = []
    for h in range(8):
        pair = block[:, (h // 2) * 128 : (h // 2 + 1) * 128].astype(jnp.float32)
        if h % 2 != h // 4:
            pair = swap_halves(pair)
        keep = lane < HEAD_DIM if h // 4 == 0 else lane >= HEAD_DIM
        rows.append(jnp.where(keep, pair, 0.0).astype(jnp.bfloat16))
    return jnp.concatenate(rows, axis=0)


def unstack_heads(stacked, span):
    lane = lax.broadcasted_iota(jnp.int32, (span, 128), 1)
    pairs = []
    for t in range(4):
        first = stacked[2 * t * span : (2 * t + 1) * span]
        second = stacked[(2 * t + 1) * span : (2 * t + 2) * span]
        if t < 2:
            second = swap_halves(second)
        else:
            first = swap_halves(first)
        pairs.append(jnp.where(lane < HEAD_DIM, first, second))
    return jnp.concatenate(pairs, axis=1)


def attend_kernel(valid_ref, q_ref, k_ref, v_ref, o_ref, p_ref):
    span = q_ref.shape[1]
    keys = k_ref.shape[0] * span
    q8 = stack_heads(q_ref[0])
    k2 = k_ref[:, 0].reshape(keys, 128)
    v2 = v_ref[:, 0].reshape(keys, 128)
    scores = lax.dot_general(q8, k2, last_last, preferred_element_type=jnp.float32)
    scores = scores * HEAD_DIM**-0.5
    first_pos = lax.axis_index("seq") * span
    q_pos = first_pos + lax.broadcasted_iota(jnp.int32, (8, span, keys), 1).reshape(8 * span, keys)
    k_pos = lax.broadcasted_iota(jnp.int32, (8 * span, keys), 1)
    allowed = (k_pos <= q_pos) & (k_pos < valid_ref[pl.program_id(0)])
    scores = jnp.where(allowed, scores, -1e30)
    unscaled = jnp.exp(scores - jnp.max(scores, axis=1, keepdims=True))
    shares = unscaled * (1.0 / jnp.sum(unscaled, axis=1, keepdims=True))
    shares = shares.astype(jnp.bfloat16)
    p_ref[0, 0] = shares
    mixed = jnp.dot(shares, v2, preferred_element_type=jnp.float32)
    o_ref[0] = unstack_heads(mixed, span).astype(jnp.bfloat16)


def attend(q, kv, valid):
    pair, span, width = q.shape
    n, kv_width = kv.shape[0], kv.shape[3] // 2
    groups = kv_width // 128
    keys = n * span
    q_spec = pl.BlockSpec((1, span, 512), lambda p, j, *_: (p, 0, j))
    flops = 4 * pair * groups * 8 * span * keys * 128
    return pl.pallas_call(
        attend_kernel,
        out_shape=(
            jax.ShapeDtypeStruct(q.shape, jnp.bfloat16),
            jax.ShapeDtypeStruct((pair, groups, 8 * span, keys), jnp.bfloat16),
        ),
        grid_spec=pltpu.PrefetchScalarGridSpec(
            num_scalar_prefetch=1,
            grid=(pair, groups),
            in_specs=[
                q_spec,
                pl.BlockSpec((n, 1, span, 128), lambda p, j, *_: (0, p, 0, j)),
                pl.BlockSpec((n, 1, span, 128), lambda p, j, *_: (0, p, 0, groups + j)),
            ],
            out_specs=(
                q_spec,
                pl.BlockSpec((1, 1, 8 * span, keys), lambda p, j, *_: (p, j, 0, 0)),
            ),
        ),
        compiler_params=pltpu.CompilerParams(vmem_limit_bytes=40 << 20),
        cost_estimate=pl.CostEstimate(
            flops=flops, transcendentals=flops // 512, bytes_accessed=8 << 20
        ),
        name="attend",
    )(valid, q, kv, kv)


def attend_back_kernel(q_ref, k_ref, v_ref, p_ref, g_ref, gq_ref, gkv_ref):
    span = q_ref.shape[1]
    keys = k_ref.shape[0] * span
    q8 = stack_heads(q_ref[0])
    g8 = stack_heads(g_ref[0])
    k2 = k_ref[:, 0].reshape(keys, 128)
    v2 = v_ref[:, 0].reshape(keys, 128)
    low = p_ref[0, 0]
    shares = low.astype(jnp.float32)
    grad_shares = lax.dot_general(g8, v2, last_last, preferred_element_type=jnp.float32)
    weighted = shares * grad_shares
    centre = jnp.sum(weighted, axis=1, keepdims=True)
    grad_scores = (weighted - shares * centre).astype(jnp.bfloat16)
    gq = jnp.dot(grad_scores, k2, preferred_element_type=jnp.float32) * HEAD_DIM**-0.5
    gq_ref[0] = unstack_heads(gq, span).astype(jnp.bfloat16)
    gk = lax.dot_general(grad_scores, q8, first_first, preferred_element_type=jnp.float32)
    gv = lax.dot_general(low, g8, first_first, preferred_element_type=jnp.float32)
    both = jnp.concatenate([gk * HEAD_DIM**-0.5, gv], axis=1).astype(jnp.bfloat16)
    gkv_ref[:, 0] = both.reshape(gkv_ref.shape[0], span, 256)


def attend_back(q, kv, shares, g):
    pair, span, _ = q.shape
    n, kv_width = kv.shape[0], kv.shape[3] // 2
    groups = kv_width // 128
    keys = n * span
    q_spec = pl.BlockSpec((1, span, 512), lambda p, j: (p, 0, j))
    flops = 10 * pair * groups * 8 * span * keys * 128
    return pl.pallas_call(
        attend_back_kernel,
        out_shape=(
            jax.ShapeDtypeStruct(q.shape, jnp.bfloat16),
            jax.ShapeDtypeStruct(kv.shape, jnp.bfloat16),
        ),
        grid=(pair, groups),
        in_specs=[
            q_spec,
            pl.BlockSpec((n, 1, span, 128), lambda p, j: (0, p, 0, j)),
            pl.BlockSpec((n, 1, span, 128), lambda p, j: (0, p, 0, groups + j)),
            pl.BlockSpec((1, 1, 8 * span, keys), lambda p, j: (p, j, 0, 0)),
            q_spec,
        ],
        out_specs=(
            q_spec,
            pl.BlockSpec((n, 1, span, 256), lambda p, j: (0, p, 0, j)),
        ),
        compiler_params=pltpu.CompilerParams(vmem_limit_bytes=40 << 20),
        cost_estimate=pl.CostEstimate(flops=flops, transcendentals=0, bytes_accessed=8 << 20),
        name="attend_back",
    )(q, kv, kv, shares, g)

def by_distance(i, q, nc):
    room = nc - 1 - q
    left_half = q <= room
    short = jnp.where(left_half, q, room)
    far = jnp.where(left_half, i, nc - 1 - i)
    step = (i + 1) // 2
    near = jnp.where(lax.rem(i, 2) == 1, q - step, q + step)
    return jnp.where(i <= 2 * short, near, far)


def ffn_kernel(n, rows, pieces, u_hbm, gy_hbm, wd_hbm, a_ref, b_ref, m_ref, ad_ref, bd_ref, md_ref, sq_ref, gram_ref,
               in_ref, down_hbm, ga_ref, gb_ref, gm_ref, norm_ref, gad_ref, gbd_ref, gmd_ref, nd_ref,
               w_parts, wd, u, gy, down, own, theirs, sib, from_left, from_right, ratio, cross, gm_all,
               w_sem, load_sem, down_sem, small_out, small_in, to_sib, sib_in, to_right, right_in, to_left, left_in):
    nc = n // 2
    f32, low = jnp.float32, jnp.bfloat16
    s, q, c = place_in_seq()
    tokens = own.shape[1]

    weights = [pltpu.make_async_copy(wd_hbm, wd, w_sem.at[0])]
    for src, dst in place_pieces(n, rows, pieces, w_parts):
        weights.append(pltpu.make_async_copy(src, dst, w_sem.at[len(weights)]))
    for cp in weights:
        cp.start()

    def loads(i):
        p = by_distance(nc - 1 - i, q, nc)
        slot = lax.rem(i, 2)
        pair = pl.ds(2 * p, 2)
        return (
            pltpu.make_async_copy(u_hbm.at[pair], u.at[slot], load_sem.at[0, slot]),
            pltpu.make_async_copy(gy_hbm.at[pair], gy.at[slot], load_sem.at[1, slot]),
        )

    for cp in loads(0):
        cp.start()
    sibling = s + 1 - 2 * c
    barrier = pltpu.get_barrier_semaphore()
    for t in range(1, n):
        pl.semaphore_signal(
            barrier, inc=1, device_id={"seq": lax.rem(s + t, n)}, device_id_type=MESH
        )

    def to_sibling(p):
        return pltpu.make_async_remote_copy(
            src_ref=theirs.at[p], dst_ref=sib.at[p], send_sem=to_sib.at[p], recv_sem=sib_in.at[p],
            device_id={"seq": sibling}, device_id_type=MESH,
        )

    def rightward(p, target):
        return pltpu.make_async_remote_copy(
            src_ref=own.at[p], dst_ref=from_left.at[p], send_sem=to_right.at[p], recv_sem=right_in.at[p],
            device_id={"seq": target}, device_id_type=MESH,
        )

    def leftward(p, target):
        return pltpu.make_async_remote_copy(
            src_ref=own.at[p], dst_ref=from_right.at[p], send_sem=to_left.at[p], recv_sem=left_in.at[p],
            device_id={"seq": target}, device_id_type=MESH,
        )

    def down_out(p):
        return pltpu.make_async_copy(
            down.at[lax.rem(p, 2)], down_hbm.at[pl.ds(2 * p, 2)], down_sem.at[lax.rem(p, 2)]
        )

    def pass_on(p):
        to_sibling(p).wait_recv()

        @pl.when(p > q)
        def _():
            @pl.when(q > 0)
            def _():
                rightward(p, s).wait_recv()
                own[p] = (own[p].astype(f32) + sib[p].astype(f32) + from_left[p].astype(f32)).astype(low)

            @pl.when(q == 0)
            def _():
                own[p] = (own[p].astype(f32) + sib[p].astype(f32)).astype(low)

            rightward(p, s + 2).start()

        @pl.when(p < q)
        def _():
            @pl.when(q < nc - 1)
            def _():
                leftward(p, s).wait_recv()
                own[p] = (own[p].astype(f32) + sib[p].astype(f32) + from_right[p].astype(f32)).astype(low)

            @pl.when(q == nc - 1)
            def _():
                own[p] = (own[p].astype(f32) + sib[p].astype(f32)).astype(low)

            leftward(p, s - 2).start()

    def starts_flow(p):
        return ((p > q) & (q == 0)) | ((p < q) & (q == nc - 1))

    w = [w_parts.at[g] for g in range(2)]
    width = u_hbm.shape[2]
    weight = lambda g: w[g][...].reshape(width, -1)
    bd = bd_ref[...].astype(low)
    ad = ad_ref[...].astype(low)
    a = [a_ref[g].astype(low) for g in range(2)]
    b = [b_ref[g].astype(low) for g in range(2)]
    for cp in weights:
        cp.wait()
    for g in range(2):
        norm, cr = column_norms(weight(g), a[g], b[g].astype(f32), dot_f32(a[g], weight(g)))
        norm_ref[g] = norm
        cross[g] = cr
        ratio[g] = m_ref[g] / norm
    for ref in (ga_ref, gb_ref, gm_ref, gad_ref, gbd_ref, gmd_ref):
        ref[...] = jnp.zeros_like(ref)
    bd_wide = bd.astype(f32)
    gram_b = jnp.dot(gram_ref[...], bd_wide, precision=highest, preferred_element_type=f32)
    squares = jnp.sum(sq_ref[...], axis=0) + SCALE * SCALE * jnp.sum(
        bd_wide * gram_b, axis=0, keepdims=True
    )
    nd_ref[...] = jnp.sqrt(squares + 1e-06)
    ratio_d = md_ref[...] / nd_ref[...]
    pl.semaphore_wait(barrier, n - 1)

    def step(i, carry):
        p = by_distance(nc - 1 - i, q, nc)
        slot = lax.rem(i, 2)
        for cp in loads(i):
            cp.wait()

        @pl.when(i + 1 < nc)
        def _():
            for cp in loads(i + 1):
                cp.start()

        x = u[slot].reshape(2 * tokens, -1)
        upstream = gy[slot].reshape(2 * tokens, -1).astype(f32)
        gb_d = (upstream * ratio_d).astype(low)
        gi_d = (SCALE * dot_nt(gb_d, bd)).astype(low)
        gh = dot_nt(gb_d, wd[...]) + dot_f32(gi_d, ad)
        inner = [dot_nt(x, a[g]).astype(low) for g in range(2)]
        before = [dot_f32(x, weight(g)) + SCALE * dot_f32(inner[g], b[g]) for g in range(2)]
        gate = before[0] * ratio[0]
        lift = before[1] * ratio[1]
        sig = 1.0 / (1.0 + jnp.exp(-gate))
        silu = gate * sig
        hidden = (silu * lift).astype(low)
        grads = [gh * lift * sig * (1.0 + gate * (1.0 - sig)), gh * silu]
        gb = [(grads[g] * ratio[g]).astype(low) for g in range(2)]
        gi = [(SCALE * dot_nt(gb[g], b[g])).astype(low) for g in range(2)]
        back = dot_nt(gb[0], weight(0)) + dot_nt(gb[1], weight(1)) + dot_f32(gi[0], a[0]) + dot_f32(gi[1], a[1])
        back = back.astype(low).reshape(2, tokens, -1)
        first, second = back[0], back[1]

        @pl.when(c == 0)
        def _():
            own[p] = first
            theirs[p] = second

        @pl.when(c == 1)
        def _():
            own[p] = second
            theirs[p] = first

        to_sibling(p).start()
        inner_d = dot_nt(hidden, ad).astype(low)
        part = dot_f32(hidden, wd[...]) + SCALE * dot_f32(inner_d, bd)

        @pl.when(i >= 2)
        def _():
            down_out(slot).wait()

        down[slot] = part.astype(low).reshape(2, tokens, -1)
        pltpu.make_async_copy(down.at[slot], down_hbm.at[pl.ds(2 * p, 2)], down_sem.at[slot]).start()
        gmd_ref[...] += jnp.sum(upstream * part, axis=0, keepdims=True)
        gad_ref[...] += dot_tn(gi_d, hidden)
        gbd_ref[...] += SCALE * dot_tn(inner_d, gb_d)
        for g in range(2):
            gm_ref[g] += jnp.sum(grads[g] * before[g], axis=0, keepdims=True)
            ga_ref[g] += dot_tn(gi[g], x)
            gb_ref[g] += SCALE * dot_tn(inner[g], gb[g])

        pl.when(starts_flow(p))(lambda: pass_on(p))
        last = by_distance(nc - i, q, nc)
        pl.when((i > 0) & jnp.logical_not(starts_flow(last)))(lambda: pass_on(last))
        return carry

    lax.fori_loop(0, nc, step, 0)

    gmd_ref[...] = gmd_ref[...] / nd_ref[...]

    def small(t, slot):
        return pltpu.make_async_remote_copy(
            src_ref=gmd_ref,
            dst_ref=gm_all.at[slot],
            send_sem=small_out.at[t],
            recv_sem=small_in.at[t],
            device_id={"seq": lax.rem(s + t, n)},
            device_id_type=MESH,
        )

    for t in range(1, n):
        small(t, s).start()
    for g in range(2):
        norm = norm_ref[g]
        gm = gm_ref[g] / norm
        gm_ref[g] = gm
        col = -gm * m_ref[g] / (norm * norm)
        b_wide = b[g].astype(f32)
        weighted = b_wide * col
        tail = lax.dot_general(
            weighted, b_wide, last_last, precision=highest, preferred_element_type=f32
        )
        spread = dot_nt(weighted.astype(low), weight(g)) + SCALE * jnp.dot(
            tail, a[g].astype(f32), precision=highest, preferred_element_type=f32
        )
        ga_ref[g] += SCALE * spread
        gb_ref[g] += SCALE * col * cross[g]

    gm_line = gmd_ref[...]
    for t in range(1, n):
        slot = lax.rem(s - t + n, n)
        small(t, slot).wait_recv()
        gm_line = gm_line + gm_all[slot]
    col = -gm_line * md_ref[...] / (nd_ref[...] * nd_ref[...])
    weighted = bd_wide * col
    tail = lax.dot_general(
        weighted, bd_wide, last_last, precision=highest, preferred_element_type=f32
    )
    gad_ref[...] += SCALE * (
        dot_nt(weighted.astype(low), wd[...])
        + SCALE * jnp.dot(tail, ad.astype(f32), precision=highest, preferred_element_type=f32)
    )
    own_gram = jnp.where(s == 0, SCALE, 0.0) * gram_b
    gbd_ref[...] += SCALE * col * (dot_f32(ad, wd[...]) + own_gram)

    to_sibling(q).wait_recv()
    in_ref[...] = own[q].astype(f32) + sib[q].astype(f32)

    @pl.when(q > 0)
    def _():
        rightward(q, s).wait_recv()
        in_ref[...] += from_left[q].astype(f32)

    @pl.when(q < nc - 1)
    def _():
        leftward(q, s).wait_recv()
        in_ref[...] += from_right[q].astype(f32)

    for i in range(min(2, nc)):
        pltpu.make_async_copy(down.at[i], down_hbm.at[pl.ds(0, 2)], down_sem.at[i]).wait()
    for t in range(1, n):
        small(t, s).wait_send()
    for p in range(nc):
        to_sibling(p).wait_send()
        pl.when(p > q)(lambda p=p: rightward(p, s).wait_send())
        pl.when(p < q)(lambda p=p: leftward(p, s).wait_send())


def share_plan(rows):
    turns = range(1, rows // 2)
    first = [(0, 0, k) for k in turns] + [(0, 1, 0)]
    second = [(0, 0, 0)] + [(0, 1, k) for k in turns]
    second += [(k, None, 0) for k in turns] + [(rows // 2, None, k) for k in turns]
    return first, second


def place_pieces(n, rows, pieces, w_parts):
    nc, half = n // 2, rows // 2
    _, q, _ = place_in_seq()
    r, b_row, a_row, diagonal = place_in_rows(rows)
    own, near = pieces[:2]
    turns = range(1, half)
    held = [(own.at[g], g, r) for g in range(2)]
    kinds = [(0, a_row(-k)) for k in turns] + [(1, b_row)]
    kinds += [(0, b_row)] + [(1, a_row(-k)) for k in turns]
    kinds += [(0, diagonal(-k)) for k in turns] + [(1, diagonal(-k)) for k in turns]
    held += [(piece, g, hold) for piece, (g, hold) in zip(pieces[2:], kinds)]
    out = [(near, w_parts.at[:, pl.ds(2 * q, 2)])]
    for i in range(1, nc):
        pair = pl.ds(2 * near_first(i, q, nc), 2)
        out += [(src.at[pair], w_parts.at[g, pair, hold]) for src, g, hold in held]
    return out


def feed_forward(n, rows, pieces, u, gy, wd, a, b, m, ad, bd, md, sq, gram, collective_id):
    nc = n // 2
    _, tokens, width = u.shape
    units = wd.shape[0]
    f32, low = jnp.float32, jnp.bfloat16
    shape = jax.ShapeDtypeStruct
    vmem = pl.BlockSpec(memory_space=pltpu.VMEM)
    hbm = pl.BlockSpec(memory_space=pl.ANY)
    dma = pltpu.SemaphoreType.DMA
    line = pltpu.VMEM((nc, tokens, width), low)
    pair = pltpu.VMEM((2, 2, tokens, width), low)
    part = pieces[0].shape[2]
    copies = 2 + (n // 2 - 1) * (2 + 2 * rows - 2)
    count = len(pieces)

    def kernel(*refs):
        ffn_kernel(n, rows, refs[:count], *refs[count:])

    return pl.pallas_call(
        kernel,
        out_shape=(
            shape((tokens, width), f32),
            shape((n, tokens, width), low),
            shape((2, 16, width), f32),
            shape((2, 16, units), f32),
            shape((2, 1, units), f32),
            shape((2, 1, units), f32),
            shape((16, units), f32),
            shape((16, width), f32),
            shape((1, width), f32),
            shape((1, width), f32),
        ),
        in_specs=[hbm] * (count + 3) + [vmem] * 8,
        out_specs=(vmem, hbm) + (vmem,) * 8,
        scratch_shapes=[
            pltpu.VMEM((2, n, rows, part, units), low),
            pltpu.VMEM((units, width), low),
            pair, pair, pair,
            line, line, line, line, line,
            pltpu.VMEM((2, 1, units), f32),
            pltpu.VMEM((2, 16, units), f32),
            pltpu.VMEM((n, 1, width), f32),
            dma((copies,)), dma((2, 2)), dma((2,)), dma((n,)), dma((n,)),
        ] + [dma((nc,))] * 6,
        compiler_params=pltpu.CompilerParams(
            collective_id=collective_id, has_side_effects=True, vmem_limit_bytes=60 << 20
        ),
        cost_estimate=pl.CostEstimate(
            flops=12 * n * tokens * width * units, transcendentals=n * tokens * units,
            bytes_accessed=32 << 20,
        ),
        name="feed_forward",
    )(*pieces, u, gy, wd, a, b, m, ad, bd, md, sq, gram)

def reduce_kernel(n, rows, ga_qkv, ga_o, gb_qkv, gb_o, ga_gu, gb_d, gm_qkv, gm_o, gm_d, gb_gu, gm_gu, n_gu, ga_d,
                  o_ga, o_gb_qo, o_gb_kv, o_gm_q, o_gm_kv, o_gm_o, o_ga_gu, o_gb_gu, o_gm_gu, o_ga_d, o_gb_d, o_gm_d, o_n,
                  part, from_sib, mid, from_rows, from_line, line_out, units, units_in, whole, units_all,
                  sib_out, sib_in, row_out, row_in, line_send, line_in, back_send, back_in, wide_send, wide_in,
                  pass_send, pass_in):
    nc = n // 2
    f32, low = jnp.float32, jnp.bfloat16
    s, q, c = place_in_seq()
    sibling = s + 1 - 2 * c
    r = lax.axis_index("rows")
    width = ga_o.shape[1]
    cols = width // (2 * rows)
    kv = (gb_qkv.shape[1] - width) // 2
    height = part.shape[2]
    piece = height // nc
    unit_rows = units.shape[1]
    size = units.shape[2]

    barrier = pltpu.get_barrier_semaphore()
    for t in range(1, n):
        pl.semaphore_signal(barrier, inc=1, device_id=(r, lax.rem(s + t, n)), device_id_type=MESH)
    for t in range(1, rows):
        pl.semaphore_signal(barrier, inc=1, device_id=(lax.rem(r + t, rows), s), device_id_type=MESH)

    gb_k, gb_v = gb_qkv[:, width : width + kv], gb_qkv[:, width + kv :]
    small = jnp.concatenate(
        [
            jnp.concatenate([gb_k[:8], gb_k[8:], gb_v[:8], gb_v[8:]], axis=1),
            gm_qkv[:, :width],
            gm_o[...],
            gm_d[...],
            jnp.concatenate([gm_qkv[:, width:], jnp.zeros((1, width - 2 * kv), f32)], axis=1),
            jnp.zeros((4, width), f32),
        ],
        axis=0,
    )
    groups = [ga_qkv[0], ga_qkv[1], ga_qkv[2], ga_o[...], gb_qkv[:, :width], gb_o[...], ga_gu[0], ga_gu[1], gb_d[...], small]
    for j in range(2 * rows):
        for g, value in enumerate(groups):
            part[j % 2, j // 2, 16 * g : 16 * g + 16] = value[:, cols * j : cols * (j + 1)].astype(low)
        if height > 160:
            part[j % 2, j // 2, 160:] = jnp.zeros((height - 160, cols), low)
    n_high = [n_gu[g].astype(low).astype(f32) for g in range(2)]
    n_rest = [n_gu[g] - n_high[g] for g in range(2)]
    tops = jnp.concatenate(
        [gm_gu[0], gm_gu[1]]
        + [v * (1.0 / rows) for v in (n_high[0], n_rest[0], n_high[1], n_rest[1])]
        + [jnp.zeros((2, size), f32)],
        axis=0,
    )
    blocks = [gb_gu[0][:8], gb_gu[0][8:], gb_gu[1][:8], gb_gu[1][8:], ga_d[:8], ga_d[8:], tops, jnp.zeros((8, size), f32)]
    per = unit_rows // 8
    for j in range(rows):
        units[j] = jnp.concatenate(blocks[per * j : per * (j + 1)], axis=0).astype(low)
    pl.semaphore_wait(barrier, n - 1 + rows - 1)

    def to_sibling():
        return remote(part.at[1 - c], from_sib, sib_out.at[0], sib_in.at[0], r, sibling)

    def member(t):
        return lax.rem(r + t + rows, rows)

    def row_send(t):
        return remote(mid.at[member(t)], from_rows.at[t], row_out.at[0, t], row_in.at[0, t], member(t), s)

    def unit_send(t):
        return remote(units.at[member(t)], units_in.at[t], row_out.at[1, t], row_in.at[1, t], member(t), s)

    def chip(t):
        return lax.rem(q + t + nc, nc)

    def line_part(t):
        return remote(line_out.at[chip(t)], from_line.at[t], line_send.at[t], line_in.at[t], r, 2 * chip(t) + c)

    def back(t, slot):
        return remote(whole.at[r, c, slot], whole.at[r, c, slot], back_send.at[0, t], back_in.at[0, t], r, 2 * chip(t) + c)

    def unit_back(t, slot):
        return remote(
            units_all.at[r, c, slot], units_all.at[r, c, slot], back_send.at[1, t], back_in.at[1, t], r, 2 * chip(t) + c
        )

    def wide(t, row):
        return remote(whole.at[row, c], whole.at[row, c], wide_send.at[0, t], wide_in.at[0, t], member(t), s)

    def unit_wide(t, row):
        return remote(units_all.at[row, c], units_all.at[row, c], wide_send.at[1, t], wide_in.at[1, t], member(t), s)

    def hand(t, row, core):
        return remote(whole.at[row, core], whole.at[row, core], pass_send.at[0, t], pass_in.at[0, t], r, sibling)

    def unit_hand(t, row, core):
        return remote(units_all.at[row, core], units_all.at[row, core], pass_send.at[1, t], pass_in.at[1, t], r, sibling)

    to_sibling().start()
    for t in range(1, rows):
        unit_send(t).start()
    to_sibling().wait_recv()
    for t in range(rows):
        mid[member(t)] = (part[c, member(t)].astype(f32) + from_sib[member(t)].astype(f32)).astype(low)
        if t:
            row_send(t).start()
    unit_sum = units[r].astype(f32)
    for t in range(1, rows):
        unit_send(t).wait_recv()
        unit_sum = unit_sum + units_in[t].astype(f32)
    units_all[r, c, q] = unit_sum.astype(low)
    for t in range(1, nc):
        unit_back(t, q).start()
    total = mid[r].astype(f32)
    for t in range(1, rows):
        row_send(t).wait_recv()
        total = total + from_rows[t].astype(f32)
    for p in range(nc):
        line_out[p] = total[piece * p : piece * (p + 1)].astype(low)
    for t in range(1, nc):
        line_part(t).start()
    own = line_out[q].astype(f32)
    for t in range(1, nc):
        line_part(t).wait_recv()
        own = own + from_line[t].astype(f32)
    whole[r, c, q] = own.astype(low)
    for t in range(1, nc):
        back(t, q).start()
    for t in range(1, nc):
        back(t, chip(-t)).wait_recv()
        unit_back(t, chip(-t)).wait_recv()
    for t in range(1, rows):
        wide(t, r).start()
        unit_wide(t, r).start()
    hand(0, r, c).start()
    unit_hand(0, r, c).start()
    for t in range(1, rows):
        wide(t, member(-t)).wait_recv()
        hand(t, member(-t), c).start()
        unit_wide(t, member(-t)).wait_recv()
        unit_hand(t, member(-t), c).start()
    for t in range(rows):
        hand(t, member(-t), 1 - c).wait_recv()
        unit_hand(t, member(-t), 1 - c).wait_recv()

    for j in range(2 * rows):
        block = jnp.concatenate([whole[j // 2, j % 2, p].astype(f32) for p in range(nc)], axis=0)
        at = slice(cols * j, cols * (j + 1))
        for g in range(4):
            o_ga[g, :, at] = block[16 * g : 16 * g + 16]
        o_gb_qo[0, :, at] = block[64:80]
        o_gb_qo[1, :, at] = block[80:96]
        o_ga_gu[0, :, at] = block[96:112]
        o_ga_gu[1, :, at] = block[112:128]
        o_gb_d[:, at] = block[128:144]
        which, start = divmod(cols * j, kv)
        o_gb_kv[which // 2, 8 * (which % 2) : 8 * (which % 2) + 8, start : start + cols] = block[144:152]
        o_gm_q[:, at] = block[152:153]
        o_gm_o[:, at] = block[153:154]
        o_gm_d[:, at] = block[154:155]
        if which < 2:
            o_gm_kv[which : which + 1, start : start + cols] = block[155:156]
    for j in range(rows):
        for dev in range(n):
            block = units_all[j, dev % 2, dev // 2].astype(f32)
            at = slice(size * dev, size * (dev + 1))
            for t in range(per):
                rows8, place = block[8 * t : 8 * t + 8], per * j + t
                half = slice(8 * (place % 2), 8 * (place % 2) + 8)
                if place < 4:
                    o_gb_gu[place // 2, half, at] = rows8
                elif place < 6:
                    o_ga_d[half, at] = rows8
                elif place == 6:
                    o_gm_gu[:, at] = rows8[:2]
                    o_n[0:1, at] = rows8[2:3] + rows8[3:4]
                    o_n[1:2, at] = rows8[4:5] + rows8[5:6]

    to_sibling().wait_send()
    for t in range(1, rows):
        row_send(t).wait_send()
        unit_send(t).wait_send()
        wide(t, r).wait_send()
        unit_wide(t, r).wait_send()
    for t in range(1, nc):
        line_part(t).wait_send()
        back(t, q).wait_send()
        unit_back(t, q).wait_send()
    for t in range(rows):
        hand(t, member(-t), c).wait_send()
        unit_hand(t, member(-t), c).wait_send()


def sum_gradients(n, rows, full, own_units, collective_id):
    nc = n // 2
    width, size = full[1].shape[1], own_units[3].shape[1]
    kv = (full[2].shape[1] - width) // 2
    wide_units = size * n
    cols = width // (2 * rows)
    height = -(-160 // (8 * nc)) * 8 * nc
    unit_rows = 64 // rows
    f32, low = jnp.float32, jnp.bfloat16
    shape = lambda *dims: jax.ShapeDtypeStruct(dims, f32)
    vmem = pl.BlockSpec(memory_space=pltpu.VMEM)
    dma = pltpu.SemaphoreType.DMA
    outs = (
        shape(4, 16, width), shape(2, 16, width), shape(2, 16, kv), shape(1, width), shape(2, kv), shape(1, width),
        shape(2, 16, width), shape(2, 16, wide_units), shape(2, wide_units), shape(16, wide_units), shape(16, width),
        shape(1, width), shape(2, wide_units),
    )
    block = (rows, height, cols)
    return pl.pallas_call(
        functools.partial(reduce_kernel, n, rows),
        out_shape=outs,
        in_specs=[vmem] * 13,
        out_specs=(vmem,) * 13,
        scratch_shapes=[
            pltpu.VMEM((2, *block), low),
            pltpu.VMEM(block, low),
            pltpu.VMEM(block, low),
            pltpu.VMEM(block, low),
            pltpu.VMEM((nc, height // nc, cols), low),
            pltpu.VMEM((nc, height // nc, cols), low),
            pltpu.VMEM((rows, unit_rows, size), low),
            pltpu.VMEM((rows, unit_rows, size), low),
            pltpu.VMEM((rows, 2, nc, height // nc, cols), low),
            pltpu.VMEM((rows, 2, nc, unit_rows, size), low),
            dma((1,)), dma((1,)), dma((2, rows)), dma((2, rows)), dma((nc,)), dma((nc,)),
            dma((2, nc)), dma((2, nc)), dma((2, rows)), dma((2, rows)), dma((2, rows)), dma((2, rows)),
        ],
        compiler_params=pltpu.CompilerParams(
            collective_id=collective_id, has_side_effects=True, vmem_limit_bytes=48 << 20
        ),
        cost_estimate=pl.CostEstimate(flops=0, transcendentals=0, bytes_accessed=64 << 20),
        name="sum_gradients",
    )(*full, *own_units)

def square_terms(weight, a_low, b_low):
    cross = dot_f32(a_low, weight)
    squares = jnp.sum(jnp.square(weight.astype(jnp.float32)), axis=0, keepdims=True)
    return squares + 2.0 * SCALE * jnp.sum(b_low.astype(jnp.float32) * cross, axis=0, keepdims=True)


def drift_stats(magnitude_vector, norms):
    drift = jnp.sqrt(jnp.mean(jnp.square(magnitude_vector - norms))) / jnp.sqrt(
        jnp.mean(jnp.square(magnitude_vector)) + 1e-06
    )
    return jnp.stack([drift, jnp.mean(norms)])


def local(
    layer_input,
    output_gradient,
    norm_gain_vectors,
    query_output_frozen,
    key_value_frozen,
    gate_up_frozen,
    down_frozen_weight,
    attention_adapter_a,
    query_output_adapter_b,
    key_value_adapter_b,
    query_magnitude,
    key_value_magnitude,
    output_magnitude,
    gate_up_adapter_a,
    gate_up_adapter_b,
    gate_up_magnitude,
    down_adapter_a,
    down_adapter_b,
    down_magnitude,
    prompt_length_list,
    response_length_list,
):
    pair_rows, span_len, model_width = layer_input.shape
    token_count = pair_rows * span_len
    kv_width = KV_HEADS * HEAD_DIM
    qkv_width = model_width + 2 * kv_width
    seq_size = lax.axis_size("seq")
    rows_size = lax.axis_size("rows")
    seq_index = lax.axis_index("seq")
    low, f32 = jnp.bfloat16, jnp.float32
    slice_units = down_frozen_weight.shape[0]
    start = seq_index * slice_units

    packed = jnp.stack(
        [
            jnp.concatenate([query_output_frozen[0], key_value_frozen[0]], axis=1),
            jnp.concatenate([key_value_frozen[1], query_output_frozen[1]], axis=1),
        ]
    )
    weights, gu_own, gu_near = gather_weights(seq_size, rows_size, packed, gate_up_frozen, 1)
    shares_1, shares_2 = share_plan(rows_size)
    weights, grad_out_rows = lax.optimization_barrier(
        (weights, output_gradient.reshape(token_count, model_width))
    )
    gy_all = lax.all_gather(grad_out_rows, "seq", axis=0, tiled=False)

    b_attn = jnp.concatenate(
        [
            query_output_adapter_b[0],
            key_value_adapter_b[0],
            key_value_adapter_b[1],
            query_output_adapter_b[1],
        ],
        axis=1,
    )
    m_attn = jnp.concatenate(
        [query_magnitude, key_value_magnitude[0], key_value_magnitude[1], output_magnitude]
    )[None]
    b_gu = lax.dynamic_slice_in_dim(gate_up_adapter_b, start, slice_units, 2)
    m_gu = lax.dynamic_slice_in_dim(gate_up_magnitude, start, slice_units, 1)[:, None]
    a_d = lax.dynamic_slice_in_dim(down_adapter_a, start, slice_units, 1)
    b_d = down_adapter_b.astype(low)
    m_d = down_magnitude[None]
    sq_d = square_terms(down_frozen_weight, a_d.astype(low), b_d)

    positions = seq_index * span_len + jnp.arange(span_len, dtype=jnp.int32)
    half_dim = HEAD_DIM // 2
    frequency = 500000.0 ** (-(jnp.arange(half_dim, dtype=f32) * 2.0) / HEAD_DIM)
    angles = positions.astype(f32)[:, None] * frequency[None, :]
    cosine = jnp.tile(jnp.cos(angles), (pair_rows, 4))
    sine = jnp.tile(jnp.sin(angles), (pair_rows, 4))
    valid_len = prompt_length_list[0] + response_length_list

    x = layer_input.reshape(token_count, model_width)
    gain_attn, gain_ffn = norm_gain_vectors[:1], norm_gain_vectors[1:]
    u1, before_qkv, q, kv, n_attn, cross_attn = project_qkv(
        x, gain_attn, attention_adapter_a, weights, b_attn, m_attn, cosine, sine
    )
    (kv_all, sq_all), gu_1 = gather_seq(
        seq_size, rows_size, [kv, sq_d], 2, (gu_own,), shares_1
    )
    kv_all = kv_all.reshape(seq_size, pair_rows, span_len, 2 * kv_width)
    q = q.reshape(pair_rows, span_len, model_width)
    att, shares = attend(q, kv_all, valid_len)
    att = att.reshape(token_count, model_width)
    b_o, m_o, n_o = b_attn[:, qkv_width:], m_attn[:, qkv_width:], n_attn[:, qkv_width:]
    a_o = attention_adapter_a[3]
    before_o, x1, u2 = project_out(att, a_o, weights, b_o, m_o, n_o, x, gain_ffn)

    (u2_all,), gu_2 = gather_seq(
        seq_size, rows_size, [u2], 3, (gu_own, *gu_1), shares_2
    )
    a_d_wide = down_adapter_a.astype(low).astype(f32)
    gram_d = jnp.dot(a_d_wide, a_d_wide.T, precision=highest)
    in_grad, down_parts, ga_gu, gb_gu, gm_gu, n_gu, ga_d, gb_d, gm_d, n_d = feed_forward(
        seq_size, rows_size, (gu_own, gu_near, *gu_1, *gu_2), u2_all, gy_all, down_frozen_weight,
        gate_up_adapter_a, b_gu, m_gu, a_d, down_adapter_b, m_d, sq_all, gram_d, 4,
    )
    before_d = lax.psum_scatter(
        down_parts.reshape(seq_size * token_count, model_width), "seq", scatter_dimension=0,
        tiled=True,
    )
    layer_result = (x1 + before_d.astype(f32) * (m_d / n_d)).astype(low)

    gx1, grad_att, ga_o, gb_o, gm_o = out_back(
        in_grad, x1, gain_ffn, grad_out_rows, before_o, att, a_o, b_o, m_o, n_o,
        cross_attn[:, qkv_width:], weights,
    )
    gq, gkv = attend_back(q, kv_all, shares, grad_att.reshape(q.shape))
    gkv = scatter_seq(seq_size, gkv.reshape(seq_size, token_count, 2 * kv_width), 5)
    grad_inputs, ga_qkv, gb_qkv, gm_qkv = qkv_back(
        gq.reshape(token_count, model_width), gkv, cosine, sine, before_qkv, u1,
        attention_adapter_a[:3], b_attn[:, :qkv_width], m_attn[:, :qkv_width],
        n_attn[:, :qkv_width], cross_attn[:, :qkv_width], x, gain_attn, gx1, weights,
    )

    sums = sum_gradients(
        seq_size, rows_size,
        (ga_qkv, ga_o, gb_qkv, gb_o, ga_gu, gb_d, gm_qkv, gm_o, gm_d),
        (gb_gu, gm_gu, n_gu, ga_d),
        6,
    )
    norms_gu = sums[12]
    summed = (*sums[:3], sums[3][0], sums[4], sums[5][0], *sums[6:11], sums[11][0])
    k_end = model_width + kv_width
    stats = jnp.stack(
        [
            drift_stats(query_magnitude, n_attn[0, :model_width]),
            drift_stats(key_value_magnitude[0], n_attn[0, model_width:k_end]),
            drift_stats(key_value_magnitude[1], n_attn[0, k_end:qkv_width]),
            drift_stats(output_magnitude, n_o[0]),
            drift_stats(gate_up_magnitude[0], norms_gu[0]),
            drift_stats(gate_up_magnitude[1], norms_gu[1]),
            drift_stats(down_magnitude, n_d[0]),
        ]
    )
    shape = (pair_rows, span_len, model_width)
    return (layer_result.reshape(shape), grad_inputs.reshape(shape), *summed, stats)

def solution(mesh):
    return jax.shard_map(
        local,
        mesh=mesh,
        in_specs=(
            P("rows", "seq", None),
            P("rows", "seq", None),
            P(),
            P(None, "seq", None),
            P(None, "seq", None),
            P(None, "seq", None),
            P("seq", None),
            P(),
            P(),
            P(),
            P(),
            P(),
            P(),
            P(),
            P(),
            P(),
            P(),
            P(),
            P(),
            P("rows"),
            P("rows"),
        ),
        out_specs=(
            P("rows", "seq", None),
            P("rows", "seq", None),
            P(),
            P(),
            P(),
            P(),
            P(),
            P(),
            P(),
            P(),
            P(),
            P(),
            P(),
            P(),
            P(),
        ),
        check_vma=False,
    )
```

```python
import functools

import jax
import jax.numpy as jnp
from jax import lax
from jax.experimental import pallas as pl
from jax.experimental.pallas import tpu as pltpu
from jax.sharding import PartitionSpec as P

HEADS = 32
KV_HEADS = 8
HEAD_DIM = 64
ADAPTER_RANK = 16
ALPHA = 32
SCALE = ALPHA / ADAPTER_RANK
TILE = 512

highest = lax.Precision.HIGHEST
last_last = (((1,), (1,)), ((), ()))
first_first = (((0,), (0,)), ((), ()))

def dot_f32(a, b):
    return jnp.dot(a, b, preferred_element_type=jnp.float32)


def dot_nt(a, b):
    return lax.dot_general(a, b, last_last, preferred_element_type=jnp.float32)


def dot_tn(a, b):
    return lax.dot_general(a, b, first_first, preferred_element_type=jnp.float32)


def unit_rms(v):
    return lax.rsqrt(jnp.mean(v * v, axis=-1, keepdims=True) + 1e-05)


def rms_back(v, gain, upstream):
    r = unit_rms(v)
    scaled = gain * upstream
    return r * scaled - v * (r * r * r) * jnp.mean(scaled * v, axis=-1, keepdims=True)


def turn(z, cosine, sine):
    width = z.shape[1]
    lane = lax.broadcasted_iota(jnp.int32, z.shape, 1)
    half = HEAD_DIM // 2
    other = jnp.where(
        lax.rem(lane, HEAD_DIM) < half, -pltpu.roll(z, width - half, 1), pltpu.roll(z, half, 1)
    )
    copies = width // cosine.shape[1]
    return z * jnp.tile(cosine, (1, copies)) + other * jnp.tile(sine, (1, copies))


def column_squares(w):
    return jnp.sum(jnp.square(w.astype(jnp.float32)), axis=0, keepdims=True)


def column_norms(w, a, b_wide, cross):
    gram_b = jnp.dot(dot_nt(a, a), b_wide, precision=highest, preferred_element_type=jnp.float32)
    squares = column_squares(w) + 2.0 * SCALE * jnp.sum(b_wide * cross, axis=0, keepdims=True)
    squares = squares + SCALE * SCALE * jnp.sum(b_wide * gram_b, axis=0, keepdims=True)
    return jnp.sqrt(squares + 1e-06), cross + SCALE * gram_b


def project_kernel(kv_tiles, x_ref, gain_ref, a_ref, w_ref, b_ref, m_ref, cos_ref, sin_ref,
                   u_ref, before_ref, q_ref, kv_ref, n_ref, cross_ref):
    j = pl.program_id(0)
    q_tiles = kv_tiles[0]

    @pl.when(j == 0)
    def _():
        v = x_ref[...].astype(jnp.float32)
        u_ref[...] = (v * unit_rms(v) * gain_ref[...]).astype(jnp.bfloat16)

    a = a_ref[0].astype(jnp.bfloat16)
    b = b_ref[...].astype(jnp.bfloat16)
    b_wide = b.astype(jnp.float32)
    w = w_ref[0]
    rows = u_ref.shape[0]

    @pl.when(j < kv_tiles[1])
    def _():
        both = dot_f32(jnp.concatenate([u_ref[...], a], axis=0), w)
        norm, cross = column_norms(w, a, b_wide, both[rows:])
        n_ref[...] = norm
        cross_ref[...] = cross
        inner = dot_nt(u_ref[...], a).astype(jnp.bfloat16)
        before = both[:rows] + SCALE * dot_f32(inner, b)
        before_ref[...] = before
        y = before * (m_ref[...] / norm)

        @pl.when(j < q_tiles)
        def _():
            q_ref[...] = turn(y, cos_ref[...], sin_ref[...]).astype(jnp.bfloat16)

        @pl.when(j == q_tiles)
        def _():
            kv_ref[...] = turn(y, cos_ref[...], sin_ref[...]).astype(jnp.bfloat16)

        @pl.when(j > q_tiles)
        def _():
            kv_ref[...] = y.astype(jnp.bfloat16)

    @pl.when(j >= kv_tiles[1])
    def _():
        norm, cross = column_norms(w, a, b_wide, dot_f32(a, w))
        n_ref[...] = norm
        cross_ref[...] = cross


def project_qkv(x, gain, a, weights, b, m, cosine, sine):
    rows, width = x.shape
    cols = b.shape[1]
    per_half = weights.shape[2] // TILE
    q_tiles = width // TILE
    k_cols = weights.shape[2] - width
    kv_tiles = (q_tiles, q_tiles + 2 * k_cols // TILE)
    last = kv_tiles[1] - 1
    full = lambda shape: pl.BlockSpec(shape, lambda j: (0,) * len(shape))
    col = lambda height: pl.BlockSpec((height, TILE), lambda j: (0, j))
    which = lambda j: jnp.where(j < q_tiles, 0, jnp.where(j > last, 3, 1 + j - q_tiles))
    f32, low = jnp.float32, jnp.bfloat16
    return pl.pallas_call(
        functools.partial(project_kernel, kv_tiles),
        out_shape=(
            pltpu.HBM((rows, width), low),
            pltpu.HBM((rows, width + 2 * k_cols), f32),
            pltpu.HBM((rows, width), low),
            pltpu.HBM((rows, 2 * k_cols), low),
            pltpu.HBM((1, cols), f32),
            pltpu.HBM((16, cols), f32),
        ),
        grid=(cols // TILE,),
        in_specs=[
            full((rows, width)),
            full((1, width)),
            pl.BlockSpec((1, 16, width), lambda j: (which(j), 0, 0)),
            pl.BlockSpec((1, width, TILE), lambda j: (j // per_half, 0, j % per_half)),
            col(16),
            col(1),
            full(cosine.shape),
            full(sine.shape),
        ],
        out_specs=(
            full((rows, width)),
            pl.BlockSpec((rows, TILE), lambda j: (0, jnp.minimum(j, last))),
            pl.BlockSpec((rows, TILE), lambda j: (0, jnp.minimum(j, q_tiles - 1))),
            pl.BlockSpec((rows, TILE), lambda j: (0, jnp.clip(j - q_tiles, 0, last - q_tiles))),
            col(1),
            col(16),
        ),
        compiler_params=pltpu.CompilerParams(vmem_limit_bytes=40 << 20),
        cost_estimate=pl.CostEstimate(
            flops=2 * rows * width * cols, transcendentals=0, bytes_accessed=2 * width * cols
        ),
        name="project_qkv",
    )(x, gain, a, weights, b, m, cosine, sine)


def out_kernel(att_ref, a_ref, w_ref, b_ref, m_ref, n_ref, x_ref, gain_ref, before_ref, x1_ref, u2_ref):
    t = pl.program_id(0)
    a = a_ref[0].astype(jnp.bfloat16)
    b = b_ref[...].astype(jnp.bfloat16)
    inner = dot_nt(att_ref[...], a).astype(jnp.bfloat16)
    before = dot_f32(att_ref[...], w_ref[0]) + SCALE * dot_f32(inner, b)
    before_ref[...] = before
    x1_ref[:, pl.ds(pl.multiple_of(t * TILE, TILE), TILE)] = (
        x_ref[...].astype(jnp.float32) + before * (m_ref[...] / n_ref[...])
    )

    @pl.when(t == pl.num_programs(0) - 1)
    def _():
        v = x1_ref[...]
        u2_ref[...] = (v * unit_rms(v) * gain_ref[...]).astype(jnp.bfloat16)


def project_out(att, a, weights, b, m, norms, x, gain):
    rows, width = att.shape
    tiles = width // TILE
    skip = (weights.shape[2] - width) // TILE
    full = lambda shape: pl.BlockSpec(shape, lambda t: (0,) * len(shape))
    col = lambda height: pl.BlockSpec((height, TILE), lambda t: (0, t))
    ahead = b.shape[1] // TILE - tiles
    later = lambda height: pl.BlockSpec((height, TILE), lambda t: (0, ahead + t))
    f32 = jnp.float32
    return pl.pallas_call(
        out_kernel,
        out_shape=(
            pltpu.HBM((rows, width), f32),
            pltpu.HBM((rows, width), f32),
            pltpu.HBM((rows, width), jnp.bfloat16),
        ),
        grid=(tiles,),
        in_specs=[
            full((rows, width)),
            pl.BlockSpec((1, 16, width), lambda t: (3, 0, 0)),
            pl.BlockSpec((1, width, TILE), lambda t: (1, 0, skip + t)),
            later(16),
            later(1),
            later(1),
            col(rows),
            full((1, width)),
        ],
        out_specs=(col(rows), full((rows, width)), full((rows, width))),
        compiler_params=pltpu.CompilerParams(vmem_limit_bytes=40 << 20),
        cost_estimate=pl.CostEstimate(
            flops=2 * rows * width * width, transcendentals=0, bytes_accessed=2 * width * width
        ),
        name="project_out",
    )(att, a, weights, b, m, norms, x, gain)


def out_back_kernel(in_ref, x1_ref, gain_ref, gy_ref, before_ref, att_ref, a_ref, b_ref, m_ref, n_ref, cross_ref,
                    w_ref, gx_ref, gatt_ref, ga_ref, gb_ref, gm_ref, lhs, gi, tail):
    t = pl.program_id(0)
    rows, width = gx_ref.shape
    low = jnp.bfloat16
    a = a_ref[0].astype(low)
    o_cols = slice(b_ref.shape[1] - width, b_ref.shape[1])

    @pl.when(t == 0)
    def _():
        gx = gy_ref[...].astype(jnp.float32) + rms_back(x1_ref[...], gain_ref[...], in_ref[...])
        gx_ref[...] = gx
        norm, m = n_ref[:, o_cols], m_ref[:, o_cols]
        gb = (gx * (m / norm)).astype(low)
        lhs[:rows] = gb
        b = b_ref[:, o_cols].astype(low)
        b_wide = b.astype(jnp.float32)
        gi[...] = (SCALE * dot_nt(gb, b)).astype(low)
        gm = jnp.sum(gx * before_ref[...], axis=0, keepdims=True) / norm
        gm_ref[...] = gm
        c = -gm * m / (norm * norm)
        weighted = b_wide * c
        lhs[rows:] = weighted.astype(low)
        tail[...] = lax.dot_general(
            weighted, b_wide, last_last, precision=highest, preferred_element_type=jnp.float32
        )
        inner = dot_nt(att_ref[...], a).astype(low)
        gb_ref[...] = SCALE * dot_tn(inner, gb) + SCALE * c * cross_ref[:, o_cols]

    span = pl.ds(pl.multiple_of(t * TILE, TILE), TILE)
    a_tile = a_ref[0, :, span].astype(low)
    gi_low = gi[...]
    back = dot_nt(lhs[...], w_ref[0, :, w_ref.shape[2] - width :])
    gatt_ref[...] = (back[:rows] + dot_f32(gi_low, a_tile)).astype(low)
    spread = back[rows:] + SCALE * jnp.dot(
        tail[...], a_tile.astype(jnp.float32), precision=highest, preferred_element_type=jnp.float32
    )
    ga_ref[...] = dot_tn(gi_low, att_ref[:, span]) + SCALE * spread


def out_back(in_grad, x1, gain, gy, before, att, a, b, m, norms, cross, weights):
    rows, width = x1.shape
    tiles = width // TILE
    full = lambda shape: pl.BlockSpec(shape, lambda t: (0,) * len(shape))
    col = lambda height: pl.BlockSpec((height, TILE), lambda t: (0, t))
    f32, low = jnp.float32, jnp.bfloat16
    wide = full((rows, width))
    return pl.pallas_call(
        out_back_kernel,
        out_shape=(
            pltpu.HBM((rows, width), f32),
            pltpu.HBM((rows, width), low),
            jax.ShapeDtypeStruct((16, width), f32),
            jax.ShapeDtypeStruct((16, width), f32),
            jax.ShapeDtypeStruct((1, width), f32),
        ),
        grid=(tiles,),
        in_specs=[wide, wide, full((1, width)), wide, wide, wide,
                  pl.BlockSpec((1, 16, width), lambda t: (3, 0, 0)),
                  full(b.shape), full(m.shape), full(norms.shape), full(cross.shape),
                  pl.BlockSpec((1, TILE, weights.shape[2]), lambda t: (1, t, 0))],
        out_specs=(wide, col(rows), col(16), full((16, width)), full((1, width))),
        scratch_shapes=[
            pltpu.VMEM((rows + 16, width), low),
            pltpu.VMEM((rows, 16), low),
            pltpu.VMEM((16, 16), f32),
        ],
        compiler_params=pltpu.CompilerParams(vmem_limit_bytes=48 << 20),
        cost_estimate=pl.CostEstimate(
            flops=2 * rows * width * width, transcendentals=0, bytes_accessed=2 * width * width
        ),
        name="out_back",
    )(in_grad, x1, gain, gy, before, att, a, b, m, norms, cross, weights)


def qkv_back_kernel(gq_ref, gkv_ref, cos_ref, sin_ref, before_ref, u_ref, a_ref, b_ref, m_ref, n_ref, cross_ref,
                    x_ref, gain_ref, gx_ref, w0_ref, w1_ref,
                    out_ref, ga_ref, gb_ref, gm_ref, lhs0, lhs1, gi, tail):
    t = pl.program_id(0)
    rows, width = gx_ref.shape
    low = jnp.bfloat16
    k_cols = w1_ref.shape[2]
    bounds = [(0, width), (width, width + k_cols), (width + k_cols, width + 2 * k_cols)]

    @pl.when(t == 0)
    def _():
        cosine, sine = cos_ref[...], -sin_ref[...]
        k_parts = [gkv_ref[:, 256 * j : 256 * j + 128] for j in range(k_cols // 128)]
        v_parts = [gkv_ref[:, 256 * j + 128 : 256 * j + 256] for j in range(k_cols // 128)]
        rounded = lambda z: z.astype(low).astype(jnp.float32)
        ups = [
            turn(gq_ref[...].astype(jnp.float32), cosine, sine),
            turn(rounded(jnp.concatenate(k_parts, axis=1)), cosine, sine),
            rounded(jnp.concatenate(v_parts, axis=1)),
        ]
        lhs0[rows:] = jnp.zeros_like(lhs0[rows:])
        lhs1[rows:] = jnp.zeros_like(lhs1[rows:])
        for p, (start, stop) in enumerate(bounds):
            g, norm, m = ups[p], n_ref[:, start:stop], m_ref[:, start:stop]
            a = a_ref[p].astype(low)
            b = b_ref[:, start:stop].astype(low)
            b_wide = b.astype(jnp.float32)
            gb = (g * (m / norm)).astype(low)
            gm = jnp.sum(g * before_ref[:, start:stop], axis=0, keepdims=True) / norm
            gm_ref[:, start:stop] = gm
            c = -gm * m / (norm * norm)
            weighted = b_wide * c
            gi[:, 16 * p : 16 * p + 16] = (SCALE * dot_nt(gb, b)).astype(low)
            tail[16 * p : 16 * p + 16] = lax.dot_general(
                weighted, b_wide, last_last, precision=highest, preferred_element_type=jnp.float32
            )
            inner = dot_nt(u_ref[...], a).astype(low)
            gb_ref[:, start:stop] = SCALE * dot_tn(inner, gb) + SCALE * c * cross_ref[:, start:stop]
            lhs, at = (lhs1, 0) if p == 2 else (lhs0, start)
            lhs[:rows, at : at + stop - start] = gb
            lhs[rows + 16 * p : rows + 16 * p + 16, at : at + stop - start] = weighted.astype(low)

    span = pl.ds(pl.multiple_of(t * TILE, TILE), TILE)
    back = dot_nt(lhs0[...], w0_ref[0]) + dot_nt(lhs1[...], w1_ref[0])
    grad_in = back[:rows]
    for p in range(3):
        a_tile = a_ref[p, :, span].astype(low)
        gi_p = gi[:, 16 * p : 16 * p + 16]
        grad_in = grad_in + dot_f32(gi_p, a_tile)
        spread = back[rows + 16 * p : rows + 16 * p + 16] + SCALE * jnp.dot(
            tail[16 * p : 16 * p + 16], a_tile.astype(jnp.float32), precision=highest,
            preferred_element_type=jnp.float32,
        )
        ga_ref[p] = dot_tn(gi_p, u_ref[:, span]) + SCALE * spread
    out_ref[:, span] = grad_in

    @pl.when(t == pl.num_programs(0) - 1)
    def _():
        v = x_ref[...].astype(jnp.float32)
        out_ref[...] = gx_ref[...] + rms_back(v, gain_ref[...], out_ref[...])


def qkv_back(gq, gkv, cosine, sine, before, u, a, b, m, norms, cross, x, gain, gx, weights):
    rows, width = gx.shape
    cols = before.shape[1]
    k_cols = (cols - width) // 2
    tiles = width // TILE
    full = lambda shape: pl.BlockSpec(shape, lambda t: (0,) * len(shape))
    f32, low = jnp.float32, jnp.bfloat16
    wide = full((rows, width))
    return pl.pallas_call(
        qkv_back_kernel,
        out_shape=(
            pltpu.HBM((rows, width), f32),
            jax.ShapeDtypeStruct((3, 16, width), f32),
            jax.ShapeDtypeStruct((16, cols), f32),
            jax.ShapeDtypeStruct((1, cols), f32),
        ),
        grid=(tiles,),
        in_specs=[wide, full(gkv.shape), full(cosine.shape), full(sine.shape), full((rows, cols)), wide,
                  full(a.shape), full(b.shape), full(m.shape), full(norms.shape), full(cross.shape),
                  wide, full((1, width)), wide,
                  pl.BlockSpec((1, TILE, width + k_cols), lambda t: (0, t, 0)),
                  pl.BlockSpec((1, TILE, k_cols), lambda t: (1, t, 0))],
        out_specs=(wide, pl.BlockSpec((3, 16, TILE), lambda t: (0, 0, t)), full((16, cols)), full((1, cols))),
        scratch_shapes=[
            pltpu.VMEM((rows + 48, width + k_cols), low),
            pltpu.VMEM((rows + 48, k_cols), low),
            pltpu.VMEM((rows, 48), low),
            pltpu.VMEM((48, 16), f32),
        ],
        compiler_params=pltpu.CompilerParams(vmem_limit_bytes=48 << 20),
        cost_estimate=pl.CostEstimate(
            flops=2 * rows * width * cols, transcendentals=0, bytes_accessed=2 * width * cols
        ),
        name="qkv_back",
    )(gq, gkv, cosine, sine, before, u, a, b, m, norms, cross, x, gain, gx, weights, weights)

MESH = pl.DeviceIdType.MESH


def place_in_seq():
    s = lax.axis_index("seq")
    return s, s // 2, lax.rem(s, 2)


def greet(nc, q, s):
    barrier = pltpu.get_barrier_semaphore()

    def signal(target):
        pl.semaphore_signal(barrier, inc=1, device_id={"seq": target}, device_id_type=MESH)

    sibling = s + 1 - 2 * lax.rem(s, 2)
    signal(sibling)
    pl.when(q > 0)(lambda: signal(s - 2))
    pl.when(q < nc - 1)(lambda: signal(s + 2))
    pl.semaphore_wait(barrier, 1 + jnp.where(q > 0, 1, 0) + jnp.where(q < nc - 1, 1, 0))
    return sibling

def near_first(i, q, nc):
    short = jnp.where(q <= nc - 1 - q, q, nc - 1 - q)
    far = jnp.where(q <= nc - 1 - q, i, nc - 1 - i)
    step = (i + 1) // 2
    near = q - step if i % 2 else q + step
    return jnp.where(i <= 2 * short, near, far)


def place_in_rows(rows):
    half = rows // 2
    r = lax.axis_index("rows")
    a, b = r // 2, lax.rem(r, 2)
    turned = lambda k: 2 * lax.rem(a + k + half, half)
    return r, 2 * a + 1 - b, lambda k: turned(k) + b, lambda k: turned(k) + 1 - b


def greet_all(n, rows):
    s = lax.axis_index("seq")
    r, b_row, a_row, _ = place_in_rows(rows)
    barrier = pltpu.get_barrier_semaphore()
    for t in range(1, n):
        pl.semaphore_signal(
            barrier, inc=1, device_id=(r, lax.rem(s + t, n)), device_id_type=MESH
        )
    pl.semaphore_signal(barrier, inc=1, device_id=(b_row, s), device_id_type=MESH)
    for k in range(1, rows // 2):
        pl.semaphore_signal(barrier, inc=1, device_id=(a_row(k), s), device_id_type=MESH)
    pl.semaphore_wait(barrier, n - 1 + rows // 2)


def remote(src, dst, send, recv, row, seq):
    return pltpu.make_async_remote_copy(
        src_ref=src, dst_ref=dst, send_sem=send, recv_sem=recv,
        device_id=(row, seq), device_id_type=MESH,
    )


def weights_kernel(n, rows, xa, xg, wd_hbm, ad_ref, bd_ref, wa, gz, near, sq_ref, gram_ref, wd, local, edge, a_in, a_sib_in, a_out, a_sib_out, z_in, z_out):
    nc, half = n // 2, rows // 2
    others = half - 1
    units = gz.shape[-1]
    s, q, c = place_in_seq()
    sibling = s + 1 - 2 * c
    r, b_row, a_row, diagonal = place_in_rows(rows)
    greet_all(n, rows)

    both, first, second = pl.ds(0, 2), pl.ds(0, 1), pl.ds(1, 1)
    LINE, FROM_B = 0, 1

    def from_a(k):
        return 1 + k

    def relay_b(k):
        return 1 + others + k

    def relay_a(k):
        return 1 + 2 * others + k

    def a_view(p, core, parts, row):
        return wa.at[parts, 2 * p + core, row]

    def content(kind):
        if kind == LINE:
            return both, r
        if kind == FROM_B:
            return both, b_row
        for k in range(1, half):
            if kind == from_a(k):
                return both, a_row(-k)
            if kind == relay_b(k):
                return second, diagonal(-k)
            if kind == relay_a(k):
                return first, diagonal(-k)

    kinds = 2 + 3 * others

    def a_send(p, parts, row, kind, target_row):
        return remote(
            a_view(p, c, parts, row), a_view(p, c, parts, row),
            a_out.at[p, kind], a_in.at[p, kind], target_row, s,
        )

    def a_arrival(p, kind):
        parts, row = content(kind)
        return a_send(p, parts, row, kind, r)

    def a_to_sibling(p, kind, core):
        parts, row = content(kind)
        return remote(
            a_view(p, core, parts, row), a_view(p, core, parts, row),
            a_sib_out.at[p, kind], a_sib_in.at[p, kind], r, sibling,
        )

    def columns(device):
        return pl.ds(pl.multiple_of(device * units, units), units)

    def z_send(p, core):
        return remote(
            xg.at[:, r, :, columns(2 * p + core)], gz.at[:, s],
            z_out.at[p, core], z_in.at[q, c], r, 2 * p + core,
        )

    def z_arrival(p, core):
        slot = gz.at[:, 2 * p + core]
        return remote(slot, slot, z_out.at[p, core], z_in.at[p, core], r, s)

    def line_send(p, src, sem, target):
        return remote(src, a_view(p, c, both, r), sem, a_in.at[p, LINE], r, target)

    own = xa.at[both, r]
    to_left = lambda: line_send(q, own, edge.at[0], s - 2)
    to_right = lambda: line_send(q, own, edge.at[1], s + 2)
    pl.when(q > 0)(lambda: to_left().start())
    pl.when(q < nc - 1)(lambda: to_right().start())
    order = [near_first(i, q, nc) for i in range(nc)]
    sib_a = lambda: remote(xa, wa.at[:, s], edge.at[2], edge.at[3], r, sibling)
    sib_g = lambda: remote(
        xg.at[:, :, :, columns(sibling)], near.at[:, c], edge.at[4], edge.at[5], r, sibling
    )
    keep_a = pltpu.make_async_copy(xa, wa.at[:, s], local.at[0])
    keep_g = pltpu.make_async_copy(xg.at[:, :, :, columns(s)], near.at[:, c], local.at[1])
    sib_a().start()
    keep_a.start()
    take_d = pltpu.make_async_copy(wd_hbm, wd, local.at[2])
    take_d.start()
    a_low = ad_ref[...].astype(jnp.bfloat16)
    gram_ref[...] = dot_nt(a_low, a_low)
    mine = pl.ds(pl.multiple_of(s * wd.shape[0], wd.shape[0]), wd.shape[0])
    b_wide = bd_ref[...].astype(jnp.bfloat16).astype(jnp.float32)
    take_d.wait()
    cross = dot_f32(ad_ref[:, mine].astype(jnp.bfloat16), wd[...])
    sq_ref[...] = column_squares(wd[...]) + 2.0 * SCALE * jnp.sum(b_wide * cross, axis=0, keepdims=True)
    for p in order[1:]:
        a_arrival(p, LINE).wait_recv()
        pl.when((p < q) & (q < nc - 1))(
            lambda p=p: line_send(p, a_view(p, c, both, r), a_out.at[p, LINE], s + 2).start()
        )
        pl.when((p > q) & (q > 0))(
            lambda p=p: line_send(p, a_view(p, c, both, r), a_out.at[p, LINE], s - 2).start()
        )
        a_send(p, both, r, FROM_B, b_row).start()
        for k in range(1, half):
            a_send(p, both, r, from_a(k), a_row(k)).start()
        a_to_sibling(p, LINE, c).start()
    for p in order[1:]:
        for core in range(2):
            z_send(p, core).start()
    sib_g().start()
    keep_g.start()
    for p in order[1:]:
        a_arrival(p, FROM_B).wait_recv()
        for k in range(1, half):
            a_send(p, first, b_row, relay_a(k), a_row(k)).start()
        a_to_sibling(p, FROM_B, c).start()
        for k in range(1, half):
            a_arrival(p, from_a(k)).wait_recv()
            a_send(p, second, a_row(-k), relay_b(k), b_row).start()
            a_to_sibling(p, from_a(k), c).start()
    for p in order[1:]:
        for k in range(1, half):
            for kind in (relay_b(k), relay_a(k)):
                a_arrival(p, kind).wait_recv()
                a_to_sibling(p, kind, c).start()
    keep_a.wait()
    keep_g.wait()
    sib_a().wait()
    sib_g().wait()
    pl.when(q > 0)(lambda: to_left().wait_send())
    pl.when(q < nc - 1)(lambda: to_right().wait_send())
    for p in order[1:]:
        pl.when(((p < q) & (q < nc - 1)) | ((p > q) & (q > 0)))(
            lambda p=p: line_send(p, a_view(p, c, both, r), a_out.at[p, LINE], s).wait_send()
        )
        for kind in range(kinds):
            a_to_sibling(p, kind, c).wait_send()
            a_to_sibling(p, kind, 1 - c).wait_recv()
        a_send(p, both, r, FROM_B, b_row).wait_send()
        for k in range(1, half):
            a_send(p, both, r, from_a(k), r).wait_send()
            a_send(p, first, b_row, relay_a(k), r).wait_send()
            a_send(p, second, a_row(-k), relay_b(k), r).wait_send()
        for core in range(2):
            z_send(p, core).wait_send()
            z_arrival(p, core).wait_recv()


def gather_weights(n, rows, xa, xg, wd, ad, bd, collective_id):
    nc = n // 2
    block = xa.shape[1]
    part = block // rows
    xa = xa.reshape(2, rows, part, xa.shape[2])
    xg = xg.reshape(2, rows, part, xg.shape[2])
    units = xg.shape[3] // n
    kinds = 2 + 3 * (rows // 2 - 1)
    dma = pltpu.SemaphoreType.DMA
    anywhere = pl.BlockSpec(memory_space=pl.ANY)
    shape = jax.ShapeDtypeStruct
    vmem = pl.BlockSpec(memory_space=pltpu.VMEM)
    wa, gz, near, sq, gram = pl.pallas_call(
        functools.partial(weights_kernel, n, rows),
        out_shape=(
            shape((2, n, rows, part, xa.shape[3]), xa.dtype),
            shape((2, n, part, units), xg.dtype),
            shape((2, 2, rows, part, units), xg.dtype),
            shape((1, wd.shape[1]), jnp.float32),
            shape((16, 16), jnp.float32),
        ),
        in_specs=[anywhere] * 3 + [vmem] * 2,
        out_specs=(anywhere,) * 3 + (vmem,) * 2,
        scratch_shapes=[pltpu.VMEM(wd.shape, wd.dtype), dma((3,)), dma((6,))] + [dma((nc, kinds))] * 4 + [dma((nc, 2))] * 2,
        compiler_params=pltpu.CompilerParams(
            collective_id=collective_id, has_side_effects=True, vmem_limit_bytes=32 << 20
        ),
        cost_estimate=pl.CostEstimate(
            flops=0, transcendentals=0, bytes_accessed=250 * 1024 * 1024
        ),
        name="gather_weights",
    )(xa, xg, wd, ad, bd)
    return wa.reshape(2, n * block, -1), gz, near, sq, gram


def gather_kernel(n, rows, count, shared, *refs):
    nc = n // 2
    sources = refs[: count + len(shared[0])]
    outs = refs[len(sources) : 2 * len(sources) - len(shared[0]) + len(shared[1])]
    local_sem, to_sib, to_left, to_right, recv, share_out, share_in = refs[len(sources) + len(outs) :]
    xs, held, swapped = sources[:count], sources[count:], outs[count:]
    s, q, c = place_in_seq()
    sibling = s + 1 - 2 * c
    r, b_row, a_row, _ = place_in_rows(rows)
    greet_all(n, rows)
    locals_ = [
        pltpu.make_async_copy(xs[k], outs[k].at[s], local_sem.at[k]) for k in range(count)
    ]
    for cp in locals_:
        cp.start()

    def copy(k, src, slot, sems, target):
        return remote(src, outs[k].at[slot], sems.at[k, slot], recv.at[k, slot], r, target)

    def share(i, p):
        source, piece, turn, _ = shared[1][i]
        pair = pl.ds(2 * p, 2)
        src = held[source].at[pair] if piece is None else held[source].at[piece, pair]
        target = b_row if turn == 0 else a_row(turn)
        return remote(src, swapped[i].at[pair], share_out.at[i, p], share_in.at[i, p], target, s)

    for k in range(count):
        pl.when(q > 0)(lambda k=k: copy(k, xs[k], s, to_left, s - 2).start())
        pl.when(q < nc - 1)(lambda k=k: copy(k, xs[k], s, to_right, s + 2).start())
        copy(k, xs[k], s, to_sib, sibling).start()
    order = [near_first(i, q, nc) for i in range(nc)]
    for p in order[1:]:
        for i in range(len(shared[1])):
            share(i, p).start()
    for p in order[1:]:
        slot = 2 * p + c
        for k in range(count):
            src = outs[k].at[slot]
            copy(k, src, slot, to_right, s).wait_recv()
            pl.when((p < q) & (q < nc - 1))(
                lambda k=k, src=src, slot=slot: copy(k, src, slot, to_right, s + 2).start()
            )
            pl.when((p > q) & (q > 0))(
                lambda k=k, src=src, slot=slot: copy(k, src, slot, to_left, s - 2).start()
            )
            copy(k, src, slot, to_sib, sibling).start()
    for cp in locals_:
        cp.wait()
    for p in range(nc):
        mine, theirs = 2 * p + c, 2 * p + 1 - c
        for k in range(count):
            copy(k, outs[k].at[theirs], theirs, to_sib, sibling).wait_recv()
            copy(k, outs[k].at[mine], mine, to_sib, sibling).wait_send()
            pl.when((q < nc - 1) & (p <= q))(
                lambda k=k, mine=mine: copy(k, outs[k].at[mine], mine, to_right, s).wait_send()
            )
            pl.when((q > 0) & (p >= q))(
                lambda k=k, mine=mine: copy(k, outs[k].at[mine], mine, to_left, s).wait_send()
            )
    for p in order[1:]:
        for i in range(len(shared[1])):
            share(i, p).wait_send()
            share(i, p).wait_recv()


def gather_seq(n, rows, arrays, collective_id, held=(), shares=()):
    nc, count = n // 2, len(arrays)
    nbytes = sum(a.size * a.dtype.itemsize for a in arrays)
    dma = pltpu.SemaphoreType.DMA
    shape = jax.ShapeDtypeStruct
    outs = [shape((n, *a.shape), a.dtype) for a in arrays]
    outs += [shape(held[source].shape[-3:], held[source].dtype) for source, _, _ in shares]
    anywhere = pl.BlockSpec(memory_space=pl.ANY)
    listed = (tuple(held), [(source, piece, turn, None) for source, piece, turn in shares])
    sems = dma((max(1, len(shares)), nc))
    got = pl.pallas_call(
        functools.partial(gather_kernel, n, rows, count, (range(len(held)), listed[1])),
        out_shape=tuple(outs),
        in_specs=[anywhere] * (count + len(held)),
        out_specs=(anywhere,) * len(outs),
        scratch_shapes=[dma((count,))] + [dma((count, n))] * 4 + [sems] * 2,
        compiler_params=pltpu.CompilerParams(collective_id=collective_id, has_side_effects=True),
        cost_estimate=pl.CostEstimate(flops=0, transcendentals=0, bytes_accessed=nbytes * n * 20),
        name="gather_seq",
    )(*arrays, *held)
    return got[:count], got[count:]

def scatter_kernel(n, x_ref, o_ref, own, sib, from_left, from_right,
                   load_sem, to_sib, sib_in, to_right, right_in, to_left, left_in):
    nc = n // 2
    s, q, c = place_in_seq()
    sibling = greet(nc, q, s)
    theirs = 1 - c

    def load(p):
        return pltpu.make_async_copy(x_ref.at[2 * p + c], own.at[p], load_sem.at[p])

    def to_sibling(p):
        return pltpu.make_async_remote_copy(
            src_ref=x_ref.at[2 * p + theirs],
            dst_ref=sib.at[p],
            send_sem=to_sib.at[p],
            recv_sem=sib_in.at[p],
            device_id={"seq": sibling},
            device_id_type=MESH,
        )

    def rightward(p, target):
        return pltpu.make_async_remote_copy(
            src_ref=own.at[p],
            dst_ref=from_left.at[p],
            send_sem=to_right.at[p],
            recv_sem=right_in.at[p],
            device_id={"seq": target},
            device_id_type=MESH,
        )

    def leftward(p, target):
        return pltpu.make_async_remote_copy(
            src_ref=own.at[p],
            dst_ref=from_right.at[p],
            send_sem=to_left.at[p],
            recv_sem=left_in.at[p],
            device_id={"seq": target},
            device_id_type=MESH,
        )

    order = []
    for t in range(nc):
        for p in (nc - 1 - t, t):
            if p not in order:
                order.append(p)
    for p in order:
        to_sibling(p).start()
        load(p).start()

    f32 = jnp.float32
    for p in order:
        load(p).wait()
        to_sibling(p).wait_recv()

        @pl.when(p > q)
        def _(p=p):
            @pl.when(q > 0)
            def _():
                rightward(p, s).wait_recv()
                total = own[p].astype(f32) + sib[p].astype(f32) + from_left[p].astype(f32)
                own[p] = total.astype(own.dtype)

            @pl.when(q == 0)
            def _():
                own[p] = (own[p].astype(f32) + sib[p].astype(f32)).astype(own.dtype)

            rightward(p, s + 2).start()

        @pl.when(p < q)
        def _(p=p):
            @pl.when(q < nc - 1)
            def _():
                leftward(p, s).wait_recv()
                total = own[p].astype(f32) + sib[p].astype(f32) + from_right[p].astype(f32)
                own[p] = total.astype(own.dtype)

            @pl.when(q == nc - 1)
            def _():
                own[p] = (own[p].astype(f32) + sib[p].astype(f32)).astype(own.dtype)

            leftward(p, s - 2).start()

    o_ref[...] = own[q].astype(f32) + sib[q].astype(f32)

    @pl.when(q > 0)
    def _():
        rightward(q, s).wait_recv()
        o_ref[...] += from_left[q].astype(f32)

    @pl.when(q < nc - 1)
    def _():
        leftward(q, s).wait_recv()
        o_ref[...] += from_right[q].astype(f32)

    for p in range(nc):
        to_sibling(p).wait_send()
        pl.when(p > q)(lambda p=p: rightward(p, s).wait_send())
        pl.when(p < q)(lambda p=p: leftward(p, s).wait_send())


def scatter_seq(n, x, collective_id):
    nc = n // 2
    _, rows, cols = x.shape
    dma = pltpu.SemaphoreType.DMA
    buf = pltpu.VMEM((nc, rows, cols), x.dtype)
    return pl.pallas_call(
        functools.partial(scatter_kernel, n),
        out_shape=jax.ShapeDtypeStruct((rows, cols), jnp.float32),
        in_specs=[pl.BlockSpec(memory_space=pl.ANY)],
        out_specs=pl.BlockSpec(memory_space=pltpu.VMEM),
        scratch_shapes=[buf] * 4 + [dma((nc,))] * 7,
        compiler_params=pltpu.CompilerParams(
            collective_id=collective_id, has_side_effects=True, vmem_limit_bytes=32 << 20
        ),
        cost_estimate=pl.CostEstimate(flops=0, transcendentals=0, bytes_accessed=x.size * 2 * 20),
        name="scatter_seq",
    )(x)

def swap_halves(x):
    return pltpu.roll(x.astype(jnp.float32), HEAD_DIM, 1)


def stack_heads(block):
    lane = lax.broadcasted_iota(jnp.int32, (block.shape[0], 128), 1)
    rows = []
    for h in range(8):
        pair = block[:, (h // 2) * 128 : (h // 2 + 1) * 128].astype(jnp.float32)
        if h % 2 != h // 4:
            pair = swap_halves(pair)
        keep = lane < HEAD_DIM if h // 4 == 0 else lane >= HEAD_DIM
        rows.append(jnp.where(keep, pair, 0.0).astype(jnp.bfloat16))
    return jnp.concatenate(rows, axis=0)


def unstack_heads(stacked, span):
    lane = lax.broadcasted_iota(jnp.int32, (span, 128), 1)
    pairs = []
    for t in range(4):
        first = stacked[2 * t * span : (2 * t + 1) * span]
        second = stacked[(2 * t + 1) * span : (2 * t + 2) * span]
        if t < 2:
            second = swap_halves(second)
        else:
            first = swap_halves(first)
        pairs.append(jnp.where(lane < HEAD_DIM, first, second))
    return jnp.concatenate(pairs, axis=1)


def attend_kernel(valid_ref, q_ref, k_ref, v_ref, o_ref, p_ref):
    span = q_ref.shape[1]
    keys = k_ref.shape[0] * span
    q8 = stack_heads(q_ref[0])
    k2 = k_ref[:, 0].reshape(keys, 128)
    v2 = v_ref[:, 0].reshape(keys, 128)
    scores = lax.dot_general(q8, k2, last_last, preferred_element_type=jnp.float32)
    scores = scores * HEAD_DIM**-0.5
    first_pos = lax.axis_index("seq") * span
    q_pos = first_pos + lax.broadcasted_iota(jnp.int32, (8, span, keys), 1).reshape(8 * span, keys)
    k_pos = lax.broadcasted_iota(jnp.int32, (8 * span, keys), 1)
    allowed = (k_pos <= q_pos) & (k_pos < valid_ref[pl.program_id(0)])
    scores = jnp.where(allowed, scores, -1e30)
    unscaled = jnp.exp(scores - jnp.max(scores, axis=1, keepdims=True))
    shares = unscaled * (1.0 / jnp.sum(unscaled, axis=1, keepdims=True))
    shares = shares.astype(jnp.bfloat16)
    p_ref[0, 0] = shares
    mixed = jnp.dot(shares, v2, preferred_element_type=jnp.float32)
    o_ref[0] = unstack_heads(mixed, span).astype(jnp.bfloat16)


def attend(q, kv, valid):
    pair, span, width = q.shape
    n, kv_width = kv.shape[0], kv.shape[3] // 2
    groups = kv_width // 128
    keys = n * span
    q_spec = pl.BlockSpec((1, span, 512), lambda p, j, *_: (p, 0, j))
    flops = 4 * pair * groups * 8 * span * keys * 128
    return pl.pallas_call(
        attend_kernel,
        out_shape=(
            pltpu.HBM(q.shape, jnp.bfloat16),
            pltpu.HBM((pair, groups, 8 * span, keys), jnp.bfloat16),
        ),
        grid_spec=pltpu.PrefetchScalarGridSpec(
            num_scalar_prefetch=1,
            grid=(pair, groups),
            in_specs=[
                q_spec,
                pl.BlockSpec((n, 1, span, 128), lambda p, j, *_: (0, p, 0, j)),
                pl.BlockSpec((n, 1, span, 128), lambda p, j, *_: (0, p, 0, groups + j)),
            ],
            out_specs=(
                q_spec,
                pl.BlockSpec((1, 1, 8 * span, keys), lambda p, j, *_: (p, j, 0, 0)),
            ),
        ),
        compiler_params=pltpu.CompilerParams(vmem_limit_bytes=40 << 20),
        cost_estimate=pl.CostEstimate(
            flops=flops, transcendentals=flops // 512, bytes_accessed=8 << 20
        ),
        name="attend",
    )(valid, q, kv, kv)


def attend_back_kernel(q_ref, k_ref, v_ref, p_ref, g_ref, gq_ref, gkv_ref):
    span = q_ref.shape[1]
    keys = k_ref.shape[0] * span
    q8 = stack_heads(q_ref[0])
    g8 = stack_heads(g_ref[0])
    k2 = k_ref[:, 0].reshape(keys, 128)
    v2 = v_ref[:, 0].reshape(keys, 128)
    low = p_ref[0, 0]
    shares = low.astype(jnp.float32)
    grad_shares = lax.dot_general(g8, v2, last_last, preferred_element_type=jnp.float32)
    weighted = shares * grad_shares
    centre = jnp.sum(weighted, axis=1, keepdims=True)
    grad_scores = (weighted - shares * centre).astype(jnp.bfloat16)
    gq = jnp.dot(grad_scores, k2, preferred_element_type=jnp.float32) * HEAD_DIM**-0.5
    gq_ref[0] = unstack_heads(gq, span).astype(jnp.bfloat16)
    gk = lax.dot_general(grad_scores, q8, first_first, preferred_element_type=jnp.float32)
    gv = lax.dot_general(low, g8, first_first, preferred_element_type=jnp.float32)
    both = jnp.concatenate([gk * HEAD_DIM**-0.5, gv], axis=1).astype(jnp.bfloat16)
    gkv_ref[:, 0] = both.reshape(gkv_ref.shape[0], span, 256)


def attend_back(q, kv, shares, g):
    pair, span, _ = q.shape
    n, kv_width = kv.shape[0], kv.shape[3] // 2
    groups = kv_width // 128
    keys = n * span
    q_spec = pl.BlockSpec((1, span, 512), lambda p, j: (p, 0, j))
    flops = 10 * pair * groups * 8 * span * keys * 128
    return pl.pallas_call(
        attend_back_kernel,
        out_shape=(
            pltpu.HBM(q.shape, jnp.bfloat16),
            pltpu.HBM(kv.shape, jnp.bfloat16),
        ),
        grid=(pair, groups),
        in_specs=[
            q_spec,
            pl.BlockSpec((n, 1, span, 128), lambda p, j: (0, p, 0, j)),
            pl.BlockSpec((n, 1, span, 128), lambda p, j: (0, p, 0, groups + j)),
            pl.BlockSpec((1, 1, 8 * span, keys), lambda p, j: (p, j, 0, 0)),
            q_spec,
        ],
        out_specs=(
            q_spec,
            pl.BlockSpec((n, 1, span, 256), lambda p, j: (0, p, 0, j)),
        ),
        compiler_params=pltpu.CompilerParams(vmem_limit_bytes=40 << 20),
        cost_estimate=pl.CostEstimate(flops=flops, transcendentals=0, bytes_accessed=8 << 20),
        name="attend_back",
    )(q, kv, kv, shares, g)

def by_distance(i, q, nc):
    room = nc - 1 - q
    left_half = q <= room
    short = jnp.where(left_half, q, room)
    far = jnp.where(left_half, i, nc - 1 - i)
    step = (i + 1) // 2
    near = jnp.where(lax.rem(i, 2) == 1, q - step, q + step)
    return jnp.where(i <= 2 * short, near, far)


def ffn_kernel(n, rows, pieces, u_hbm, gy0_hbm, gy1_hbm, wd_hbm, a_ref, b_ref, m_ref, ad_ref, bd_ref, md_ref, sq_ref, gram_ref,
               in_ref, down_hbm, ga_ref, gb_ref, gm_ref, norm_ref, gad_ref, gbd_ref, gmd_ref, nd_ref,
               w_parts, wd, u, gy, down, own, theirs, sib, from_left, from_right, ratio, cross, gm_all,
               w_sem, load_sem, down_sem, small_out, small_in, to_sib, sib_in, to_right, right_in, to_left, left_in):
    nc = n // 2
    f32, low = jnp.float32, jnp.bfloat16
    s, q, c = place_in_seq()
    tokens = own.shape[1]

    weights = [pltpu.make_async_copy(wd_hbm, wd, w_sem.at[0])]
    for src, dst in place_pieces(n, rows, pieces, w_parts):
        weights.append(pltpu.make_async_copy(src, dst, w_sem.at[len(weights)]))
    for cp in weights:
        cp.start()

    def loads(i):
        p = by_distance(nc - 1 - i, q, nc)
        slot = lax.rem(i, 2)
        pair = pl.ds(2 * p, 2)
        return (
            pltpu.make_async_copy(u_hbm.at[pair], u.at[slot], load_sem.at[0, slot]),
            pltpu.make_async_copy(
                gy0_hbm.at[pair], gy.at[slot, :, : tokens // 2], load_sem.at[1, slot]
            ),
            pltpu.make_async_copy(
                gy1_hbm.at[pair], gy.at[slot, :, tokens // 2 :], load_sem.at[2, slot]
            ),
        )

    for cp in loads(0):
        cp.start()
    sibling = s + 1 - 2 * c
    barrier = pltpu.get_barrier_semaphore()
    for t in range(1, n):
        pl.semaphore_signal(
            barrier, inc=1, device_id={"seq": lax.rem(s + t, n)}, device_id_type=MESH
        )

    def to_sibling(p):
        return pltpu.make_async_remote_copy(
            src_ref=theirs.at[p], dst_ref=sib.at[p], send_sem=to_sib.at[p], recv_sem=sib_in.at[p],
            device_id={"seq": sibling}, device_id_type=MESH,
        )

    def rightward(p, target):
        return pltpu.make_async_remote_copy(
            src_ref=own.at[p], dst_ref=from_left.at[p], send_sem=to_right.at[p], recv_sem=right_in.at[p],
            device_id={"seq": target}, device_id_type=MESH,
        )

    def leftward(p, target):
        return pltpu.make_async_remote_copy(
            src_ref=own.at[p], dst_ref=from_right.at[p], send_sem=to_left.at[p], recv_sem=left_in.at[p],
            device_id={"seq": target}, device_id_type=MESH,
        )

    def down_out(p):
        return pltpu.make_async_copy(
            down.at[lax.rem(p, 2)], down_hbm.at[pl.ds(2 * p, 2)], down_sem.at[lax.rem(p, 2)]
        )

    def pass_on(p):
        to_sibling(p).wait_recv()

        @pl.when(p > q)
        def _():
            @pl.when(q > 0)
            def _():
                rightward(p, s).wait_recv()
                own[p] = (own[p].astype(f32) + sib[p].astype(f32) + from_left[p].astype(f32)).astype(low)

            @pl.when(q == 0)
            def _():
                own[p] = (own[p].astype(f32) + sib[p].astype(f32)).astype(low)

            rightward(p, s + 2).start()

        @pl.when(p < q)
        def _():
            @pl.when(q < nc - 1)
            def _():
                leftward(p, s).wait_recv()
                own[p] = (own[p].astype(f32) + sib[p].astype(f32) + from_right[p].astype(f32)).astype(low)

            @pl.when(q == nc - 1)
            def _():
                own[p] = (own[p].astype(f32) + sib[p].astype(f32)).astype(low)

            leftward(p, s - 2).start()

    def starts_flow(p):
        return ((p > q) & (q == 0)) | ((p < q) & (q == nc - 1))

    w = [w_parts.at[g] for g in range(2)]
    width = u_hbm.shape[2]
    weight = lambda g: w[g][...].reshape(width, -1)
    units = wd.shape[0]
    mine = pl.ds(pl.multiple_of(s * units, units), units)
    bd = bd_ref[...].astype(low)
    ad = ad_ref[:, mine].astype(low)
    a = [a_ref[g].astype(low) for g in range(2)]
    b = [b_ref[g, :, mine].astype(low) for g in range(2)]
    m = [m_ref[g : g + 1, mine] for g in range(2)]
    for cp in weights:
        cp.wait()
    for g in range(2):
        norm, cr = column_norms(weight(g), a[g], b[g].astype(f32), dot_f32(a[g], weight(g)))
        norm_ref[g] = norm
        cross[g] = cr
        ratio[g] = m[g] / norm
    for ref in (ga_ref, gb_ref, gm_ref, gad_ref, gbd_ref, gmd_ref):
        ref[...] = jnp.zeros_like(ref)
    bd_wide = bd.astype(f32)
    gram_b = jnp.dot(gram_ref[...], bd_wide, precision=highest, preferred_element_type=f32)
    squares = jnp.sum(sq_ref[...], axis=0) + SCALE * SCALE * jnp.sum(
        bd_wide * gram_b, axis=0, keepdims=True
    )
    nd_ref[...] = jnp.sqrt(squares + 1e-06)
    ratio_d = md_ref[...] / nd_ref[...]
    pl.semaphore_wait(barrier, n - 1)

    def step(i, carry):
        p = by_distance(nc - 1 - i, q, nc)
        slot = lax.rem(i, 2)
        for cp in loads(i):
            cp.wait()

        @pl.when(i + 1 < nc)
        def _():
            for cp in loads(i + 1):
                cp.start()

        x = u[slot].reshape(2 * tokens, -1)
        upstream = gy[slot].reshape(2 * tokens, -1).astype(f32)
        gb_d = (upstream * ratio_d).astype(low)
        gi_d = (SCALE * dot_nt(gb_d, bd)).astype(low)
        gh = dot_nt(gb_d, wd[...]) + dot_f32(gi_d, ad)
        inner = [dot_nt(x, a[g]).astype(low) for g in range(2)]
        before = [dot_f32(x, weight(g)) + SCALE * dot_f32(inner[g], b[g]) for g in range(2)]
        gate = before[0] * ratio[0]
        lift = before[1] * ratio[1]
        sig = 1.0 / (1.0 + jnp.exp(-gate))
        silu = gate * sig
        hidden = (silu * lift).astype(low)
        grads = [gh * lift * sig * (1.0 + gate * (1.0 - sig)), gh * silu]
        gb = [(grads[g] * ratio[g]).astype(low) for g in range(2)]
        gi = [(SCALE * dot_nt(gb[g], b[g])).astype(low) for g in range(2)]
        back = dot_nt(gb[0], weight(0)) + dot_nt(gb[1], weight(1)) + dot_f32(gi[0], a[0]) + dot_f32(gi[1], a[1])
        back = back.astype(low).reshape(2, tokens, -1)
        first, second = back[0], back[1]

        @pl.when(c == 0)
        def _():
            own[p] = first
            theirs[p] = second

        @pl.when(c == 1)
        def _():
            own[p] = second
            theirs[p] = first

        to_sibling(p).start()
        inner_d = dot_nt(hidden, ad).astype(low)
        part = dot_f32(hidden, wd[...]) + SCALE * dot_f32(inner_d, bd)

        @pl.when(i >= 2)
        def _():
            down_out(slot).wait()

        down[slot] = part.astype(low).reshape(2, tokens, -1)
        pltpu.make_async_copy(down.at[slot], down_hbm.at[pl.ds(2 * p, 2)], down_sem.at[slot]).start()
        gmd_ref[...] += jnp.sum(upstream * part, axis=0, keepdims=True)
        gad_ref[...] += dot_tn(gi_d, hidden)
        gbd_ref[...] += SCALE * dot_tn(inner_d, gb_d)
        for g in range(2):
            gm_ref[g] += jnp.sum(grads[g] * before[g], axis=0, keepdims=True)
            ga_ref[g] += dot_tn(gi[g], x)
            gb_ref[g] += SCALE * dot_tn(inner[g], gb[g])

        pl.when(starts_flow(p))(lambda: pass_on(p))
        last = by_distance(nc - i, q, nc)
        pl.when((i > 0) & jnp.logical_not(starts_flow(last)))(lambda: pass_on(last))
        return carry

    lax.fori_loop(0, nc, step, 0)

    gmd_ref[...] = gmd_ref[...] / nd_ref[...]

    def small(t, slot):
        return pltpu.make_async_remote_copy(
            src_ref=gmd_ref,
            dst_ref=gm_all.at[slot],
            send_sem=small_out.at[t],
            recv_sem=small_in.at[t],
            device_id={"seq": lax.rem(s + t, n)},
            device_id_type=MESH,
        )

    for t in range(1, n):
        small(t, s).start()
    for g in range(2):
        norm = norm_ref[g]
        gm = gm_ref[g] / norm
        gm_ref[g] = gm
        col = -gm * m[g] / (norm * norm)
        b_wide = b[g].astype(f32)
        weighted = b_wide * col
        tail = lax.dot_general(
            weighted, b_wide, last_last, precision=highest, preferred_element_type=f32
        )
        spread = dot_nt(weighted.astype(low), weight(g)) + SCALE * jnp.dot(
            tail, a[g].astype(f32), precision=highest, preferred_element_type=f32
        )
        ga_ref[g] += SCALE * spread
        gb_ref[g] += SCALE * col * cross[g]

    gm_line = gmd_ref[...]
    for t in range(1, n):
        slot = lax.rem(s - t + n, n)
        small(t, slot).wait_recv()
        gm_line = gm_line + gm_all[slot]
    col = -gm_line * md_ref[...] / (nd_ref[...] * nd_ref[...])
    weighted = bd_wide * col
    tail = lax.dot_general(
        weighted, bd_wide, last_last, precision=highest, preferred_element_type=f32
    )
    gad_ref[...] += SCALE * (
        dot_nt(weighted.astype(low), wd[...])
        + SCALE * jnp.dot(tail, ad.astype(f32), precision=highest, preferred_element_type=f32)
    )
    own_gram = jnp.where(s == 0, SCALE, 0.0) * gram_b
    gbd_ref[...] += SCALE * col * (dot_f32(ad, wd[...]) + own_gram)

    to_sibling(q).wait_recv()
    in_ref[...] = own[q].astype(f32) + sib[q].astype(f32)

    @pl.when(q > 0)
    def _():
        rightward(q, s).wait_recv()
        in_ref[...] += from_left[q].astype(f32)

    @pl.when(q < nc - 1)
    def _():
        leftward(q, s).wait_recv()
        in_ref[...] += from_right[q].astype(f32)

    for i in range(min(2, nc)):
        pltpu.make_async_copy(down.at[i], down_hbm.at[pl.ds(0, 2)], down_sem.at[i]).wait()
    for t in range(1, n):
        small(t, s).wait_send()
    for p in range(nc):
        to_sibling(p).wait_send()
        pl.when(p > q)(lambda p=p: rightward(p, s).wait_send())
        pl.when(p < q)(lambda p=p: leftward(p, s).wait_send())


def share_plan(rows):
    turns = range(1, rows // 2)
    first = [(0, 0, k) for k in turns] + [(0, 1, 0)]
    second = [(0, 0, 0)] + [(0, 1, k) for k in turns]
    second += [(k, None, 0) for k in turns] + [(rows // 2, None, k) for k in turns]
    return first, second


def place_pieces(n, rows, pieces, w_parts):
    nc, half = n // 2, rows // 2
    _, q, _ = place_in_seq()
    r, b_row, a_row, diagonal = place_in_rows(rows)
    own, near = pieces[:2]
    turns = range(1, half)
    held = [(own.at[g], g, r) for g in range(2)]
    kinds = [(0, a_row(-k)) for k in turns] + [(1, b_row)]
    kinds += [(0, b_row)] + [(1, a_row(-k)) for k in turns]
    kinds += [(0, diagonal(-k)) for k in turns] + [(1, diagonal(-k)) for k in turns]
    held += [(piece, g, hold) for piece, (g, hold) in zip(pieces[2:], kinds)]
    out = [(near, w_parts.at[:, pl.ds(2 * q, 2)])]
    for i in range(1, nc):
        pair = pl.ds(2 * near_first(i, q, nc), 2)
        out += [(src.at[pair], w_parts.at[g, pair, hold]) for src, g, hold in held]
    return out


def feed_forward(n, rows, pieces, u, gy0, gy1, wd, a, b, m, ad, bd, md, sq, gram, collective_id):
    nc = n // 2
    _, tokens, width = u.shape
    units = wd.shape[0]
    f32, low = jnp.float32, jnp.bfloat16
    shape = jax.ShapeDtypeStruct
    vmem = pl.BlockSpec(memory_space=pltpu.VMEM)
    hbm = pl.BlockSpec(memory_space=pl.ANY)
    dma = pltpu.SemaphoreType.DMA
    line = pltpu.VMEM((nc, tokens, width), low)
    pair = pltpu.VMEM((2, 2, tokens, width), low)
    part = pieces[0].shape[2]
    copies = 2 + (n // 2 - 1) * (2 + 2 * rows - 2)
    count = len(pieces)

    def kernel(*refs):
        ffn_kernel(n, rows, refs[:count], *refs[count:])

    return pl.pallas_call(
        kernel,
        out_shape=(
            shape((tokens, width), f32),
            shape((n, tokens, width), low),
            shape((2, 16, width), f32),
            shape((2, 16, units), f32),
            shape((2, 1, units), f32),
            shape((2, 1, units), f32),
            shape((16, units), f32),
            shape((16, width), f32),
            shape((1, width), f32),
            shape((1, width), f32),
        ),
        in_specs=[hbm] * (count + 4) + [vmem] * 8,
        out_specs=(vmem, hbm) + (vmem,) * 8,
        scratch_shapes=[
            pltpu.VMEM((2, n, rows, part, units), low),
            pltpu.VMEM((units, width), low),
            pair, pair, pair,
            line, line, line, line, line,
            pltpu.VMEM((2, 1, units), f32),
            pltpu.VMEM((2, 16, units), f32),
            pltpu.VMEM((n, 1, width), f32),
            dma((copies,)), dma((3, 2)), dma((2,)), dma((n,)), dma((n,)),
        ] + [dma((nc,))] * 6,
        compiler_params=pltpu.CompilerParams(
            collective_id=collective_id, has_side_effects=True, vmem_limit_bytes=60 << 20
        ),
        cost_estimate=pl.CostEstimate(
            flops=12 * n * tokens * width * units, transcendentals=n * tokens * units,
            bytes_accessed=32 << 20,
        ),
        name="feed_forward",
    )(*pieces, u, gy0, gy1, wd, a, b, m, ad, bd, md, sq, gram)

def reduce_kernel(n, rows, ga_qkv, ga_o, gb_qkv, gb_o, ga_gu, gb_d, gm_qkv, gm_o, gm_d, gb_gu, gm_gu, n_gu, ga_d,
                  whole, units_all, part, from_sib, mid, from_rows, from_line, line_out, units, units_in,
                  sib_out, sib_in, row_out, row_in, line_send, line_in, back_send, back_in, wide_send, wide_in,
                  pass_send, pass_in):
    nc = n // 2
    f32, low = jnp.float32, jnp.bfloat16
    s, q, c = place_in_seq()
    sibling = s + 1 - 2 * c
    r = lax.axis_index("rows")
    width = ga_o.shape[1]
    cols = width // (2 * rows)
    kv = (gb_qkv.shape[1] - width) // 2
    height = part.shape[2]
    piece = height // nc
    unit_rows = units.shape[1]
    size = units.shape[2]

    barrier = pltpu.get_barrier_semaphore()
    for t in range(1, n):
        pl.semaphore_signal(barrier, inc=1, device_id=(r, lax.rem(s + t, n)), device_id_type=MESH)
    for t in range(1, rows):
        pl.semaphore_signal(barrier, inc=1, device_id=(lax.rem(r + t, rows), s), device_id_type=MESH)

    gb_k, gb_v = gb_qkv[:, width : width + kv], gb_qkv[:, width + kv :]
    small = jnp.concatenate(
        [
            jnp.concatenate([gb_k[:8], gb_k[8:], gb_v[:8], gb_v[8:]], axis=1),
            gm_qkv[:, :width],
            gm_o[...],
            gm_d[...],
            jnp.concatenate([gm_qkv[:, width:], jnp.zeros((1, width - 2 * kv), f32)], axis=1),
            jnp.zeros((4, width), f32),
        ],
        axis=0,
    )
    groups = [ga_qkv[0], ga_qkv[1], ga_qkv[2], ga_o[...], gb_qkv[:, :width], gb_o[...], ga_gu[0], ga_gu[1], gb_d[...], small]
    for j in range(2 * rows):
        for g, value in enumerate(groups):
            part[j % 2, j // 2, 16 * g : 16 * g + 16] = value[:, cols * j : cols * (j + 1)].astype(low)
        if height > 160:
            part[j % 2, j // 2, 160:] = jnp.zeros((height - 160, cols), low)
    n_high = [n_gu[g].astype(low).astype(f32) for g in range(2)]
    n_rest = [n_gu[g] - n_high[g] for g in range(2)]
    tops = jnp.concatenate(
        [gm_gu[0], gm_gu[1]]
        + [v * (1.0 / rows) for v in (n_high[0], n_rest[0], n_high[1], n_rest[1])]
        + [jnp.zeros((2, size), f32)],
        axis=0,
    )
    blocks = [gb_gu[0][:8], gb_gu[0][8:], gb_gu[1][:8], gb_gu[1][8:], ga_d[:8], ga_d[8:], tops, jnp.zeros((8, size), f32)]
    per = unit_rows // 8
    for j in range(rows):
        units[j] = jnp.concatenate(blocks[per * j : per * (j + 1)], axis=0).astype(low)
    pl.semaphore_wait(barrier, n - 1 + rows - 1)

    def to_sibling():
        return remote(part.at[1 - c], from_sib, sib_out.at[0], sib_in.at[0], r, sibling)

    def member(t):
        return lax.rem(r + t + rows, rows)

    def row_send(t):
        return remote(mid.at[member(t)], from_rows.at[t], row_out.at[0, t], row_in.at[0, t], member(t), s)

    def unit_send(t):
        return remote(units.at[member(t)], units_in.at[t], row_out.at[1, t], row_in.at[1, t], member(t), s)

    def chip(t):
        return lax.rem(q + t + nc, nc)

    def line_part(t):
        return remote(line_out.at[chip(t)], from_line.at[t], line_send.at[t], line_in.at[t], r, 2 * chip(t) + c)

    def back(t, slot):
        return remote(whole.at[r, c, slot], whole.at[r, c, slot], back_send.at[0, t], back_in.at[0, t], r, 2 * chip(t) + c)

    def unit_back(t, slot):
        return remote(
            units_all.at[r, c, slot], units_all.at[r, c, slot], back_send.at[1, t], back_in.at[1, t], r, 2 * chip(t) + c
        )

    def wide(t, row):
        return remote(whole.at[row, c], whole.at[row, c], wide_send.at[0, t], wide_in.at[0, t], member(t), s)

    def unit_wide(t, row):
        return remote(units_all.at[row, c], units_all.at[row, c], wide_send.at[1, t], wide_in.at[1, t], member(t), s)

    def hand(t, row, core):
        return remote(whole.at[row, core], whole.at[row, core], pass_send.at[0, t], pass_in.at[0, t], r, sibling)

    def unit_hand(t, row, core):
        return remote(units_all.at[row, core], units_all.at[row, core], pass_send.at[1, t], pass_in.at[1, t], r, sibling)

    to_sibling().start()
    for t in range(1, rows):
        unit_send(t).start()
    to_sibling().wait_recv()
    for t in range(rows):
        mid[member(t)] = (part[c, member(t)].astype(f32) + from_sib[member(t)].astype(f32)).astype(low)
        if t:
            row_send(t).start()
    unit_sum = units[r].astype(f32)
    for t in range(1, rows):
        unit_send(t).wait_recv()
        unit_sum = unit_sum + units_in[t].astype(f32)
    units_all[r, c, q] = unit_sum.astype(low)
    for t in range(1, nc):
        unit_back(t, q).start()
    total = mid[r].astype(f32)
    for t in range(1, rows):
        row_send(t).wait_recv()
        total = total + from_rows[t].astype(f32)
    for p in range(nc):
        line_out[p] = total[piece * p : piece * (p + 1)].astype(low)
    for t in range(1, nc):
        line_part(t).start()
    own = line_out[q].astype(f32)
    for t in range(1, nc):
        line_part(t).wait_recv()
        own = own + from_line[t].astype(f32)
    whole[r, c, q] = own.astype(low)
    for t in range(1, nc):
        back(t, q).start()
    for t in range(1, nc):
        back(t, chip(-t)).wait_recv()
        unit_back(t, chip(-t)).wait_recv()
    for t in range(1, rows):
        wide(t, r).start()
        unit_wide(t, r).start()
    hand(0, r, c).start()
    unit_hand(0, r, c).start()
    for t in range(1, rows):
        wide(t, member(-t)).wait_recv()
        hand(t, member(-t), c).start()
        unit_wide(t, member(-t)).wait_recv()
        unit_hand(t, member(-t), c).start()
    for t in range(rows):
        hand(t, member(-t), 1 - c).wait_recv()
        unit_hand(t, member(-t), 1 - c).wait_recv()

    to_sibling().wait_send()
    for t in range(1, rows):
        row_send(t).wait_send()
        unit_send(t).wait_send()
        wide(t, r).wait_send()
        unit_wide(t, r).wait_send()
    for t in range(1, nc):
        line_part(t).wait_send()
        back(t, q).wait_send()
        unit_back(t, q).wait_send()
    for t in range(rows):
        hand(t, member(-t), c).wait_send()
        unit_hand(t, member(-t), c).wait_send()


def sum_gradients(n, rows, full, own_units, collective_id):
    nc = n // 2
    width, size = full[1].shape[1], own_units[3].shape[1]
    cols = width // (2 * rows)
    height = -(-160 // (8 * nc)) * 8 * nc
    unit_rows = 64 // rows
    low = jnp.bfloat16
    vmem = pl.BlockSpec(memory_space=pltpu.VMEM)
    dma = pltpu.SemaphoreType.DMA
    block = (rows, height, cols)
    return pl.pallas_call(
        functools.partial(reduce_kernel, n, rows),
        out_shape=(
            jax.ShapeDtypeStruct((rows, 2, nc, height // nc, cols), low),
            jax.ShapeDtypeStruct((rows, 2, nc, unit_rows, size), low),
        ),
        in_specs=[vmem] * 13,
        out_specs=(vmem,) * 2,
        scratch_shapes=[
            pltpu.VMEM((2, *block), low),
            pltpu.VMEM(block, low),
            pltpu.VMEM(block, low),
            pltpu.VMEM(block, low),
            pltpu.VMEM((nc, height // nc, cols), low),
            pltpu.VMEM((nc, height // nc, cols), low),
            pltpu.VMEM((rows, unit_rows, size), low),
            pltpu.VMEM((rows, unit_rows, size), low),
            dma((1,)), dma((1,)), dma((2, rows)), dma((2, rows)), dma((nc,)), dma((nc,)),
            dma((2, nc)), dma((2, nc)), dma((2, rows)), dma((2, rows)), dma((2, rows)), dma((2, rows)),
        ],
        compiler_params=pltpu.CompilerParams(
            collective_id=collective_id, has_side_effects=True, vmem_limit_bytes=48 << 20
        ),
        cost_estimate=pl.CostEstimate(flops=0, transcendentals=0, bytes_accessed=64 << 20),
        name="sum_gradients",
    )(*full, *own_units)


def finish_kernel(n, rows, whole, units_all, x1, before, m_attn, n_attn, m_d, n_d, m_gu,
                  o_out, o_ga, o_gb_qo, o_gb_kv, o_gm_q, o_gm_kv, o_gm_o, o_ga_gu, o_gb_gu, o_gm_gu, o_ga_d, o_gb_d,
                  o_gm_d, o_stats, n_gu):
    f32 = jnp.float32
    nc = n // 2
    width = o_gb_d.shape[1]
    kv = o_gb_kv.shape[2]
    cols = width // (2 * rows)
    size = units_all.shape[4]
    per = units_all.shape[3] // 8
    o_out[...] = (x1[...] + before[...].astype(f32) * (m_d[...] / n_d[...])).astype(o_out.dtype)
    for j in range(2 * rows):
        block = jnp.concatenate([whole[j // 2, j % 2, p].astype(f32) for p in range(nc)], axis=0)
        at = slice(cols * j, cols * (j + 1))
        for g in range(4):
            o_ga[g, :, at] = block[16 * g : 16 * g + 16]
        o_gb_qo[0, :, at] = block[64:80]
        o_gb_qo[1, :, at] = block[80:96]
        o_ga_gu[0, :, at] = block[96:112]
        o_ga_gu[1, :, at] = block[112:128]
        o_gb_d[:, at] = block[128:144]
        which, start = divmod(cols * j, kv)
        o_gb_kv[which // 2, 8 * (which % 2) : 8 * (which % 2) + 8, start : start + cols] = block[144:152]
        o_gm_q[at] = block[152]
        o_gm_o[at] = block[153]
        o_gm_d[at] = block[154]
        if which < 2:
            o_gm_kv[which : which + 1, start : start + cols] = block[155:156]
    for j in range(rows):
        for dev in range(n):
            block = units_all[j, dev % 2, dev // 2].astype(f32)
            at = slice(size * dev, size * (dev + 1))
            for t in range(per):
                rows8, place = block[8 * t : 8 * t + 8], per * j + t
                half = slice(8 * (place % 2), 8 * (place % 2) + 8)
                if place < 4:
                    o_gb_gu[place // 2, half, at] = rows8
                elif place < 6:
                    o_ga_d[half, at] = rows8
                elif place == 6:
                    o_gm_gu[:, at] = rows8[:2]
                    n_gu[0:1, at] = rows8[2:3] + rows8[3:4]
                    n_gu[1:2, at] = rows8[4:5] + rows8[5:6]


    row = lax.broadcasted_iota(jnp.int32, o_stats.shape, 0)
    col = lax.broadcasted_iota(jnp.int32, o_stats.shape, 1)
    bounds = [(0, width), (width, width + kv), (width + kv, width + 2 * kv), (width + 2 * kv, 2 * width + 2 * kv)]
    both = [(m_attn[:, i:j], n_attn[:, i:j]) for i, j in bounds]
    both += [(m_gu[g : g + 1, :], n_gu[g : g + 1, :]) for g in range(2)] + [(m_d[...], n_d[...])]
    stats = jnp.zeros(o_stats.shape, f32)
    for p, (m, norm) in enumerate(both):
        drift = jnp.mean(jnp.square(m - norm), axis=1, keepdims=True)
        drift = jnp.sqrt(drift) / jnp.sqrt(jnp.mean(jnp.square(m), axis=1, keepdims=True) + 1e-06)
        stats = jnp.where((row == p) & (col == 0), drift, stats)
        stats = jnp.where((row == p) & (col == 1), jnp.mean(norm, axis=1, keepdims=True), stats)
    o_stats[...] = stats


def finish(n, rows, sums, x1, before, m_attn, n_attn, m_d, n_d, m_gu):
    tokens, width = x1.shape
    kv = (m_attn.shape[1] - 2 * width) // 2
    units = m_gu.shape[1]
    shape = lambda *dims: pltpu.HBM(dims, jnp.float32)
    vmem = pl.BlockSpec(memory_space=pltpu.VMEM)
    return pl.pallas_call(
        functools.partial(finish_kernel, n, rows),
        out_shape=(
            pltpu.HBM((tokens, width), jnp.bfloat16), shape(4, 16, width), shape(2, 16, width), shape(2, 16, kv),
            shape(width), shape(2, kv), shape(width), shape(2, 16, width), shape(2, 16, units), shape(2, units),
            shape(16, units), shape(16, width), shape(width), shape(7, 2),
        ),
        in_specs=[vmem] * 2 + [pl.BlockSpec()] * 7,
        scratch_shapes=[pltpu.VMEM((2, units), jnp.float32)],
        compiler_params=pltpu.CompilerParams(vmem_limit_bytes=40 << 20),
        cost_estimate=pl.CostEstimate(flops=0, transcendentals=0, bytes_accessed=8 << 20),
        name="finish",
    )(*sums, x1, before, m_attn, n_attn, m_d, n_d, m_gu)

def local(
    layer_input,
    output_gradient,
    norm_gain_vectors,
    query_output_frozen,
    key_value_frozen,
    gate_up_frozen,
    down_frozen_weight,
    attention_adapter_a,
    query_output_adapter_b,
    key_value_adapter_b,
    query_magnitude,
    key_value_magnitude,
    output_magnitude,
    gate_up_adapter_a,
    gate_up_adapter_b,
    gate_up_magnitude,
    down_adapter_a,
    down_adapter_b,
    down_magnitude,
    prompt_length_list,
    response_length_list,
):
    pair_rows, span_len, model_width = layer_input.shape
    token_count = pair_rows * span_len
    kv_width = KV_HEADS * HEAD_DIM
    seq_size = lax.axis_size("seq")
    rows_size = lax.axis_size("rows")
    seq_index = lax.axis_index("seq")
    f32 = jnp.float32

    packed = jnp.stack(
        [
            jnp.concatenate([query_output_frozen[0], key_value_frozen[0]], axis=1),
            jnp.concatenate([key_value_frozen[1], query_output_frozen[1]], axis=1),
        ]
    )
    weights, gu_own, gu_near, sq_d, gram_d = gather_weights(
        seq_size, rows_size, packed, gate_up_frozen, down_frozen_weight, down_adapter_a,
        down_adapter_b, 1,
    )
    shares_1, shares_2 = share_plan(rows_size)
    grad_out_rows = output_gradient.reshape(token_count, model_width)
    half_0, half_1 = jnp.split(grad_out_rows, 2)
    weights, half_0 = lax.optimization_barrier((weights, half_0))
    gy_0 = lax.all_gather(half_0, "seq", axis=0, tiled=False)

    b_attn = jnp.concatenate(
        [
            query_output_adapter_b[0],
            key_value_adapter_b[0],
            key_value_adapter_b[1],
            query_output_adapter_b[1],
        ],
        axis=1,
    )
    m_attn = jnp.concatenate(
        [query_magnitude, key_value_magnitude[0], key_value_magnitude[1], output_magnitude]
    )[None]
    m_d = down_magnitude[None]

    positions = seq_index * span_len + jnp.arange(span_len, dtype=jnp.int32)
    half_dim = HEAD_DIM // 2
    frequency = 500000.0 ** (-(jnp.arange(half_dim, dtype=f32) * 2.0) / HEAD_DIM)
    angles = positions.astype(f32)[:, None] * frequency[None, :]
    cosine = jnp.tile(jnp.cos(angles), (pair_rows, 4))
    sine = jnp.tile(jnp.sin(angles), (pair_rows, 4))
    valid_len = prompt_length_list[0] + response_length_list

    x = layer_input.reshape(token_count, model_width)
    gain_attn, gain_ffn = norm_gain_vectors[:1], norm_gain_vectors[1:]
    u1, before_qkv, q, kv, n_attn, cross_attn = project_qkv(
        x, gain_attn, attention_adapter_a, weights, b_attn, m_attn, cosine, sine
    )
    (kv_all, sq_all), gu_1 = gather_seq(
        seq_size, rows_size, [kv, sq_d], 2, (gu_own,), shares_1
    )
    kv_all, half_1 = lax.optimization_barrier((kv_all, half_1))
    gy_1 = lax.all_gather(half_1, "seq", axis=0, tiled=False)
    kv_all = kv_all.reshape(seq_size, pair_rows, span_len, 2 * kv_width)
    q = q.reshape(pair_rows, span_len, model_width)
    att, shares = attend(q, kv_all, valid_len)
    att = att.reshape(token_count, model_width)
    before_o, x1, u2 = project_out(
        att, attention_adapter_a, weights, b_attn, m_attn, n_attn, x, gain_ffn
    )

    (u2_all,), gu_2 = gather_seq(
        seq_size, rows_size, [u2], 3, (gu_own, *gu_1), shares_2
    )
    in_grad, down_parts, ga_gu, gb_gu, gm_gu, n_gu, ga_d, gb_d, gm_d, n_d = feed_forward(
        seq_size, rows_size, (gu_own, gu_near, *gu_1, *gu_2), u2_all, gy_0, gy_1,
        down_frozen_weight, gate_up_adapter_a, gate_up_adapter_b, gate_up_magnitude, down_adapter_a,
        down_adapter_b, m_d, sq_all, gram_d, 4,
    )
    before_d = lax.psum_scatter(
        down_parts.reshape(seq_size * token_count, model_width), "seq", scatter_dimension=0,
        tiled=True,
    )

    gx1, grad_att, ga_o, gb_o, gm_o = out_back(
        in_grad, x1, gain_ffn, grad_out_rows, before_o, att, attention_adapter_a, b_attn, m_attn,
        n_attn, cross_attn, weights,
    )
    gq, gkv = attend_back(q, kv_all, shares, grad_att.reshape(q.shape))
    gkv = scatter_seq(seq_size, gkv.reshape(seq_size, token_count, 2 * kv_width), 5)
    grad_inputs, ga_qkv, gb_qkv, gm_qkv = qkv_back(
        gq.reshape(token_count, model_width), gkv, cosine, sine, before_qkv, u1,
        attention_adapter_a, b_attn, m_attn, n_attn, cross_attn, x, gain_attn, gx1, weights,
    )

    sums = sum_gradients(
        seq_size, rows_size,
        (ga_qkv, ga_o, gb_qkv, gb_o, ga_gu, gb_d, gm_qkv, gm_o, gm_d),
        (gb_gu, gm_gu, n_gu, ga_d),
        6,
    )
    layer_result, *summed, stats = finish(
        seq_size, rows_size, sums, x1, before_d, m_attn, n_attn, m_d, n_d, gate_up_magnitude
    )
    shape = (pair_rows, span_len, model_width)
    return (layer_result.reshape(shape), grad_inputs.reshape(shape), *summed, stats)

def solution(mesh):
    return jax.shard_map(
        local,
        mesh=mesh,
        in_specs=(
            P("rows", "seq", None),
            P("rows", "seq", None),
            P(),
            P(None, "seq", None),
            P(None, "seq", None),
            P(None, "seq", None),
            P("seq", None),
            P(),
            P(),
            P(),
            P(),
            P(),
            P(),
            P(),
            P(),
            P(),
            P(),
            P(),
            P(),
            P("rows"),
            P("rows"),
        ),
        out_specs=(
            P("rows", "seq", None),
            P("rows", "seq", None),
            P(),
            P(),
            P(),
            P(),
            P(),
            P(),
            P(),
            P(),
            P(),
            P(),
            P(),
            P(),
            P(),
        ),
        check_vma=False,
    )
```

```python
import functools

import jax
import jax.numpy as jnp
from jax import lax
from jax.experimental import pallas as pl
from jax.experimental.pallas import tpu as pltpu
from jax.sharding import PartitionSpec as P

HEADS = 32
KV_HEADS = 8
HEAD_DIM = 64
ADAPTER_RANK = 16
ALPHA = 32
SCALE = ALPHA / ADAPTER_RANK
TILE = 512

highest = lax.Precision.HIGHEST
last_last = (((1,), (1,)), ((), ()))
first_first = (((0,), (0,)), ((), ()))

def dot_f32(a, b):
    return jnp.dot(a, b, preferred_element_type=jnp.float32)


def dot_nt(a, b):
    return lax.dot_general(a, b, last_last, preferred_element_type=jnp.float32)


def dot_tn(a, b):
    return lax.dot_general(a, b, first_first, preferred_element_type=jnp.float32)


def unit_rms(v):
    return lax.rsqrt(jnp.mean(v * v, axis=-1, keepdims=True) + 1e-05)


def rms_back(v, gain, upstream):
    r = unit_rms(v)
    scaled = gain * upstream
    return r * scaled - v * (r * r * r) * jnp.mean(scaled * v, axis=-1, keepdims=True)


def turn(z, cosine, sine):
    width = z.shape[1]
    lane = lax.broadcasted_iota(jnp.int32, z.shape, 1)
    half = HEAD_DIM // 2
    other = jnp.where(
        lax.rem(lane, HEAD_DIM) < half, -pltpu.roll(z, width - half, 1), pltpu.roll(z, half, 1)
    )
    copies = width // cosine.shape[1]
    return z * jnp.tile(cosine, (1, copies)) + other * jnp.tile(sine, (1, copies))


def column_squares(w):
    return jnp.sum(jnp.square(w.astype(jnp.float32)), axis=0, keepdims=True)


def two_terms(value):
    high = value.astype(jnp.bfloat16)
    return jnp.concatenate([high, (value - high.astype(jnp.float32)).astype(jnp.bfloat16)], axis=0)


def dot_two(terms, b):
    both = dot_f32(terms, b)
    half = both.shape[0] // 2
    return both[:half] + both[half:]


def column_norms(w, gram, b, cross):
    b_wide = b.astype(jnp.float32)
    gram_b = dot_two(gram, b)
    squares = column_squares(w) + 2.0 * SCALE * jnp.sum(b_wide * cross, axis=0, keepdims=True)
    squares = squares + SCALE * SCALE * jnp.sum(b_wide * gram_b, axis=0, keepdims=True)
    return jnp.sqrt(squares + 1e-06), cross + SCALE * gram_b


def project_kernel(kv_tiles, u_ref, inner_ref, gram_ref, a_ref, w_ref, b_ref, m_ref, cos_ref, sin_ref,
                   before_ref, q_ref, kv_ref, n_ref, cross_ref):
    j = pl.program_id(0)
    q_tiles, last = kv_tiles
    a = a_ref[0].astype(jnp.bfloat16)
    b = b_ref[...].astype(jnp.bfloat16)
    w = w_ref[0]
    rows = u_ref.shape[0]

    @pl.when(j <= last)
    def _():
        both = dot_f32(jnp.concatenate([u_ref[...], a], axis=0), w)
        norm, cross = column_norms(w, gram_ref[0], b, both[rows:])
        n_ref[...] = norm
        cross_ref[...] = cross
        before = both[:rows] + SCALE * dot_f32(inner_ref[0], b)
        before_ref[...] = before
        y = before * (m_ref[...] / norm)

        @pl.when(j < q_tiles)
        def _():
            q_ref[...] = turn(y, cos_ref[...], sin_ref[...]).astype(jnp.bfloat16)

        @pl.when(j == q_tiles)
        def _():
            kv_ref[...] = turn(y, cos_ref[...], sin_ref[...]).astype(jnp.bfloat16)

        @pl.when(j > q_tiles)
        def _():
            kv_ref[...] = y.astype(jnp.bfloat16)

    @pl.when(j > last)
    def _():
        norm, cross = column_norms(w, gram_ref[0], b, dot_f32(a, w))
        n_ref[...] = norm
        cross_ref[...] = cross


def project_qkv(u, inner, grams, a, weights, b, m, cosine, sine):
    rows, width = u.shape
    cols = b.shape[1]
    per_half = weights.shape[2] // TILE
    q_tiles = width // TILE
    k_cols = weights.shape[2] - width
    last = q_tiles + 2 * k_cols // TILE - 1
    full = lambda shape: pl.BlockSpec(shape, lambda j: (0,) * len(shape))
    col = lambda height: pl.BlockSpec((height, TILE), lambda j: (0, j))
    which = lambda j: jnp.where(j < q_tiles, 0, jnp.where(j > last, 3, 1 + j - q_tiles))
    f32, low = jnp.float32, jnp.bfloat16
    return pl.pallas_call(
        functools.partial(project_kernel, (q_tiles, last)),
        out_shape=(
            pltpu.HBM((rows, width + 2 * k_cols), f32),
            pltpu.HBM((rows, width), low),
            pltpu.HBM((rows, 2 * k_cols), low),
            pltpu.HBM((1, cols), f32),
            pltpu.HBM((16, cols), f32),
        ),
        grid=(cols // TILE,),
        in_specs=[
            full((rows, width)),
            pl.BlockSpec((1, rows, 16), lambda j: (jnp.minimum(which(j), 2), 0, 0)),
            pl.BlockSpec((1, 32, 16), lambda j: (which(j), 0, 0)),
            pl.BlockSpec((1, 16, width), lambda j: (which(j), 0, 0)),
            pl.BlockSpec((1, width, TILE), lambda j: (j // per_half, 0, j % per_half)),
            col(16),
            col(1),
            full(cosine.shape),
            full(sine.shape),
        ],
        out_specs=(
            pl.BlockSpec((rows, TILE), lambda j: (0, jnp.minimum(j, last))),
            pl.BlockSpec((rows, TILE), lambda j: (0, jnp.minimum(j, q_tiles - 1))),
            pl.BlockSpec((rows, TILE), lambda j: (0, jnp.clip(j - q_tiles, 0, last - q_tiles))),
            col(1),
            col(16),
        ),
        compiler_params=pltpu.CompilerParams(vmem_limit_bytes=40 << 20),
        cost_estimate=pl.CostEstimate(
            flops=2 * rows * width * cols, transcendentals=0, bytes_accessed=2 * width * cols
        ),
        name="project_qkv",
    )(u, inner, grams, a, weights, b, m, cosine, sine)


def out_kernel(att_ref, a_ref, w_ref, b_ref, m_ref, n_ref, x_ref, gain_ref, next_ref,
               before_ref, x1_ref, u2_ref, inner_ref):
    t = pl.program_id(0)
    a = a_ref[0].astype(jnp.bfloat16)
    b = b_ref[...].astype(jnp.bfloat16)
    inner = dot_nt(att_ref[...], a).astype(jnp.bfloat16)
    before = dot_f32(att_ref[...], w_ref[0]) + SCALE * dot_f32(inner, b)
    before_ref[...] = before
    x1_ref[:, pl.ds(pl.multiple_of(t * TILE, TILE), TILE)] = (
        x_ref[...].astype(jnp.float32) + before * (m_ref[...] / n_ref[...])
    )

    @pl.when(t == pl.num_programs(0) - 1)
    def _():
        v = x1_ref[...]
        u2 = (v * unit_rms(v) * gain_ref[...]).astype(jnp.bfloat16)
        u2_ref[...] = u2
        following = next_ref[...].reshape(-1, u2.shape[1]).astype(jnp.bfloat16)
        inner_ref[...] = jnp.zeros_like(inner_ref)
        inner_ref[:, : following.shape[0]] = dot_nt(u2, following).astype(jnp.bfloat16)


def project_out(att, a, weights, b, m, norms, x, gain, following):
    rows, width = att.shape
    tiles = width // TILE
    skip = (weights.shape[2] - width) // TILE
    full = lambda shape: pl.BlockSpec(shape, lambda t: (0,) * len(shape))
    col = lambda height: pl.BlockSpec((height, TILE), lambda t: (0, t))
    ahead = b.shape[1] // TILE - tiles
    later = lambda height: pl.BlockSpec((height, TILE), lambda t: (0, ahead + t))
    f32 = jnp.float32
    return pl.pallas_call(
        out_kernel,
        out_shape=(
            pltpu.HBM((rows, width), f32),
            pltpu.HBM((rows, width), f32),
            pltpu.HBM((rows, width), jnp.bfloat16),
            pltpu.HBM((rows, 128), jnp.bfloat16),
        ),
        grid=(tiles,),
        in_specs=[
            full((rows, width)),
            pl.BlockSpec((1, 16, width), lambda t: (3, 0, 0)),
            pl.BlockSpec((1, width, TILE), lambda t: (1, 0, skip + t)),
            later(16),
            later(1),
            later(1),
            col(rows),
            full((1, width)),
            full(following.shape),
        ],
        out_specs=(col(rows), full((rows, width)), full((rows, width)), full((rows, 128))),
        compiler_params=pltpu.CompilerParams(vmem_limit_bytes=40 << 20),
        cost_estimate=pl.CostEstimate(
            flops=2 * rows * width * width, transcendentals=0, bytes_accessed=2 * width * width
        ),
        name="project_out",
    )(att, a, weights, b, m, norms, x, gain, following)


def out_back_kernel(in_ref, x1_ref, gain_ref, gy_ref, before_ref, att_ref, a_ref, b_ref, m_ref, n_ref, cross_ref,
                    w_ref, gx_ref, gatt_ref, ga_ref, gb_ref, gm_ref, lhs, gi, tail):
    t = pl.program_id(0)
    rows, width = gx_ref.shape
    low = jnp.bfloat16
    a = a_ref[0].astype(low)
    o_cols = slice(b_ref.shape[1] - width, b_ref.shape[1])

    @pl.when(t == 0)
    def _():
        gx = gy_ref[...].astype(jnp.float32) + rms_back(x1_ref[...], gain_ref[...], in_ref[...])
        gx_ref[...] = gx
        norm, m = n_ref[:, o_cols], m_ref[:, o_cols]
        gb = (gx * (m / norm)).astype(low)
        lhs[:rows] = gb
        b = b_ref[:, o_cols].astype(low)
        gi[...] = (SCALE * dot_nt(gb, b)).astype(low)
        gm = jnp.sum(gx * before_ref[...], axis=0, keepdims=True) / norm
        gm_ref[...] = gm
        c = -gm * m / (norm * norm)
        weighted = (b.astype(jnp.float32) * c).astype(low)
        lhs[rows:] = weighted
        tail[...] = two_terms(dot_nt(weighted, b))
        inner = dot_nt(att_ref[...], a).astype(low)
        gb_ref[...] = SCALE * dot_tn(inner, gb) + SCALE * c * cross_ref[:, o_cols]

    span = pl.ds(pl.multiple_of(t * TILE, TILE), TILE)
    a_tile = a_ref[0, :, span].astype(low)
    gi_low = gi[...]
    back = dot_nt(lhs[...], w_ref[0, :, w_ref.shape[2] - width :])
    gatt_ref[...] = (back[:rows] + dot_f32(gi_low, a_tile)).astype(low)
    spread = back[rows:] + SCALE * dot_two(tail[...], a_tile)
    ga_ref[...] = dot_tn(gi_low, att_ref[:, span]) + SCALE * spread


def out_back(in_grad, x1, gain, gy, before, att, a, b, m, norms, cross, weights):
    rows, width = x1.shape
    tiles = width // TILE
    full = lambda shape: pl.BlockSpec(shape, lambda t: (0,) * len(shape))
    col = lambda height: pl.BlockSpec((height, TILE), lambda t: (0, t))
    f32, low = jnp.float32, jnp.bfloat16
    wide = full((rows, width))
    return pl.pallas_call(
        out_back_kernel,
        out_shape=(
            pltpu.HBM((rows, width), f32),
            pltpu.HBM((rows, width), low),
            jax.ShapeDtypeStruct((16, width), f32),
            jax.ShapeDtypeStruct((16, width), f32),
            jax.ShapeDtypeStruct((1, width), f32),
        ),
        grid=(tiles,),
        in_specs=[wide, wide, full((1, width)), wide, wide, wide,
                  pl.BlockSpec((1, 16, width), lambda t: (3, 0, 0)),
                  full(b.shape), full(m.shape), full(norms.shape), full(cross.shape),
                  pl.BlockSpec((1, TILE, weights.shape[2]), lambda t: (1, t, 0))],
        out_specs=(wide, col(rows), col(16), full((16, width)), full((1, width))),
        scratch_shapes=[
            pltpu.VMEM((rows + 16, width), low),
            pltpu.VMEM((rows, 16), low),
            pltpu.VMEM((32, 16), low),
        ],
        compiler_params=pltpu.CompilerParams(vmem_limit_bytes=48 << 20),
        cost_estimate=pl.CostEstimate(
            flops=2 * rows * width * width, transcendentals=0, bytes_accessed=2 * width * width
        ),
        name="out_back",
    )(in_grad, x1, gain, gy, before, att, a, b, m, norms, cross, weights)


def qkv_back_kernel(gq_ref, gkv_ref, cos_ref, sin_ref, before_ref, u_ref, inner_ref, a_ref, b_ref, m_ref, n_ref, cross_ref,
                    x_ref, gain_ref, gx_ref, w0_ref, w1_ref,
                    out_ref, ga_ref, gb_ref, gm_ref, lhs0, lhs1, gi, tail):
    t = pl.program_id(0)
    rows, width = gx_ref.shape
    low = jnp.bfloat16
    k_cols = w1_ref.shape[2]
    bounds = [(0, width), (width, width + k_cols), (width + k_cols, width + 2 * k_cols)]

    @pl.when(t == 0)
    def _():
        cosine, sine = cos_ref[...], -sin_ref[...]
        k_parts = [gkv_ref[:, 256 * j : 256 * j + 128] for j in range(k_cols // 128)]
        v_parts = [gkv_ref[:, 256 * j + 128 : 256 * j + 256] for j in range(k_cols // 128)]
        rounded = lambda z: z.astype(low).astype(jnp.float32)
        ups = [
            turn(gq_ref[...].astype(jnp.float32), cosine, sine),
            turn(rounded(jnp.concatenate(k_parts, axis=1)), cosine, sine),
            rounded(jnp.concatenate(v_parts, axis=1)),
        ]
        lhs0[rows:] = jnp.zeros_like(lhs0[rows:])
        lhs1[rows:] = jnp.zeros_like(lhs1[rows:])
        for p, (start, stop) in enumerate(bounds):
            g, norm, m = ups[p], n_ref[:, start:stop], m_ref[:, start:stop]
            b = b_ref[:, start:stop].astype(low)
            gb = (g * (m / norm)).astype(low)
            gm = jnp.sum(g * before_ref[:, start:stop], axis=0, keepdims=True) / norm
            gm_ref[:, start:stop] = gm
            c = -gm * m / (norm * norm)
            weighted = (b.astype(jnp.float32) * c).astype(low)
            gi[:, 16 * p : 16 * p + 16] = (SCALE * dot_nt(gb, b)).astype(low)
            tail[p] = two_terms(dot_nt(weighted, b))
            gb_ref[:, start:stop] = SCALE * dot_tn(inner_ref[p], gb) + SCALE * c * cross_ref[:, start:stop]
            lhs, at = (lhs1, 0) if p == 2 else (lhs0, start)
            lhs[:rows, at : at + stop - start] = gb
            lhs[rows + 16 * p : rows + 16 * p + 16, at : at + stop - start] = weighted

    span = pl.ds(pl.multiple_of(t * TILE, TILE), TILE)
    back = dot_nt(lhs0[...], w0_ref[0]) + dot_nt(lhs1[...], w1_ref[0])
    grad_in = back[:rows]
    for p in range(3):
        a_tile = a_ref[p, :, span].astype(low)
        gi_p = gi[:, 16 * p : 16 * p + 16]
        grad_in = grad_in + dot_f32(gi_p, a_tile)
        spread = back[rows + 16 * p : rows + 16 * p + 16] + SCALE * dot_two(tail[p], a_tile)
        ga_ref[p] = dot_tn(gi_p, u_ref[:, span]) + SCALE * spread
    out_ref[:, span] = grad_in

    @pl.when(t == pl.num_programs(0) - 1)
    def _():
        v = x_ref[...].astype(jnp.float32)
        out_ref[...] = gx_ref[...] + rms_back(v, gain_ref[...], out_ref[...])


def qkv_back(gq, gkv, cosine, sine, before, u, inner, a, b, m, norms, cross, x, gain, gx, weights):
    rows, width = gx.shape
    cols = before.shape[1]
    k_cols = (cols - width) // 2
    tiles = width // TILE
    full = lambda shape: pl.BlockSpec(shape, lambda t: (0,) * len(shape))
    f32, low = jnp.float32, jnp.bfloat16
    wide = full((rows, width))
    return pl.pallas_call(
        qkv_back_kernel,
        out_shape=(
            pltpu.HBM((rows, width), f32),
            jax.ShapeDtypeStruct((3, 16, width), f32),
            jax.ShapeDtypeStruct((16, cols), f32),
            jax.ShapeDtypeStruct((1, cols), f32),
        ),
        grid=(tiles,),
        in_specs=[wide, full(gkv.shape), full(cosine.shape), full(sine.shape), full((rows, cols)), wide, full(inner.shape),
                  full(a.shape), full(b.shape), full(m.shape), full(norms.shape), full(cross.shape),
                  wide, full((1, width)), wide,
                  pl.BlockSpec((1, TILE, width + k_cols), lambda t: (0, t, 0)),
                  pl.BlockSpec((1, TILE, k_cols), lambda t: (1, t, 0))],
        out_specs=(wide, pl.BlockSpec((3, 16, TILE), lambda t: (0, 0, t)), full((16, cols)), full((1, cols))),
        scratch_shapes=[
            pltpu.VMEM((rows + 48, width + k_cols), low),
            pltpu.VMEM((rows + 48, k_cols), low),
            pltpu.VMEM((rows, 48), low),
            pltpu.VMEM((3, 32, 16), low),
        ],
        compiler_params=pltpu.CompilerParams(vmem_limit_bytes=48 << 20),
        cost_estimate=pl.CostEstimate(
            flops=2 * rows * width * cols, transcendentals=0, bytes_accessed=2 * width * cols
        ),
        name="qkv_back",
    )(gq, gkv, cosine, sine, before, u, inner, a, b, m, norms, cross, x, gain, gx, weights, weights)

MESH = pl.DeviceIdType.MESH


def place_in_seq():
    s = lax.axis_index("seq")
    return s, s // 2, lax.rem(s, 2)


def greet(nc, q, s):
    barrier = pltpu.get_barrier_semaphore()

    def signal(target):
        pl.semaphore_signal(barrier, inc=1, device_id={"seq": target}, device_id_type=MESH)

    sibling = s + 1 - 2 * lax.rem(s, 2)
    signal(sibling)
    pl.when(q > 0)(lambda: signal(s - 2))
    pl.when(q < nc - 1)(lambda: signal(s + 2))
    pl.semaphore_wait(barrier, 1 + jnp.where(q > 0, 1, 0) + jnp.where(q < nc - 1, 1, 0))
    return sibling

def near_first(i, q, nc):
    short = jnp.where(q <= nc - 1 - q, q, nc - 1 - q)
    far = jnp.where(q <= nc - 1 - q, i, nc - 1 - i)
    step = (i + 1) // 2
    near = q - step if i % 2 else q + step
    return jnp.where(i <= 2 * short, near, far)


def place_in_rows(rows):
    half = rows // 2
    r = lax.axis_index("rows")
    a, b = r // 2, lax.rem(r, 2)
    turned = lambda k: 2 * lax.rem(a + k + half, half)
    return r, 2 * a + 1 - b, lambda k: turned(k) + b, lambda k: turned(k) + 1 - b


def greet_all(n, rows):
    s = lax.axis_index("seq")
    r, b_row, a_row, _ = place_in_rows(rows)
    barrier = pltpu.get_barrier_semaphore()
    for t in range(1, n):
        pl.semaphore_signal(
            barrier, inc=1, device_id=(r, lax.rem(s + t, n)), device_id_type=MESH
        )
    pl.semaphore_signal(barrier, inc=1, device_id=(b_row, s), device_id_type=MESH)
    for k in range(1, rows // 2):
        pl.semaphore_signal(barrier, inc=1, device_id=(a_row(k), s), device_id_type=MESH)
    pl.semaphore_wait(barrier, n - 1 + rows // 2)


def remote(src, dst, send, recv, row, seq):
    return pltpu.make_async_remote_copy(
        src_ref=src, dst_ref=dst, send_sem=send, recv_sem=recv,
        device_id=(row, seq), device_id_type=MESH,
    )


def weights_kernel(n, rows, qo, kv, xg, wd_hbm, ad_hbm, bd_hbm, x_hbm, gain_ref, aa_hbm, ag_hbm,
                   wa, gz, near, sq_ref, gram_ref, u_hbm, inner_ref,
                   wd, ad_ref, bd_ref, x_ref, aa_ref, ag_ref, local, edge, a_in, a_sib_in, a_out, a_sib_out, z_in, z_out):
    nc, half = n // 2, rows // 2
    others = half - 1
    units = gz.shape[-1]
    s, q, c = place_in_seq()
    sibling = s + 1 - 2 * c
    r, b_row, a_row, diagonal = place_in_rows(rows)
    greet_all(n, rows)

    both, first, second = pl.ds(0, 2), pl.ds(0, 1), pl.ds(1, 1)
    LINE, FROM_B = 0, 1

    def from_a(k):
        return 1 + k

    def relay_b(k):
        return 1 + others + k

    def relay_a(k):
        return 1 + 2 * others + k

    def a_view(p, core, parts, row):
        return wa.at[parts, 2 * p + core, row]

    def content(kind):
        if kind == LINE:
            return both, r
        if kind == FROM_B:
            return both, b_row
        for k in range(1, half):
            if kind == from_a(k):
                return both, a_row(-k)
            if kind == relay_b(k):
                return second, diagonal(-k)
            if kind == relay_a(k):
                return first, diagonal(-k)

    kinds = 2 + 3 * others

    def a_send(p, parts, row, kind, target_row):
        return remote(
            a_view(p, c, parts, row), a_view(p, c, parts, row),
            a_out.at[p, kind], a_in.at[p, kind], target_row, s,
        )

    def a_arrival(p, kind):
        parts, row = content(kind)
        return a_send(p, parts, row, kind, r)

    def a_to_sibling(p, kind, core):
        parts, row = content(kind)
        return remote(
            a_view(p, core, parts, row), a_view(p, core, parts, row),
            a_sib_out.at[p, kind], a_sib_in.at[p, kind], r, sibling,
        )

    def columns(device):
        return pl.ds(pl.multiple_of(device * units, units), units)

    def z_send(p, core):
        return remote(
            xg.at[:, r, :, columns(2 * p + core)], gz.at[:, s],
            z_out.at[p, core], z_in.at[q, c], r, 2 * p + core,
        )

    def z_arrival(p, core):
        slot = gz.at[:, 2 * p + core]
        return remote(slot, slot, z_out.at[p, core], z_in.at[p, core], r, s)

    def line_send(p, sem, target):
        view = a_view(p, c, both, r)
        return remote(view, view, sem, a_in.at[p, LINE], r, target)

    wide, k_cols = qo.shape[-1], kv.shape[-1]
    blocks = [(qo, 0, 0), (kv, 0, wide), (kv, 1, 0), (qo, 1, k_cols)]

    def own_blocks(part, out):
        for source, i, start in blocks:
            columns_of = pl.ds(start, source.shape[-1])
            out(source.at[i, part], wa.at[i, s, part, :, columns_of])

    def own_line(sem, target):
        own_blocks(
            r, lambda src, dst: remote(src, dst, sem, a_in.at[q, LINE], r, target).start()
        )

    pl.when(q > 0)(lambda: own_line(edge.at[0], s - 2))
    pl.when(q < nc - 1)(lambda: own_line(edge.at[1], s + 2))
    order = [near_first(i, q, nc) for i in range(nc)]
    whole_block = wa.at[:, s]
    sib_a = lambda: remote(whole_block, whole_block, edge.at[2], edge.at[3], r, sibling)
    sib_g = lambda: remote(
        xg.at[:, :, :, columns(sibling)], near.at[:, c], edge.at[4], edge.at[5], r, sibling
    )
    keep_a = pltpu.make_async_copy(whole_block, whole_block, local.at[0])
    keep_g = pltpu.make_async_copy(xg.at[:, :, :, columns(s)], near.at[:, c], local.at[1])
    all_parts = pl.ds(0, rows)
    own_blocks(all_parts, lambda src, dst: remote(src, dst, edge.at[2], edge.at[3], r, sibling).start())
    own_blocks(all_parts, lambda src, dst: pltpu.make_async_copy(src, dst, local.at[0]).start())
    takes = [
        pltpu.make_async_copy(src, dst, local.at[3 + i])
        for i, (src, dst) in enumerate(
            [(x_hbm, x_ref), (aa_hbm, aa_ref), (ag_hbm, ag_ref), (ad_hbm, ad_ref), (bd_hbm, bd_ref), (wd_hbm, wd)]
        )
    ]
    for cp in takes:
        cp.start()
    for cp in takes:
        cp.wait()
    low = jnp.bfloat16
    v = x_ref[...].astype(jnp.float32)
    u = (v * unit_rms(v) * gain_ref[...]).astype(low)
    x_ref[...] = u
    keep_u = pltpu.make_async_copy(x_ref, u_hbm, local.at[2])
    keep_u.start()
    for g in range(4):
        a = aa_ref[g].astype(low)
        gram_ref[g] = two_terms(dot_nt(a, a))
        if g < 3:
            inner_ref[g] = dot_nt(u, a).astype(low)
    for g in range(2):
        a = ag_ref[g].astype(low)
        gram_ref[4 + g] = two_terms(dot_nt(a, a))

    def down_squares():
        a = ad_ref[...].astype(low)
        gram_ref[6] = two_terms(dot_nt(a, a))
        mine = pl.ds(pl.multiple_of(s * wd.shape[0], wd.shape[0]), wd.shape[0])
        cross = dot_f32(ad_ref[:, mine].astype(low), wd[...])
        b_wide = bd_ref[...].astype(low).astype(jnp.float32)
        sq_ref[...] = column_squares(wd[...]) + 2.0 * SCALE * jnp.sum(b_wide * cross, axis=0, keepdims=True)

    for p in order[1:]:
        a_arrival(p, LINE).wait_recv()
        pl.when((p < q) & (q < nc - 1))(
            lambda p=p: line_send(p, a_out.at[p, LINE], s + 2).start()
        )
        pl.when((p > q) & (q > 0))(
            lambda p=p: line_send(p, a_out.at[p, LINE], s - 2).start()
        )
        a_send(p, both, r, FROM_B, b_row).start()
        for k in range(1, half):
            a_send(p, both, r, from_a(k), a_row(k)).start()
        a_to_sibling(p, LINE, c).start()
    for p in order[1:]:
        for core in range(2):
            z_send(p, core).start()
    sib_g().start()
    keep_g.start()
    down_squares()
    keep_u.wait()
    for p in order[1:]:
        a_arrival(p, FROM_B).wait_recv()
        for k in range(1, half):
            a_send(p, first, b_row, relay_a(k), a_row(k)).start()
        a_to_sibling(p, FROM_B, c).start()
        for k in range(1, half):
            a_arrival(p, from_a(k)).wait_recv()
            a_send(p, second, a_row(-k), relay_b(k), b_row).start()
            a_to_sibling(p, from_a(k), c).start()
    for p in order[1:]:
        for k in range(1, half):
            for kind in (relay_b(k), relay_a(k)):
                a_arrival(p, kind).wait_recv()
                a_to_sibling(p, kind, c).start()
    keep_a.wait()
    keep_g.wait()
    sib_a().wait()
    sib_g().wait()
    pl.when(q > 0)(lambda: line_send(q, edge.at[0], s).wait_send())
    pl.when(q < nc - 1)(lambda: line_send(q, edge.at[1], s).wait_send())
    for p in order[1:]:
        pl.when(((p < q) & (q < nc - 1)) | ((p > q) & (q > 0)))(
            lambda p=p: line_send(p, a_out.at[p, LINE], s).wait_send()
        )
        for kind in range(kinds):
            a_to_sibling(p, kind, c).wait_send()
            a_to_sibling(p, kind, 1 - c).wait_recv()
        a_send(p, both, r, FROM_B, b_row).wait_send()
        for k in range(1, half):
            a_send(p, both, r, from_a(k), r).wait_send()
            a_send(p, first, b_row, relay_a(k), r).wait_send()
            a_send(p, second, a_row(-k), relay_b(k), r).wait_send()
        for core in range(2):
            z_send(p, core).wait_send()
            z_arrival(p, core).wait_recv()


def gather_weights(n, rows, qo, kv, xg, wd, ad, bd, x, gain, aa, ag, collective_id):
    nc = n // 2
    _, block, width = qo.shape
    part = block // rows
    cols = width + kv.shape[2]
    qo = qo.reshape(2, rows, part, width)
    kv = kv.reshape(2, rows, part, kv.shape[2])
    xg = xg.reshape(2, rows, part, xg.shape[2])
    units = xg.shape[3] // n
    kinds = 2 + 3 * (rows // 2 - 1)
    dma = pltpu.SemaphoreType.DMA
    anywhere = pl.BlockSpec(memory_space=pl.ANY)
    vmem = pl.BlockSpec(memory_space=pltpu.VMEM)
    low = qo.dtype
    wa, gz, near, sq, grams, u, inner = pl.pallas_call(
        functools.partial(weights_kernel, n, rows),
        out_shape=(
            pltpu.HBM((2, n, rows, part, cols), low),
            pltpu.HBM((2, n, part, units), low),
            pltpu.HBM((2, 2, rows, part, units), low),
            jax.ShapeDtypeStruct((1, width), jnp.float32),
            jax.ShapeDtypeStruct((7, 32, 16), low),
            pltpu.HBM(x.shape, low),
            jax.ShapeDtypeStruct((3, x.shape[0], 16), low),
        ),
        in_specs=[anywhere] * 7 + [vmem] + [anywhere] * 2,
        out_specs=(anywhere,) * 3 + (vmem,) * 2 + (anywhere, vmem),
        scratch_shapes=[pltpu.VMEM(v.shape, v.dtype) for v in (wd, ad, bd, x, aa, ag)]
        + [dma((9,)), dma((6,))]
        + [dma((nc, kinds))] * 4
        + [dma((nc, 2))] * 2,
        compiler_params=pltpu.CompilerParams(
            collective_id=collective_id, has_side_effects=True, vmem_limit_bytes=32 << 20
        ),
        cost_estimate=pl.CostEstimate(
            flops=0, transcendentals=0, bytes_accessed=250 * 1024 * 1024
        ),
        name="gather_weights",
    )(qo, kv, xg, wd, ad, bd, x, gain, aa, ag)
    return wa.reshape(2, n * block, cols), gz, near, sq, grams, u, inner


def gather_kernel(n, rows, count, shared, *refs):
    nc = n // 2
    sources = refs[: count + len(shared[0])]
    outs = refs[len(sources) : 2 * len(sources) - len(shared[0]) + len(shared[1])]
    local_sem, to_sib, to_left, to_right, recv, share_out, share_in = refs[len(sources) + len(outs) :]
    xs, held, swapped = sources[:count], sources[count:], outs[count:]
    s, q, c = place_in_seq()
    sibling = s + 1 - 2 * c
    r, b_row, a_row, _ = place_in_rows(rows)
    greet_all(n, rows)
    locals_ = [
        pltpu.make_async_copy(xs[k], outs[k].at[s], local_sem.at[k]) for k in range(count)
    ]
    for cp in locals_:
        cp.start()

    def copy(k, src, slot, sems, target):
        return remote(src, outs[k].at[slot], sems.at[k, slot], recv.at[k, slot], r, target)

    def share(i, p):
        source, piece, turn, _ = shared[1][i]
        pair = pl.ds(2 * p, 2)
        src = held[source].at[pair] if piece is None else held[source].at[piece, pair]
        target = b_row if turn == 0 else a_row(turn)
        return remote(src, swapped[i].at[pair], share_out.at[i, p], share_in.at[i, p], target, s)

    for k in range(count):
        pl.when(q > 0)(lambda k=k: copy(k, xs[k], s, to_left, s - 2).start())
        pl.when(q < nc - 1)(lambda k=k: copy(k, xs[k], s, to_right, s + 2).start())
        copy(k, xs[k], s, to_sib, sibling).start()
    order = [near_first(i, q, nc) for i in range(nc)]
    for p in order[1:]:
        for i in range(len(shared[1])):
            share(i, p).start()
    for p in order[1:]:
        slot = 2 * p + c
        for k in range(count):
            src = outs[k].at[slot]
            copy(k, src, slot, to_right, s).wait_recv()
            pl.when((p < q) & (q < nc - 1))(
                lambda k=k, src=src, slot=slot: copy(k, src, slot, to_right, s + 2).start()
            )
            pl.when((p > q) & (q > 0))(
                lambda k=k, src=src, slot=slot: copy(k, src, slot, to_left, s - 2).start()
            )
            copy(k, src, slot, to_sib, sibling).start()
    for cp in locals_:
        cp.wait()
    for p in range(nc):
        mine, theirs = 2 * p + c, 2 * p + 1 - c
        for k in range(count):
            copy(k, outs[k].at[theirs], theirs, to_sib, sibling).wait_recv()
            copy(k, outs[k].at[mine], mine, to_sib, sibling).wait_send()
            pl.when((q < nc - 1) & (p <= q))(
                lambda k=k, mine=mine: copy(k, outs[k].at[mine], mine, to_right, s).wait_send()
            )
            pl.when((q > 0) & (p >= q))(
                lambda k=k, mine=mine: copy(k, outs[k].at[mine], mine, to_left, s).wait_send()
            )
    for p in order[1:]:
        for i in range(len(shared[1])):
            share(i, p).wait_send()
            share(i, p).wait_recv()


def gather_seq(n, rows, arrays, collective_id, held=(), shares=()):
    nc, count = n // 2, len(arrays)
    nbytes = sum(a.size * a.dtype.itemsize for a in arrays)
    dma = pltpu.SemaphoreType.DMA
    shape = jax.ShapeDtypeStruct
    outs = [shape((n, *a.shape), a.dtype) for a in arrays]
    outs += [shape(held[source].shape[-3:], held[source].dtype) for source, _, _ in shares]
    anywhere = pl.BlockSpec(memory_space=pl.ANY)
    listed = (tuple(held), [(source, piece, turn, None) for source, piece, turn in shares])
    sems = dma((max(1, len(shares)), nc))
    got = pl.pallas_call(
        functools.partial(gather_kernel, n, rows, count, (range(len(held)), listed[1])),
        out_shape=tuple(outs),
        in_specs=[anywhere] * (count + len(held)),
        out_specs=(anywhere,) * len(outs),
        scratch_shapes=[dma((count,))] + [dma((count, n))] * 4 + [sems] * 2,
        compiler_params=pltpu.CompilerParams(collective_id=collective_id, has_side_effects=True),
        cost_estimate=pl.CostEstimate(flops=0, transcendentals=0, bytes_accessed=nbytes * n * 20),
        name="gather_seq",
    )(*arrays, *held)
    return got[:count], got[count:]

def scatter_kernel(n, x_ref, o_ref, own, sib, from_left, from_right,
                   load_sem, to_sib, sib_in, to_right, right_in, to_left, left_in):
    nc = n // 2
    s, q, c = place_in_seq()
    sibling = greet(nc, q, s)
    theirs = 1 - c

    def load(p):
        return pltpu.make_async_copy(x_ref.at[2 * p + c], own.at[p], load_sem.at[p])

    def to_sibling(p):
        return pltpu.make_async_remote_copy(
            src_ref=x_ref.at[2 * p + theirs],
            dst_ref=sib.at[p],
            send_sem=to_sib.at[p],
            recv_sem=sib_in.at[p],
            device_id={"seq": sibling},
            device_id_type=MESH,
        )

    def rightward(p, target):
        return pltpu.make_async_remote_copy(
            src_ref=own.at[p],
            dst_ref=from_left.at[p],
            send_sem=to_right.at[p],
            recv_sem=right_in.at[p],
            device_id={"seq": target},
            device_id_type=MESH,
        )

    def leftward(p, target):
        return pltpu.make_async_remote_copy(
            src_ref=own.at[p],
            dst_ref=from_right.at[p],
            send_sem=to_left.at[p],
            recv_sem=left_in.at[p],
            device_id={"seq": target},
            device_id_type=MESH,
        )

    order = []
    for t in range(nc):
        for p in (nc - 1 - t, t):
            if p not in order:
                order.append(p)
    for p in order:
        to_sibling(p).start()
        load(p).start()

    f32 = jnp.float32
    for p in order:
        load(p).wait()
        to_sibling(p).wait_recv()

        @pl.when(p > q)
        def _(p=p):
            @pl.when(q > 0)
            def _():
                rightward(p, s).wait_recv()
                total = own[p].astype(f32) + sib[p].astype(f32) + from_left[p].astype(f32)
                own[p] = total.astype(own.dtype)

            @pl.when(q == 0)
            def _():
                own[p] = (own[p].astype(f32) + sib[p].astype(f32)).astype(own.dtype)

            rightward(p, s + 2).start()

        @pl.when(p < q)
        def _(p=p):
            @pl.when(q < nc - 1)
            def _():
                leftward(p, s).wait_recv()
                total = own[p].astype(f32) + sib[p].astype(f32) + from_right[p].astype(f32)
                own[p] = total.astype(own.dtype)

            @pl.when(q == nc - 1)
            def _():
                own[p] = (own[p].astype(f32) + sib[p].astype(f32)).astype(own.dtype)

            leftward(p, s - 2).start()

    o_ref[...] = own[q].astype(f32) + sib[q].astype(f32)

    @pl.when(q > 0)
    def _():
        rightward(q, s).wait_recv()
        o_ref[...] += from_left[q].astype(f32)

    @pl.when(q < nc - 1)
    def _():
        leftward(q, s).wait_recv()
        o_ref[...] += from_right[q].astype(f32)

    for p in range(nc):
        to_sibling(p).wait_send()
        pl.when(p > q)(lambda p=p: rightward(p, s).wait_send())
        pl.when(p < q)(lambda p=p: leftward(p, s).wait_send())


def scatter_seq(n, x, collective_id):
    nc = n // 2
    _, rows, cols = x.shape
    dma = pltpu.SemaphoreType.DMA
    buf = pltpu.VMEM((nc, rows, cols), x.dtype)
    return pl.pallas_call(
        functools.partial(scatter_kernel, n),
        out_shape=jax.ShapeDtypeStruct((rows, cols), jnp.float32),
        in_specs=[pl.BlockSpec(memory_space=pl.ANY)],
        out_specs=pl.BlockSpec(memory_space=pltpu.VMEM),
        scratch_shapes=[buf] * 4 + [dma((nc,))] * 7,
        compiler_params=pltpu.CompilerParams(
            collective_id=collective_id, has_side_effects=True, vmem_limit_bytes=32 << 20
        ),
        cost_estimate=pl.CostEstimate(flops=0, transcendentals=0, bytes_accessed=x.size * 2 * 20),
        name="scatter_seq",
    )(x)

def swap_halves(x):
    return pltpu.roll(x.astype(jnp.float32), HEAD_DIM, 1)


def stack_heads(block):
    lane = lax.broadcasted_iota(jnp.int32, (block.shape[0], 128), 1)
    rows = []
    for h in range(8):
        pair = block[:, (h // 2) * 128 : (h // 2 + 1) * 128].astype(jnp.float32)
        if h % 2 != h // 4:
            pair = swap_halves(pair)
        keep = lane < HEAD_DIM if h // 4 == 0 else lane >= HEAD_DIM
        rows.append(jnp.where(keep, pair, 0.0).astype(jnp.bfloat16))
    return jnp.concatenate(rows, axis=0)


def unstack_heads(stacked, span):
    lane = lax.broadcasted_iota(jnp.int32, (span, 128), 1)
    pairs = []
    for t in range(4):
        first = stacked[2 * t * span : (2 * t + 1) * span]
        second = stacked[(2 * t + 1) * span : (2 * t + 2) * span]
        if t < 2:
            second = swap_halves(second)
        else:
            first = swap_halves(first)
        pairs.append(jnp.where(lane < HEAD_DIM, first, second))
    return jnp.concatenate(pairs, axis=1)


def attend_kernel(valid_ref, q_ref, k_ref, v_ref, o_ref, p_ref):
    span = q_ref.shape[1]
    keys = k_ref.shape[0] * span
    q8 = stack_heads(q_ref[0])
    k2 = k_ref[:, 0].reshape(keys, 128)
    v2 = v_ref[:, 0].reshape(keys, 128)
    scores = lax.dot_general(q8, k2, last_last, preferred_element_type=jnp.float32)
    scores = scores * HEAD_DIM**-0.5
    first_pos = lax.axis_index("seq") * span
    q_pos = first_pos + lax.broadcasted_iota(jnp.int32, (8, span, keys), 1).reshape(8 * span, keys)
    k_pos = lax.broadcasted_iota(jnp.int32, (8 * span, keys), 1)
    allowed = (k_pos <= q_pos) & (k_pos < valid_ref[pl.program_id(0)])
    scores = jnp.where(allowed, scores, -1e30)
    unscaled = jnp.exp(scores - jnp.max(scores, axis=1, keepdims=True))
    shares = unscaled * (1.0 / jnp.sum(unscaled, axis=1, keepdims=True))
    shares = shares.astype(jnp.bfloat16)
    p_ref[0, 0] = shares
    mixed = jnp.dot(shares, v2, preferred_element_type=jnp.float32)
    o_ref[0] = unstack_heads(mixed, span).astype(jnp.bfloat16)


def attend(q, kv, valid):
    pair, span, width = q.shape
    n, kv_width = kv.shape[0], kv.shape[3] // 2
    groups = kv_width // 128
    keys = n * span
    q_spec = pl.BlockSpec((1, span, 512), lambda p, j, *_: (p, 0, j))
    flops = 4 * pair * groups * 8 * span * keys * 128
    return pl.pallas_call(
        attend_kernel,
        out_shape=(
            pltpu.HBM(q.shape, jnp.bfloat16),
            pltpu.HBM((pair, groups, 8 * span, keys), jnp.bfloat16),
        ),
        grid_spec=pltpu.PrefetchScalarGridSpec(
            num_scalar_prefetch=1,
            grid=(pair, groups),
            in_specs=[
                q_spec,
                pl.BlockSpec((n, 1, span, 128), lambda p, j, *_: (0, p, 0, j)),
                pl.BlockSpec((n, 1, span, 128), lambda p, j, *_: (0, p, 0, groups + j)),
            ],
            out_specs=(
                q_spec,
                pl.BlockSpec((1, 1, 8 * span, keys), lambda p, j, *_: (p, j, 0, 0)),
            ),
        ),
        compiler_params=pltpu.CompilerParams(vmem_limit_bytes=40 << 20),
        cost_estimate=pl.CostEstimate(
            flops=flops, transcendentals=flops // 512, bytes_accessed=8 << 20
        ),
        name="attend",
    )(valid, q, kv, kv)


def attend_back_kernel(q_ref, k_ref, v_ref, p_ref, g_ref, gq_ref, gkv_ref):
    span = q_ref.shape[1]
    keys = k_ref.shape[0] * span
    q8 = stack_heads(q_ref[0])
    g8 = stack_heads(g_ref[0])
    k2 = k_ref[:, 0].reshape(keys, 128)
    v2 = v_ref[:, 0].reshape(keys, 128)
    low = p_ref[0, 0]
    shares = low.astype(jnp.float32)
    grad_shares = lax.dot_general(g8, v2, last_last, preferred_element_type=jnp.float32)
    weighted = shares * grad_shares
    centre = jnp.sum(weighted, axis=1, keepdims=True)
    grad_scores = (weighted - shares * centre).astype(jnp.bfloat16)
    gq = jnp.dot(grad_scores, k2, preferred_element_type=jnp.float32) * HEAD_DIM**-0.5
    gq_ref[0] = unstack_heads(gq, span).astype(jnp.bfloat16)
    gk = lax.dot_general(grad_scores, q8, first_first, preferred_element_type=jnp.float32)
    gv = lax.dot_general(low, g8, first_first, preferred_element_type=jnp.float32)
    both = jnp.concatenate([gk * HEAD_DIM**-0.5, gv], axis=1).astype(jnp.bfloat16)
    gkv_ref[:, 0] = both.reshape(gkv_ref.shape[0], span, 256)


def attend_back(q, kv, shares, g):
    pair, span, _ = q.shape
    n, kv_width = kv.shape[0], kv.shape[3] // 2
    groups = kv_width // 128
    keys = n * span
    q_spec = pl.BlockSpec((1, span, 512), lambda p, j: (p, 0, j))
    flops = 10 * pair * groups * 8 * span * keys * 128
    return pl.pallas_call(
        attend_back_kernel,
        out_shape=(
            pltpu.HBM(q.shape, jnp.bfloat16),
            pltpu.HBM(kv.shape, jnp.bfloat16),
        ),
        grid=(pair, groups),
        in_specs=[
            q_spec,
            pl.BlockSpec((n, 1, span, 128), lambda p, j: (0, p, 0, j)),
            pl.BlockSpec((n, 1, span, 128), lambda p, j: (0, p, 0, groups + j)),
            pl.BlockSpec((1, 1, 8 * span, keys), lambda p, j: (p, j, 0, 0)),
            q_spec,
        ],
        out_specs=(
            q_spec,
            pl.BlockSpec((n, 1, span, 256), lambda p, j: (0, p, 0, j)),
        ),
        compiler_params=pltpu.CompilerParams(vmem_limit_bytes=40 << 20),
        cost_estimate=pl.CostEstimate(flops=flops, transcendentals=0, bytes_accessed=8 << 20),
        name="attend_back",
    )(q, kv, kv, shares, g)

def by_distance(i, q, nc):
    room = nc - 1 - q
    left_half = q <= room
    short = jnp.where(left_half, q, room)
    far = jnp.where(left_half, i, nc - 1 - i)
    step = (i + 1) // 2
    near = jnp.where(lax.rem(i, 2) == 1, q - step, q + step)
    return jnp.where(i <= 2 * short, near, far)


def ffn_kernel(n, rows, pieces, u_hbm, inner_hbm, gy0_hbm, gy1_hbm, wd_hbm, a_ref, b_ref, m_ref, ad_ref, bd_ref, md_ref, sq_ref, gram_ref,
               in_ref, down0_hbm, down1_hbm, ga_ref, gb_ref, gm_ref, norm_ref, gad_ref, gbd_ref, gmd_ref, nd_ref,
               w_parts, wd, u, side, gy, down, own, theirs, sib, from_left, from_right, ratio, cross, gm_all,
               w_sem, load_sem, down_sem, small_out, small_in, to_sib, sib_in, to_right, right_in, to_left, left_in):
    nc = n // 2
    f32, low = jnp.float32, jnp.bfloat16
    s, q, c = place_in_seq()
    tokens = own.shape[1]

    weights = [pltpu.make_async_copy(wd_hbm, wd, w_sem.at[0])]
    for src, dst in place_pieces(n, rows, pieces, w_parts):
        weights.append(pltpu.make_async_copy(src, dst, w_sem.at[len(weights)]))
    for cp in weights:
        cp.start()

    def loads(i):
        p = by_distance(nc - 1 - i, q, nc)
        slot = lax.rem(i, 2)
        pair = pl.ds(2 * p, 2)
        return (
            pltpu.make_async_copy(u_hbm.at[pair], u.at[slot], load_sem.at[0, slot]),
            pltpu.make_async_copy(
                gy0_hbm.at[pair], gy.at[slot, :, : tokens // 2], load_sem.at[1, slot]
            ),
            pltpu.make_async_copy(
                gy1_hbm.at[pair], gy.at[slot, :, tokens // 2 :], load_sem.at[2, slot]
            ),
            pltpu.make_async_copy(inner_hbm.at[pair], side.at[slot], load_sem.at[3, slot]),
        )

    for cp in loads(0):
        cp.start()
    sibling = s + 1 - 2 * c
    barrier = pltpu.get_barrier_semaphore()
    for t in range(1, n):
        pl.semaphore_signal(
            barrier, inc=1, device_id={"seq": lax.rem(s + t, n)}, device_id_type=MESH
        )

    def to_sibling(p):
        return pltpu.make_async_remote_copy(
            src_ref=theirs.at[p], dst_ref=sib.at[p], send_sem=to_sib.at[p], recv_sem=sib_in.at[p],
            device_id={"seq": sibling}, device_id_type=MESH,
        )

    def rightward(p, target):
        return pltpu.make_async_remote_copy(
            src_ref=own.at[p], dst_ref=from_left.at[p], send_sem=to_right.at[p], recv_sem=right_in.at[p],
            device_id={"seq": target}, device_id_type=MESH,
        )

    def leftward(p, target):
        return pltpu.make_async_remote_copy(
            src_ref=own.at[p], dst_ref=from_right.at[p], send_sem=to_left.at[p], recv_sem=left_in.at[p],
            device_id={"seq": target}, device_id_type=MESH,
        )

    def down_out(slot, p):
        half = tokens // 2
        return [
            pltpu.make_async_copy(
                down.at[slot, :, half * k : half * (k + 1)], out.at[pl.ds(2 * p, 2)], down_sem.at[k, slot]
            )
            for k, out in enumerate((down0_hbm, down1_hbm))
        ]

    def pass_on(p):
        to_sibling(p).wait_recv()

        @pl.when(p > q)
        def _():
            @pl.when(q > 0)
            def _():
                rightward(p, s).wait_recv()
                own[p] = (own[p].astype(f32) + sib[p].astype(f32) + from_left[p].astype(f32)).astype(low)

            @pl.when(q == 0)
            def _():
                own[p] = (own[p].astype(f32) + sib[p].astype(f32)).astype(low)

            rightward(p, s + 2).start()

        @pl.when(p < q)
        def _():
            @pl.when(q < nc - 1)
            def _():
                leftward(p, s).wait_recv()
                own[p] = (own[p].astype(f32) + sib[p].astype(f32) + from_right[p].astype(f32)).astype(low)

            @pl.when(q == nc - 1)
            def _():
                own[p] = (own[p].astype(f32) + sib[p].astype(f32)).astype(low)

            leftward(p, s - 2).start()

    def starts_flow(p):
        return ((p > q) & (q == 0)) | ((p < q) & (q == nc - 1))

    w = [w_parts.at[g] for g in range(2)]
    width = u_hbm.shape[2]
    weight = lambda g: w[g][...].reshape(width, -1)
    units = wd.shape[0]
    mine = pl.ds(pl.multiple_of(s * units, units), units)
    bd = bd_ref[...].astype(low)
    ad = ad_ref[:, mine].astype(low)
    a = [a_ref[g].astype(low) for g in range(2)]
    b = [b_ref[g, :, mine].astype(low) for g in range(2)]
    m = [m_ref[g : g + 1, mine] for g in range(2)]
    for cp in weights:
        cp.wait()
    a_both = jnp.concatenate(a, axis=0)
    for g in range(2):
        norm, cr = column_norms(weight(g), gram_ref[4 + g], b[g], dot_f32(a[g], weight(g)))
        norm_ref[g] = norm
        cross[g] = cr
        ratio[g] = m[g] / norm
    for ref in (ga_ref, gb_ref, gm_ref, gad_ref, gbd_ref, gmd_ref):
        ref[...] = jnp.zeros_like(ref)
    bd_wide = bd.astype(f32)
    gram_b = dot_two(gram_ref[6], bd)
    squares = jnp.sum(sq_ref[...], axis=0) + SCALE * SCALE * jnp.sum(
        bd_wide * gram_b, axis=0, keepdims=True
    )
    nd_ref[...] = jnp.sqrt(squares + 1e-06)
    ratio_d = md_ref[...] / nd_ref[...]
    pl.semaphore_wait(barrier, n - 1)

    def step(i, carry):
        p = by_distance(nc - 1 - i, q, nc)
        slot = lax.rem(i, 2)
        for cp in loads(i):
            cp.wait()

        @pl.when(i + 1 < nc)
        def _():
            for cp in loads(i + 1):
                cp.start()

        x = u[slot].reshape(2 * tokens, -1)
        upstream = gy[slot].reshape(2 * tokens, -1).astype(f32)
        gb_d = (upstream * ratio_d).astype(low)
        gi_d = (SCALE * dot_nt(gb_d, bd)).astype(low)
        gh = dot_nt(gb_d, wd[...]) + dot_f32(gi_d, ad)
        sides = side[slot].reshape(2 * tokens, -1)
        inner = [sides[:, 16 * g : 16 * g + 16] for g in range(2)]
        before = [dot_f32(x, weight(g)) + SCALE * dot_f32(inner[g], b[g]) for g in range(2)]
        gate = before[0] * ratio[0]
        lift = before[1] * ratio[1]
        sig = 1.0 / (1.0 + jnp.exp(-gate))
        silu = gate * sig
        hidden = (silu * lift).astype(low)
        grads = [gh * lift * sig * (1.0 + gate * (1.0 - sig)), gh * silu]
        gb = [(grads[g] * ratio[g]).astype(low) for g in range(2)]
        gi = jnp.concatenate([(SCALE * dot_nt(gb[g], b[g])).astype(low) for g in range(2)], axis=1)
        back = dot_nt(gb[0], weight(0)) + dot_nt(gb[1], weight(1)) + dot_f32(gi, a_both)
        back = back.astype(low).reshape(2, tokens, -1)
        first, second = back[0], back[1]

        @pl.when(c == 0)
        def _():
            own[p] = first
            theirs[p] = second

        @pl.when(c == 1)
        def _():
            own[p] = second
            theirs[p] = first

        to_sibling(p).start()
        inner_d = dot_nt(hidden, ad).astype(low)
        part = dot_f32(hidden, wd[...]) + SCALE * dot_f32(inner_d, bd)

        @pl.when(i >= 2)
        def _():
            for cp in down_out(slot, p):
                cp.wait()

        down[slot] = part.astype(low).reshape(2, tokens, -1)
        for cp in down_out(slot, p):
            cp.start()
        gmd_ref[...] += jnp.sum(upstream * part, axis=0, keepdims=True)
        gad_ref[...] += dot_tn(gi_d, hidden)
        gbd_ref[...] += SCALE * dot_tn(inner_d, gb_d)
        ga_ref[...] += dot_tn(gi, x).reshape(ga_ref.shape)
        for g in range(2):
            gm_ref[g] += jnp.sum(grads[g] * before[g], axis=0, keepdims=True)
            gb_ref[g] += SCALE * dot_tn(inner[g], gb[g])

        pl.when(starts_flow(p))(lambda: pass_on(p))
        last = by_distance(nc - i, q, nc)
        pl.when((i > 0) & jnp.logical_not(starts_flow(last)))(lambda: pass_on(last))
        return carry

    lax.fori_loop(0, nc, step, 0)

    gmd_ref[...] = gmd_ref[...] / nd_ref[...]

    def small(t, slot):
        return pltpu.make_async_remote_copy(
            src_ref=gmd_ref,
            dst_ref=gm_all.at[slot],
            send_sem=small_out.at[t],
            recv_sem=small_in.at[t],
            device_id={"seq": lax.rem(s + t, n)},
            device_id_type=MESH,
        )

    for t in range(1, n):
        small(t, s).start()
    for g in range(2):
        norm = norm_ref[g]
        gm = gm_ref[g] / norm
        gm_ref[g] = gm
        col = -gm * m[g] / (norm * norm)
        weighted = (b[g].astype(f32) * col).astype(low)
        tail = two_terms(dot_nt(weighted, b[g]))
        ga_ref[g] += SCALE * (dot_nt(weighted, weight(g)) + SCALE * dot_two(tail, a[g]))
        gb_ref[g] += SCALE * col * cross[g]

    gm_line = gmd_ref[...]
    for t in range(1, n):
        slot = lax.rem(s - t + n, n)
        small(t, slot).wait_recv()
        gm_line = gm_line + gm_all[slot]
    col = -gm_line * md_ref[...] / (nd_ref[...] * nd_ref[...])
    weighted = (bd_wide * col).astype(low)
    tail = two_terms(dot_nt(weighted, bd))
    gad_ref[...] += SCALE * (dot_nt(weighted, wd[...]) + SCALE * dot_two(tail, ad))
    own_gram = jnp.where(s == 0, SCALE, 0.0) * gram_b
    gbd_ref[...] += SCALE * col * (dot_f32(ad, wd[...]) + own_gram)

    to_sibling(q).wait_recv()
    in_ref[...] = own[q].astype(f32) + sib[q].astype(f32)

    @pl.when(q > 0)
    def _():
        rightward(q, s).wait_recv()
        in_ref[...] += from_left[q].astype(f32)

    @pl.when(q < nc - 1)
    def _():
        leftward(q, s).wait_recv()
        in_ref[...] += from_right[q].astype(f32)

    for i in range(min(2, nc)):
        for cp in down_out(i, 0):
            cp.wait()
    for t in range(1, n):
        small(t, s).wait_send()
    for p in range(nc):
        to_sibling(p).wait_send()
        pl.when(p > q)(lambda p=p: rightward(p, s).wait_send())
        pl.when(p < q)(lambda p=p: leftward(p, s).wait_send())


def share_plan(rows):
    turns = range(1, rows // 2)
    first = [(0, 0, k) for k in turns] + [(0, 1, 0)]
    second = [(0, 0, 0)] + [(0, 1, k) for k in turns]
    second += [(k, None, 0) for k in turns] + [(rows // 2, None, k) for k in turns]
    return first, second


def place_pieces(n, rows, pieces, w_parts):
    nc, half = n // 2, rows // 2
    _, q, _ = place_in_seq()
    r, b_row, a_row, diagonal = place_in_rows(rows)
    own, near = pieces[:2]
    turns = range(1, half)
    held = [(own.at[g], g, r) for g in range(2)]
    kinds = [(0, a_row(-k)) for k in turns] + [(1, b_row)]
    kinds += [(0, b_row)] + [(1, a_row(-k)) for k in turns]
    kinds += [(0, diagonal(-k)) for k in turns] + [(1, diagonal(-k)) for k in turns]
    held += [(piece, g, hold) for piece, (g, hold) in zip(pieces[2:], kinds)]
    out = [(near, w_parts.at[:, pl.ds(2 * q, 2)])]
    for i in range(1, nc):
        pair = pl.ds(2 * near_first(i, q, nc), 2)
        out += [(src.at[pair], w_parts.at[g, pair, hold]) for src, g, hold in held]
    return out


def feed_forward(n, rows, pieces, u, inner, gy0, gy1, wd, a, b, m, ad, bd, md, sq, gram, collective_id):
    nc = n // 2
    _, tokens, width = u.shape
    units = wd.shape[0]
    f32, low = jnp.float32, jnp.bfloat16
    shape = jax.ShapeDtypeStruct
    vmem = pl.BlockSpec(memory_space=pltpu.VMEM)
    hbm = pl.BlockSpec(memory_space=pl.ANY)
    dma = pltpu.SemaphoreType.DMA
    line = pltpu.VMEM((nc, tokens, width), low)
    pair = pltpu.VMEM((2, 2, tokens, width), low)
    part = pieces[0].shape[2]
    copies = 2 + (n // 2 - 1) * (2 + 2 * rows - 2)
    count = len(pieces)

    def kernel(*refs):
        ffn_kernel(n, rows, refs[:count], *refs[count:])

    return pl.pallas_call(
        kernel,
        out_shape=(
            shape((tokens, width), f32),
            pltpu.HBM((n, tokens // 2, width), low),
            pltpu.HBM((n, tokens // 2, width), low),
            shape((2, 16, width), f32),
            shape((2, 16, units), f32),
            shape((2, 1, units), f32),
            shape((2, 1, units), f32),
            shape((16, units), f32),
            shape((16, width), f32),
            shape((1, width), f32),
            shape((1, width), f32),
        ),
        in_specs=[hbm] * (count + 5) + [vmem] * 8,
        out_specs=(vmem, hbm, hbm) + (vmem,) * 8,
        scratch_shapes=[
            pltpu.VMEM((2, n, rows, part, units), low),
            pltpu.VMEM((units, width), low),
            pair,
            pltpu.VMEM((2, 2, tokens, 128), low),
            pair,
            pair,
            line, line, line, line, line,
            pltpu.VMEM((2, 1, units), f32),
            pltpu.VMEM((2, 16, units), f32),
            pltpu.VMEM((n, 1, width), f32),
            dma((copies,)), dma((4, 2)), dma((2, 2)), dma((n,)), dma((n,)),
        ] + [dma((nc,))] * 6,
        compiler_params=pltpu.CompilerParams(
            collective_id=collective_id, has_side_effects=True, vmem_limit_bytes=60 << 20
        ),
        cost_estimate=pl.CostEstimate(
            flops=12 * n * tokens * width * units, transcendentals=n * tokens * units,
            bytes_accessed=32 << 20,
        ),
        name="feed_forward",
    )(*pieces, u, inner, gy0, gy1, wd, a, b, m, ad, bd, md, sq, gram)

def reduce_kernel(n, rows, ga_qkv, ga_o, gb_qkv, gb_o, ga_gu, gb_d, gm_qkv, gm_o, gm_d, gb_gu, gm_gu, n_gu, ga_d,
                  whole, units_all, part, from_sib, mid, from_rows, from_line, line_out, units, units_in,
                  sib_out, sib_in, row_out, row_in, line_send, line_in, back_send, back_in, wide_send, wide_in,
                  pass_send, pass_in):
    nc = n // 2
    f32, low = jnp.float32, jnp.bfloat16
    s, q, c = place_in_seq()
    sibling = s + 1 - 2 * c
    r = lax.axis_index("rows")
    width = ga_o.shape[1]
    cols = width // (2 * rows)
    kv = (gb_qkv.shape[1] - width) // 2
    height = part.shape[2]
    piece = height // nc
    unit_rows = units.shape[1]
    size = units.shape[2]

    barrier = pltpu.get_barrier_semaphore()
    for t in range(1, n):
        pl.semaphore_signal(barrier, inc=1, device_id=(r, lax.rem(s + t, n)), device_id_type=MESH)
    for t in range(1, rows):
        pl.semaphore_signal(barrier, inc=1, device_id=(lax.rem(r + t, rows), s), device_id_type=MESH)

    gb_k, gb_v = gb_qkv[:, width : width + kv], gb_qkv[:, width + kv :]
    small = jnp.concatenate(
        [
            jnp.concatenate([gb_k[:8], gb_k[8:], gb_v[:8], gb_v[8:]], axis=1),
            gm_qkv[:, :width],
            gm_o[...],
            gm_d[...],
            jnp.concatenate([gm_qkv[:, width:], jnp.zeros((1, width - 2 * kv), f32)], axis=1),
            jnp.zeros((4, width), f32),
        ],
        axis=0,
    )
    groups = [ga_qkv[0], ga_qkv[1], ga_qkv[2], ga_o[...], gb_qkv[:, :width], gb_o[...], ga_gu[0], ga_gu[1], gb_d[...], small]
    for j in range(2 * rows):
        for g, value in enumerate(groups):
            part[j % 2, j // 2, 16 * g : 16 * g + 16] = value[:, cols * j : cols * (j + 1)].astype(low)
        if height > 160:
            part[j % 2, j // 2, 160:] = jnp.zeros((height - 160, cols), low)
    n_high = [n_gu[g].astype(low).astype(f32) for g in range(2)]
    n_rest = [n_gu[g] - n_high[g] for g in range(2)]
    tops = jnp.concatenate(
        [gm_gu[0], gm_gu[1]]
        + [v * (1.0 / rows) for v in (n_high[0], n_rest[0], n_high[1], n_rest[1])]
        + [jnp.zeros((2, size), f32)],
        axis=0,
    )
    blocks = [gb_gu[0][:8], gb_gu[0][8:], gb_gu[1][:8], gb_gu[1][8:], ga_d[:8], ga_d[8:], tops, jnp.zeros((8, size), f32)]
    per = unit_rows // 8
    for j in range(rows):
        units[j] = jnp.concatenate(blocks[per * j : per * (j + 1)], axis=0).astype(low)
    pl.semaphore_wait(barrier, n - 1 + rows - 1)

    def to_sibling():
        return remote(part.at[1 - c], from_sib, sib_out.at[0], sib_in.at[0], r, sibling)

    def member(t):
        return lax.rem(r + t + rows, rows)

    def row_send(t):
        return remote(mid.at[member(t)], from_rows.at[t], row_out.at[0, t], row_in.at[0, t], member(t), s)

    def unit_send(t):
        return remote(units.at[member(t)], units_in.at[t], row_out.at[1, t], row_in.at[1, t], member(t), s)

    def chip(t):
        return lax.rem(q + t + nc, nc)

    def line_part(t):
        return remote(line_out.at[chip(t)], from_line.at[t], line_send.at[t], line_in.at[t], r, 2 * chip(t) + c)

    def back(t, slot):
        return remote(whole.at[r, c, slot], whole.at[r, c, slot], back_send.at[0, t], back_in.at[0, t], r, 2 * chip(t) + c)

    def unit_back(t, slot):
        return remote(
            units_all.at[r, c, slot], units_all.at[r, c, slot], back_send.at[1, t], back_in.at[1, t], r, 2 * chip(t) + c
        )

    def wide(t, row):
        return remote(whole.at[row, c], whole.at[row, c], wide_send.at[0, t], wide_in.at[0, t], member(t), s)

    def unit_wide(t, row):
        return remote(units_all.at[row, c], units_all.at[row, c], wide_send.at[1, t], wide_in.at[1, t], member(t), s)

    def hand(t, row, core):
        return remote(whole.at[row, core], whole.at[row, core], pass_send.at[0, t], pass_in.at[0, t], r, sibling)

    def unit_hand(t, row, core):
        return remote(units_all.at[row, core], units_all.at[row, core], pass_send.at[1, t], pass_in.at[1, t], r, sibling)

    to_sibling().start()
    for t in range(1, rows):
        unit_send(t).start()
    to_sibling().wait_recv()
    for t in range(rows):
        mid[member(t)] = (part[c, member(t)].astype(f32) + from_sib[member(t)].astype(f32)).astype(low)
        if t:
            row_send(t).start()
    unit_sum = units[r].astype(f32)
    for t in range(1, rows):
        unit_send(t).wait_recv()
        unit_sum = unit_sum + units_in[t].astype(f32)
    units_all[r, c, q] = unit_sum.astype(low)
    for t in range(1, nc):
        unit_back(t, q).start()
    total = mid[r].astype(f32)
    for t in range(1, rows):
        row_send(t).wait_recv()
        total = total + from_rows[t].astype(f32)
    for p in range(nc):
        line_out[p] = total[piece * p : piece * (p + 1)].astype(low)
    for t in range(1, nc):
        line_part(t).start()
    own = line_out[q].astype(f32)
    for t in range(1, nc):
        line_part(t).wait_recv()
        own = own + from_line[t].astype(f32)
    whole[r, c, q] = own.astype(low)
    for t in range(1, nc):
        back(t, q).start()
    for t in range(1, nc):
        back(t, chip(-t)).wait_recv()
        unit_back(t, chip(-t)).wait_recv()
    for t in range(1, rows):
        wide(t, r).start()
        unit_wide(t, r).start()
    hand(0, r, c).start()
    unit_hand(0, r, c).start()
    for t in range(1, rows):
        wide(t, member(-t)).wait_recv()
        hand(t, member(-t), c).start()
        unit_wide(t, member(-t)).wait_recv()
        unit_hand(t, member(-t), c).start()
    for t in range(rows):
        hand(t, member(-t), 1 - c).wait_recv()
        unit_hand(t, member(-t), 1 - c).wait_recv()

    to_sibling().wait_send()
    for t in range(1, rows):
        row_send(t).wait_send()
        unit_send(t).wait_send()
        wide(t, r).wait_send()
        unit_wide(t, r).wait_send()
    for t in range(1, nc):
        line_part(t).wait_send()
        back(t, q).wait_send()
        unit_back(t, q).wait_send()
    for t in range(rows):
        hand(t, member(-t), c).wait_send()
        unit_hand(t, member(-t), c).wait_send()


def sum_gradients(n, rows, full, own_units, collective_id):
    nc = n // 2
    width, size = full[1].shape[1], own_units[3].shape[1]
    cols = width // (2 * rows)
    height = -(-160 // (8 * nc)) * 8 * nc
    unit_rows = 64 // rows
    low = jnp.bfloat16
    vmem = pl.BlockSpec(memory_space=pltpu.VMEM)
    dma = pltpu.SemaphoreType.DMA
    block = (rows, height, cols)
    return pl.pallas_call(
        functools.partial(reduce_kernel, n, rows),
        out_shape=(
            jax.ShapeDtypeStruct((rows, 2, nc, height // nc, cols), low),
            jax.ShapeDtypeStruct((rows, 2, nc, unit_rows, size), low),
        ),
        in_specs=[vmem] * 13,
        out_specs=(vmem,) * 2,
        scratch_shapes=[
            pltpu.VMEM((2, *block), low),
            pltpu.VMEM(block, low),
            pltpu.VMEM(block, low),
            pltpu.VMEM(block, low),
            pltpu.VMEM((nc, height // nc, cols), low),
            pltpu.VMEM((nc, height // nc, cols), low),
            pltpu.VMEM((rows, unit_rows, size), low),
            pltpu.VMEM((rows, unit_rows, size), low),
            dma((1,)), dma((1,)), dma((2, rows)), dma((2, rows)), dma((nc,)), dma((nc,)),
            dma((2, nc)), dma((2, nc)), dma((2, rows)), dma((2, rows)), dma((2, rows)), dma((2, rows)),
        ],
        compiler_params=pltpu.CompilerParams(
            collective_id=collective_id, has_side_effects=True, vmem_limit_bytes=48 << 20
        ),
        cost_estimate=pl.CostEstimate(flops=0, transcendentals=0, bytes_accessed=64 << 20),
        name="sum_gradients",
    )(*full, *own_units)


def finish_kernel(n, rows, whole, units_all, x1, before_0, before_1, m_attn, n_attn, m_d, n_d, m_gu,
                  o_out, o_ga, o_gb_qo, o_gb_kv, o_gm_q, o_gm_kv, o_gm_o, o_ga_gu, o_gb_gu, o_gm_gu, o_ga_d, o_gb_d,
                  o_gm_d, o_stats, n_gu):
    f32 = jnp.float32
    nc = n // 2
    width = o_gb_d.shape[1]
    kv = o_gb_kv.shape[2]
    cols = width // (2 * rows)
    size = units_all.shape[4]
    per = units_all.shape[3] // 8
    half = x1.shape[0] // 2
    for k, before in enumerate((before_0, before_1)):
        own = slice(half * k, half * (k + 1))
        o_out[own] = (x1[own] + before[...].astype(f32) * (m_d[...] / n_d[...])).astype(o_out.dtype)
    for j in range(2 * rows):
        block = jnp.concatenate([whole[j // 2, j % 2, p].astype(f32) for p in range(nc)], axis=0)
        at = slice(cols * j, cols * (j + 1))
        for g in range(4):
            o_ga[g, :, at] = block[16 * g : 16 * g + 16]
        o_gb_qo[0, :, at] = block[64:80]
        o_gb_qo[1, :, at] = block[80:96]
        o_ga_gu[0, :, at] = block[96:112]
        o_ga_gu[1, :, at] = block[112:128]
        o_gb_d[:, at] = block[128:144]
        which, start = divmod(cols * j, kv)
        o_gb_kv[which // 2, 8 * (which % 2) : 8 * (which % 2) + 8, start : start + cols] = block[144:152]
        o_gm_q[at] = block[152]
        o_gm_o[at] = block[153]
        o_gm_d[at] = block[154]
        if which < 2:
            o_gm_kv[which : which + 1, start : start + cols] = block[155:156]
    for j in range(rows):
        for dev in range(n):
            block = units_all[j, dev % 2, dev // 2].astype(f32)
            at = slice(size * dev, size * (dev + 1))
            for t in range(per):
                rows8, place = block[8 * t : 8 * t + 8], per * j + t
                half = slice(8 * (place % 2), 8 * (place % 2) + 8)
                if place < 4:
                    o_gb_gu[place // 2, half, at] = rows8
                elif place < 6:
                    o_ga_d[half, at] = rows8
                elif place == 6:
                    o_gm_gu[:, at] = rows8[:2]
                    n_gu[0:1, at] = rows8[2:3] + rows8[3:4]
                    n_gu[1:2, at] = rows8[4:5] + rows8[5:6]


    row = lax.broadcasted_iota(jnp.int32, o_stats.shape, 0)
    col = lax.broadcasted_iota(jnp.int32, o_stats.shape, 1)
    bounds = [(0, width), (width, width + kv), (width + kv, width + 2 * kv), (width + 2 * kv, 2 * width + 2 * kv)]
    both = [(m_attn[:, i:j], n_attn[:, i:j]) for i, j in bounds]
    both += [(m_gu[g : g + 1, :], n_gu[g : g + 1, :]) for g in range(2)] + [(m_d[...], n_d[...])]
    stats = jnp.zeros(o_stats.shape, f32)
    for p, (m, norm) in enumerate(both):
        drift = jnp.mean(jnp.square(m - norm), axis=1, keepdims=True)
        drift = jnp.sqrt(drift) / jnp.sqrt(jnp.mean(jnp.square(m), axis=1, keepdims=True) + 1e-06)
        stats = jnp.where((row == p) & (col == 0), drift, stats)
        stats = jnp.where((row == p) & (col == 1), jnp.mean(norm, axis=1, keepdims=True), stats)
    o_stats[...] = stats


def finish(n, rows, sums, x1, before_0, before_1, m_attn, n_attn, m_d, n_d, m_gu):
    tokens, width = x1.shape
    kv = (m_attn.shape[1] - 2 * width) // 2
    units = m_gu.shape[1]
    shape = lambda *dims: pltpu.HBM(dims, jnp.float32)
    vmem = pl.BlockSpec(memory_space=pltpu.VMEM)
    return pl.pallas_call(
        functools.partial(finish_kernel, n, rows),
        out_shape=(
            pltpu.HBM((tokens, width), jnp.bfloat16), shape(4, 16, width), shape(2, 16, width), shape(2, 16, kv),
            shape(width), shape(2, kv), shape(width), shape(2, 16, width), shape(2, 16, units), shape(2, units),
            shape(16, units), shape(16, width), shape(width), shape(7, 2),
        ),
        in_specs=[vmem] * 2 + [pl.BlockSpec()] * 8,
        scratch_shapes=[pltpu.VMEM((2, units), jnp.float32)],
        compiler_params=pltpu.CompilerParams(vmem_limit_bytes=40 << 20),
        cost_estimate=pl.CostEstimate(flops=0, transcendentals=0, bytes_accessed=8 << 20),
        name="finish",
    )(*sums, x1, before_0, before_1, m_attn, n_attn, m_d, n_d, m_gu)

def local(
    layer_input,
    output_gradient,
    norm_gain_vectors,
    query_output_frozen,
    key_value_frozen,
    gate_up_frozen,
    down_frozen_weight,
    attention_adapter_a,
    query_output_adapter_b,
    key_value_adapter_b,
    query_magnitude,
    key_value_magnitude,
    output_magnitude,
    gate_up_adapter_a,
    gate_up_adapter_b,
    gate_up_magnitude,
    down_adapter_a,
    down_adapter_b,
    down_magnitude,
    prompt_length_list,
    response_length_list,
):
    pair_rows, span_len, model_width = layer_input.shape
    token_count = pair_rows * span_len
    kv_width = KV_HEADS * HEAD_DIM
    seq_size = lax.axis_size("seq")
    rows_size = lax.axis_size("rows")
    seq_index = lax.axis_index("seq")
    f32 = jnp.float32

    x = layer_input.reshape(token_count, model_width)
    gain_attn, gain_ffn = norm_gain_vectors[:1], norm_gain_vectors[1:]
    weights, gu_own, gu_near, sq_d, grams, u1, inner_1 = gather_weights(
        seq_size, rows_size, query_output_frozen, key_value_frozen, gate_up_frozen,
        down_frozen_weight, down_adapter_a, down_adapter_b, x, gain_attn, attention_adapter_a,
        gate_up_adapter_a, 1,
    )
    shares_1, shares_2 = share_plan(rows_size)
    grad_out_rows = output_gradient.reshape(token_count, model_width)
    half_0, half_1 = jnp.split(grad_out_rows, 2)
    weights, half_0 = lax.optimization_barrier((weights, half_0))
    gy_0 = lax.all_gather(half_0, "seq", axis=0, tiled=False)

    b_attn = jnp.concatenate(
        [
            query_output_adapter_b[0],
            key_value_adapter_b[0],
            key_value_adapter_b[1],
            query_output_adapter_b[1],
        ],
        axis=1,
    )
    m_attn = jnp.concatenate(
        [query_magnitude, key_value_magnitude[0], key_value_magnitude[1], output_magnitude]
    )[None]
    m_d = down_magnitude[None]

    positions = seq_index * span_len + jnp.arange(span_len, dtype=jnp.int32)
    half_dim = HEAD_DIM // 2
    frequency = 500000.0 ** (-(jnp.arange(half_dim, dtype=f32) * 2.0) / HEAD_DIM)
    angles = positions.astype(f32)[:, None] * frequency[None, :]
    cosine = jnp.tile(jnp.cos(angles), (pair_rows, 4))
    sine = jnp.tile(jnp.sin(angles), (pair_rows, 4))
    valid_len = prompt_length_list[0] + response_length_list

    before_qkv, q, kv, n_attn, cross_attn = project_qkv(
        u1, inner_1, grams, attention_adapter_a, weights, b_attn, m_attn, cosine, sine
    )
    (kv_all, sq_all), gu_1 = gather_seq(
        seq_size, rows_size, [kv, sq_d], 2, (gu_own,), shares_1
    )
    kv_all, half_1 = lax.optimization_barrier((kv_all, half_1))
    gy_1 = lax.all_gather(half_1, "seq", axis=0, tiled=False)
    kv_all = kv_all.reshape(seq_size, pair_rows, span_len, 2 * kv_width)
    q = q.reshape(pair_rows, span_len, model_width)
    att, shares = attend(q, kv_all, valid_len)
    att = att.reshape(token_count, model_width)
    before_o, x1, u2, inner_2 = project_out(
        att, attention_adapter_a, weights, b_attn, m_attn, n_attn, x, gain_ffn, gate_up_adapter_a
    )

    (u2_all, inner_all), gu_2 = gather_seq(
        seq_size, rows_size, [u2, inner_2], 3, (gu_own, *gu_1), shares_2
    )
    in_grad, down_0, down_1, ga_gu, gb_gu, gm_gu, n_gu, ga_d, gb_d, gm_d, n_d = feed_forward(
        seq_size, rows_size, (gu_own, gu_near, *gu_1, *gu_2), u2_all, inner_all, gy_0, gy_1,
        down_frozen_weight, gate_up_adapter_a, gate_up_adapter_b, gate_up_magnitude, down_adapter_a,
        down_adapter_b, m_d, sq_all, grams, 4,
    )
    flat = lambda v: v.reshape(-1, model_width)
    before_0 = lax.psum_scatter(flat(down_0), "seq", scatter_dimension=0, tiled=True)

    gx1, grad_att, ga_o, gb_o, gm_o = out_back(
        in_grad, x1, gain_ffn, grad_out_rows, before_o, att, attention_adapter_a, b_attn, m_attn,
        n_attn, cross_attn, weights,
    )
    gq, gkv = attend_back(q, kv_all, shares, grad_att.reshape(q.shape))
    gkv = scatter_seq(seq_size, gkv.reshape(seq_size, token_count, 2 * kv_width), 5)
    gkv, down_1 = lax.optimization_barrier((gkv, down_1))
    before_1 = lax.psum_scatter(flat(down_1), "seq", scatter_dimension=0, tiled=True)
    grad_inputs, ga_qkv, gb_qkv, gm_qkv = qkv_back(
        gq.reshape(token_count, model_width), gkv, cosine, sine, before_qkv, u1, inner_1,
        attention_adapter_a, b_attn, m_attn, n_attn, cross_attn, x, gain_attn, gx1, weights,
    )

    sums = sum_gradients(
        seq_size, rows_size,
        (ga_qkv, ga_o, gb_qkv, gb_o, ga_gu, gb_d, gm_qkv, gm_o, gm_d),
        (gb_gu, gm_gu, n_gu, ga_d),
        6,
    )
    layer_result, *summed, stats = finish(
        seq_size, rows_size, sums, x1, before_0, before_1, m_attn, n_attn, m_d, n_d, gate_up_magnitude
    )
    shape = (pair_rows, span_len, model_width)
    return (layer_result.reshape(shape), grad_inputs.reshape(shape), *summed, stats)

def solution(mesh):
    return jax.shard_map(
        local,
        mesh=mesh,
        in_specs=(
            P("rows", "seq", None),
            P("rows", "seq", None),
            P(),
            P(None, "seq", None),
            P(None, "seq", None),
            P(None, "seq", None),
            P("seq", None),
            P(),
            P(),
            P(),
            P(),
            P(),
            P(),
            P(),
            P(),
            P(),
            P(),
            P(),
            P(),
            P("rows"),
            P("rows"),
        ),
        out_specs=(
            P("rows", "seq", None),
            P("rows", "seq", None),
            P(),
            P(),
            P(),
            P(),
            P(),
            P(),
            P(),
            P(),
            P(),
            P(),
            P(),
            P(),
            P(),
        ),
        check_vma=False,
    )
```

```python
import functools

import jax
import jax.numpy as jnp
from jax import lax
from jax.experimental import pallas as pl
from jax.experimental.pallas import tpu as pltpu
from jax.sharding import PartitionSpec as P

HEADS = 32
KV_HEADS = 8
HEAD_DIM = 64
ADAPTER_RANK = 16
ALPHA = 32
SCALE = ALPHA / ADAPTER_RANK
TILE = 512

highest = lax.Precision.HIGHEST
last_last = (((1,), (1,)), ((), ()))
first_first = (((0,), (0,)), ((), ()))

def dot_f32(a, b):
    return jnp.dot(a, b, preferred_element_type=jnp.float32)


def dot_nt(a, b):
    return lax.dot_general(a, b, last_last, preferred_element_type=jnp.float32)


def dot_tn(a, b):
    return lax.dot_general(a, b, first_first, preferred_element_type=jnp.float32)


def in_hbm(*arrays):
    return [pltpu.with_memory_space_constraint(v, pltpu.HBM) for v in arrays]


def unit_rms(v):
    return lax.rsqrt(jnp.mean(v * v, axis=-1, keepdims=True) + 1e-05)


def rms_back(v, gain, upstream):
    r = unit_rms(v)
    scaled = gain * upstream
    return r * scaled - v * (r * r * r) * jnp.mean(scaled * v, axis=-1, keepdims=True)


def turn(z, cosine, sine):
    width = z.shape[1]
    lane = lax.broadcasted_iota(jnp.int32, z.shape, 1)
    half = HEAD_DIM // 2
    other = jnp.where(
        lax.rem(lane, HEAD_DIM) < half, -pltpu.roll(z, width - half, 1), pltpu.roll(z, half, 1)
    )
    copies = width // cosine.shape[1]
    return z * jnp.tile(cosine, (1, copies)) + other * jnp.tile(sine, (1, copies))


def column_squares(w):
    return jnp.sum(jnp.square(w.astype(jnp.float32)), axis=0, keepdims=True)


def two_terms(value):
    high = value.astype(jnp.bfloat16)
    return jnp.concatenate([high, (value - high.astype(jnp.float32)).astype(jnp.bfloat16)], axis=0)


def dot_two(terms, b):
    both = dot_f32(terms, b)
    half = both.shape[0] // 2
    return both[:half] + both[half:]


def column_norms(w, gram, b, cross):
    b_wide = b.astype(jnp.float32)
    gram_b = dot_two(gram, b)
    squares = column_squares(w) + 2.0 * SCALE * jnp.sum(b_wide * cross, axis=0, keepdims=True)
    squares = squares + SCALE * SCALE * jnp.sum(b_wide * gram_b, axis=0, keepdims=True)
    return jnp.sqrt(squares + 1e-06), cross + SCALE * gram_b


def project_kernel(kv_tiles, u_ref, inner_ref, gram_ref, a_ref, w_ref, b_ref, m_ref, cos_ref, sin_ref,
                   before_ref, q_ref, kv_ref, n_ref, cross_ref):
    j = pl.program_id(0)
    q_tiles, last = kv_tiles
    a = a_ref[0].astype(jnp.bfloat16)
    b = b_ref[...].astype(jnp.bfloat16)
    w = w_ref[0]
    rows = u_ref.shape[0]

    @pl.when(j <= last)
    def _():
        both = dot_f32(jnp.concatenate([u_ref[...], a], axis=0), w)
        norm, cross = column_norms(w, gram_ref[0], b, both[rows:])
        n_ref[...] = norm
        cross_ref[...] = cross
        before = both[:rows] + SCALE * dot_f32(inner_ref[0], b)
        before_ref[...] = before
        y = before * (m_ref[...] / norm)

        @pl.when(j < q_tiles)
        def _():
            q_ref[...] = turn(y, cos_ref[...], sin_ref[...]).astype(jnp.bfloat16)

        @pl.when(j == q_tiles)
        def _():
            kv_ref[...] = turn(y, cos_ref[...], sin_ref[...]).astype(jnp.bfloat16)

        @pl.when(j > q_tiles)
        def _():
            kv_ref[...] = y.astype(jnp.bfloat16)

    @pl.when(j > last)
    def _():
        norm, cross = column_norms(w, gram_ref[0], b, dot_f32(a, w))
        n_ref[...] = norm
        cross_ref[...] = cross


def project_qkv(u, inner, grams, a, weights, b, m, cosine, sine):
    rows, width = u.shape
    cols = b.shape[1]
    per_half = weights.shape[2] // TILE
    q_tiles = width // TILE
    k_cols = weights.shape[2] - width
    last = q_tiles + 2 * k_cols // TILE - 1
    full = lambda shape: pl.BlockSpec(shape, lambda j: (0,) * len(shape))
    col = lambda height: pl.BlockSpec((height, TILE), lambda j: (0, j))
    which = lambda j: jnp.where(j < q_tiles, 0, jnp.where(j > last, 3, 1 + j - q_tiles))
    f32, low = jnp.float32, jnp.bfloat16
    return pl.pallas_call(
        functools.partial(project_kernel, (q_tiles, last)),
        out_shape=(
            pltpu.HBM((rows, width + 2 * k_cols), f32),
            pltpu.HBM((rows, width), low),
            pltpu.HBM((rows, 2 * k_cols), low),
            pltpu.HBM((1, cols), f32),
            pltpu.HBM((16, cols), f32),
        ),
        grid=(cols // TILE,),
        in_specs=[
            full((rows, width)),
            pl.BlockSpec((1, rows, 16), lambda j: (jnp.minimum(which(j), 2), 0, 0)),
            pl.BlockSpec((1, 32, 16), lambda j: (which(j), 0, 0)),
            pl.BlockSpec((1, 16, width), lambda j: (which(j), 0, 0)),
            pl.BlockSpec((1, width, TILE), lambda j: (j // per_half, 0, j % per_half)),
            col(16),
            col(1),
            full(cosine.shape),
            full(sine.shape),
        ],
        out_specs=(
            pl.BlockSpec((rows, TILE), lambda j: (0, jnp.minimum(j, last))),
            pl.BlockSpec((rows, TILE), lambda j: (0, jnp.minimum(j, q_tiles - 1))),
            pl.BlockSpec((rows, TILE), lambda j: (0, jnp.clip(j - q_tiles, 0, last - q_tiles))),
            col(1),
            col(16),
        ),
        compiler_params=pltpu.CompilerParams(vmem_limit_bytes=40 << 20),
        cost_estimate=pl.CostEstimate(
            flops=2 * rows * width * cols, transcendentals=0, bytes_accessed=2 * width * cols
        ),
        name="project_qkv",
    )(*in_hbm(u), inner, grams, *in_hbm(a, weights, b), m, cosine, sine)


def out_kernel(att_ref, a_ref, w_ref, b_ref, m_ref, n_ref, x_ref, gain_ref, next_ref,
               before_ref, x1_ref, u2_ref, inner_ref):
    t = pl.program_id(0)
    a = a_ref[0].astype(jnp.bfloat16)
    b = b_ref[...].astype(jnp.bfloat16)
    inner = dot_nt(att_ref[...], a).astype(jnp.bfloat16)
    before = dot_f32(att_ref[...], w_ref[0]) + SCALE * dot_f32(inner, b)
    before_ref[...] = before
    x1_ref[:, pl.ds(pl.multiple_of(t * TILE, TILE), TILE)] = (
        x_ref[...].astype(jnp.float32) + before * (m_ref[...] / n_ref[...])
    )

    @pl.when(t == pl.num_programs(0) - 1)
    def _():
        v = x1_ref[...]
        u2 = (v * unit_rms(v) * gain_ref[...]).astype(jnp.bfloat16)
        u2_ref[...] = u2
        following = next_ref[...].reshape(-1, u2.shape[1]).astype(jnp.bfloat16)
        inner_ref[...] = jnp.zeros_like(inner_ref)
        inner_ref[:, : following.shape[0]] = dot_nt(u2, following).astype(jnp.bfloat16)


def project_out(att, a, weights, b, m, norms, x, gain, following):
    rows, width = att.shape
    tiles = width // TILE
    skip = (weights.shape[2] - width) // TILE
    full = lambda shape: pl.BlockSpec(shape, lambda t: (0,) * len(shape))
    col = lambda height: pl.BlockSpec((height, TILE), lambda t: (0, t))
    ahead = b.shape[1] // TILE - tiles
    later = lambda height: pl.BlockSpec((height, TILE), lambda t: (0, ahead + t))
    f32 = jnp.float32
    return pl.pallas_call(
        out_kernel,
        out_shape=(
            pltpu.HBM((rows, width), f32),
            pltpu.HBM((rows, width), f32),
            pltpu.HBM((rows, width), jnp.bfloat16),
            pltpu.HBM((rows, 128), jnp.bfloat16),
        ),
        grid=(tiles,),
        in_specs=[
            full((rows, width)),
            pl.BlockSpec((1, 16, width), lambda t: (3, 0, 0)),
            pl.BlockSpec((1, width, TILE), lambda t: (1, 0, skip + t)),
            later(16),
            later(1),
            later(1),
            col(rows),
            full((1, width)),
            full(following.shape),
        ],
        out_specs=(col(rows), full((rows, width)), full((rows, width)), full((rows, 128))),
        compiler_params=pltpu.CompilerParams(vmem_limit_bytes=40 << 20),
        cost_estimate=pl.CostEstimate(
            flops=2 * rows * width * width, transcendentals=0, bytes_accessed=2 * width * width
        ),
        name="project_out",
    )(*in_hbm(att, a, weights, b), m, norms, *in_hbm(x), gain, *in_hbm(following))


def out_back_kernel(in_ref, x1_ref, gain_ref, gy_ref, before_ref, att_ref, a_ref, b_ref, m_ref, n_ref, cross_ref,
                    w_ref, gx_ref, gatt_ref, ga_ref, gb_ref, gm_ref, lhs, gi, tail):
    t = pl.program_id(0)
    rows, width = gx_ref.shape
    low = jnp.bfloat16
    a = a_ref[0].astype(low)
    o_cols = slice(b_ref.shape[1] - width, b_ref.shape[1])

    @pl.when(t == 0)
    def _():
        gx = gy_ref[...].astype(jnp.float32) + rms_back(x1_ref[...], gain_ref[...], in_ref[...])
        gx_ref[...] = gx
        norm, m = n_ref[:, o_cols], m_ref[:, o_cols]
        gb = (gx * (m / norm)).astype(low)
        lhs[:rows] = gb
        b = b_ref[:, o_cols].astype(low)
        gi[...] = (SCALE * dot_nt(gb, b)).astype(low)
        gm = jnp.sum(gx * before_ref[...], axis=0, keepdims=True) / norm
        gm_ref[...] = gm
        c = -gm * m / (norm * norm)
        weighted = (b.astype(jnp.float32) * c).astype(low)
        lhs[rows:] = weighted
        tail[...] = two_terms(dot_nt(weighted, b))
        inner = dot_nt(att_ref[...], a).astype(low)
        gb_ref[...] = SCALE * dot_tn(inner, gb) + SCALE * c * cross_ref[:, o_cols]

    span = pl.ds(pl.multiple_of(t * TILE, TILE), TILE)
    a_tile = a_ref[0, :, span].astype(low)
    gi_low = gi[...]
    back = dot_nt(lhs[...], w_ref[0, :, w_ref.shape[2] - width :])
    gatt_ref[...] = (back[:rows] + dot_f32(gi_low, a_tile)).astype(low)
    spread = back[rows:] + SCALE * dot_two(tail[...], a_tile)
    ga_ref[...] = dot_tn(gi_low, att_ref[:, span]) + SCALE * spread


def out_back(in_grad, x1, gain, gy, before, att, a, b, m, norms, cross, weights):
    rows, width = x1.shape
    tiles = width // TILE
    full = lambda shape: pl.BlockSpec(shape, lambda t: (0,) * len(shape))
    col = lambda height: pl.BlockSpec((height, TILE), lambda t: (0, t))
    f32, low = jnp.float32, jnp.bfloat16
    wide = full((rows, width))
    return pl.pallas_call(
        out_back_kernel,
        out_shape=(
            pltpu.HBM((rows, width), f32),
            pltpu.HBM((rows, width), low),
            jax.ShapeDtypeStruct((16, width), f32),
            jax.ShapeDtypeStruct((16, width), f32),
            jax.ShapeDtypeStruct((1, width), f32),
        ),
        grid=(tiles,),
        in_specs=[wide, wide, full((1, width)), wide, wide, wide,
                  pl.BlockSpec((1, 16, width), lambda t: (3, 0, 0)),
                  full(b.shape), full(m.shape), full(norms.shape), full(cross.shape),
                  pl.BlockSpec((1, TILE, weights.shape[2]), lambda t: (1, t, 0))],
        out_specs=(wide, col(rows), col(16), full((16, width)), full((1, width))),
        scratch_shapes=[
            pltpu.VMEM((rows + 16, width), low),
            pltpu.VMEM((rows, 16), low),
            pltpu.VMEM((32, 16), low),
        ],
        compiler_params=pltpu.CompilerParams(vmem_limit_bytes=48 << 20),
        cost_estimate=pl.CostEstimate(flops=0, transcendentals=0, bytes_accessed=1 << 20),
        name="out_back",
    )(in_grad, *in_hbm(x1), gain, *in_hbm(gy, before, att, a, b), m, norms, *in_hbm(cross, weights))


def qkv_back_kernel(gq_ref, gkv_ref, cos_ref, sin_ref, before_ref, u_ref, inner_ref, a_ref, b_ref, m_ref, n_ref, cross_ref,
                    x_ref, gain_ref, gx_ref, w0_ref, w1_ref,
                    out_ref, ga_ref, gb_ref, gm_ref, lhs0, lhs1, gi, tail):
    t = pl.program_id(0)
    rows, width = gx_ref.shape
    low = jnp.bfloat16
    k_cols = w1_ref.shape[2]
    bounds = [(0, width), (width, width + k_cols), (width + k_cols, width + 2 * k_cols)]

    @pl.when(t == 0)
    def _():
        cosine, sine = cos_ref[...], -sin_ref[...]
        k_parts = [gkv_ref[:, 256 * j : 256 * j + 128] for j in range(k_cols // 128)]
        v_parts = [gkv_ref[:, 256 * j + 128 : 256 * j + 256] for j in range(k_cols // 128)]
        rounded = lambda z: z.astype(low).astype(jnp.float32)
        ups = [
            turn(gq_ref[...].astype(jnp.float32), cosine, sine),
            turn(rounded(jnp.concatenate(k_parts, axis=1)), cosine, sine),
            rounded(jnp.concatenate(v_parts, axis=1)),
        ]
        lhs0[rows:] = jnp.zeros_like(lhs0[rows:])
        lhs1[rows:] = jnp.zeros_like(lhs1[rows:])
        for p, (start, stop) in enumerate(bounds):
            g, norm, m = ups[p], n_ref[:, start:stop], m_ref[:, start:stop]
            b = b_ref[:, start:stop].astype(low)
            gb = (g * (m / norm)).astype(low)
            gm = jnp.sum(g * before_ref[:, start:stop], axis=0, keepdims=True) / norm
            gm_ref[:, start:stop] = gm
            c = -gm * m / (norm * norm)
            weighted = (b.astype(jnp.float32) * c).astype(low)
            gi[:, 16 * p : 16 * p + 16] = (SCALE * dot_nt(gb, b)).astype(low)
            tail[p] = two_terms(dot_nt(weighted, b))
            gb_ref[:, start:stop] = SCALE * dot_tn(inner_ref[p], gb) + SCALE * c * cross_ref[:, start:stop]
            lhs, at = (lhs1, 0) if p == 2 else (lhs0, start)
            lhs[:rows, at : at + stop - start] = gb
            lhs[rows + 16 * p : rows + 16 * p + 16, at : at + stop - start] = weighted

    span = pl.ds(pl.multiple_of(t * TILE, TILE), TILE)
    back = dot_nt(lhs0[...], w0_ref[0]) + dot_nt(lhs1[...], w1_ref[0])
    grad_in = back[:rows]
    for p in range(3):
        a_tile = a_ref[p, :, span].astype(low)
        gi_p = gi[:, 16 * p : 16 * p + 16]
        grad_in = grad_in + dot_f32(gi_p, a_tile)
        spread = back[rows + 16 * p : rows + 16 * p + 16] + SCALE * dot_two(tail[p], a_tile)
        ga_ref[p] = dot_tn(gi_p, u_ref[:, span]) + SCALE * spread
    out_ref[:, span] = grad_in

    @pl.when(t == pl.num_programs(0) - 1)
    def _():
        v = x_ref[...].astype(jnp.float32)
        out_ref[...] = gx_ref[...] + rms_back(v, gain_ref[...], out_ref[...])


def qkv_back(gq, gkv, cosine, sine, before, u, inner, a, b, m, norms, cross, x, gain, gx, weights):
    rows, width = gx.shape
    cols = before.shape[1]
    k_cols = (cols - width) // 2
    tiles = width // TILE
    full = lambda shape: pl.BlockSpec(shape, lambda t: (0,) * len(shape))
    f32, low = jnp.float32, jnp.bfloat16
    wide = full((rows, width))
    return pl.pallas_call(
        qkv_back_kernel,
        out_shape=(
            pltpu.HBM((rows, width), f32),
            jax.ShapeDtypeStruct((3, 16, width), f32),
            jax.ShapeDtypeStruct((16, cols), f32),
            jax.ShapeDtypeStruct((1, cols), f32),
        ),
        grid=(tiles,),
        in_specs=[wide, full(gkv.shape), full(cosine.shape), full(sine.shape), full((rows, cols)), wide, full(inner.shape),
                  full(a.shape), full(b.shape), full(m.shape), full(norms.shape), full(cross.shape),
                  wide, full((1, width)), wide,
                  pl.BlockSpec((1, TILE, width + k_cols), lambda t: (0, t, 0)),
                  pl.BlockSpec((1, TILE, k_cols), lambda t: (1, t, 0))],
        out_specs=(wide, pl.BlockSpec((3, 16, TILE), lambda t: (0, 0, t)), full((16, cols)), full((1, cols))),
        scratch_shapes=[
            pltpu.VMEM((rows + 48, width + k_cols), low),
            pltpu.VMEM((rows + 48, k_cols), low),
            pltpu.VMEM((rows, 48), low),
            pltpu.VMEM((3, 32, 16), low),
        ],
        compiler_params=pltpu.CompilerParams(vmem_limit_bytes=48 << 20),
        cost_estimate=pl.CostEstimate(flops=0, transcendentals=0, bytes_accessed=1 << 20),
        name="qkv_back",
    )(*in_hbm(gq), gkv, cosine, sine, *in_hbm(before, u), inner, *in_hbm(a, b), m, norms, *in_hbm(cross, x), gain,
      *in_hbm(gx, weights, weights))

MESH = pl.DeviceIdType.MESH


def place_in_seq():
    s = lax.axis_index("seq")
    return s, s // 2, lax.rem(s, 2)


def greet(nc, q, s):
    barrier = pltpu.get_barrier_semaphore()

    def signal(target):
        pl.semaphore_signal(barrier, inc=1, device_id={"seq": target}, device_id_type=MESH)

    sibling = s + 1 - 2 * lax.rem(s, 2)
    signal(sibling)
    pl.when(q > 0)(lambda: signal(s - 2))
    pl.when(q < nc - 1)(lambda: signal(s + 2))
    pl.semaphore_wait(barrier, 1 + jnp.where(q > 0, 1, 0) + jnp.where(q < nc - 1, 1, 0))
    return sibling

def near_first(i, q, nc):
    short = jnp.where(q <= nc - 1 - q, q, nc - 1 - q)
    far = jnp.where(q <= nc - 1 - q, i, nc - 1 - i)
    step = (i + 1) // 2
    near = q - step if i % 2 else q + step
    return jnp.where(i <= 2 * short, near, far)


def place_in_rows(rows):
    half = rows // 2
    r = lax.axis_index("rows")
    a, b = r // 2, lax.rem(r, 2)
    turned = lambda k: 2 * lax.rem(a + k + half, half)
    return r, 2 * a + 1 - b, lambda k: turned(k) + b, lambda k: turned(k) + 1 - b


def greet_all(n, rows):
    s = lax.axis_index("seq")
    r, b_row, a_row, _ = place_in_rows(rows)
    barrier = pltpu.get_barrier_semaphore()
    for t in range(1, n):
        pl.semaphore_signal(
            barrier, inc=1, device_id=(r, lax.rem(s + t, n)), device_id_type=MESH
        )
    pl.semaphore_signal(barrier, inc=1, device_id=(b_row, s), device_id_type=MESH)
    for k in range(1, rows // 2):
        pl.semaphore_signal(barrier, inc=1, device_id=(a_row(k), s), device_id_type=MESH)
    pl.semaphore_wait(barrier, n - 1 + rows // 2)


def remote(src, dst, send, recv, row, seq):
    return pltpu.make_async_remote_copy(
        src_ref=src, dst_ref=dst, send_sem=send, recv_sem=recv,
        device_id=(row, seq), device_id_type=MESH,
    )


def weights_kernel(n, rows, qo, kv, xg, wd_hbm, ad_hbm, bd_hbm, x_hbm, gain_ref, aa_hbm, ag_hbm,
                   wa, gz, near, sq_ref, gram_ref, u_hbm, inner_ref,
                   wd, ad_ref, bd_ref, x_ref, aa_ref, ag_ref, local, edge, a_in, a_sib_in, a_out, a_sib_out, z_in, z_out):
    nc, half = n // 2, rows // 2
    others = half - 1
    units = gz.shape[-1]
    s, q, c = place_in_seq()
    sibling = s + 1 - 2 * c
    r, b_row, a_row, diagonal = place_in_rows(rows)
    greet_all(n, rows)

    both, first, second = pl.ds(0, 2), pl.ds(0, 1), pl.ds(1, 1)
    LINE, FROM_B = 0, 1

    def from_a(k):
        return 1 + k

    def relay_b(k):
        return 1 + others + k

    def relay_a(k):
        return 1 + 2 * others + k

    def a_view(p, core, parts, row):
        return wa.at[parts, 2 * p + core, row]

    def content(kind):
        if kind == LINE:
            return both, r
        if kind == FROM_B:
            return both, b_row
        for k in range(1, half):
            if kind == from_a(k):
                return both, a_row(-k)
            if kind == relay_b(k):
                return second, diagonal(-k)
            if kind == relay_a(k):
                return first, diagonal(-k)

    kinds = 2 + 3 * others

    def a_send(p, parts, row, kind, target_row):
        return remote(
            a_view(p, c, parts, row), a_view(p, c, parts, row),
            a_out.at[p, kind], a_in.at[p, kind], target_row, s,
        )

    def a_arrival(p, kind):
        parts, row = content(kind)
        return a_send(p, parts, row, kind, r)

    def a_to_sibling(p, kind, core):
        parts, row = content(kind)
        return remote(
            a_view(p, core, parts, row), a_view(p, core, parts, row),
            a_sib_out.at[p, kind], a_sib_in.at[p, kind], r, sibling,
        )

    def columns(device):
        return pl.ds(pl.multiple_of(device * units, units), units)

    def z_send(p, core):
        return remote(
            xg.at[:, r, :, columns(2 * p + core)], gz.at[:, s],
            z_out.at[p, core], z_in.at[q, c], r, 2 * p + core,
        )

    def z_arrival(p, core):
        slot = gz.at[:, 2 * p + core]
        return remote(slot, slot, z_out.at[p, core], z_in.at[p, core], r, s)

    def line_send(p, sem, target):
        view = a_view(p, c, both, r)
        return remote(view, view, sem, a_in.at[p, LINE], r, target)

    wide, k_cols = qo.shape[-1], kv.shape[-1]
    blocks = [(qo, 0, 0), (kv, 0, wide), (kv, 1, 0), (qo, 1, k_cols)]

    def own_blocks(part, out):
        for source, i, start in blocks:
            columns_of = pl.ds(start, source.shape[-1])
            out(source.at[i, part], wa.at[i, s, part, :, columns_of])

    def own_line(sem, target):
        own_blocks(
            r, lambda src, dst: remote(src, dst, sem, a_in.at[q, LINE], r, target).start()
        )

    pl.when(q > 0)(lambda: own_line(edge.at[0], s - 2))
    pl.when(q < nc - 1)(lambda: own_line(edge.at[1], s + 2))
    order = [near_first(i, q, nc) for i in range(nc)]
    whole_block = wa.at[:, s]
    sib_a = lambda: remote(whole_block, whole_block, edge.at[2], edge.at[3], r, sibling)
    sib_g = lambda: remote(
        xg.at[:, :, :, columns(sibling)], near.at[:, c], edge.at[4], edge.at[5], r, sibling
    )
    keep_a = pltpu.make_async_copy(whole_block, whole_block, local.at[0])
    keep_g = pltpu.make_async_copy(xg.at[:, :, :, columns(s)], near.at[:, c], local.at[1])
    all_parts = pl.ds(0, rows)
    own_blocks(all_parts, lambda src, dst: remote(src, dst, edge.at[2], edge.at[3], r, sibling).start())
    own_blocks(all_parts, lambda src, dst: pltpu.make_async_copy(src, dst, local.at[0]).start())
    takes = [
        pltpu.make_async_copy(src, dst, local.at[3 + i])
        for i, (src, dst) in enumerate(
            [(x_hbm, x_ref), (aa_hbm, aa_ref), (ag_hbm, ag_ref), (ad_hbm, ad_ref), (bd_hbm, bd_ref), (wd_hbm, wd)]
        )
    ]
    for cp in takes:
        cp.start()
    for cp in takes:
        cp.wait()
    low = jnp.bfloat16
    v = x_ref[...].astype(jnp.float32)
    u = (v * unit_rms(v) * gain_ref[...]).astype(low)
    x_ref[...] = u
    keep_u = pltpu.make_async_copy(x_ref, u_hbm, local.at[2])
    keep_u.start()
    for g in range(4):
        a = aa_ref[g].astype(low)
        gram_ref[g] = two_terms(dot_nt(a, a))
        if g < 3:
            inner_ref[g] = dot_nt(u, a).astype(low)
    for g in range(2):
        a = ag_ref[g].astype(low)
        gram_ref[4 + g] = two_terms(dot_nt(a, a))

    def down_squares():
        a = ad_ref[...].astype(low)
        gram_ref[6] = two_terms(dot_nt(a, a))
        mine = pl.ds(pl.multiple_of(s * wd.shape[0], wd.shape[0]), wd.shape[0])
        cross = dot_f32(ad_ref[:, mine].astype(low), wd[...])
        b_wide = bd_ref[...].astype(low).astype(jnp.float32)
        sq_ref[...] = column_squares(wd[...]) + 2.0 * SCALE * jnp.sum(b_wide * cross, axis=0, keepdims=True)

    for p in order[1:]:
        a_arrival(p, LINE).wait_recv()
        pl.when((p < q) & (q < nc - 1))(
            lambda p=p: line_send(p, a_out.at[p, LINE], s + 2).start()
        )
        pl.when((p > q) & (q > 0))(
            lambda p=p: line_send(p, a_out.at[p, LINE], s - 2).start()
        )
        a_send(p, both, r, FROM_B, b_row).start()
        for k in range(1, half):
            a_send(p, both, r, from_a(k), a_row(k)).start()
        a_to_sibling(p, LINE, c).start()
    for p in order[1:]:
        for core in range(2):
            z_send(p, core).start()
    sib_g().start()
    keep_g.start()
    down_squares()
    keep_u.wait()
    for p in order[1:]:
        a_arrival(p, FROM_B).wait_recv()
        for k in range(1, half):
            a_send(p, first, b_row, relay_a(k), a_row(k)).start()
        a_to_sibling(p, FROM_B, c).start()
        for k in range(1, half):
            a_arrival(p, from_a(k)).wait_recv()
            a_send(p, second, a_row(-k), relay_b(k), b_row).start()
            a_to_sibling(p, from_a(k), c).start()
    for p in order[1:]:
        for k in range(1, half):
            for kind in (relay_b(k), relay_a(k)):
                a_arrival(p, kind).wait_recv()
                a_to_sibling(p, kind, c).start()
    keep_a.wait()
    keep_g.wait()
    sib_a().wait()
    sib_g().wait()
    pl.when(q > 0)(lambda: line_send(q, edge.at[0], s).wait_send())
    pl.when(q < nc - 1)(lambda: line_send(q, edge.at[1], s).wait_send())
    for p in order[1:]:
        pl.when(((p < q) & (q < nc - 1)) | ((p > q) & (q > 0)))(
            lambda p=p: line_send(p, a_out.at[p, LINE], s).wait_send()
        )
        for kind in range(kinds):
            a_to_sibling(p, kind, c).wait_send()
            a_to_sibling(p, kind, 1 - c).wait_recv()
        a_send(p, both, r, FROM_B, b_row).wait_send()
        for k in range(1, half):
            a_send(p, both, r, from_a(k), r).wait_send()
            a_send(p, first, b_row, relay_a(k), r).wait_send()
            a_send(p, second, a_row(-k), relay_b(k), r).wait_send()
        for core in range(2):
            z_send(p, core).wait_send()
            z_arrival(p, core).wait_recv()


def gather_weights(n, rows, qo, kv, xg, wd, ad, bd, x, gain, aa, ag, collective_id):
    nc = n // 2
    _, block, width = qo.shape
    part = block // rows
    cols = width + kv.shape[2]
    qo = qo.reshape(2, rows, part, width)
    kv = kv.reshape(2, rows, part, kv.shape[2])
    xg = xg.reshape(2, rows, part, xg.shape[2])
    units = xg.shape[3] // n
    kinds = 2 + 3 * (rows // 2 - 1)
    dma = pltpu.SemaphoreType.DMA
    anywhere = pl.BlockSpec(memory_space=pltpu.HBM)
    vmem = pl.BlockSpec(memory_space=pltpu.VMEM)
    low = qo.dtype
    wa, gz, near, sq, grams, u, inner = pl.pallas_call(
        functools.partial(weights_kernel, n, rows),
        out_shape=(
            pltpu.HBM((2, n, rows, part, cols), low),
            pltpu.HBM((2, n, part, units), low),
            pltpu.HBM((2, 2, rows, part, units), low),
            jax.ShapeDtypeStruct((1, width), jnp.float32),
            jax.ShapeDtypeStruct((7, 32, 16), low),
            pltpu.HBM(x.shape, low),
            jax.ShapeDtypeStruct((3, x.shape[0], 16), low),
        ),
        in_specs=[anywhere] * 7 + [vmem] + [anywhere] * 2,
        out_specs=(anywhere,) * 3 + (vmem,) * 2 + (anywhere, vmem),
        scratch_shapes=[pltpu.VMEM(v.shape, v.dtype) for v in (wd, ad, bd, x, aa, ag)]
        + [dma((9,)), dma((6,))]
        + [dma((nc, kinds))] * 4
        + [dma((nc, 2))] * 2,
        compiler_params=pltpu.CompilerParams(
            collective_id=collective_id, has_side_effects=True, vmem_limit_bytes=32 << 20
        ),
        cost_estimate=pl.CostEstimate(
            flops=0, transcendentals=0, bytes_accessed=250 * 1024 * 1024
        ),
        name="gather_weights",
    )(*in_hbm(qo, kv, xg, wd, ad, bd, x), gain, *in_hbm(aa, ag))
    return wa.reshape(2, n * block, cols), gz, near, sq, grams, u, inner


def gather_kernel(n, rows, count, shared, *refs):
    nc = n // 2
    sources = refs[: count + len(shared[0])]
    outs = refs[len(sources) : 2 * len(sources) - len(shared[0]) + len(shared[1])]
    local_sem, to_sib, to_left, to_right, recv, share_out, share_in = refs[len(sources) + len(outs) :]
    xs, held, swapped = sources[:count], sources[count:], outs[count:]
    s, q, c = place_in_seq()
    sibling = s + 1 - 2 * c
    r, b_row, a_row, _ = place_in_rows(rows)
    greet_all(n, rows)
    locals_ = [
        pltpu.make_async_copy(xs[k], outs[k].at[s], local_sem.at[k]) for k in range(count)
    ]
    for cp in locals_:
        cp.start()

    def copy(k, src, slot, sems, target):
        return remote(src, outs[k].at[slot], sems.at[k, slot], recv.at[k, slot], r, target)

    def share(i, p):
        source, piece, turn, _ = shared[1][i]
        pair = pl.ds(2 * p, 2)
        src = held[source].at[pair] if piece is None else held[source].at[piece, pair]
        target = b_row if turn == 0 else a_row(turn)
        return remote(src, swapped[i].at[pair], share_out.at[i, p], share_in.at[i, p], target, s)

    for k in range(count):
        pl.when(q > 0)(lambda k=k: copy(k, xs[k], s, to_left, s - 2).start())
        pl.when(q < nc - 1)(lambda k=k: copy(k, xs[k], s, to_right, s + 2).start())
        copy(k, xs[k], s, to_sib, sibling).start()
    order = [near_first(i, q, nc) for i in range(nc)]
    for p in order[1:]:
        for i in range(len(shared[1])):
            share(i, p).start()
    for p in order[1:]:
        slot = 2 * p + c
        for k in range(count):
            src = outs[k].at[slot]
            copy(k, src, slot, to_right, s).wait_recv()
            pl.when((p < q) & (q < nc - 1))(
                lambda k=k, src=src, slot=slot: copy(k, src, slot, to_right, s + 2).start()
            )
            pl.when((p > q) & (q > 0))(
                lambda k=k, src=src, slot=slot: copy(k, src, slot, to_left, s - 2).start()
            )
            copy(k, src, slot, to_sib, sibling).start()
    for cp in locals_:
        cp.wait()
    for p in range(nc):
        mine, theirs = 2 * p + c, 2 * p + 1 - c
        for k in range(count):
            copy(k, outs[k].at[theirs], theirs, to_sib, sibling).wait_recv()
            copy(k, outs[k].at[mine], mine, to_sib, sibling).wait_send()
            pl.when((q < nc - 1) & (p <= q))(
                lambda k=k, mine=mine: copy(k, outs[k].at[mine], mine, to_right, s).wait_send()
            )
            pl.when((q > 0) & (p >= q))(
                lambda k=k, mine=mine: copy(k, outs[k].at[mine], mine, to_left, s).wait_send()
            )
    for p in order[1:]:
        for i in range(len(shared[1])):
            share(i, p).wait_send()
            share(i, p).wait_recv()


def gather_seq(n, rows, arrays, collective_id, held=(), shares=()):
    nc, count = n // 2, len(arrays)
    nbytes = sum(a.size * a.dtype.itemsize for a in arrays)
    dma = pltpu.SemaphoreType.DMA
    shape = jax.ShapeDtypeStruct
    outs = [shape((n, *a.shape), a.dtype) for a in arrays]
    outs += [shape(held[source].shape[-3:], held[source].dtype) for source, _, _ in shares]
    anywhere = pl.BlockSpec(memory_space=pltpu.HBM)
    listed = (tuple(held), [(source, piece, turn, None) for source, piece, turn in shares])
    sems = dma((max(1, len(shares)), nc))
    got = pl.pallas_call(
        functools.partial(gather_kernel, n, rows, count, (range(len(held)), listed[1])),
        out_shape=tuple(outs),
        in_specs=[anywhere] * (count + len(held)),
        out_specs=(anywhere,) * len(outs),
        scratch_shapes=[dma((count,))] + [dma((count, n))] * 4 + [sems] * 2,
        compiler_params=pltpu.CompilerParams(collective_id=collective_id, has_side_effects=True),
        cost_estimate=pl.CostEstimate(flops=0, transcendentals=0, bytes_accessed=nbytes * n * 20),
        name="gather_seq",
    )(*arrays, *held)
    return got[:count], got[count:]

def scatter_kernel(n, x_ref, o_ref, own, sib, from_left, from_right,
                   load_sem, to_sib, sib_in, to_right, right_in, to_left, left_in):
    nc = n // 2
    s, q, c = place_in_seq()
    sibling = greet(nc, q, s)
    theirs = 1 - c

    def load(p):
        return pltpu.make_async_copy(x_ref.at[2 * p + c], own.at[p], load_sem.at[p])

    def to_sibling(p):
        return pltpu.make_async_remote_copy(
            src_ref=x_ref.at[2 * p + theirs],
            dst_ref=sib.at[p],
            send_sem=to_sib.at[p],
            recv_sem=sib_in.at[p],
            device_id={"seq": sibling},
            device_id_type=MESH,
        )

    def rightward(p, target):
        return pltpu.make_async_remote_copy(
            src_ref=own.at[p],
            dst_ref=from_left.at[p],
            send_sem=to_right.at[p],
            recv_sem=right_in.at[p],
            device_id={"seq": target},
            device_id_type=MESH,
        )

    def leftward(p, target):
        return pltpu.make_async_remote_copy(
            src_ref=own.at[p],
            dst_ref=from_right.at[p],
            send_sem=to_left.at[p],
            recv_sem=left_in.at[p],
            device_id={"seq": target},
            device_id_type=MESH,
        )

    order = []
    for t in range(nc):
        for p in (nc - 1 - t, t):
            if p not in order:
                order.append(p)
    for p in order:
        to_sibling(p).start()
        load(p).start()

    f32 = jnp.float32
    for p in order:
        load(p).wait()
        to_sibling(p).wait_recv()

        @pl.when(p > q)
        def _(p=p):
            @pl.when(q > 0)
            def _():
                rightward(p, s).wait_recv()
                total = own[p].astype(f32) + sib[p].astype(f32) + from_left[p].astype(f32)
                own[p] = total.astype(own.dtype)

            @pl.when(q == 0)
            def _():
                own[p] = (own[p].astype(f32) + sib[p].astype(f32)).astype(own.dtype)

            rightward(p, s + 2).start()

        @pl.when(p < q)
        def _(p=p):
            @pl.when(q < nc - 1)
            def _():
                leftward(p, s).wait_recv()
                total = own[p].astype(f32) + sib[p].astype(f32) + from_right[p].astype(f32)
                own[p] = total.astype(own.dtype)

            @pl.when(q == nc - 1)
            def _():
                own[p] = (own[p].astype(f32) + sib[p].astype(f32)).astype(own.dtype)

            leftward(p, s - 2).start()

    o_ref[...] = own[q].astype(f32) + sib[q].astype(f32)

    @pl.when(q > 0)
    def _():
        rightward(q, s).wait_recv()
        o_ref[...] += from_left[q].astype(f32)

    @pl.when(q < nc - 1)
    def _():
        leftward(q, s).wait_recv()
        o_ref[...] += from_right[q].astype(f32)

    for p in range(nc):
        to_sibling(p).wait_send()
        pl.when(p > q)(lambda p=p: rightward(p, s).wait_send())
        pl.when(p < q)(lambda p=p: leftward(p, s).wait_send())


def scatter_seq(n, x, collective_id):
    nc = n // 2
    _, rows, cols = x.shape
    dma = pltpu.SemaphoreType.DMA
    buf = pltpu.VMEM((nc, rows, cols), x.dtype)
    return pl.pallas_call(
        functools.partial(scatter_kernel, n),
        out_shape=jax.ShapeDtypeStruct((rows, cols), jnp.float32),
        in_specs=[pl.BlockSpec(memory_space=pltpu.HBM)],
        out_specs=pl.BlockSpec(memory_space=pltpu.VMEM),
        scratch_shapes=[buf] * 4 + [dma((nc,))] * 7,
        compiler_params=pltpu.CompilerParams(
            collective_id=collective_id, has_side_effects=True, vmem_limit_bytes=32 << 20
        ),
        cost_estimate=pl.CostEstimate(flops=0, transcendentals=0, bytes_accessed=1 << 20),
        name="scatter_seq",
    )(*in_hbm(x))

def swap_halves(x):
    return pltpu.roll(x.astype(jnp.float32), HEAD_DIM, 1)


def stack_heads(block):
    lane = lax.broadcasted_iota(jnp.int32, (block.shape[0], 128), 1)
    rows = []
    for h in range(8):
        pair = block[:, (h // 2) * 128 : (h // 2 + 1) * 128].astype(jnp.float32)
        if h % 2 != h // 4:
            pair = swap_halves(pair)
        keep = lane < HEAD_DIM if h // 4 == 0 else lane >= HEAD_DIM
        rows.append(jnp.where(keep, pair, 0.0).astype(jnp.bfloat16))
    return jnp.concatenate(rows, axis=0)


def unstack_heads(stacked, span):
    lane = lax.broadcasted_iota(jnp.int32, (span, 128), 1)
    pairs = []
    for t in range(4):
        first = stacked[2 * t * span : (2 * t + 1) * span]
        second = stacked[(2 * t + 1) * span : (2 * t + 2) * span]
        if t < 2:
            second = swap_halves(second)
        else:
            first = swap_halves(first)
        pairs.append(jnp.where(lane < HEAD_DIM, first, second))
    return jnp.concatenate(pairs, axis=1)


def attend_kernel(valid_ref, q_ref, k_ref, v_ref, o_ref, p_ref):
    span = q_ref.shape[1]
    keys = k_ref.shape[0] * span
    q8 = stack_heads(q_ref[0])
    k2 = k_ref[:, 0].reshape(keys, 128)
    v2 = v_ref[:, 0].reshape(keys, 128)
    scores = lax.dot_general(q8, k2, last_last, preferred_element_type=jnp.float32)
    scores = scores * HEAD_DIM**-0.5
    first_pos = lax.axis_index("seq") * span
    q_pos = first_pos + lax.broadcasted_iota(jnp.int32, (8, span, keys), 1).reshape(8 * span, keys)
    k_pos = lax.broadcasted_iota(jnp.int32, (8 * span, keys), 1)
    allowed = (k_pos <= q_pos) & (k_pos < valid_ref[pl.program_id(0)])
    scores = jnp.where(allowed, scores, -1e30)
    unscaled = jnp.exp(scores - jnp.max(scores, axis=1, keepdims=True))
    shares = unscaled * (1.0 / jnp.sum(unscaled, axis=1, keepdims=True))
    shares = shares.astype(jnp.bfloat16)
    p_ref[0, 0] = shares
    mixed = jnp.dot(shares, v2, preferred_element_type=jnp.float32)
    o_ref[0] = unstack_heads(mixed, span).astype(jnp.bfloat16)


def attend(q, kv, valid):
    pair, span, width = q.shape
    n, kv_width = kv.shape[0], kv.shape[3] // 2
    groups = kv_width // 128
    keys = n * span
    q_spec = pl.BlockSpec((1, span, 512), lambda p, j, *_: (p, 0, j))
    flops = 4 * pair * groups * 8 * span * keys * 128
    return pl.pallas_call(
        attend_kernel,
        out_shape=(
            pltpu.HBM(q.shape, jnp.bfloat16),
            pltpu.HBM((pair, groups, 8 * span, keys), jnp.bfloat16),
        ),
        grid_spec=pltpu.PrefetchScalarGridSpec(
            num_scalar_prefetch=1,
            grid=(pair, groups),
            in_specs=[
                q_spec,
                pl.BlockSpec((n, 1, span, 128), lambda p, j, *_: (0, p, 0, j)),
                pl.BlockSpec((n, 1, span, 128), lambda p, j, *_: (0, p, 0, groups + j)),
            ],
            out_specs=(
                q_spec,
                pl.BlockSpec((1, 1, 8 * span, keys), lambda p, j, *_: (p, j, 0, 0)),
            ),
        ),
        compiler_params=pltpu.CompilerParams(vmem_limit_bytes=40 << 20),
        cost_estimate=pl.CostEstimate(
            flops=flops, transcendentals=flops // 512, bytes_accessed=8 << 20
        ),
        name="attend",
    )(valid, *in_hbm(q, kv, kv))


def attend_back_kernel(q_ref, k_ref, v_ref, p_ref, g_ref, gq_ref, gkv_ref):
    span = q_ref.shape[1]
    keys = k_ref.shape[0] * span
    q8 = stack_heads(q_ref[0])
    g8 = stack_heads(g_ref[0])
    k2 = k_ref[:, 0].reshape(keys, 128)
    v2 = v_ref[:, 0].reshape(keys, 128)
    low = p_ref[0, 0]
    shares = low.astype(jnp.float32)
    grad_shares = lax.dot_general(g8, v2, last_last, preferred_element_type=jnp.float32)
    weighted = shares * grad_shares
    centre = jnp.sum(weighted, axis=1, keepdims=True)
    grad_scores = (weighted - shares * centre).astype(jnp.bfloat16)
    gq = jnp.dot(grad_scores, k2, preferred_element_type=jnp.float32) * HEAD_DIM**-0.5
    gq_ref[0] = unstack_heads(gq, span).astype(jnp.bfloat16)
    gk = lax.dot_general(grad_scores, q8, first_first, preferred_element_type=jnp.float32)
    gv = lax.dot_general(low, g8, first_first, preferred_element_type=jnp.float32)
    both = jnp.concatenate([gk * HEAD_DIM**-0.5, gv], axis=1).astype(jnp.bfloat16)
    gkv_ref[:, 0] = both.reshape(gkv_ref.shape[0], span, 256)


def attend_back(q, kv, shares, g):
    pair, span, _ = q.shape
    n, kv_width = kv.shape[0], kv.shape[3] // 2
    groups = kv_width // 128
    keys = n * span
    q_spec = pl.BlockSpec((1, span, 512), lambda p, j: (p, 0, j))
    return pl.pallas_call(
        attend_back_kernel,
        out_shape=(
            pltpu.HBM(q.shape, jnp.bfloat16),
            pltpu.HBM(kv.shape, jnp.bfloat16),
        ),
        grid=(pair, groups),
        in_specs=[
            q_spec,
            pl.BlockSpec((n, 1, span, 128), lambda p, j: (0, p, 0, j)),
            pl.BlockSpec((n, 1, span, 128), lambda p, j: (0, p, 0, groups + j)),
            pl.BlockSpec((1, 1, 8 * span, keys), lambda p, j: (p, j, 0, 0)),
            q_spec,
        ],
        out_specs=(
            q_spec,
            pl.BlockSpec((n, 1, span, 256), lambda p, j: (0, p, 0, j)),
        ),
        compiler_params=pltpu.CompilerParams(vmem_limit_bytes=40 << 20),
        cost_estimate=pl.CostEstimate(flops=0, transcendentals=0, bytes_accessed=1 << 20),
        name="attend_back",
    )(*in_hbm(q, kv, kv, shares, g))

def by_distance(i, q, nc):
    room = nc - 1 - q
    left_half = q <= room
    short = jnp.where(left_half, q, room)
    far = jnp.where(left_half, i, nc - 1 - i)
    step = (i + 1) // 2
    near = jnp.where(lax.rem(i, 2) == 1, q - step, q + step)
    return jnp.where(i <= 2 * short, near, far)


def ffn_kernel(n, rows, pieces, u_hbm, inner_hbm, gy0_hbm, gy1_hbm, wd_hbm, a_ref, b_ref, m_ref, ad_ref, bd_ref, md_ref, sq_ref, gram_ref,
               in_ref, down0_hbm, down1_hbm, ga_ref, gb_ref, gm_ref, norm_ref, gad_ref, gbd_ref, gmd_ref, nd_ref,
               w_parts, wd, u, side, gy, down, own, theirs, sib, from_left, from_right, ratio, cross, gm_all,
               w_sem, load_sem, down_sem, small_out, small_in, to_sib, sib_in, to_right, right_in, to_left, left_in):
    nc = n // 2
    f32, low = jnp.float32, jnp.bfloat16
    s, q, c = place_in_seq()
    tokens = own.shape[1]

    weights = [pltpu.make_async_copy(wd_hbm, wd, w_sem.at[0])]
    for src, dst in place_pieces(n, rows, pieces, w_parts):
        weights.append(pltpu.make_async_copy(src, dst, w_sem.at[len(weights)]))
    for cp in weights:
        cp.start()

    def loads(i):
        p = by_distance(nc - 1 - i, q, nc)
        slot = lax.rem(i, 2)
        pair = pl.ds(2 * p, 2)
        return (
            pltpu.make_async_copy(u_hbm.at[pair], u.at[slot], load_sem.at[0, slot]),
            pltpu.make_async_copy(
                gy0_hbm.at[pair], gy.at[slot, :, : tokens // 2], load_sem.at[1, slot]
            ),
            pltpu.make_async_copy(
                gy1_hbm.at[pair], gy.at[slot, :, tokens // 2 :], load_sem.at[2, slot]
            ),
            pltpu.make_async_copy(inner_hbm.at[pair], side.at[slot], load_sem.at[3, slot]),
        )

    for cp in loads(0):
        cp.start()
    sibling = s + 1 - 2 * c
    barrier = pltpu.get_barrier_semaphore()
    for t in range(1, n):
        pl.semaphore_signal(
            barrier, inc=1, device_id={"seq": lax.rem(s + t, n)}, device_id_type=MESH
        )

    def to_sibling(p):
        return pltpu.make_async_remote_copy(
            src_ref=theirs.at[p], dst_ref=sib.at[p], send_sem=to_sib.at[p], recv_sem=sib_in.at[p],
            device_id={"seq": sibling}, device_id_type=MESH,
        )

    def rightward(p, target):
        return pltpu.make_async_remote_copy(
            src_ref=own.at[p], dst_ref=from_left.at[p], send_sem=to_right.at[p], recv_sem=right_in.at[p],
            device_id={"seq": target}, device_id_type=MESH,
        )

    def leftward(p, target):
        return pltpu.make_async_remote_copy(
            src_ref=own.at[p], dst_ref=from_right.at[p], send_sem=to_left.at[p], recv_sem=left_in.at[p],
            device_id={"seq": target}, device_id_type=MESH,
        )

    def down_out(slot, p):
        half = tokens // 2
        return [
            pltpu.make_async_copy(
                down.at[slot, :, half * k : half * (k + 1)], out.at[pl.ds(2 * p, 2)], down_sem.at[k, slot]
            )
            for k, out in enumerate((down0_hbm, down1_hbm))
        ]

    def pass_on(p):
        to_sibling(p).wait_recv()

        @pl.when(p > q)
        def _():
            @pl.when(q > 0)
            def _():
                rightward(p, s).wait_recv()
                own[p] = (own[p].astype(f32) + sib[p].astype(f32) + from_left[p].astype(f32)).astype(low)

            @pl.when(q == 0)
            def _():
                own[p] = (own[p].astype(f32) + sib[p].astype(f32)).astype(low)

            rightward(p, s + 2).start()

        @pl.when(p < q)
        def _():
            @pl.when(q < nc - 1)
            def _():
                leftward(p, s).wait_recv()
                own[p] = (own[p].astype(f32) + sib[p].astype(f32) + from_right[p].astype(f32)).astype(low)

            @pl.when(q == nc - 1)
            def _():
                own[p] = (own[p].astype(f32) + sib[p].astype(f32)).astype(low)

            leftward(p, s - 2).start()

    def starts_flow(p):
        return ((p > q) & (q == 0)) | ((p < q) & (q == nc - 1))

    w = [w_parts.at[g] for g in range(2)]
    width = u_hbm.shape[2]
    weight = lambda g: w[g][...].reshape(width, -1)
    units = wd.shape[0]
    mine = pl.ds(pl.multiple_of(s * units, units), units)
    bd = bd_ref[...].astype(low)
    ad = ad_ref[:, mine].astype(low)
    a = [a_ref[g].astype(low) for g in range(2)]
    b = [b_ref[g, :, mine].astype(low) for g in range(2)]
    m = [m_ref[g : g + 1, mine] for g in range(2)]
    for cp in weights:
        cp.wait()
    a_both = jnp.concatenate(a, axis=0)
    for g in range(2):
        norm, cr = column_norms(weight(g), gram_ref[4 + g], b[g], dot_f32(a[g], weight(g)))
        norm_ref[g] = norm
        cross[g] = cr
        ratio[g] = m[g] / norm
    for ref in (ga_ref, gb_ref, gm_ref, gad_ref, gbd_ref, gmd_ref):
        ref[...] = jnp.zeros_like(ref)
    bd_wide = bd.astype(f32)
    gram_b = dot_two(gram_ref[6], bd)
    squares = jnp.sum(sq_ref[...], axis=0) + SCALE * SCALE * jnp.sum(
        bd_wide * gram_b, axis=0, keepdims=True
    )
    nd_ref[...] = jnp.sqrt(squares + 1e-06)
    ratio_d = md_ref[...] / nd_ref[...]
    pl.semaphore_wait(barrier, n - 1)

    def step(i, carry):
        p = by_distance(nc - 1 - i, q, nc)
        slot = lax.rem(i, 2)
        for cp in loads(i):
            cp.wait()

        @pl.when(i + 1 < nc)
        def _():
            for cp in loads(i + 1):
                cp.start()

        x = u[slot].reshape(2 * tokens, -1)
        upstream = gy[slot].reshape(2 * tokens, -1).astype(f32)
        gb_d = (upstream * ratio_d).astype(low)
        gi_d = (SCALE * dot_nt(gb_d, bd)).astype(low)
        gh = dot_nt(gb_d, wd[...]) + dot_f32(gi_d, ad)
        sides = side[slot].reshape(2 * tokens, -1)
        inner = [sides[:, 16 * g : 16 * g + 16] for g in range(2)]
        before = [dot_f32(x, weight(g)) + SCALE * dot_f32(inner[g], b[g]) for g in range(2)]
        gate = before[0] * ratio[0]
        lift = before[1] * ratio[1]
        sig = 1.0 / (1.0 + jnp.exp(-gate))
        silu = gate * sig
        hidden = (silu * lift).astype(low)
        grads = [gh * lift * sig * (1.0 + gate * (1.0 - sig)), gh * silu]
        gb = [(grads[g] * ratio[g]).astype(low) for g in range(2)]
        gi = jnp.concatenate([(SCALE * dot_nt(gb[g], b[g])).astype(low) for g in range(2)], axis=1)
        back = dot_nt(gb[0], weight(0)) + dot_nt(gb[1], weight(1)) + dot_f32(gi, a_both)
        back = back.astype(low).reshape(2, tokens, -1)
        first, second = back[0], back[1]

        @pl.when(c == 0)
        def _():
            own[p] = first
            theirs[p] = second

        @pl.when(c == 1)
        def _():
            own[p] = second
            theirs[p] = first

        to_sibling(p).start()
        inner_d = dot_nt(hidden, ad).astype(low)
        part = dot_f32(hidden, wd[...]) + SCALE * dot_f32(inner_d, bd)

        @pl.when(i >= 2)
        def _():
            for cp in down_out(slot, p):
                cp.wait()

        down[slot] = part.astype(low).reshape(2, tokens, -1)
        for cp in down_out(slot, p):
            cp.start()
        gmd_ref[...] += jnp.sum(upstream * part, axis=0, keepdims=True)
        gad_ref[...] += dot_tn(gi_d, hidden)
        gbd_ref[...] += SCALE * dot_tn(inner_d, gb_d)
        ga_ref[...] += dot_tn(gi, x).reshape(ga_ref.shape)
        for g in range(2):
            gm_ref[g] += jnp.sum(grads[g] * before[g], axis=0, keepdims=True)
            gb_ref[g] += SCALE * dot_tn(inner[g], gb[g])

        pl.when(starts_flow(p))(lambda: pass_on(p))
        last = by_distance(nc - i, q, nc)
        pl.when((i > 0) & jnp.logical_not(starts_flow(last)))(lambda: pass_on(last))
        return carry

    lax.fori_loop(0, nc, step, 0)

    gmd_ref[...] = gmd_ref[...] / nd_ref[...]

    def small(t, slot):
        return pltpu.make_async_remote_copy(
            src_ref=gmd_ref,
            dst_ref=gm_all.at[slot],
            send_sem=small_out.at[t],
            recv_sem=small_in.at[t],
            device_id={"seq": lax.rem(s + t, n)},
            device_id_type=MESH,
        )

    for t in range(1, n):
        small(t, s).start()
    for g in range(2):
        norm = norm_ref[g]
        gm = gm_ref[g] / norm
        gm_ref[g] = gm
        col = -gm * m[g] / (norm * norm)
        weighted = (b[g].astype(f32) * col).astype(low)
        tail = two_terms(dot_nt(weighted, b[g]))
        ga_ref[g] += SCALE * (dot_nt(weighted, weight(g)) + SCALE * dot_two(tail, a[g]))
        gb_ref[g] += SCALE * col * cross[g]

    gm_line = gmd_ref[...]
    for t in range(1, n):
        slot = lax.rem(s - t + n, n)
        small(t, slot).wait_recv()
        gm_line = gm_line + gm_all[slot]
    col = -gm_line * md_ref[...] / (nd_ref[...] * nd_ref[...])
    weighted = (bd_wide * col).astype(low)
    tail = two_terms(dot_nt(weighted, bd))
    gad_ref[...] += SCALE * (dot_nt(weighted, wd[...]) + SCALE * dot_two(tail, ad))
    own_gram = jnp.where(s == 0, SCALE, 0.0) * gram_b
    gbd_ref[...] += SCALE * col * (dot_f32(ad, wd[...]) + own_gram)

    to_sibling(q).wait_recv()
    in_ref[...] = own[q].astype(f32) + sib[q].astype(f32)

    @pl.when(q > 0)
    def _():
        rightward(q, s).wait_recv()
        in_ref[...] += from_left[q].astype(f32)

    @pl.when(q < nc - 1)
    def _():
        leftward(q, s).wait_recv()
        in_ref[...] += from_right[q].astype(f32)

    for i in range(min(2, nc)):
        for cp in down_out(i, 0):
            cp.wait()
    for t in range(1, n):
        small(t, s).wait_send()
    for p in range(nc):
        to_sibling(p).wait_send()
        pl.when(p > q)(lambda p=p: rightward(p, s).wait_send())
        pl.when(p < q)(lambda p=p: leftward(p, s).wait_send())


def share_plan(rows):
    turns = range(1, rows // 2)
    first = [(0, 0, k) for k in turns] + [(0, 1, 0)]
    second = [(0, 0, 0)] + [(0, 1, k) for k in turns]
    second += [(k, None, 0) for k in turns] + [(rows // 2, None, k) for k in turns]
    return first, second


def place_pieces(n, rows, pieces, w_parts):
    nc, half = n // 2, rows // 2
    _, q, _ = place_in_seq()
    r, b_row, a_row, diagonal = place_in_rows(rows)
    own, near = pieces[:2]
    turns = range(1, half)
    held = [(own.at[g], g, r) for g in range(2)]
    kinds = [(0, a_row(-k)) for k in turns] + [(1, b_row)]
    kinds += [(0, b_row)] + [(1, a_row(-k)) for k in turns]
    kinds += [(0, diagonal(-k)) for k in turns] + [(1, diagonal(-k)) for k in turns]
    held += [(piece, g, hold) for piece, (g, hold) in zip(pieces[2:], kinds)]
    out = [(near, w_parts.at[:, pl.ds(2 * q, 2)])]
    for i in range(1, nc):
        pair = pl.ds(2 * near_first(i, q, nc), 2)
        out += [(src.at[pair], w_parts.at[g, pair, hold]) for src, g, hold in held]
    return out


def feed_forward(n, rows, pieces, u, inner, gy0, gy1, wd, a, b, m, ad, bd, md, sq, gram, collective_id):
    nc = n // 2
    _, tokens, width = u.shape
    units = wd.shape[0]
    f32, low = jnp.float32, jnp.bfloat16
    shape = jax.ShapeDtypeStruct
    vmem = pl.BlockSpec(memory_space=pltpu.VMEM)
    hbm = pl.BlockSpec(memory_space=pltpu.HBM)
    dma = pltpu.SemaphoreType.DMA
    line = pltpu.VMEM((nc, tokens, width), low)
    pair = pltpu.VMEM((2, 2, tokens, width), low)
    part = pieces[0].shape[2]
    copies = 2 + (n // 2 - 1) * (2 + 2 * rows - 2)
    count = len(pieces)

    def kernel(*refs):
        ffn_kernel(n, rows, refs[:count], *refs[count:])

    return pl.pallas_call(
        kernel,
        out_shape=(
            shape((tokens, width), f32),
            pltpu.HBM((n, tokens // 2, width), low),
            pltpu.HBM((n, tokens // 2, width), low),
            shape((2, 16, width), f32),
            shape((2, 16, units), f32),
            shape((2, 1, units), f32),
            shape((2, 1, units), f32),
            shape((16, units), f32),
            shape((16, width), f32),
            shape((1, width), f32),
            shape((1, width), f32),
        ),
        in_specs=[hbm] * (count + 5) + [vmem] * 8,
        out_specs=(vmem, hbm, hbm) + (vmem,) * 8,
        scratch_shapes=[
            pltpu.VMEM((2, n, rows, part, units), low),
            pltpu.VMEM((units, width), low),
            pair,
            pltpu.VMEM((2, 2, tokens, 128), low),
            pair,
            pair,
            line, line, line, line, line,
            pltpu.VMEM((2, 1, units), f32),
            pltpu.VMEM((2, 16, units), f32),
            pltpu.VMEM((n, 1, width), f32),
            dma((copies,)), dma((4, 2)), dma((2, 2)), dma((n,)), dma((n,)),
        ] + [dma((nc,))] * 6,
        compiler_params=pltpu.CompilerParams(
            collective_id=collective_id, has_side_effects=True, vmem_limit_bytes=60 << 20
        ),
        cost_estimate=pl.CostEstimate(
            flops=12 * n * tokens * width * units, transcendentals=n * tokens * units,
            bytes_accessed=32 << 20,
        ),
        name="feed_forward",
    )(*pieces, u, inner, gy0, gy1, wd, a, b, m, ad, bd, md, sq, gram)

def reduce_kernel(n, rows, ga_qkv, ga_o, gb_qkv, gb_o, ga_gu, gb_d, gm_qkv, gm_o, gm_d, gb_gu, gm_gu, n_gu, ga_d,
                  whole, units_all, part, from_sib, mid, from_rows, from_line, line_out, units, units_in,
                  sib_out, sib_in, row_out, row_in, line_send, line_in, back_send, back_in, wide_send, wide_in,
                  pass_send, pass_in):
    nc = n // 2
    f32, low = jnp.float32, jnp.bfloat16
    s, q, c = place_in_seq()
    sibling = s + 1 - 2 * c
    r = lax.axis_index("rows")
    width = ga_o.shape[1]
    cols = width // (2 * rows)
    kv = (gb_qkv.shape[1] - width) // 2
    height = part.shape[2]
    piece = height // nc
    unit_rows = units.shape[1]
    size = units.shape[2]

    barrier = pltpu.get_barrier_semaphore()
    for t in range(1, n):
        pl.semaphore_signal(barrier, inc=1, device_id=(r, lax.rem(s + t, n)), device_id_type=MESH)
    for t in range(1, rows):
        pl.semaphore_signal(barrier, inc=1, device_id=(lax.rem(r + t, rows), s), device_id_type=MESH)

    gb_k, gb_v = gb_qkv[:, width : width + kv], gb_qkv[:, width + kv :]
    small = jnp.concatenate(
        [
            jnp.concatenate([gb_k[:8], gb_k[8:], gb_v[:8], gb_v[8:]], axis=1),
            gm_qkv[:, :width],
            gm_o[...],
            gm_d[...],
            jnp.concatenate([gm_qkv[:, width:], jnp.zeros((1, width - 2 * kv), f32)], axis=1),
            jnp.zeros((4, width), f32),
        ],
        axis=0,
    )
    groups = [ga_qkv[0], ga_qkv[1], ga_qkv[2], ga_o[...], gb_qkv[:, :width], gb_o[...], ga_gu[0], ga_gu[1], gb_d[...], small]
    for j in range(2 * rows):
        for g, value in enumerate(groups):
            part[j % 2, j // 2, 16 * g : 16 * g + 16] = value[:, cols * j : cols * (j + 1)].astype(low)
        if height > 160:
            part[j % 2, j // 2, 160:] = jnp.zeros((height - 160, cols), low)
    n_high = [n_gu[g].astype(low).astype(f32) for g in range(2)]
    n_rest = [n_gu[g] - n_high[g] for g in range(2)]
    tops = jnp.concatenate(
        [gm_gu[0], gm_gu[1]]
        + [v * (1.0 / rows) for v in (n_high[0], n_rest[0], n_high[1], n_rest[1])]
        + [jnp.zeros((2, size), f32)],
        axis=0,
    )
    blocks = [gb_gu[0][:8], gb_gu[0][8:], gb_gu[1][:8], gb_gu[1][8:], ga_d[:8], ga_d[8:], tops, jnp.zeros((8, size), f32)]
    per = unit_rows // 8
    for j in range(rows):
        units[j] = jnp.concatenate(blocks[per * j : per * (j + 1)], axis=0).astype(low)
    pl.semaphore_wait(barrier, n - 1 + rows - 1)

    def to_sibling():
        return remote(part.at[1 - c], from_sib, sib_out.at[0], sib_in.at[0], r, sibling)

    def member(t):
        return lax.rem(r + t + rows, rows)

    def row_send(t):
        return remote(mid.at[member(t)], from_rows.at[t], row_out.at[0, t], row_in.at[0, t], member(t), s)

    def unit_send(t):
        return remote(units.at[member(t)], units_in.at[t], row_out.at[1, t], row_in.at[1, t], member(t), s)

    def chip(t):
        return lax.rem(q + t + nc, nc)

    def line_part(t):
        return remote(line_out.at[chip(t)], from_line.at[t], line_send.at[t], line_in.at[t], r, 2 * chip(t) + c)

    def back(t, slot):
        return remote(whole.at[r, c, slot], whole.at[r, c, slot], back_send.at[0, t], back_in.at[0, t], r, 2 * chip(t) + c)

    def unit_back(t, slot):
        return remote(
            units_all.at[r, c, slot], units_all.at[r, c, slot], back_send.at[1, t], back_in.at[1, t], r, 2 * chip(t) + c
        )

    def wide(t, row):
        return remote(whole.at[row, c], whole.at[row, c], wide_send.at[0, t], wide_in.at[0, t], member(t), s)

    def unit_wide(t, row):
        return remote(units_all.at[row, c], units_all.at[row, c], wide_send.at[1, t], wide_in.at[1, t], member(t), s)

    def hand(t, row, core):
        return remote(whole.at[row, core], whole.at[row, core], pass_send.at[0, t], pass_in.at[0, t], r, sibling)

    def unit_hand(t, row, core):
        return remote(units_all.at[row, core], units_all.at[row, core], pass_send.at[1, t], pass_in.at[1, t], r, sibling)

    to_sibling().start()
    for t in range(1, rows):
        unit_send(t).start()
    to_sibling().wait_recv()
    for t in range(rows):
        mid[member(t)] = (part[c, member(t)].astype(f32) + from_sib[member(t)].astype(f32)).astype(low)
        if t:
            row_send(t).start()
    unit_sum = units[r].astype(f32)
    for t in range(1, rows):
        unit_send(t).wait_recv()
        unit_sum = unit_sum + units_in[t].astype(f32)
    units_all[r, c, q] = unit_sum.astype(low)
    for t in range(1, nc):
        unit_back(t, q).start()
    total = mid[r].astype(f32)
    for t in range(1, rows):
        row_send(t).wait_recv()
        total = total + from_rows[t].astype(f32)
    for p in range(nc):
        line_out[p] = total[piece * p : piece * (p + 1)].astype(low)
    for t in range(1, nc):
        line_part(t).start()
    own = line_out[q].astype(f32)
    for t in range(1, nc):
        line_part(t).wait_recv()
        own = own + from_line[t].astype(f32)
    whole[r, c, q] = own.astype(low)
    for t in range(1, nc):
        back(t, q).start()
    for t in range(1, nc):
        back(t, chip(-t)).wait_recv()
        unit_back(t, chip(-t)).wait_recv()
    for t in range(1, rows):
        wide(t, r).start()
        unit_wide(t, r).start()
    hand(0, r, c).start()
    unit_hand(0, r, c).start()
    for t in range(1, rows):
        wide(t, member(-t)).wait_recv()
        hand(t, member(-t), c).start()
        unit_wide(t, member(-t)).wait_recv()
        unit_hand(t, member(-t), c).start()
    for t in range(rows):
        hand(t, member(-t), 1 - c).wait_recv()
        unit_hand(t, member(-t), 1 - c).wait_recv()

    to_sibling().wait_send()
    for t in range(1, rows):
        row_send(t).wait_send()
        unit_send(t).wait_send()
        wide(t, r).wait_send()
        unit_wide(t, r).wait_send()
    for t in range(1, nc):
        line_part(t).wait_send()
        back(t, q).wait_send()
        unit_back(t, q).wait_send()
    for t in range(rows):
        hand(t, member(-t), c).wait_send()
        unit_hand(t, member(-t), c).wait_send()


def sum_gradients(n, rows, full, own_units, collective_id):
    nc = n // 2
    width, size = full[1].shape[1], own_units[3].shape[1]
    cols = width // (2 * rows)
    height = -(-160 // (8 * nc)) * 8 * nc
    unit_rows = 64 // rows
    low = jnp.bfloat16
    vmem = pl.BlockSpec(memory_space=pltpu.VMEM)
    dma = pltpu.SemaphoreType.DMA
    block = (rows, height, cols)
    return pl.pallas_call(
        functools.partial(reduce_kernel, n, rows),
        out_shape=(
            jax.ShapeDtypeStruct((rows, 2, nc, height // nc, cols), low),
            jax.ShapeDtypeStruct((rows, 2, nc, unit_rows, size), low),
        ),
        in_specs=[vmem] * 13,
        out_specs=(vmem,) * 2,
        scratch_shapes=[
            pltpu.VMEM((2, *block), low),
            pltpu.VMEM(block, low),
            pltpu.VMEM(block, low),
            pltpu.VMEM(block, low),
            pltpu.VMEM((nc, height // nc, cols), low),
            pltpu.VMEM((nc, height // nc, cols), low),
            pltpu.VMEM((rows, unit_rows, size), low),
            pltpu.VMEM((rows, unit_rows, size), low),
            dma((1,)), dma((1,)), dma((2, rows)), dma((2, rows)), dma((nc,)), dma((nc,)),
            dma((2, nc)), dma((2, nc)), dma((2, rows)), dma((2, rows)), dma((2, rows)), dma((2, rows)),
        ],
        compiler_params=pltpu.CompilerParams(
            collective_id=collective_id, has_side_effects=True, vmem_limit_bytes=48 << 20
        ),
        cost_estimate=pl.CostEstimate(flops=0, transcendentals=0, bytes_accessed=1 << 20),
        name="sum_gradients",
    )(*full, *own_units)


def finish_kernel(n, rows, whole, units_all, x1, before_0, before_1, m_attn, n_attn, m_d, n_d, m_gu,
                  o_out, o_ga, o_gb_qo, o_gb_kv, o_gm_q, o_gm_kv, o_gm_o, o_ga_gu, o_gb_gu, o_gm_gu, o_ga_d, o_gb_d,
                  o_gm_d, o_stats, n_gu):
    f32 = jnp.float32
    nc = n // 2
    width = o_gb_d.shape[1]
    kv = o_gb_kv.shape[2]
    cols = width // (2 * rows)
    size = units_all.shape[4]
    per = units_all.shape[3] // 8
    half = x1.shape[0] // 2
    for k, before in enumerate((before_0, before_1)):
        own = slice(half * k, half * (k + 1))
        o_out[own] = (x1[own] + before[...].astype(f32) * (m_d[...] / n_d[...])).astype(o_out.dtype)
    for j in range(2 * rows):
        block = jnp.concatenate([whole[j // 2, j % 2, p].astype(f32) for p in range(nc)], axis=0)
        at = slice(cols * j, cols * (j + 1))
        for g in range(4):
            o_ga[g, :, at] = block[16 * g : 16 * g + 16]
        o_gb_qo[0, :, at] = block[64:80]
        o_gb_qo[1, :, at] = block[80:96]
        o_ga_gu[0, :, at] = block[96:112]
        o_ga_gu[1, :, at] = block[112:128]
        o_gb_d[:, at] = block[128:144]
        which, start = divmod(cols * j, kv)
        o_gb_kv[which // 2, 8 * (which % 2) : 8 * (which % 2) + 8, start : start + cols] = block[144:152]
        o_gm_q[at] = block[152]
        o_gm_o[at] = block[153]
        o_gm_d[at] = block[154]
        if which < 2:
            o_gm_kv[which : which + 1, start : start + cols] = block[155:156]
    for j in range(rows):
        for dev in range(n):
            block = units_all[j, dev % 2, dev // 2].astype(f32)
            at = slice(size * dev, size * (dev + 1))
            for t in range(per):
                rows8, place = block[8 * t : 8 * t + 8], per * j + t
                half = slice(8 * (place % 2), 8 * (place % 2) + 8)
                if place < 4:
                    o_gb_gu[place // 2, half, at] = rows8
                elif place < 6:
                    o_ga_d[half, at] = rows8
                elif place == 6:
                    o_gm_gu[:, at] = rows8[:2]
                    n_gu[0:1, at] = rows8[2:3] + rows8[3:4]
                    n_gu[1:2, at] = rows8[4:5] + rows8[5:6]


    row = lax.broadcasted_iota(jnp.int32, o_stats.shape, 0)
    col = lax.broadcasted_iota(jnp.int32, o_stats.shape, 1)
    bounds = [(0, width), (width, width + kv), (width + kv, width + 2 * kv), (width + 2 * kv, 2 * width + 2 * kv)]
    both = [(m_attn[:, i:j], n_attn[:, i:j]) for i, j in bounds]
    both += [(m_gu[g : g + 1, :], n_gu[g : g + 1, :]) for g in range(2)] + [(m_d[...], n_d[...])]
    stats = jnp.zeros(o_stats.shape, f32)
    for p, (m, norm) in enumerate(both):
        drift = jnp.mean(jnp.square(m - norm), axis=1, keepdims=True)
        drift = jnp.sqrt(drift) / jnp.sqrt(jnp.mean(jnp.square(m), axis=1, keepdims=True) + 1e-06)
        stats = jnp.where((row == p) & (col == 0), drift, stats)
        stats = jnp.where((row == p) & (col == 1), jnp.mean(norm, axis=1, keepdims=True), stats)
    o_stats[...] = stats


def finish(n, rows, sums, x1, before_0, before_1, m_attn, n_attn, m_d, n_d, m_gu):
    tokens, width = x1.shape
    kv = (m_attn.shape[1] - 2 * width) // 2
    units = m_gu.shape[1]
    shape = lambda *dims: pltpu.HBM(dims, jnp.float32)
    vmem = pl.BlockSpec(memory_space=pltpu.VMEM)
    return pl.pallas_call(
        functools.partial(finish_kernel, n, rows),
        out_shape=(
            pltpu.HBM((tokens, width), jnp.bfloat16), shape(4, 16, width), shape(2, 16, width), shape(2, 16, kv),
            shape(width), shape(2, kv), shape(width), shape(2, 16, width), shape(2, 16, units), shape(2, units),
            shape(16, units), shape(16, width), shape(width), shape(7, 2),
        ),
        in_specs=[vmem] * 2 + [pl.BlockSpec()] * 8,
        scratch_shapes=[pltpu.VMEM((2, units), jnp.float32)],
        compiler_params=pltpu.CompilerParams(vmem_limit_bytes=40 << 20),
        cost_estimate=pl.CostEstimate(flops=0, transcendentals=0, bytes_accessed=8 << 20),
        name="finish",
    )(*sums, *in_hbm(x1, before_0, before_1), m_attn, n_attn, m_d, n_d, m_gu)

def local(
    layer_input,
    output_gradient,
    norm_gain_vectors,
    query_output_frozen,
    key_value_frozen,
    gate_up_frozen,
    down_frozen_weight,
    attention_adapter_a,
    query_output_adapter_b,
    key_value_adapter_b,
    query_magnitude,
    key_value_magnitude,
    output_magnitude,
    gate_up_adapter_a,
    gate_up_adapter_b,
    gate_up_magnitude,
    down_adapter_a,
    down_adapter_b,
    down_magnitude,
    prompt_length_list,
    response_length_list,
):
    pair_rows, span_len, model_width = layer_input.shape
    token_count = pair_rows * span_len
    kv_width = KV_HEADS * HEAD_DIM
    seq_size = lax.axis_size("seq")
    rows_size = lax.axis_size("rows")
    seq_index = lax.axis_index("seq")
    f32 = jnp.float32

    x = layer_input.reshape(token_count, model_width)
    gain_attn, gain_ffn = norm_gain_vectors[:1], norm_gain_vectors[1:]
    weights, gu_own, gu_near, sq_d, grams, u1, inner_1 = gather_weights(
        seq_size, rows_size, query_output_frozen, key_value_frozen, gate_up_frozen,
        down_frozen_weight, down_adapter_a, down_adapter_b, x, gain_attn, attention_adapter_a,
        gate_up_adapter_a, 1,
    )
    shares_1, shares_2 = share_plan(rows_size)
    grad_out_rows = output_gradient.reshape(token_count, model_width)
    half_0, half_1 = jnp.split(grad_out_rows, 2)
    weights, half_0 = lax.optimization_barrier((weights, half_0))
    gy_0 = lax.all_gather(half_0, "seq", axis=0, tiled=False)

    b_attn = jnp.concatenate(
        [
            query_output_adapter_b[0],
            key_value_adapter_b[0],
            key_value_adapter_b[1],
            query_output_adapter_b[1],
        ],
        axis=1,
    )
    m_attn = jnp.concatenate(
        [query_magnitude, key_value_magnitude[0], key_value_magnitude[1], output_magnitude]
    )[None]
    m_d = down_magnitude[None]

    positions = seq_index * span_len + jnp.arange(span_len, dtype=jnp.int32)
    half_dim = HEAD_DIM // 2
    frequency = 500000.0 ** (-(jnp.arange(half_dim, dtype=f32) * 2.0) / HEAD_DIM)
    angles = positions.astype(f32)[:, None] * frequency[None, :]
    cosine = jnp.tile(jnp.cos(angles), (pair_rows, 4))
    sine = jnp.tile(jnp.sin(angles), (pair_rows, 4))
    valid_len = prompt_length_list[0] + response_length_list

    before_qkv, q, kv, n_attn, cross_attn = project_qkv(
        u1, inner_1, grams, attention_adapter_a, weights, b_attn, m_attn, cosine, sine
    )
    (kv_all, sq_all), gu_1 = gather_seq(
        seq_size, rows_size, [kv, sq_d], 2, (gu_own,), shares_1
    )
    kv_all, half_1 = lax.optimization_barrier((kv_all, half_1))
    gy_1 = lax.all_gather(half_1, "seq", axis=0, tiled=False)
    kv_all = kv_all.reshape(seq_size, pair_rows, span_len, 2 * kv_width)
    q = q.reshape(pair_rows, span_len, model_width)
    att, shares = attend(q, kv_all, valid_len)
    att = att.reshape(token_count, model_width)
    before_o, x1, u2, inner_2 = project_out(
        att, attention_adapter_a, weights, b_attn, m_attn, n_attn, x, gain_ffn, gate_up_adapter_a
    )

    (u2_all, inner_all), gu_2 = gather_seq(
        seq_size, rows_size, [u2, inner_2], 3, (gu_own, *gu_1), shares_2
    )
    in_grad, down_0, down_1, ga_gu, gb_gu, gm_gu, n_gu, ga_d, gb_d, gm_d, n_d = feed_forward(
        seq_size, rows_size, (gu_own, gu_near, *gu_1, *gu_2), u2_all, inner_all, gy_0, gy_1,
        down_frozen_weight, gate_up_adapter_a, gate_up_adapter_b, gate_up_magnitude, down_adapter_a,
        down_adapter_b, m_d, sq_all, grams, 4,
    )
    flat = lambda v: v.reshape(-1, model_width)
    before_0 = lax.psum_scatter(flat(down_0), "seq", scatter_dimension=0, tiled=True)

    gx1, grad_att, ga_o, gb_o, gm_o = out_back(
        in_grad, x1, gain_ffn, grad_out_rows, before_o, att, attention_adapter_a, b_attn, m_attn,
        n_attn, cross_attn, weights,
    )
    gq, gkv = attend_back(q, kv_all, shares, grad_att.reshape(q.shape))
    gkv = scatter_seq(seq_size, gkv.reshape(seq_size, token_count, 2 * kv_width), 5)
    gkv, down_1, before_0 = lax.optimization_barrier((gkv, down_1, before_0))
    before_1 = lax.psum_scatter(flat(down_1), "seq", scatter_dimension=0, tiled=True)
    grad_inputs, ga_qkv, gb_qkv, gm_qkv = qkv_back(
        gq.reshape(token_count, model_width), gkv, cosine, sine, before_qkv, u1, inner_1,
        attention_adapter_a, b_attn, m_attn, n_attn, cross_attn, x, gain_attn, gx1, weights,
    )

    sums = sum_gradients(
        seq_size, rows_size,
        (ga_qkv, ga_o, gb_qkv, gb_o, ga_gu, gb_d, gm_qkv, gm_o, gm_d),
        (gb_gu, gm_gu, n_gu, ga_d),
        6,
    )
    layer_result, *summed, stats = finish(
        seq_size, rows_size, sums, x1, before_0, before_1, m_attn, n_attn, m_d, n_d, gate_up_magnitude
    )
    shape = (pair_rows, span_len, model_width)
    return (layer_result.reshape(shape), grad_inputs.reshape(shape), *summed, stats)

def solution(mesh):
    return jax.shard_map(
        local,
        mesh=mesh,
        in_specs=(
            P("rows", "seq", None),
            P("rows", "seq", None),
            P(),
            P(None, "seq", None),
            P(None, "seq", None),
            P(None, "seq", None),
            P("seq", None),
            P(),
            P(),
            P(),
            P(),
            P(),
            P(),
            P(),
            P(),
            P(),
            P(),
            P(),
            P(),
            P("rows"),
            P("rows"),
        ),
        out_specs=(
            P("rows", "seq", None),
            P("rows", "seq", None),
            P(),
            P(),
            P(),
            P(),
            P(),
            P(),
            P(),
            P(),
            P(),
            P(),
            P(),
            P(),
            P(),
        ),
        check_vma=False,
    )
```

```python
import functools

import jax
import jax.numpy as jnp
from jax import lax
from jax.experimental import pallas as pl
from jax.experimental.pallas import tpu as pltpu
from jax.sharding import PartitionSpec as P

HEADS = 32
KV_HEADS = 8
HEAD_DIM = 64
ADAPTER_RANK = 16
ALPHA = 32
SCALE = ALPHA / ADAPTER_RANK
TILE = 512

highest = lax.Precision.HIGHEST
last_last = (((1,), (1,)), ((), ()))
first_first = (((0,), (0,)), ((), ()))

def dot_f32(a, b):
    return jnp.dot(a, b, preferred_element_type=jnp.float32)


def dot_nt(a, b):
    return lax.dot_general(a, b, last_last, preferred_element_type=jnp.float32)


def dot_tn(a, b):
    return lax.dot_general(a, b, first_first, preferred_element_type=jnp.float32)


def in_hbm(*arrays):
    return [pltpu.with_memory_space_constraint(v, pltpu.HBM) for v in arrays]


def unit_rms(v):
    return lax.rsqrt(jnp.mean(v * v, axis=-1, keepdims=True) + 1e-05)


def rms_back(v, gain, upstream):
    r = unit_rms(v)
    scaled = gain * upstream
    return r * scaled - v * (r * r * r) * jnp.mean(scaled * v, axis=-1, keepdims=True)


def turn(z, cosine, sine):
    width = z.shape[1]
    lane = lax.broadcasted_iota(jnp.int32, z.shape, 1)
    half = HEAD_DIM // 2
    other = jnp.where(
        lax.rem(lane, HEAD_DIM) < half, -pltpu.roll(z, width - half, 1), pltpu.roll(z, half, 1)
    )
    copies = width // cosine.shape[1]
    return z * jnp.tile(cosine, (1, copies)) + other * jnp.tile(sine, (1, copies))


def column_squares(w):
    return jnp.sum(jnp.square(w.astype(jnp.float32)), axis=0, keepdims=True)


def two_terms(value):
    high = value.astype(jnp.bfloat16)
    return jnp.concatenate([high, (value - high.astype(jnp.float32)).astype(jnp.bfloat16)], axis=0)


def dot_two(terms, b):
    both = dot_f32(terms, b)
    half = both.shape[0] // 2
    return both[:half] + both[half:]


def column_norms(w, gram, b, cross):
    b_wide = b.astype(jnp.float32)
    gram_b = dot_two(gram, b)
    squares = column_squares(w) + 2.0 * SCALE * jnp.sum(b_wide * cross, axis=0, keepdims=True)
    squares = squares + SCALE * SCALE * jnp.sum(b_wide * gram_b, axis=0, keepdims=True)
    return jnp.sqrt(squares + 1e-06), cross + SCALE * gram_b


def project_kernel(kv_tiles, u_ref, inner_ref, gram_ref, a_ref, w_ref, b_ref, m_ref, cos_ref, sin_ref,
                   before_ref, q_ref, kv_ref, n_ref, cross_ref):
    j = pl.program_id(0)
    q_tiles, last = kv_tiles
    a = a_ref[0].astype(jnp.bfloat16)
    b = b_ref[...].astype(jnp.bfloat16)
    w = w_ref[0]
    rows = u_ref.shape[0]

    @pl.when(j <= last)
    def _():
        both = dot_f32(jnp.concatenate([u_ref[...], a], axis=0), w)
        norm, cross = column_norms(w, gram_ref[0], b, both[rows:])
        n_ref[...] = norm
        cross_ref[...] = cross
        before = both[:rows] + SCALE * dot_f32(inner_ref[0], b)
        before_ref[...] = before
        y = before * (m_ref[...] / norm)

        @pl.when(j < q_tiles)
        def _():
            q_ref[...] = turn(y, cos_ref[...], sin_ref[...]).astype(jnp.bfloat16)

        @pl.when(j == q_tiles)
        def _():
            kv_ref[...] = turn(y, cos_ref[...], sin_ref[...]).astype(jnp.bfloat16)

        @pl.when(j > q_tiles)
        def _():
            kv_ref[...] = y.astype(jnp.bfloat16)

    @pl.when(j > last)
    def _():
        norm, cross = column_norms(w, gram_ref[0], b, dot_f32(a, w))
        n_ref[...] = norm
        cross_ref[...] = cross


def project_qkv(u, inner, grams, a, weights, b, m, cosine, sine):
    rows, width = u.shape
    cols = b.shape[1]
    per_half = weights.shape[2] // TILE
    q_tiles = width // TILE
    k_cols = weights.shape[2] - width
    last = q_tiles + 2 * k_cols // TILE - 1
    full = lambda shape: pl.BlockSpec(shape, lambda j: (0,) * len(shape))
    col = lambda height: pl.BlockSpec((height, TILE), lambda j: (0, j))
    which = lambda j: jnp.where(j < q_tiles, 0, jnp.where(j > last, 3, 1 + j - q_tiles))
    f32, low = jnp.float32, jnp.bfloat16
    return pl.pallas_call(
        functools.partial(project_kernel, (q_tiles, last)),
        out_shape=(
            pltpu.HBM((rows, width + 2 * k_cols), f32),
            pltpu.HBM((rows, width), low),
            pltpu.HBM((rows, 2 * k_cols), low),
            pltpu.HBM((1, cols), f32),
            pltpu.HBM((16, cols), f32),
        ),
        grid=(cols // TILE,),
        in_specs=[
            full((rows, width)),
            pl.BlockSpec((1, rows, 16), lambda j: (jnp.minimum(which(j), 2), 0, 0)),
            pl.BlockSpec((1, 32, 16), lambda j: (which(j), 0, 0)),
            pl.BlockSpec((1, 16, width), lambda j: (which(j), 0, 0)),
            pl.BlockSpec((1, width, TILE), lambda j: (j // per_half, 0, j % per_half)),
            col(16),
            col(1),
            full(cosine.shape),
            full(sine.shape),
        ],
        out_specs=(
            pl.BlockSpec((rows, TILE), lambda j: (0, jnp.minimum(j, last))),
            pl.BlockSpec((rows, TILE), lambda j: (0, jnp.minimum(j, q_tiles - 1))),
            pl.BlockSpec((rows, TILE), lambda j: (0, jnp.clip(j - q_tiles, 0, last - q_tiles))),
            col(1),
            col(16),
        ),
        compiler_params=pltpu.CompilerParams(vmem_limit_bytes=40 << 20),
        cost_estimate=pl.CostEstimate(
            flops=2 * rows * width * cols, transcendentals=0, bytes_accessed=2 * width * cols
        ),
        name="project_qkv",
    )(*in_hbm(u), inner, grams, *in_hbm(a, weights, b), m, cosine, sine)


def out_kernel(att_ref, a_ref, w_ref, b_ref, m_ref, n_ref, x_ref, gain_ref, next_ref,
               before_ref, x1_ref, u2_ref, inner_ref):
    t = pl.program_id(0)
    a = a_ref[0].astype(jnp.bfloat16)
    b = b_ref[...].astype(jnp.bfloat16)
    inner = dot_nt(att_ref[...], a).astype(jnp.bfloat16)
    before = dot_f32(att_ref[...], w_ref[0]) + SCALE * dot_f32(inner, b)
    before_ref[...] = before
    x1_ref[:, pl.ds(pl.multiple_of(t * TILE, TILE), TILE)] = (
        x_ref[...].astype(jnp.float32) + before * (m_ref[...] / n_ref[...])
    )

    @pl.when(t == pl.num_programs(0) - 1)
    def _():
        v = x1_ref[...]
        u2 = (v * unit_rms(v) * gain_ref[...]).astype(jnp.bfloat16)
        u2_ref[...] = u2
        following = next_ref[...].reshape(-1, u2.shape[1]).astype(jnp.bfloat16)
        inner_ref[...] = jnp.zeros_like(inner_ref)
        inner_ref[:, : following.shape[0]] = dot_nt(u2, following).astype(jnp.bfloat16)


def project_out(att, a, weights, b, m, norms, x, gain, following):
    rows, width = att.shape
    tiles = width // TILE
    skip = (weights.shape[2] - width) // TILE
    full = lambda shape: pl.BlockSpec(shape, lambda t: (0,) * len(shape))
    col = lambda height: pl.BlockSpec((height, TILE), lambda t: (0, t))
    ahead = b.shape[1] // TILE - tiles
    later = lambda height: pl.BlockSpec((height, TILE), lambda t: (0, ahead + t))
    f32 = jnp.float32
    return pl.pallas_call(
        out_kernel,
        out_shape=(
            pltpu.HBM((rows, width), f32),
            pltpu.HBM((rows, width), f32),
            pltpu.HBM((rows, width), jnp.bfloat16),
            pltpu.HBM((rows, 128), jnp.bfloat16),
        ),
        grid=(tiles,),
        in_specs=[
            full((rows, width)),
            pl.BlockSpec((1, 16, width), lambda t: (3, 0, 0)),
            pl.BlockSpec((1, width, TILE), lambda t: (1, 0, skip + t)),
            later(16),
            later(1),
            later(1),
            col(rows),
            full((1, width)),
            full(following.shape),
        ],
        out_specs=(col(rows), full((rows, width)), full((rows, width)), full((rows, 128))),
        compiler_params=pltpu.CompilerParams(vmem_limit_bytes=40 << 20),
        cost_estimate=pl.CostEstimate(
            flops=2 * rows * width * width, transcendentals=0, bytes_accessed=2 * width * width
        ),
        name="project_out",
    )(*in_hbm(att, a, weights, b), m, norms, *in_hbm(x), gain, *in_hbm(following))


def out_back_kernel(in_ref, x1_ref, gain_ref, gy_ref, before_ref, att_ref, a_ref, b_ref, m_ref, n_ref, cross_ref,
                    w_ref, gx_ref, gatt_ref, ga_ref, gb_ref, gm_ref, lhs, gi, tail):
    t = pl.program_id(0)
    rows, width = gx_ref.shape
    low = jnp.bfloat16
    a = a_ref[0].astype(low)
    o_cols = slice(b_ref.shape[1] - width, b_ref.shape[1])

    @pl.when(t == 0)
    def _():
        gx = gy_ref[...].astype(jnp.float32) + rms_back(x1_ref[...], gain_ref[...], in_ref[...])
        gx_ref[...] = gx
        norm, m = n_ref[:, o_cols], m_ref[:, o_cols]
        gb = (gx * (m / norm)).astype(low)
        lhs[:rows] = gb
        b = b_ref[:, o_cols].astype(low)
        gi[...] = (SCALE * dot_nt(gb, b)).astype(low)
        gm = jnp.sum(gx * before_ref[...], axis=0, keepdims=True) / norm
        gm_ref[...] = gm
        c = -gm * m / (norm * norm)
        weighted = (b.astype(jnp.float32) * c).astype(low)
        lhs[rows:] = weighted
        tail[...] = two_terms(dot_nt(weighted, b))
        inner = dot_nt(att_ref[...], a).astype(low)
        gb_ref[...] = SCALE * dot_tn(inner, gb) + SCALE * c * cross_ref[:, o_cols]

    span = pl.ds(pl.multiple_of(t * TILE, TILE), TILE)
    a_tile = a_ref[0, :, span].astype(low)
    gi_low = gi[...]
    back = dot_nt(lhs[...], w_ref[0, :, w_ref.shape[2] - width :])
    gatt_ref[...] = (back[:rows] + dot_f32(gi_low, a_tile)).astype(low)
    spread = back[rows:] + SCALE * dot_two(tail[...], a_tile)
    ga_ref[...] = dot_tn(gi_low, att_ref[:, span]) + SCALE * spread


def out_back(in_grad, x1, gain, gy, before, att, a, b, m, norms, cross, weights):
    rows, width = x1.shape
    tiles = width // TILE
    full = lambda shape: pl.BlockSpec(shape, lambda t: (0,) * len(shape))
    col = lambda height: pl.BlockSpec((height, TILE), lambda t: (0, t))
    f32, low = jnp.float32, jnp.bfloat16
    wide = full((rows, width))
    return pl.pallas_call(
        out_back_kernel,
        out_shape=(
            pltpu.HBM((rows, width), f32),
            pltpu.HBM((rows, width), low),
            jax.ShapeDtypeStruct((16, width), f32),
            jax.ShapeDtypeStruct((16, width), f32),
            jax.ShapeDtypeStruct((1, width), f32),
        ),
        grid=(tiles,),
        in_specs=[wide, wide, full((1, width)), wide, wide, wide,
                  pl.BlockSpec((1, 16, width), lambda t: (3, 0, 0)),
                  full(b.shape), full(m.shape), full(norms.shape), full(cross.shape),
                  pl.BlockSpec((1, TILE, weights.shape[2]), lambda t: (1, t, 0))],
        out_specs=(wide, col(rows), col(16), full((16, width)), full((1, width))),
        scratch_shapes=[
            pltpu.VMEM((rows + 16, width), low),
            pltpu.VMEM((rows, 16), low),
            pltpu.VMEM((32, 16), low),
        ],
        compiler_params=pltpu.CompilerParams(vmem_limit_bytes=48 << 20),
        cost_estimate=pl.CostEstimate(flops=0, transcendentals=0, bytes_accessed=1 << 20),
        name="out_back",
    )(in_grad, *in_hbm(x1), gain, *in_hbm(gy, before, att, a, b), m, norms, *in_hbm(cross, weights))


def qkv_back_kernel(gq_ref, gkv_ref, cos_ref, sin_ref, before_ref, u_ref, inner_ref, a_ref, b_ref, m_ref, n_ref, cross_ref,
                    x_ref, gain_ref, gx_ref, w0_ref, w1_ref,
                    out_ref, ga_ref, gb_ref, gm_ref, lhs0, lhs1, gi, tail):
    t = pl.program_id(0)
    rows, width = gx_ref.shape
    low = jnp.bfloat16
    k_cols = w1_ref.shape[2]
    bounds = [(0, width), (width, width + k_cols), (width + k_cols, width + 2 * k_cols)]

    @pl.when(t == 0)
    def _():
        cosine, sine = cos_ref[...], -sin_ref[...]
        k_parts = [gkv_ref[:, 256 * j : 256 * j + 128] for j in range(k_cols // 128)]
        v_parts = [gkv_ref[:, 256 * j + 128 : 256 * j + 256] for j in range(k_cols // 128)]
        rounded = lambda z: z.astype(low).astype(jnp.float32)
        ups = [
            turn(gq_ref[...].astype(jnp.float32), cosine, sine),
            turn(rounded(jnp.concatenate(k_parts, axis=1)), cosine, sine),
            rounded(jnp.concatenate(v_parts, axis=1)),
        ]
        lhs0[rows:] = jnp.zeros_like(lhs0[rows:])
        lhs1[rows:] = jnp.zeros_like(lhs1[rows:])
        for p, (start, stop) in enumerate(bounds):
            g, norm, m = ups[p], n_ref[:, start:stop], m_ref[:, start:stop]
            b = b_ref[:, start:stop].astype(low)
            gb = (g * (m / norm)).astype(low)
            gm = jnp.sum(g * before_ref[:, start:stop], axis=0, keepdims=True) / norm
            gm_ref[:, start:stop] = gm
            c = -gm * m / (norm * norm)
            weighted = (b.astype(jnp.float32) * c).astype(low)
            gi[:, 16 * p : 16 * p + 16] = (SCALE * dot_nt(gb, b)).astype(low)
            tail[p] = two_terms(dot_nt(weighted, b))
            gb_ref[:, start:stop] = SCALE * dot_tn(inner_ref[p], gb) + SCALE * c * cross_ref[:, start:stop]
            lhs, at = (lhs1, 0) if p == 2 else (lhs0, start)
            lhs[:rows, at : at + stop - start] = gb
            lhs[rows + 16 * p : rows + 16 * p + 16, at : at + stop - start] = weighted

    span = pl.ds(pl.multiple_of(t * TILE, TILE), TILE)
    back = dot_nt(lhs0[...], w0_ref[0]) + dot_nt(lhs1[...], w1_ref[0])
    grad_in = back[:rows]
    for p in range(3):
        a_tile = a_ref[p, :, span].astype(low)
        gi_p = gi[:, 16 * p : 16 * p + 16]
        grad_in = grad_in + dot_f32(gi_p, a_tile)
        spread = back[rows + 16 * p : rows + 16 * p + 16] + SCALE * dot_two(tail[p], a_tile)
        ga_ref[p] = dot_tn(gi_p, u_ref[:, span]) + SCALE * spread
    out_ref[:, span] = grad_in

    @pl.when(t == pl.num_programs(0) - 1)
    def _():
        v = x_ref[...].astype(jnp.float32)
        out_ref[...] = gx_ref[...] + rms_back(v, gain_ref[...], out_ref[...])


def qkv_back(gq, gkv, cosine, sine, before, u, inner, a, b, m, norms, cross, x, gain, gx, weights):
    rows, width = gx.shape
    cols = before.shape[1]
    k_cols = (cols - width) // 2
    tiles = width // TILE
    full = lambda shape: pl.BlockSpec(shape, lambda t: (0,) * len(shape))
    f32, low = jnp.float32, jnp.bfloat16
    wide = full((rows, width))
    return pl.pallas_call(
        qkv_back_kernel,
        out_shape=(
            pltpu.HBM((rows, width), f32),
            jax.ShapeDtypeStruct((3, 16, width), f32),
            jax.ShapeDtypeStruct((16, cols), f32),
            jax.ShapeDtypeStruct((1, cols), f32),
        ),
        grid=(tiles,),
        in_specs=[wide, full(gkv.shape), full(cosine.shape), full(sine.shape), full((rows, cols)), wide, full(inner.shape),
                  full(a.shape), full(b.shape), full(m.shape), full(norms.shape), full(cross.shape),
                  wide, full((1, width)), wide,
                  pl.BlockSpec((1, TILE, width + k_cols), lambda t: (0, t, 0)),
                  pl.BlockSpec((1, TILE, k_cols), lambda t: (1, t, 0))],
        out_specs=(wide, pl.BlockSpec((3, 16, TILE), lambda t: (0, 0, t)), full((16, cols)), full((1, cols))),
        scratch_shapes=[
            pltpu.VMEM((rows + 48, width + k_cols), low),
            pltpu.VMEM((rows + 48, k_cols), low),
            pltpu.VMEM((rows, 48), low),
            pltpu.VMEM((3, 32, 16), low),
        ],
        compiler_params=pltpu.CompilerParams(vmem_limit_bytes=48 << 20),
        cost_estimate=pl.CostEstimate(flops=0, transcendentals=0, bytes_accessed=1 << 20),
        name="qkv_back",
    )(*in_hbm(gq), gkv, cosine, sine, *in_hbm(before, u), inner, *in_hbm(a, b), m, norms, *in_hbm(cross, x), gain,
      *in_hbm(gx, weights, weights))

MESH = pl.DeviceIdType.MESH


def place_in_seq():
    s = lax.axis_index("seq")
    return s, s // 2, lax.rem(s, 2)

def near_first(i, q, nc):
    short = jnp.where(q <= nc - 1 - q, q, nc - 1 - q)
    far = jnp.where(q <= nc - 1 - q, i, nc - 1 - i)
    step = (i + 1) // 2
    near = q - step if i % 2 else q + step
    return jnp.where(i <= 2 * short, near, far)


def place_in_rows(rows):
    half = rows // 2
    r = lax.axis_index("rows")
    a, b = r // 2, lax.rem(r, 2)
    turned = lambda k: 2 * lax.rem(a + k + half, half)
    return r, 2 * a + 1 - b, lambda k: turned(k) + b, lambda k: turned(k) + 1 - b


def greet_all(n, rows):
    s = lax.axis_index("seq")
    r, b_row, a_row, _ = place_in_rows(rows)
    barrier = pltpu.get_barrier_semaphore()
    for t in range(1, n):
        pl.semaphore_signal(
            barrier, inc=1, device_id=(r, lax.rem(s + t, n)), device_id_type=MESH
        )
    pl.semaphore_signal(barrier, inc=1, device_id=(b_row, s), device_id_type=MESH)
    for k in range(1, rows // 2):
        pl.semaphore_signal(barrier, inc=1, device_id=(a_row(k), s), device_id_type=MESH)
    pl.semaphore_wait(barrier, n - 1 + rows // 2)


def remote(src, dst, send, recv, row, seq):
    return pltpu.make_async_remote_copy(
        src_ref=src, dst_ref=dst, send_sem=send, recv_sem=recv,
        device_id=(row, seq), device_id_type=MESH,
    )


def weights_kernel(n, rows, qo, kv, xg, wd_hbm, ad_hbm, bd_hbm, x_hbm, gain_ref, aa_hbm, ag_hbm,
                   wa, gz, near, sq_ref, gram_ref, u_hbm, inner_ref,
                   wd, ad_ref, bd_ref, x_ref, aa_ref, ag_ref, own_ref, cols_ref, local, edge, a_in, a_sib_in, a_out, a_sib_out, z_in, z_out):
    nc, half = n // 2, rows // 2
    others = half - 1
    units = gz.shape[-1]
    s, q, c = place_in_seq()
    sibling = s + 1 - 2 * c
    r, b_row, a_row, diagonal = place_in_rows(rows)
    greet_all(n, rows)

    both, first, second = pl.ds(0, 2), pl.ds(0, 1), pl.ds(1, 1)
    LINE, FROM_B = 0, 1

    def from_a(k):
        return 1 + k

    def relay_b(k):
        return 1 + others + k

    def relay_a(k):
        return 1 + 2 * others + k

    def a_view(p, core, parts, row):
        return wa.at[parts, 2 * p + core, row]

    def content(kind):
        if kind == LINE:
            return both, r
        if kind == FROM_B:
            return both, b_row
        for k in range(1, half):
            if kind == from_a(k):
                return both, a_row(-k)
            if kind == relay_b(k):
                return second, diagonal(-k)
            if kind == relay_a(k):
                return first, diagonal(-k)

    kinds = 2 + 3 * others

    def a_send(p, parts, row, kind, target_row):
        return remote(
            a_view(p, c, parts, row), a_view(p, c, parts, row),
            a_out.at[p, kind], a_in.at[p, kind], target_row, s,
        )

    def a_arrival(p, kind):
        parts, row = content(kind)
        return a_send(p, parts, row, kind, r)

    def a_to_sibling(p, kind, core):
        parts, row = content(kind)
        return remote(
            a_view(p, core, parts, row), a_view(p, core, parts, row),
            a_sib_out.at[p, kind], a_sib_in.at[p, kind], r, sibling,
        )

    def columns(device):
        return pl.ds(pl.multiple_of(device * units, units), units)

    def z_send(p, core):
        return remote(
            xg.at[:, r, :, columns(2 * p + core)], gz.at[:, s],
            z_out.at[p, core], z_in.at[q, c], r, 2 * p + core,
        )

    def z_arrival(p, core):
        slot = gz.at[:, 2 * p + core]
        return remote(slot, slot, z_out.at[p, core], z_in.at[p, core], r, s)

    def line_send(p, sem, target):
        view = a_view(p, c, both, r)
        return remote(view, view, sem, a_in.at[p, LINE], r, target)

    wide, k_cols = qo.shape[-1], kv.shape[-1]
    blocks = [(qo, 0, 0), (kv, 0, wide), (kv, 1, 0), (qo, 1, k_cols)]

    def own_blocks(part, out):
        for source, i, start in blocks:
            columns_of = pl.ds(start, source.shape[-1])
            out(source.at[i, part], i, columns_of)

    def own_line(sem, target):
        own_blocks(
            r,
            lambda src, i, cols: remote(
                src, wa.at[i, s, r, :, cols], sem, a_in.at[q, LINE], r, target
            ).start(),
        )

    pl.when(q > 0)(lambda: own_line(edge.at[0], s - 2))
    pl.when(q < nc - 1)(lambda: own_line(edge.at[1], s + 2))
    order = [near_first(i, q, nc) for i in range(nc)]
    whole_block = wa.at[:, s]
    sib_a = lambda: remote(whole_block, whole_block, edge.at[2], edge.at[3], r, sibling)
    sib_g = lambda: remote(
        xg.at[:, :, :, columns(sibling)], near.at[:, c], edge.at[4], edge.at[5], r, sibling
    )
    keep_a = pltpu.make_async_copy(own_ref, whole_block, local.at[0])
    keep_g = pltpu.make_async_copy(cols_ref, near.at[:, c], local.at[1])
    all_parts = pl.ds(0, rows)
    own_blocks(
        all_parts,
        lambda src, i, cols: remote(
            src, wa.at[i, s, :, :, cols], edge.at[2], edge.at[3], r, sibling
        ).start(),
    )
    own_blocks(
        all_parts,
        lambda src, i, cols: pltpu.make_async_copy(
            src, own_ref.at[i, :, :, cols], local.at[9]
        ).start(),
    )
    take_cols = pltpu.make_async_copy(xg.at[:, :, :, columns(s)], cols_ref, local.at[10])
    take_cols.start()
    takes = [
        pltpu.make_async_copy(src, dst, local.at[3 + i])
        for i, (src, dst) in enumerate(
            [(x_hbm, x_ref), (aa_hbm, aa_ref), (ag_hbm, ag_ref), (ad_hbm, ad_ref), (bd_hbm, bd_ref), (wd_hbm, wd)]
        )
    ]
    for cp in takes:
        cp.start()
    for cp in takes:
        cp.wait()
    pltpu.make_async_copy(own_ref, own_ref, local.at[9]).wait()
    keep_a.start()
    take_cols.wait()
    keep_g.start()
    low = jnp.bfloat16
    v = x_ref[...].astype(jnp.float32)
    u = (v * unit_rms(v) * gain_ref[...]).astype(low)
    x_ref[...] = u
    keep_u = pltpu.make_async_copy(x_ref, u_hbm, local.at[2])
    keep_u.start()
    for g in range(4):
        a = aa_ref[g].astype(low)
        gram_ref[g] = two_terms(dot_nt(a, a))
        if g < 3:
            inner_ref[g] = dot_nt(u, a).astype(low)
    for g in range(2):
        a = ag_ref[g].astype(low)
        gram_ref[4 + g] = two_terms(dot_nt(a, a))

    def down_squares():
        a = ad_ref[...].astype(low)
        gram_ref[6] = two_terms(dot_nt(a, a))
        mine = pl.ds(pl.multiple_of(s * wd.shape[0], wd.shape[0]), wd.shape[0])
        cross = dot_f32(ad_ref[:, mine].astype(low), wd[...])
        b_wide = bd_ref[...].astype(low).astype(jnp.float32)
        sq_ref[...] = column_squares(wd[...]) + 2.0 * SCALE * jnp.sum(b_wide * cross, axis=0, keepdims=True)

    for p in order[1:]:
        a_arrival(p, LINE).wait_recv()
        pl.when((p < q) & (q < nc - 1))(
            lambda p=p: line_send(p, a_out.at[p, LINE], s + 2).start()
        )
        pl.when((p > q) & (q > 0))(
            lambda p=p: line_send(p, a_out.at[p, LINE], s - 2).start()
        )
        a_send(p, both, r, FROM_B, b_row).start()
        for k in range(1, half):
            a_send(p, both, r, from_a(k), a_row(k)).start()
        a_to_sibling(p, LINE, c).start()
    for p in order[1:]:
        for core in range(2):
            z_send(p, core).start()
    sib_g().start()
    down_squares()
    keep_u.wait()
    for p in order[1:]:
        a_arrival(p, FROM_B).wait_recv()
        for k in range(1, half):
            a_send(p, first, b_row, relay_a(k), a_row(k)).start()
        a_to_sibling(p, FROM_B, c).start()
        for k in range(1, half):
            a_arrival(p, from_a(k)).wait_recv()
            a_send(p, second, a_row(-k), relay_b(k), b_row).start()
            a_to_sibling(p, from_a(k), c).start()
    for p in order[1:]:
        for k in range(1, half):
            for kind in (relay_b(k), relay_a(k)):
                a_arrival(p, kind).wait_recv()
                a_to_sibling(p, kind, c).start()
    keep_a.wait()
    keep_g.wait()
    sib_a().wait()
    sib_g().wait()
    pl.when(q > 0)(lambda: line_send(q, edge.at[0], s).wait_send())
    pl.when(q < nc - 1)(lambda: line_send(q, edge.at[1], s).wait_send())
    for p in order[1:]:
        pl.when(((p < q) & (q < nc - 1)) | ((p > q) & (q > 0)))(
            lambda p=p: line_send(p, a_out.at[p, LINE], s).wait_send()
        )
        for kind in range(kinds):
            a_to_sibling(p, kind, c).wait_send()
            a_to_sibling(p, kind, 1 - c).wait_recv()
        a_send(p, both, r, FROM_B, b_row).wait_send()
        for k in range(1, half):
            a_send(p, both, r, from_a(k), r).wait_send()
            a_send(p, first, b_row, relay_a(k), r).wait_send()
            a_send(p, second, a_row(-k), relay_b(k), r).wait_send()
        for core in range(2):
            z_send(p, core).wait_send()
            z_arrival(p, core).wait_recv()


def gather_weights(n, rows, qo, kv, xg, wd, ad, bd, x, gain, aa, ag, collective_id):
    nc = n // 2
    _, block, width = qo.shape
    part = block // rows
    cols = width + kv.shape[2]
    qo = qo.reshape(2, rows, part, width)
    kv = kv.reshape(2, rows, part, kv.shape[2])
    xg = xg.reshape(2, rows, part, xg.shape[2])
    units = xg.shape[3] // n
    kinds = 2 + 3 * (rows // 2 - 1)
    dma = pltpu.SemaphoreType.DMA
    anywhere = pl.BlockSpec(memory_space=pltpu.HBM)
    vmem = pl.BlockSpec(memory_space=pltpu.VMEM)
    low = qo.dtype
    wa, gz, near, sq, grams, u, inner = pl.pallas_call(
        functools.partial(weights_kernel, n, rows),
        out_shape=(
            pltpu.HBM((2, n, rows, part, cols), low),
            pltpu.HBM((2, n, part, units), low),
            pltpu.HBM((2, 2, rows, part, units), low),
            jax.ShapeDtypeStruct((1, width), jnp.float32),
            jax.ShapeDtypeStruct((7, 32, 16), low),
            pltpu.HBM(x.shape, low),
            jax.ShapeDtypeStruct((3, x.shape[0], 16), low),
        ),
        in_specs=[anywhere] * 7 + [vmem] + [anywhere] * 2,
        out_specs=(anywhere,) * 3 + (vmem,) * 2 + (anywhere, vmem),
        scratch_shapes=[pltpu.VMEM(v.shape, v.dtype) for v in (wd, ad, bd, x, aa, ag)]
        + [pltpu.VMEM((2, rows, part, cols), low), pltpu.VMEM((2, rows, part, units), low)]
        + [dma((11,)), dma((6,))]
        + [dma((nc, kinds))] * 4
        + [dma((nc, 2))] * 2,
        compiler_params=pltpu.CompilerParams(
            collective_id=collective_id, has_side_effects=True, vmem_limit_bytes=32 << 20
        ),
        cost_estimate=pl.CostEstimate(
            flops=0, transcendentals=0, bytes_accessed=250 * 1024 * 1024
        ),
        name="gather_weights",
    )(*in_hbm(qo, kv, xg, wd, ad, bd, x), gain, *in_hbm(aa, ag))
    return wa.reshape(2, n * block, cols), gz, near, sq, grams, u, inner


def gather_kernel(n, rows, count, shared, *refs):
    nc = n // 2
    sources = refs[: count + len(shared[0])]
    outs = refs[len(sources) : 2 * len(sources) - len(shared[0]) + len(shared[1])]
    scratch = refs[len(sources) + len(outs) :]
    held_here = scratch[:count]
    local_sem, to_sib, to_left, to_right, recv, share_out, share_in = scratch[count:]
    xs, held, swapped = sources[:count], sources[count:], outs[count:]
    s, q, c = place_in_seq()
    sibling = s + 1 - 2 * c
    r, b_row, a_row, _ = place_in_rows(rows)
    greet_all(n, rows)
    takes = [pltpu.make_async_copy(xs[k], held_here[k], local_sem.at[0, k]) for k in range(count)]
    keeps = [
        pltpu.make_async_copy(held_here[k], outs[k].at[s], local_sem.at[1, k]) for k in range(count)
    ]
    for cp in takes:
        cp.start()

    def copy(k, src, slot, sems, target):
        return remote(src, outs[k].at[slot], sems.at[k, slot], recv.at[k, slot], r, target)

    def share(i, p):
        source, piece, turn, _ = shared[1][i]
        pair = pl.ds(2 * p, 2)
        src = held[source].at[pair] if piece is None else held[source].at[piece, pair]
        target = b_row if turn == 0 else a_row(turn)
        return remote(src, swapped[i].at[pair], share_out.at[i, p], share_in.at[i, p], target, s)

    for k in range(count):
        pl.when(q > 0)(lambda k=k: copy(k, xs[k], s, to_left, s - 2).start())
        pl.when(q < nc - 1)(lambda k=k: copy(k, xs[k], s, to_right, s + 2).start())
        copy(k, xs[k], s, to_sib, sibling).start()
    order = [near_first(i, q, nc) for i in range(nc)]
    for p in order[1:]:
        for i in range(len(shared[1])):
            share(i, p).start()
    for take, keep in zip(takes, keeps):
        take.wait()
        keep.start()
    for p in order[1:]:
        slot = 2 * p + c
        for k in range(count):
            src = outs[k].at[slot]
            copy(k, src, slot, to_right, s).wait_recv()
            pl.when((p < q) & (q < nc - 1))(
                lambda k=k, src=src, slot=slot: copy(k, src, slot, to_right, s + 2).start()
            )
            pl.when((p > q) & (q > 0))(
                lambda k=k, src=src, slot=slot: copy(k, src, slot, to_left, s - 2).start()
            )
            copy(k, src, slot, to_sib, sibling).start()
    for cp in keeps:
        cp.wait()
    for p in range(nc):
        mine, theirs = 2 * p + c, 2 * p + 1 - c
        for k in range(count):
            copy(k, outs[k].at[theirs], theirs, to_sib, sibling).wait_recv()
            copy(k, outs[k].at[mine], mine, to_sib, sibling).wait_send()
            pl.when((q < nc - 1) & (p <= q))(
                lambda k=k, mine=mine: copy(k, outs[k].at[mine], mine, to_right, s).wait_send()
            )
            pl.when((q > 0) & (p >= q))(
                lambda k=k, mine=mine: copy(k, outs[k].at[mine], mine, to_left, s).wait_send()
            )
    for p in order[1:]:
        for i in range(len(shared[1])):
            share(i, p).wait_send()
            share(i, p).wait_recv()


def gather_seq(n, rows, arrays, collective_id, held=(), shares=()):
    nc, count = n // 2, len(arrays)
    nbytes = sum(a.size * a.dtype.itemsize for a in arrays)
    dma = pltpu.SemaphoreType.DMA
    shape = jax.ShapeDtypeStruct
    outs = [shape((n, *a.shape), a.dtype) for a in arrays]
    outs += [shape(held[source].shape[-3:], held[source].dtype) for source, _, _ in shares]
    anywhere = pl.BlockSpec(memory_space=pltpu.HBM)
    listed = (tuple(held), [(source, piece, turn, None) for source, piece, turn in shares])
    sems = dma((max(1, len(shares)), nc))
    got = pl.pallas_call(
        functools.partial(gather_kernel, n, rows, count, (range(len(held)), listed[1])),
        out_shape=tuple(outs),
        in_specs=[anywhere] * (count + len(held)),
        out_specs=(anywhere,) * len(outs),
        scratch_shapes=[pltpu.VMEM(a.shape, a.dtype) for a in arrays]
        + [dma((2, count))]
        + [dma((count, n))] * 4
        + [sems] * 2,
        compiler_params=pltpu.CompilerParams(collective_id=collective_id, has_side_effects=True),
        cost_estimate=pl.CostEstimate(flops=0, transcendentals=0, bytes_accessed=nbytes * n * 20),
        name="gather_seq",
    )(*arrays, *held)
    return got[:count], got[count:]

def swap_halves(x):
    return pltpu.roll(x.astype(jnp.float32), HEAD_DIM, 1)


def stack_heads(block):
    lane = lax.broadcasted_iota(jnp.int32, (block.shape[0], 128), 1)
    rows = []
    for h in range(8):
        pair = block[:, (h // 2) * 128 : (h // 2 + 1) * 128].astype(jnp.float32)
        if h % 2 != h // 4:
            pair = swap_halves(pair)
        keep = lane < HEAD_DIM if h // 4 == 0 else lane >= HEAD_DIM
        rows.append(jnp.where(keep, pair, 0.0).astype(jnp.bfloat16))
    return jnp.concatenate(rows, axis=0)


def unstack_heads(stacked, span):
    lane = lax.broadcasted_iota(jnp.int32, (span, 128), 1)
    pairs = []
    for t in range(4):
        first = stacked[2 * t * span : (2 * t + 1) * span]
        second = stacked[(2 * t + 1) * span : (2 * t + 2) * span]
        if t < 2:
            second = swap_halves(second)
        else:
            first = swap_halves(first)
        pairs.append(jnp.where(lane < HEAD_DIM, first, second))
    return jnp.concatenate(pairs, axis=1)


def attend_kernel(valid_ref, q_ref, k_ref, v_ref, o_ref, p_ref):
    span = q_ref.shape[1]
    keys = k_ref.shape[0] * span
    q8 = stack_heads(q_ref[0])
    k2 = k_ref[:, 0].reshape(keys, 128)
    v2 = v_ref[:, 0].reshape(keys, 128)
    scores = lax.dot_general(q8, k2, last_last, preferred_element_type=jnp.float32)
    scores = scores * HEAD_DIM**-0.5
    first_pos = lax.axis_index("seq") * span
    q_pos = first_pos + lax.broadcasted_iota(jnp.int32, (8, span, keys), 1).reshape(8 * span, keys)
    k_pos = lax.broadcasted_iota(jnp.int32, (8 * span, keys), 1)
    allowed = (k_pos <= q_pos) & (k_pos < valid_ref[pl.program_id(0)])
    scores = jnp.where(allowed, scores, -1e30)
    unscaled = jnp.exp(scores - jnp.max(scores, axis=1, keepdims=True))
    shares = unscaled * (1.0 / jnp.sum(unscaled, axis=1, keepdims=True))
    shares = shares.astype(jnp.bfloat16)
    p_ref[0, 0] = shares
    mixed = jnp.dot(shares, v2, preferred_element_type=jnp.float32)
    o_ref[0] = unstack_heads(mixed, span).astype(jnp.bfloat16)


def attend(q, kv, valid):
    pair, span, width = q.shape
    n, kv_width = kv.shape[0], kv.shape[3] // 2
    groups = kv_width // 128
    keys = n * span
    q_spec = pl.BlockSpec((1, span, 512), lambda p, j, *_: (p, 0, j))
    flops = 4 * pair * groups * 8 * span * keys * 128
    return pl.pallas_call(
        attend_kernel,
        out_shape=(
            pltpu.HBM(q.shape, jnp.bfloat16),
            pltpu.HBM((pair, groups, 8 * span, keys), jnp.bfloat16),
        ),
        grid_spec=pltpu.PrefetchScalarGridSpec(
            num_scalar_prefetch=1,
            grid=(pair, groups),
            in_specs=[
                q_spec,
                pl.BlockSpec((n, 1, span, 128), lambda p, j, *_: (0, p, 0, j)),
                pl.BlockSpec((n, 1, span, 128), lambda p, j, *_: (0, p, 0, groups + j)),
            ],
            out_specs=(
                q_spec,
                pl.BlockSpec((1, 1, 8 * span, keys), lambda p, j, *_: (p, j, 0, 0)),
            ),
        ),
        compiler_params=pltpu.CompilerParams(vmem_limit_bytes=40 << 20),
        cost_estimate=pl.CostEstimate(
            flops=flops, transcendentals=flops // 512, bytes_accessed=8 << 20
        ),
        name="attend",
    )(valid, *in_hbm(q, kv, kv))


def attend_back_kernel(q_ref, k_ref, v_ref, p_ref, g_ref, gq_ref, gkv_ref):
    span = q_ref.shape[1]
    keys = k_ref.shape[0] * span
    q8 = stack_heads(q_ref[0])
    g8 = stack_heads(g_ref[0])
    k2 = k_ref[:, 0].reshape(keys, 128)
    v2 = v_ref[:, 0].reshape(keys, 128)
    low = p_ref[0, 0]
    shares = low.astype(jnp.float32)
    grad_shares = lax.dot_general(g8, v2, last_last, preferred_element_type=jnp.float32)
    weighted = shares * grad_shares
    centre = jnp.sum(weighted, axis=1, keepdims=True)
    grad_scores = (weighted - shares * centre).astype(jnp.bfloat16)
    gq = jnp.dot(grad_scores, k2, preferred_element_type=jnp.float32) * HEAD_DIM**-0.5
    gq_ref[0] = unstack_heads(gq, span).astype(jnp.bfloat16)
    gk = lax.dot_general(grad_scores, q8, first_first, preferred_element_type=jnp.float32)
    gv = lax.dot_general(low, g8, first_first, preferred_element_type=jnp.float32)
    both = jnp.concatenate([gk * HEAD_DIM**-0.5, gv], axis=1).astype(jnp.bfloat16)
    gkv_ref[:, 0] = both.reshape(gkv_ref.shape[0], span, 256)


def attend_back(q, kv, shares, g):
    pair, span, _ = q.shape
    n, kv_width = kv.shape[0], kv.shape[3] // 2
    groups = kv_width // 128
    keys = n * span
    q_spec = pl.BlockSpec((1, span, 512), lambda p, j: (p, 0, j))
    return pl.pallas_call(
        attend_back_kernel,
        out_shape=(
            pltpu.HBM(q.shape, jnp.bfloat16),
            pltpu.HBM(kv.shape, jnp.bfloat16),
        ),
        grid=(pair, groups),
        in_specs=[
            q_spec,
            pl.BlockSpec((n, 1, span, 128), lambda p, j: (0, p, 0, j)),
            pl.BlockSpec((n, 1, span, 128), lambda p, j: (0, p, 0, groups + j)),
            pl.BlockSpec((1, 1, 8 * span, keys), lambda p, j: (p, j, 0, 0)),
            q_spec,
        ],
        out_specs=(
            q_spec,
            pl.BlockSpec((n, 1, span, 256), lambda p, j: (0, p, 0, j)),
        ),
        compiler_params=pltpu.CompilerParams(vmem_limit_bytes=40 << 20),
        cost_estimate=pl.CostEstimate(flops=0, transcendentals=0, bytes_accessed=1 << 20),
        name="attend_back",
    )(*in_hbm(q, kv, kv, shares, g))

def by_distance(i, q, nc):
    room = nc - 1 - q
    left_half = q <= room
    short = jnp.where(left_half, q, room)
    far = jnp.where(left_half, i, nc - 1 - i)
    step = (i + 1) // 2
    near = jnp.where(lax.rem(i, 2) == 1, q - step, q + step)
    return jnp.where(i <= 2 * short, near, far)


def ffn_kernel(n, rows, pieces, u_hbm, inner_hbm, gy0_hbm, gy1_hbm, wd_hbm, a_ref, b_ref, m_ref, ad_ref, bd_ref, md_ref, sq_ref, gram_ref,
               in_ref, down0_hbm, down1_hbm, ga_ref, gb_ref, gm_ref, norm_ref, gad_ref, gbd_ref, gmd_ref, nd_ref,
               w_parts, wd, u, side, gy, down, own, theirs, sib, from_left, from_right, ratio, cross, gm_all,
               w_sem, load_sem, down_sem, small_out, small_in, to_sib, sib_in, to_right, right_in, to_left, left_in):
    nc = n // 2
    f32, low = jnp.float32, jnp.bfloat16
    s, q, c = place_in_seq()
    tokens = own.shape[1]

    weights = [pltpu.make_async_copy(wd_hbm, wd, w_sem.at[0])]
    for src, dst in place_pieces(n, rows, pieces, w_parts):
        weights.append(pltpu.make_async_copy(src, dst, w_sem.at[len(weights)]))
    for cp in weights:
        cp.start()

    def loads(i):
        p = by_distance(nc - 1 - i, q, nc)
        slot = lax.rem(i, 2)
        pair = pl.ds(2 * p, 2)
        return (
            pltpu.make_async_copy(u_hbm.at[pair], u.at[slot], load_sem.at[0, slot]),
            pltpu.make_async_copy(
                gy0_hbm.at[pair], gy.at[slot, :, : tokens // 2], load_sem.at[1, slot]
            ),
            pltpu.make_async_copy(
                gy1_hbm.at[pair], gy.at[slot, :, tokens // 2 :], load_sem.at[2, slot]
            ),
            pltpu.make_async_copy(inner_hbm.at[pair], side.at[slot], load_sem.at[3, slot]),
        )

    for cp in loads(0):
        cp.start()
    sibling = s + 1 - 2 * c
    barrier = pltpu.get_barrier_semaphore()
    for t in range(1, n):
        pl.semaphore_signal(
            barrier, inc=1, device_id={"seq": lax.rem(s + t, n)}, device_id_type=MESH
        )

    def to_sibling(p):
        return pltpu.make_async_remote_copy(
            src_ref=theirs.at[p], dst_ref=sib.at[p], send_sem=to_sib.at[p], recv_sem=sib_in.at[p],
            device_id={"seq": sibling}, device_id_type=MESH,
        )

    def rightward(p, target):
        return pltpu.make_async_remote_copy(
            src_ref=own.at[p], dst_ref=from_left.at[p], send_sem=to_right.at[p], recv_sem=right_in.at[p],
            device_id={"seq": target}, device_id_type=MESH,
        )

    def leftward(p, target):
        return pltpu.make_async_remote_copy(
            src_ref=own.at[p], dst_ref=from_right.at[p], send_sem=to_left.at[p], recv_sem=left_in.at[p],
            device_id={"seq": target}, device_id_type=MESH,
        )

    def down_out(slot, p):
        half = tokens // 2
        return [
            pltpu.make_async_copy(
                down.at[slot, :, half * k : half * (k + 1)], out.at[pl.ds(2 * p, 2)], down_sem.at[k, slot]
            )
            for k, out in enumerate((down0_hbm, down1_hbm))
        ]

    def pass_on(p):
        to_sibling(p).wait_recv()

        @pl.when(p > q)
        def _():
            @pl.when(q > 0)
            def _():
                rightward(p, s).wait_recv()
                own[p] = (own[p].astype(f32) + sib[p].astype(f32) + from_left[p].astype(f32)).astype(low)

            @pl.when(q == 0)
            def _():
                own[p] = (own[p].astype(f32) + sib[p].astype(f32)).astype(low)

            rightward(p, s + 2).start()

        @pl.when(p < q)
        def _():
            @pl.when(q < nc - 1)
            def _():
                leftward(p, s).wait_recv()
                own[p] = (own[p].astype(f32) + sib[p].astype(f32) + from_right[p].astype(f32)).astype(low)

            @pl.when(q == nc - 1)
            def _():
                own[p] = (own[p].astype(f32) + sib[p].astype(f32)).astype(low)

            leftward(p, s - 2).start()

    def starts_flow(p):
        return ((p > q) & (q == 0)) | ((p < q) & (q == nc - 1))

    w = [w_parts.at[g] for g in range(2)]
    width = u_hbm.shape[2]
    weight = lambda g: w[g][...].reshape(width, -1)
    units = wd.shape[0]
    mine = pl.ds(pl.multiple_of(s * units, units), units)
    bd = bd_ref[...].astype(low)
    ad = ad_ref[:, mine].astype(low)
    a = [a_ref[g].astype(low) for g in range(2)]
    b = [b_ref[g, :, mine].astype(low) for g in range(2)]
    m = [m_ref[g : g + 1, mine] for g in range(2)]
    for cp in weights:
        cp.wait()
    a_both = jnp.concatenate(a, axis=0)
    for g in range(2):
        norm, cr = column_norms(weight(g), gram_ref[4 + g], b[g], dot_f32(a[g], weight(g)))
        norm_ref[g] = norm
        cross[g] = cr
        ratio[g] = m[g] / norm
    for ref in (ga_ref, gb_ref, gm_ref, gad_ref, gbd_ref, gmd_ref):
        ref[...] = jnp.zeros_like(ref)
    bd_wide = bd.astype(f32)
    gram_b = dot_two(gram_ref[6], bd)
    squares = jnp.sum(sq_ref[...], axis=0) + SCALE * SCALE * jnp.sum(
        bd_wide * gram_b, axis=0, keepdims=True
    )
    nd_ref[...] = jnp.sqrt(squares + 1e-06)
    ratio_d = md_ref[...] / nd_ref[...]
    pl.semaphore_wait(barrier, n - 1)

    def step(i, carry):
        p = by_distance(nc - 1 - i, q, nc)
        slot = lax.rem(i, 2)
        for cp in loads(i):
            cp.wait()

        @pl.when(i + 1 < nc)
        def _():
            for cp in loads(i + 1):
                cp.start()

        x = u[slot].reshape(2 * tokens, -1)
        upstream = gy[slot].reshape(2 * tokens, -1).astype(f32)
        gb_d = (upstream * ratio_d).astype(low)
        gi_d = (SCALE * dot_nt(gb_d, bd)).astype(low)
        gh = dot_nt(gb_d, wd[...]) + dot_f32(gi_d, ad)
        sides = side[slot].reshape(2 * tokens, -1)
        inner = [sides[:, 16 * g : 16 * g + 16] for g in range(2)]
        before = [dot_f32(x, weight(g)) + SCALE * dot_f32(inner[g], b[g]) for g in range(2)]
        gate = before[0] * ratio[0]
        lift = before[1] * ratio[1]
        sig = 1.0 / (1.0 + jnp.exp(-gate))
        silu = gate * sig
        hidden = (silu * lift).astype(low)
        grads = [gh * lift * sig * (1.0 + gate * (1.0 - sig)), gh * silu]
        gb = [(grads[g] * ratio[g]).astype(low) for g in range(2)]
        gi = jnp.concatenate([(SCALE * dot_nt(gb[g], b[g])).astype(low) for g in range(2)], axis=1)
        back = dot_nt(gb[0], weight(0)) + dot_nt(gb[1], weight(1)) + dot_f32(gi, a_both)
        back = back.astype(low).reshape(2, tokens, -1)
        first, second = back[0], back[1]

        @pl.when(c == 0)
        def _():
            own[p] = first
            theirs[p] = second

        @pl.when(c == 1)
        def _():
            own[p] = second
            theirs[p] = first

        to_sibling(p).start()
        inner_d = dot_nt(hidden, ad).astype(low)
        part = dot_f32(hidden, wd[...]) + SCALE * dot_f32(inner_d, bd)

        @pl.when(i >= 2)
        def _():
            for cp in down_out(slot, p):
                cp.wait()

        down[slot] = part.astype(low).reshape(2, tokens, -1)
        for cp in down_out(slot, p):
            cp.start()
        gmd_ref[...] += jnp.sum(upstream * part, axis=0, keepdims=True)
        gad_ref[...] += dot_tn(gi_d, hidden)
        gbd_ref[...] += SCALE * dot_tn(inner_d, gb_d)
        ga_ref[...] += dot_tn(gi, x).reshape(ga_ref.shape)
        for g in range(2):
            gm_ref[g] += jnp.sum(grads[g] * before[g], axis=0, keepdims=True)
            gb_ref[g] += SCALE * dot_tn(inner[g], gb[g])

        last = by_distance(nc - i, q, nc)
        pl.when((i > 0) & (i < nc - 1) & jnp.logical_not(starts_flow(last)))(lambda: pass_on(last))
        pl.when(starts_flow(p) | (i == nc - 2))(lambda: pass_on(p))
        return carry

    lax.fori_loop(0, nc, step, 0)

    gmd_ref[...] = gmd_ref[...] / nd_ref[...]

    def small(t, slot):
        return pltpu.make_async_remote_copy(
            src_ref=gmd_ref,
            dst_ref=gm_all.at[slot],
            send_sem=small_out.at[t],
            recv_sem=small_in.at[t],
            device_id={"seq": lax.rem(s + t, n)},
            device_id_type=MESH,
        )

    for t in range(1, n):
        small(t, s).start()
    for g in range(2):
        norm = norm_ref[g]
        gm = gm_ref[g] / norm
        gm_ref[g] = gm
        col = -gm * m[g] / (norm * norm)
        weighted = (b[g].astype(f32) * col).astype(low)
        tail = two_terms(dot_nt(weighted, b[g]))
        ga_ref[g] += SCALE * (dot_nt(weighted, weight(g)) + SCALE * dot_two(tail, a[g]))
        gb_ref[g] += SCALE * col * cross[g]

    gm_line = gmd_ref[...]
    for t in range(1, n):
        slot = lax.rem(s - t + n, n)
        small(t, slot).wait_recv()
        gm_line = gm_line + gm_all[slot]
    col = -gm_line * md_ref[...] / (nd_ref[...] * nd_ref[...])
    weighted = (bd_wide * col).astype(low)
    tail = two_terms(dot_nt(weighted, bd))
    gad_ref[...] += SCALE * (dot_nt(weighted, wd[...]) + SCALE * dot_two(tail, ad))
    own_gram = jnp.where(s == 0, SCALE, 0.0) * gram_b
    gbd_ref[...] += SCALE * col * (dot_f32(ad, wd[...]) + own_gram)

    to_sibling(q).wait_recv()
    in_ref[...] = own[q].astype(f32) + sib[q].astype(f32)

    @pl.when(q > 0)
    def _():
        rightward(q, s).wait_recv()
        in_ref[...] += from_left[q].astype(f32)

    @pl.when(q < nc - 1)
    def _():
        leftward(q, s).wait_recv()
        in_ref[...] += from_right[q].astype(f32)

    for i in range(min(2, nc)):
        for cp in down_out(i, 0):
            cp.wait()
    for t in range(1, n):
        small(t, s).wait_send()
    for p in range(nc):
        to_sibling(p).wait_send()
        pl.when(p > q)(lambda p=p: rightward(p, s).wait_send())
        pl.when(p < q)(lambda p=p: leftward(p, s).wait_send())


def share_plan(rows):
    turns = range(1, rows // 2)
    first = [(0, 0, k) for k in turns] + [(0, 1, 0)]
    second = [(0, 0, 0)] + [(0, 1, k) for k in turns]
    second += [(k, None, 0) for k in turns] + [(rows // 2, None, k) for k in turns]
    return first, second


def place_pieces(n, rows, pieces, w_parts):
    nc, half = n // 2, rows // 2
    _, q, _ = place_in_seq()
    r, b_row, a_row, diagonal = place_in_rows(rows)
    own, near = pieces[:2]
    turns = range(1, half)
    held = [(own.at[g], g, r) for g in range(2)]
    kinds = [(0, a_row(-k)) for k in turns] + [(1, b_row)]
    kinds += [(0, b_row)] + [(1, a_row(-k)) for k in turns]
    kinds += [(0, diagonal(-k)) for k in turns] + [(1, diagonal(-k)) for k in turns]
    held += [(piece, g, hold) for piece, (g, hold) in zip(pieces[2:], kinds)]
    out = [(near, w_parts.at[:, pl.ds(2 * q, 2)])]
    for i in range(1, nc):
        pair = pl.ds(2 * near_first(i, q, nc), 2)
        out += [(src.at[pair], w_parts.at[g, pair, hold]) for src, g, hold in held]
    return out


def feed_forward(n, rows, pieces, u, inner, gy0, gy1, wd, a, b, m, ad, bd, md, sq, gram, collective_id):
    nc = n // 2
    _, tokens, width = u.shape
    units = wd.shape[0]
    f32, low = jnp.float32, jnp.bfloat16
    shape = jax.ShapeDtypeStruct
    vmem = pl.BlockSpec(memory_space=pltpu.VMEM)
    hbm = pl.BlockSpec(memory_space=pltpu.HBM)
    dma = pltpu.SemaphoreType.DMA
    line = pltpu.VMEM((nc, tokens, width), low)
    pair = pltpu.VMEM((2, 2, tokens, width), low)
    part = pieces[0].shape[2]
    copies = 2 + (n // 2 - 1) * (2 + 2 * rows - 2)
    count = len(pieces)

    def kernel(*refs):
        ffn_kernel(n, rows, refs[:count], *refs[count:])

    return pl.pallas_call(
        kernel,
        out_shape=(
            shape((tokens, width), f32),
            pltpu.HBM((n, tokens // 2, width), low),
            pltpu.HBM((n, tokens // 2, width), low),
            shape((2, 16, width), f32),
            shape((2, 16, units), f32),
            shape((2, 1, units), f32),
            shape((2, 1, units), f32),
            shape((16, units), f32),
            shape((16, width), f32),
            shape((1, width), f32),
            shape((1, width), f32),
        ),
        in_specs=[hbm] * (count + 5) + [vmem] * 8,
        out_specs=(vmem, hbm, hbm) + (vmem,) * 8,
        scratch_shapes=[
            pltpu.VMEM((2, n, rows, part, units), low),
            pltpu.VMEM((units, width), low),
            pair,
            pltpu.VMEM((2, 2, tokens, 128), low),
            pair,
            pair,
            line, line, line, line, line,
            pltpu.VMEM((2, 1, units), f32),
            pltpu.VMEM((2, 16, units), f32),
            pltpu.VMEM((n, 1, width), f32),
            dma((copies,)), dma((4, 2)), dma((2, 2)), dma((n,)), dma((n,)),
        ] + [dma((nc,))] * 6,
        compiler_params=pltpu.CompilerParams(
            collective_id=collective_id, has_side_effects=True, vmem_limit_bytes=60 << 20
        ),
        cost_estimate=pl.CostEstimate(
            flops=12 * n * tokens * width * units, transcendentals=n * tokens * units,
            bytes_accessed=32 << 20,
        ),
        name="feed_forward",
    )(*pieces, u, inner, gy0, gy1, wd, a, b, m, ad, bd, md, sq, gram)

def greet_cross(n, rows, wait=True):
    s, r = lax.axis_index("seq"), lax.axis_index("rows")
    barrier = pltpu.get_barrier_semaphore()
    for t in range(1, n):
        pl.semaphore_signal(barrier, inc=1, device_id=(r, lax.rem(s + t, n)), device_id_type=MESH)
    for t in range(1, rows):
        pl.semaphore_signal(barrier, inc=1, device_id=(lax.rem(r + t, rows), s), device_id_type=MESH)
    if wait:
        pl.semaphore_wait(barrier, n + rows - 2)


def scatter_kernel(n, rows, x_ref, gb_gu, gm_gu, n_gu, ga_d, o_ref, units_all, own, sib, from_left, from_right,
                   units, units_in, load_sem, to_sib, sib_in, to_right, right_in, to_left, left_in,
                   row_out, row_in, back_send, back_in, wide_send, wide_in, pass_send, pass_in):
    nc = n // 2
    s, q, c = place_in_seq()
    sibling = s + 1 - 2 * c
    theirs = 1 - c
    r = lax.axis_index("rows")
    greet_cross(n, rows)
    f32, low = jnp.float32, jnp.bfloat16
    unit_rows, size = units.shape[1:]

    def load(p):
        return pltpu.make_async_copy(x_ref.at[2 * p + c], own.at[p], load_sem.at[p])

    def to_sibling(p):
        return pltpu.make_async_remote_copy(
            src_ref=x_ref.at[2 * p + theirs],
            dst_ref=sib.at[p],
            send_sem=to_sib.at[p],
            recv_sem=sib_in.at[p],
            device_id={"seq": sibling},
            device_id_type=MESH,
        )

    def rightward(p, target):
        return pltpu.make_async_remote_copy(
            src_ref=own.at[p],
            dst_ref=from_left.at[p],
            send_sem=to_right.at[p],
            recv_sem=right_in.at[p],
            device_id={"seq": target},
            device_id_type=MESH,
        )

    def leftward(p, target):
        return pltpu.make_async_remote_copy(
            src_ref=own.at[p],
            dst_ref=from_right.at[p],
            send_sem=to_left.at[p],
            recv_sem=left_in.at[p],
            device_id={"seq": target},
            device_id_type=MESH,
        )

    order = []
    for t in range(nc):
        for p in (nc - 1 - t, t):
            if p not in order:
                order.append(p)
    for p in order:
        to_sibling(p).start()
        load(p).start()

    n_high = [n_gu[g].astype(low).astype(f32) for g in range(2)]
    n_rest = [n_gu[g] - n_high[g] for g in range(2)]
    tops = jnp.concatenate(
        [gm_gu[0], gm_gu[1]]
        + [v * (1.0 / rows) for v in (n_high[0], n_rest[0], n_high[1], n_rest[1])]
        + [jnp.zeros((2, size), f32)],
        axis=0,
    )
    blocks = [gb_gu[0][:8], gb_gu[0][8:], gb_gu[1][:8], gb_gu[1][8:], ga_d[:8], ga_d[8:], tops, jnp.zeros((8, size), f32)]
    per = unit_rows // 8
    for j in range(rows):
        units[j] = jnp.concatenate(blocks[per * j : per * (j + 1)], axis=0).astype(low)

    def member(t):
        return lax.rem(r + t + rows, rows)

    def chip(t):
        return lax.rem(q + t + nc, nc)

    def unit_send(t):
        return remote(units.at[member(t)], units_in.at[t], row_out.at[t], row_in.at[t], member(t), s)

    def unit_back(t, slot):
        place = units_all.at[r, c, slot]
        return remote(place, place, back_send.at[t], back_in.at[t], r, 2 * chip(t) + c)

    def unit_wide(t, row):
        place = units_all.at[row, c]
        return remote(place, place, wide_send.at[t], wide_in.at[t], member(t), s)

    def unit_hand(t, row, core):
        place = units_all.at[row, core]
        return remote(place, place, pass_send.at[t], pass_in.at[t], r, sibling)

    def sum_units():
        total = units[r].astype(f32)
        for t in range(1, rows):
            unit_send(t).wait_recv()
            total = total + units_in[t].astype(f32)
        units_all[r, c, q] = total.astype(low)
        for t in range(1, nc):
            unit_back(t, q).start()

    def spread_units():
        for t in range(1, nc):
            unit_back(t, chip(-t)).wait_recv()
        for t in range(1, rows):
            unit_wide(t, r).start()
        unit_hand(0, r, c).start()

    for t in range(1, rows):
        unit_send(t).start()
    for step, p in enumerate(order):
        if step == 1:
            sum_units()
        if step == nc // 2:
            spread_units()
        load(p).wait()
        to_sibling(p).wait_recv()

        @pl.when(p > q)
        def _(p=p):
            @pl.when(q > 0)
            def _():
                rightward(p, s).wait_recv()
                total = own[p].astype(f32) + sib[p].astype(f32) + from_left[p].astype(f32)
                own[p] = total.astype(own.dtype)

            @pl.when(q == 0)
            def _():
                own[p] = (own[p].astype(f32) + sib[p].astype(f32)).astype(own.dtype)

            rightward(p, s + 2).start()

        @pl.when(p < q)
        def _(p=p):
            @pl.when(q < nc - 1)
            def _():
                leftward(p, s).wait_recv()
                total = own[p].astype(f32) + sib[p].astype(f32) + from_right[p].astype(f32)
                own[p] = total.astype(own.dtype)

            @pl.when(q == nc - 1)
            def _():
                own[p] = (own[p].astype(f32) + sib[p].astype(f32)).astype(own.dtype)

            leftward(p, s - 2).start()

    o_ref[...] = own[q].astype(f32) + sib[q].astype(f32)

    @pl.when(q > 0)
    def _():
        rightward(q, s).wait_recv()
        o_ref[...] += from_left[q].astype(f32)

    @pl.when(q < nc - 1)
    def _():
        leftward(q, s).wait_recv()
        o_ref[...] += from_right[q].astype(f32)

    for t in range(1, rows):
        unit_wide(t, member(-t)).wait_recv()
        unit_hand(t, member(-t), c).start()
    for t in range(rows):
        unit_hand(t, member(-t), theirs).wait_recv()
        unit_hand(t, member(-t), c).wait_send()
    for t in range(1, rows):
        unit_send(t).wait_send()
        unit_wide(t, r).wait_send()
    for t in range(1, nc):
        unit_back(t, q).wait_send()
    for p in range(nc):
        to_sibling(p).wait_send()
        pl.when(p > q)(lambda p=p: rightward(p, s).wait_send())
        pl.when(p < q)(lambda p=p: leftward(p, s).wait_send())


def scatter_seq(n, rows, x, own_units, collective_id):
    nc = n // 2
    _, height, cols = x.shape
    size = own_units[3].shape[1]
    unit_rows = 64 // rows
    low = jnp.bfloat16
    dma = pltpu.SemaphoreType.DMA
    buf = pltpu.VMEM((nc, height, cols), x.dtype)
    small = pltpu.VMEM((rows, unit_rows, size), low)
    vmem = pl.BlockSpec(memory_space=pltpu.VMEM)
    return pl.pallas_call(
        functools.partial(scatter_kernel, n, rows),
        out_shape=(
            jax.ShapeDtypeStruct((height, cols), jnp.float32),
            jax.ShapeDtypeStruct((rows, 2, nc, unit_rows, size), low),
        ),
        in_specs=[pl.BlockSpec(memory_space=pltpu.HBM)] + [vmem] * 4,
        out_specs=(vmem,) * 2,
        scratch_shapes=[buf] * 4 + [small] * 2 + [dma((nc,))] * 7
        + [dma((rows,))] * 2 + [dma((nc,))] * 2 + [dma((rows,))] * 4,
        compiler_params=pltpu.CompilerParams(
            collective_id=collective_id, has_side_effects=True, vmem_limit_bytes=32 << 20
        ),
        cost_estimate=pl.CostEstimate(flops=0, transcendentals=0, bytes_accessed=1 << 20),
        name="scatter_seq",
    )(*in_hbm(x), *own_units)


def reduce_kernel(n, rows, ga_qkv, ga_o, gb_qkv, gb_o, ga_gu, gb_d, gm_qkv, gm_o, gm_d,
                  whole, part, from_sib, mid, from_rows, from_line, line_out,
                  sib_out, sib_in, row_out, row_in, line_send, line_in, back_send, back_in, wide_send, wide_in,
                  pass_send, pass_in):
    nc = n // 2
    f32, low = jnp.float32, jnp.bfloat16
    s, q, c = place_in_seq()
    sibling = s + 1 - 2 * c
    r = lax.axis_index("rows")
    width = ga_o.shape[1]
    cols = width // (2 * rows)
    kv = (gb_qkv.shape[1] - width) // 2
    height = part.shape[2]
    piece = height // nc

    greet_cross(n, rows, wait=False)
    gb_k, gb_v = gb_qkv[:, width : width + kv], gb_qkv[:, width + kv :]
    small = jnp.concatenate(
        [
            jnp.concatenate([gb_k[:8], gb_k[8:], gb_v[:8], gb_v[8:]], axis=1),
            gm_qkv[:, :width],
            gm_o[...],
            gm_d[...],
            jnp.concatenate([gm_qkv[:, width:], jnp.zeros((1, width - 2 * kv), f32)], axis=1),
            jnp.zeros((4, width), f32),
        ],
        axis=0,
    )
    groups = [ga_qkv[0], ga_qkv[1], ga_qkv[2], ga_o[...], gb_qkv[:, :width], gb_o[...], ga_gu[0], ga_gu[1], gb_d[...], small]
    for j in range(2 * rows):
        for g, value in enumerate(groups):
            part[j % 2, j // 2, 16 * g : 16 * g + 16] = value[:, cols * j : cols * (j + 1)].astype(low)
        if height > 160:
            part[j % 2, j // 2, 160:] = jnp.zeros((height - 160, cols), low)
    pl.semaphore_wait(pltpu.get_barrier_semaphore(), n + rows - 2)

    def to_sibling():
        return remote(part.at[1 - c], from_sib, sib_out.at[0], sib_in.at[0], r, sibling)

    def member(t):
        return lax.rem(r + t + rows, rows)

    def row_send(t):
        return remote(mid.at[member(t)], from_rows.at[t], row_out.at[t], row_in.at[t], member(t), s)

    def chip(t):
        return lax.rem(q + t + nc, nc)

    def line_part(t):
        return remote(line_out.at[chip(t)], from_line.at[t], line_send.at[t], line_in.at[t], r, 2 * chip(t) + c)

    def back(t, slot):
        return remote(whole.at[r, c, slot], whole.at[r, c, slot], back_send.at[t], back_in.at[t], r, 2 * chip(t) + c)

    def wide(t, row):
        return remote(whole.at[row, c], whole.at[row, c], wide_send.at[t], wide_in.at[t], member(t), s)

    def hand(t, row, core):
        return remote(whole.at[row, core], whole.at[row, core], pass_send.at[t], pass_in.at[t], r, sibling)

    to_sibling().start()
    to_sibling().wait_recv()
    for t in range(rows):
        mid[member(t)] = (part[c, member(t)].astype(f32) + from_sib[member(t)].astype(f32)).astype(low)
        if t:
            row_send(t).start()
    total = mid[r].astype(f32)
    for t in range(1, rows):
        row_send(t).wait_recv()
        total = total + from_rows[t].astype(f32)
    for p in range(nc):
        line_out[p] = total[piece * p : piece * (p + 1)].astype(low)
    for t in range(1, nc):
        line_part(t).start()
    own = line_out[q].astype(f32)
    for t in range(1, nc):
        line_part(t).wait_recv()
        own = own + from_line[t].astype(f32)
    whole[r, c, q] = own.astype(low)
    for t in range(1, nc):
        back(t, q).start()
    for t in range(1, nc):
        back(t, chip(-t)).wait_recv()
    for t in range(1, rows):
        wide(t, r).start()
    hand(0, r, c).start()
    for t in range(1, rows):
        wide(t, member(-t)).wait_recv()
        hand(t, member(-t), c).start()
    for t in range(rows):
        hand(t, member(-t), 1 - c).wait_recv()

    to_sibling().wait_send()
    for t in range(1, rows):
        row_send(t).wait_send()
        wide(t, r).wait_send()
    for t in range(1, nc):
        line_part(t).wait_send()
        back(t, q).wait_send()
    for t in range(rows):
        hand(t, member(-t), c).wait_send()


def sum_gradients(n, rows, full, collective_id):
    nc = n // 2
    width = full[1].shape[1]
    cols = width // (2 * rows)
    height = -(-160 // (8 * nc)) * 8 * nc
    low = jnp.bfloat16
    vmem = pl.BlockSpec(memory_space=pltpu.VMEM)
    dma = pltpu.SemaphoreType.DMA
    block = (rows, height, cols)
    return pl.pallas_call(
        functools.partial(reduce_kernel, n, rows),
        out_shape=jax.ShapeDtypeStruct((rows, 2, nc, height // nc, cols), low),
        in_specs=[vmem] * 9,
        out_specs=vmem,
        scratch_shapes=[
            pltpu.VMEM((2, *block), low),
            pltpu.VMEM(block, low),
            pltpu.VMEM(block, low),
            pltpu.VMEM(block, low),
            pltpu.VMEM((nc, height // nc, cols), low),
            pltpu.VMEM((nc, height // nc, cols), low),
            dma((1,)), dma((1,)), dma((rows,)), dma((rows,)), dma((nc,)), dma((nc,)),
            dma((nc,)), dma((nc,)), dma((rows,)), dma((rows,)), dma((rows,)), dma((rows,)),
        ],
        compiler_params=pltpu.CompilerParams(
            collective_id=collective_id, has_side_effects=True, vmem_limit_bytes=48 << 20
        ),
        cost_estimate=pl.CostEstimate(flops=0, transcendentals=0, bytes_accessed=1 << 20),
        name="sum_gradients",
    )(*full)


def finish_kernel(n, rows, whole, units_all, x1, before_0, before_1, m_attn, n_attn, m_d, n_d, m_gu,
                  o_out, o_ga, o_gb_qo, o_gb_kv, o_gm_q, o_gm_kv, o_gm_o, o_ga_gu, o_gb_gu, o_gm_gu, o_ga_d, o_gb_d,
                  o_gm_d, o_stats, n_gu):
    f32 = jnp.float32
    nc = n // 2
    width = o_gb_d.shape[1]
    kv = o_gb_kv.shape[2]
    cols = width // (2 * rows)
    size = units_all.shape[4]
    per = units_all.shape[3] // 8
    half = x1.shape[0] // 2
    for k, before in enumerate((before_0, before_1)):
        own = slice(half * k, half * (k + 1))
        o_out[own] = (x1[own] + before[...].astype(f32) * (m_d[...] / n_d[...])).astype(o_out.dtype)
    for j in range(2 * rows):
        block = jnp.concatenate([whole[j // 2, j % 2, p].astype(f32) for p in range(nc)], axis=0)
        at = slice(cols * j, cols * (j + 1))
        for g in range(4):
            o_ga[g, :, at] = block[16 * g : 16 * g + 16]
        o_gb_qo[0, :, at] = block[64:80]
        o_gb_qo[1, :, at] = block[80:96]
        o_ga_gu[0, :, at] = block[96:112]
        o_ga_gu[1, :, at] = block[112:128]
        o_gb_d[:, at] = block[128:144]
        which, start = divmod(cols * j, kv)
        o_gb_kv[which // 2, 8 * (which % 2) : 8 * (which % 2) + 8, start : start + cols] = block[144:152]
        o_gm_q[at] = block[152]
        o_gm_o[at] = block[153]
        o_gm_d[at] = block[154]
        if which < 2:
            o_gm_kv[which : which + 1, start : start + cols] = block[155:156]
    for j in range(rows):
        for dev in range(n):
            block = units_all[j, dev % 2, dev // 2].astype(f32)
            at = slice(size * dev, size * (dev + 1))
            for t in range(per):
                rows8, place = block[8 * t : 8 * t + 8], per * j + t
                half = slice(8 * (place % 2), 8 * (place % 2) + 8)
                if place < 4:
                    o_gb_gu[place // 2, half, at] = rows8
                elif place < 6:
                    o_ga_d[half, at] = rows8
                elif place == 6:
                    o_gm_gu[:, at] = rows8[:2]
                    n_gu[0:1, at] = rows8[2:3] + rows8[3:4]
                    n_gu[1:2, at] = rows8[4:5] + rows8[5:6]


    row = lax.broadcasted_iota(jnp.int32, o_stats.shape, 0)
    col = lax.broadcasted_iota(jnp.int32, o_stats.shape, 1)
    bounds = [(0, width), (width, width + kv), (width + kv, width + 2 * kv), (width + 2 * kv, 2 * width + 2 * kv)]
    both = [(m_attn[:, i:j], n_attn[:, i:j]) for i, j in bounds]
    both += [(m_gu[g : g + 1, :], n_gu[g : g + 1, :]) for g in range(2)] + [(m_d[...], n_d[...])]
    stats = jnp.zeros(o_stats.shape, f32)
    for p, (m, norm) in enumerate(both):
        drift = jnp.mean(jnp.square(m - norm), axis=1, keepdims=True)
        drift = jnp.sqrt(drift) / jnp.sqrt(jnp.mean(jnp.square(m), axis=1, keepdims=True) + 1e-06)
        stats = jnp.where((row == p) & (col == 0), drift, stats)
        stats = jnp.where((row == p) & (col == 1), jnp.mean(norm, axis=1, keepdims=True), stats)
    o_stats[...] = stats


def finish(n, rows, sums, units, x1, before_0, before_1, m_attn, n_attn, m_d, n_d, m_gu):
    tokens, width = x1.shape
    kv = (m_attn.shape[1] - 2 * width) // 2
    wide_units = m_gu.shape[1]
    shape = lambda *dims: pltpu.HBM(dims, jnp.float32)
    vmem = pl.BlockSpec(memory_space=pltpu.VMEM)
    return pl.pallas_call(
        functools.partial(finish_kernel, n, rows),
        out_shape=(
            pltpu.HBM((tokens, width), jnp.bfloat16), shape(4, 16, width), shape(2, 16, width), shape(2, 16, kv),
            shape(width), shape(2, kv), shape(width), shape(2, 16, width), shape(2, 16, wide_units), shape(2, wide_units),
            shape(16, wide_units), shape(16, width), shape(width), shape(7, 2),
        ),
        in_specs=[vmem] * 2 + [pl.BlockSpec()] * 8,
        scratch_shapes=[pltpu.VMEM((2, wide_units), jnp.float32)],
        compiler_params=pltpu.CompilerParams(vmem_limit_bytes=40 << 20),
        cost_estimate=pl.CostEstimate(flops=0, transcendentals=0, bytes_accessed=8 << 20),
        name="finish",
    )(sums, units, *in_hbm(x1, before_0, before_1), m_attn, n_attn, m_d, n_d, m_gu)

def local(
    layer_input,
    output_gradient,
    norm_gain_vectors,
    query_output_frozen,
    key_value_frozen,
    gate_up_frozen,
    down_frozen_weight,
    attention_adapter_a,
    query_output_adapter_b,
    key_value_adapter_b,
    query_magnitude,
    key_value_magnitude,
    output_magnitude,
    gate_up_adapter_a,
    gate_up_adapter_b,
    gate_up_magnitude,
    down_adapter_a,
    down_adapter_b,
    down_magnitude,
    prompt_length_list,
    response_length_list,
):
    pair_rows, span_len, model_width = layer_input.shape
    token_count = pair_rows * span_len
    kv_width = KV_HEADS * HEAD_DIM
    seq_size = lax.axis_size("seq")
    rows_size = lax.axis_size("rows")
    seq_index = lax.axis_index("seq")
    f32 = jnp.float32

    x = layer_input.reshape(token_count, model_width)
    gain_attn, gain_ffn = norm_gain_vectors[:1], norm_gain_vectors[1:]
    weights, gu_own, gu_near, sq_d, grams, u1, inner_1 = gather_weights(
        seq_size, rows_size, query_output_frozen, key_value_frozen, gate_up_frozen,
        down_frozen_weight, down_adapter_a, down_adapter_b, x, gain_attn, attention_adapter_a,
        gate_up_adapter_a, 1,
    )
    shares_1, shares_2 = share_plan(rows_size)
    grad_out_rows = output_gradient.reshape(token_count, model_width)
    half_0, half_1 = jnp.split(grad_out_rows, 2)
    weights, half_0 = lax.optimization_barrier((weights, half_0))
    gy_0 = lax.all_gather(half_0, "seq", axis=0, tiled=False)

    b_attn = jnp.concatenate(
        [
            query_output_adapter_b[0],
            key_value_adapter_b[0],
            key_value_adapter_b[1],
            query_output_adapter_b[1],
        ],
        axis=1,
    )
    m_attn = jnp.concatenate(
        [query_magnitude, key_value_magnitude[0], key_value_magnitude[1], output_magnitude]
    )[None]
    m_d = down_magnitude[None]

    positions = seq_index * span_len + jnp.arange(span_len, dtype=jnp.int32)
    half_dim = HEAD_DIM // 2
    frequency = 500000.0 ** (-(jnp.arange(half_dim, dtype=f32) * 2.0) / HEAD_DIM)
    angles = positions.astype(f32)[:, None] * frequency[None, :]
    cosine = jnp.tile(jnp.cos(angles), (pair_rows, 4))
    sine = jnp.tile(jnp.sin(angles), (pair_rows, 4))
    valid_len = prompt_length_list[0] + response_length_list

    before_qkv, q, kv, n_attn, cross_attn = project_qkv(
        u1, inner_1, grams, attention_adapter_a, weights, b_attn, m_attn, cosine, sine
    )
    (kv_all, sq_all), gu_1 = gather_seq(
        seq_size, rows_size, [kv, sq_d], 2, (gu_own,), shares_1
    )
    kv_all, half_1 = lax.optimization_barrier((kv_all, half_1))
    gy_1 = lax.all_gather(half_1, "seq", axis=0, tiled=False)
    kv_all = kv_all.reshape(seq_size, pair_rows, span_len, 2 * kv_width)
    q = q.reshape(pair_rows, span_len, model_width)
    att, shares = attend(q, kv_all, valid_len)
    att = att.reshape(token_count, model_width)
    before_o, x1, u2, inner_2 = project_out(
        att, attention_adapter_a, weights, b_attn, m_attn, n_attn, x, gain_ffn, gate_up_adapter_a
    )

    (u2_all, inner_all), gu_2 = gather_seq(
        seq_size, rows_size, [u2, inner_2], 3, (gu_own, *gu_1), shares_2
    )
    in_grad, down_0, down_1, ga_gu, gb_gu, gm_gu, n_gu, ga_d, gb_d, gm_d, n_d = feed_forward(
        seq_size, rows_size, (gu_own, gu_near, *gu_1, *gu_2), u2_all, inner_all, gy_0, gy_1,
        down_frozen_weight, gate_up_adapter_a, gate_up_adapter_b, gate_up_magnitude, down_adapter_a,
        down_adapter_b, m_d, sq_all, grams, 4,
    )
    flat = lambda v: v.reshape(-1, model_width)
    before_0 = lax.psum_scatter(flat(down_0), "seq", scatter_dimension=0, tiled=True)

    gx1, grad_att, ga_o, gb_o, gm_o = out_back(
        in_grad, x1, gain_ffn, grad_out_rows, before_o, att, attention_adapter_a, b_attn, m_attn,
        n_attn, cross_attn, weights,
    )
    gq, gkv = attend_back(q, kv_all, shares, grad_att.reshape(q.shape))
    gkv, units = scatter_seq(
        seq_size, rows_size, gkv.reshape(seq_size, token_count, 2 * kv_width),
        (gb_gu, gm_gu, n_gu, ga_d), 5,
    )
    gkv, down_1, before_0 = lax.optimization_barrier((gkv, down_1, before_0))
    before_1 = lax.psum_scatter(flat(down_1), "seq", scatter_dimension=0, tiled=True)
    grad_inputs, ga_qkv, gb_qkv, gm_qkv = qkv_back(
        gq.reshape(token_count, model_width), gkv, cosine, sine, before_qkv, u1, inner_1,
        attention_adapter_a, b_attn, m_attn, n_attn, cross_attn, x, gain_attn, gx1, weights,
    )

    sums = sum_gradients(
        seq_size, rows_size,
        (ga_qkv, ga_o, gb_qkv, gb_o, ga_gu, gb_d, gm_qkv, gm_o, gm_d),
        6,
    )
    layer_result, *summed, stats = finish(
        seq_size, rows_size, sums, units, x1, before_0, before_1, m_attn, n_attn, m_d, n_d, gate_up_magnitude
    )
    shape = (pair_rows, span_len, model_width)
    return (layer_result.reshape(shape), grad_inputs.reshape(shape), *summed, stats)

def solution(mesh):
    return jax.shard_map(
        local,
        mesh=mesh,
        in_specs=(
            P("rows", "seq", None),
            P("rows", "seq", None),
            P(),
            P(None, "seq", None),
            P(None, "seq", None),
            P(None, "seq", None),
            P("seq", None),
            P(),
            P(),
            P(),
            P(),
            P(),
            P(),
            P(),
            P(),
            P(),
            P(),
            P(),
            P(),
            P("rows"),
            P("rows"),
        ),
        out_specs=(
            P("rows", "seq", None),
            P("rows", "seq", None),
            P(),
            P(),
            P(),
            P(),
            P(),
            P(),
            P(),
            P(),
            P(),
            P(),
            P(),
            P(),
            P(),
        ),
        check_vma=False,
    )
```

```python
import functools

import jax
import jax.numpy as jnp
from jax import lax
from jax.experimental import pallas as pl
from jax.experimental.pallas import tpu as pltpu
from jax.sharding import PartitionSpec as P

HEADS = 32
KV_HEADS = 8
HEAD_DIM = 64
ADAPTER_RANK = 16
ALPHA = 32
SCALE = ALPHA / ADAPTER_RANK
TILE = 512

highest = lax.Precision.HIGHEST
last_last = (((1,), (1,)), ((), ()))
first_first = (((0,), (0,)), ((), ()))

def dot_f32(a, b):
    return jnp.dot(a, b, preferred_element_type=jnp.float32)


def dot_nt(a, b):
    return lax.dot_general(a, b, last_last, preferred_element_type=jnp.float32)


def dot_tn(a, b):
    return lax.dot_general(a, b, first_first, preferred_element_type=jnp.float32)


def in_hbm(*arrays):
    return [pltpu.with_memory_space_constraint(v, pltpu.HBM) for v in arrays]


def unit_rms(v):
    return lax.rsqrt(jnp.mean(v * v, axis=-1, keepdims=True) + 1e-05)


def rms_back(v, gain, upstream):
    r = unit_rms(v)
    scaled = gain * upstream
    return r * scaled - v * (r * r * r) * jnp.mean(scaled * v, axis=-1, keepdims=True)


def turn(z, cosine, sine):
    width = z.shape[1]
    lane = lax.broadcasted_iota(jnp.int32, z.shape, 1)
    half = HEAD_DIM // 2
    other = jnp.where(
        lax.rem(lane, HEAD_DIM) < half, -pltpu.roll(z, width - half, 1), pltpu.roll(z, half, 1)
    )
    copies = width // cosine.shape[1]
    return z * jnp.tile(cosine, (1, copies)) + other * jnp.tile(sine, (1, copies))


def column_squares(w):
    return jnp.sum(jnp.square(w.astype(jnp.float32)), axis=0, keepdims=True)


def two_terms(value):
    high = value.astype(jnp.bfloat16)
    return jnp.concatenate([high, (value - high.astype(jnp.float32)).astype(jnp.bfloat16)], axis=0)


def dot_two(terms, b):
    both = dot_f32(terms, b)
    half = both.shape[0] // 2
    return both[:half] + both[half:]


def column_norms(w, gram, b, cross):
    b_wide = b.astype(jnp.float32)
    gram_b = dot_two(gram, b)
    squares = column_squares(w) + 2.0 * SCALE * jnp.sum(b_wide * cross, axis=0, keepdims=True)
    squares = squares + SCALE * SCALE * jnp.sum(b_wide * gram_b, axis=0, keepdims=True)
    return jnp.sqrt(squares + 1e-06), cross + SCALE * gram_b


def project_kernel(kv_tiles, u_ref, inner_ref, gram_ref, a_ref, w_ref, b_ref, m_ref, cos_ref, sin_ref,
                   before_ref, q_ref, kv_ref, n_ref, cross_ref):
    j = pl.program_id(0)
    q_tiles, last = kv_tiles
    a = a_ref[0].astype(jnp.bfloat16)
    b = b_ref[...].astype(jnp.bfloat16)
    w = w_ref[0]
    rows = u_ref.shape[0]

    @pl.when(j <= last)
    def _():
        both = dot_f32(jnp.concatenate([u_ref[...], a], axis=0), w)
        norm, cross = column_norms(w, gram_ref[0], b, both[rows:])
        n_ref[...] = norm
        cross_ref[...] = cross
        before = both[:rows] + SCALE * dot_f32(inner_ref[0], b)
        before_ref[...] = before
        y = before * (m_ref[...] / norm)

        @pl.when(j < q_tiles)
        def _():
            q_ref[...] = turn(y, cos_ref[...], sin_ref[...]).astype(jnp.bfloat16)

        @pl.when(j == q_tiles)
        def _():
            kv_ref[...] = turn(y, cos_ref[...], sin_ref[...]).astype(jnp.bfloat16)

        @pl.when(j > q_tiles)
        def _():
            kv_ref[...] = y.astype(jnp.bfloat16)

    @pl.when(j > last)
    def _():
        norm, cross = column_norms(w, gram_ref[0], b, dot_f32(a, w))
        n_ref[...] = norm
        cross_ref[...] = cross


def project_qkv(u, inner, grams, a, weights, b, m, cosine, sine):
    rows, width = u.shape
    cols = b.shape[1]
    per_half = weights.shape[2] // TILE
    q_tiles = width // TILE
    k_cols = weights.shape[2] - width
    last = q_tiles + 2 * k_cols // TILE - 1
    full = lambda shape: pl.BlockSpec(shape, lambda j: (0,) * len(shape))
    col = lambda height: pl.BlockSpec((height, TILE), lambda j: (0, j))
    which = lambda j: jnp.where(j < q_tiles, 0, jnp.where(j > last, 3, 1 + j - q_tiles))
    f32, low = jnp.float32, jnp.bfloat16
    return pl.pallas_call(
        functools.partial(project_kernel, (q_tiles, last)),
        out_shape=(
            pltpu.HBM((rows, width + 2 * k_cols), f32),
            pltpu.HBM((rows, width), low),
            pltpu.HBM((rows, 2 * k_cols), low),
            pltpu.HBM((1, cols), f32),
            pltpu.HBM((16, cols), f32),
        ),
        grid=(cols // TILE,),
        in_specs=[
            full((rows, width)),
            pl.BlockSpec((1, rows, 16), lambda j: (jnp.minimum(which(j), 2), 0, 0)),
            pl.BlockSpec((1, 32, 16), lambda j: (which(j), 0, 0)),
            pl.BlockSpec((1, 16, width), lambda j: (which(j), 0, 0)),
            pl.BlockSpec((1, width, TILE), lambda j: (j // per_half, 0, j % per_half)),
            col(16),
            col(1),
            full(cosine.shape),
            full(sine.shape),
        ],
        out_specs=(
            pl.BlockSpec((rows, TILE), lambda j: (0, jnp.minimum(j, last))),
            pl.BlockSpec((rows, TILE), lambda j: (0, jnp.minimum(j, q_tiles - 1))),
            pl.BlockSpec((rows, TILE), lambda j: (0, jnp.clip(j - q_tiles, 0, last - q_tiles))),
            col(1),
            col(16),
        ),
        compiler_params=pltpu.CompilerParams(vmem_limit_bytes=40 << 20),
        cost_estimate=pl.CostEstimate(
            flops=2 * rows * width * cols, transcendentals=0, bytes_accessed=2 * width * cols
        ),
        name="project_qkv",
    )(*in_hbm(u), inner, grams, *in_hbm(a, weights, b), m, cosine, sine)


def out_kernel(att_ref, a_ref, w_ref, b_ref, m_ref, n_ref, x_ref, gain_ref, next_ref,
               before_ref, x1_ref, u2_ref, inner_ref):
    t = pl.program_id(0)
    a = a_ref[0].astype(jnp.bfloat16)
    b = b_ref[...].astype(jnp.bfloat16)
    inner = dot_nt(att_ref[...], a).astype(jnp.bfloat16)
    before = dot_f32(att_ref[...], w_ref[0]) + SCALE * dot_f32(inner, b)
    before_ref[...] = before
    x1_ref[:, pl.ds(pl.multiple_of(t * TILE, TILE), TILE)] = (
        x_ref[...].astype(jnp.float32) + before * (m_ref[...] / n_ref[...])
    )

    @pl.when(t == pl.num_programs(0) - 1)
    def _():
        v = x1_ref[...]
        u2 = (v * unit_rms(v) * gain_ref[...]).astype(jnp.bfloat16)
        u2_ref[...] = u2
        following = next_ref[...].reshape(-1, u2.shape[1]).astype(jnp.bfloat16)
        inner_ref[...] = jnp.zeros_like(inner_ref)
        inner_ref[:, : following.shape[0]] = dot_nt(u2, following).astype(jnp.bfloat16)


def project_out(att, a, weights, b, m, norms, x, gain, following):
    rows, width = att.shape
    tiles = width // TILE
    skip = (weights.shape[2] - width) // TILE
    full = lambda shape: pl.BlockSpec(shape, lambda t: (0,) * len(shape))
    col = lambda height: pl.BlockSpec((height, TILE), lambda t: (0, t))
    ahead = b.shape[1] // TILE - tiles
    later = lambda height: pl.BlockSpec((height, TILE), lambda t: (0, ahead + t))
    f32 = jnp.float32
    return pl.pallas_call(
        out_kernel,
        out_shape=(
            pltpu.HBM((rows, width), f32),
            pltpu.HBM((rows, width), f32),
            pltpu.HBM((rows, width), jnp.bfloat16),
            pltpu.HBM((rows, 128), jnp.bfloat16),
        ),
        grid=(tiles,),
        in_specs=[
            full((rows, width)),
            pl.BlockSpec((1, 16, width), lambda t: (3, 0, 0)),
            pl.BlockSpec((1, width, TILE), lambda t: (1, 0, skip + t)),
            later(16),
            later(1),
            later(1),
            col(rows),
            full((1, width)),
            full(following.shape),
        ],
        out_specs=(col(rows), full((rows, width)), full((rows, width)), full((rows, 128))),
        compiler_params=pltpu.CompilerParams(vmem_limit_bytes=40 << 20),
        cost_estimate=pl.CostEstimate(
            flops=2 * rows * width * width, transcendentals=0, bytes_accessed=2 * width * width
        ),
        name="project_out",
    )(*in_hbm(att, a, weights, b), m, norms, *in_hbm(x), gain, *in_hbm(following))


def out_back_kernel(in_ref, x1_ref, gain_ref, gy_ref, before_ref, att_ref, a_ref, b_ref, m_ref, n_ref, cross_ref,
                    w_ref, gx_ref, gatt_ref, ga_ref, gb_ref, gm_ref, lhs, gi, tail):
    t = pl.program_id(0)
    rows, width = gx_ref.shape
    low = jnp.bfloat16
    a = a_ref[0].astype(low)
    o_cols = slice(b_ref.shape[1] - width, b_ref.shape[1])

    @pl.when(t == 0)
    def _():
        gx = gy_ref[...].astype(jnp.float32) + rms_back(x1_ref[...], gain_ref[...], in_ref[...])
        gx_ref[...] = gx
        norm, m = n_ref[:, o_cols], m_ref[:, o_cols]
        gb = (gx * (m / norm)).astype(low)
        lhs[:rows] = gb
        b = b_ref[:, o_cols].astype(low)
        gi[...] = (SCALE * dot_nt(gb, b)).astype(low)
        gm = jnp.sum(gx * before_ref[...], axis=0, keepdims=True) / norm
        gm_ref[...] = gm
        c = -gm * m / (norm * norm)
        weighted = (b.astype(jnp.float32) * c).astype(low)
        lhs[rows:] = weighted
        tail[...] = two_terms(dot_nt(weighted, b))
        inner = dot_nt(att_ref[...], a).astype(low)
        gb_ref[...] = SCALE * dot_tn(inner, gb) + SCALE * c * cross_ref[:, o_cols]

    span = pl.ds(pl.multiple_of(t * TILE, TILE), TILE)
    a_tile = a_ref[0, :, span].astype(low)
    gi_low = gi[...]
    back = dot_nt(lhs[...], w_ref[0, :, w_ref.shape[2] - width :])
    gatt_ref[...] = (back[:rows] + dot_f32(gi_low, a_tile)).astype(low)
    spread = back[rows:] + SCALE * dot_two(tail[...], a_tile)
    ga_ref[...] = dot_tn(gi_low, att_ref[:, span]) + SCALE * spread


def out_back(in_grad, x1, gain, gy, before, att, a, b, m, norms, cross, weights):
    rows, width = x1.shape
    tiles = width // TILE
    full = lambda shape: pl.BlockSpec(shape, lambda t: (0,) * len(shape))
    col = lambda height: pl.BlockSpec((height, TILE), lambda t: (0, t))
    f32, low = jnp.float32, jnp.bfloat16
    wide = full((rows, width))
    return pl.pallas_call(
        out_back_kernel,
        out_shape=(
            pltpu.HBM((rows, width), f32),
            pltpu.HBM((rows, width), low),
            jax.ShapeDtypeStruct((16, width), f32),
            jax.ShapeDtypeStruct((16, width), f32),
            jax.ShapeDtypeStruct((1, width), f32),
        ),
        grid=(tiles,),
        in_specs=[wide, wide, full((1, width)), wide, wide, wide,
                  pl.BlockSpec((1, 16, width), lambda t: (3, 0, 0)),
                  full(b.shape), full(m.shape), full(norms.shape), full(cross.shape),
                  pl.BlockSpec((1, TILE, weights.shape[2]), lambda t: (1, t, 0))],
        out_specs=(wide, col(rows), col(16), full((16, width)), full((1, width))),
        scratch_shapes=[
            pltpu.VMEM((rows + 16, width), low),
            pltpu.VMEM((rows, 16), low),
            pltpu.VMEM((32, 16), low),
        ],
        compiler_params=pltpu.CompilerParams(vmem_limit_bytes=48 << 20),
        cost_estimate=pl.CostEstimate(flops=0, transcendentals=0, bytes_accessed=1 << 20),
        name="out_back",
    )(*in_hbm(in_grad, x1), gain, *in_hbm(gy, before, att, a, b), m, norms, *in_hbm(cross, weights))


def qkv_back_kernel(gq_ref, gkv_ref, cos_ref, sin_ref, before_ref, u_ref, inner_ref, a_ref, b_ref, m_ref, n_ref, cross_ref,
                    x_ref, gain_ref, gx_ref, w0_ref, w1_ref,
                    out_ref, ga_ref, gb_ref, gm_ref, lhs0, lhs1, gi, tail):
    t = pl.program_id(0)
    rows, width = gx_ref.shape
    low = jnp.bfloat16
    k_cols = w1_ref.shape[2]
    bounds = [(0, width), (width, width + k_cols), (width + k_cols, width + 2 * k_cols)]

    @pl.when(t == 0)
    def _():
        cosine, sine = cos_ref[...], -sin_ref[...]
        k_parts = [gkv_ref[:, 256 * j : 256 * j + 128] for j in range(k_cols // 128)]
        v_parts = [gkv_ref[:, 256 * j + 128 : 256 * j + 256] for j in range(k_cols // 128)]
        rounded = lambda z: z.astype(low).astype(jnp.float32)
        ups = [
            turn(gq_ref[...].astype(jnp.float32), cosine, sine),
            turn(rounded(jnp.concatenate(k_parts, axis=1)), cosine, sine),
            rounded(jnp.concatenate(v_parts, axis=1)),
        ]
        lhs0[rows:] = jnp.zeros_like(lhs0[rows:])
        lhs1[rows:] = jnp.zeros_like(lhs1[rows:])
        for p, (start, stop) in enumerate(bounds):
            g, norm, m = ups[p], n_ref[:, start:stop], m_ref[:, start:stop]
            b = b_ref[:, start:stop].astype(low)
            gb = (g * (m / norm)).astype(low)
            gm = jnp.sum(g * before_ref[:, start:stop], axis=0, keepdims=True) / norm
            gm_ref[:, start:stop] = gm
            c = -gm * m / (norm * norm)
            weighted = (b.astype(jnp.float32) * c).astype(low)
            gi[:, 16 * p : 16 * p + 16] = (SCALE * dot_nt(gb, b)).astype(low)
            tail[p] = two_terms(dot_nt(weighted, b))
            gb_ref[:, start:stop] = SCALE * dot_tn(inner_ref[p], gb) + SCALE * c * cross_ref[:, start:stop]
            lhs, at = (lhs1, 0) if p == 2 else (lhs0, start)
            lhs[:rows, at : at + stop - start] = gb
            lhs[rows + 16 * p : rows + 16 * p + 16, at : at + stop - start] = weighted

    span = pl.ds(pl.multiple_of(t * TILE, TILE), TILE)
    back = dot_nt(lhs0[...], w0_ref[0]) + dot_nt(lhs1[...], w1_ref[0])
    grad_in = back[:rows]
    for p in range(3):
        a_tile = a_ref[p, :, span].astype(low)
        gi_p = gi[:, 16 * p : 16 * p + 16]
        grad_in = grad_in + dot_f32(gi_p, a_tile)
        spread = back[rows + 16 * p : rows + 16 * p + 16] + SCALE * dot_two(tail[p], a_tile)
        ga_ref[p] = dot_tn(gi_p, u_ref[:, span]) + SCALE * spread
    out_ref[:, span] = grad_in

    @pl.when(t == pl.num_programs(0) - 1)
    def _():
        v = x_ref[...].astype(jnp.float32)
        out_ref[...] = gx_ref[...] + rms_back(v, gain_ref[...], out_ref[...])


def qkv_back(gq, gkv, cosine, sine, before, u, inner, a, b, m, norms, cross, x, gain, gx, weights):
    rows, width = gx.shape
    cols = before.shape[1]
    k_cols = (cols - width) // 2
    tiles = width // TILE
    full = lambda shape: pl.BlockSpec(shape, lambda t: (0,) * len(shape))
    f32, low = jnp.float32, jnp.bfloat16
    wide = full((rows, width))
    return pl.pallas_call(
        qkv_back_kernel,
        out_shape=(
            pltpu.HBM((rows, width), f32),
            jax.ShapeDtypeStruct((3, 16, width), f32),
            jax.ShapeDtypeStruct((16, cols), f32),
            jax.ShapeDtypeStruct((1, cols), f32),
        ),
        grid=(tiles,),
        in_specs=[wide, full(gkv.shape), full(cosine.shape), full(sine.shape), full((rows, cols)), wide, full(inner.shape),
                  full(a.shape), full(b.shape), full(m.shape), full(norms.shape), full(cross.shape),
                  wide, full((1, width)), wide,
                  pl.BlockSpec((1, TILE, width + k_cols), lambda t: (0, t, 0)),
                  pl.BlockSpec((1, TILE, k_cols), lambda t: (1, t, 0))],
        out_specs=(wide, pl.BlockSpec((3, 16, TILE), lambda t: (0, 0, t)), full((16, cols)), full((1, cols))),
        scratch_shapes=[
            pltpu.VMEM((rows + 48, width + k_cols), low),
            pltpu.VMEM((rows + 48, k_cols), low),
            pltpu.VMEM((rows, 48), low),
            pltpu.VMEM((3, 32, 16), low),
        ],
        compiler_params=pltpu.CompilerParams(vmem_limit_bytes=48 << 20),
        cost_estimate=pl.CostEstimate(flops=0, transcendentals=0, bytes_accessed=1 << 20),
        name="qkv_back",
    )(*in_hbm(gq), gkv, cosine, sine, *in_hbm(before, u), inner, *in_hbm(a, b), m, norms, *in_hbm(cross, x), gain,
      *in_hbm(gx, weights, weights))

MESH = pl.DeviceIdType.MESH


def place_in_seq():
    s = lax.axis_index("seq")
    return s, s // 2, lax.rem(s, 2)

def near_first(i, q, nc):
    short = jnp.where(q <= nc - 1 - q, q, nc - 1 - q)
    far = jnp.where(q <= nc - 1 - q, i, nc - 1 - i)
    step = (i + 1) // 2
    near = q - step if i % 2 else q + step
    return jnp.where(i <= 2 * short, near, far)


def place_in_rows(rows):
    half = rows // 2
    r = lax.axis_index("rows")
    a, b = r // 2, lax.rem(r, 2)
    turned = lambda k: 2 * lax.rem(a + k + half, half)
    return r, 2 * a + 1 - b, lambda k: turned(k) + b, lambda k: turned(k) + 1 - b


def greet_all(n, rows):
    s = lax.axis_index("seq")
    r, b_row, a_row, _ = place_in_rows(rows)
    barrier = pltpu.get_barrier_semaphore()
    for t in range(1, n):
        pl.semaphore_signal(
            barrier, inc=1, device_id=(r, lax.rem(s + t, n)), device_id_type=MESH
        )
    pl.semaphore_signal(barrier, inc=1, device_id=(b_row, s), device_id_type=MESH)
    for k in range(1, rows // 2):
        pl.semaphore_signal(barrier, inc=1, device_id=(a_row(k), s), device_id_type=MESH)
    pl.semaphore_wait(barrier, n - 1 + rows // 2)


def remote(src, dst, send, recv, row, seq):
    return pltpu.make_async_remote_copy(
        src_ref=src, dst_ref=dst, send_sem=send, recv_sem=recv,
        device_id=(row, seq), device_id_type=MESH,
    )


def weights_kernel(n, rows, qo, kv, xg, wd_hbm, ad_hbm, bd_hbm, x_hbm, gain_ref, aa_hbm, ag_hbm,
                   wa, gz, near, sq_ref, gram_ref, u_hbm, inner_ref,
                   wd, ad_ref, bd_ref, x_ref, aa_ref, ag_ref, own_ref, cols_ref, local, edge, a_in, a_sib_in, a_out, a_sib_out, z_in, z_out):
    nc, half = n // 2, rows // 2
    others = half - 1
    units = gz.shape[-1]
    s, q, c = place_in_seq()
    sibling = s + 1 - 2 * c
    r, b_row, a_row, diagonal = place_in_rows(rows)
    greet_all(n, rows)

    both, first, second = pl.ds(0, 2), pl.ds(0, 1), pl.ds(1, 1)
    LINE, FROM_B = 0, 1

    def from_a(k):
        return 1 + k

    def relay_b(k):
        return 1 + others + k

    def relay_a(k):
        return 1 + 2 * others + k

    def a_view(p, core, parts, row):
        return wa.at[parts, 2 * p + core, row]

    def content(kind):
        if kind == LINE:
            return both, r
        if kind == FROM_B:
            return both, b_row
        for k in range(1, half):
            if kind == from_a(k):
                return both, a_row(-k)
            if kind == relay_b(k):
                return second, diagonal(-k)
            if kind == relay_a(k):
                return first, diagonal(-k)

    kinds = 2 + 3 * others

    def a_send(p, parts, row, kind, target_row):
        return remote(
            a_view(p, c, parts, row), a_view(p, c, parts, row),
            a_out.at[p, kind], a_in.at[p, kind], target_row, s,
        )

    def a_arrival(p, kind):
        parts, row = content(kind)
        return a_send(p, parts, row, kind, r)

    def a_to_sibling(p, kind, core):
        parts, row = content(kind)
        return remote(
            a_view(p, core, parts, row), a_view(p, core, parts, row),
            a_sib_out.at[p, kind], a_sib_in.at[p, kind], r, sibling,
        )

    def columns(device):
        return pl.ds(pl.multiple_of(device * units, units), units)

    def z_send(p, core):
        return remote(
            xg.at[:, r, :, columns(2 * p + core)], gz.at[:, s],
            z_out.at[p, core], z_in.at[q, c], r, 2 * p + core,
        )

    def z_arrival(p, core):
        slot = gz.at[:, 2 * p + core]
        return remote(slot, slot, z_out.at[p, core], z_in.at[p, core], r, s)

    def line_send(p, sem, target):
        view = a_view(p, c, both, r)
        return remote(view, view, sem, a_in.at[p, LINE], r, target)

    wide, k_cols = qo.shape[-1], kv.shape[-1]
    blocks = [(qo, 0, 0), (kv, 0, wide), (kv, 1, 0), (qo, 1, k_cols)]

    def own_blocks(part, out):
        for source, i, start in blocks:
            columns_of = pl.ds(start, source.shape[-1])
            out(source.at[i, part], i, columns_of)

    def own_line(sem, target):
        own_blocks(
            r,
            lambda src, i, cols: remote(
                src, wa.at[i, s, r, :, cols], sem, a_in.at[q, LINE], r, target
            ).start(),
        )

    pl.when(q > 0)(lambda: own_line(edge.at[0], s - 2))
    pl.when(q < nc - 1)(lambda: own_line(edge.at[1], s + 2))
    order = [near_first(i, q, nc) for i in range(nc)]
    whole_block = wa.at[:, s]
    sib_a = lambda: remote(whole_block, whole_block, edge.at[2], edge.at[3], r, sibling)
    sib_g = lambda: remote(
        xg.at[:, :, :, columns(sibling)], near.at[:, c], edge.at[4], edge.at[5], r, sibling
    )
    keep_a = pltpu.make_async_copy(own_ref, whole_block, local.at[0])
    keep_g = pltpu.make_async_copy(cols_ref, near.at[:, c], local.at[1])
    all_parts = pl.ds(0, rows)
    own_blocks(
        all_parts,
        lambda src, i, cols: remote(
            src, wa.at[i, s, :, :, cols], edge.at[2], edge.at[3], r, sibling
        ).start(),
    )
    own_blocks(
        all_parts,
        lambda src, i, cols: pltpu.make_async_copy(
            src, own_ref.at[i, :, :, cols], local.at[9]
        ).start(),
    )
    take_cols = pltpu.make_async_copy(xg.at[:, :, :, columns(s)], cols_ref, local.at[10])
    take_cols.start()
    takes = [
        pltpu.make_async_copy(src, dst, local.at[3 + i])
        for i, (src, dst) in enumerate(
            [(x_hbm, x_ref), (aa_hbm, aa_ref), (ag_hbm, ag_ref), (ad_hbm, ad_ref), (bd_hbm, bd_ref), (wd_hbm, wd)]
        )
    ]
    for cp in takes:
        cp.start()
    for cp in takes:
        cp.wait()
    pltpu.make_async_copy(own_ref, own_ref, local.at[9]).wait()
    keep_a.start()
    take_cols.wait()
    keep_g.start()
    low = jnp.bfloat16
    v = x_ref[...].astype(jnp.float32)
    u = (v * unit_rms(v) * gain_ref[...]).astype(low)
    x_ref[...] = u
    keep_u = pltpu.make_async_copy(x_ref, u_hbm, local.at[2])
    keep_u.start()
    for g in range(4):
        a = aa_ref[g].astype(low)
        gram_ref[g] = two_terms(dot_nt(a, a))
        if g < 3:
            inner_ref[g] = dot_nt(u, a).astype(low)
    for g in range(2):
        a = ag_ref[g].astype(low)
        gram_ref[4 + g] = two_terms(dot_nt(a, a))

    def down_squares():
        a = ad_ref[...].astype(low)
        gram_ref[6] = two_terms(dot_nt(a, a))
        mine = pl.ds(pl.multiple_of(s * wd.shape[0], wd.shape[0]), wd.shape[0])
        cross = dot_f32(ad_ref[:, mine].astype(low), wd[...])
        b_wide = bd_ref[...].astype(low).astype(jnp.float32)
        sq_ref[...] = column_squares(wd[...]) + 2.0 * SCALE * jnp.sum(b_wide * cross, axis=0, keepdims=True)

    for p in order[1:]:
        a_arrival(p, LINE).wait_recv()
        pl.when((p < q) & (q < nc - 1))(
            lambda p=p: line_send(p, a_out.at[p, LINE], s + 2).start()
        )
        pl.when((p > q) & (q > 0))(
            lambda p=p: line_send(p, a_out.at[p, LINE], s - 2).start()
        )
        a_send(p, both, r, FROM_B, b_row).start()
        for k in range(1, half):
            a_send(p, both, r, from_a(k), a_row(k)).start()
        a_to_sibling(p, LINE, c).start()
    for p in order[1:]:
        for core in range(2):
            z_send(p, core).start()
    sib_g().start()
    down_squares()
    keep_u.wait()
    for p in order[1:]:
        a_arrival(p, FROM_B).wait_recv()
        for k in range(1, half):
            a_send(p, first, b_row, relay_a(k), a_row(k)).start()
        a_to_sibling(p, FROM_B, c).start()
        for k in range(1, half):
            a_arrival(p, from_a(k)).wait_recv()
            a_send(p, second, a_row(-k), relay_b(k), b_row).start()
            a_to_sibling(p, from_a(k), c).start()
    for p in order[1:]:
        for k in range(1, half):
            for kind in (relay_b(k), relay_a(k)):
                a_arrival(p, kind).wait_recv()
                a_to_sibling(p, kind, c).start()
    keep_a.wait()
    keep_g.wait()
    sib_a().wait()
    sib_g().wait()
    pl.when(q > 0)(lambda: line_send(q, edge.at[0], s).wait_send())
    pl.when(q < nc - 1)(lambda: line_send(q, edge.at[1], s).wait_send())
    for p in order[1:]:
        pl.when(((p < q) & (q < nc - 1)) | ((p > q) & (q > 0)))(
            lambda p=p: line_send(p, a_out.at[p, LINE], s).wait_send()
        )
        for kind in range(kinds):
            a_to_sibling(p, kind, c).wait_send()
            a_to_sibling(p, kind, 1 - c).wait_recv()
        a_send(p, both, r, FROM_B, b_row).wait_send()
        for k in range(1, half):
            a_send(p, both, r, from_a(k), r).wait_send()
            a_send(p, first, b_row, relay_a(k), r).wait_send()
            a_send(p, second, a_row(-k), relay_b(k), r).wait_send()
        for core in range(2):
            z_send(p, core).wait_send()
            z_arrival(p, core).wait_recv()


def gather_weights(n, rows, qo, kv, xg, wd, ad, bd, x, gain, aa, ag, collective_id):
    nc = n // 2
    _, block, width = qo.shape
    part = block // rows
    cols = width + kv.shape[2]
    qo = qo.reshape(2, rows, part, width)
    kv = kv.reshape(2, rows, part, kv.shape[2])
    xg = xg.reshape(2, rows, part, xg.shape[2])
    units = xg.shape[3] // n
    kinds = 2 + 3 * (rows // 2 - 1)
    dma = pltpu.SemaphoreType.DMA
    anywhere = pl.BlockSpec(memory_space=pltpu.HBM)
    vmem = pl.BlockSpec(memory_space=pltpu.VMEM)
    low = qo.dtype
    wa, gz, near, sq, grams, u, inner = pl.pallas_call(
        functools.partial(weights_kernel, n, rows),
        out_shape=(
            pltpu.HBM((2, n, rows, part, cols), low),
            pltpu.HBM((2, n, part, units), low),
            pltpu.HBM((2, 2, rows, part, units), low),
            jax.ShapeDtypeStruct((1, width), jnp.float32),
            jax.ShapeDtypeStruct((7, 32, 16), low),
            pltpu.HBM(x.shape, low),
            jax.ShapeDtypeStruct((3, x.shape[0], 16), low),
        ),
        in_specs=[anywhere] * 7 + [vmem] + [anywhere] * 2,
        out_specs=(anywhere,) * 3 + (vmem,) * 2 + (anywhere, vmem),
        scratch_shapes=[pltpu.VMEM(v.shape, v.dtype) for v in (wd, ad, bd, x, aa, ag)]
        + [pltpu.VMEM((2, rows, part, cols), low), pltpu.VMEM((2, rows, part, units), low)]
        + [dma((11,)), dma((6,))]
        + [dma((nc, kinds))] * 4
        + [dma((nc, 2))] * 2,
        compiler_params=pltpu.CompilerParams(
            collective_id=collective_id, has_side_effects=True, vmem_limit_bytes=32 << 20
        ),
        cost_estimate=pl.CostEstimate(
            flops=0, transcendentals=0, bytes_accessed=250 * 1024 * 1024
        ),
        name="gather_weights",
    )(*in_hbm(qo, kv, xg, wd, ad, bd, x), gain, *in_hbm(aa, ag))
    return wa.reshape(2, n * block, cols), gz, near, sq, grams, u, inner


def gather_kernel(n, rows, count, shared, *refs):
    nc = n // 2
    sources = refs[: count + len(shared[0])]
    outs = refs[len(sources) : 2 * len(sources) - len(shared[0]) + len(shared[1])]
    scratch = refs[len(sources) + len(outs) :]
    held_here = scratch[:count]
    local_sem, to_sib, to_left, to_right, recv, share_out, share_in = scratch[count:]
    xs, held, swapped = sources[:count], sources[count:], outs[count:]
    s, q, c = place_in_seq()
    sibling = s + 1 - 2 * c
    r, b_row, a_row, _ = place_in_rows(rows)
    greet_all(n, rows)
    takes = [pltpu.make_async_copy(xs[k], held_here[k], local_sem.at[0, k]) for k in range(count)]
    keeps = [
        pltpu.make_async_copy(held_here[k], outs[k].at[s], local_sem.at[1, k]) for k in range(count)
    ]
    for cp in takes:
        cp.start()

    def copy(k, src, slot, sems, target):
        return remote(src, outs[k].at[slot], sems.at[k, slot], recv.at[k, slot], r, target)

    def share(i, p):
        source, piece, turn, _ = shared[1][i]
        pair = pl.ds(2 * p, 2)
        src = held[source].at[pair] if piece is None else held[source].at[piece, pair]
        target = b_row if turn == 0 else a_row(turn)
        return remote(src, swapped[i].at[pair], share_out.at[i, p], share_in.at[i, p], target, s)

    for k in range(count):
        pl.when(q > 0)(lambda k=k: copy(k, xs[k], s, to_left, s - 2).start())
        pl.when(q < nc - 1)(lambda k=k: copy(k, xs[k], s, to_right, s + 2).start())
        copy(k, xs[k], s, to_sib, sibling).start()
    order = [near_first(i, q, nc) for i in range(nc)]
    for p in order[1:]:
        for i in range(len(shared[1])):
            share(i, p).start()
    for take, keep in zip(takes, keeps):
        take.wait()
        keep.start()
    for p in order[1:]:
        slot = 2 * p + c
        for k in range(count):
            src = outs[k].at[slot]
            copy(k, src, slot, to_right, s).wait_recv()
            pl.when((p < q) & (q < nc - 1))(
                lambda k=k, src=src, slot=slot: copy(k, src, slot, to_right, s + 2).start()
            )
            pl.when((p > q) & (q > 0))(
                lambda k=k, src=src, slot=slot: copy(k, src, slot, to_left, s - 2).start()
            )
            copy(k, src, slot, to_sib, sibling).start()
    for cp in keeps:
        cp.wait()
    for p in range(nc):
        mine, theirs = 2 * p + c, 2 * p + 1 - c
        for k in range(count):
            copy(k, outs[k].at[theirs], theirs, to_sib, sibling).wait_recv()
            copy(k, outs[k].at[mine], mine, to_sib, sibling).wait_send()
            pl.when((q < nc - 1) & (p <= q))(
                lambda k=k, mine=mine: copy(k, outs[k].at[mine], mine, to_right, s).wait_send()
            )
            pl.when((q > 0) & (p >= q))(
                lambda k=k, mine=mine: copy(k, outs[k].at[mine], mine, to_left, s).wait_send()
            )
    for p in order[1:]:
        for i in range(len(shared[1])):
            share(i, p).wait_send()
            share(i, p).wait_recv()


def gather_seq(n, rows, arrays, collective_id, held=(), shares=()):
    nc, count = n // 2, len(arrays)
    nbytes = sum(a.size * a.dtype.itemsize for a in arrays)
    dma = pltpu.SemaphoreType.DMA
    shape = jax.ShapeDtypeStruct
    outs = [shape((n, *a.shape), a.dtype) for a in arrays]
    outs += [shape(held[source].shape[-3:], held[source].dtype) for source, _, _ in shares]
    anywhere = pl.BlockSpec(memory_space=pltpu.HBM)
    listed = (tuple(held), [(source, piece, turn, None) for source, piece, turn in shares])
    sems = dma((max(1, len(shares)), nc))
    got = pl.pallas_call(
        functools.partial(gather_kernel, n, rows, count, (range(len(held)), listed[1])),
        out_shape=tuple(outs),
        in_specs=[anywhere] * (count + len(held)),
        out_specs=(anywhere,) * len(outs),
        scratch_shapes=[pltpu.VMEM(a.shape, a.dtype) for a in arrays]
        + [dma((2, count))]
        + [dma((count, n))] * 4
        + [sems] * 2,
        compiler_params=pltpu.CompilerParams(collective_id=collective_id, has_side_effects=True),
        cost_estimate=pl.CostEstimate(flops=0, transcendentals=0, bytes_accessed=nbytes * n * 20),
        name="gather_seq",
    )(*arrays, *held)
    return got[:count], got[count:]

def swap_halves(x):
    return pltpu.roll(x.astype(jnp.float32), HEAD_DIM, 1)


def stack_heads(block):
    lane = lax.broadcasted_iota(jnp.int32, (block.shape[0], 128), 1)
    rows = []
    for h in range(8):
        pair = block[:, (h // 2) * 128 : (h // 2 + 1) * 128].astype(jnp.float32)
        if h % 2 != h // 4:
            pair = swap_halves(pair)
        keep = lane < HEAD_DIM if h // 4 == 0 else lane >= HEAD_DIM
        rows.append(jnp.where(keep, pair, 0.0).astype(jnp.bfloat16))
    return jnp.concatenate(rows, axis=0)


def unstack_heads(stacked, span):
    lane = lax.broadcasted_iota(jnp.int32, (span, 128), 1)
    pairs = []
    for t in range(4):
        first = stacked[2 * t * span : (2 * t + 1) * span]
        second = stacked[(2 * t + 1) * span : (2 * t + 2) * span]
        if t < 2:
            second = swap_halves(second)
        else:
            first = swap_halves(first)
        pairs.append(jnp.where(lane < HEAD_DIM, first, second))
    return jnp.concatenate(pairs, axis=1)


def key_blocks(kv_ref):
    n, _, span, width = kv_ref.shape
    at = pl.multiple_of(pl.program_id(1) * 128, 128)
    pick = lambda start: kv_ref[:, 0, :, pl.ds(start, 128)].reshape(n * span, 128)
    return pick(at), pick(width // 2 + at)


def attend_kernel(valid_ref, q_ref, kv_ref, o_ref, p_ref, s_ref):
    span = q_ref.shape[1]
    keys = kv_ref.shape[0] * span
    q8 = stack_heads(q_ref[0]) * jnp.bfloat16(HEAD_DIM**-0.5)
    k2, v2 = key_blocks(kv_ref)
    s_ref[...] = lax.dot_general(q8, k2, last_last, preferred_element_type=jnp.float32)
    q_pos = lax.axis_index("seq") * span + lax.broadcasted_iota(jnp.int32, (span, 1), 0)
    limit = jnp.minimum(q_pos + 1, valid_ref[pl.program_id(0)])
    allowed = lax.broadcasted_iota(jnp.int32, (span, keys), 1) < limit
    for h in range(8):
        head = slice(h * span, (h + 1) * span)
        scores = jnp.where(allowed, s_ref[head], -1e30)
        unscaled = jnp.exp(scores - jnp.max(scores, axis=1, keepdims=True))
        shares = unscaled * (1.0 / jnp.sum(unscaled, axis=1, keepdims=True))
        p_ref[0, 0, head] = shares.astype(jnp.bfloat16)
    mixed = jnp.dot(p_ref[0, 0], v2, preferred_element_type=jnp.float32)
    o_ref[0] = unstack_heads(mixed, span).astype(jnp.bfloat16)


def attend(q, kv, valid):
    pair, span, width = q.shape
    n, kv_width = kv.shape[0], kv.shape[3] // 2
    groups = kv_width // 128
    keys = n * span
    q_spec = pl.BlockSpec((1, span, 512), lambda p, j, *_: (p, 0, j))
    flops = 4 * pair * groups * 8 * span * keys * 128
    return pl.pallas_call(
        attend_kernel,
        out_shape=(
            pltpu.HBM(q.shape, jnp.bfloat16),
            pltpu.HBM((pair, groups, 8 * span, keys), jnp.bfloat16),
        ),
        grid_spec=pltpu.PrefetchScalarGridSpec(
            num_scalar_prefetch=1,
            grid=(pair, groups),
            in_specs=[
                q_spec,
                pl.BlockSpec((n, 1, span, 2 * kv_width), lambda p, j, *_: (0, p, 0, 0)),
            ],
            out_specs=(
                q_spec,
                pl.BlockSpec((1, 1, 8 * span, keys), lambda p, j, *_: (p, j, 0, 0)),
            ),
            scratch_shapes=[pltpu.VMEM((8 * span, keys), jnp.float32)],
        ),
        compiler_params=pltpu.CompilerParams(vmem_limit_bytes=40 << 20),
        cost_estimate=pl.CostEstimate(
            flops=flops, transcendentals=flops // 512, bytes_accessed=8 << 20
        ),
        name="attend",
    )(valid, *in_hbm(q, kv))


def attend_back_kernel(q_ref, kv_ref, p_ref, g_ref, gq_ref, gkv_ref, s_ref, g_scores):
    span = q_ref.shape[1]
    keys = kv_ref.shape[0] * span
    q8 = stack_heads(q_ref[0]) * jnp.bfloat16(HEAD_DIM**-0.5)
    g8 = stack_heads(g_ref[0])
    k2, v2 = key_blocks(kv_ref)
    low = p_ref[0, 0]
    s_ref[...] = lax.dot_general(g8, v2, last_last, preferred_element_type=jnp.float32)
    for h in range(8):
        head = slice(h * span, (h + 1) * span)
        shares = p_ref[0, 0, head].astype(jnp.float32)
        weighted = shares * s_ref[head]
        centre = jnp.sum(weighted, axis=1, keepdims=True)
        g_scores[head] = (weighted - shares * centre).astype(jnp.bfloat16)
    grad_scores = g_scores[...]
    gq = jnp.dot(grad_scores, k2, preferred_element_type=jnp.float32) * HEAD_DIM**-0.5
    gq_ref[0] = unstack_heads(gq, span).astype(jnp.bfloat16)
    gk = lax.dot_general(grad_scores, q8, first_first, preferred_element_type=jnp.float32)
    gv = lax.dot_general(low, g8, first_first, preferred_element_type=jnp.float32)
    both = jnp.concatenate([gk, gv], axis=1).astype(jnp.bfloat16)
    at = pl.multiple_of(pl.program_id(1) * 256, 256)
    gkv_ref[:, 0, :, pl.ds(at, 256)] = both.reshape(gkv_ref.shape[0], span, 256)


def attend_back(q, kv, shares, g):
    pair, span, _ = q.shape
    n, kv_width = kv.shape[0], kv.shape[3] // 2
    groups = kv_width // 128
    keys = n * span
    q_spec = pl.BlockSpec((1, span, 512), lambda p, j: (p, 0, j))
    return pl.pallas_call(
        attend_back_kernel,
        out_shape=(
            pltpu.HBM(q.shape, jnp.bfloat16),
            pltpu.HBM(kv.shape, jnp.bfloat16),
        ),
        grid=(pair, groups),
        in_specs=[
            q_spec,
            pl.BlockSpec((n, 1, span, 2 * kv_width), lambda p, j: (0, p, 0, 0)),
            pl.BlockSpec((1, 1, 8 * span, keys), lambda p, j: (p, j, 0, 0)),
            q_spec,
        ],
        out_specs=(
            q_spec,
            pl.BlockSpec((n, 1, span, 2 * kv_width), lambda p, j: (0, p, 0, 0)),
        ),
        scratch_shapes=[
            pltpu.VMEM((8 * span, keys), jnp.float32),
            pltpu.VMEM((8 * span, keys), jnp.bfloat16),
        ],
        compiler_params=pltpu.CompilerParams(vmem_limit_bytes=40 << 20),
        cost_estimate=pl.CostEstimate(flops=0, transcendentals=0, bytes_accessed=1 << 20),
        name="attend_back",
    )(*in_hbm(q, kv, shares, g))

def by_distance(i, q, nc):
    room = nc - 1 - q
    left_half = q <= room
    short = jnp.where(left_half, q, room)
    far = jnp.where(left_half, i, nc - 1 - i)
    step = (i + 1) // 2
    near = jnp.where(lax.rem(i, 2) == 1, q - step, q + step)
    return jnp.where(i <= 2 * short, near, far)


def ffn_kernel(n, rows, pieces, u_hbm, inner_hbm, gy0_hbm, gy1_hbm, wd_hbm, a_ref, b_ref, m_ref, ad_ref, bd_ref, md_ref, sq_ref, gram_ref,
               in_ref, down0_hbm, down1_hbm, ga_ref, gb_ref, gm_ref, norm_ref, gad_ref, gbd_ref, gmd_ref, nd_ref,
               w_parts, wd, u, side, gy, down, own, theirs, sib, from_left, from_right, ratio, cross, gm_all,
               w_sem, load_sem, down_sem, small_out, small_in, to_sib, sib_in, to_right, right_in, to_left, left_in):
    nc = n // 2
    f32, low = jnp.float32, jnp.bfloat16
    s, q, c = place_in_seq()
    tokens = own.shape[1]

    weights = [pltpu.make_async_copy(wd_hbm, wd, w_sem.at[0])]
    for src, dst in place_pieces(n, rows, pieces, w_parts):
        weights.append(pltpu.make_async_copy(src, dst, w_sem.at[len(weights)]))
    for cp in weights:
        cp.start()

    def loads(i):
        p = by_distance(nc - 1 - i, q, nc)
        slot = lax.rem(i, 2)
        pair = pl.ds(2 * p, 2)
        return (
            pltpu.make_async_copy(u_hbm.at[pair], u.at[slot], load_sem.at[0, slot]),
            pltpu.make_async_copy(
                gy0_hbm.at[pair], gy.at[slot, :, : tokens // 2], load_sem.at[1, slot]
            ),
            pltpu.make_async_copy(
                gy1_hbm.at[pair], gy.at[slot, :, tokens // 2 :], load_sem.at[2, slot]
            ),
            pltpu.make_async_copy(inner_hbm.at[pair], side.at[slot], load_sem.at[3, slot]),
        )

    for cp in loads(0):
        cp.start()
    sibling = s + 1 - 2 * c
    barrier = pltpu.get_barrier_semaphore()
    for t in range(1, n):
        pl.semaphore_signal(
            barrier, inc=1, device_id={"seq": lax.rem(s + t, n)}, device_id_type=MESH
        )

    def to_sibling(p):
        return pltpu.make_async_remote_copy(
            src_ref=theirs.at[p], dst_ref=sib.at[p], send_sem=to_sib.at[p], recv_sem=sib_in.at[p],
            device_id={"seq": sibling}, device_id_type=MESH,
        )

    def rightward(p, target):
        return pltpu.make_async_remote_copy(
            src_ref=own.at[p], dst_ref=from_left.at[p], send_sem=to_right.at[p], recv_sem=right_in.at[p],
            device_id={"seq": target}, device_id_type=MESH,
        )

    def leftward(p, target):
        return pltpu.make_async_remote_copy(
            src_ref=own.at[p], dst_ref=from_right.at[p], send_sem=to_left.at[p], recv_sem=left_in.at[p],
            device_id={"seq": target}, device_id_type=MESH,
        )

    def down_out(slot, p):
        half = tokens // 2
        return [
            pltpu.make_async_copy(
                down.at[slot, :, half * k : half * (k + 1)], out.at[pl.ds(2 * p, 2)], down_sem.at[k, slot]
            )
            for k, out in enumerate((down0_hbm, down1_hbm))
        ]

    def pass_on(p):
        to_sibling(p).wait_recv()

        @pl.when(p > q)
        def _():
            @pl.when(q > 0)
            def _():
                rightward(p, s).wait_recv()
                own[p] = (own[p].astype(f32) + sib[p].astype(f32) + from_left[p].astype(f32)).astype(low)

            @pl.when(q == 0)
            def _():
                own[p] = (own[p].astype(f32) + sib[p].astype(f32)).astype(low)

            rightward(p, s + 2).start()

        @pl.when(p < q)
        def _():
            @pl.when(q < nc - 1)
            def _():
                leftward(p, s).wait_recv()
                own[p] = (own[p].astype(f32) + sib[p].astype(f32) + from_right[p].astype(f32)).astype(low)

            @pl.when(q == nc - 1)
            def _():
                own[p] = (own[p].astype(f32) + sib[p].astype(f32)).astype(low)

            leftward(p, s - 2).start()

    def starts_flow(p):
        return ((p > q) & (q == 0)) | ((p < q) & (q == nc - 1))

    w = [w_parts.at[g] for g in range(2)]
    width = u_hbm.shape[2]
    weight = lambda g: w[g][...].reshape(width, -1)
    units = wd.shape[0]
    mine = pl.ds(pl.multiple_of(s * units, units), units)
    bd = bd_ref[...].astype(low)
    ad = ad_ref[:, mine].astype(low)
    a = [a_ref[g].astype(low) for g in range(2)]
    b = [b_ref[g, :, mine].astype(low) for g in range(2)]
    m = [m_ref[g : g + 1, mine] for g in range(2)]
    for cp in weights:
        cp.wait()
    a_both = jnp.concatenate(a, axis=0)
    for g in range(2):
        norm, cr = column_norms(weight(g), gram_ref[4 + g], b[g], dot_f32(a[g], weight(g)))
        norm_ref[g] = norm
        cross[g] = cr
        ratio[g] = m[g] / norm
    for ref in (ga_ref, gb_ref, gm_ref, gad_ref, gbd_ref, gmd_ref):
        ref[...] = jnp.zeros_like(ref)
    bd_wide = bd.astype(f32)
    gram_b = dot_two(gram_ref[6], bd)
    squares = jnp.sum(sq_ref[...], axis=0) + SCALE * SCALE * jnp.sum(
        bd_wide * gram_b, axis=0, keepdims=True
    )
    nd_ref[...] = jnp.sqrt(squares + 1e-06)
    ratio_d = md_ref[...] / nd_ref[...]
    pl.semaphore_wait(barrier, n - 1)

    def step(i, carry):
        p = by_distance(nc - 1 - i, q, nc)
        slot = lax.rem(i, 2)
        for cp in loads(i):
            cp.wait()

        @pl.when(i + 1 < nc)
        def _():
            for cp in loads(i + 1):
                cp.start()

        x = u[slot].reshape(2 * tokens, -1)
        upstream = gy[slot].reshape(2 * tokens, -1).astype(f32)
        gb_d = (upstream * ratio_d).astype(low)
        gi_d = (SCALE * dot_nt(gb_d, bd)).astype(low)
        gh = dot_nt(gb_d, wd[...]) + dot_f32(gi_d, ad)
        sides = side[slot].reshape(2 * tokens, -1)
        inner = [sides[:, 16 * g : 16 * g + 16] for g in range(2)]
        before = [dot_f32(x, weight(g)) + SCALE * dot_f32(inner[g], b[g]) for g in range(2)]
        gate = before[0] * ratio[0]
        lift = before[1] * ratio[1]
        sig = 1.0 / (1.0 + jnp.exp(-gate))
        silu = gate * sig
        hidden = (silu * lift).astype(low)
        grads = [gh * lift * sig * (1.0 + gate * (1.0 - sig)), gh * silu]
        gb = [(grads[g] * ratio[g]).astype(low) for g in range(2)]
        gi = jnp.concatenate([(SCALE * dot_nt(gb[g], b[g])).astype(low) for g in range(2)], axis=1)
        back = dot_nt(gb[0], weight(0)) + dot_nt(gb[1], weight(1)) + dot_f32(gi, a_both)
        back = back.astype(low).reshape(2, tokens, -1)
        first, second = back[0], back[1]

        @pl.when(c == 0)
        def _():
            own[p] = first
            theirs[p] = second

        @pl.when(c == 1)
        def _():
            own[p] = second
            theirs[p] = first

        to_sibling(p).start()
        inner_d = dot_nt(hidden, ad).astype(low)
        part = dot_f32(hidden, wd[...]) + SCALE * dot_f32(inner_d, bd)

        @pl.when(i >= 2)
        def _():
            for cp in down_out(slot, p):
                cp.wait()

        down[slot] = part.astype(low).reshape(2, tokens, -1)
        for cp in down_out(slot, p):
            cp.start()
        gmd_ref[...] += jnp.sum(upstream * part, axis=0, keepdims=True)
        gad_ref[...] += dot_tn(gi_d, hidden)
        gbd_ref[...] += SCALE * dot_tn(inner_d, gb_d)
        ga_ref[...] += dot_tn(gi, x).reshape(ga_ref.shape)
        for g in range(2):
            gm_ref[g] += jnp.sum(grads[g] * before[g], axis=0, keepdims=True)
            gb_ref[g] += SCALE * dot_tn(inner[g], gb[g])

        last = by_distance(nc - i, q, nc)
        pl.when((i > 0) & (i < nc - 1) & jnp.logical_not(starts_flow(last)))(lambda: pass_on(last))
        pl.when(starts_flow(p) | (i == nc - 2))(lambda: pass_on(p))
        return carry

    lax.fori_loop(0, nc, step, 0)

    gmd_ref[...] = gmd_ref[...] / nd_ref[...]

    def small(t, slot):
        return pltpu.make_async_remote_copy(
            src_ref=gmd_ref,
            dst_ref=gm_all.at[slot],
            send_sem=small_out.at[t],
            recv_sem=small_in.at[t],
            device_id={"seq": lax.rem(s + t, n)},
            device_id_type=MESH,
        )

    for t in range(1, n):
        small(t, s).start()
    for g in range(2):
        norm = norm_ref[g]
        gm = gm_ref[g] / norm
        gm_ref[g] = gm
        col = -gm * m[g] / (norm * norm)
        weighted = (b[g].astype(f32) * col).astype(low)
        tail = two_terms(dot_nt(weighted, b[g]))
        ga_ref[g] += SCALE * (dot_nt(weighted, weight(g)) + SCALE * dot_two(tail, a[g]))
        gb_ref[g] += SCALE * col * cross[g]

    gm_line = gmd_ref[...]
    for t in range(1, n):
        slot = lax.rem(s - t + n, n)
        small(t, slot).wait_recv()
        gm_line = gm_line + gm_all[slot]
    col = -gm_line * md_ref[...] / (nd_ref[...] * nd_ref[...])
    weighted = (bd_wide * col).astype(low)
    tail = two_terms(dot_nt(weighted, bd))
    gad_ref[...] += SCALE * (dot_nt(weighted, wd[...]) + SCALE * dot_two(tail, ad))
    own_gram = jnp.where(s == 0, SCALE, 0.0) * gram_b
    gbd_ref[...] += SCALE * col * (dot_f32(ad, wd[...]) + own_gram)

    to_sibling(q).wait_recv()
    in_ref[...] = own[q].astype(f32) + sib[q].astype(f32)

    @pl.when(q > 0)
    def _():
        rightward(q, s).wait_recv()
        in_ref[...] += from_left[q].astype(f32)

    @pl.when(q < nc - 1)
    def _():
        leftward(q, s).wait_recv()
        in_ref[...] += from_right[q].astype(f32)

    for i in range(min(2, nc)):
        for cp in down_out(i, 0):
            cp.wait()
    for t in range(1, n):
        small(t, s).wait_send()
    for p in range(nc):
        to_sibling(p).wait_send()
        pl.when(p > q)(lambda p=p: rightward(p, s).wait_send())
        pl.when(p < q)(lambda p=p: leftward(p, s).wait_send())


def share_plan(rows):
    turns = range(1, rows // 2)
    first = [(0, 0, k) for k in turns] + [(0, 1, 0)]
    second = [(0, 0, 0)] + [(0, 1, k) for k in turns]
    second += [(k, None, 0) for k in turns] + [(rows // 2, None, k) for k in turns]
    return first, second


def place_pieces(n, rows, pieces, w_parts):
    nc, half = n // 2, rows // 2
    _, q, _ = place_in_seq()
    r, b_row, a_row, diagonal = place_in_rows(rows)
    own, near = pieces[:2]
    turns = range(1, half)
    held = [(own.at[g], g, r) for g in range(2)]
    kinds = [(0, a_row(-k)) for k in turns] + [(1, b_row)]
    kinds += [(0, b_row)] + [(1, a_row(-k)) for k in turns]
    kinds += [(0, diagonal(-k)) for k in turns] + [(1, diagonal(-k)) for k in turns]
    held += [(piece, g, hold) for piece, (g, hold) in zip(pieces[2:], kinds)]
    out = [(near, w_parts.at[:, pl.ds(2 * q, 2)])]
    for i in range(1, nc):
        pair = pl.ds(2 * near_first(i, q, nc), 2)
        out += [(src.at[pair], w_parts.at[g, pair, hold]) for src, g, hold in held]
    return out


def feed_forward(n, rows, pieces, u, inner, gy0, gy1, wd, a, b, m, ad, bd, md, sq, gram, collective_id):
    nc = n // 2
    _, tokens, width = u.shape
    units = wd.shape[0]
    f32, low = jnp.float32, jnp.bfloat16
    shape = jax.ShapeDtypeStruct
    vmem = pl.BlockSpec(memory_space=pltpu.VMEM)
    hbm = pl.BlockSpec(memory_space=pltpu.HBM)
    dma = pltpu.SemaphoreType.DMA
    line = pltpu.VMEM((nc, tokens, width), low)
    pair = pltpu.VMEM((2, 2, tokens, width), low)
    part = pieces[0].shape[2]
    copies = 2 + (n // 2 - 1) * (2 + 2 * rows - 2)
    count = len(pieces)

    def kernel(*refs):
        ffn_kernel(n, rows, refs[:count], *refs[count:])

    return pl.pallas_call(
        kernel,
        out_shape=(
            shape((tokens, width), f32),
            pltpu.HBM((n, tokens // 2, width), low),
            pltpu.HBM((n, tokens // 2, width), low),
            shape((2, 16, width), f32),
            shape((2, 16, units), f32),
            shape((2, 1, units), f32),
            shape((2, 1, units), f32),
            shape((16, units), f32),
            shape((16, width), f32),
            shape((1, width), f32),
            shape((1, width), f32),
        ),
        in_specs=[hbm] * (count + 5) + [vmem] * 8,
        out_specs=(vmem, hbm, hbm) + (vmem,) * 8,
        scratch_shapes=[
            pltpu.VMEM((2, n, rows, part, units), low),
            pltpu.VMEM((units, width), low),
            pair,
            pltpu.VMEM((2, 2, tokens, 128), low),
            pair,
            pair,
            line, line, line, line, line,
            pltpu.VMEM((2, 1, units), f32),
            pltpu.VMEM((2, 16, units), f32),
            pltpu.VMEM((n, 1, width), f32),
            dma((copies,)), dma((4, 2)), dma((2, 2)), dma((n,)), dma((n,)),
        ] + [dma((nc,))] * 6,
        compiler_params=pltpu.CompilerParams(
            collective_id=collective_id, has_side_effects=True, vmem_limit_bytes=60 << 20
        ),
        cost_estimate=pl.CostEstimate(
            flops=12 * n * tokens * width * units, transcendentals=n * tokens * units,
            bytes_accessed=32 << 20,
        ),
        name="feed_forward",
    )(*pieces, u, inner, gy0, gy1, wd, a, b, m, ad, bd, md, sq, gram)

def greet_cross(n, rows, wait=True):
    s, r = lax.axis_index("seq"), lax.axis_index("rows")
    barrier = pltpu.get_barrier_semaphore()
    for t in range(1, n):
        pl.semaphore_signal(barrier, inc=1, device_id=(r, lax.rem(s + t, n)), device_id_type=MESH)
    for t in range(1, rows):
        pl.semaphore_signal(barrier, inc=1, device_id=(lax.rem(r + t, rows), s), device_id_type=MESH)
    if wait:
        pl.semaphore_wait(barrier, n + rows - 2)


def scatter_kernel(n, rows, x_ref, gb_gu, gm_gu, n_gu, ga_d, o_ref, units_all, own, sib, from_left, from_right,
                   units, units_in, load_sem, to_sib, sib_in, to_right, right_in, to_left, left_in,
                   row_out, row_in, back_send, back_in, wide_send, wide_in, pass_send, pass_in):
    nc = n // 2
    s, q, c = place_in_seq()
    sibling = s + 1 - 2 * c
    theirs = 1 - c
    r = lax.axis_index("rows")
    greet_cross(n, rows)
    f32, low = jnp.float32, jnp.bfloat16
    unit_rows, size = units.shape[1:]

    def load(p):
        return pltpu.make_async_copy(x_ref.at[2 * p + c], own.at[p], load_sem.at[p])

    def to_sibling(p):
        return pltpu.make_async_remote_copy(
            src_ref=x_ref.at[2 * p + theirs],
            dst_ref=sib.at[p],
            send_sem=to_sib.at[p],
            recv_sem=sib_in.at[p],
            device_id={"seq": sibling},
            device_id_type=MESH,
        )

    def rightward(p, target):
        return pltpu.make_async_remote_copy(
            src_ref=own.at[p],
            dst_ref=from_left.at[p],
            send_sem=to_right.at[p],
            recv_sem=right_in.at[p],
            device_id={"seq": target},
            device_id_type=MESH,
        )

    def leftward(p, target):
        return pltpu.make_async_remote_copy(
            src_ref=own.at[p],
            dst_ref=from_right.at[p],
            send_sem=to_left.at[p],
            recv_sem=left_in.at[p],
            device_id={"seq": target},
            device_id_type=MESH,
        )

    order = []
    for t in range(nc):
        for p in (nc - 1 - t, t):
            if p not in order:
                order.append(p)
    for p in order:
        to_sibling(p).start()
        load(p).start()

    n_high = [n_gu[g].astype(low).astype(f32) for g in range(2)]
    n_rest = [n_gu[g] - n_high[g] for g in range(2)]
    tops = jnp.concatenate(
        [gm_gu[0], gm_gu[1]]
        + [v * (1.0 / rows) for v in (n_high[0], n_rest[0], n_high[1], n_rest[1])]
        + [jnp.zeros((2, size), f32)],
        axis=0,
    )
    blocks = [gb_gu[0][:8], gb_gu[0][8:], gb_gu[1][:8], gb_gu[1][8:], ga_d[:8], ga_d[8:], tops, jnp.zeros((8, size), f32)]
    per = unit_rows // 8
    for j in range(rows):
        units[j] = jnp.concatenate(blocks[per * j : per * (j + 1)], axis=0).astype(low)

    def member(t):
        return lax.rem(r + t + rows, rows)

    def chip(t):
        return lax.rem(q + t + nc, nc)

    def unit_send(t):
        return remote(units.at[member(t)], units_in.at[t], row_out.at[t], row_in.at[t], member(t), s)

    def unit_back(t, slot):
        place = units_all.at[r, c, slot]
        return remote(place, place, back_send.at[t], back_in.at[t], r, 2 * chip(t) + c)

    def unit_wide(t, row):
        place = units_all.at[row, c]
        return remote(place, place, wide_send.at[t], wide_in.at[t], member(t), s)

    def unit_hand(t, row, core):
        place = units_all.at[row, core]
        return remote(place, place, pass_send.at[t], pass_in.at[t], r, sibling)

    def sum_units():
        total = units[r].astype(f32)
        for t in range(1, rows):
            unit_send(t).wait_recv()
            total = total + units_in[t].astype(f32)
        units_all[r, c, q] = total.astype(low)
        for t in range(1, nc):
            unit_back(t, q).start()

    def spread_units():
        for t in range(1, nc):
            unit_back(t, chip(-t)).wait_recv()
        for t in range(1, rows):
            unit_wide(t, r).start()
        unit_hand(0, r, c).start()

    for t in range(1, rows):
        unit_send(t).start()
    sum_units()
    for step, p in enumerate(order):
        if step == 1:
            spread_units()
        load(p).wait()
        to_sibling(p).wait_recv()

        @pl.when(p > q)
        def _(p=p):
            @pl.when(q > 0)
            def _():
                rightward(p, s).wait_recv()
                total = own[p].astype(f32) + sib[p].astype(f32) + from_left[p].astype(f32)
                own[p] = total.astype(own.dtype)

            @pl.when(q == 0)
            def _():
                own[p] = (own[p].astype(f32) + sib[p].astype(f32)).astype(own.dtype)

            rightward(p, s + 2).start()

        @pl.when(p < q)
        def _(p=p):
            @pl.when(q < nc - 1)
            def _():
                leftward(p, s).wait_recv()
                total = own[p].astype(f32) + sib[p].astype(f32) + from_right[p].astype(f32)
                own[p] = total.astype(own.dtype)

            @pl.when(q == nc - 1)
            def _():
                own[p] = (own[p].astype(f32) + sib[p].astype(f32)).astype(own.dtype)

            leftward(p, s - 2).start()

    o_ref[...] = own[q].astype(f32) + sib[q].astype(f32)

    @pl.when(q > 0)
    def _():
        rightward(q, s).wait_recv()
        o_ref[...] += from_left[q].astype(f32)

    @pl.when(q < nc - 1)
    def _():
        leftward(q, s).wait_recv()
        o_ref[...] += from_right[q].astype(f32)

    for t in range(1, rows):
        unit_wide(t, member(-t)).wait_recv()
        unit_hand(t, member(-t), c).start()
    for t in range(rows):
        unit_hand(t, member(-t), theirs).wait_recv()
        unit_hand(t, member(-t), c).wait_send()
    for t in range(1, rows):
        unit_send(t).wait_send()
        unit_wide(t, r).wait_send()
    for t in range(1, nc):
        unit_back(t, q).wait_send()
    for p in range(nc):
        to_sibling(p).wait_send()
        pl.when(p > q)(lambda p=p: rightward(p, s).wait_send())
        pl.when(p < q)(lambda p=p: leftward(p, s).wait_send())


def scatter_seq(n, rows, x, own_units, collective_id):
    nc = n // 2
    _, height, cols = x.shape
    size = own_units[3].shape[1]
    unit_rows = 64 // rows
    low = jnp.bfloat16
    dma = pltpu.SemaphoreType.DMA
    buf = pltpu.VMEM((nc, height, cols), x.dtype)
    small = pltpu.VMEM((rows, unit_rows, size), low)
    vmem = pl.BlockSpec(memory_space=pltpu.VMEM)
    return pl.pallas_call(
        functools.partial(scatter_kernel, n, rows),
        out_shape=(
            jax.ShapeDtypeStruct((height, cols), jnp.float32),
            jax.ShapeDtypeStruct((rows, 2, nc, unit_rows, size), low),
        ),
        in_specs=[pl.BlockSpec(memory_space=pltpu.HBM)] + [vmem] * 4,
        out_specs=(vmem,) * 2,
        scratch_shapes=[buf] * 4 + [small] * 2 + [dma((nc,))] * 7
        + [dma((rows,))] * 2 + [dma((nc,))] * 2 + [dma((rows,))] * 4,
        compiler_params=pltpu.CompilerParams(
            collective_id=collective_id, has_side_effects=True, vmem_limit_bytes=32 << 20
        ),
        cost_estimate=pl.CostEstimate(flops=0, transcendentals=0, bytes_accessed=1 << 20),
        name="scatter_seq",
    )(*in_hbm(x), *own_units)


def reduce_kernel(n, rows, ga_qkv, ga_o, gb_qkv, gb_o, ga_gu, gb_d, gm_qkv, gm_o, gm_d,
                  whole, part, from_sib, mid, from_rows, from_line, line_out,
                  sib_out, sib_in, row_out, row_in, line_send, line_in, back_send, back_in, wide_send, wide_in,
                  pass_send, pass_in):
    nc = n // 2
    f32, low = jnp.float32, jnp.bfloat16
    s, q, c = place_in_seq()
    sibling = s + 1 - 2 * c
    r = lax.axis_index("rows")
    width = ga_o.shape[1]
    cols = width // (2 * rows)
    kv = (gb_qkv.shape[1] - width) // 2
    height = part.shape[2]
    piece = height // nc

    greet_cross(n, rows, wait=False)
    gb_k, gb_v = gb_qkv[:, width : width + kv], gb_qkv[:, width + kv :]
    small = jnp.concatenate(
        [
            jnp.concatenate([gb_k[:8], gb_k[8:], gb_v[:8], gb_v[8:]], axis=1),
            gm_qkv[:, :width],
            gm_o[...],
            gm_d[...],
            jnp.concatenate([gm_qkv[:, width:], jnp.zeros((1, width - 2 * kv), f32)], axis=1),
            jnp.zeros((4, width), f32),
        ],
        axis=0,
    )
    groups = [ga_qkv[0], ga_qkv[1], ga_qkv[2], ga_o[...], gb_qkv[:, :width], gb_o[...], ga_gu[0], ga_gu[1], gb_d[...], small]
    for j in range(2 * rows):
        for g, value in enumerate(groups):
            part[j % 2, j // 2, 16 * g : 16 * g + 16] = value[:, cols * j : cols * (j + 1)].astype(low)
        if height > 160:
            part[j % 2, j // 2, 160:] = jnp.zeros((height - 160, cols), low)
    pl.semaphore_wait(pltpu.get_barrier_semaphore(), n + rows - 2)

    def to_sibling():
        return remote(part.at[1 - c], from_sib, sib_out.at[0], sib_in.at[0], r, sibling)

    def member(t):
        return lax.rem(r + t + rows, rows)

    def row_send(t):
        return remote(mid.at[member(t)], from_rows.at[t], row_out.at[t], row_in.at[t], member(t), s)

    def chip(t):
        return lax.rem(q + t + nc, nc)

    def line_part(t):
        return remote(line_out.at[chip(t)], from_line.at[t], line_send.at[t], line_in.at[t], r, 2 * chip(t) + c)

    def back(t, slot):
        return remote(whole.at[r, c, slot], whole.at[r, c, slot], back_send.at[t], back_in.at[t], r, 2 * chip(t) + c)

    def wide(t, row):
        return remote(whole.at[row, c], whole.at[row, c], wide_send.at[t], wide_in.at[t], member(t), s)

    def hand(t, row, core):
        return remote(whole.at[row, core], whole.at[row, core], pass_send.at[t], pass_in.at[t], r, sibling)

    to_sibling().start()
    to_sibling().wait_recv()
    for t in range(rows):
        mid[member(t)] = (part[c, member(t)].astype(f32) + from_sib[member(t)].astype(f32)).astype(low)
        if t:
            row_send(t).start()
    total = mid[r].astype(f32)
    for t in range(1, rows):
        row_send(t).wait_recv()
        total = total + from_rows[t].astype(f32)
    for p in range(nc):
        line_out[p] = total[piece * p : piece * (p + 1)].astype(low)
    for t in range(1, nc):
        line_part(t).start()
    own = line_out[q].astype(f32)
    for t in range(1, nc):
        line_part(t).wait_recv()
        own = own + from_line[t].astype(f32)
    whole[r, c, q] = own.astype(low)
    for t in range(1, nc):
        back(t, q).start()
    for t in range(1, nc):
        back(t, chip(-t)).wait_recv()
    for t in range(1, rows):
        wide(t, r).start()
    hand(0, r, c).start()
    for t in range(1, rows):
        wide(t, member(-t)).wait_recv()
        hand(t, member(-t), c).start()
    for t in range(rows):
        hand(t, member(-t), 1 - c).wait_recv()

    to_sibling().wait_send()
    for t in range(1, rows):
        row_send(t).wait_send()
        wide(t, r).wait_send()
    for t in range(1, nc):
        line_part(t).wait_send()
        back(t, q).wait_send()
    for t in range(rows):
        hand(t, member(-t), c).wait_send()


def sum_gradients(n, rows, full, collective_id):
    nc = n // 2
    width = full[1].shape[1]
    cols = width // (2 * rows)
    height = -(-160 // (8 * nc)) * 8 * nc
    low = jnp.bfloat16
    vmem = pl.BlockSpec(memory_space=pltpu.VMEM)
    dma = pltpu.SemaphoreType.DMA
    block = (rows, height, cols)
    return pl.pallas_call(
        functools.partial(reduce_kernel, n, rows),
        out_shape=jax.ShapeDtypeStruct((rows, 2, nc, height // nc, cols), low),
        in_specs=[vmem] * 9,
        out_specs=vmem,
        scratch_shapes=[
            pltpu.VMEM((2, *block), low),
            pltpu.VMEM(block, low),
            pltpu.VMEM(block, low),
            pltpu.VMEM(block, low),
            pltpu.VMEM((nc, height // nc, cols), low),
            pltpu.VMEM((nc, height // nc, cols), low),
            dma((1,)), dma((1,)), dma((rows,)), dma((rows,)), dma((nc,)), dma((nc,)),
            dma((nc,)), dma((nc,)), dma((rows,)), dma((rows,)), dma((rows,)), dma((rows,)),
        ],
        compiler_params=pltpu.CompilerParams(
            collective_id=collective_id, has_side_effects=True, vmem_limit_bytes=48 << 20
        ),
        cost_estimate=pl.CostEstimate(flops=0, transcendentals=0, bytes_accessed=1 << 20),
        name="sum_gradients",
    )(*full)


def finish_kernel(n, rows, whole, units_all, x1, before_0, before_1, m_attn, n_attn, m_d, n_d, m_gu,
                  o_out, o_ga, o_gb_qo, o_gb_kv, o_gm_q, o_gm_kv, o_gm_o, o_ga_gu, o_gb_gu, o_gm_gu, o_ga_d, o_gb_d,
                  o_gm_d, o_stats, n_gu):
    f32 = jnp.float32
    nc = n // 2
    width = o_gb_d.shape[1]
    kv = o_gb_kv.shape[2]
    cols = width // (2 * rows)
    size = units_all.shape[4]
    per = units_all.shape[3] // 8
    half = x1.shape[0] // 2
    for k, before in enumerate((before_0, before_1)):
        own = slice(half * k, half * (k + 1))
        o_out[own] = (x1[own] + before[...].astype(f32) * (m_d[...] / n_d[...])).astype(o_out.dtype)
    for j in range(2 * rows):
        block = jnp.concatenate([whole[j // 2, j % 2, p].astype(f32) for p in range(nc)], axis=0)
        at = slice(cols * j, cols * (j + 1))
        for g in range(4):
            o_ga[g, :, at] = block[16 * g : 16 * g + 16]
        o_gb_qo[0, :, at] = block[64:80]
        o_gb_qo[1, :, at] = block[80:96]
        o_ga_gu[0, :, at] = block[96:112]
        o_ga_gu[1, :, at] = block[112:128]
        o_gb_d[:, at] = block[128:144]
        which, start = divmod(cols * j, kv)
        o_gb_kv[which // 2, 8 * (which % 2) : 8 * (which % 2) + 8, start : start + cols] = block[144:152]
        o_gm_q[at] = block[152]
        o_gm_o[at] = block[153]
        o_gm_d[at] = block[154]
        if which < 2:
            o_gm_kv[which : which + 1, start : start + cols] = block[155:156]
    for j in range(rows):
        for dev in range(n):
            block = units_all[j, dev % 2, dev // 2].astype(f32)
            at = slice(size * dev, size * (dev + 1))
            for t in range(per):
                rows8, place = block[8 * t : 8 * t + 8], per * j + t
                half = slice(8 * (place % 2), 8 * (place % 2) + 8)
                if place < 4:
                    o_gb_gu[place // 2, half, at] = rows8
                elif place < 6:
                    o_ga_d[half, at] = rows8
                elif place == 6:
                    o_gm_gu[:, at] = rows8[:2]
                    n_gu[0:1, at] = rows8[2:3] + rows8[3:4]
                    n_gu[1:2, at] = rows8[4:5] + rows8[5:6]


    row = lax.broadcasted_iota(jnp.int32, o_stats.shape, 0)
    col = lax.broadcasted_iota(jnp.int32, o_stats.shape, 1)
    bounds = [(0, width), (width, width + kv), (width + kv, width + 2 * kv), (width + 2 * kv, 2 * width + 2 * kv)]
    both = [(m_attn[:, i:j], n_attn[:, i:j]) for i, j in bounds]
    both += [(m_gu[g : g + 1, :], n_gu[g : g + 1, :]) for g in range(2)] + [(m_d[...], n_d[...])]
    stats = jnp.zeros(o_stats.shape, f32)
    for p, (m, norm) in enumerate(both):
        drift = jnp.mean(jnp.square(m - norm), axis=1, keepdims=True)
        drift = jnp.sqrt(drift) / jnp.sqrt(jnp.mean(jnp.square(m), axis=1, keepdims=True) + 1e-06)
        stats = jnp.where((row == 0) & (col == p), drift, stats)
        stats = jnp.where((row == 1) & (col == p), jnp.mean(norm, axis=1, keepdims=True), stats)
    o_stats[...] = stats


def finish(n, rows, sums, units, x1, before_0, before_1, m_attn, n_attn, m_d, n_d, m_gu):
    tokens, width = x1.shape
    kv = (m_attn.shape[1] - 2 * width) // 2
    wide_units = m_gu.shape[1]
    shape = lambda *dims: pltpu.HBM(dims, jnp.float32)
    vmem = pl.BlockSpec(memory_space=pltpu.VMEM)
    return pl.pallas_call(
        functools.partial(finish_kernel, n, rows),
        out_shape=(
            pltpu.HBM((tokens, width), jnp.bfloat16), shape(4, 16, width), shape(2, 16, width), shape(2, 16, kv),
            shape(width), shape(2, kv), shape(width), shape(2, 16, width), shape(2, 16, wide_units), shape(2, wide_units),
            shape(16, wide_units), shape(16, width), shape(width), shape(2, 7),
        ),
        in_specs=[vmem] * 2 + [pl.BlockSpec()] * 8,
        scratch_shapes=[pltpu.VMEM((2, wide_units), jnp.float32)],
        compiler_params=pltpu.CompilerParams(vmem_limit_bytes=40 << 20),
        cost_estimate=pl.CostEstimate(flops=0, transcendentals=0, bytes_accessed=8 << 20),
        name="finish",
    )(sums, units, *in_hbm(x1, before_0, before_1), m_attn, n_attn, m_d, n_d, m_gu)

def local(
    layer_input,
    output_gradient,
    norm_gain_vectors,
    query_output_frozen,
    key_value_frozen,
    gate_up_frozen,
    down_frozen_weight,
    attention_adapter_a,
    query_output_adapter_b,
    key_value_adapter_b,
    query_magnitude,
    key_value_magnitude,
    output_magnitude,
    gate_up_adapter_a,
    gate_up_adapter_b,
    gate_up_magnitude,
    down_adapter_a,
    down_adapter_b,
    down_magnitude,
    prompt_length_list,
    response_length_list,
):
    pair_rows, span_len, model_width = layer_input.shape
    token_count = pair_rows * span_len
    kv_width = KV_HEADS * HEAD_DIM
    seq_size = lax.axis_size("seq")
    rows_size = lax.axis_size("rows")
    seq_index = lax.axis_index("seq")
    f32 = jnp.float32

    x = layer_input.reshape(token_count, model_width)
    gain_attn, gain_ffn = norm_gain_vectors[:1], norm_gain_vectors[1:]
    weights, gu_own, gu_near, sq_d, grams, u1, inner_1 = gather_weights(
        seq_size, rows_size, query_output_frozen, key_value_frozen, gate_up_frozen,
        down_frozen_weight, down_adapter_a, down_adapter_b, x, gain_attn, attention_adapter_a,
        gate_up_adapter_a, 1,
    )
    shares_1, shares_2 = share_plan(rows_size)
    grad_out_rows = output_gradient.reshape(token_count, model_width)
    half_0, half_1 = jnp.split(grad_out_rows, 2)
    weights, half_0 = lax.optimization_barrier((weights, half_0))
    gy_0 = lax.all_gather(half_0, "seq", axis=0, tiled=False)

    b_attn = jnp.concatenate(
        [
            query_output_adapter_b[0],
            key_value_adapter_b[0],
            key_value_adapter_b[1],
            query_output_adapter_b[1],
        ],
        axis=1,
    )
    m_attn = jnp.concatenate(
        [query_magnitude, key_value_magnitude[0], key_value_magnitude[1], output_magnitude]
    )[None]
    m_d = down_magnitude[None]

    positions = seq_index * span_len + jnp.arange(span_len, dtype=jnp.int32)
    half_dim = HEAD_DIM // 2
    frequency = 500000.0 ** (-(jnp.arange(half_dim, dtype=f32) * 2.0) / HEAD_DIM)
    angles = positions.astype(f32)[:, None] * frequency[None, :]
    cosine = jnp.tile(jnp.cos(angles), (pair_rows, 4))
    sine = jnp.tile(jnp.sin(angles), (pair_rows, 4))
    valid_len = prompt_length_list[0] + response_length_list

    before_qkv, q, kv, n_attn, cross_attn = project_qkv(
        u1, inner_1, grams, attention_adapter_a, weights, b_attn, m_attn, cosine, sine
    )
    (kv_all, sq_all), gu_1 = gather_seq(
        seq_size, rows_size, [kv, sq_d], 2, (gu_own,), shares_1
    )
    kv_all, half_1 = lax.optimization_barrier((kv_all, half_1))
    gy_1 = lax.all_gather(half_1, "seq", axis=0, tiled=False)
    kv_all = kv_all.reshape(seq_size, pair_rows, span_len, 2 * kv_width)
    q = q.reshape(pair_rows, span_len, model_width)
    att, shares = attend(q, kv_all, valid_len)
    att = att.reshape(token_count, model_width)
    before_o, x1, u2, inner_2 = project_out(
        att, attention_adapter_a, weights, b_attn, m_attn, n_attn, x, gain_ffn, gate_up_adapter_a
    )

    (u2_all, inner_all), gu_2 = gather_seq(
        seq_size, rows_size, [u2, inner_2], 3, (gu_own, *gu_1), shares_2
    )
    in_grad, down_0, down_1, ga_gu, gb_gu, gm_gu, n_gu, ga_d, gb_d, gm_d, n_d = feed_forward(
        seq_size, rows_size, (gu_own, gu_near, *gu_1, *gu_2), u2_all, inner_all, gy_0, gy_1,
        down_frozen_weight, gate_up_adapter_a, gate_up_adapter_b, gate_up_magnitude, down_adapter_a,
        down_adapter_b, m_d, sq_all, grams, 4,
    )
    flat = lambda v: v.reshape(-1, model_width)
    before_0 = lax.psum_scatter(flat(down_0), "seq", scatter_dimension=0, tiled=True)

    gx1, grad_att, ga_o, gb_o, gm_o = out_back(
        in_grad, x1, gain_ffn, grad_out_rows, before_o, att, attention_adapter_a, b_attn, m_attn,
        n_attn, cross_attn, weights,
    )
    gq, gkv = attend_back(q, kv_all, shares, grad_att.reshape(q.shape))
    gkv, units = scatter_seq(
        seq_size, rows_size, gkv.reshape(seq_size, token_count, 2 * kv_width),
        (gb_gu, gm_gu, n_gu, ga_d), 5,
    )
    gkv, down_1, before_0 = lax.optimization_barrier((gkv, down_1, before_0))
    before_1 = lax.psum_scatter(flat(down_1), "seq", scatter_dimension=0, tiled=True)
    grad_inputs, ga_qkv, gb_qkv, gm_qkv = qkv_back(
        gq.reshape(token_count, model_width), gkv, cosine, sine, before_qkv, u1, inner_1,
        attention_adapter_a, b_attn, m_attn, n_attn, cross_attn, x, gain_attn, gx1, weights,
    )

    sums = sum_gradients(
        seq_size, rows_size,
        (ga_qkv, ga_o, gb_qkv, gb_o, ga_gu, gb_d, gm_qkv, gm_o, gm_d),
        6,
    )
    layer_result, *summed, stats = finish(
        seq_size, rows_size, sums, units, x1, before_0, before_1, m_attn, n_attn, m_d, n_d, gate_up_magnitude
    )
    shape = (pair_rows, span_len, model_width)
    return (layer_result.reshape(shape), grad_inputs.reshape(shape), *summed, stats.T)

def solution(mesh):
    return jax.shard_map(
        local,
        mesh=mesh,
        in_specs=(
            P("rows", "seq", None),
            P("rows", "seq", None),
            P(),
            P(None, "seq", None),
            P(None, "seq", None),
            P(None, "seq", None),
            P("seq", None),
            P(),
            P(),
            P(),
            P(),
            P(),
            P(),
            P(),
            P(),
            P(),
            P(),
            P(),
            P(),
            P("rows"),
            P("rows"),
        ),
        out_specs=(
            P("rows", "seq", None),
            P("rows", "seq", None),
            P(),
            P(),
            P(),
            P(),
            P(),
            P(),
            P(),
            P(),
            P(),
            P(),
            P(),
            P(),
            P(),
        ),
        check_vma=False,
    )
```

```python
import functools

import jax
import jax.numpy as jnp
from jax import lax
from jax.experimental import pallas as pl
from jax.experimental.pallas import tpu as pltpu
from jax.sharding import PartitionSpec as P

HEADS = 32
KV_HEADS = 8
HEAD_DIM = 64
ADAPTER_RANK = 16
ALPHA = 32
SCALE = ALPHA / ADAPTER_RANK
TILE = 512

highest = lax.Precision.HIGHEST
last_last = (((1,), (1,)), ((), ()))
first_first = (((0,), (0,)), ((), ()))

def dot_f32(a, b):
    return jnp.dot(a, b, preferred_element_type=jnp.float32)


def dot_nt(a, b):
    return lax.dot_general(a, b, last_last, preferred_element_type=jnp.float32)


def dot_tn(a, b):
    return lax.dot_general(a, b, first_first, preferred_element_type=jnp.float32)


def in_hbm(*arrays):
    return [pltpu.with_memory_space_constraint(v, pltpu.HBM) for v in arrays]


def unit_rms(v):
    return lax.rsqrt(jnp.mean(v * v, axis=-1, keepdims=True) + 1e-05)


def rms_back(v, gain, upstream):
    r = unit_rms(v)
    scaled = gain * upstream
    return r * scaled - v * (r * r * r) * jnp.mean(scaled * v, axis=-1, keepdims=True)


def turn(z, cosine, sine):
    width = z.shape[1]
    lane = lax.broadcasted_iota(jnp.int32, z.shape, 1)
    half = HEAD_DIM // 2
    other = jnp.where(
        lax.rem(lane, HEAD_DIM) < half, -pltpu.roll(z, width - half, 1), pltpu.roll(z, half, 1)
    )
    copies = width // cosine.shape[1]
    return z * jnp.tile(cosine, (1, copies)) + other * jnp.tile(sine, (1, copies))


def column_squares(w):
    return jnp.sum(jnp.square(w.astype(jnp.float32)), axis=0, keepdims=True)


def two_terms(value):
    high = value.astype(jnp.bfloat16)
    return jnp.concatenate([high, (value - high.astype(jnp.float32)).astype(jnp.bfloat16)], axis=0)


def dot_two(terms, b):
    both = dot_f32(terms, b)
    half = both.shape[0] // 2
    return both[:half] + both[half:]


def column_norms(w, gram, b, cross):
    b_wide = b.astype(jnp.float32)
    gram_b = dot_two(gram, b)
    squares = column_squares(w) + 2.0 * SCALE * jnp.sum(b_wide * cross, axis=0, keepdims=True)
    squares = squares + SCALE * SCALE * jnp.sum(b_wide * gram_b, axis=0, keepdims=True)
    return jnp.sqrt(squares + 1e-06), cross + SCALE * gram_b


def project_kernel(n, rows, plan, k_tiles, q_tiles, u_ref, inner_ref, gram_ref, a_ref, w_ref, b_ref, m_ref, cos_ref,
                   sin_ref, sq_ref, held, before_ref, q_ref, n_ref, cross_ref, kv_all, sq_all, *refs):
    swapped = refs[: len(plan)]
    kv_ref, keep_sem, to_sib, to_left, to_right, recv, share_out, share_in = refs[len(plan) :]
    j = pl.program_id(0)
    last = pl.num_programs(0) - 1
    nc = n // 2
    s, q, c = place_in_seq()
    sibling = s + 1 - 2 * c
    r, b_row, a_row, _ = place_in_rows(rows)
    order = [near_first(i, q, nc) for i in range(nc)]
    sources, outs = (kv_ref, sq_ref), (kv_all, sq_all)

    def copy(k, src, slot, sems, target):
        return remote(src, outs[k].at[slot], sems.at[k, slot], recv.at[k, slot], r, target)

    def share(i, chip):
        _, piece, turn = plan[i]
        pair = pl.ds(2 * chip, 2)
        target = b_row if turn == 0 else a_row(turn)
        return remote(
            held.at[piece, pair], swapped[i].at[pair], share_out.at[i, chip], share_in.at[i, chip], target, s
        )

    def keep(k):
        return pltpu.make_async_copy(sources[k], outs[k].at[s], keep_sem.at[k])

    @pl.when(j == 0)
    def _():
        greet_all(n, rows)
        for chip in order[1:]:
            for i in range(len(plan)):
                share(i, chip).start()

    a = a_ref[0].astype(jnp.bfloat16)
    b = b_ref[...].astype(jnp.bfloat16)
    w = w_ref[0]
    height = u_ref.shape[0]

    @pl.when(j < 2 * k_tiles + q_tiles)
    def _():
        both = dot_f32(jnp.concatenate([u_ref[...], a], axis=0), w)
        norm, cross = column_norms(w, gram_ref[0], b, both[height:])
        n_ref[...] = norm
        cross_ref[...] = cross
        before = both[:height] + SCALE * dot_f32(inner_ref[0], b)
        before_ref[...] = before
        y = before * (m_ref[...] / norm)

        @pl.when(j >= 2 * k_tiles)
        def _():
            q_ref[...] = turn(y, cos_ref[...], sin_ref[...]).astype(jnp.bfloat16)

        for t in range(2 * k_tiles):

            @pl.when(j == t)
            def _(t=t):
                z = turn(y, cos_ref[...], sin_ref[...]) if t < k_tiles else y
                kv_ref[:, TILE * t : TILE * (t + 1)] = z.astype(jnp.bfloat16)

    @pl.when(j >= 2 * k_tiles + q_tiles)
    def _():
        norm, cross = column_norms(w, gram_ref[0], b, dot_f32(a, w))
        n_ref[...] = norm
        cross_ref[...] = cross

    @pl.when(j == 2 * k_tiles - 1)
    def _():
        for k in range(2):
            pl.when(q > 0)(lambda k=k: copy(k, sources[k], s, to_left, s - 2).start())
            pl.when(q < nc - 1)(lambda k=k: copy(k, sources[k], s, to_right, s + 2).start())
            copy(k, sources[k], s, to_sib, sibling).start()
            keep(k).start()

    def pass_on(chip):
        slot = 2 * chip + c
        for k in range(2):
            src = outs[k].at[slot]
            copy(k, src, slot, to_right, s).wait_recv()
            pl.when((chip < q) & (q < nc - 1))(
                lambda k=k, src=src: copy(k, src, slot, to_right, s + 2).start()
            )
            pl.when((chip > q) & (q > 0))(
                lambda k=k, src=src: copy(k, src, slot, to_left, s - 2).start()
            )
            copy(k, src, slot, to_sib, sibling).start()

    for i in range(1, nc):
        at = min(2 * k_tiles + 2 * i, 2 * k_tiles + 2 * q_tiles - 1)
        pl.when(j == at)(lambda i=i: pass_on(order[i]))

    @pl.when(j == last)
    def _():
        for k in range(2):
            keep(k).wait()
            for chip in range(nc):
                mine, theirs = 2 * chip + c, 2 * chip + 1 - c
                copy(k, outs[k].at[theirs], theirs, to_sib, sibling).wait_recv()
                copy(k, outs[k].at[mine], mine, to_sib, sibling).wait_send()
                pl.when((q < nc - 1) & (chip <= q))(
                    lambda k=k, mine=mine: copy(k, outs[k].at[mine], mine, to_right, s).wait_send()
                )
                pl.when((q > 0) & (chip >= q))(
                    lambda k=k, mine=mine: copy(k, outs[k].at[mine], mine, to_left, s).wait_send()
                )
        for chip in order[1:]:
            for i in range(len(plan)):
                share(i, chip).wait_send()
                share(i, chip).wait_recv()


def project_qkv(n, rows, u, inner, grams, a, weights, b, m, cosine, sine, sq, held, plan, collective_id):
    tokens, width = u.shape
    cols = b.shape[1]
    nc = n // 2
    per_half = weights.shape[2] // TILE
    q_tiles = width // TILE
    k_cols = weights.shape[2] - width
    k_tiles = k_cols // TILE
    kv_tiles = 2 * k_tiles
    full = lambda shape: pl.BlockSpec(shape, lambda j: (0,) * len(shape))

    def column(j):
        return jnp.where(j < kv_tiles, q_tiles + j, jnp.where(j < kv_tiles + q_tiles, j - kv_tiles, j))

    def which(j):
        return jnp.where(
            j < k_tiles, 1, jnp.where(j < kv_tiles, 2, jnp.where(j < kv_tiles + q_tiles, 0, 3))
        )

    def before_tile(j):
        return (0, column(jnp.minimum(j, kv_tiles + q_tiles - 1)))

    col = lambda height: pl.BlockSpec((height, TILE), lambda j: (0, column(j)))
    f32, low = jnp.float32, jnp.bfloat16
    hbm = pl.BlockSpec(memory_space=pltpu.HBM)
    dma = pltpu.SemaphoreType.DMA
    got = pl.pallas_call(
        functools.partial(project_kernel, n, rows, plan, k_tiles, q_tiles),
        out_shape=(
            pltpu.HBM((tokens, width + 2 * k_cols), f32),
            pltpu.HBM((tokens, width), low),
            pltpu.HBM((1, cols), f32),
            pltpu.HBM((16, cols), f32),
            pltpu.HBM((n, tokens, 2 * k_cols), low),
            pltpu.HBM((n, *sq.shape), f32),
            *(pltpu.HBM(held.shape[-3:], low) for _ in plan),
        ),
        grid=(cols // TILE,),
        in_specs=[
            full((tokens, width)),
            pl.BlockSpec((1, tokens, 16), lambda j: (jnp.minimum(which(j), 2), 0, 0)),
            pl.BlockSpec((1, 32, 16), lambda j: (which(j), 0, 0)),
            pl.BlockSpec((1, 16, width), lambda j: (which(j), 0, 0)),
            pl.BlockSpec((1, width, TILE), lambda j: (column(j) // per_half, 0, lax.rem(column(j), per_half))),
            col(16),
            col(1),
            full(cosine.shape),
            full(sine.shape),
            hbm,
            hbm,
        ],
        out_specs=(
            pl.BlockSpec((tokens, TILE), before_tile),
            pl.BlockSpec((tokens, TILE), lambda j: (0, jnp.clip(j - kv_tiles, 0, q_tiles - 1))),
            col(1),
            col(16),
            *([hbm] * (2 + len(plan))),
        ),
        scratch_shapes=[pltpu.VMEM((tokens, 2 * k_cols), low), dma((2,))]
        + [dma((2, n))] * 4
        + [dma((len(plan), nc))] * 2,
        compiler_params=pltpu.CompilerParams(
            collective_id=collective_id, has_side_effects=True, vmem_limit_bytes=40 << 20
        ),
        cost_estimate=pl.CostEstimate(
            flops=2 * tokens * width * cols, transcendentals=0, bytes_accessed=64 << 20
        ),
        name="project_qkv",
    )(*in_hbm(u), inner, grams, *in_hbm(a, weights, b), m, cosine, sine, *in_hbm(sq, held))
    return (*got[:6], got[6:])


def out_kernel(att_ref, a_ref, w_ref, b_ref, m_ref, n_ref, x_ref, gain_ref, next_ref,
               before_ref, x1_ref, u2_ref, inner_ref):
    t = pl.program_id(0)
    a = a_ref[0].astype(jnp.bfloat16)
    b = b_ref[...].astype(jnp.bfloat16)
    inner = dot_nt(att_ref[...], a).astype(jnp.bfloat16)
    before = dot_f32(att_ref[...], w_ref[0]) + SCALE * dot_f32(inner, b)
    before_ref[...] = before
    x1_ref[:, pl.ds(pl.multiple_of(t * TILE, TILE), TILE)] = (
        x_ref[...].astype(jnp.float32) + before * (m_ref[...] / n_ref[...])
    )

    @pl.when(t == pl.num_programs(0) - 1)
    def _():
        v = x1_ref[...]
        u2 = (v * unit_rms(v) * gain_ref[1:]).astype(jnp.bfloat16)
        u2_ref[...] = u2
        following = next_ref[...].reshape(-1, u2.shape[1]).astype(jnp.bfloat16)
        inner_ref[...] = jnp.zeros_like(inner_ref)
        inner_ref[:, : following.shape[0]] = dot_nt(u2, following).astype(jnp.bfloat16)


def project_out(att, a, weights, b, m, norms, x, gain, following):
    rows, width = att.shape
    tiles = width // TILE
    skip = (weights.shape[2] - width) // TILE
    full = lambda shape: pl.BlockSpec(shape, lambda t: (0,) * len(shape))
    col = lambda height: pl.BlockSpec((height, TILE), lambda t: (0, t))
    ahead = b.shape[1] // TILE - tiles
    later = lambda height: pl.BlockSpec((height, TILE), lambda t: (0, ahead + t))
    f32 = jnp.float32
    return pl.pallas_call(
        out_kernel,
        out_shape=(
            pltpu.HBM((rows, width), f32),
            pltpu.HBM((rows, width), f32),
            pltpu.HBM((rows, width), jnp.bfloat16),
            pltpu.HBM((rows, 128), jnp.bfloat16),
        ),
        grid=(tiles,),
        in_specs=[
            full((rows, width)),
            pl.BlockSpec((1, 16, width), lambda t: (3, 0, 0)),
            pl.BlockSpec((1, width, TILE), lambda t: (1, 0, skip + t)),
            later(16),
            later(1),
            later(1),
            col(rows),
            full((2, width)),
            full(following.shape),
        ],
        out_specs=(col(rows), full((rows, width)), full((rows, width)), full((rows, 128))),
        compiler_params=pltpu.CompilerParams(vmem_limit_bytes=40 << 20),
        cost_estimate=pl.CostEstimate(
            flops=2 * rows * width * width, transcendentals=0, bytes_accessed=2 * width * width
        ),
        name="project_out",
    )(*in_hbm(att, a, weights, b), m, norms, *in_hbm(x), gain, *in_hbm(following))


def out_back_kernel(in_ref, x1_ref, gain_ref, gy_ref, before_ref, att_ref, a_ref, b_ref, m_ref, n_ref, cross_ref,
                    w_ref, gx_ref, gatt_ref, ga_ref, gb_ref, gm_ref, lhs, gi, tail):
    t = pl.program_id(0)
    rows, width = gx_ref.shape
    low = jnp.bfloat16
    a = a_ref[0].astype(low)
    o_cols = slice(b_ref.shape[1] - width, b_ref.shape[1])

    @pl.when(t == 0)
    def _():
        gx = gy_ref[...].astype(jnp.float32) + rms_back(x1_ref[...], gain_ref[1:], in_ref[...])
        gx_ref[...] = gx
        norm, m = n_ref[:, o_cols], m_ref[:, o_cols]
        gb = (gx * (m / norm)).astype(low)
        lhs[:rows] = gb
        b = b_ref[:, o_cols].astype(low)
        gi[...] = (SCALE * dot_nt(gb, b)).astype(low)
        gm = jnp.sum(gx * before_ref[...], axis=0, keepdims=True) / norm
        gm_ref[...] = gm
        c = -gm * m / (norm * norm)
        weighted = (b.astype(jnp.float32) * c).astype(low)
        lhs[rows:] = weighted
        tail[...] = two_terms(dot_nt(weighted, b))
        inner = dot_nt(att_ref[...], a).astype(low)
        gb_ref[...] = SCALE * dot_tn(inner, gb) + SCALE * c * cross_ref[:, o_cols]

    span = pl.ds(pl.multiple_of(t * TILE, TILE), TILE)
    a_tile = a_ref[0, :, span].astype(low)
    gi_low = gi[...]
    back = dot_nt(lhs[...], w_ref[0, :, w_ref.shape[2] - width :])
    gatt_ref[...] = (back[:rows] + dot_f32(gi_low, a_tile)).astype(low)
    spread = back[rows:] + SCALE * dot_two(tail[...], a_tile)
    ga_ref[...] = dot_tn(gi_low, att_ref[:, span]) + SCALE * spread


def out_back(in_grad, x1, gain, gy, before, att, a, b, m, norms, cross, weights):
    rows, width = x1.shape
    tiles = width // TILE
    full = lambda shape: pl.BlockSpec(shape, lambda t: (0,) * len(shape))
    col = lambda height: pl.BlockSpec((height, TILE), lambda t: (0, t))
    f32, low = jnp.float32, jnp.bfloat16
    wide = full((rows, width))
    return pl.pallas_call(
        out_back_kernel,
        out_shape=(
            pltpu.HBM((rows, width), f32),
            pltpu.HBM((rows, width), low),
            jax.ShapeDtypeStruct((16, width), f32),
            jax.ShapeDtypeStruct((16, width), f32),
            jax.ShapeDtypeStruct((1, width), f32),
        ),
        grid=(tiles,),
        in_specs=[wide, wide, full((2, width)), wide, wide, wide,
                  pl.BlockSpec((1, 16, width), lambda t: (3, 0, 0)),
                  full(b.shape), full(m.shape), full(norms.shape), full(cross.shape),
                  pl.BlockSpec((1, TILE, weights.shape[2]), lambda t: (1, t, 0))],
        out_specs=(wide, col(rows), col(16), full((16, width)), full((1, width))),
        scratch_shapes=[
            pltpu.VMEM((rows + 16, width), low),
            pltpu.VMEM((rows, 16), low),
            pltpu.VMEM((32, 16), low),
        ],
        compiler_params=pltpu.CompilerParams(vmem_limit_bytes=48 << 20),
        cost_estimate=pl.CostEstimate(flops=0, transcendentals=0, bytes_accessed=1 << 20),
        name="out_back",
    )(*in_hbm(in_grad, x1), gain, *in_hbm(gy, before, att, a, b), m, norms, *in_hbm(cross, weights))


def qkv_back_kernel(gq_ref, gkv_ref, cos_ref, sin_ref, before_ref, u_ref, inner_ref, a_ref, b_ref, m_ref, n_ref, cross_ref,
                    x_ref, gain_ref, gx_ref, w0_ref, w1_ref,
                    out_ref, ga_ref, gb_ref, gm_ref, lhs0, lhs1, gi, tail):
    t = pl.program_id(0)
    rows, width = gx_ref.shape
    low = jnp.bfloat16
    k_cols = w1_ref.shape[2]
    bounds = [(0, width), (width, width + k_cols), (width + k_cols, width + 2 * k_cols)]

    @pl.when(t == 0)
    def _():
        cosine, sine = cos_ref[...], -sin_ref[...]
        k_parts = [gkv_ref[:, 256 * j : 256 * j + 128] for j in range(k_cols // 128)]
        v_parts = [gkv_ref[:, 256 * j + 128 : 256 * j + 256] for j in range(k_cols // 128)]
        rounded = lambda z: z.astype(low).astype(jnp.float32)
        ups = [
            turn(gq_ref[...].astype(jnp.float32), cosine, sine),
            turn(rounded(jnp.concatenate(k_parts, axis=1)), cosine, sine),
            rounded(jnp.concatenate(v_parts, axis=1)),
        ]
        lhs0[rows:] = jnp.zeros_like(lhs0[rows:])
        lhs1[rows:] = jnp.zeros_like(lhs1[rows:])
        for p, (start, stop) in enumerate(bounds):
            g, norm, m = ups[p], n_ref[:, start:stop], m_ref[:, start:stop]
            b = b_ref[:, start:stop].astype(low)
            gb = (g * (m / norm)).astype(low)
            gm = jnp.sum(g * before_ref[:, start:stop], axis=0, keepdims=True) / norm
            gm_ref[:, start:stop] = gm
            c = -gm * m / (norm * norm)
            weighted = (b.astype(jnp.float32) * c).astype(low)
            gi[:, 16 * p : 16 * p + 16] = (SCALE * dot_nt(gb, b)).astype(low)
            tail[p] = two_terms(dot_nt(weighted, b))
            gb_ref[:, start:stop] = SCALE * dot_tn(inner_ref[p], gb) + SCALE * c * cross_ref[:, start:stop]
            lhs, at = (lhs1, 0) if p == 2 else (lhs0, start)
            lhs[:rows, at : at + stop - start] = gb
            lhs[rows + 16 * p : rows + 16 * p + 16, at : at + stop - start] = weighted

    span = pl.ds(pl.multiple_of(t * TILE, TILE), TILE)
    back = dot_nt(lhs0[...], w0_ref[0]) + dot_nt(lhs1[...], w1_ref[0])
    grad_in = back[:rows]
    for p in range(3):
        a_tile = a_ref[p, :, span].astype(low)
        gi_p = gi[:, 16 * p : 16 * p + 16]
        grad_in = grad_in + dot_f32(gi_p, a_tile)
        spread = back[rows + 16 * p : rows + 16 * p + 16] + SCALE * dot_two(tail[p], a_tile)
        ga_ref[p] = dot_tn(gi_p, u_ref[:, span]) + SCALE * spread
    out_ref[:, span] = grad_in

    @pl.when(t == pl.num_programs(0) - 1)
    def _():
        v = x_ref[...].astype(jnp.float32)
        out_ref[...] = gx_ref[...] + rms_back(v, gain_ref[:1], out_ref[...])


def qkv_back(gq, gkv, cosine, sine, before, u, inner, a, b, m, norms, cross, x, gain, gx, weights):
    rows, width = gx.shape
    cols = before.shape[1]
    k_cols = (cols - width) // 2
    tiles = width // TILE
    full = lambda shape: pl.BlockSpec(shape, lambda t: (0,) * len(shape))
    f32, low = jnp.float32, jnp.bfloat16
    wide = full((rows, width))
    return pl.pallas_call(
        qkv_back_kernel,
        out_shape=(
            pltpu.HBM((rows, width), f32),
            jax.ShapeDtypeStruct((3, 16, width), f32),
            jax.ShapeDtypeStruct((16, cols), f32),
            jax.ShapeDtypeStruct((1, cols), f32),
        ),
        grid=(tiles,),
        in_specs=[wide, full(gkv.shape), full(cosine.shape), full(sine.shape), full((rows, cols)), wide, full(inner.shape),
                  full(a.shape), full(b.shape), full(m.shape), full(norms.shape), full(cross.shape),
                  wide, full((2, width)), wide,
                  pl.BlockSpec((1, TILE, width + k_cols), lambda t: (0, t, 0)),
                  pl.BlockSpec((1, TILE, k_cols), lambda t: (1, t, 0))],
        out_specs=(wide, pl.BlockSpec((3, 16, TILE), lambda t: (0, 0, t)), full((16, cols)), full((1, cols))),
        scratch_shapes=[
            pltpu.VMEM((rows + 48, width + k_cols), low),
            pltpu.VMEM((rows + 48, k_cols), low),
            pltpu.VMEM((rows, 48), low),
            pltpu.VMEM((3, 32, 16), low),
        ],
        compiler_params=pltpu.CompilerParams(vmem_limit_bytes=48 << 20),
        cost_estimate=pl.CostEstimate(flops=0, transcendentals=0, bytes_accessed=1 << 20),
        name="qkv_back",
    )(*in_hbm(gq), gkv, cosine, sine, *in_hbm(before, u), inner, *in_hbm(a, b), m, norms, *in_hbm(cross, x), gain,
      *in_hbm(gx, weights, weights))

MESH = pl.DeviceIdType.MESH


def place_in_seq():
    s = lax.axis_index("seq")
    return s, s // 2, lax.rem(s, 2)

def near_first(i, q, nc):
    short = jnp.where(q <= nc - 1 - q, q, nc - 1 - q)
    far = jnp.where(q <= nc - 1 - q, i, nc - 1 - i)
    step = (i + 1) // 2
    near = q - step if i % 2 else q + step
    return jnp.where(i <= 2 * short, near, far)


def place_in_rows(rows):
    half = rows // 2
    r = lax.axis_index("rows")
    a, b = r // 2, lax.rem(r, 2)
    turned = lambda k: 2 * lax.rem(a + k + half, half)
    return r, 2 * a + 1 - b, lambda k: turned(k) + b, lambda k: turned(k) + 1 - b


def greet_all(n, rows):
    s = lax.axis_index("seq")
    r, b_row, a_row, _ = place_in_rows(rows)
    barrier = pltpu.get_barrier_semaphore()
    for t in range(1, n):
        pl.semaphore_signal(
            barrier, inc=1, device_id=(r, lax.rem(s + t, n)), device_id_type=MESH
        )
    pl.semaphore_signal(barrier, inc=1, device_id=(b_row, s), device_id_type=MESH)
    for k in range(1, rows // 2):
        pl.semaphore_signal(barrier, inc=1, device_id=(a_row(k), s), device_id_type=MESH)
    pl.semaphore_wait(barrier, n - 1 + rows // 2)


def remote(src, dst, send, recv, row, seq):
    return pltpu.make_async_remote_copy(
        src_ref=src, dst_ref=dst, send_sem=send, recv_sem=recv,
        device_id=(row, seq), device_id_type=MESH,
    )


def weights_kernel(n, rows, qo, kv, xg, wd_hbm, ad_hbm, bd_hbm, x_hbm, gain_ref, aa_hbm, ag_hbm, gy_hbm,
                   wa, gz, near, sq_ref, gram_ref, u_hbm, inner_ref, gy0_hbm, gy1_hbm,
                   wd, ad_ref, bd_ref, x_ref, aa_ref, ag_ref, gy_ref, own_ref, cols_ref, local, edge, a_in, a_sib_in, a_out, a_sib_out, z_in, z_out):
    nc, half = n // 2, rows // 2
    others = half - 1
    units = gz.shape[-1]
    s, q, c = place_in_seq()
    sibling = s + 1 - 2 * c
    r, b_row, a_row, diagonal = place_in_rows(rows)
    greet_all(n, rows)

    both, first, second = pl.ds(0, 2), pl.ds(0, 1), pl.ds(1, 1)
    LINE, FROM_B = 0, 1

    def from_a(k):
        return 1 + k

    def relay_b(k):
        return 1 + others + k

    def relay_a(k):
        return 1 + 2 * others + k

    def a_view(p, core, parts, row):
        return wa.at[parts, 2 * p + core, row]

    def content(kind):
        if kind == LINE:
            return both, r
        if kind == FROM_B:
            return both, b_row
        for k in range(1, half):
            if kind == from_a(k):
                return both, a_row(-k)
            if kind == relay_b(k):
                return second, diagonal(-k)
            if kind == relay_a(k):
                return first, diagonal(-k)

    kinds = 2 + 3 * others

    def a_send(p, parts, row, kind, target_row):
        return remote(
            a_view(p, c, parts, row), a_view(p, c, parts, row),
            a_out.at[p, kind], a_in.at[p, kind], target_row, s,
        )

    def a_arrival(p, kind):
        parts, row = content(kind)
        return a_send(p, parts, row, kind, r)

    def a_to_sibling(p, kind, core):
        parts, row = content(kind)
        return remote(
            a_view(p, core, parts, row), a_view(p, core, parts, row),
            a_sib_out.at[p, kind], a_sib_in.at[p, kind], r, sibling,
        )

    def columns(device):
        return pl.ds(pl.multiple_of(device * units, units), units)

    def z_send(p, core):
        return remote(
            xg.at[:, r, :, columns(2 * p + core)], gz.at[:, s],
            z_out.at[p, core], z_in.at[q, c], r, 2 * p + core,
        )

    def z_arrival(p, core):
        slot = gz.at[:, 2 * p + core]
        return remote(slot, slot, z_out.at[p, core], z_in.at[p, core], r, s)

    def line_send(p, sem, target):
        view = a_view(p, c, both, r)
        return remote(view, view, sem, a_in.at[p, LINE], r, target)

    wide, k_cols = qo.shape[-1], kv.shape[-1]
    blocks = [(qo, 0, 0), (kv, 0, wide), (kv, 1, 0), (qo, 1, k_cols)]

    def own_blocks(part, out):
        for source, i, start in blocks:
            columns_of = pl.ds(start, source.shape[-1])
            out(source.at[i, part], i, columns_of)

    def own_line(sem, target):
        own_blocks(
            r,
            lambda src, i, cols: remote(
                src, wa.at[i, s, r, :, cols], sem, a_in.at[q, LINE], r, target
            ).start(),
        )

    pl.when(q > 0)(lambda: own_line(edge.at[0], s - 2))
    pl.when(q < nc - 1)(lambda: own_line(edge.at[1], s + 2))
    order = [near_first(i, q, nc) for i in range(nc)]
    whole_block = wa.at[:, s]
    sib_a = lambda: remote(whole_block, whole_block, edge.at[2], edge.at[3], r, sibling)
    sib_g = lambda: remote(
        xg.at[:, :, :, columns(sibling)], near.at[:, c], edge.at[4], edge.at[5], r, sibling
    )
    keep_a = pltpu.make_async_copy(own_ref, whole_block, local.at[0])
    keep_g = pltpu.make_async_copy(cols_ref, near.at[:, c], local.at[1])
    all_parts = pl.ds(0, rows)
    own_blocks(
        all_parts,
        lambda src, i, cols: remote(
            src, wa.at[i, s, :, :, cols], edge.at[2], edge.at[3], r, sibling
        ).start(),
    )
    own_blocks(
        all_parts,
        lambda src, i, cols: pltpu.make_async_copy(
            src, own_ref.at[i, :, :, cols], local.at[12]
        ).start(),
    )
    take_cols = pltpu.make_async_copy(xg.at[:, :, :, columns(s)], cols_ref, local.at[13])
    take_cols.start()
    takes = [
        pltpu.make_async_copy(src, dst, local.at[5 + i])
        for i, (src, dst) in enumerate(
            [(x_hbm, x_ref), (aa_hbm, aa_ref), (ag_hbm, ag_ref), (ad_hbm, ad_ref), (bd_hbm, bd_ref), (wd_hbm, wd),
             (gy_hbm, gy_ref)]
        )
    ]
    for cp in takes:
        cp.start()
    for cp in takes:
        cp.wait()
    pltpu.make_async_copy(own_ref, own_ref, local.at[12]).wait()
    keep_a.start()
    take_cols.wait()
    keep_g.start()
    low = jnp.bfloat16
    v = x_ref[...].astype(jnp.float32)
    u = (v * unit_rms(v) * gain_ref[:1]).astype(low)
    x_ref[...] = u
    keep_u = pltpu.make_async_copy(x_ref, u_hbm, local.at[2])
    keep_u.start()
    tokens = x_ref.shape[0] // 2
    halves = [
        pltpu.make_async_copy(gy_ref.at[pl.ds(tokens * k, tokens)], out, local.at[3 + k])
        for k, out in enumerate((gy0_hbm, gy1_hbm))
    ]
    for cp in halves:
        cp.start()
    for g in range(4):
        a = aa_ref[g].astype(low)
        gram_ref[g] = two_terms(dot_nt(a, a))
        if g < 3:
            inner_ref[g] = dot_nt(u, a).astype(low)
    for g in range(2):
        a = ag_ref[g].astype(low)
        gram_ref[4 + g] = two_terms(dot_nt(a, a))

    def down_squares():
        a = ad_ref[...].astype(low)
        gram_ref[6] = two_terms(dot_nt(a, a))
        mine = pl.ds(pl.multiple_of(s * wd.shape[0], wd.shape[0]), wd.shape[0])
        cross = dot_f32(ad_ref[:, mine].astype(low), wd[...])
        b_wide = bd_ref[...].astype(low).astype(jnp.float32)
        sq_ref[...] = column_squares(wd[...]) + 2.0 * SCALE * jnp.sum(b_wide * cross, axis=0, keepdims=True)

    for p in order[1:]:
        a_arrival(p, LINE).wait_recv()
        pl.when((p < q) & (q < nc - 1))(
            lambda p=p: line_send(p, a_out.at[p, LINE], s + 2).start()
        )
        pl.when((p > q) & (q > 0))(
            lambda p=p: line_send(p, a_out.at[p, LINE], s - 2).start()
        )
        a_send(p, both, r, FROM_B, b_row).start()
        for k in range(1, half):
            a_send(p, both, r, from_a(k), a_row(k)).start()
        a_to_sibling(p, LINE, c).start()
    for p in order[1:]:
        for core in range(2):
            z_send(p, core).start()
    sib_g().start()
    down_squares()
    keep_u.wait()
    for cp in halves:
        cp.wait()
    for p in order[1:]:
        a_arrival(p, FROM_B).wait_recv()
        for k in range(1, half):
            a_send(p, first, b_row, relay_a(k), a_row(k)).start()
        a_to_sibling(p, FROM_B, c).start()
        for k in range(1, half):
            a_arrival(p, from_a(k)).wait_recv()
            a_send(p, second, a_row(-k), relay_b(k), b_row).start()
            a_to_sibling(p, from_a(k), c).start()
    for p in order[1:]:
        for k in range(1, half):
            for kind in (relay_b(k), relay_a(k)):
                a_arrival(p, kind).wait_recv()
                a_to_sibling(p, kind, c).start()
    keep_a.wait()
    keep_g.wait()
    sib_a().wait()
    sib_g().wait()
    pl.when(q > 0)(lambda: line_send(q, edge.at[0], s).wait_send())
    pl.when(q < nc - 1)(lambda: line_send(q, edge.at[1], s).wait_send())
    for p in order[1:]:
        pl.when(((p < q) & (q < nc - 1)) | ((p > q) & (q > 0)))(
            lambda p=p: line_send(p, a_out.at[p, LINE], s).wait_send()
        )
        for kind in range(kinds):
            a_to_sibling(p, kind, c).wait_send()
            a_to_sibling(p, kind, 1 - c).wait_recv()
        a_send(p, both, r, FROM_B, b_row).wait_send()
        for k in range(1, half):
            a_send(p, both, r, from_a(k), r).wait_send()
            a_send(p, first, b_row, relay_a(k), r).wait_send()
            a_send(p, second, a_row(-k), relay_b(k), r).wait_send()
        for core in range(2):
            z_send(p, core).wait_send()
            z_arrival(p, core).wait_recv()


def gather_weights(n, rows, qo, kv, xg, wd, ad, bd, x, gains, aa, ag, gy, collective_id):
    nc = n // 2
    _, block, width = qo.shape
    part = block // rows
    cols = width + kv.shape[2]
    qo = qo.reshape(2, rows, part, width)
    kv = kv.reshape(2, rows, part, kv.shape[2])
    xg = xg.reshape(2, rows, part, xg.shape[2])
    units = xg.shape[3] // n
    kinds = 2 + 3 * (rows // 2 - 1)
    dma = pltpu.SemaphoreType.DMA
    anywhere = pl.BlockSpec(memory_space=pltpu.HBM)
    vmem = pl.BlockSpec(memory_space=pltpu.VMEM)
    low = qo.dtype
    wa, gz, near, sq, grams, u, inner, *halves = pl.pallas_call(
        functools.partial(weights_kernel, n, rows),
        out_shape=(
            pltpu.HBM((2, n, rows, part, cols), low),
            pltpu.HBM((2, n, part, units), low),
            pltpu.HBM((2, 2, rows, part, units), low),
            jax.ShapeDtypeStruct((1, width), jnp.float32),
            jax.ShapeDtypeStruct((7, 32, 16), low),
            pltpu.HBM(x.shape, low),
            jax.ShapeDtypeStruct((3, x.shape[0], 16), low),
            *([pltpu.HBM((gy.shape[0] // 2, width), low)] * 2),
        ),
        in_specs=[anywhere] * 7 + [vmem] + [anywhere] * 3,
        out_specs=(anywhere,) * 3 + (vmem,) * 2 + (anywhere, vmem) + (anywhere,) * 2,
        scratch_shapes=[pltpu.VMEM(v.shape, v.dtype) for v in (wd, ad, bd, x, aa, ag, gy)]
        + [pltpu.VMEM((2, rows, part, cols), low), pltpu.VMEM((2, rows, part, units), low)]
        + [dma((14,)), dma((6,))]
        + [dma((nc, kinds))] * 4
        + [dma((nc, 2))] * 2,
        compiler_params=pltpu.CompilerParams(
            collective_id=collective_id, has_side_effects=True, vmem_limit_bytes=32 << 20
        ),
        cost_estimate=pl.CostEstimate(
            flops=0, transcendentals=0, bytes_accessed=250 * 1024 * 1024
        ),
        name="gather_weights",
    )(*in_hbm(qo, kv, xg, wd, ad, bd, x), gains, *in_hbm(aa, ag, gy))
    return wa.reshape(2, n * block, cols), gz, near, sq, grams, u, inner, halves


def gather_kernel(n, rows, count, shared, *refs):
    nc = n // 2
    sources = refs[: count + len(shared[0])]
    outs = refs[len(sources) : 2 * len(sources) - len(shared[0]) + len(shared[1])]
    scratch = refs[len(sources) + len(outs) :]
    held_here = scratch[:count]
    local_sem, to_sib, to_left, to_right, recv, share_out, share_in = scratch[count:]
    xs, held, swapped = sources[:count], sources[count:], outs[count:]
    s, q, c = place_in_seq()
    sibling = s + 1 - 2 * c
    r, b_row, a_row, _ = place_in_rows(rows)
    greet_all(n, rows)
    takes = [pltpu.make_async_copy(xs[k], held_here[k], local_sem.at[0, k]) for k in range(count)]
    keeps = [
        pltpu.make_async_copy(held_here[k], outs[k].at[s], local_sem.at[1, k]) for k in range(count)
    ]
    for cp in takes:
        cp.start()

    def copy(k, src, slot, sems, target):
        return remote(src, outs[k].at[slot], sems.at[k, slot], recv.at[k, slot], r, target)

    def share(i, p):
        source, piece, turn, _ = shared[1][i]
        pair = pl.ds(2 * p, 2)
        src = held[source].at[pair] if piece is None else held[source].at[piece, pair]
        target = b_row if turn == 0 else a_row(turn)
        return remote(src, swapped[i].at[pair], share_out.at[i, p], share_in.at[i, p], target, s)

    for k in range(count):
        pl.when(q > 0)(lambda k=k: copy(k, xs[k], s, to_left, s - 2).start())
        pl.when(q < nc - 1)(lambda k=k: copy(k, xs[k], s, to_right, s + 2).start())
        copy(k, xs[k], s, to_sib, sibling).start()
    order = [near_first(i, q, nc) for i in range(nc)]
    for p in order[1:]:
        for i in range(len(shared[1])):
            share(i, p).start()
    for take, keep in zip(takes, keeps):
        take.wait()
        keep.start()
    for p in order[1:]:
        slot = 2 * p + c
        for k in range(count):
            src = outs[k].at[slot]
            copy(k, src, slot, to_right, s).wait_recv()
            pl.when((p < q) & (q < nc - 1))(
                lambda k=k, src=src, slot=slot: copy(k, src, slot, to_right, s + 2).start()
            )
            pl.when((p > q) & (q > 0))(
                lambda k=k, src=src, slot=slot: copy(k, src, slot, to_left, s - 2).start()
            )
            copy(k, src, slot, to_sib, sibling).start()
    for cp in keeps:
        cp.wait()
    for p in range(nc):
        mine, theirs = 2 * p + c, 2 * p + 1 - c
        for k in range(count):
            copy(k, outs[k].at[theirs], theirs, to_sib, sibling).wait_recv()
            copy(k, outs[k].at[mine], mine, to_sib, sibling).wait_send()
            pl.when((q < nc - 1) & (p <= q))(
                lambda k=k, mine=mine: copy(k, outs[k].at[mine], mine, to_right, s).wait_send()
            )
            pl.when((q > 0) & (p >= q))(
                lambda k=k, mine=mine: copy(k, outs[k].at[mine], mine, to_left, s).wait_send()
            )
    for p in order[1:]:
        for i in range(len(shared[1])):
            share(i, p).wait_send()
            share(i, p).wait_recv()


def gather_seq(n, rows, arrays, collective_id, held=(), shares=()):
    nc, count = n // 2, len(arrays)
    nbytes = sum(a.size * a.dtype.itemsize for a in arrays)
    dma = pltpu.SemaphoreType.DMA
    shape = jax.ShapeDtypeStruct
    outs = [shape((n, *a.shape), a.dtype) for a in arrays]
    outs += [shape(held[source].shape[-3:], held[source].dtype) for source, _, _ in shares]
    anywhere = pl.BlockSpec(memory_space=pltpu.HBM)
    listed = (tuple(held), [(source, piece, turn, None) for source, piece, turn in shares])
    sems = dma((max(1, len(shares)), nc))
    got = pl.pallas_call(
        functools.partial(gather_kernel, n, rows, count, (range(len(held)), listed[1])),
        out_shape=tuple(outs),
        in_specs=[anywhere] * (count + len(held)),
        out_specs=(anywhere,) * len(outs),
        scratch_shapes=[pltpu.VMEM(a.shape, a.dtype) for a in arrays]
        + [dma((2, count))]
        + [dma((count, n))] * 4
        + [sems] * 2,
        compiler_params=pltpu.CompilerParams(collective_id=collective_id, has_side_effects=True),
        cost_estimate=pl.CostEstimate(flops=0, transcendentals=0, bytes_accessed=nbytes * n * 20),
        name="gather_seq",
    )(*arrays, *held)
    return got[:count], got[count:]

def swap_halves(x):
    return pltpu.roll(x.astype(jnp.float32), HEAD_DIM, 1)


def stack_heads(block):
    lane = lax.broadcasted_iota(jnp.int32, (block.shape[0], 128), 1)
    rows = []
    for h in range(8):
        pair = block[:, (h // 2) * 128 : (h // 2 + 1) * 128].astype(jnp.float32)
        if h % 2 != h // 4:
            pair = swap_halves(pair)
        keep = lane < HEAD_DIM if h // 4 == 0 else lane >= HEAD_DIM
        rows.append(jnp.where(keep, pair, 0.0).astype(jnp.bfloat16))
    return jnp.concatenate(rows, axis=0)


def unstack_heads(stacked, span):
    lane = lax.broadcasted_iota(jnp.int32, (span, 128), 1)
    pairs = []
    for t in range(4):
        first = stacked[2 * t * span : (2 * t + 1) * span]
        second = stacked[(2 * t + 1) * span : (2 * t + 2) * span]
        if t < 2:
            second = swap_halves(second)
        else:
            first = swap_halves(first)
        pairs.append(jnp.where(lane < HEAD_DIM, first, second))
    return jnp.concatenate(pairs, axis=1)


def key_blocks(kv_ref):
    n, _, span, width = kv_ref.shape
    at = pl.multiple_of(pl.program_id(1) * 128, 128)
    pick = lambda start: kv_ref[:, 0, :, pl.ds(start, 128)].reshape(n * span, 128)
    return pick(at), pick(width // 2 + at)


def attend_kernel(valid_ref, q_ref, kv_ref, o_ref, p_ref, s_ref):
    span = q_ref.shape[1]
    keys = kv_ref.shape[0] * span
    q8 = stack_heads(q_ref[0]) * jnp.bfloat16(HEAD_DIM**-0.5)
    k2, v2 = key_blocks(kv_ref)
    s_ref[...] = lax.dot_general(q8, k2, last_last, preferred_element_type=jnp.float32)
    q_pos = lax.axis_index("seq") * span + lax.broadcasted_iota(jnp.int32, (span, 1), 0)
    limit = jnp.minimum(q_pos + 1, valid_ref[pl.program_id(0)])
    allowed = lax.broadcasted_iota(jnp.int32, (span, keys), 1) < limit
    for h in range(8):
        head = slice(h * span, (h + 1) * span)
        scores = jnp.where(allowed, s_ref[head], -1e30)
        unscaled = jnp.exp(scores - jnp.max(scores, axis=1, keepdims=True))
        shares = unscaled * (1.0 / jnp.sum(unscaled, axis=1, keepdims=True))
        p_ref[0, 0, head] = shares.astype(jnp.bfloat16)
    mixed = jnp.dot(p_ref[0, 0], v2, preferred_element_type=jnp.float32)
    o_ref[0] = unstack_heads(mixed, span).astype(jnp.bfloat16)


def attend(q, kv, valid):
    pair, span, width = q.shape
    n, kv_width = kv.shape[0], kv.shape[3] // 2
    groups = kv_width // 128
    keys = n * span
    q_spec = pl.BlockSpec((1, span, 512), lambda p, j, *_: (p, 0, j))
    flops = 4 * pair * groups * 8 * span * keys * 128
    return pl.pallas_call(
        attend_kernel,
        out_shape=(
            pltpu.HBM(q.shape, jnp.bfloat16),
            pltpu.HBM((pair, groups, 8 * span, keys), jnp.bfloat16),
        ),
        grid_spec=pltpu.PrefetchScalarGridSpec(
            num_scalar_prefetch=1,
            grid=(pair, groups),
            in_specs=[
                q_spec,
                pl.BlockSpec((n, 1, span, 2 * kv_width), lambda p, j, *_: (0, p, 0, 0)),
            ],
            out_specs=(
                q_spec,
                pl.BlockSpec((1, 1, 8 * span, keys), lambda p, j, *_: (p, j, 0, 0)),
            ),
            scratch_shapes=[pltpu.VMEM((8 * span, keys), jnp.float32)],
        ),
        compiler_params=pltpu.CompilerParams(vmem_limit_bytes=40 << 20),
        cost_estimate=pl.CostEstimate(
            flops=flops, transcendentals=flops // 512, bytes_accessed=8 << 20
        ),
        name="attend",
    )(valid, *in_hbm(q, kv))


def attend_back_kernel(q_ref, kv_ref, p_ref, g_ref, gq_ref, gkv_ref, s_ref, g_scores):
    span = q_ref.shape[1]
    keys = kv_ref.shape[0] * span
    q8 = stack_heads(q_ref[0]) * jnp.bfloat16(HEAD_DIM**-0.5)
    g8 = stack_heads(g_ref[0])
    k2, v2 = key_blocks(kv_ref)
    low = p_ref[0, 0]
    s_ref[...] = lax.dot_general(g8, v2, last_last, preferred_element_type=jnp.float32)
    for h in range(8):
        head = slice(h * span, (h + 1) * span)
        shares = p_ref[0, 0, head].astype(jnp.float32)
        weighted = shares * s_ref[head]
        centre = jnp.sum(weighted, axis=1, keepdims=True)
        g_scores[head] = (weighted - shares * centre).astype(jnp.bfloat16)
    grad_scores = g_scores[...]
    gq = jnp.dot(grad_scores, k2, preferred_element_type=jnp.float32) * HEAD_DIM**-0.5
    gq_ref[0] = unstack_heads(gq, span).astype(jnp.bfloat16)
    gk = lax.dot_general(grad_scores, q8, first_first, preferred_element_type=jnp.float32)
    gv = lax.dot_general(low, g8, first_first, preferred_element_type=jnp.float32)
    both = jnp.concatenate([gk, gv], axis=1).astype(jnp.bfloat16)
    at = pl.multiple_of(pl.program_id(1) * 256, 256)
    gkv_ref[:, 0, :, pl.ds(at, 256)] = both.reshape(gkv_ref.shape[0], span, 256)


def attend_back(q, kv, shares, g):
    pair, span, _ = q.shape
    n, kv_width = kv.shape[0], kv.shape[3] // 2
    groups = kv_width // 128
    keys = n * span
    q_spec = pl.BlockSpec((1, span, 512), lambda p, j: (p, 0, j))
    return pl.pallas_call(
        attend_back_kernel,
        out_shape=(
            pltpu.HBM(q.shape, jnp.bfloat16),
            pltpu.HBM(kv.shape, jnp.bfloat16),
        ),
        grid=(pair, groups),
        in_specs=[
            q_spec,
            pl.BlockSpec((n, 1, span, 2 * kv_width), lambda p, j: (0, p, 0, 0)),
            pl.BlockSpec((1, 1, 8 * span, keys), lambda p, j: (p, j, 0, 0)),
            q_spec,
        ],
        out_specs=(
            q_spec,
            pl.BlockSpec((n, 1, span, 2 * kv_width), lambda p, j: (0, p, 0, 0)),
        ),
        scratch_shapes=[
            pltpu.VMEM((8 * span, keys), jnp.float32),
            pltpu.VMEM((8 * span, keys), jnp.bfloat16),
        ],
        compiler_params=pltpu.CompilerParams(vmem_limit_bytes=40 << 20),
        cost_estimate=pl.CostEstimate(flops=0, transcendentals=0, bytes_accessed=1 << 20),
        name="attend_back",
    )(*in_hbm(q, kv, shares, g))

def by_distance(i, q, nc):
    room = nc - 1 - q
    left_half = q <= room
    short = jnp.where(left_half, q, room)
    far = jnp.where(left_half, i, nc - 1 - i)
    step = (i + 1) // 2
    near = jnp.where(lax.rem(i, 2) == 1, q - step, q + step)
    return jnp.where(i <= 2 * short, near, far)


def ffn_kernel(n, rows, pieces, u_hbm, inner_hbm, gy0_hbm, gy1_hbm, wd_hbm, a_ref, b_ref, m_ref, ad_ref, bd_ref, md_ref, sq_ref, gram_ref,
               in_ref, down0_hbm, down1_hbm, ga_ref, gb_ref, gm_ref, norm_ref, gad_ref, gbd_ref, gmd_ref, nd_ref,
               w_parts, wd, u, side, gy, down, own, theirs, sib, from_left, from_right, ratio, cross, gm_all,
               w_sem, load_sem, down_sem, small_out, small_in, to_sib, sib_in, to_right, right_in, to_left, left_in):
    nc = n // 2
    f32, low = jnp.float32, jnp.bfloat16
    s, q, c = place_in_seq()
    tokens = own.shape[1]

    weights = [pltpu.make_async_copy(wd_hbm, wd, w_sem.at[0])]
    for src, dst in place_pieces(n, rows, pieces, w_parts):
        weights.append(pltpu.make_async_copy(src, dst, w_sem.at[len(weights)]))
    for cp in weights:
        cp.start()

    def loads(i):
        p = by_distance(nc - 1 - i, q, nc)
        slot = lax.rem(i, 2)
        pair = pl.ds(2 * p, 2)
        return (
            pltpu.make_async_copy(u_hbm.at[pair], u.at[slot], load_sem.at[0, slot]),
            pltpu.make_async_copy(
                gy0_hbm.at[pair], gy.at[slot, :, : tokens // 2], load_sem.at[1, slot]
            ),
            pltpu.make_async_copy(
                gy1_hbm.at[pair], gy.at[slot, :, tokens // 2 :], load_sem.at[2, slot]
            ),
            pltpu.make_async_copy(inner_hbm.at[pair], side.at[slot], load_sem.at[3, slot]),
        )

    for cp in loads(0):
        cp.start()
    sibling = s + 1 - 2 * c
    barrier = pltpu.get_barrier_semaphore()
    for t in range(1, n):
        pl.semaphore_signal(
            barrier, inc=1, device_id={"seq": lax.rem(s + t, n)}, device_id_type=MESH
        )

    def to_sibling(p):
        return pltpu.make_async_remote_copy(
            src_ref=theirs.at[p], dst_ref=sib.at[p], send_sem=to_sib.at[p], recv_sem=sib_in.at[p],
            device_id={"seq": sibling}, device_id_type=MESH,
        )

    def rightward(p, target):
        return pltpu.make_async_remote_copy(
            src_ref=own.at[p], dst_ref=from_left.at[p], send_sem=to_right.at[p], recv_sem=right_in.at[p],
            device_id={"seq": target}, device_id_type=MESH,
        )

    def leftward(p, target):
        return pltpu.make_async_remote_copy(
            src_ref=own.at[p], dst_ref=from_right.at[p], send_sem=to_left.at[p], recv_sem=left_in.at[p],
            device_id={"seq": target}, device_id_type=MESH,
        )

    def down_out(slot, p):
        half = tokens // 2
        return [
            pltpu.make_async_copy(
                down.at[slot, :, half * k : half * (k + 1)], out.at[pl.ds(2 * p, 2)], down_sem.at[k, slot]
            )
            for k, out in enumerate((down0_hbm, down1_hbm))
        ]

    def pass_on(p):
        to_sibling(p).wait_recv()

        @pl.when(p > q)
        def _():
            @pl.when(q > 0)
            def _():
                rightward(p, s).wait_recv()
                own[p] = (own[p].astype(f32) + sib[p].astype(f32) + from_left[p].astype(f32)).astype(low)

            @pl.when(q == 0)
            def _():
                own[p] = (own[p].astype(f32) + sib[p].astype(f32)).astype(low)

            rightward(p, s + 2).start()

        @pl.when(p < q)
        def _():
            @pl.when(q < nc - 1)
            def _():
                leftward(p, s).wait_recv()
                own[p] = (own[p].astype(f32) + sib[p].astype(f32) + from_right[p].astype(f32)).astype(low)

            @pl.when(q == nc - 1)
            def _():
                own[p] = (own[p].astype(f32) + sib[p].astype(f32)).astype(low)

            leftward(p, s - 2).start()

    def starts_flow(p):
        return ((p > q) & (q == 0)) | ((p < q) & (q == nc - 1))

    w = [w_parts.at[g] for g in range(2)]
    width = u_hbm.shape[2]
    weight = lambda g: w[g][...].reshape(width, -1)
    units = wd.shape[0]
    mine = pl.ds(pl.multiple_of(s * units, units), units)
    bd = bd_ref[...].astype(low)
    ad = ad_ref[:, mine].astype(low)
    a = [a_ref[g].astype(low) for g in range(2)]
    b = [b_ref[g, :, mine].astype(low) for g in range(2)]
    m = [m_ref[g : g + 1, mine] for g in range(2)]
    for cp in weights:
        cp.wait()
    a_both = jnp.concatenate(a, axis=0)
    for g in range(2):
        norm, cr = column_norms(weight(g), gram_ref[4 + g], b[g], dot_f32(a[g], weight(g)))
        norm_ref[g] = norm
        cross[g] = cr
        ratio[g] = m[g] / norm
    for ref in (ga_ref, gb_ref, gm_ref, gad_ref, gbd_ref, gmd_ref):
        ref[...] = jnp.zeros_like(ref)
    bd_wide = bd.astype(f32)
    gram_b = dot_two(gram_ref[6], bd)
    squares = jnp.sum(sq_ref[...], axis=0) + SCALE * SCALE * jnp.sum(
        bd_wide * gram_b, axis=0, keepdims=True
    )
    nd_ref[...] = jnp.sqrt(squares + 1e-06)
    ratio_d = md_ref[...] / nd_ref[...]
    pl.semaphore_wait(barrier, n - 1)

    def step(i, carry):
        p = by_distance(nc - 1 - i, q, nc)
        slot = lax.rem(i, 2)
        for cp in loads(i):
            cp.wait()

        @pl.when(i + 1 < nc)
        def _():
            for cp in loads(i + 1):
                cp.start()

        x = u[slot].reshape(2 * tokens, -1)
        upstream = gy[slot].reshape(2 * tokens, -1).astype(f32)
        gb_d = (upstream * ratio_d).astype(low)
        gi_d = (SCALE * dot_nt(gb_d, bd)).astype(low)
        gh = dot_nt(gb_d, wd[...]) + dot_f32(gi_d, ad)
        sides = side[slot].reshape(2 * tokens, -1)
        inner = [sides[:, 16 * g : 16 * g + 16] for g in range(2)]
        before = [dot_f32(x, weight(g)) + SCALE * dot_f32(inner[g], b[g]) for g in range(2)]
        gate = before[0] * ratio[0]
        lift = before[1] * ratio[1]
        sig = 1.0 / (1.0 + jnp.exp(-gate))
        silu = gate * sig
        hidden = (silu * lift).astype(low)
        grads = [gh * lift * sig * (1.0 + gate * (1.0 - sig)), gh * silu]
        gb = [(grads[g] * ratio[g]).astype(low) for g in range(2)]
        gi = jnp.concatenate([(SCALE * dot_nt(gb[g], b[g])).astype(low) for g in range(2)], axis=1)
        back = dot_nt(gb[0], weight(0)) + dot_nt(gb[1], weight(1)) + dot_f32(gi, a_both)
        back = back.astype(low).reshape(2, tokens, -1)
        first, second = back[0], back[1]

        @pl.when(c == 0)
        def _():
            own[p] = first
            theirs[p] = second

        @pl.when(c == 1)
        def _():
            own[p] = second
            theirs[p] = first

        to_sibling(p).start()
        inner_d = dot_nt(hidden, ad).astype(low)
        part = dot_f32(hidden, wd[...]) + SCALE * dot_f32(inner_d, bd)

        @pl.when(i >= 2)
        def _():
            for cp in down_out(slot, p):
                cp.wait()

        down[slot] = part.astype(low).reshape(2, tokens, -1)
        for cp in down_out(slot, p):
            cp.start()
        gmd_ref[...] += jnp.sum(upstream * part, axis=0, keepdims=True)
        gad_ref[...] += dot_tn(gi_d, hidden)
        gbd_ref[...] += SCALE * dot_tn(inner_d, gb_d)
        ga_ref[...] += dot_tn(gi, x).reshape(ga_ref.shape)
        for g in range(2):
            gm_ref[g] += jnp.sum(grads[g] * before[g], axis=0, keepdims=True)
            gb_ref[g] += SCALE * dot_tn(inner[g], gb[g])

        last = by_distance(nc - i, q, nc)
        pl.when((i > 0) & (i < nc - 1) & jnp.logical_not(starts_flow(last)))(lambda: pass_on(last))
        pl.when(starts_flow(p) | (i == nc - 2))(lambda: pass_on(p))
        return carry

    lax.fori_loop(0, nc, step, 0)

    gmd_ref[...] = gmd_ref[...] / nd_ref[...]

    def small(t, slot):
        return pltpu.make_async_remote_copy(
            src_ref=gmd_ref,
            dst_ref=gm_all.at[slot],
            send_sem=small_out.at[t],
            recv_sem=small_in.at[t],
            device_id={"seq": lax.rem(s + t, n)},
            device_id_type=MESH,
        )

    for t in range(1, n):
        small(t, s).start()
    for g in range(2):
        norm = norm_ref[g]
        gm = gm_ref[g] / norm
        gm_ref[g] = gm
        col = -gm * m[g] / (norm * norm)
        weighted = (b[g].astype(f32) * col).astype(low)
        tail = two_terms(dot_nt(weighted, b[g]))
        ga_ref[g] += SCALE * (dot_nt(weighted, weight(g)) + SCALE * dot_two(tail, a[g]))
        gb_ref[g] += SCALE * col * cross[g]

    gm_line = gmd_ref[...]
    for t in range(1, n):
        slot = lax.rem(s - t + n, n)
        small(t, slot).wait_recv()
        gm_line = gm_line + gm_all[slot]
    col = -gm_line * md_ref[...] / (nd_ref[...] * nd_ref[...])
    weighted = (bd_wide * col).astype(low)
    tail = two_terms(dot_nt(weighted, bd))
    gad_ref[...] += SCALE * (dot_nt(weighted, wd[...]) + SCALE * dot_two(tail, ad))
    own_gram = jnp.where(s == 0, SCALE, 0.0) * gram_b
    gbd_ref[...] += SCALE * col * (dot_f32(ad, wd[...]) + own_gram)

    to_sibling(q).wait_recv()
    in_ref[...] = own[q].astype(f32) + sib[q].astype(f32)

    @pl.when(q > 0)
    def _():
        rightward(q, s).wait_recv()
        in_ref[...] += from_left[q].astype(f32)

    @pl.when(q < nc - 1)
    def _():
        leftward(q, s).wait_recv()
        in_ref[...] += from_right[q].astype(f32)

    for i in range(min(2, nc)):
        for cp in down_out(i, 0):
            cp.wait()
    for t in range(1, n):
        small(t, s).wait_send()
    for p in range(nc):
        to_sibling(p).wait_send()
        pl.when(p > q)(lambda p=p: rightward(p, s).wait_send())
        pl.when(p < q)(lambda p=p: leftward(p, s).wait_send())


def share_plan(rows):
    turns = range(1, rows // 2)
    first = [(0, 0, k) for k in turns] + [(0, 1, 0)]
    second = [(0, 0, 0)] + [(0, 1, k) for k in turns]
    second += [(k, None, 0) for k in turns] + [(rows // 2, None, k) for k in turns]
    return first, second


def place_pieces(n, rows, pieces, w_parts):
    nc, half = n // 2, rows // 2
    _, q, _ = place_in_seq()
    r, b_row, a_row, diagonal = place_in_rows(rows)
    own, near = pieces[:2]
    turns = range(1, half)
    held = [(own.at[g], g, r) for g in range(2)]
    kinds = [(0, a_row(-k)) for k in turns] + [(1, b_row)]
    kinds += [(0, b_row)] + [(1, a_row(-k)) for k in turns]
    kinds += [(0, diagonal(-k)) for k in turns] + [(1, diagonal(-k)) for k in turns]
    held += [(piece, g, hold) for piece, (g, hold) in zip(pieces[2:], kinds)]
    out = [(near, w_parts.at[:, pl.ds(2 * q, 2)])]
    for i in range(1, nc):
        pair = pl.ds(2 * near_first(i, q, nc), 2)
        out += [(src.at[pair], w_parts.at[g, pair, hold]) for src, g, hold in held]
    return out


def feed_forward(n, rows, pieces, u, inner, gy0, gy1, wd, a, b, m, ad, bd, md, sq, gram, collective_id):
    nc = n // 2
    _, tokens, width = u.shape
    units = wd.shape[0]
    f32, low = jnp.float32, jnp.bfloat16
    shape = jax.ShapeDtypeStruct
    vmem = pl.BlockSpec(memory_space=pltpu.VMEM)
    hbm = pl.BlockSpec(memory_space=pltpu.HBM)
    dma = pltpu.SemaphoreType.DMA
    line = pltpu.VMEM((nc, tokens, width), low)
    pair = pltpu.VMEM((2, 2, tokens, width), low)
    part = pieces[0].shape[2]
    copies = 2 + (n // 2 - 1) * (2 + 2 * rows - 2)
    count = len(pieces)

    def kernel(*refs):
        ffn_kernel(n, rows, refs[:count], *refs[count:])

    return pl.pallas_call(
        kernel,
        out_shape=(
            shape((tokens, width), f32),
            pltpu.HBM((n, tokens // 2, width), low),
            pltpu.HBM((n, tokens // 2, width), low),
            shape((2, 16, width), f32),
            shape((2, 16, units), f32),
            shape((2, 1, units), f32),
            shape((2, 1, units), f32),
            shape((16, units), f32),
            shape((16, width), f32),
            shape((1, width), f32),
            shape((1, width), f32),
        ),
        in_specs=[hbm] * (count + 5) + [vmem] * 8,
        out_specs=(vmem, hbm, hbm) + (vmem,) * 8,
        scratch_shapes=[
            pltpu.VMEM((2, n, rows, part, units), low),
            pltpu.VMEM((units, width), low),
            pair,
            pltpu.VMEM((2, 2, tokens, 128), low),
            pair,
            pair,
            line, line, line, line, line,
            pltpu.VMEM((2, 1, units), f32),
            pltpu.VMEM((2, 16, units), f32),
            pltpu.VMEM((n, 1, width), f32),
            dma((copies,)), dma((4, 2)), dma((2, 2)), dma((n,)), dma((n,)),
        ] + [dma((nc,))] * 6,
        compiler_params=pltpu.CompilerParams(
            collective_id=collective_id, has_side_effects=True, vmem_limit_bytes=60 << 20
        ),
        cost_estimate=pl.CostEstimate(
            flops=12 * n * tokens * width * units, transcendentals=n * tokens * units,
            bytes_accessed=32 << 20,
        ),
        name="feed_forward",
    )(*pieces, u, inner, gy0, gy1, wd, a, b, m, ad, bd, md, sq, gram)

def greet_cross(n, rows, wait=True):
    s, r = lax.axis_index("seq"), lax.axis_index("rows")
    barrier = pltpu.get_barrier_semaphore()
    for t in range(1, n):
        pl.semaphore_signal(barrier, inc=1, device_id=(r, lax.rem(s + t, n)), device_id_type=MESH)
    for t in range(1, rows):
        pl.semaphore_signal(barrier, inc=1, device_id=(lax.rem(r + t, rows), s), device_id_type=MESH)
    if wait:
        pl.semaphore_wait(barrier, n + rows - 2)


def scatter_kernel(n, rows, x_ref, gb_gu, gm_gu, n_gu, ga_d, o_ref, units_all, own, sib, from_left, from_right,
                   units, units_in, load_sem, to_sib, sib_in, to_right, right_in, to_left, left_in,
                   row_out, row_in, back_send, back_in, wide_send, wide_in, pass_send, pass_in):
    nc = n // 2
    s, q, c = place_in_seq()
    sibling = s + 1 - 2 * c
    theirs = 1 - c
    r = lax.axis_index("rows")
    greet_cross(n, rows)
    f32, low = jnp.float32, jnp.bfloat16
    unit_rows, size = units.shape[1:]

    def load(p):
        return pltpu.make_async_copy(x_ref.at[2 * p + c], own.at[p], load_sem.at[p])

    def to_sibling(p):
        return pltpu.make_async_remote_copy(
            src_ref=x_ref.at[2 * p + theirs],
            dst_ref=sib.at[p],
            send_sem=to_sib.at[p],
            recv_sem=sib_in.at[p],
            device_id={"seq": sibling},
            device_id_type=MESH,
        )

    def rightward(p, target):
        return pltpu.make_async_remote_copy(
            src_ref=own.at[p],
            dst_ref=from_left.at[p],
            send_sem=to_right.at[p],
            recv_sem=right_in.at[p],
            device_id={"seq": target},
            device_id_type=MESH,
        )

    def leftward(p, target):
        return pltpu.make_async_remote_copy(
            src_ref=own.at[p],
            dst_ref=from_right.at[p],
            send_sem=to_left.at[p],
            recv_sem=left_in.at[p],
            device_id={"seq": target},
            device_id_type=MESH,
        )

    order = []
    for t in range(nc):
        for p in (nc - 1 - t, t):
            if p not in order:
                order.append(p)
    for p in order:
        to_sibling(p).start()
        load(p).start()

    n_high = [n_gu[g].astype(low).astype(f32) for g in range(2)]
    n_rest = [n_gu[g] - n_high[g] for g in range(2)]
    tops = jnp.concatenate(
        [gm_gu[0], gm_gu[1]]
        + [v * (1.0 / rows) for v in (n_high[0], n_rest[0], n_high[1], n_rest[1])]
        + [jnp.zeros((2, size), f32)],
        axis=0,
    )
    blocks = [gb_gu[0][:8], gb_gu[0][8:], gb_gu[1][:8], gb_gu[1][8:], ga_d[:8], ga_d[8:], tops, jnp.zeros((8, size), f32)]
    per = unit_rows // 8
    for j in range(rows):
        units[j] = jnp.concatenate(blocks[per * j : per * (j + 1)], axis=0).astype(low)

    def member(t):
        return lax.rem(r + t + rows, rows)

    def chip(t):
        return lax.rem(q + t + nc, nc)

    def unit_send(t):
        return remote(units.at[member(t)], units_in.at[t], row_out.at[t], row_in.at[t], member(t), s)

    def unit_back(t, slot):
        place = units_all.at[r, c, slot]
        return remote(place, place, back_send.at[t], back_in.at[t], r, 2 * chip(t) + c)

    def unit_wide(t, row):
        place = units_all.at[row, c]
        return remote(place, place, wide_send.at[t], wide_in.at[t], member(t), s)

    def unit_hand(t, row, core):
        place = units_all.at[row, core]
        return remote(place, place, pass_send.at[t], pass_in.at[t], r, sibling)

    def sum_units():
        total = units[r].astype(f32)
        for t in range(1, rows):
            unit_send(t).wait_recv()
            total = total + units_in[t].astype(f32)
        units_all[r, c, q] = total.astype(low)
        for t in range(1, nc):
            unit_back(t, q).start()

    def spread_units():
        for t in range(1, nc):
            unit_back(t, chip(-t)).wait_recv()
        for t in range(1, rows):
            unit_wide(t, r).start()
        unit_hand(0, r, c).start()

    for t in range(1, rows):
        unit_send(t).start()
    sum_units()
    for step, p in enumerate(order):
        if step == 1:
            spread_units()
        load(p).wait()
        to_sibling(p).wait_recv()

        @pl.when(p > q)
        def _(p=p):
            @pl.when(q > 0)
            def _():
                rightward(p, s).wait_recv()
                total = own[p].astype(f32) + sib[p].astype(f32) + from_left[p].astype(f32)
                own[p] = total.astype(own.dtype)

            @pl.when(q == 0)
            def _():
                own[p] = (own[p].astype(f32) + sib[p].astype(f32)).astype(own.dtype)

            rightward(p, s + 2).start()

        @pl.when(p < q)
        def _(p=p):
            @pl.when(q < nc - 1)
            def _():
                leftward(p, s).wait_recv()
                total = own[p].astype(f32) + sib[p].astype(f32) + from_right[p].astype(f32)
                own[p] = total.astype(own.dtype)

            @pl.when(q == nc - 1)
            def _():
                own[p] = (own[p].astype(f32) + sib[p].astype(f32)).astype(own.dtype)

            leftward(p, s - 2).start()

    o_ref[...] = own[q].astype(f32) + sib[q].astype(f32)

    @pl.when(q > 0)
    def _():
        rightward(q, s).wait_recv()
        o_ref[...] += from_left[q].astype(f32)

    @pl.when(q < nc - 1)
    def _():
        leftward(q, s).wait_recv()
        o_ref[...] += from_right[q].astype(f32)

    for t in range(1, rows):
        unit_wide(t, member(-t)).wait_recv()
        unit_hand(t, member(-t), c).start()
    for t in range(rows):
        unit_hand(t, member(-t), theirs).wait_recv()
        unit_hand(t, member(-t), c).wait_send()
    for t in range(1, rows):
        unit_send(t).wait_send()
        unit_wide(t, r).wait_send()
    for t in range(1, nc):
        unit_back(t, q).wait_send()
    for p in range(nc):
        to_sibling(p).wait_send()
        pl.when(p > q)(lambda p=p: rightward(p, s).wait_send())
        pl.when(p < q)(lambda p=p: leftward(p, s).wait_send())


def scatter_seq(n, rows, x, own_units, collective_id):
    nc = n // 2
    _, height, cols = x.shape
    size = own_units[3].shape[1]
    unit_rows = 64 // rows
    low = jnp.bfloat16
    dma = pltpu.SemaphoreType.DMA
    buf = pltpu.VMEM((nc, height, cols), x.dtype)
    small = pltpu.VMEM((rows, unit_rows, size), low)
    vmem = pl.BlockSpec(memory_space=pltpu.VMEM)
    return pl.pallas_call(
        functools.partial(scatter_kernel, n, rows),
        out_shape=(
            jax.ShapeDtypeStruct((height, cols), jnp.float32),
            jax.ShapeDtypeStruct((rows, 2, nc, unit_rows, size), low),
        ),
        in_specs=[pl.BlockSpec(memory_space=pltpu.HBM)] + [vmem] * 4,
        out_specs=(vmem,) * 2,
        scratch_shapes=[buf] * 4 + [small] * 2 + [dma((nc,))] * 7
        + [dma((rows,))] * 2 + [dma((nc,))] * 2 + [dma((rows,))] * 4,
        compiler_params=pltpu.CompilerParams(
            collective_id=collective_id, has_side_effects=True, vmem_limit_bytes=32 << 20
        ),
        cost_estimate=pl.CostEstimate(flops=0, transcendentals=0, bytes_accessed=1 << 20),
        name="scatter_seq",
    )(*in_hbm(x), *own_units)


def reduce_kernel(n, rows, ga_qkv, ga_o, gb_qkv, gb_o, ga_gu, gb_d, gm_qkv, gm_o, gm_d,
                  whole, part, from_sib, mid, from_rows, from_line, line_out,
                  sib_out, sib_in, row_out, row_in, line_send, line_in, back_send, back_in, wide_send, wide_in,
                  pass_send, pass_in):
    nc = n // 2
    f32, low = jnp.float32, jnp.bfloat16
    s, q, c = place_in_seq()
    sibling = s + 1 - 2 * c
    r = lax.axis_index("rows")
    width = ga_o.shape[1]
    cols = width // (2 * rows)
    kv = (gb_qkv.shape[1] - width) // 2
    height = part.shape[2]
    piece = height // nc

    greet_cross(n, rows, wait=False)
    gb_k, gb_v = gb_qkv[:, width : width + kv], gb_qkv[:, width + kv :]
    small = jnp.concatenate(
        [
            jnp.concatenate([gb_k[:8], gb_k[8:], gb_v[:8], gb_v[8:]], axis=1),
            gm_qkv[:, :width],
            gm_o[...],
            gm_d[...],
            jnp.concatenate([gm_qkv[:, width:], jnp.zeros((1, width - 2 * kv), f32)], axis=1),
            jnp.zeros((4, width), f32),
        ],
        axis=0,
    )
    groups = [ga_qkv[0], ga_qkv[1], ga_qkv[2], ga_o[...], gb_qkv[:, :width], gb_o[...], ga_gu[0], ga_gu[1], gb_d[...], small]
    for j in range(2 * rows):
        for g, value in enumerate(groups):
            part[j % 2, j // 2, 16 * g : 16 * g + 16] = value[:, cols * j : cols * (j + 1)].astype(low)
        if height > 160:
            part[j % 2, j // 2, 160:] = jnp.zeros((height - 160, cols), low)
    pl.semaphore_wait(pltpu.get_barrier_semaphore(), n + rows - 2)

    def to_sibling():
        return remote(part.at[1 - c], from_sib, sib_out.at[0], sib_in.at[0], r, sibling)

    def member(t):
        return lax.rem(r + t + rows, rows)

    def row_send(t):
        return remote(mid.at[member(t)], from_rows.at[t], row_out.at[t], row_in.at[t], member(t), s)

    def chip(t):
        return lax.rem(q + t + nc, nc)

    def line_part(t):
        return remote(line_out.at[chip(t)], from_line.at[t], line_send.at[t], line_in.at[t], r, 2 * chip(t) + c)

    def back(t, slot):
        return remote(whole.at[r, c, slot], whole.at[r, c, slot], back_send.at[t], back_in.at[t], r, 2 * chip(t) + c)

    def wide(t, row):
        return remote(whole.at[row, c], whole.at[row, c], wide_send.at[t], wide_in.at[t], member(t), s)

    def hand(t, row, core):
        return remote(whole.at[row, core], whole.at[row, core], pass_send.at[t], pass_in.at[t], r, sibling)

    to_sibling().start()
    to_sibling().wait_recv()
    for t in range(rows):
        mid[member(t)] = (part[c, member(t)].astype(f32) + from_sib[member(t)].astype(f32)).astype(low)
        if t:
            row_send(t).start()
    total = mid[r].astype(f32)
    for t in range(1, rows):
        row_send(t).wait_recv()
        total = total + from_rows[t].astype(f32)
    for p in range(nc):
        line_out[p] = total[piece * p : piece * (p + 1)].astype(low)
    for t in range(1, nc):
        line_part(t).start()
    own = line_out[q].astype(f32)
    for t in range(1, nc):
        line_part(t).wait_recv()
        own = own + from_line[t].astype(f32)
    whole[r, c, q] = own.astype(low)
    for t in range(1, nc):
        back(t, q).start()
    for t in range(1, nc):
        back(t, chip(-t)).wait_recv()
    for t in range(1, rows):
        wide(t, r).start()
    hand(0, r, c).start()
    for t in range(1, rows):
        wide(t, member(-t)).wait_recv()
        hand(t, member(-t), c).start()
    for t in range(rows):
        hand(t, member(-t), 1 - c).wait_recv()

    to_sibling().wait_send()
    for t in range(1, rows):
        row_send(t).wait_send()
        wide(t, r).wait_send()
    for t in range(1, nc):
        line_part(t).wait_send()
        back(t, q).wait_send()
    for t in range(rows):
        hand(t, member(-t), c).wait_send()


def sum_gradients(n, rows, full, collective_id):
    nc = n // 2
    width = full[1].shape[1]
    cols = width // (2 * rows)
    height = -(-160 // (8 * nc)) * 8 * nc
    low = jnp.bfloat16
    vmem = pl.BlockSpec(memory_space=pltpu.VMEM)
    dma = pltpu.SemaphoreType.DMA
    block = (rows, height, cols)
    return pl.pallas_call(
        functools.partial(reduce_kernel, n, rows),
        out_shape=jax.ShapeDtypeStruct((rows, 2, nc, height // nc, cols), low),
        in_specs=[vmem] * 9,
        out_specs=vmem,
        scratch_shapes=[
            pltpu.VMEM((2, *block), low),
            pltpu.VMEM(block, low),
            pltpu.VMEM(block, low),
            pltpu.VMEM(block, low),
            pltpu.VMEM((nc, height // nc, cols), low),
            pltpu.VMEM((nc, height // nc, cols), low),
            dma((1,)), dma((1,)), dma((rows,)), dma((rows,)), dma((nc,)), dma((nc,)),
            dma((nc,)), dma((nc,)), dma((rows,)), dma((rows,)), dma((rows,)), dma((rows,)),
        ],
        compiler_params=pltpu.CompilerParams(
            collective_id=collective_id, has_side_effects=True, vmem_limit_bytes=48 << 20
        ),
        cost_estimate=pl.CostEstimate(flops=0, transcendentals=0, bytes_accessed=1 << 20),
        name="sum_gradients",
    )(*full)


def finish_kernel(n, rows, whole, units_all, x1, before_0, before_1, m_attn, n_attn, m_d, n_d, m_gu,
                  o_out, o_ga, o_gb_qo, o_gb_kv, o_gm_q, o_gm_kv, o_gm_o, o_ga_gu, o_gb_gu, o_gm_gu, o_ga_d, o_gb_d,
                  o_gm_d, o_stats, n_gu):
    f32 = jnp.float32
    nc = n // 2
    width = o_gb_d.shape[1]
    kv = o_gb_kv.shape[2]
    cols = width // (2 * rows)
    size = units_all.shape[4]
    per = units_all.shape[3] // 8
    half = x1.shape[0] // 2
    for k, before in enumerate((before_0, before_1)):
        own = slice(half * k, half * (k + 1))
        o_out[own] = (x1[own] + before[...].astype(f32) * (m_d[...] / n_d[...])).astype(o_out.dtype)
    for j in range(2 * rows):
        block = jnp.concatenate([whole[j // 2, j % 2, p].astype(f32) for p in range(nc)], axis=0)
        at = slice(cols * j, cols * (j + 1))
        for g in range(4):
            o_ga[g, :, at] = block[16 * g : 16 * g + 16]
        o_gb_qo[0, :, at] = block[64:80]
        o_gb_qo[1, :, at] = block[80:96]
        o_ga_gu[0, :, at] = block[96:112]
        o_ga_gu[1, :, at] = block[112:128]
        o_gb_d[:, at] = block[128:144]
        which, start = divmod(cols * j, kv)
        o_gb_kv[which // 2, 8 * (which % 2) : 8 * (which % 2) + 8, start : start + cols] = block[144:152]
        o_gm_q[at] = block[152]
        o_gm_o[at] = block[153]
        o_gm_d[at] = block[154]
        if which < 2:
            o_gm_kv[which : which + 1, start : start + cols] = block[155:156]
    for j in range(rows):
        for dev in range(n):
            block = units_all[j, dev % 2, dev // 2].astype(f32)
            at = slice(size * dev, size * (dev + 1))
            for t in range(per):
                rows8, place = block[8 * t : 8 * t + 8], per * j + t
                half = slice(8 * (place % 2), 8 * (place % 2) + 8)
                if place < 4:
                    o_gb_gu[place // 2, half, at] = rows8
                elif place < 6:
                    o_ga_d[half, at] = rows8
                elif place == 6:
                    o_gm_gu[:, at] = rows8[:2]
                    n_gu[0:1, at] = rows8[2:3] + rows8[3:4]
                    n_gu[1:2, at] = rows8[4:5] + rows8[5:6]


    row = lax.broadcasted_iota(jnp.int32, o_stats.shape, 0)
    col = lax.broadcasted_iota(jnp.int32, o_stats.shape, 1)
    bounds = [(0, width), (width, width + kv), (width + kv, width + 2 * kv), (width + 2 * kv, 2 * width + 2 * kv)]
    both = [(m_attn[:, i:j], n_attn[:, i:j]) for i, j in bounds]
    both += [(m_gu[g : g + 1, :], n_gu[g : g + 1, :]) for g in range(2)] + [(m_d[...], n_d[...])]
    stats = jnp.zeros(o_stats.shape, f32)
    for p, (m, norm) in enumerate(both):
        drift = jnp.mean(jnp.square(m - norm), axis=1, keepdims=True)
        drift = jnp.sqrt(drift) / jnp.sqrt(jnp.mean(jnp.square(m), axis=1, keepdims=True) + 1e-06)
        stats = jnp.where((row == 0) & (col == p), drift, stats)
        stats = jnp.where((row == 1) & (col == p), jnp.mean(norm, axis=1, keepdims=True), stats)
    o_stats[...] = stats


def finish(n, rows, sums, units, x1, before_0, before_1, m_attn, n_attn, m_d, n_d, m_gu):
    tokens, width = x1.shape
    kv = (m_attn.shape[1] - 2 * width) // 2
    wide_units = m_gu.shape[1]
    shape = lambda *dims: pltpu.HBM(dims, jnp.float32)
    vmem = pl.BlockSpec(memory_space=pltpu.VMEM)
    return pl.pallas_call(
        functools.partial(finish_kernel, n, rows),
        out_shape=(
            pltpu.HBM((tokens, width), jnp.bfloat16), shape(4, 16, width), shape(2, 16, width), shape(2, 16, kv),
            shape(width), shape(2, kv), shape(width), shape(2, 16, width), shape(2, 16, wide_units), shape(2, wide_units),
            shape(16, wide_units), shape(16, width), shape(width), shape(2, 7),
        ),
        in_specs=[vmem] * 2 + [pl.BlockSpec()] * 8,
        scratch_shapes=[pltpu.VMEM((2, wide_units), jnp.float32)],
        compiler_params=pltpu.CompilerParams(vmem_limit_bytes=40 << 20),
        cost_estimate=pl.CostEstimate(flops=0, transcendentals=0, bytes_accessed=8 << 20),
        name="finish",
    )(sums, units, *in_hbm(x1, before_0, before_1), m_attn, n_attn, m_d, n_d, m_gu)

def local(
    layer_input,
    output_gradient,
    norm_gain_vectors,
    query_output_frozen,
    key_value_frozen,
    gate_up_frozen,
    down_frozen_weight,
    attention_adapter_a,
    query_output_adapter_b,
    key_value_adapter_b,
    query_magnitude,
    key_value_magnitude,
    output_magnitude,
    gate_up_adapter_a,
    gate_up_adapter_b,
    gate_up_magnitude,
    down_adapter_a,
    down_adapter_b,
    down_magnitude,
    prompt_length_list,
    response_length_list,
):
    pair_rows, span_len, model_width = layer_input.shape
    token_count = pair_rows * span_len
    kv_width = KV_HEADS * HEAD_DIM
    seq_size = lax.axis_size("seq")
    rows_size = lax.axis_size("rows")
    seq_index = lax.axis_index("seq")
    f32 = jnp.float32

    x = layer_input.reshape(token_count, model_width)
    grad_out_rows = output_gradient.reshape(token_count, model_width)
    weights, gu_own, gu_near, sq_d, grams, u1, inner_1, gy_halves = gather_weights(
        seq_size, rows_size, query_output_frozen, key_value_frozen, gate_up_frozen,
        down_frozen_weight, down_adapter_a, down_adapter_b, x, norm_gain_vectors,
        attention_adapter_a, gate_up_adapter_a, grad_out_rows, 1,
    )
    shares_1, shares_2 = share_plan(rows_size)
    gy_0 = lax.all_gather(gy_halves[0], "seq", axis=0, tiled=False)

    b_attn = jnp.concatenate(
        [
            query_output_adapter_b[0],
            key_value_adapter_b[0],
            key_value_adapter_b[1],
            query_output_adapter_b[1],
        ],
        axis=1,
    )
    m_attn = jnp.concatenate(
        [query_magnitude, key_value_magnitude[0], key_value_magnitude[1], output_magnitude]
    )[None]
    m_d = down_magnitude[None]

    positions = seq_index * span_len + jnp.arange(span_len, dtype=jnp.int32)
    half_dim = HEAD_DIM // 2
    frequency = 500000.0 ** (-(jnp.arange(half_dim, dtype=f32) * 2.0) / HEAD_DIM)
    angles = positions.astype(f32)[:, None] * frequency[None, :]
    cosine = jnp.tile(jnp.cos(angles), (pair_rows, 4))
    sine = jnp.tile(jnp.sin(angles), (pair_rows, 4))
    valid_len = prompt_length_list[0] + response_length_list

    before_qkv, q, n_attn, cross_attn, kv_all, sq_all, gu_1 = project_qkv(
        seq_size, rows_size, u1, inner_1, grams, attention_adapter_a, weights, b_attn, m_attn,
        cosine, sine, sq_d, gu_own, shares_1, 2,
    )
    kv_all, half_1 = lax.optimization_barrier((kv_all, gy_halves[1]))
    gy_1 = lax.all_gather(half_1, "seq", axis=0, tiled=False)
    kv_all = kv_all.reshape(seq_size, pair_rows, span_len, 2 * kv_width)
    q = q.reshape(pair_rows, span_len, model_width)
    att, shares = attend(q, kv_all, valid_len)
    att = att.reshape(token_count, model_width)
    before_o, x1, u2, inner_2 = project_out(
        att, attention_adapter_a, weights, b_attn, m_attn, n_attn, x, norm_gain_vectors, gate_up_adapter_a
    )

    (u2_all, inner_all), gu_2 = gather_seq(
        seq_size, rows_size, [u2, inner_2], 3, (gu_own, *gu_1), shares_2
    )
    in_grad, down_0, down_1, ga_gu, gb_gu, gm_gu, n_gu, ga_d, gb_d, gm_d, n_d = feed_forward(
        seq_size, rows_size, (gu_own, gu_near, *gu_1, *gu_2), u2_all, inner_all, gy_0, gy_1,
        down_frozen_weight, gate_up_adapter_a, gate_up_adapter_b, gate_up_magnitude, down_adapter_a,
        down_adapter_b, m_d, sq_all, grams, 4,
    )
    flat = lambda v: v.reshape(-1, model_width)
    before_0 = lax.psum_scatter(flat(down_0), "seq", scatter_dimension=0, tiled=True)

    gx1, grad_att, ga_o, gb_o, gm_o = out_back(
        in_grad, x1, norm_gain_vectors, grad_out_rows, before_o, att, attention_adapter_a, b_attn, m_attn,
        n_attn, cross_attn, weights,
    )
    gq, gkv = attend_back(q, kv_all, shares, grad_att.reshape(q.shape))
    gkv, units = scatter_seq(
        seq_size, rows_size, gkv.reshape(seq_size, token_count, 2 * kv_width),
        (gb_gu, gm_gu, n_gu, ga_d), 5,
    )
    gkv, down_1, before_0 = lax.optimization_barrier((gkv, down_1, before_0))
    before_1 = lax.psum_scatter(flat(down_1), "seq", scatter_dimension=0, tiled=True)
    grad_inputs, ga_qkv, gb_qkv, gm_qkv = qkv_back(
        gq.reshape(token_count, model_width), gkv, cosine, sine, before_qkv, u1, inner_1,
        attention_adapter_a, b_attn, m_attn, n_attn, cross_attn, x, norm_gain_vectors, gx1, weights,
    )

    sums = sum_gradients(
        seq_size, rows_size,
        (ga_qkv, ga_o, gb_qkv, gb_o, ga_gu, gb_d, gm_qkv, gm_o, gm_d),
        6,
    )
    layer_result, *summed, stats = finish(
        seq_size, rows_size, sums, units, x1, before_0, before_1, m_attn, n_attn, m_d, n_d, gate_up_magnitude
    )
    shape = (pair_rows, span_len, model_width)
    return (layer_result.reshape(shape), grad_inputs.reshape(shape), *summed, stats.T)

def solution(mesh):
    return jax.shard_map(
        local,
        mesh=mesh,
        in_specs=(
            P("rows", "seq", None),
            P("rows", "seq", None),
            P(),
            P(None, "seq", None),
            P(None, "seq", None),
            P(None, "seq", None),
            P("seq", None),
            P(),
            P(),
            P(),
            P(),
            P(),
            P(),
            P(),
            P(),
            P(),
            P(),
            P(),
            P(),
            P("rows"),
            P("rows"),
        ),
        out_specs=(
            P("rows", "seq", None),
            P("rows", "seq", None),
            P(),
            P(),
            P(),
            P(),
            P(),
            P(),
            P(),
            P(),
            P(),
            P(),
            P(),
            P(),
            P(),
        ),
        check_vma=False,
    )
```

```python
import functools

import jax
import jax.numpy as jnp
from jax import lax
from jax.experimental import pallas as pl
from jax.experimental.pallas import tpu as pltpu
from jax.sharding import PartitionSpec as P

HEADS = 32
KV_HEADS = 8
HEAD_DIM = 64
ADAPTER_RANK = 16
ALPHA = 32
SCALE = ALPHA / ADAPTER_RANK
TILE = 512

highest = lax.Precision.HIGHEST
last_last = (((1,), (1,)), ((), ()))
first_first = (((0,), (0,)), ((), ()))

def dot_f32(a, b):
    return jnp.dot(a, b, preferred_element_type=jnp.float32)


def dot_nt(a, b):
    return lax.dot_general(a, b, last_last, preferred_element_type=jnp.float32)


def dot_tn(a, b):
    return lax.dot_general(a, b, first_first, preferred_element_type=jnp.float32)


def in_hbm(*arrays):
    return [pltpu.with_memory_space_constraint(v, pltpu.HBM) for v in arrays]


def unit_rms(v):
    return lax.rsqrt(jnp.mean(v * v, axis=-1, keepdims=True) + 1e-05)


def rms_back(v, gain, upstream):
    r = unit_rms(v)
    scaled = gain * upstream
    return r * scaled - v * (r * r * r) * jnp.mean(scaled * v, axis=-1, keepdims=True)


def turn(z, cosine, sine):
    width = z.shape[1]
    lane = lax.broadcasted_iota(jnp.int32, z.shape, 1)
    half = HEAD_DIM // 2
    other = jnp.where(
        lax.rem(lane, HEAD_DIM) < half, -pltpu.roll(z, width - half, 1), pltpu.roll(z, half, 1)
    )
    copies = width // cosine.shape[1]
    return z * jnp.tile(cosine, (1, copies)) + other * jnp.tile(sine, (1, copies))


def column_squares(w):
    return jnp.sum(jnp.square(w.astype(jnp.float32)), axis=0, keepdims=True)


def two_terms(value):
    high = value.astype(jnp.bfloat16)
    return jnp.concatenate([high, (value - high.astype(jnp.float32)).astype(jnp.bfloat16)], axis=0)


def dot_two(terms, b):
    both = dot_f32(terms, b)
    half = both.shape[0] // 2
    return both[:half] + both[half:]


def column_norms(w, gram, b, cross):
    b_wide = b.astype(jnp.float32)
    gram_b = dot_two(gram, b)
    squares = column_squares(w) + 2.0 * SCALE * jnp.sum(b_wide * cross, axis=0, keepdims=True)
    squares = squares + SCALE * SCALE * jnp.sum(b_wide * gram_b, axis=0, keepdims=True)
    return jnp.sqrt(squares + 1e-06), cross + SCALE * gram_b


def project_kernel(n, rows, plan, k_tiles, q_tiles, u_ref, inner_ref, gram_ref, a_ref, w_ref, b_ref, m_ref, cos_ref,
                   sin_ref, sq_ref, held, before_ref, q_ref, n_ref, cross_ref, kv_all, sq_all, *refs):
    swapped = refs[: len(plan)]
    kv_ref, keep_sem, to_sib, to_left, to_right, recv, share_out, share_in = refs[len(plan) :]
    j = pl.program_id(0)
    last = pl.num_programs(0) - 1
    nc = n // 2
    s, q, c = place_in_seq()
    sibling = s + 1 - 2 * c
    r, b_row, a_row, _ = place_in_rows(rows)
    order = [near_first(i, q, nc) for i in range(nc)]
    sources, outs = (kv_ref, sq_ref), (kv_all, sq_all)

    def copy(k, src, slot, sems, target):
        return remote(src, outs[k].at[slot], sems.at[k, slot], recv.at[k, slot], r, target)

    def share(i, chip):
        _, piece, turn = plan[i]
        pair = pl.ds(2 * chip, 2)
        target = b_row if turn == 0 else a_row(turn)
        return remote(
            held.at[piece, pair], swapped[i].at[pair], share_out.at[i, chip], share_in.at[i, chip], target, s
        )

    def keep(k):
        return pltpu.make_async_copy(sources[k], outs[k].at[s], keep_sem.at[k])

    @pl.when(j == 0)
    def _():
        greet_all(n, rows)
        for chip in order[1:]:
            for i in range(len(plan)):
                share(i, chip).start()

    a = a_ref[0].astype(jnp.bfloat16)
    b = b_ref[...].astype(jnp.bfloat16)
    w = w_ref[0]
    height = u_ref.shape[0]

    @pl.when(j < 2 * k_tiles + q_tiles)
    def _():
        both = dot_f32(jnp.concatenate([u_ref[...], a], axis=0), w)
        norm, cross = column_norms(w, gram_ref[0], b, both[height:])
        n_ref[...] = norm
        cross_ref[...] = cross
        before = both[:height] + SCALE * dot_f32(inner_ref[0], b)
        before_ref[...] = before
        y = before * (m_ref[...] / norm)

        @pl.when(j >= 2 * k_tiles)
        def _():
            q_ref[...] = turn(y, cos_ref[...], sin_ref[...]).astype(jnp.bfloat16)

        for t in range(2 * k_tiles):

            @pl.when(j == t)
            def _(t=t):
                z = turn(y, cos_ref[...], sin_ref[...]) if t < k_tiles else y
                kv_ref[:, TILE * t : TILE * (t + 1)] = z.astype(jnp.bfloat16)

    @pl.when(j >= 2 * k_tiles + q_tiles)
    def _():
        norm, cross = column_norms(w, gram_ref[0], b, dot_f32(a, w))
        n_ref[...] = norm
        cross_ref[...] = cross

    @pl.when(j == 2 * k_tiles - 1)
    def _():
        for k in range(2):
            pl.when(q > 0)(lambda k=k: copy(k, sources[k], s, to_left, s - 2).start())
            pl.when(q < nc - 1)(lambda k=k: copy(k, sources[k], s, to_right, s + 2).start())
            copy(k, sources[k], s, to_sib, sibling).start()
            keep(k).start()

    def pass_on(chip):
        slot = 2 * chip + c
        for k in range(2):
            src = outs[k].at[slot]
            copy(k, src, slot, to_right, s).wait_recv()
            pl.when((chip < q) & (q < nc - 1))(
                lambda k=k, src=src: copy(k, src, slot, to_right, s + 2).start()
            )
            pl.when((chip > q) & (q > 0))(
                lambda k=k, src=src: copy(k, src, slot, to_left, s - 2).start()
            )
            copy(k, src, slot, to_sib, sibling).start()

    for i in range(1, nc):
        at = min(2 * k_tiles + 2 * i, 2 * k_tiles + 2 * q_tiles - 1)
        pl.when(j == at)(lambda i=i: pass_on(order[i]))

    @pl.when(j == last)
    def _():
        for k in range(2):
            keep(k).wait()
            for chip in range(nc):
                mine, theirs = 2 * chip + c, 2 * chip + 1 - c
                copy(k, outs[k].at[theirs], theirs, to_sib, sibling).wait_recv()
                copy(k, outs[k].at[mine], mine, to_sib, sibling).wait_send()
                pl.when((q < nc - 1) & (chip <= q))(
                    lambda k=k, mine=mine: copy(k, outs[k].at[mine], mine, to_right, s).wait_send()
                )
                pl.when((q > 0) & (chip >= q))(
                    lambda k=k, mine=mine: copy(k, outs[k].at[mine], mine, to_left, s).wait_send()
                )
        for chip in order[1:]:
            for i in range(len(plan)):
                share(i, chip).wait_send()
                share(i, chip).wait_recv()


def project_qkv(n, rows, u, inner, grams, a, weights, b, m, cosine, sine, sq, held, plan, collective_id):
    tokens, width = u.shape
    cols = b.shape[1]
    nc = n // 2
    per_half = weights.shape[2] // TILE
    q_tiles = width // TILE
    k_cols = weights.shape[2] - width
    k_tiles = k_cols // TILE
    kv_tiles = 2 * k_tiles
    full = lambda shape: pl.BlockSpec(shape, lambda j: (0,) * len(shape))

    def column(j):
        return jnp.where(j < kv_tiles, q_tiles + j, jnp.where(j < kv_tiles + q_tiles, j - kv_tiles, j))

    def which(j):
        return jnp.where(
            j < k_tiles, 1, jnp.where(j < kv_tiles, 2, jnp.where(j < kv_tiles + q_tiles, 0, 3))
        )

    def before_tile(j):
        return (0, column(jnp.minimum(j, kv_tiles + q_tiles - 1)))

    col = lambda height: pl.BlockSpec((height, TILE), lambda j: (0, column(j)))
    f32, low = jnp.float32, jnp.bfloat16
    hbm = pl.BlockSpec(memory_space=pltpu.HBM)
    dma = pltpu.SemaphoreType.DMA
    got = pl.pallas_call(
        functools.partial(project_kernel, n, rows, plan, k_tiles, q_tiles),
        out_shape=(
            pltpu.HBM((tokens, width + 2 * k_cols), f32),
            pltpu.HBM((tokens, width), low),
            pltpu.HBM((1, cols), f32),
            pltpu.HBM((16, cols), f32),
            pltpu.HBM((n, tokens, 2 * k_cols), low),
            pltpu.HBM((n, *sq.shape), f32),
            *(pltpu.HBM(held.shape[-3:], low) for _ in plan),
        ),
        grid=(cols // TILE,),
        in_specs=[
            full((tokens, width)),
            pl.BlockSpec((1, tokens, 16), lambda j: (jnp.minimum(which(j), 2), 0, 0)),
            pl.BlockSpec((1, 32, 16), lambda j: (which(j), 0, 0)),
            pl.BlockSpec((1, 16, width), lambda j: (which(j), 0, 0)),
            pl.BlockSpec((1, width, TILE), lambda j: (column(j) // per_half, 0, lax.rem(column(j), per_half))),
            col(16),
            col(1),
            full(cosine.shape),
            full(sine.shape),
            hbm,
            hbm,
        ],
        out_specs=(
            pl.BlockSpec((tokens, TILE), before_tile),
            pl.BlockSpec((tokens, TILE), lambda j: (0, jnp.clip(j - kv_tiles, 0, q_tiles - 1))),
            col(1),
            col(16),
            *([hbm] * (2 + len(plan))),
        ),
        scratch_shapes=[pltpu.VMEM((tokens, 2 * k_cols), low), dma((2,))]
        + [dma((2, n))] * 4
        + [dma((len(plan), nc))] * 2,
        compiler_params=pltpu.CompilerParams(
            collective_id=collective_id, has_side_effects=True, vmem_limit_bytes=40 << 20
        ),
        cost_estimate=pl.CostEstimate(
            flops=2 * tokens * width * cols, transcendentals=0, bytes_accessed=64 << 20
        ),
        name="project_qkv",
    )(*in_hbm(u), inner, grams, *in_hbm(a, weights, b), m, cosine, sine, *in_hbm(sq, held))
    return (*got[:6], got[6:])


def out_kernel(att_ref, a_ref, w_ref, b_ref, m_ref, n_ref, x_ref, gain_ref, next_ref,
               before_ref, x1_ref, u2_ref, inner_ref):
    t = pl.program_id(0)
    a = a_ref[0].astype(jnp.bfloat16)
    b = b_ref[...].astype(jnp.bfloat16)
    inner = dot_nt(att_ref[...], a).astype(jnp.bfloat16)
    before = dot_f32(att_ref[...], w_ref[0]) + SCALE * dot_f32(inner, b)
    before_ref[...] = before
    x1_ref[:, pl.ds(pl.multiple_of(t * TILE, TILE), TILE)] = (
        x_ref[...].astype(jnp.float32) + before * (m_ref[...] / n_ref[...])
    )

    @pl.when(t == pl.num_programs(0) - 1)
    def _():
        v = x1_ref[...]
        u2 = (v * unit_rms(v) * gain_ref[1:]).astype(jnp.bfloat16)
        u2_ref[...] = u2
        following = next_ref[...].reshape(-1, u2.shape[1]).astype(jnp.bfloat16)
        inner_ref[...] = jnp.zeros_like(inner_ref)
        inner_ref[:, : following.shape[0]] = dot_nt(u2, following).astype(jnp.bfloat16)


def project_out(att, a, weights, b, m, norms, x, gain, following):
    rows, width = att.shape
    tiles = width // TILE
    skip = (weights.shape[2] - width) // TILE
    full = lambda shape: pl.BlockSpec(shape, lambda t: (0,) * len(shape))
    col = lambda height: pl.BlockSpec((height, TILE), lambda t: (0, t))
    ahead = b.shape[1] // TILE - tiles
    later = lambda height: pl.BlockSpec((height, TILE), lambda t: (0, ahead + t))
    f32 = jnp.float32
    return pl.pallas_call(
        out_kernel,
        out_shape=(
            pltpu.HBM((rows, width), f32),
            pltpu.HBM((rows, width), f32),
            pltpu.HBM((rows, width), jnp.bfloat16),
            pltpu.HBM((rows, 128), jnp.bfloat16),
        ),
        grid=(tiles,),
        in_specs=[
            full((rows, width)),
            pl.BlockSpec((1, 16, width), lambda t: (3, 0, 0)),
            pl.BlockSpec((1, width, TILE), lambda t: (1, 0, skip + t)),
            later(16),
            later(1),
            later(1),
            col(rows),
            full((2, width)),
            full(following.shape),
        ],
        out_specs=(col(rows), full((rows, width)), full((rows, width)), full((rows, 128))),
        compiler_params=pltpu.CompilerParams(vmem_limit_bytes=40 << 20),
        cost_estimate=pl.CostEstimate(
            flops=2 * rows * width * width, transcendentals=0, bytes_accessed=2 * width * width
        ),
        name="project_out",
    )(*in_hbm(att, a, weights, b), m, norms, *in_hbm(x), gain, *in_hbm(following))


def out_back_kernel(in_ref, x1_ref, gain_ref, gy_ref, before_ref, att_ref, a_ref, b_ref, m_ref, n_ref, cross_ref,
                    w_ref, gx_ref, gatt_ref, ga_ref, gb_ref, gm_ref, lhs, gi, tail):
    t = pl.program_id(0)
    rows, width = gx_ref.shape
    low = jnp.bfloat16
    a = a_ref[0].astype(low)
    o_cols = slice(b_ref.shape[1] - width, b_ref.shape[1])

    @pl.when(t == 0)
    def _():
        gx = gy_ref[...].astype(jnp.float32) + rms_back(x1_ref[...], gain_ref[1:], in_ref[...])
        gx_ref[...] = gx
        norm, m = n_ref[:, o_cols], m_ref[:, o_cols]
        gb = (gx * (m / norm)).astype(low)
        lhs[:rows] = gb
        b = b_ref[:, o_cols].astype(low)
        gi[...] = (SCALE * dot_nt(gb, b)).astype(low)
        gm = jnp.sum(gx * before_ref[...], axis=0, keepdims=True) / norm
        gm_ref[...] = gm
        c = -gm * m / (norm * norm)
        weighted = (b.astype(jnp.float32) * c).astype(low)
        lhs[rows:] = weighted
        tail[...] = two_terms(dot_nt(weighted, b))
        inner = dot_nt(att_ref[...], a).astype(low)
        gb_ref[...] = SCALE * dot_tn(inner, gb) + SCALE * c * cross_ref[:, o_cols]

    span = pl.ds(pl.multiple_of(t * TILE, TILE), TILE)
    a_tile = a_ref[0, :, span].astype(low)
    gi_low = gi[...]
    back = dot_nt(lhs[...], w_ref[0, :, w_ref.shape[2] - width :])
    gatt_ref[...] = (back[:rows] + dot_f32(gi_low, a_tile)).astype(low)
    spread = back[rows:] + SCALE * dot_two(tail[...], a_tile)
    ga_ref[...] = dot_tn(gi_low, att_ref[:, span]) + SCALE * spread


def out_back(in_grad, x1, gain, gy, before, att, a, b, m, norms, cross, weights):
    rows, width = x1.shape
    tiles = width // TILE
    full = lambda shape: pl.BlockSpec(shape, lambda t: (0,) * len(shape))
    col = lambda height: pl.BlockSpec((height, TILE), lambda t: (0, t))
    f32, low = jnp.float32, jnp.bfloat16
    wide = full((rows, width))
    return pl.pallas_call(
        out_back_kernel,
        out_shape=(
            pltpu.HBM((rows, width), f32),
            pltpu.HBM((rows, width), low),
            jax.ShapeDtypeStruct((16, width), f32),
            jax.ShapeDtypeStruct((16, width), f32),
            jax.ShapeDtypeStruct((1, width), f32),
        ),
        grid=(tiles,),
        in_specs=[wide, wide, full((2, width)), wide, wide, wide,
                  pl.BlockSpec((1, 16, width), lambda t: (3, 0, 0)),
                  full(b.shape), full(m.shape), full(norms.shape), full(cross.shape),
                  pl.BlockSpec((1, TILE, weights.shape[2]), lambda t: (1, t, 0))],
        out_specs=(wide, col(rows), col(16), full((16, width)), full((1, width))),
        scratch_shapes=[
            pltpu.VMEM((rows + 16, width), low),
            pltpu.VMEM((rows, 16), low),
            pltpu.VMEM((32, 16), low),
        ],
        compiler_params=pltpu.CompilerParams(vmem_limit_bytes=48 << 20),
        cost_estimate=pl.CostEstimate(flops=0, transcendentals=0, bytes_accessed=1 << 20),
        name="out_back",
    )(*in_hbm(in_grad, x1), gain, *in_hbm(gy, before, att, a, b), m, norms, *in_hbm(cross, weights))


def qkv_back_kernel(gq_ref, gkv_ref, cos_ref, sin_ref, before_ref, u_ref, inner_ref, a_ref, b_ref, m_ref, n_ref, cross_ref,
                    x_ref, gain_ref, gx_ref, w0_ref, w1_ref,
                    out_ref, ga_ref, gb_ref, gm_ref, lhs0, lhs1, gi, tail):
    t = pl.program_id(0)
    rows, width = gx_ref.shape
    low = jnp.bfloat16
    k_cols = w1_ref.shape[2]
    bounds = [(0, width), (width, width + k_cols), (width + k_cols, width + 2 * k_cols)]

    @pl.when(t == 0)
    def _():
        cosine, sine = cos_ref[...], -sin_ref[...]
        k_parts = [gkv_ref[:, 256 * j : 256 * j + 128] for j in range(k_cols // 128)]
        v_parts = [gkv_ref[:, 256 * j + 128 : 256 * j + 256] for j in range(k_cols // 128)]
        rounded = lambda z: z.astype(low).astype(jnp.float32)
        ups = [
            turn(gq_ref[...].astype(jnp.float32), cosine, sine),
            turn(rounded(jnp.concatenate(k_parts, axis=1)), cosine, sine),
            rounded(jnp.concatenate(v_parts, axis=1)),
        ]
        lhs0[rows:] = jnp.zeros_like(lhs0[rows:])
        lhs1[rows:] = jnp.zeros_like(lhs1[rows:])
        for p, (start, stop) in enumerate(bounds):
            g, norm, m = ups[p], n_ref[:, start:stop], m_ref[:, start:stop]
            b = b_ref[:, start:stop].astype(low)
            gb = (g * (m / norm)).astype(low)
            gm = jnp.sum(g * before_ref[:, start:stop], axis=0, keepdims=True) / norm
            gm_ref[:, start:stop] = gm
            c = -gm * m / (norm * norm)
            weighted = (b.astype(jnp.float32) * c).astype(low)
            gi[:, 16 * p : 16 * p + 16] = (SCALE * dot_nt(gb, b)).astype(low)
            tail[p] = two_terms(dot_nt(weighted, b))
            gb_ref[:, start:stop] = SCALE * dot_tn(inner_ref[p], gb) + SCALE * c * cross_ref[:, start:stop]
            lhs, at = (lhs1, 0) if p == 2 else (lhs0, start)
            lhs[:rows, at : at + stop - start] = gb
            lhs[rows + 16 * p : rows + 16 * p + 16, at : at + stop - start] = weighted

    span = pl.ds(pl.multiple_of(t * TILE, TILE), TILE)
    back = dot_nt(lhs0[...], w0_ref[0]) + dot_nt(lhs1[...], w1_ref[0])
    grad_in = back[:rows]
    for p in range(3):
        a_tile = a_ref[p, :, span].astype(low)
        gi_p = gi[:, 16 * p : 16 * p + 16]
        grad_in = grad_in + dot_f32(gi_p, a_tile)
        spread = back[rows + 16 * p : rows + 16 * p + 16] + SCALE * dot_two(tail[p], a_tile)
        ga_ref[p] = dot_tn(gi_p, u_ref[:, span]) + SCALE * spread
    out_ref[:, span] = grad_in

    @pl.when(t == pl.num_programs(0) - 1)
    def _():
        v = x_ref[...].astype(jnp.float32)
        out_ref[...] = gx_ref[...] + rms_back(v, gain_ref[:1], out_ref[...])


def qkv_back(gq, gkv, cosine, sine, before, u, inner, a, b, m, norms, cross, x, gain, gx, weights):
    rows, width = gx.shape
    cols = before.shape[1]
    k_cols = (cols - width) // 2
    tiles = width // TILE
    full = lambda shape: pl.BlockSpec(shape, lambda t: (0,) * len(shape))
    f32, low = jnp.float32, jnp.bfloat16
    wide = full((rows, width))
    return pl.pallas_call(
        qkv_back_kernel,
        out_shape=(
            pltpu.HBM((rows, width), f32),
            jax.ShapeDtypeStruct((3, 16, width), f32),
            jax.ShapeDtypeStruct((16, cols), f32),
            jax.ShapeDtypeStruct((1, cols), f32),
        ),
        grid=(tiles,),
        in_specs=[wide, full(gkv.shape), full(cosine.shape), full(sine.shape), full((rows, cols)), wide, full(inner.shape),
                  full(a.shape), full(b.shape), full(m.shape), full(norms.shape), full(cross.shape),
                  wide, full((2, width)), wide,
                  pl.BlockSpec((1, TILE, width + k_cols), lambda t: (0, t, 0)),
                  pl.BlockSpec((1, TILE, k_cols), lambda t: (1, t, 0))],
        out_specs=(wide, pl.BlockSpec((3, 16, TILE), lambda t: (0, 0, t)), full((16, cols)), full((1, cols))),
        scratch_shapes=[
            pltpu.VMEM((rows + 48, width + k_cols), low),
            pltpu.VMEM((rows + 48, k_cols), low),
            pltpu.VMEM((rows, 48), low),
            pltpu.VMEM((3, 32, 16), low),
        ],
        compiler_params=pltpu.CompilerParams(vmem_limit_bytes=48 << 20),
        cost_estimate=pl.CostEstimate(flops=0, transcendentals=0, bytes_accessed=1 << 20),
        name="qkv_back",
    )(*in_hbm(gq), gkv, cosine, sine, *in_hbm(before, u), inner, *in_hbm(a, b), m, norms, *in_hbm(cross, x), gain,
      *in_hbm(gx, weights, weights))

MESH = pl.DeviceIdType.MESH


def place_in_seq():
    s = lax.axis_index("seq")
    return s, s // 2, lax.rem(s, 2)

def near_first(i, q, nc):
    short = jnp.where(q <= nc - 1 - q, q, nc - 1 - q)
    far = jnp.where(q <= nc - 1 - q, i, nc - 1 - i)
    step = (i + 1) // 2
    near = q - step if i % 2 else q + step
    return jnp.where(i <= 2 * short, near, far)


def place_in_rows(rows):
    half = rows // 2
    r = lax.axis_index("rows")
    a, b = r // 2, lax.rem(r, 2)
    turned = lambda k: 2 * lax.rem(a + k + half, half)
    return r, 2 * a + 1 - b, lambda k: turned(k) + b, lambda k: turned(k) + 1 - b


def greet_all(n, rows):
    s = lax.axis_index("seq")
    r, b_row, a_row, _ = place_in_rows(rows)
    barrier = pltpu.get_barrier_semaphore()
    for t in range(1, n):
        pl.semaphore_signal(
            barrier, inc=1, device_id=(r, lax.rem(s + t, n)), device_id_type=MESH
        )
    pl.semaphore_signal(barrier, inc=1, device_id=(b_row, s), device_id_type=MESH)
    for k in range(1, rows // 2):
        pl.semaphore_signal(barrier, inc=1, device_id=(a_row(k), s), device_id_type=MESH)
    pl.semaphore_wait(barrier, n - 1 + rows // 2)


def remote(src, dst, send, recv, row, seq):
    return pltpu.make_async_remote_copy(
        src_ref=src, dst_ref=dst, send_sem=send, recv_sem=recv,
        device_id=(row, seq), device_id_type=MESH,
    )


def weights_kernel(n, rows, qo, kv, xg, wd_hbm, ad_hbm, bd_hbm, x_hbm, gain_ref, aa_hbm, ag_hbm, gy_hbm,
                   wa, gz, near, sq_ref, gram_ref, u_hbm, inner_ref, gy0_hbm, gy1_hbm,
                   wd, ad_ref, bd_ref, x_ref, aa_ref, ag_ref, gy_ref, own_ref, cols_ref, local, edge, a_in, a_sib_in, a_out, a_sib_out, z_in, z_out):
    nc, half = n // 2, rows // 2
    others = half - 1
    units = gz.shape[-1]
    s, q, c = place_in_seq()
    sibling = s + 1 - 2 * c
    r, b_row, a_row, diagonal = place_in_rows(rows)
    greet_all(n, rows)

    both, first, second = pl.ds(0, 2), pl.ds(0, 1), pl.ds(1, 1)
    LINE, FROM_B = 0, 1

    def from_a(k):
        return 1 + k

    def relay_b(k):
        return 1 + others + k

    def relay_a(k):
        return 1 + 2 * others + k

    def a_view(p, core, parts, row):
        return wa.at[parts, 2 * p + core, row]

    def content(kind):
        if kind == LINE:
            return both, r
        if kind == FROM_B:
            return both, b_row
        for k in range(1, half):
            if kind == from_a(k):
                return both, a_row(-k)
            if kind == relay_b(k):
                return second, diagonal(-k)
            if kind == relay_a(k):
                return first, diagonal(-k)

    kinds = 2 + 3 * others

    def a_send(p, parts, row, kind, target_row):
        return remote(
            a_view(p, c, parts, row), a_view(p, c, parts, row),
            a_out.at[p, kind], a_in.at[p, kind], target_row, s,
        )

    def a_arrival(p, kind):
        parts, row = content(kind)
        return a_send(p, parts, row, kind, r)

    def a_to_sibling(p, kind, core):
        parts, row = content(kind)
        return remote(
            a_view(p, core, parts, row), a_view(p, core, parts, row),
            a_sib_out.at[p, kind], a_sib_in.at[p, kind], r, sibling,
        )

    def columns(device):
        return pl.ds(pl.multiple_of(device * units, units), units)

    def z_send(p, core):
        return remote(
            xg.at[:, r, :, columns(2 * p + core)], gz.at[:, s],
            z_out.at[p, core], z_in.at[q, c], r, 2 * p + core,
        )

    def z_arrival(p, core):
        slot = gz.at[:, 2 * p + core]
        return remote(slot, slot, z_out.at[p, core], z_in.at[p, core], r, s)

    def line_send(p, sem, target):
        view = a_view(p, c, both, r)
        return remote(view, view, sem, a_in.at[p, LINE], r, target)

    wide, k_cols = qo.shape[-1], kv.shape[-1]
    blocks = [(qo, 0, 0), (kv, 0, wide), (kv, 1, 0), (qo, 1, k_cols)]

    def own_blocks(part, out):
        for source, i, start in blocks:
            columns_of = pl.ds(start, source.shape[-1])
            out(source.at[i, part], i, columns_of)

    def own_line(sem, target):
        own_blocks(
            r,
            lambda src, i, cols: remote(
                src, wa.at[i, s, r, :, cols], sem, a_in.at[q, LINE], r, target
            ).start(),
        )

    pl.when(q > 0)(lambda: own_line(edge.at[0], s - 2))
    pl.when(q < nc - 1)(lambda: own_line(edge.at[1], s + 2))
    order = [near_first(i, q, nc) for i in range(nc)]
    whole_block = wa.at[:, s]
    sib_a = lambda: remote(whole_block, whole_block, edge.at[2], edge.at[3], r, sibling)
    sib_g = lambda: remote(
        xg.at[:, :, :, columns(sibling)], near.at[:, c], edge.at[4], edge.at[5], r, sibling
    )
    keep_a = pltpu.make_async_copy(own_ref, whole_block, local.at[0])
    keep_g = pltpu.make_async_copy(cols_ref, near.at[:, c], local.at[1])
    all_parts = pl.ds(0, rows)
    own_blocks(
        all_parts,
        lambda src, i, cols: remote(
            src, wa.at[i, s, :, :, cols], edge.at[2], edge.at[3], r, sibling
        ).start(),
    )
    own_blocks(
        all_parts,
        lambda src, i, cols: pltpu.make_async_copy(
            src, own_ref.at[i, :, :, cols], local.at[12]
        ).start(),
    )
    take_cols = pltpu.make_async_copy(xg.at[:, :, :, columns(s)], cols_ref, local.at[13])
    take_cols.start()
    takes = [
        pltpu.make_async_copy(src, dst, local.at[5 + i])
        for i, (src, dst) in enumerate(
            [(x_hbm, x_ref), (aa_hbm, aa_ref), (ag_hbm, ag_ref), (ad_hbm, ad_ref), (bd_hbm, bd_ref), (wd_hbm, wd),
             (gy_hbm, gy_ref)]
        )
    ]
    for cp in takes:
        cp.start()
    for cp in takes:
        cp.wait()
    pltpu.make_async_copy(own_ref, own_ref, local.at[12]).wait()
    keep_a.start()
    take_cols.wait()
    keep_g.start()
    low = jnp.bfloat16
    v = x_ref[...].astype(jnp.float32)
    u = (v * unit_rms(v) * gain_ref[:1]).astype(low)
    x_ref[...] = u
    keep_u = pltpu.make_async_copy(x_ref, u_hbm, local.at[2])
    keep_u.start()
    tokens = x_ref.shape[0] // 2
    halves = [
        pltpu.make_async_copy(gy_ref.at[pl.ds(tokens * k, tokens)], out, local.at[3 + k])
        for k, out in enumerate((gy0_hbm, gy1_hbm))
    ]
    for cp in halves:
        cp.start()
    for g in range(4):
        a = aa_ref[g].astype(low)
        gram_ref[g] = two_terms(dot_nt(a, a))
        if g < 3:
            inner_ref[g] = dot_nt(u, a).astype(low)
    for g in range(2):
        a = ag_ref[g].astype(low)
        gram_ref[4 + g] = two_terms(dot_nt(a, a))

    def down_squares():
        a = ad_ref[...].astype(low)
        gram_ref[6] = two_terms(dot_nt(a, a))
        mine = pl.ds(pl.multiple_of(s * wd.shape[0], wd.shape[0]), wd.shape[0])
        cross = dot_f32(ad_ref[:, mine].astype(low), wd[...])
        b_wide = bd_ref[...].astype(low).astype(jnp.float32)
        sq_ref[...] = column_squares(wd[...]) + 2.0 * SCALE * jnp.sum(b_wide * cross, axis=0, keepdims=True)

    for p in order[1:]:
        a_arrival(p, LINE).wait_recv()
        pl.when((p < q) & (q < nc - 1))(
            lambda p=p: line_send(p, a_out.at[p, LINE], s + 2).start()
        )
        pl.when((p > q) & (q > 0))(
            lambda p=p: line_send(p, a_out.at[p, LINE], s - 2).start()
        )
        a_send(p, both, r, FROM_B, b_row).start()
        for k in range(1, half):
            a_send(p, both, r, from_a(k), a_row(k)).start()
        a_to_sibling(p, LINE, c).start()
    for p in order[1:]:
        for core in range(2):
            z_send(p, core).start()
    sib_g().start()
    down_squares()
    keep_u.wait()
    for cp in halves:
        cp.wait()
    for p in order[1:]:
        a_arrival(p, FROM_B).wait_recv()
        for k in range(1, half):
            a_send(p, first, b_row, relay_a(k), a_row(k)).start()
        a_to_sibling(p, FROM_B, c).start()
        for k in range(1, half):
            a_arrival(p, from_a(k)).wait_recv()
            a_send(p, second, a_row(-k), relay_b(k), b_row).start()
            a_to_sibling(p, from_a(k), c).start()
    for p in order[1:]:
        for k in range(1, half):
            for kind in (relay_b(k), relay_a(k)):
                a_arrival(p, kind).wait_recv()
                a_to_sibling(p, kind, c).start()
    keep_a.wait()
    keep_g.wait()
    sib_a().wait()
    sib_g().wait()
    pl.when(q > 0)(lambda: line_send(q, edge.at[0], s).wait_send())
    pl.when(q < nc - 1)(lambda: line_send(q, edge.at[1], s).wait_send())
    for p in order[1:]:
        pl.when(((p < q) & (q < nc - 1)) | ((p > q) & (q > 0)))(
            lambda p=p: line_send(p, a_out.at[p, LINE], s).wait_send()
        )
        for kind in range(kinds):
            a_to_sibling(p, kind, c).wait_send()
            a_to_sibling(p, kind, 1 - c).wait_recv()
        a_send(p, both, r, FROM_B, b_row).wait_send()
        for k in range(1, half):
            a_send(p, both, r, from_a(k), r).wait_send()
            a_send(p, first, b_row, relay_a(k), r).wait_send()
            a_send(p, second, a_row(-k), relay_b(k), r).wait_send()
        for core in range(2):
            z_send(p, core).wait_send()
            z_arrival(p, core).wait_recv()


def gather_weights(n, rows, qo, kv, xg, wd, ad, bd, x, gains, aa, ag, gy, collective_id):
    nc = n // 2
    _, block, width = qo.shape
    part = block // rows
    cols = width + kv.shape[2]
    qo = qo.reshape(2, rows, part, width)
    kv = kv.reshape(2, rows, part, kv.shape[2])
    xg = xg.reshape(2, rows, part, xg.shape[2])
    units = xg.shape[3] // n
    kinds = 2 + 3 * (rows // 2 - 1)
    dma = pltpu.SemaphoreType.DMA
    anywhere = pl.BlockSpec(memory_space=pltpu.HBM)
    vmem = pl.BlockSpec(memory_space=pltpu.VMEM)
    low = qo.dtype
    wa, gz, near, sq, grams, u, inner, *halves = pl.pallas_call(
        functools.partial(weights_kernel, n, rows),
        out_shape=(
            pltpu.HBM((2, n, rows, part, cols), low),
            pltpu.HBM((2, n, part, units), low),
            pltpu.HBM((2, 2, rows, part, units), low),
            jax.ShapeDtypeStruct((1, width), jnp.float32),
            jax.ShapeDtypeStruct((7, 32, 16), low),
            pltpu.HBM(x.shape, low),
            jax.ShapeDtypeStruct((3, x.shape[0], 16), low),
            *([pltpu.HBM((gy.shape[0] // 2, width), low)] * 2),
        ),
        in_specs=[anywhere] * 7 + [vmem] + [anywhere] * 3,
        out_specs=(anywhere,) * 3 + (vmem,) * 2 + (anywhere, vmem) + (anywhere,) * 2,
        scratch_shapes=[pltpu.VMEM(v.shape, v.dtype) for v in (wd, ad, bd, x, aa, ag, gy)]
        + [pltpu.VMEM((2, rows, part, cols), low), pltpu.VMEM((2, rows, part, units), low)]
        + [dma((14,)), dma((6,))]
        + [dma((nc, kinds))] * 4
        + [dma((nc, 2))] * 2,
        compiler_params=pltpu.CompilerParams(
            collective_id=collective_id, has_side_effects=True, vmem_limit_bytes=32 << 20
        ),
        cost_estimate=pl.CostEstimate(
            flops=0, transcendentals=0, bytes_accessed=250 * 1024 * 1024
        ),
        name="gather_weights",
    )(*in_hbm(qo, kv, xg, wd, ad, bd, x), gains, *in_hbm(aa, ag, gy))
    return wa.reshape(2, n * block, cols), gz, near, sq, grams, u, inner, halves


def gather_kernel(n, rows, count, shared, *refs):
    nc = n // 2
    sources = refs[: count + len(shared[0])]
    outs = refs[len(sources) : 2 * len(sources) - len(shared[0]) + len(shared[1])]
    scratch = refs[len(sources) + len(outs) :]
    held_here = scratch[:count]
    local_sem, to_sib, to_left, to_right, recv, share_out, share_in = scratch[count:]
    xs, held, swapped = sources[:count], sources[count:], outs[count:]
    s, q, c = place_in_seq()
    sibling = s + 1 - 2 * c
    r, b_row, a_row, _ = place_in_rows(rows)
    greet_all(n, rows)
    takes = [pltpu.make_async_copy(xs[k], held_here[k], local_sem.at[0, k]) for k in range(count)]
    keeps = [
        pltpu.make_async_copy(held_here[k], outs[k].at[s], local_sem.at[1, k]) for k in range(count)
    ]
    for cp in takes:
        cp.start()

    def copy(k, src, slot, sems, target):
        return remote(src, outs[k].at[slot], sems.at[k, slot], recv.at[k, slot], r, target)

    def share(i, p):
        source, piece, turn, _ = shared[1][i]
        pair = pl.ds(2 * p, 2)
        src = held[source].at[pair] if piece is None else held[source].at[piece, pair]
        target = b_row if turn == 0 else a_row(turn)
        return remote(src, swapped[i].at[pair], share_out.at[i, p], share_in.at[i, p], target, s)

    for k in range(count):
        pl.when(q > 0)(lambda k=k: copy(k, xs[k], s, to_left, s - 2).start())
        pl.when(q < nc - 1)(lambda k=k: copy(k, xs[k], s, to_right, s + 2).start())
        copy(k, xs[k], s, to_sib, sibling).start()
    order = [near_first(i, q, nc) for i in range(nc)]
    for p in order[1:]:
        for i in range(len(shared[1])):
            share(i, p).start()
    for take, keep in zip(takes, keeps):
        take.wait()
        keep.start()
    for p in order[1:]:
        slot = 2 * p + c
        for k in range(count):
            src = outs[k].at[slot]
            copy(k, src, slot, to_right, s).wait_recv()
            pl.when((p < q) & (q < nc - 1))(
                lambda k=k, src=src, slot=slot: copy(k, src, slot, to_right, s + 2).start()
            )
            pl.when((p > q) & (q > 0))(
                lambda k=k, src=src, slot=slot: copy(k, src, slot, to_left, s - 2).start()
            )
            copy(k, src, slot, to_sib, sibling).start()
    for cp in keeps:
        cp.wait()
    for p in range(nc):
        mine, theirs = 2 * p + c, 2 * p + 1 - c
        for k in range(count):
            copy(k, outs[k].at[theirs], theirs, to_sib, sibling).wait_recv()
            copy(k, outs[k].at[mine], mine, to_sib, sibling).wait_send()
            pl.when((q < nc - 1) & (p <= q))(
                lambda k=k, mine=mine: copy(k, outs[k].at[mine], mine, to_right, s).wait_send()
            )
            pl.when((q > 0) & (p >= q))(
                lambda k=k, mine=mine: copy(k, outs[k].at[mine], mine, to_left, s).wait_send()
            )
    for p in order[1:]:
        for i in range(len(shared[1])):
            share(i, p).wait_send()
            share(i, p).wait_recv()


def gather_seq(n, rows, arrays, collective_id, held=(), shares=()):
    nc, count = n // 2, len(arrays)
    nbytes = sum(a.size * a.dtype.itemsize for a in arrays)
    dma = pltpu.SemaphoreType.DMA
    shape = jax.ShapeDtypeStruct
    outs = [shape((n, *a.shape), a.dtype) for a in arrays]
    outs += [shape(held[source].shape[-3:], held[source].dtype) for source, _, _ in shares]
    anywhere = pl.BlockSpec(memory_space=pltpu.HBM)
    listed = (tuple(held), [(source, piece, turn, None) for source, piece, turn in shares])
    sems = dma((max(1, len(shares)), nc))
    got = pl.pallas_call(
        functools.partial(gather_kernel, n, rows, count, (range(len(held)), listed[1])),
        out_shape=tuple(outs),
        in_specs=[anywhere] * (count + len(held)),
        out_specs=(anywhere,) * len(outs),
        scratch_shapes=[pltpu.VMEM(a.shape, a.dtype) for a in arrays]
        + [dma((2, count))]
        + [dma((count, n))] * 4
        + [sems] * 2,
        compiler_params=pltpu.CompilerParams(collective_id=collective_id, has_side_effects=True),
        cost_estimate=pl.CostEstimate(flops=0, transcendentals=0, bytes_accessed=nbytes * n * 20),
        name="gather_seq",
    )(*arrays, *held)
    return got[:count], got[count:]

def swap_halves(x):
    return pltpu.roll(x.astype(jnp.float32), HEAD_DIM, 1)


def stack_heads(block):
    lane = lax.broadcasted_iota(jnp.int32, (block.shape[0], 128), 1)
    rows = []
    for h in range(8):
        pair = block[:, (h // 2) * 128 : (h // 2 + 1) * 128].astype(jnp.float32)
        if h % 2 != h // 4:
            pair = swap_halves(pair)
        keep = lane < HEAD_DIM if h // 4 == 0 else lane >= HEAD_DIM
        rows.append(jnp.where(keep, pair, 0.0).astype(jnp.bfloat16))
    return jnp.concatenate(rows, axis=0)


def unstack_heads(stacked, span):
    lane = lax.broadcasted_iota(jnp.int32, (span, 128), 1)
    pairs = []
    for t in range(4):
        first = stacked[2 * t * span : (2 * t + 1) * span]
        second = stacked[(2 * t + 1) * span : (2 * t + 2) * span]
        if t < 2:
            second = swap_halves(second)
        else:
            first = swap_halves(first)
        pairs.append(jnp.where(lane < HEAD_DIM, first, second))
    return jnp.concatenate(pairs, axis=1)


def key_blocks(kv_ref, j):
    n, _, span, width = kv_ref.shape
    pick = lambda start: kv_ref[:, 0, :, start : start + 128].reshape(n * span, 128)
    return pick(128 * j), pick(width // 2 + 128 * j)


def attend_kernel(valid_ref, q_ref, kv_ref, o_ref, p_ref, s_ref):
    span = q_ref.shape[1]
    keys = kv_ref.shape[0] * span
    q_pos = lax.axis_index("seq") * span + lax.broadcasted_iota(jnp.int32, (span, 1), 0)
    limit = jnp.minimum(q_pos + 1, valid_ref[pl.program_id(0)])
    allowed = lax.broadcasted_iota(jnp.int32, (span, keys), 1) < limit
    for j in range(p_ref.shape[1]):
        at = slice(512 * j, 512 * (j + 1))
        q8 = stack_heads(q_ref[0, :, at]) * jnp.bfloat16(HEAD_DIM**-0.5)
        k2, v2 = key_blocks(kv_ref, j)
        s_ref[j % 2] = dot_nt(q8, k2)
        for h in range(8):
            head = slice(h * span, (h + 1) * span)
            scores = jnp.where(allowed, s_ref[j % 2, head], -1e30)
            unscaled = jnp.exp(scores - jnp.max(scores, axis=1, keepdims=True))
            shares = unscaled * (1.0 / jnp.sum(unscaled, axis=1, keepdims=True))
            p_ref[0, j, head] = shares.astype(jnp.bfloat16)
        o_ref[0, :, at] = unstack_heads(dot_f32(p_ref[0, j], v2), span).astype(jnp.bfloat16)


def attend(q, kv, valid):
    pair, span, width = q.shape
    n, kv_width = kv.shape[0], kv.shape[3] // 2
    groups = kv_width // 128
    keys = n * span
    q_spec = pl.BlockSpec((1, span, width), lambda p, *_: (p, 0, 0))
    flops = 4 * pair * groups * 8 * span * keys * 128
    return pl.pallas_call(
        attend_kernel,
        out_shape=(
            pltpu.HBM(q.shape, jnp.bfloat16),
            pltpu.HBM((pair, groups, 8 * span, keys), jnp.bfloat16),
        ),
        grid_spec=pltpu.PrefetchScalarGridSpec(
            num_scalar_prefetch=1,
            grid=(pair,),
            in_specs=[q_spec, pl.BlockSpec((n, 1, span, 2 * kv_width), lambda p, *_: (0, p, 0, 0))],
            out_specs=(
                q_spec,
                pl.BlockSpec((1, groups, 8 * span, keys), lambda p, *_: (p, 0, 0, 0)),
            ),
            scratch_shapes=[pltpu.VMEM((2, 8 * span, keys), jnp.float32)],
        ),
        compiler_params=pltpu.CompilerParams(vmem_limit_bytes=40 << 20),
        cost_estimate=pl.CostEstimate(
            flops=flops, transcendentals=flops // 512, bytes_accessed=8 << 20
        ),
        name="attend",
    )(valid, *in_hbm(q, kv))


def attend_back_kernel(q_ref, kv_ref, p_ref, g_ref, gq_ref, gkv_ref, s_ref, g_scores):
    span = q_ref.shape[1]
    n = kv_ref.shape[0]
    for j in range(p_ref.shape[1]):
        at = slice(512 * j, 512 * (j + 1))
        q8 = stack_heads(q_ref[0, :, at]) * jnp.bfloat16(HEAD_DIM**-0.5)
        g8 = stack_heads(g_ref[0, :, at])
        k2, v2 = key_blocks(kv_ref, j)
        s_ref[j % 2] = dot_nt(g8, v2)
        for h in range(8):
            head = slice(h * span, (h + 1) * span)
            shares = p_ref[0, j, head].astype(jnp.float32)
            weighted = shares * s_ref[j % 2, head]
            centre = jnp.sum(weighted, axis=1, keepdims=True)
            g_scores[j % 2, head] = (weighted - shares * centre).astype(jnp.bfloat16)
        grad_scores = g_scores[j % 2]
        gq = dot_f32(grad_scores, k2) * HEAD_DIM**-0.5
        gq_ref[0, :, at] = unstack_heads(gq, span).astype(jnp.bfloat16)
        both = jnp.concatenate([dot_tn(grad_scores, q8), dot_tn(p_ref[0, j], g8)], axis=1)
        gkv_ref[:, 0, :, 256 * j : 256 * (j + 1)] = both.astype(jnp.bfloat16).reshape(n, span, 256)


def attend_back(q, kv, shares, g):
    pair, span, width = q.shape
    n, kv_width = kv.shape[0], kv.shape[3] // 2
    groups = kv_width // 128
    keys = n * span
    q_spec = pl.BlockSpec((1, span, width), lambda p: (p, 0, 0))
    kv_spec = pl.BlockSpec((n, 1, span, 2 * kv_width), lambda p: (0, p, 0, 0))
    return pl.pallas_call(
        attend_back_kernel,
        out_shape=(
            pltpu.HBM(q.shape, jnp.bfloat16),
            pltpu.HBM(kv.shape, jnp.bfloat16),
        ),
        grid=(pair,),
        in_specs=[
            q_spec,
            kv_spec,
            pl.BlockSpec((1, groups, 8 * span, keys), lambda p: (p, 0, 0, 0)),
            q_spec,
        ],
        out_specs=(q_spec, kv_spec),
        scratch_shapes=[
            pltpu.VMEM((2, 8 * span, keys), jnp.float32),
            pltpu.VMEM((2, 8 * span, keys), jnp.bfloat16),
        ],
        compiler_params=pltpu.CompilerParams(vmem_limit_bytes=48 << 20),
        cost_estimate=pl.CostEstimate(flops=0, transcendentals=0, bytes_accessed=1 << 20),
        name="attend_back",
    )(*in_hbm(q, kv, shares, g))

def by_distance(i, q, nc):
    room = nc - 1 - q
    left_half = q <= room
    short = jnp.where(left_half, q, room)
    far = jnp.where(left_half, i, nc - 1 - i)
    step = (i + 1) // 2
    near = jnp.where(lax.rem(i, 2) == 1, q - step, q + step)
    return jnp.where(i <= 2 * short, near, far)


def ffn_kernel(n, rows, pieces, u_hbm, inner_hbm, gy0_hbm, gy1_hbm, wd_hbm, a_ref, b_ref, m_ref, ad_ref, bd_ref, md_ref, sq_ref, gram_ref,
               in_ref, down0_hbm, down1_hbm, ga_ref, gb_ref, gm_ref, norm_ref, gad_ref, gbd_ref, gmd_ref, nd_ref,
               w_parts, wd, u, side, gy, down, own, theirs, sib, from_left, from_right, ratio, cross, gm_all,
               w_sem, load_sem, down_sem, small_out, small_in, to_sib, sib_in, to_right, right_in, to_left, left_in):
    nc = n // 2
    f32, low = jnp.float32, jnp.bfloat16
    s, q, c = place_in_seq()
    tokens = own.shape[1]

    weights = [pltpu.make_async_copy(wd_hbm, wd, w_sem.at[0])]
    for src, dst in place_pieces(n, rows, pieces, w_parts):
        weights.append(pltpu.make_async_copy(src, dst, w_sem.at[len(weights)]))
    for cp in weights:
        cp.start()

    def loads(i):
        p = by_distance(nc - 1 - i, q, nc)
        slot = lax.rem(i, 2)
        pair = pl.ds(2 * p, 2)
        return (
            pltpu.make_async_copy(u_hbm.at[pair], u.at[slot], load_sem.at[0, slot]),
            pltpu.make_async_copy(
                gy0_hbm.at[pair], gy.at[slot, :, : tokens // 2], load_sem.at[1, slot]
            ),
            pltpu.make_async_copy(
                gy1_hbm.at[pair], gy.at[slot, :, tokens // 2 :], load_sem.at[2, slot]
            ),
            pltpu.make_async_copy(inner_hbm.at[pair], side.at[slot], load_sem.at[3, slot]),
        )

    for cp in loads(0):
        cp.start()
    sibling = s + 1 - 2 * c
    barrier = pltpu.get_barrier_semaphore()
    for t in range(1, n):
        pl.semaphore_signal(
            barrier, inc=1, device_id={"seq": lax.rem(s + t, n)}, device_id_type=MESH
        )

    def to_sibling(p):
        return pltpu.make_async_remote_copy(
            src_ref=theirs.at[p], dst_ref=sib.at[p], send_sem=to_sib.at[p], recv_sem=sib_in.at[p],
            device_id={"seq": sibling}, device_id_type=MESH,
        )

    def rightward(p, target):
        return pltpu.make_async_remote_copy(
            src_ref=own.at[p], dst_ref=from_left.at[p], send_sem=to_right.at[p], recv_sem=right_in.at[p],
            device_id={"seq": target}, device_id_type=MESH,
        )

    def leftward(p, target):
        return pltpu.make_async_remote_copy(
            src_ref=own.at[p], dst_ref=from_right.at[p], send_sem=to_left.at[p], recv_sem=left_in.at[p],
            device_id={"seq": target}, device_id_type=MESH,
        )

    def down_out(slot, p):
        half = tokens // 2
        return [
            pltpu.make_async_copy(
                down.at[slot, :, half * k : half * (k + 1)], out.at[pl.ds(2 * p, 2)], down_sem.at[k, slot]
            )
            for k, out in enumerate((down0_hbm, down1_hbm))
        ]

    def pass_on(p):
        to_sibling(p).wait_recv()

        @pl.when(p > q)
        def _():
            @pl.when(q > 0)
            def _():
                rightward(p, s).wait_recv()
                own[p] = (own[p].astype(f32) + sib[p].astype(f32) + from_left[p].astype(f32)).astype(low)

            @pl.when(q == 0)
            def _():
                own[p] = (own[p].astype(f32) + sib[p].astype(f32)).astype(low)

            rightward(p, s + 2).start()

        @pl.when(p < q)
        def _():
            @pl.when(q < nc - 1)
            def _():
                leftward(p, s).wait_recv()
                own[p] = (own[p].astype(f32) + sib[p].astype(f32) + from_right[p].astype(f32)).astype(low)

            @pl.when(q == nc - 1)
            def _():
                own[p] = (own[p].astype(f32) + sib[p].astype(f32)).astype(low)

            leftward(p, s - 2).start()

    def starts_flow(p):
        return ((p > q) & (q == 0)) | ((p < q) & (q == nc - 1))

    w = [w_parts.at[g] for g in range(2)]
    width = u_hbm.shape[2]
    weight = lambda g: w[g][...].reshape(width, -1)
    units = wd.shape[0]
    mine = pl.ds(pl.multiple_of(s * units, units), units)
    bd = bd_ref[...].astype(low)
    ad = ad_ref[:, mine].astype(low)
    a = [a_ref[g].astype(low) for g in range(2)]
    b = [b_ref[g, :, mine].astype(low) for g in range(2)]
    m = [m_ref[g : g + 1, mine] for g in range(2)]
    for cp in weights:
        cp.wait()
    a_both = jnp.concatenate(a, axis=0)
    for g in range(2):
        norm, cr = column_norms(weight(g), gram_ref[4 + g], b[g], dot_f32(a[g], weight(g)))
        norm_ref[g] = norm
        cross[g] = cr
        ratio[g] = m[g] / norm
    for ref in (ga_ref, gb_ref, gm_ref, gad_ref, gbd_ref, gmd_ref):
        ref[...] = jnp.zeros_like(ref)
    bd_wide = bd.astype(f32)
    gram_b = dot_two(gram_ref[6], bd)
    squares = jnp.sum(sq_ref[...], axis=0) + SCALE * SCALE * jnp.sum(
        bd_wide * gram_b, axis=0, keepdims=True
    )
    nd_ref[...] = jnp.sqrt(squares + 1e-06)
    ratio_d = md_ref[...] / nd_ref[...]
    pl.semaphore_wait(barrier, n - 1)

    def step(i, carry):
        p = by_distance(nc - 1 - i, q, nc)
        slot = lax.rem(i, 2)
        for cp in loads(i):
            cp.wait()

        @pl.when(i + 1 < nc)
        def _():
            for cp in loads(i + 1):
                cp.start()

        x = u[slot].reshape(2 * tokens, -1)
        upstream = gy[slot].reshape(2 * tokens, -1).astype(f32)
        gb_d = (upstream * ratio_d).astype(low)
        gi_d = (SCALE * dot_nt(gb_d, bd)).astype(low)
        gh = dot_nt(gb_d, wd[...]) + dot_f32(gi_d, ad)
        sides = side[slot].reshape(2 * tokens, -1)
        inner = [sides[:, 16 * g : 16 * g + 16] for g in range(2)]
        before = [dot_f32(x, weight(g)) + SCALE * dot_f32(inner[g], b[g]) for g in range(2)]
        gate = before[0] * ratio[0]
        lift = before[1] * ratio[1]
        sig = 1.0 / (1.0 + jnp.exp(-gate))
        silu = gate * sig
        hidden = (silu * lift).astype(low)
        grads = [gh * lift * sig * (1.0 + gate * (1.0 - sig)), gh * silu]
        gb = [(grads[g] * ratio[g]).astype(low) for g in range(2)]
        gi = jnp.concatenate([(SCALE * dot_nt(gb[g], b[g])).astype(low) for g in range(2)], axis=1)
        back = dot_nt(gb[0], weight(0)) + dot_nt(gb[1], weight(1)) + dot_f32(gi, a_both)
        back = back.astype(low).reshape(2, tokens, -1)
        first, second = back[0], back[1]

        @pl.when(c == 0)
        def _():
            own[p] = first
            theirs[p] = second

        @pl.when(c == 1)
        def _():
            own[p] = second
            theirs[p] = first

        to_sibling(p).start()
        inner_d = dot_nt(hidden, ad).astype(low)
        part = dot_f32(hidden, wd[...]) + SCALE * dot_f32(inner_d, bd)

        @pl.when(i >= 2)
        def _():
            for cp in down_out(slot, p):
                cp.wait()

        down[slot] = part.astype(low).reshape(2, tokens, -1)
        for cp in down_out(slot, p):
            cp.start()
        gmd_ref[...] += jnp.sum(upstream * part, axis=0, keepdims=True)
        gad_ref[...] += dot_tn(gi_d, hidden)
        gbd_ref[...] += SCALE * dot_tn(inner_d, gb_d)
        ga_ref[...] += dot_tn(gi, x).reshape(ga_ref.shape)
        for g in range(2):
            gm_ref[g] += jnp.sum(grads[g] * before[g], axis=0, keepdims=True)
            gb_ref[g] += SCALE * dot_tn(inner[g], gb[g])

        last = by_distance(nc - i, q, nc)
        pl.when((i > 0) & (i < nc - 1) & jnp.logical_not(starts_flow(last)))(lambda: pass_on(last))
        pl.when(starts_flow(p) | (i == nc - 2))(lambda: pass_on(p))
        return carry

    lax.fori_loop(0, nc, step, 0)

    gmd_ref[...] = gmd_ref[...] / nd_ref[...]

    def small(t, slot):
        return pltpu.make_async_remote_copy(
            src_ref=gmd_ref,
            dst_ref=gm_all.at[slot],
            send_sem=small_out.at[t],
            recv_sem=small_in.at[t],
            device_id={"seq": lax.rem(s + t, n)},
            device_id_type=MESH,
        )

    for t in range(1, n):
        small(t, s).start()
    for g in range(2):
        norm = norm_ref[g]
        gm = gm_ref[g] / norm
        gm_ref[g] = gm
        col = -gm * m[g] / (norm * norm)
        weighted = (b[g].astype(f32) * col).astype(low)
        tail = two_terms(dot_nt(weighted, b[g]))
        ga_ref[g] += SCALE * (dot_nt(weighted, weight(g)) + SCALE * dot_two(tail, a[g]))
        gb_ref[g] += SCALE * col * cross[g]

    gm_line = gmd_ref[...]
    for t in range(1, n):
        slot = lax.rem(s - t + n, n)
        small(t, slot).wait_recv()
        gm_line = gm_line + gm_all[slot]
    col = -gm_line * md_ref[...] / (nd_ref[...] * nd_ref[...])
    weighted = (bd_wide * col).astype(low)
    tail = two_terms(dot_nt(weighted, bd))
    gad_ref[...] += SCALE * (dot_nt(weighted, wd[...]) + SCALE * dot_two(tail, ad))
    own_gram = jnp.where(s == 0, SCALE, 0.0) * gram_b
    gbd_ref[...] += SCALE * col * (dot_f32(ad, wd[...]) + own_gram)

    to_sibling(q).wait_recv()
    in_ref[...] = own[q].astype(f32) + sib[q].astype(f32)

    @pl.when(q > 0)
    def _():
        rightward(q, s).wait_recv()
        in_ref[...] += from_left[q].astype(f32)

    @pl.when(q < nc - 1)
    def _():
        leftward(q, s).wait_recv()
        in_ref[...] += from_right[q].astype(f32)

    for i in range(min(2, nc)):
        for cp in down_out(i, 0):
            cp.wait()
    for t in range(1, n):
        small(t, s).wait_send()
    for p in range(nc):
        to_sibling(p).wait_send()
        pl.when(p > q)(lambda p=p: rightward(p, s).wait_send())
        pl.when(p < q)(lambda p=p: leftward(p, s).wait_send())


def share_plan(rows):
    turns = range(1, rows // 2)
    first = [(0, 0, k) for k in turns] + [(0, 1, 0)]
    second = [(0, 0, 0)] + [(0, 1, k) for k in turns]
    second += [(k, None, 0) for k in turns] + [(rows // 2, None, k) for k in turns]
    return first, second


def place_pieces(n, rows, pieces, w_parts):
    nc, half = n // 2, rows // 2
    _, q, _ = place_in_seq()
    r, b_row, a_row, diagonal = place_in_rows(rows)
    own, near = pieces[:2]
    turns = range(1, half)
    held = [(own.at[g], g, r) for g in range(2)]
    kinds = [(0, a_row(-k)) for k in turns] + [(1, b_row)]
    kinds += [(0, b_row)] + [(1, a_row(-k)) for k in turns]
    kinds += [(0, diagonal(-k)) for k in turns] + [(1, diagonal(-k)) for k in turns]
    held += [(piece, g, hold) for piece, (g, hold) in zip(pieces[2:], kinds)]
    out = [(near, w_parts.at[:, pl.ds(2 * q, 2)])]
    for i in range(1, nc):
        pair = pl.ds(2 * near_first(i, q, nc), 2)
        out += [(src.at[pair], w_parts.at[g, pair, hold]) for src, g, hold in held]
    return out


def feed_forward(n, rows, pieces, u, inner, gy0, gy1, wd, a, b, m, ad, bd, md, sq, gram, collective_id):
    nc = n // 2
    _, tokens, width = u.shape
    units = wd.shape[0]
    f32, low = jnp.float32, jnp.bfloat16
    shape = jax.ShapeDtypeStruct
    vmem = pl.BlockSpec(memory_space=pltpu.VMEM)
    hbm = pl.BlockSpec(memory_space=pltpu.HBM)
    dma = pltpu.SemaphoreType.DMA
    line = pltpu.VMEM((nc, tokens, width), low)
    pair = pltpu.VMEM((2, 2, tokens, width), low)
    part = pieces[0].shape[2]
    copies = 2 + (n // 2 - 1) * (2 + 2 * rows - 2)
    count = len(pieces)

    def kernel(*refs):
        ffn_kernel(n, rows, refs[:count], *refs[count:])

    return pl.pallas_call(
        kernel,
        out_shape=(
            shape((tokens, width), f32),
            pltpu.HBM((n, tokens // 2, width), low),
            pltpu.HBM((n, tokens // 2, width), low),
            shape((2, 16, width), f32),
            shape((2, 16, units), f32),
            shape((2, 1, units), f32),
            shape((2, 1, units), f32),
            shape((16, units), f32),
            shape((16, width), f32),
            shape((1, width), f32),
            shape((1, width), f32),
        ),
        in_specs=[hbm] * (count + 5) + [vmem] * 8,
        out_specs=(vmem, hbm, hbm) + (vmem,) * 8,
        scratch_shapes=[
            pltpu.VMEM((2, n, rows, part, units), low),
            pltpu.VMEM((units, width), low),
            pair,
            pltpu.VMEM((2, 2, tokens, 128), low),
            pair,
            pair,
            line, line, line, line, line,
            pltpu.VMEM((2, 1, units), f32),
            pltpu.VMEM((2, 16, units), f32),
            pltpu.VMEM((n, 1, width), f32),
            dma((copies,)), dma((4, 2)), dma((2, 2)), dma((n,)), dma((n,)),
        ] + [dma((nc,))] * 6,
        compiler_params=pltpu.CompilerParams(
            collective_id=collective_id, has_side_effects=True, vmem_limit_bytes=60 << 20
        ),
        cost_estimate=pl.CostEstimate(
            flops=12 * n * tokens * width * units, transcendentals=n * tokens * units,
            bytes_accessed=32 << 20,
        ),
        name="feed_forward",
    )(*pieces, u, inner, gy0, gy1, wd, a, b, m, ad, bd, md, sq, gram)

def greet_cross(n, rows, wait=True):
    s, r = lax.axis_index("seq"), lax.axis_index("rows")
    barrier = pltpu.get_barrier_semaphore()
    for t in range(1, n):
        pl.semaphore_signal(barrier, inc=1, device_id=(r, lax.rem(s + t, n)), device_id_type=MESH)
    for t in range(1, rows):
        pl.semaphore_signal(barrier, inc=1, device_id=(lax.rem(r + t, rows), s), device_id_type=MESH)
    if wait:
        pl.semaphore_wait(barrier, n + rows - 2)


def scatter_kernel(n, rows, x_ref, gb_gu, gm_gu, n_gu, ga_d, o_ref, units_all, own, sib, from_left, from_right,
                   units, units_in, load_sem, to_sib, sib_in, to_right, right_in, to_left, left_in,
                   row_out, row_in, back_send, back_in, wide_send, wide_in, pass_send, pass_in):
    nc = n // 2
    s, q, c = place_in_seq()
    sibling = s + 1 - 2 * c
    theirs = 1 - c
    r = lax.axis_index("rows")
    greet_cross(n, rows)
    f32, low = jnp.float32, jnp.bfloat16
    unit_rows, size = units.shape[1:]

    cut = own.shape[1] // 2
    part = lambda k: pl.ds(k * cut, cut)

    def load(p):
        return pltpu.make_async_copy(x_ref.at[2 * p + c], own.at[p], load_sem.at[p])

    def to_sibling(p, k):
        return pltpu.make_async_remote_copy(
            src_ref=x_ref.at[2 * p + theirs, part(k)],
            dst_ref=sib.at[p, part(k)],
            send_sem=to_sib.at[p, k],
            recv_sem=sib_in.at[p, k],
            device_id={"seq": sibling},
            device_id_type=MESH,
        )

    def rightward(p, k, target):
        return pltpu.make_async_remote_copy(
            src_ref=own.at[p, part(k)],
            dst_ref=from_left.at[p, part(k)],
            send_sem=to_right.at[p, k],
            recv_sem=right_in.at[p, k],
            device_id={"seq": target},
            device_id_type=MESH,
        )

    def leftward(p, k, target):
        return pltpu.make_async_remote_copy(
            src_ref=own.at[p, part(k)],
            dst_ref=from_right.at[p, part(k)],
            send_sem=to_left.at[p, k],
            recv_sem=left_in.at[p, k],
            device_id={"seq": target},
            device_id_type=MESH,
        )

    order = []
    for t in range(nc):
        for p in (nc - 1 - t, t):
            if p not in order:
                order.append(p)
    for p in order:
        load(p).start()
        for k in range(2):
            to_sibling(p, k).start()

    n_high = [n_gu[g].astype(low).astype(f32) for g in range(2)]
    n_rest = [n_gu[g] - n_high[g] for g in range(2)]
    tops = jnp.concatenate(
        [gm_gu[0], gm_gu[1]]
        + [v * (1.0 / rows) for v in (n_high[0], n_rest[0], n_high[1], n_rest[1])]
        + [jnp.zeros((2, size), f32)],
        axis=0,
    )
    blocks = [gb_gu[0][:8], gb_gu[0][8:], gb_gu[1][:8], gb_gu[1][8:], ga_d[:8], ga_d[8:], tops, jnp.zeros((8, size), f32)]
    per = unit_rows // 8
    for j in range(rows):
        units[j] = jnp.concatenate(blocks[per * j : per * (j + 1)], axis=0).astype(low)

    def member(t):
        return lax.rem(r + t + rows, rows)

    def chip(t):
        return lax.rem(q + t + nc, nc)

    def unit_send(t):
        return remote(units.at[member(t)], units_in.at[t], row_out.at[t], row_in.at[t], member(t), s)

    def unit_back(t, slot):
        place = units_all.at[r, c, slot]
        return remote(place, place, back_send.at[t], back_in.at[t], r, 2 * chip(t) + c)

    def unit_wide(t, row):
        place = units_all.at[row, c]
        return remote(place, place, wide_send.at[t], wide_in.at[t], member(t), s)

    def unit_hand(t, row, core):
        place = units_all.at[row, core]
        return remote(place, place, pass_send.at[t], pass_in.at[t], r, sibling)

    def sum_units():
        total = units[r].astype(f32)
        for t in range(1, rows):
            unit_send(t).wait_recv()
            total = total + units_in[t].astype(f32)
        units_all[r, c, q] = total.astype(low)
        for t in range(1, nc):
            unit_back(t, q).start()

    def spread_units():
        for t in range(1, nc):
            unit_back(t, chip(-t)).wait_recv()
        for t in range(1, rows):
            unit_wide(t, r).start()
        unit_hand(0, r, c).start()

    for t in range(1, rows):
        unit_send(t).start()
    def add_and_send(p, k, flow, arrived, more, target):
        at = part(k)

        @pl.when(more)
        def _():
            flow(p, k, s).wait_recv()
            total = own[p, at].astype(f32) + sib[p, at].astype(f32) + arrived[p, at].astype(f32)
            own[p, at] = total.astype(own.dtype)

        @pl.when(jnp.logical_not(more))
        def _():
            own[p, at] = (own[p, at].astype(f32) + sib[p, at].astype(f32)).astype(own.dtype)

        flow(p, k, target).start()

    sum_units()
    for step, p in enumerate(jnp.where(q <= nc - 1 - q, p, nc - 1 - p) for p in order):
        if step == 1:
            spread_units()
        load(p).wait()
        for k in range(2):
            to_sibling(p, k).wait_recv()
            pl.when(p > q)(lambda p=p, k=k: add_and_send(p, k, rightward, from_left, q > 0, s + 2))
            pl.when(p < q)(
                lambda p=p, k=k: add_and_send(p, k, leftward, from_right, q < nc - 1, s - 2)
            )

    o_ref[...] = own[q].astype(f32) + sib[q].astype(f32)

    @pl.when(q > 0)
    def _():
        for k in range(2):
            rightward(q, k, s).wait_recv()
        o_ref[...] += from_left[q].astype(f32)

    @pl.when(q < nc - 1)
    def _():
        for k in range(2):
            leftward(q, k, s).wait_recv()
        o_ref[...] += from_right[q].astype(f32)

    for t in range(1, rows):
        unit_wide(t, member(-t)).wait_recv()
        unit_hand(t, member(-t), c).start()
    for t in range(rows):
        unit_hand(t, member(-t), theirs).wait_recv()
        unit_hand(t, member(-t), c).wait_send()
    for t in range(1, rows):
        unit_send(t).wait_send()
        unit_wide(t, r).wait_send()
    for t in range(1, nc):
        unit_back(t, q).wait_send()
    for p in range(nc):
        for k in range(2):
            to_sibling(p, k).wait_send()
            pl.when(p > q)(lambda p=p, k=k: rightward(p, k, s).wait_send())
            pl.when(p < q)(lambda p=p, k=k: leftward(p, k, s).wait_send())


def scatter_seq(n, rows, x, own_units, collective_id):
    nc = n // 2
    _, height, cols = x.shape
    size = own_units[3].shape[1]
    unit_rows = 64 // rows
    low = jnp.bfloat16
    dma = pltpu.SemaphoreType.DMA
    buf = pltpu.VMEM((nc, height, cols), x.dtype)
    small = pltpu.VMEM((rows, unit_rows, size), low)
    vmem = pl.BlockSpec(memory_space=pltpu.VMEM)
    return pl.pallas_call(
        functools.partial(scatter_kernel, n, rows),
        out_shape=(
            jax.ShapeDtypeStruct((height, cols), jnp.float32),
            jax.ShapeDtypeStruct((rows, 2, nc, unit_rows, size), low),
        ),
        in_specs=[pl.BlockSpec(memory_space=pltpu.HBM)] + [vmem] * 4,
        out_specs=(vmem,) * 2,
        scratch_shapes=[buf] * 4 + [small] * 2 + [dma((nc,))] + [dma((nc, 2))] * 6
        + [dma((rows,))] * 2 + [dma((nc,))] * 2 + [dma((rows,))] * 4,
        compiler_params=pltpu.CompilerParams(
            collective_id=collective_id, has_side_effects=True, vmem_limit_bytes=32 << 20
        ),
        cost_estimate=pl.CostEstimate(flops=0, transcendentals=0, bytes_accessed=1 << 20),
        name="scatter_seq",
    )(*in_hbm(x), *own_units)


def reduce_kernel(n, rows, ga_qkv, ga_o, gb_qkv, gb_o, ga_gu, gb_d, gm_qkv, gm_o, gm_d,
                  whole, part, from_sib, mid, from_rows, from_line, line_out,
                  sib_out, sib_in, row_out, row_in, line_send, line_in, back_send, back_in, wide_send, wide_in,
                  pass_send, pass_in):
    nc = n // 2
    f32, low = jnp.float32, jnp.bfloat16
    s, q, c = place_in_seq()
    sibling = s + 1 - 2 * c
    r = lax.axis_index("rows")
    width = ga_o.shape[1]
    cols = width // (2 * rows)
    kv = (gb_qkv.shape[1] - width) // 2
    height = part.shape[2]
    piece = height // nc

    greet_cross(n, rows, wait=False)
    gb_k, gb_v = gb_qkv[:, width : width + kv], gb_qkv[:, width + kv :]
    small = jnp.concatenate(
        [
            jnp.concatenate([gb_k[:8], gb_k[8:], gb_v[:8], gb_v[8:]], axis=1),
            gm_qkv[:, :width],
            gm_o[...],
            gm_d[...],
            jnp.concatenate([gm_qkv[:, width:], jnp.zeros((1, width - 2 * kv), f32)], axis=1),
            jnp.zeros((4, width), f32),
        ],
        axis=0,
    )
    groups = [ga_qkv[0], ga_qkv[1], ga_qkv[2], ga_o[...], gb_qkv[:, :width], gb_o[...], ga_gu[0], ga_gu[1], gb_d[...], small]
    for j in range(2 * rows):
        for g, value in enumerate(groups):
            part[j % 2, j // 2, 16 * g : 16 * g + 16] = value[:, cols * j : cols * (j + 1)].astype(low)
        if height > 160:
            part[j % 2, j // 2, 160:] = jnp.zeros((height - 160, cols), low)
    pl.semaphore_wait(pltpu.get_barrier_semaphore(), n + rows - 2)

    def to_sibling():
        return remote(part.at[1 - c], from_sib, sib_out.at[0], sib_in.at[0], r, sibling)

    def member(t):
        return lax.rem(r + t + rows, rows)

    def row_send(t):
        return remote(mid.at[member(t)], from_rows.at[t], row_out.at[t], row_in.at[t], member(t), s)

    def chip(t):
        return lax.rem(q + t + nc, nc)

    def line_part(t):
        return remote(line_out.at[chip(t)], from_line.at[t], line_send.at[t], line_in.at[t], r, 2 * chip(t) + c)

    def back(t, slot):
        return remote(whole.at[r, c, slot], whole.at[r, c, slot], back_send.at[t], back_in.at[t], r, 2 * chip(t) + c)

    def wide(t, row):
        return remote(whole.at[row, c], whole.at[row, c], wide_send.at[t], wide_in.at[t], member(t), s)

    def hand(t, row, core):
        return remote(whole.at[row, core], whole.at[row, core], pass_send.at[t], pass_in.at[t], r, sibling)

    to_sibling().start()
    to_sibling().wait_recv()
    for t in range(rows):
        mid[member(t)] = (part[c, member(t)].astype(f32) + from_sib[member(t)].astype(f32)).astype(low)
        if t:
            row_send(t).start()
    total = mid[r].astype(f32)
    for t in range(1, rows):
        row_send(t).wait_recv()
        total = total + from_rows[t].astype(f32)
    for p in range(nc):
        line_out[p] = total[piece * p : piece * (p + 1)].astype(low)
    for t in range(1, nc):
        line_part(t).start()
    own = line_out[q].astype(f32)
    for t in range(1, nc):
        line_part(t).wait_recv()
        own = own + from_line[t].astype(f32)
    whole[r, c, q] = own.astype(low)
    for t in range(1, nc):
        back(t, q).start()
    for t in range(1, nc):
        back(t, chip(-t)).wait_recv()
    for t in range(1, rows):
        wide(t, r).start()
    hand(0, r, c).start()
    for t in range(1, rows):
        wide(t, member(-t)).wait_recv()
        hand(t, member(-t), c).start()
    for t in range(rows):
        hand(t, member(-t), 1 - c).wait_recv()

    to_sibling().wait_send()
    for t in range(1, rows):
        row_send(t).wait_send()
        wide(t, r).wait_send()
    for t in range(1, nc):
        line_part(t).wait_send()
        back(t, q).wait_send()
    for t in range(rows):
        hand(t, member(-t), c).wait_send()


def sum_gradients(n, rows, full, collective_id):
    nc = n // 2
    width = full[1].shape[1]
    cols = width // (2 * rows)
    height = -(-160 // (8 * nc)) * 8 * nc
    low = jnp.bfloat16
    vmem = pl.BlockSpec(memory_space=pltpu.VMEM)
    dma = pltpu.SemaphoreType.DMA
    block = (rows, height, cols)
    return pl.pallas_call(
        functools.partial(reduce_kernel, n, rows),
        out_shape=jax.ShapeDtypeStruct((rows, 2, nc, height // nc, cols), low),
        in_specs=[vmem] * 9,
        out_specs=vmem,
        scratch_shapes=[
            pltpu.VMEM((2, *block), low),
            pltpu.VMEM(block, low),
            pltpu.VMEM(block, low),
            pltpu.VMEM(block, low),
            pltpu.VMEM((nc, height // nc, cols), low),
            pltpu.VMEM((nc, height // nc, cols), low),
            dma((1,)), dma((1,)), dma((rows,)), dma((rows,)), dma((nc,)), dma((nc,)),
            dma((nc,)), dma((nc,)), dma((rows,)), dma((rows,)), dma((rows,)), dma((rows,)),
        ],
        compiler_params=pltpu.CompilerParams(
            collective_id=collective_id, has_side_effects=True, vmem_limit_bytes=48 << 20
        ),
        cost_estimate=pl.CostEstimate(flops=0, transcendentals=0, bytes_accessed=1 << 20),
        name="sum_gradients",
    )(*full)


def finish_kernel(n, rows, whole, units_all, x1, before_0, before_1, m_attn, n_attn, m_d, n_d, m_gu,
                  o_out, o_ga, o_gb_qo, o_gb_kv, o_gm_q, o_gm_kv, o_gm_o, o_ga_gu, o_gb_gu, o_gm_gu, o_ga_d, o_gb_d,
                  o_gm_d, o_stats, n_gu):
    f32 = jnp.float32
    nc = n // 2
    width = o_gb_d.shape[1]
    kv = o_gb_kv.shape[2]
    cols = width // (2 * rows)
    size = units_all.shape[4]
    per = units_all.shape[3] // 8
    half = x1.shape[0] // 2
    for k, before in enumerate((before_0, before_1)):
        own = slice(half * k, half * (k + 1))
        o_out[own] = (x1[own] + before[...].astype(f32) * (m_d[...] / n_d[...])).astype(o_out.dtype)
    for j in range(2 * rows):
        block = jnp.concatenate([whole[j // 2, j % 2, p].astype(f32) for p in range(nc)], axis=0)
        at = slice(cols * j, cols * (j + 1))
        for g in range(4):
            o_ga[g, :, at] = block[16 * g : 16 * g + 16]
        o_gb_qo[0, :, at] = block[64:80]
        o_gb_qo[1, :, at] = block[80:96]
        o_ga_gu[0, :, at] = block[96:112]
        o_ga_gu[1, :, at] = block[112:128]
        o_gb_d[:, at] = block[128:144]
        which, start = divmod(cols * j, kv)
        o_gb_kv[which // 2, 8 * (which % 2) : 8 * (which % 2) + 8, start : start + cols] = block[144:152]
        o_gm_q[at] = block[152]
        o_gm_o[at] = block[153]
        o_gm_d[at] = block[154]
        if which < 2:
            o_gm_kv[which : which + 1, start : start + cols] = block[155:156]
    for j in range(rows):
        for dev in range(n):
            block = units_all[j, dev % 2, dev // 2].astype(f32)
            at = slice(size * dev, size * (dev + 1))
            for t in range(per):
                rows8, place = block[8 * t : 8 * t + 8], per * j + t
                half = slice(8 * (place % 2), 8 * (place % 2) + 8)
                if place < 4:
                    o_gb_gu[place // 2, half, at] = rows8
                elif place < 6:
                    o_ga_d[half, at] = rows8
                elif place == 6:
                    o_gm_gu[:, at] = rows8[:2]
                    n_gu[0:1, at] = rows8[2:3] + rows8[3:4]
                    n_gu[1:2, at] = rows8[4:5] + rows8[5:6]


    row = lax.broadcasted_iota(jnp.int32, o_stats.shape, 0)
    col = lax.broadcasted_iota(jnp.int32, o_stats.shape, 1)
    bounds = [(0, width), (width, width + kv), (width + kv, width + 2 * kv), (width + 2 * kv, 2 * width + 2 * kv)]
    both = [(m_attn[:, i:j], n_attn[:, i:j]) for i, j in bounds]
    both += [(m_gu[g : g + 1, :], n_gu[g : g + 1, :]) for g in range(2)] + [(m_d[...], n_d[...])]
    stats = jnp.zeros(o_stats.shape, f32)
    for p, (m, norm) in enumerate(both):
        drift = jnp.mean(jnp.square(m - norm), axis=1, keepdims=True)
        drift = jnp.sqrt(drift) / jnp.sqrt(jnp.mean(jnp.square(m), axis=1, keepdims=True) + 1e-06)
        stats = jnp.where((row == 0) & (col == p), drift, stats)
        stats = jnp.where((row == 1) & (col == p), jnp.mean(norm, axis=1, keepdims=True), stats)
    o_stats[...] = stats


def finish(n, rows, sums, units, x1, before_0, before_1, m_attn, n_attn, m_d, n_d, m_gu):
    tokens, width = x1.shape
    kv = (m_attn.shape[1] - 2 * width) // 2
    wide_units = m_gu.shape[1]
    shape = lambda *dims: pltpu.HBM(dims, jnp.float32)
    vmem = pl.BlockSpec(memory_space=pltpu.VMEM)
    return pl.pallas_call(
        functools.partial(finish_kernel, n, rows),
        out_shape=(
            pltpu.HBM((tokens, width), jnp.bfloat16), shape(4, 16, width), shape(2, 16, width), shape(2, 16, kv),
            shape(width), shape(2, kv), shape(width), shape(2, 16, width), shape(2, 16, wide_units), shape(2, wide_units),
            shape(16, wide_units), shape(16, width), shape(width), shape(2, 7),
        ),
        in_specs=[vmem] * 2 + [pl.BlockSpec()] * 8,
        scratch_shapes=[pltpu.VMEM((2, wide_units), jnp.float32)],
        compiler_params=pltpu.CompilerParams(vmem_limit_bytes=40 << 20),
        cost_estimate=pl.CostEstimate(flops=0, transcendentals=0, bytes_accessed=8 << 20),
        name="finish",
    )(sums, units, *in_hbm(x1, before_0, before_1), m_attn, n_attn, m_d, n_d, m_gu)

def local(
    layer_input,
    output_gradient,
    norm_gain_vectors,
    query_output_frozen,
    key_value_frozen,
    gate_up_frozen,
    down_frozen_weight,
    attention_adapter_a,
    query_output_adapter_b,
    key_value_adapter_b,
    query_magnitude,
    key_value_magnitude,
    output_magnitude,
    gate_up_adapter_a,
    gate_up_adapter_b,
    gate_up_magnitude,
    down_adapter_a,
    down_adapter_b,
    down_magnitude,
    prompt_length_list,
    response_length_list,
):
    pair_rows, span_len, model_width = layer_input.shape
    token_count = pair_rows * span_len
    kv_width = KV_HEADS * HEAD_DIM
    seq_size = lax.axis_size("seq")
    rows_size = lax.axis_size("rows")
    seq_index = lax.axis_index("seq")
    f32 = jnp.float32

    x = layer_input.reshape(token_count, model_width)
    grad_out_rows = output_gradient.reshape(token_count, model_width)
    weights, gu_own, gu_near, sq_d, grams, u1, inner_1, gy_halves = gather_weights(
        seq_size, rows_size, query_output_frozen, key_value_frozen, gate_up_frozen,
        down_frozen_weight, down_adapter_a, down_adapter_b, x, norm_gain_vectors,
        attention_adapter_a, gate_up_adapter_a, grad_out_rows, 1,
    )
    shares_1, shares_2 = share_plan(rows_size)
    gy_0 = lax.all_gather(gy_halves[0], "seq", axis=0, tiled=False)

    b_attn = jnp.concatenate(
        [
            query_output_adapter_b[0],
            key_value_adapter_b[0],
            key_value_adapter_b[1],
            query_output_adapter_b[1],
        ],
        axis=1,
    )
    m_attn = jnp.concatenate(
        [query_magnitude, key_value_magnitude[0], key_value_magnitude[1], output_magnitude]
    )[None]
    m_d = down_magnitude[None]

    positions = seq_index * span_len + jnp.arange(span_len, dtype=jnp.int32)
    half_dim = HEAD_DIM // 2
    frequency = 500000.0 ** (-(jnp.arange(half_dim, dtype=f32) * 2.0) / HEAD_DIM)
    angles = positions.astype(f32)[:, None] * frequency[None, :]
    cosine = jnp.tile(jnp.cos(angles), (pair_rows, 4))
    sine = jnp.tile(jnp.sin(angles), (pair_rows, 4))
    valid_len = prompt_length_list[0] + response_length_list

    before_qkv, q, n_attn, cross_attn, kv_all, sq_all, gu_1 = project_qkv(
        seq_size, rows_size, u1, inner_1, grams, attention_adapter_a, weights, b_attn, m_attn,
        cosine, sine, sq_d, gu_own, shares_1, 2,
    )
    kv_all, half_1 = lax.optimization_barrier((kv_all, gy_halves[1]))
    gy_1 = lax.all_gather(half_1, "seq", axis=0, tiled=False)
    kv_all = kv_all.reshape(seq_size, pair_rows, span_len, 2 * kv_width)
    q = q.reshape(pair_rows, span_len, model_width)
    att, shares = attend(q, kv_all, valid_len)
    att = att.reshape(token_count, model_width)
    before_o, x1, u2, inner_2 = project_out(
        att, attention_adapter_a, weights, b_attn, m_attn, n_attn, x, norm_gain_vectors, gate_up_adapter_a
    )

    (u2_all, inner_all), gu_2 = gather_seq(
        seq_size, rows_size, [u2, inner_2], 3, (gu_own, *gu_1), shares_2
    )
    in_grad, down_0, down_1, ga_gu, gb_gu, gm_gu, n_gu, ga_d, gb_d, gm_d, n_d = feed_forward(
        seq_size, rows_size, (gu_own, gu_near, *gu_1, *gu_2), u2_all, inner_all, gy_0, gy_1,
        down_frozen_weight, gate_up_adapter_a, gate_up_adapter_b, gate_up_magnitude, down_adapter_a,
        down_adapter_b, m_d, sq_all, grams, 4,
    )
    flat = lambda v: v.reshape(-1, model_width)
    before_0 = lax.psum_scatter(flat(down_0), "seq", scatter_dimension=0, tiled=True)

    gx1, grad_att, ga_o, gb_o, gm_o = out_back(
        in_grad, x1, norm_gain_vectors, grad_out_rows, before_o, att, attention_adapter_a, b_attn, m_attn,
        n_attn, cross_attn, weights,
    )
    gq, gkv = attend_back(q, kv_all, shares, grad_att.reshape(q.shape))
    gkv, units = scatter_seq(
        seq_size, rows_size, gkv.reshape(seq_size, token_count, 2 * kv_width),
        (gb_gu, gm_gu, n_gu, ga_d), 5,
    )
    gkv, down_1, before_0 = lax.optimization_barrier((gkv, down_1, before_0))
    before_1 = lax.psum_scatter(flat(down_1), "seq", scatter_dimension=0, tiled=True)
    grad_inputs, ga_qkv, gb_qkv, gm_qkv = qkv_back(
        gq.reshape(token_count, model_width), gkv, cosine, sine, before_qkv, u1, inner_1,
        attention_adapter_a, b_attn, m_attn, n_attn, cross_attn, x, norm_gain_vectors, gx1, weights,
    )

    sums = sum_gradients(
        seq_size, rows_size,
        (ga_qkv, ga_o, gb_qkv, gb_o, ga_gu, gb_d, gm_qkv, gm_o, gm_d),
        6,
    )
    layer_result, *summed, stats = finish(
        seq_size, rows_size, sums, units, x1, before_0, before_1, m_attn, n_attn, m_d, n_d, gate_up_magnitude
    )
    shape = (pair_rows, span_len, model_width)
    return (layer_result.reshape(shape), grad_inputs.reshape(shape), *summed, stats.T)

def solution(mesh):
    return jax.shard_map(
        local,
        mesh=mesh,
        in_specs=(
            P("rows", "seq", None),
            P("rows", "seq", None),
            P(),
            P(None, "seq", None),
            P(None, "seq", None),
            P(None, "seq", None),
            P("seq", None),
            P(),
            P(),
            P(),
            P(),
            P(),
            P(),
            P(),
            P(),
            P(),
            P(),
            P(),
            P(),
            P("rows"),
            P("rows"),
        ),
        out_specs=(
            P("rows", "seq", None),
            P("rows", "seq", None),
            P(),
            P(),
            P(),
            P(),
            P(),
            P(),
            P(),
            P(),
            P(),
            P(),
            P(),
            P(),
            P(),
        ),
        check_vma=False,
    )
```

```python
import functools

import jax
import jax.numpy as jnp
from jax import lax
from jax.experimental import pallas as pl
from jax.experimental.pallas import tpu as pltpu
from jax.sharding import PartitionSpec as P

HEADS = 32
KV_HEADS = 8
HEAD_DIM = 64
ADAPTER_RANK = 16
ALPHA = 32
SCALE = ALPHA / ADAPTER_RANK
TILE = 512

highest = lax.Precision.HIGHEST
last_last = (((1,), (1,)), ((), ()))
first_first = (((0,), (0,)), ((), ()))

def dot_f32(a, b):
    return jnp.dot(a, b, preferred_element_type=jnp.float32)


def dot_nt(a, b):
    return lax.dot_general(a, b, last_last, preferred_element_type=jnp.float32)


def dot_tn(a, b):
    return lax.dot_general(a, b, first_first, preferred_element_type=jnp.float32)


def in_hbm(*arrays):
    return [pltpu.with_memory_space_constraint(v, pltpu.HBM) for v in arrays]


def unit_rms(v):
    return lax.rsqrt(jnp.mean(v * v, axis=-1, keepdims=True) + 1e-05)


def rms_back(v, gain, upstream):
    r = unit_rms(v)
    scaled = gain * upstream
    return r * scaled - v * (r * r * r) * jnp.mean(scaled * v, axis=-1, keepdims=True)


def turn(z, cosine, sine):
    width = z.shape[1]
    lane = lax.broadcasted_iota(jnp.int32, z.shape, 1)
    half = HEAD_DIM // 2
    other = jnp.where(
        lax.rem(lane, HEAD_DIM) < half, -pltpu.roll(z, width - half, 1), pltpu.roll(z, half, 1)
    )
    copies = width // cosine.shape[1]
    return z * jnp.tile(cosine, (1, copies)) + other * jnp.tile(sine, (1, copies))


def column_squares(w):
    return jnp.sum(jnp.square(w.astype(jnp.float32)), axis=0, keepdims=True)


def two_terms(value):
    high = value.astype(jnp.bfloat16)
    return jnp.concatenate([high, (value - high.astype(jnp.float32)).astype(jnp.bfloat16)], axis=0)


def dot_two(terms, b):
    both = dot_f32(terms, b)
    half = both.shape[0] // 2
    return both[:half] + both[half:]


def column_norms(w, gram, b, cross):
    b_wide = b.astype(jnp.float32)
    gram_b = dot_two(gram, b)
    squares = column_squares(w) + 2.0 * SCALE * jnp.sum(b_wide * cross, axis=0, keepdims=True)
    squares = squares + SCALE * SCALE * jnp.sum(b_wide * gram_b, axis=0, keepdims=True)
    return jnp.sqrt(squares + 1e-06), cross + SCALE * gram_b


def project_kernel(n, rows, plan, k_tiles, q_tiles, u_ref, inner_ref, gram_ref, a_ref, w_ref, b_ref, m_ref, cos_ref,
                   sin_ref, sq_ref, held, before_ref, q_ref, n_ref, cross_ref, kv_all, sq_all, *refs):
    swapped = refs[: len(plan)]
    kv_ref, keep_sem, to_sib, to_left, to_right, recv, share_out, share_in = refs[len(plan) :]
    j = pl.program_id(0)
    last = pl.num_programs(0) - 1
    nc = n // 2
    s, q, c = place_in_seq()
    sibling = s + 1 - 2 * c
    r, b_row, a_row, _ = place_in_rows(rows)
    order = [near_first(i, q, nc) for i in range(nc)]
    sources, outs = (kv_ref, sq_ref), (kv_all, sq_all)

    def copy(k, src, slot, sems, target):
        return remote(src, outs[k].at[slot], sems.at[k, slot], recv.at[k, slot], r, target)

    def share(i, chip):
        _, piece, turn = plan[i]
        pair = pl.ds(2 * chip, 2)
        target = b_row if turn == 0 else a_row(turn)
        return remote(
            held.at[piece, pair], swapped[i].at[pair], share_out.at[i, chip], share_in.at[i, chip], target, s
        )

    def keep(k):
        return pltpu.make_async_copy(sources[k], outs[k].at[s], keep_sem.at[k])

    @pl.when(j == 0)
    def _():
        greet_all(n, rows)
        for chip in order[1:]:
            for i in range(len(plan)):
                share(i, chip).start()

    a = a_ref[0].astype(jnp.bfloat16)
    b = b_ref[...].astype(jnp.bfloat16)
    w = w_ref[0]
    height = u_ref.shape[0]

    @pl.when(j < 2 * k_tiles + q_tiles)
    def _():
        both = dot_f32(jnp.concatenate([u_ref[...], a], axis=0), w)
        norm, cross = column_norms(w, gram_ref[0], b, both[height:])
        n_ref[...] = norm
        cross_ref[...] = cross
        before = both[:height] + SCALE * dot_f32(inner_ref[0], b)
        before_ref[...] = before
        y = before * (m_ref[...] / norm)

        @pl.when(j >= 2 * k_tiles)
        def _():
            q_ref[...] = turn(y, cos_ref[...], sin_ref[...]).astype(jnp.bfloat16)

        for t in range(2 * k_tiles):

            @pl.when(j == t)
            def _(t=t):
                z = turn(y, cos_ref[...], sin_ref[...]) if t < k_tiles else y
                kv_ref[:, TILE * t : TILE * (t + 1)] = z.astype(jnp.bfloat16)

    @pl.when(j >= 2 * k_tiles + q_tiles)
    def _():
        norm, cross = column_norms(w, gram_ref[0], b, dot_f32(a, w))
        n_ref[...] = norm
        cross_ref[...] = cross

    @pl.when(j == 2 * k_tiles - 1)
    def _():
        for k in range(2):
            pl.when(q > 0)(lambda k=k: copy(k, sources[k], s, to_left, s - 2).start())
            pl.when(q < nc - 1)(lambda k=k: copy(k, sources[k], s, to_right, s + 2).start())
            copy(k, sources[k], s, to_sib, sibling).start()
            keep(k).start()

    def pass_on(chip):
        slot = 2 * chip + c
        for k in range(2):
            src = outs[k].at[slot]
            copy(k, src, slot, to_right, s).wait_recv()
            pl.when((chip < q) & (q < nc - 1))(
                lambda k=k, src=src: copy(k, src, slot, to_right, s + 2).start()
            )
            pl.when((chip > q) & (q > 0))(
                lambda k=k, src=src: copy(k, src, slot, to_left, s - 2).start()
            )
            copy(k, src, slot, to_sib, sibling).start()

    for i in range(1, nc):
        at = min(2 * k_tiles + 2 * i, 2 * k_tiles + 2 * q_tiles - 1)
        pl.when(j == at)(lambda i=i: pass_on(order[i]))

    @pl.when(j == last)
    def _():
        for k in range(2):
            keep(k).wait()
            for chip in range(nc):
                mine, theirs = 2 * chip + c, 2 * chip + 1 - c
                copy(k, outs[k].at[theirs], theirs, to_sib, sibling).wait_recv()
                copy(k, outs[k].at[mine], mine, to_sib, sibling).wait_send()
                pl.when((q < nc - 1) & (chip <= q))(
                    lambda k=k, mine=mine: copy(k, outs[k].at[mine], mine, to_right, s).wait_send()
                )
                pl.when((q > 0) & (chip >= q))(
                    lambda k=k, mine=mine: copy(k, outs[k].at[mine], mine, to_left, s).wait_send()
                )
        for chip in order[1:]:
            for i in range(len(plan)):
                share(i, chip).wait_send()
                share(i, chip).wait_recv()


def project_qkv(n, rows, u, inner, grams, a, weights, b, m, cosine, sine, sq, held, plan, collective_id):
    tokens, width = u.shape
    cols = b.shape[1]
    nc = n // 2
    per_half = weights.shape[2] // TILE
    q_tiles = width // TILE
    k_cols = weights.shape[2] - width
    k_tiles = k_cols // TILE
    kv_tiles = 2 * k_tiles
    full = lambda shape: pl.BlockSpec(shape, lambda j: (0,) * len(shape))

    def column(j):
        return jnp.where(j < kv_tiles, q_tiles + j, jnp.where(j < kv_tiles + q_tiles, j - kv_tiles, j))

    def which(j):
        return jnp.where(
            j < k_tiles, 1, jnp.where(j < kv_tiles, 2, jnp.where(j < kv_tiles + q_tiles, 0, 3))
        )

    def before_tile(j):
        return (0, column(jnp.minimum(j, kv_tiles + q_tiles - 1)))

    col = lambda height: pl.BlockSpec((height, TILE), lambda j: (0, column(j)))
    f32, low = jnp.float32, jnp.bfloat16
    hbm = pl.BlockSpec(memory_space=pltpu.HBM)
    dma = pltpu.SemaphoreType.DMA
    got = pl.pallas_call(
        functools.partial(project_kernel, n, rows, plan, k_tiles, q_tiles),
        out_shape=(
            pltpu.HBM((tokens, width + 2 * k_cols), f32),
            pltpu.HBM((tokens, width), low),
            pltpu.HBM((1, cols), f32),
            pltpu.HBM((16, cols), f32),
            pltpu.HBM((n, tokens, 2 * k_cols), low),
            pltpu.HBM((n, *sq.shape), f32),
            *(pltpu.HBM(held.shape[-3:], low) for _ in plan),
        ),
        grid=(cols // TILE,),
        in_specs=[
            full((tokens, width)),
            pl.BlockSpec((1, tokens, 16), lambda j: (jnp.minimum(which(j), 2), 0, 0)),
            pl.BlockSpec((1, 32, 16), lambda j: (which(j), 0, 0)),
            pl.BlockSpec((1, 16, width), lambda j: (which(j), 0, 0)),
            pl.BlockSpec((1, width, TILE), lambda j: (column(j) // per_half, 0, lax.rem(column(j), per_half))),
            col(16),
            col(1),
            full(cosine.shape),
            full(sine.shape),
            hbm,
            hbm,
        ],
        out_specs=(
            pl.BlockSpec((tokens, TILE), before_tile),
            pl.BlockSpec((tokens, TILE), lambda j: (0, jnp.clip(j - kv_tiles, 0, q_tiles - 1))),
            col(1),
            col(16),
            *([hbm] * (2 + len(plan))),
        ),
        scratch_shapes=[pltpu.VMEM((tokens, 2 * k_cols), low), dma((2,))]
        + [dma((2, n))] * 4
        + [dma((len(plan), nc))] * 2,
        compiler_params=pltpu.CompilerParams(
            collective_id=collective_id, has_side_effects=True, vmem_limit_bytes=40 << 20
        ),
        cost_estimate=pl.CostEstimate(
            flops=2 * tokens * width * cols, transcendentals=0, bytes_accessed=64 << 20
        ),
        name="project_qkv",
    )(*in_hbm(u), inner, grams, *in_hbm(a, weights, b), m, cosine, sine, *in_hbm(sq, held))
    return (*got[:6], got[6:])


def out_kernel(att_ref, a_ref, w_ref, b_ref, m_ref, n_ref, x_ref, gain_ref, next_ref,
               before_ref, x1_ref, u2_ref, inner_ref):
    t = pl.program_id(0)
    a = a_ref[0].astype(jnp.bfloat16)
    b = b_ref[...].astype(jnp.bfloat16)
    inner = dot_nt(att_ref[...], a).astype(jnp.bfloat16)
    before = dot_f32(att_ref[...], w_ref[0]) + SCALE * dot_f32(inner, b)
    before_ref[...] = before
    x1_ref[:, pl.ds(pl.multiple_of(t * TILE, TILE), TILE)] = (
        x_ref[...].astype(jnp.float32) + before * (m_ref[...] / n_ref[...])
    )

    @pl.when(t == pl.num_programs(0) - 1)
    def _():
        v = x1_ref[...]
        u2 = (v * unit_rms(v) * gain_ref[1:]).astype(jnp.bfloat16)
        u2_ref[...] = u2
        following = next_ref[...].reshape(-1, u2.shape[1]).astype(jnp.bfloat16)
        inner_ref[...] = jnp.zeros_like(inner_ref)
        inner_ref[:, : following.shape[0]] = dot_nt(u2, following).astype(jnp.bfloat16)


def project_out(att, a, weights, b, m, norms, x, gain, following):
    rows, width = att.shape
    tiles = width // TILE
    skip = (weights.shape[2] - width) // TILE
    full = lambda shape: pl.BlockSpec(shape, lambda t: (0,) * len(shape))
    col = lambda height: pl.BlockSpec((height, TILE), lambda t: (0, t))
    ahead = b.shape[1] // TILE - tiles
    later = lambda height: pl.BlockSpec((height, TILE), lambda t: (0, ahead + t))
    f32 = jnp.float32
    return pl.pallas_call(
        out_kernel,
        out_shape=(
            pltpu.HBM((rows, width), f32),
            pltpu.HBM((rows, width), f32),
            pltpu.HBM((rows, width), jnp.bfloat16),
            pltpu.HBM((rows, 128), jnp.bfloat16),
        ),
        grid=(tiles,),
        in_specs=[
            full((rows, width)),
            pl.BlockSpec((1, 16, width), lambda t: (3, 0, 0)),
            pl.BlockSpec((1, width, TILE), lambda t: (1, 0, skip + t)),
            later(16),
            later(1),
            later(1),
            col(rows),
            full((2, width)),
            full(following.shape),
        ],
        out_specs=(col(rows), full((rows, width)), full((rows, width)), full((rows, 128))),
        compiler_params=pltpu.CompilerParams(vmem_limit_bytes=40 << 20),
        cost_estimate=pl.CostEstimate(
            flops=2 * rows * width * width, transcendentals=0, bytes_accessed=2 * width * width
        ),
        name="project_out",
    )(*in_hbm(att, a, weights, b), m, norms, *in_hbm(x), gain, *in_hbm(following))


def out_back_kernel(in_ref, x1_ref, gain_ref, gy_ref, before_ref, att_ref, a_ref, b_ref, m_ref, n_ref, cross_ref,
                    w_ref, gx_ref, gatt_ref, ga_ref, gb_ref, gm_ref, lhs, gi, tail):
    t = pl.program_id(0)
    rows, width = gx_ref.shape
    low = jnp.bfloat16
    a = a_ref[0].astype(low)
    o_cols = slice(b_ref.shape[1] - width, b_ref.shape[1])

    @pl.when(t == 0)
    def _():
        gx = gy_ref[...].astype(jnp.float32) + rms_back(x1_ref[...], gain_ref[1:], in_ref[...])
        gx_ref[...] = gx
        norm, m = n_ref[:, o_cols], m_ref[:, o_cols]
        gb = (gx * (m / norm)).astype(low)
        lhs[:rows] = gb
        b = b_ref[:, o_cols].astype(low)
        gi[...] = (SCALE * dot_nt(gb, b)).astype(low)
        gm = jnp.sum(gx * before_ref[...], axis=0, keepdims=True) / norm
        gm_ref[...] = gm
        c = -gm * m / (norm * norm)
        weighted = (b.astype(jnp.float32) * c).astype(low)
        lhs[rows:] = weighted
        tail[...] = two_terms(dot_nt(weighted, b))
        inner = dot_nt(att_ref[...], a).astype(low)
        gb_ref[...] = SCALE * dot_tn(inner, gb) + SCALE * c * cross_ref[:, o_cols]

    span = pl.ds(pl.multiple_of(t * TILE, TILE), TILE)
    a_tile = a_ref[0, :, span].astype(low)
    gi_low = gi[...]
    back = dot_nt(lhs[...], w_ref[0, :, w_ref.shape[2] - width :])
    gatt_ref[...] = (back[:rows] + dot_f32(gi_low, a_tile)).astype(low)
    spread = back[rows:] + SCALE * dot_two(tail[...], a_tile)
    ga_ref[...] = dot_tn(gi_low, att_ref[:, span]) + SCALE * spread


def out_back(in_grad, x1, gain, gy, before, att, a, b, m, norms, cross, weights):
    rows, width = x1.shape
    tiles = width // TILE
    full = lambda shape: pl.BlockSpec(shape, lambda t: (0,) * len(shape))
    col = lambda height: pl.BlockSpec((height, TILE), lambda t: (0, t))
    f32, low = jnp.float32, jnp.bfloat16
    wide = full((rows, width))
    return pl.pallas_call(
        out_back_kernel,
        out_shape=(
            pltpu.HBM((rows, width), f32),
            pltpu.HBM((rows, width), low),
            jax.ShapeDtypeStruct((16, width), f32),
            jax.ShapeDtypeStruct((16, width), f32),
            jax.ShapeDtypeStruct((1, width), f32),
        ),
        grid=(tiles,),
        in_specs=[wide, wide, full((2, width)), wide, wide, wide,
                  pl.BlockSpec((1, 16, width), lambda t: (3, 0, 0)),
                  full(b.shape), full(m.shape), full(norms.shape), full(cross.shape),
                  pl.BlockSpec((1, TILE, weights.shape[2]), lambda t: (1, t, 0))],
        out_specs=(wide, col(rows), col(16), full((16, width)), full((1, width))),
        scratch_shapes=[
            pltpu.VMEM((rows + 16, width), low),
            pltpu.VMEM((rows, 16), low),
            pltpu.VMEM((32, 16), low),
        ],
        compiler_params=pltpu.CompilerParams(vmem_limit_bytes=48 << 20),
        cost_estimate=pl.CostEstimate(flops=0, transcendentals=0, bytes_accessed=1 << 20),
        name="out_back",
    )(*in_hbm(in_grad, x1), gain, *in_hbm(gy, before, att, a, b), m, norms, *in_hbm(cross, weights))


def qkv_back_kernel(gq_ref, gkv_ref, cos_ref, sin_ref, before_ref, u_ref, inner_ref, a_ref, b_ref, m_ref, n_ref, cross_ref,
                    x_ref, gain_ref, gx_ref, w0_ref, w1_ref,
                    out_ref, ga_ref, gb_ref, gm_ref, lhs0, lhs1, gi, tail):
    t = pl.program_id(0)
    rows, width = gx_ref.shape
    low = jnp.bfloat16
    k_cols = w1_ref.shape[2]
    bounds = [(0, width), (width, width + k_cols), (width + k_cols, width + 2 * k_cols)]

    @pl.when(t == 0)
    def _():
        cosine, sine = cos_ref[...], -sin_ref[...]
        k_parts = [gkv_ref[:, 256 * j : 256 * j + 128] for j in range(k_cols // 128)]
        v_parts = [gkv_ref[:, 256 * j + 128 : 256 * j + 256] for j in range(k_cols // 128)]
        rounded = lambda z: z.astype(low).astype(jnp.float32)
        ups = [
            turn(gq_ref[...].astype(jnp.float32), cosine, sine),
            turn(rounded(jnp.concatenate(k_parts, axis=1)), cosine, sine),
            rounded(jnp.concatenate(v_parts, axis=1)),
        ]
        lhs0[rows:] = jnp.zeros_like(lhs0[rows:])
        lhs1[rows:] = jnp.zeros_like(lhs1[rows:])
        for p, (start, stop) in enumerate(bounds):
            g, norm, m = ups[p], n_ref[:, start:stop], m_ref[:, start:stop]
            b = b_ref[:, start:stop].astype(low)
            gb = (g * (m / norm)).astype(low)
            gm = jnp.sum(g * before_ref[:, start:stop], axis=0, keepdims=True) / norm
            gm_ref[:, start:stop] = gm
            c = -gm * m / (norm * norm)
            weighted = (b.astype(jnp.float32) * c).astype(low)
            gi[:, 16 * p : 16 * p + 16] = (SCALE * dot_nt(gb, b)).astype(low)
            tail[p] = two_terms(dot_nt(weighted, b))
            gb_ref[:, start:stop] = SCALE * dot_tn(inner_ref[p], gb) + SCALE * c * cross_ref[:, start:stop]
            lhs, at = (lhs1, 0) if p == 2 else (lhs0, start)
            lhs[:rows, at : at + stop - start] = gb
            lhs[rows + 16 * p : rows + 16 * p + 16, at : at + stop - start] = weighted

    span = pl.ds(pl.multiple_of(t * TILE, TILE), TILE)
    back = dot_nt(lhs0[...], w0_ref[0]) + dot_nt(lhs1[...], w1_ref[0])
    grad_in = back[:rows]
    for p in range(3):
        a_tile = a_ref[p, :, span].astype(low)
        gi_p = gi[:, 16 * p : 16 * p + 16]
        grad_in = grad_in + dot_f32(gi_p, a_tile)
        spread = back[rows + 16 * p : rows + 16 * p + 16] + SCALE * dot_two(tail[p], a_tile)
        ga_ref[p] = dot_tn(gi_p, u_ref[:, span]) + SCALE * spread
    out_ref[:, span] = grad_in

    @pl.when(t == pl.num_programs(0) - 1)
    def _():
        v = x_ref[...].astype(jnp.float32)
        out_ref[...] = gx_ref[...] + rms_back(v, gain_ref[:1], out_ref[...])


def qkv_back(gq, gkv, cosine, sine, before, u, inner, a, b, m, norms, cross, x, gain, gx, weights):
    rows, width = gx.shape
    cols = before.shape[1]
    k_cols = (cols - width) // 2
    tiles = width // TILE
    full = lambda shape: pl.BlockSpec(shape, lambda t: (0,) * len(shape))
    f32, low = jnp.float32, jnp.bfloat16
    wide = full((rows, width))
    return pl.pallas_call(
        qkv_back_kernel,
        out_shape=(
            pltpu.HBM((rows, width), f32),
            jax.ShapeDtypeStruct((3, 16, width), f32),
            jax.ShapeDtypeStruct((16, cols), f32),
            jax.ShapeDtypeStruct((1, cols), f32),
        ),
        grid=(tiles,),
        in_specs=[wide, full(gkv.shape), full(cosine.shape), full(sine.shape), full((rows, cols)), wide, full(inner.shape),
                  full(a.shape), full(b.shape), full(m.shape), full(norms.shape), full(cross.shape),
                  wide, full((2, width)), wide,
                  pl.BlockSpec((1, TILE, width + k_cols), lambda t: (0, t, 0)),
                  pl.BlockSpec((1, TILE, k_cols), lambda t: (1, t, 0))],
        out_specs=(wide, pl.BlockSpec((3, 16, TILE), lambda t: (0, 0, t)), full((16, cols)), full((1, cols))),
        scratch_shapes=[
            pltpu.VMEM((rows + 48, width + k_cols), low),
            pltpu.VMEM((rows + 48, k_cols), low),
            pltpu.VMEM((rows, 48), low),
            pltpu.VMEM((3, 32, 16), low),
        ],
        compiler_params=pltpu.CompilerParams(vmem_limit_bytes=48 << 20),
        cost_estimate=pl.CostEstimate(flops=0, transcendentals=0, bytes_accessed=1 << 20),
        name="qkv_back",
    )(*in_hbm(gq), gkv, cosine, sine, *in_hbm(before, u), inner, *in_hbm(a, b), m, norms, *in_hbm(cross, x), gain,
      *in_hbm(gx, weights, weights))

MESH = pl.DeviceIdType.MESH


def place_in_seq():
    s = lax.axis_index("seq")
    return s, s // 2, lax.rem(s, 2)

def near_first(i, q, nc):
    short = jnp.where(q <= nc - 1 - q, q, nc - 1 - q)
    far = jnp.where(q <= nc - 1 - q, i, nc - 1 - i)
    step = (i + 1) // 2
    near = q - step if i % 2 else q + step
    return jnp.where(i <= 2 * short, near, far)


def place_in_rows(rows):
    half = rows // 2
    r = lax.axis_index("rows")
    a, b = r // 2, lax.rem(r, 2)
    turned = lambda k: 2 * lax.rem(a + k + half, half)
    return r, 2 * a + 1 - b, lambda k: turned(k) + b, lambda k: turned(k) + 1 - b


def greet_all(n, rows):
    s = lax.axis_index("seq")
    r, b_row, a_row, _ = place_in_rows(rows)
    barrier = pltpu.get_barrier_semaphore()
    for t in range(1, n):
        pl.semaphore_signal(
            barrier, inc=1, device_id=(r, lax.rem(s + t, n)), device_id_type=MESH
        )
    pl.semaphore_signal(barrier, inc=1, device_id=(b_row, s), device_id_type=MESH)
    for k in range(1, rows // 2):
        pl.semaphore_signal(barrier, inc=1, device_id=(a_row(k), s), device_id_type=MESH)
    pl.semaphore_wait(barrier, n - 1 + rows // 2)


def remote(src, dst, send, recv, row, seq):
    return pltpu.make_async_remote_copy(
        src_ref=src, dst_ref=dst, send_sem=send, recv_sem=recv,
        device_id=(row, seq), device_id_type=MESH,
    )


def weights_kernel(n, rows, qo, kv, xg, wd_hbm, ad_hbm, bd_hbm, x_hbm, gain_ref, aa_hbm, ag_hbm, gy_hbm,
                   wa, gz, near, sq_ref, gram_ref, u_hbm, inner_ref, gy0_hbm, gy1_hbm,
                   wd, ad_ref, bd_ref, x_ref, aa_ref, ag_ref, gy_ref, own_ref, cols_ref, local, edge, a_in, a_sib_in, a_out, a_sib_out, z_in, z_out):
    nc, half = n // 2, rows // 2
    others = half - 1
    units = gz.shape[-1]
    s, q, c = place_in_seq()
    sibling = s + 1 - 2 * c
    r, b_row, a_row, diagonal = place_in_rows(rows)
    greet_all(n, rows)

    both, first, second = pl.ds(0, 2), pl.ds(0, 1), pl.ds(1, 1)
    LINE, FROM_B = 0, 1

    def from_a(k):
        return 1 + k

    def relay_b(k):
        return 1 + others + k

    def relay_a(k):
        return 1 + 2 * others + k

    def a_view(p, core, parts, row):
        return wa.at[parts, 2 * p + core, row]

    def content(kind):
        if kind == LINE:
            return both, r
        if kind == FROM_B:
            return both, b_row
        for k in range(1, half):
            if kind == from_a(k):
                return both, a_row(-k)
            if kind == relay_b(k):
                return second, diagonal(-k)
            if kind == relay_a(k):
                return first, diagonal(-k)

    kinds = 2 + 3 * others

    def a_send(p, parts, row, kind, target_row):
        return remote(
            a_view(p, c, parts, row), a_view(p, c, parts, row),
            a_out.at[p, kind], a_in.at[p, kind], target_row, s,
        )

    def a_arrival(p, kind):
        parts, row = content(kind)
        return a_send(p, parts, row, kind, r)

    def a_to_sibling(p, kind, core):
        parts, row = content(kind)
        return remote(
            a_view(p, core, parts, row), a_view(p, core, parts, row),
            a_sib_out.at[p, kind], a_sib_in.at[p, kind], r, sibling,
        )

    def columns(device):
        return pl.ds(pl.multiple_of(device * units, units), units)

    def z_send(p, core):
        return remote(
            xg.at[:, r, :, columns(2 * p + core)], gz.at[:, s],
            z_out.at[p, core], z_in.at[q, c], r, 2 * p + core,
        )

    def z_arrival(p, core):
        slot = gz.at[:, 2 * p + core]
        return remote(slot, slot, z_out.at[p, core], z_in.at[p, core], r, s)

    def line_send(p, sem, target):
        view = a_view(p, c, both, r)
        return remote(view, view, sem, a_in.at[p, LINE], r, target)

    wide, k_cols = qo.shape[-1], kv.shape[-1]
    blocks = [(qo, 0, 0), (kv, 0, wide), (kv, 1, 0), (qo, 1, k_cols)]

    def own_blocks(part, out):
        for source, i, start in blocks:
            columns_of = pl.ds(start, source.shape[-1])
            out(source.at[i, part], i, columns_of)

    def own_line(sem, target):
        own_blocks(
            r,
            lambda src, i, cols: remote(
                src, wa.at[i, s, r, :, cols], sem, a_in.at[q, LINE], r, target
            ).start(),
        )

    pl.when(q > 0)(lambda: own_line(edge.at[0], s - 2))
    pl.when(q < nc - 1)(lambda: own_line(edge.at[1], s + 2))
    order = [near_first(i, q, nc) for i in range(nc)]
    whole_block = wa.at[:, s]
    sib_a = lambda: remote(whole_block, whole_block, edge.at[2], edge.at[3], r, sibling)
    sib_g = lambda: remote(
        xg.at[:, :, :, columns(sibling)], near.at[:, c], edge.at[4], edge.at[5], r, sibling
    )
    keep_a = pltpu.make_async_copy(own_ref, whole_block, local.at[0])
    keep_g = pltpu.make_async_copy(cols_ref, near.at[:, c], local.at[1])
    all_parts = pl.ds(0, rows)
    own_blocks(
        all_parts,
        lambda src, i, cols: remote(
            src, wa.at[i, s, :, :, cols], edge.at[2], edge.at[3], r, sibling
        ).start(),
    )
    own_blocks(
        all_parts,
        lambda src, i, cols: pltpu.make_async_copy(
            src, own_ref.at[i, :, :, cols], local.at[12]
        ).start(),
    )
    take_cols = pltpu.make_async_copy(xg.at[:, :, :, columns(s)], cols_ref, local.at[13])
    take_cols.start()
    takes = [
        pltpu.make_async_copy(src, dst, local.at[5 + i])
        for i, (src, dst) in enumerate(
            [(x_hbm, x_ref), (aa_hbm, aa_ref), (ag_hbm, ag_ref), (ad_hbm, ad_ref), (bd_hbm, bd_ref), (wd_hbm, wd),
             (gy_hbm, gy_ref)]
        )
    ]
    for cp in takes:
        cp.start()
    for cp in takes:
        cp.wait()
    pltpu.make_async_copy(own_ref, own_ref, local.at[12]).wait()
    keep_a.start()
    take_cols.wait()
    keep_g.start()
    low = jnp.bfloat16
    v = x_ref[...].astype(jnp.float32)
    u = (v * unit_rms(v) * gain_ref[:1]).astype(low)
    x_ref[...] = u
    keep_u = pltpu.make_async_copy(x_ref, u_hbm, local.at[2])
    keep_u.start()
    tokens = x_ref.shape[0] // 2
    halves = [
        pltpu.make_async_copy(gy_ref.at[pl.ds(tokens * k, tokens)], out, local.at[3 + k])
        for k, out in enumerate((gy0_hbm, gy1_hbm))
    ]
    for cp in halves:
        cp.start()
    for g in range(4):
        a = aa_ref[g].astype(low)
        gram_ref[g] = two_terms(dot_nt(a, a))
        if g < 3:
            inner_ref[g] = dot_nt(u, a).astype(low)
    for g in range(2):
        a = ag_ref[g].astype(low)
        gram_ref[4 + g] = two_terms(dot_nt(a, a))

    def down_squares():
        a = ad_ref[...].astype(low)
        gram_ref[6] = two_terms(dot_nt(a, a))
        mine = pl.ds(pl.multiple_of(s * wd.shape[0], wd.shape[0]), wd.shape[0])
        cross = dot_f32(ad_ref[:, mine].astype(low), wd[...])
        b_wide = bd_ref[...].astype(low).astype(jnp.float32)
        sq_ref[...] = column_squares(wd[...]) + 2.0 * SCALE * jnp.sum(b_wide * cross, axis=0, keepdims=True)

    for p in order[1:]:
        a_arrival(p, LINE).wait_recv()
        pl.when((p < q) & (q < nc - 1))(
            lambda p=p: line_send(p, a_out.at[p, LINE], s + 2).start()
        )
        pl.when((p > q) & (q > 0))(
            lambda p=p: line_send(p, a_out.at[p, LINE], s - 2).start()
        )
        a_send(p, both, r, FROM_B, b_row).start()
        for k in range(1, half):
            a_send(p, both, r, from_a(k), a_row(k)).start()
        a_to_sibling(p, LINE, c).start()
    for p in order[1:]:
        for core in range(2):
            z_send(p, core).start()
    sib_g().start()
    down_squares()
    keep_u.wait()
    for cp in halves:
        cp.wait()
    for p in order[1:]:
        a_arrival(p, FROM_B).wait_recv()
        for k in range(1, half):
            a_send(p, first, b_row, relay_a(k), a_row(k)).start()
        a_to_sibling(p, FROM_B, c).start()
        for k in range(1, half):
            a_arrival(p, from_a(k)).wait_recv()
            a_send(p, second, a_row(-k), relay_b(k), b_row).start()
            a_to_sibling(p, from_a(k), c).start()
    for p in order[1:]:
        for k in range(1, half):
            for kind in (relay_b(k), relay_a(k)):
                a_arrival(p, kind).wait_recv()
                a_to_sibling(p, kind, c).start()
    keep_a.wait()
    keep_g.wait()
    sib_a().wait()
    sib_g().wait()
    pl.when(q > 0)(lambda: line_send(q, edge.at[0], s).wait_send())
    pl.when(q < nc - 1)(lambda: line_send(q, edge.at[1], s).wait_send())
    for p in order[1:]:
        pl.when(((p < q) & (q < nc - 1)) | ((p > q) & (q > 0)))(
            lambda p=p: line_send(p, a_out.at[p, LINE], s).wait_send()
        )
        for kind in range(kinds):
            a_to_sibling(p, kind, c).wait_send()
            a_to_sibling(p, kind, 1 - c).wait_recv()
        a_send(p, both, r, FROM_B, b_row).wait_send()
        for k in range(1, half):
            a_send(p, both, r, from_a(k), r).wait_send()
            a_send(p, first, b_row, relay_a(k), r).wait_send()
            a_send(p, second, a_row(-k), relay_b(k), r).wait_send()
        for core in range(2):
            z_send(p, core).wait_send()
            z_arrival(p, core).wait_recv()


def gather_weights(n, rows, qo, kv, xg, wd, ad, bd, x, gains, aa, ag, gy, collective_id):
    nc = n // 2
    _, block, width = qo.shape
    part = block // rows
    cols = width + kv.shape[2]
    qo = qo.reshape(2, rows, part, width)
    kv = kv.reshape(2, rows, part, kv.shape[2])
    xg = xg.reshape(2, rows, part, xg.shape[2])
    units = xg.shape[3] // n
    kinds = 2 + 3 * (rows // 2 - 1)
    dma = pltpu.SemaphoreType.DMA
    anywhere = pl.BlockSpec(memory_space=pltpu.HBM)
    vmem = pl.BlockSpec(memory_space=pltpu.VMEM)
    low = qo.dtype
    wa, gz, near, sq, grams, u, inner, *halves = pl.pallas_call(
        functools.partial(weights_kernel, n, rows),
        out_shape=(
            pltpu.HBM((2, n, rows, part, cols), low),
            pltpu.HBM((2, n, part, units), low),
            pltpu.HBM((2, 2, rows, part, units), low),
            jax.ShapeDtypeStruct((1, width), jnp.float32),
            jax.ShapeDtypeStruct((7, 32, 16), low),
            pltpu.HBM(x.shape, low),
            jax.ShapeDtypeStruct((3, x.shape[0], 16), low),
            *([pltpu.HBM((gy.shape[0] // 2, width), low)] * 2),
        ),
        in_specs=[anywhere] * 7 + [vmem] + [anywhere] * 3,
        out_specs=(anywhere,) * 3 + (vmem,) * 2 + (anywhere, vmem) + (anywhere,) * 2,
        scratch_shapes=[pltpu.VMEM(v.shape, v.dtype) for v in (wd, ad, bd, x, aa, ag, gy)]
        + [pltpu.VMEM((2, rows, part, cols), low), pltpu.VMEM((2, rows, part, units), low)]
        + [dma((14,)), dma((6,))]
        + [dma((nc, kinds))] * 4
        + [dma((nc, 2))] * 2,
        compiler_params=pltpu.CompilerParams(
            collective_id=collective_id, has_side_effects=True, vmem_limit_bytes=32 << 20
        ),
        cost_estimate=pl.CostEstimate(
            flops=0, transcendentals=0, bytes_accessed=250 * 1024 * 1024
        ),
        name="gather_weights",
    )(*in_hbm(qo, kv, xg, wd, ad, bd, x), gains, *in_hbm(aa, ag, gy))
    return wa.reshape(2, n * block, cols), gz, near, sq, grams, u, inner, halves


def gather_kernel(n, rows, count, shared, *refs):
    nc = n // 2
    sources = refs[: count + len(shared[0])]
    outs = refs[len(sources) : 2 * len(sources) - len(shared[0]) + len(shared[1])]
    scratch = refs[len(sources) + len(outs) :]
    held_here = scratch[:count]
    local_sem, to_sib, to_left, to_right, recv, share_out, share_in = scratch[count:]
    xs, held, swapped = sources[:count], sources[count:], outs[count:]
    s, q, c = place_in_seq()
    sibling = s + 1 - 2 * c
    r, b_row, a_row, _ = place_in_rows(rows)
    greet_all(n, rows)
    takes = [pltpu.make_async_copy(xs[k], held_here[k], local_sem.at[0, k]) for k in range(count)]
    keeps = [
        pltpu.make_async_copy(held_here[k], outs[k].at[s], local_sem.at[1, k]) for k in range(count)
    ]
    for cp in takes:
        cp.start()

    def copy(k, src, slot, sems, target):
        return remote(src, outs[k].at[slot], sems.at[k, slot], recv.at[k, slot], r, target)

    def share(i, p):
        source, piece, turn, _ = shared[1][i]
        pair = pl.ds(2 * p, 2)
        src = held[source].at[pair] if piece is None else held[source].at[piece, pair]
        target = b_row if turn == 0 else a_row(turn)
        return remote(src, swapped[i].at[pair], share_out.at[i, p], share_in.at[i, p], target, s)

    for k in range(count):
        pl.when(q > 0)(lambda k=k: copy(k, xs[k], s, to_left, s - 2).start())
        pl.when(q < nc - 1)(lambda k=k: copy(k, xs[k], s, to_right, s + 2).start())
        copy(k, xs[k], s, to_sib, sibling).start()
    order = [near_first(i, q, nc) for i in range(nc)]
    for p in order[1:]:
        for i in range(len(shared[1])):
            share(i, p).start()
    for take, keep in zip(takes, keeps):
        take.wait()
        keep.start()
    for p in order[1:]:
        slot = 2 * p + c
        for k in range(count):
            src = outs[k].at[slot]
            copy(k, src, slot, to_right, s).wait_recv()
            pl.when((p < q) & (q < nc - 1))(
                lambda k=k, src=src, slot=slot: copy(k, src, slot, to_right, s + 2).start()
            )
            pl.when((p > q) & (q > 0))(
                lambda k=k, src=src, slot=slot: copy(k, src, slot, to_left, s - 2).start()
            )
            copy(k, src, slot, to_sib, sibling).start()
    for cp in keeps:
        cp.wait()
    for p in range(nc):
        mine, theirs = 2 * p + c, 2 * p + 1 - c
        for k in range(count):
            copy(k, outs[k].at[theirs], theirs, to_sib, sibling).wait_recv()
            copy(k, outs[k].at[mine], mine, to_sib, sibling).wait_send()
            pl.when((q < nc - 1) & (p <= q))(
                lambda k=k, mine=mine: copy(k, outs[k].at[mine], mine, to_right, s).wait_send()
            )
            pl.when((q > 0) & (p >= q))(
                lambda k=k, mine=mine: copy(k, outs[k].at[mine], mine, to_left, s).wait_send()
            )
    for p in order[1:]:
        for i in range(len(shared[1])):
            share(i, p).wait_send()
            share(i, p).wait_recv()


def gather_seq(n, rows, arrays, collective_id, held=(), shares=()):
    nc, count = n // 2, len(arrays)
    nbytes = sum(a.size * a.dtype.itemsize for a in arrays)
    dma = pltpu.SemaphoreType.DMA
    shape = jax.ShapeDtypeStruct
    outs = [shape((n, *a.shape), a.dtype) for a in arrays]
    outs += [shape(held[source].shape[-3:], held[source].dtype) for source, _, _ in shares]
    anywhere = pl.BlockSpec(memory_space=pltpu.HBM)
    listed = (tuple(held), [(source, piece, turn, None) for source, piece, turn in shares])
    sems = dma((max(1, len(shares)), nc))
    got = pl.pallas_call(
        functools.partial(gather_kernel, n, rows, count, (range(len(held)), listed[1])),
        out_shape=tuple(outs),
        in_specs=[anywhere] * (count + len(held)),
        out_specs=(anywhere,) * len(outs),
        scratch_shapes=[pltpu.VMEM(a.shape, a.dtype) for a in arrays]
        + [dma((2, count))]
        + [dma((count, n))] * 4
        + [sems] * 2,
        compiler_params=pltpu.CompilerParams(collective_id=collective_id, has_side_effects=True),
        cost_estimate=pl.CostEstimate(flops=0, transcendentals=0, bytes_accessed=nbytes * n * 20),
        name="gather_seq",
    )(*arrays, *held)
    return got[:count], got[count:]

def swap_halves(x):
    return pltpu.roll(x.astype(jnp.float32), HEAD_DIM, 1)


def stack_heads(block):
    lane = lax.broadcasted_iota(jnp.int32, (block.shape[0], 128), 1)
    rows = []
    for h in range(8):
        pair = block[:, (h // 2) * 128 : (h // 2 + 1) * 128].astype(jnp.float32)
        if h % 2 != h // 4:
            pair = swap_halves(pair)
        keep = lane < HEAD_DIM if h // 4 == 0 else lane >= HEAD_DIM
        rows.append(jnp.where(keep, pair, 0.0).astype(jnp.bfloat16))
    return jnp.concatenate(rows, axis=0)


def unstack_heads(stacked, span):
    lane = lax.broadcasted_iota(jnp.int32, (span, 128), 1)
    pairs = []
    for t in range(4):
        first = stacked[2 * t * span : (2 * t + 1) * span]
        second = stacked[(2 * t + 1) * span : (2 * t + 2) * span]
        if t < 2:
            second = swap_halves(second)
        else:
            first = swap_halves(first)
        pairs.append(jnp.where(lane < HEAD_DIM, first, second))
    return jnp.concatenate(pairs, axis=1)


def key_blocks(kv_ref, j):
    n, _, span, width = kv_ref.shape
    pick = lambda start: kv_ref[:, 0, :, start : start + 128].reshape(n * span, 128)
    return pick(128 * j), pick(width // 2 + 128 * j)


def attend_kernel(valid_ref, q_ref, kv_ref, o_ref, p_ref, s_ref):
    span = q_ref.shape[1]
    keys = kv_ref.shape[0] * span
    q_pos = lax.axis_index("seq") * span + lax.broadcasted_iota(jnp.int32, (span, 1), 0)
    limit = jnp.minimum(q_pos + 1, valid_ref[pl.program_id(0)])
    allowed = lax.broadcasted_iota(jnp.int32, (span, keys), 1) < limit
    for j in range(p_ref.shape[1]):
        at = slice(512 * j, 512 * (j + 1))
        q8 = stack_heads(q_ref[0, :, at]) * jnp.bfloat16(HEAD_DIM**-0.5)
        k2, v2 = key_blocks(kv_ref, j)
        s_ref[j % 2] = dot_nt(q8, k2)
        for h in range(8):
            head = slice(h * span, (h + 1) * span)
            scores = jnp.where(allowed, s_ref[j % 2, head], -1e30)
            unscaled = jnp.exp(scores - jnp.max(scores, axis=1, keepdims=True))
            shares = unscaled * (1.0 / jnp.sum(unscaled, axis=1, keepdims=True))
            p_ref[0, j, head] = shares.astype(jnp.bfloat16)
        o_ref[0, :, at] = unstack_heads(dot_f32(p_ref[0, j], v2), span).astype(jnp.bfloat16)


def attend(q, kv, valid):
    pair, span, width = q.shape
    n, kv_width = kv.shape[0], kv.shape[3] // 2
    groups = kv_width // 128
    keys = n * span
    q_spec = pl.BlockSpec((1, span, width), lambda p, *_: (p, 0, 0))
    flops = 4 * pair * groups * 8 * span * keys * 128
    return pl.pallas_call(
        attend_kernel,
        out_shape=(
            pltpu.HBM(q.shape, jnp.bfloat16),
            pltpu.HBM((pair, groups, 8 * span, keys), jnp.bfloat16),
        ),
        grid_spec=pltpu.PrefetchScalarGridSpec(
            num_scalar_prefetch=1,
            grid=(pair,),
            in_specs=[q_spec, pl.BlockSpec((n, 1, span, 2 * kv_width), lambda p, *_: (0, p, 0, 0))],
            out_specs=(
                q_spec,
                pl.BlockSpec((1, groups, 8 * span, keys), lambda p, *_: (p, 0, 0, 0)),
            ),
            scratch_shapes=[pltpu.VMEM((2, 8 * span, keys), jnp.float32)],
        ),
        compiler_params=pltpu.CompilerParams(vmem_limit_bytes=40 << 20),
        cost_estimate=pl.CostEstimate(
            flops=flops, transcendentals=flops // 512, bytes_accessed=8 << 20
        ),
        name="attend",
    )(valid, *in_hbm(q, kv))


def attend_back_kernel(q_ref, kv_ref, p_ref, g_ref, gq_ref, gkv_ref, s_ref, g_scores):
    span = q_ref.shape[1]
    n = kv_ref.shape[0]
    for j in range(p_ref.shape[1]):
        at = slice(512 * j, 512 * (j + 1))
        q8 = stack_heads(q_ref[0, :, at]) * jnp.bfloat16(HEAD_DIM**-0.5)
        g8 = stack_heads(g_ref[0, :, at])
        k2, v2 = key_blocks(kv_ref, j)
        s_ref[j % 2] = dot_nt(g8, v2)
        for h in range(8):
            head = slice(h * span, (h + 1) * span)
            shares = p_ref[0, j, head].astype(jnp.float32)
            weighted = shares * s_ref[j % 2, head]
            centre = jnp.sum(weighted, axis=1, keepdims=True)
            g_scores[j % 2, head] = (weighted - shares * centre).astype(jnp.bfloat16)
        grad_scores = g_scores[j % 2]
        gq = dot_f32(grad_scores, k2) * HEAD_DIM**-0.5
        gq_ref[0, :, at] = unstack_heads(gq, span).astype(jnp.bfloat16)
        both = jnp.concatenate([dot_tn(grad_scores, q8), dot_tn(p_ref[0, j], g8)], axis=1)
        gkv_ref[:, 0, :, 256 * j : 256 * (j + 1)] = both.astype(jnp.bfloat16).reshape(n, span, 256)


def attend_back(q, kv, shares, g):
    pair, span, width = q.shape
    n, kv_width = kv.shape[0], kv.shape[3] // 2
    groups = kv_width // 128
    keys = n * span
    q_spec = pl.BlockSpec((1, span, width), lambda p: (p, 0, 0))
    kv_spec = pl.BlockSpec((n, 1, span, 2 * kv_width), lambda p: (0, p, 0, 0))
    return pl.pallas_call(
        attend_back_kernel,
        out_shape=(
            pltpu.HBM(q.shape, jnp.bfloat16),
            pltpu.HBM(kv.shape, jnp.bfloat16),
        ),
        grid=(pair,),
        in_specs=[
            q_spec,
            kv_spec,
            pl.BlockSpec((1, groups, 8 * span, keys), lambda p: (p, 0, 0, 0)),
            q_spec,
        ],
        out_specs=(q_spec, kv_spec),
        scratch_shapes=[
            pltpu.VMEM((2, 8 * span, keys), jnp.float32),
            pltpu.VMEM((2, 8 * span, keys), jnp.bfloat16),
        ],
        compiler_params=pltpu.CompilerParams(vmem_limit_bytes=48 << 20),
        cost_estimate=pl.CostEstimate(flops=0, transcendentals=0, bytes_accessed=1 << 20),
        name="attend_back",
    )(*in_hbm(q, kv, shares, g))

def by_distance(i, q, nc):
    room = nc - 1 - q
    left_half = q <= room
    short = jnp.where(left_half, q, room)
    far = jnp.where(left_half, i, nc - 1 - i)
    step = (i + 1) // 2
    near = jnp.where(lax.rem(i, 2) == 1, q - step, q + step)
    return jnp.where(i <= 2 * short, near, far)


def ffn_kernel(n, rows, pieces, u_hbm, inner_hbm, gy0_hbm, gy1_hbm, wd_hbm, a_ref, b_ref, m_ref, ad_ref, bd_ref, md_ref, sq_ref, gram_ref,
               in_ref, down0_hbm, down1_hbm, ga_ref, gb_ref, gm_ref, norm_ref, gad_ref, gbd_ref, gmd_ref, nd_ref,
               w_parts, wd, u, side, gy, down, own, theirs, sib, from_left, from_right, ratio, cross, gm_all,
               w_sem, load_sem, down_sem, small_out, small_in, to_sib, sib_in, to_right, right_in, to_left, left_in):
    nc = n // 2
    f32, low = jnp.float32, jnp.bfloat16
    s, q, c = place_in_seq()
    tokens = own.shape[1]

    weights = [pltpu.make_async_copy(wd_hbm, wd, w_sem.at[0])]
    for src, dst in place_pieces(n, rows, pieces, w_parts):
        weights.append(pltpu.make_async_copy(src, dst, w_sem.at[len(weights)]))
    for cp in weights:
        cp.start()

    def loads(i):
        p = by_distance(nc - 1 - i, q, nc)
        slot = lax.rem(i, 2)
        pair = pl.ds(2 * p, 2)
        return (
            pltpu.make_async_copy(u_hbm.at[pair], u.at[slot], load_sem.at[0, slot]),
            pltpu.make_async_copy(
                gy0_hbm.at[pair], gy.at[slot, :, : tokens // 2], load_sem.at[1, slot]
            ),
            pltpu.make_async_copy(
                gy1_hbm.at[pair], gy.at[slot, :, tokens // 2 :], load_sem.at[2, slot]
            ),
            pltpu.make_async_copy(inner_hbm.at[pair], side.at[slot], load_sem.at[3, slot]),
        )

    for cp in loads(0):
        cp.start()
    sibling = s + 1 - 2 * c
    barrier = pltpu.get_barrier_semaphore()
    for t in range(1, n):
        pl.semaphore_signal(
            barrier, inc=1, device_id={"seq": lax.rem(s + t, n)}, device_id_type=MESH
        )

    def to_sibling(p):
        return pltpu.make_async_remote_copy(
            src_ref=theirs.at[p], dst_ref=sib.at[p], send_sem=to_sib.at[p], recv_sem=sib_in.at[p],
            device_id={"seq": sibling}, device_id_type=MESH,
        )

    def rightward(p, target):
        return pltpu.make_async_remote_copy(
            src_ref=own.at[p], dst_ref=from_left.at[p], send_sem=to_right.at[p], recv_sem=right_in.at[p],
            device_id={"seq": target}, device_id_type=MESH,
        )

    def leftward(p, target):
        return pltpu.make_async_remote_copy(
            src_ref=own.at[p], dst_ref=from_right.at[p], send_sem=to_left.at[p], recv_sem=left_in.at[p],
            device_id={"seq": target}, device_id_type=MESH,
        )

    def down_out(slot, p):
        half = tokens // 2
        return [
            pltpu.make_async_copy(
                down.at[slot, :, half * k : half * (k + 1)], out.at[pl.ds(2 * p, 2)], down_sem.at[k, slot]
            )
            for k, out in enumerate((down0_hbm, down1_hbm))
        ]

    def pass_on(p):
        to_sibling(p).wait_recv()

        @pl.when(p > q)
        def _():
            @pl.when(q > 0)
            def _():
                rightward(p, s).wait_recv()
                own[p] = (own[p].astype(f32) + sib[p].astype(f32) + from_left[p].astype(f32)).astype(low)

            @pl.when(q == 0)
            def _():
                own[p] = (own[p].astype(f32) + sib[p].astype(f32)).astype(low)

            rightward(p, s + 2).start()

        @pl.when(p < q)
        def _():
            @pl.when(q < nc - 1)
            def _():
                leftward(p, s).wait_recv()
                own[p] = (own[p].astype(f32) + sib[p].astype(f32) + from_right[p].astype(f32)).astype(low)

            @pl.when(q == nc - 1)
            def _():
                own[p] = (own[p].astype(f32) + sib[p].astype(f32)).astype(low)

            leftward(p, s - 2).start()

    def starts_flow(p):
        return ((p > q) & (q == 0)) | ((p < q) & (q == nc - 1))

    w = [w_parts.at[g] for g in range(2)]
    width = u_hbm.shape[2]
    weight = lambda g: w[g][...].reshape(width, -1)
    units = wd.shape[0]
    mine = pl.ds(pl.multiple_of(s * units, units), units)
    bd = bd_ref[...].astype(low)
    ad = ad_ref[:, mine].astype(low)
    a = [a_ref[g].astype(low) for g in range(2)]
    b = [b_ref[g, :, mine].astype(low) for g in range(2)]
    m = [m_ref[g : g + 1, mine] for g in range(2)]
    for cp in weights:
        cp.wait()
    a_both = jnp.concatenate(a, axis=0)
    for g in range(2):
        norm, cr = column_norms(weight(g), gram_ref[4 + g], b[g], dot_f32(a[g], weight(g)))
        norm_ref[g] = norm
        cross[g] = cr
        ratio[g] = m[g] / norm
    for ref in (ga_ref, gb_ref, gm_ref, gad_ref, gbd_ref, gmd_ref):
        ref[...] = jnp.zeros_like(ref)
    bd_wide = bd.astype(f32)
    gram_b = dot_two(gram_ref[6], bd)
    squares = jnp.sum(sq_ref[...], axis=0) + SCALE * SCALE * jnp.sum(
        bd_wide * gram_b, axis=0, keepdims=True
    )
    nd_ref[...] = jnp.sqrt(squares + 1e-06)
    ratio_d = md_ref[...] / nd_ref[...]
    pl.semaphore_wait(barrier, n - 1)

    def step(i, carry):
        p = by_distance(nc - 1 - i, q, nc)
        slot = lax.rem(i, 2)
        for cp in loads(i):
            cp.wait()

        @pl.when(i + 1 < nc)
        def _():
            for cp in loads(i + 1):
                cp.start()

        x = u[slot].reshape(2 * tokens, -1)
        upstream = gy[slot].reshape(2 * tokens, -1).astype(f32)
        gb_d = (upstream * ratio_d).astype(low)
        gi_d = (SCALE * dot_nt(gb_d, bd)).astype(low)
        gh = dot_nt(gb_d, wd[...]) + dot_f32(gi_d, ad)
        sides = side[slot].reshape(2 * tokens, -1)
        inner = [sides[:, 16 * g : 16 * g + 16] for g in range(2)]
        before = [dot_f32(x, weight(g)) + SCALE * dot_f32(inner[g], b[g]) for g in range(2)]
        gate = before[0] * ratio[0]
        lift = before[1] * ratio[1]
        sig = 1.0 / (1.0 + jnp.exp(-gate))
        silu = gate * sig
        hidden = (silu * lift).astype(low)
        grads = [gh * lift * sig * (1.0 + gate * (1.0 - sig)), gh * silu]
        gb = [(grads[g] * ratio[g]).astype(low) for g in range(2)]
        gi = jnp.concatenate([(SCALE * dot_nt(gb[g], b[g])).astype(low) for g in range(2)], axis=1)
        back = dot_nt(gb[0], weight(0)) + dot_nt(gb[1], weight(1)) + dot_f32(gi, a_both)
        back = back.astype(low).reshape(2, tokens, -1)
        first, second = back[0], back[1]

        @pl.when(c == 0)
        def _():
            own[p] = first
            theirs[p] = second

        @pl.when(c == 1)
        def _():
            own[p] = second
            theirs[p] = first

        to_sibling(p).start()
        inner_d = dot_nt(hidden, ad).astype(low)
        part = dot_f32(hidden, wd[...]) + SCALE * dot_f32(inner_d, bd)

        @pl.when(i >= 2)
        def _():
            for cp in down_out(slot, p):
                cp.wait()

        down[slot] = part.astype(low).reshape(2, tokens, -1)
        for cp in down_out(slot, p):
            cp.start()
        gmd_ref[...] += jnp.sum(upstream * part, axis=0, keepdims=True)
        gad_ref[...] += dot_tn(gi_d, hidden)
        gbd_ref[...] += SCALE * dot_tn(inner_d, gb_d)
        ga_ref[...] += dot_tn(gi, x).reshape(ga_ref.shape)
        for g in range(2):
            gm_ref[g] += jnp.sum(grads[g] * before[g], axis=0, keepdims=True)
            gb_ref[g] += SCALE * dot_tn(inner[g], gb[g])

        last = by_distance(nc - i, q, nc)
        pl.when((i > 0) & (i < nc - 1) & jnp.logical_not(starts_flow(last)))(lambda: pass_on(last))
        pl.when(starts_flow(p) | (i == nc - 2))(lambda: pass_on(p))
        return carry

    lax.fori_loop(0, nc, step, 0)

    gmd_ref[...] = gmd_ref[...] / nd_ref[...]

    def small(t, slot):
        return pltpu.make_async_remote_copy(
            src_ref=gmd_ref,
            dst_ref=gm_all.at[slot],
            send_sem=small_out.at[t],
            recv_sem=small_in.at[t],
            device_id={"seq": lax.rem(s + t, n)},
            device_id_type=MESH,
        )

    for t in range(1, n):
        small(t, s).start()
    for g in range(2):
        norm = norm_ref[g]
        gm = gm_ref[g] / norm
        gm_ref[g] = gm
        col = -gm * m[g] / (norm * norm)
        weighted = (b[g].astype(f32) * col).astype(low)
        tail = two_terms(dot_nt(weighted, b[g]))
        ga_ref[g] += SCALE * (dot_nt(weighted, weight(g)) + SCALE * dot_two(tail, a[g]))
        gb_ref[g] += SCALE * col * cross[g]

    gm_line = gmd_ref[...]
    for t in range(1, n):
        slot = lax.rem(s - t + n, n)
        small(t, slot).wait_recv()
        gm_line = gm_line + gm_all[slot]
    col = -gm_line * md_ref[...] / (nd_ref[...] * nd_ref[...])
    weighted = (bd_wide * col).astype(low)
    tail = two_terms(dot_nt(weighted, bd))
    gad_ref[...] += SCALE * (dot_nt(weighted, wd[...]) + SCALE * dot_two(tail, ad))
    own_gram = jnp.where(s == 0, SCALE, 0.0) * gram_b
    gbd_ref[...] += SCALE * col * (dot_f32(ad, wd[...]) + own_gram)

    to_sibling(q).wait_recv()
    in_ref[...] = own[q].astype(f32) + sib[q].astype(f32)

    @pl.when(q > 0)
    def _():
        rightward(q, s).wait_recv()
        in_ref[...] += from_left[q].astype(f32)

    @pl.when(q < nc - 1)
    def _():
        leftward(q, s).wait_recv()
        in_ref[...] += from_right[q].astype(f32)

    for i in range(min(2, nc)):
        for cp in down_out(i, 0):
            cp.wait()
    for t in range(1, n):
        small(t, s).wait_send()
    for p in range(nc):
        to_sibling(p).wait_send()
        pl.when(p > q)(lambda p=p: rightward(p, s).wait_send())
        pl.when(p < q)(lambda p=p: leftward(p, s).wait_send())


def share_plan(rows):
    turns = range(1, rows // 2)
    first = [(0, 0, k) for k in turns] + [(0, 1, 0)]
    second = [(0, 0, 0)] + [(0, 1, k) for k in turns]
    second += [(k, None, 0) for k in turns] + [(rows // 2, None, k) for k in turns]
    return first, second


def place_pieces(n, rows, pieces, w_parts):
    nc, half = n // 2, rows // 2
    _, q, _ = place_in_seq()
    r, b_row, a_row, diagonal = place_in_rows(rows)
    own, near = pieces[:2]
    turns = range(1, half)
    held = [(own.at[g], g, r) for g in range(2)]
    kinds = [(0, a_row(-k)) for k in turns] + [(1, b_row)]
    kinds += [(0, b_row)] + [(1, a_row(-k)) for k in turns]
    kinds += [(0, diagonal(-k)) for k in turns] + [(1, diagonal(-k)) for k in turns]
    held += [(piece, g, hold) for piece, (g, hold) in zip(pieces[2:], kinds)]
    out = [(near, w_parts.at[:, pl.ds(2 * q, 2)])]
    for i in range(1, nc):
        pair = pl.ds(2 * near_first(i, q, nc), 2)
        out += [(src.at[pair], w_parts.at[g, pair, hold]) for src, g, hold in held]
    return out


def feed_forward(n, rows, pieces, u, inner, gy0, gy1, wd, a, b, m, ad, bd, md, sq, gram, collective_id):
    nc = n // 2
    _, tokens, width = u.shape
    units = wd.shape[0]
    f32, low = jnp.float32, jnp.bfloat16
    shape = jax.ShapeDtypeStruct
    vmem = pl.BlockSpec(memory_space=pltpu.VMEM)
    hbm = pl.BlockSpec(memory_space=pltpu.HBM)
    dma = pltpu.SemaphoreType.DMA
    line = pltpu.VMEM((nc, tokens, width), low)
    pair = pltpu.VMEM((2, 2, tokens, width), low)
    part = pieces[0].shape[2]
    copies = 2 + (n // 2 - 1) * (2 + 2 * rows - 2)
    count = len(pieces)

    def kernel(*refs):
        ffn_kernel(n, rows, refs[:count], *refs[count:])

    return pl.pallas_call(
        kernel,
        out_shape=(
            shape((tokens, width), f32),
            pltpu.HBM((n, tokens // 2, width), low),
            pltpu.HBM((n, tokens // 2, width), low),
            shape((2, 16, width), f32),
            shape((2, 16, units), f32),
            shape((2, 1, units), f32),
            shape((2, 1, units), f32),
            shape((16, units), f32),
            shape((16, width), f32),
            shape((1, width), f32),
            shape((1, width), f32),
        ),
        in_specs=[hbm] * (count + 5) + [vmem] * 8,
        out_specs=(vmem, hbm, hbm) + (vmem,) * 8,
        scratch_shapes=[
            pltpu.VMEM((2, n, rows, part, units), low),
            pltpu.VMEM((units, width), low),
            pair,
            pltpu.VMEM((2, 2, tokens, 128), low),
            pair,
            pair,
            line, line, line, line, line,
            pltpu.VMEM((2, 1, units), f32),
            pltpu.VMEM((2, 16, units), f32),
            pltpu.VMEM((n, 1, width), f32),
            dma((copies,)), dma((4, 2)), dma((2, 2)), dma((n,)), dma((n,)),
        ] + [dma((nc,))] * 6,
        compiler_params=pltpu.CompilerParams(
            collective_id=collective_id, has_side_effects=True, vmem_limit_bytes=60 << 20
        ),
        cost_estimate=pl.CostEstimate(
            flops=12 * n * tokens * width * units, transcendentals=n * tokens * units,
            bytes_accessed=32 << 20,
        ),
        name="feed_forward",
    )(*pieces, u, inner, gy0, gy1, wd, a, b, m, ad, bd, md, sq, gram)

def greet_cross(n, rows, wait=True):
    s, r = lax.axis_index("seq"), lax.axis_index("rows")
    barrier = pltpu.get_barrier_semaphore()
    for t in range(1, n):
        pl.semaphore_signal(barrier, inc=1, device_id=(r, lax.rem(s + t, n)), device_id_type=MESH)
    for t in range(1, rows):
        pl.semaphore_signal(barrier, inc=1, device_id=(lax.rem(r + t, rows), s), device_id_type=MESH)
    if wait:
        pl.semaphore_wait(barrier, n + rows - 2)


def scatter_kernel(n, rows, x_ref, gb_gu, gm_gu, n_gu, ga_d, o_ref, units_all, own, sib, from_left, from_right,
                   units, units_in, load_sem, to_sib, sib_in, to_right, right_in, to_left, left_in,
                   row_out, row_in, back_send, back_in, wide_send, wide_in, pass_send, pass_in):
    nc = n // 2
    s, q, c = place_in_seq()
    sibling = s + 1 - 2 * c
    theirs = 1 - c
    r = lax.axis_index("rows")
    greet_cross(n, rows)
    f32, low = jnp.float32, jnp.bfloat16
    unit_rows, size = units.shape[1:]

    cut = own.shape[1] // 4
    part = lambda k: pl.ds(k * cut, cut)

    def load(p):
        return pltpu.make_async_copy(x_ref.at[2 * p + c], own.at[p], load_sem.at[p])

    def to_sibling(p, k):
        return pltpu.make_async_remote_copy(
            src_ref=x_ref.at[2 * p + theirs, part(k)],
            dst_ref=sib.at[p, part(k)],
            send_sem=to_sib.at[p, k],
            recv_sem=sib_in.at[p, k],
            device_id={"seq": sibling},
            device_id_type=MESH,
        )

    def rightward(p, k, target):
        return pltpu.make_async_remote_copy(
            src_ref=own.at[p, part(k)],
            dst_ref=from_left.at[p, part(k)],
            send_sem=to_right.at[p, k],
            recv_sem=right_in.at[p, k],
            device_id={"seq": target},
            device_id_type=MESH,
        )

    def leftward(p, k, target):
        return pltpu.make_async_remote_copy(
            src_ref=own.at[p, part(k)],
            dst_ref=from_right.at[p, part(k)],
            send_sem=to_left.at[p, k],
            recv_sem=left_in.at[p, k],
            device_id={"seq": target},
            device_id_type=MESH,
        )

    order = []
    for t in range(nc):
        for p in (nc - 1 - t, t):
            if p not in order:
                order.append(p)
    for p in order:
        load(p).start()
        for k in range(4):
            to_sibling(p, k).start()

    n_high = [n_gu[g].astype(low).astype(f32) for g in range(2)]
    n_rest = [n_gu[g] - n_high[g] for g in range(2)]
    tops = jnp.concatenate(
        [gm_gu[0], gm_gu[1]]
        + [v * (1.0 / rows) for v in (n_high[0], n_rest[0], n_high[1], n_rest[1])]
        + [jnp.zeros((2, size), f32)],
        axis=0,
    )
    blocks = [gb_gu[0][:8], gb_gu[0][8:], gb_gu[1][:8], gb_gu[1][8:], ga_d[:8], ga_d[8:], tops, jnp.zeros((8, size), f32)]
    per = unit_rows // 8
    for j in range(rows):
        units[j] = jnp.concatenate(blocks[per * j : per * (j + 1)], axis=0).astype(low)

    def member(t):
        return lax.rem(r + t + rows, rows)

    def chip(t):
        return lax.rem(q + t + nc, nc)

    def unit_send(t):
        return remote(units.at[member(t)], units_in.at[t], row_out.at[t], row_in.at[t], member(t), s)

    def unit_back(t, slot):
        place = units_all.at[r, c, slot]
        return remote(place, place, back_send.at[t], back_in.at[t], r, 2 * chip(t) + c)

    def unit_wide(t, row):
        place = units_all.at[row, c]
        return remote(place, place, wide_send.at[t], wide_in.at[t], member(t), s)

    def unit_hand(t, row, core):
        place = units_all.at[row, core]
        return remote(place, place, pass_send.at[t], pass_in.at[t], r, sibling)

    def sum_units():
        total = units[r].astype(f32)
        for t in range(1, rows):
            unit_send(t).wait_recv()
            total = total + units_in[t].astype(f32)
        units_all[r, c, q] = total.astype(low)
        for t in range(1, nc):
            unit_back(t, q).start()

    def spread_units():
        for t in range(1, nc):
            unit_back(t, chip(-t)).wait_recv()
        for t in range(1, rows):
            unit_wide(t, r).start()
        unit_hand(0, r, c).start()

    for t in range(1, rows):
        unit_send(t).start()
    def add_and_send(p, k, flow, arrived, more, target):
        at = part(k)

        @pl.when(more)
        def _():
            flow(p, k, s).wait_recv()
            total = own[p, at].astype(f32) + sib[p, at].astype(f32) + arrived[p, at].astype(f32)
            own[p, at] = total.astype(own.dtype)

        @pl.when(jnp.logical_not(more))
        def _():
            own[p, at] = (own[p, at].astype(f32) + sib[p, at].astype(f32)).astype(own.dtype)

        flow(p, k, target).start()

    sum_units()
    for step, p in enumerate(jnp.where(q <= nc - 1 - q, p, nc - 1 - p) for p in order):
        if step == 1:
            spread_units()
        load(p).wait()
        for k in range(4):
            to_sibling(p, k).wait_recv()
            pl.when(p > q)(lambda p=p, k=k: add_and_send(p, k, rightward, from_left, q > 0, s + 2))
            pl.when(p < q)(
                lambda p=p, k=k: add_and_send(p, k, leftward, from_right, q < nc - 1, s - 2)
            )

    o_ref[...] = own[q].astype(f32) + sib[q].astype(f32)

    @pl.when(q > 0)
    def _():
        for k in range(4):
            rightward(q, k, s).wait_recv()
        o_ref[...] += from_left[q].astype(f32)

    @pl.when(q < nc - 1)
    def _():
        for k in range(4):
            leftward(q, k, s).wait_recv()
        o_ref[...] += from_right[q].astype(f32)

    for t in range(1, rows):
        unit_wide(t, member(-t)).wait_recv()
        unit_hand(t, member(-t), c).start()
    for t in range(rows):
        unit_hand(t, member(-t), theirs).wait_recv()
        unit_hand(t, member(-t), c).wait_send()
    for t in range(1, rows):
        unit_send(t).wait_send()
        unit_wide(t, r).wait_send()
    for t in range(1, nc):
        unit_back(t, q).wait_send()
    for p in range(nc):
        for k in range(4):
            to_sibling(p, k).wait_send()
            pl.when(p > q)(lambda p=p, k=k: rightward(p, k, s).wait_send())
            pl.when(p < q)(lambda p=p, k=k: leftward(p, k, s).wait_send())


def scatter_seq(n, rows, x, own_units, collective_id):
    nc = n // 2
    _, height, cols = x.shape
    size = own_units[3].shape[1]
    unit_rows = 64 // rows
    low = jnp.bfloat16
    dma = pltpu.SemaphoreType.DMA
    buf = pltpu.VMEM((nc, height, cols), x.dtype)
    small = pltpu.VMEM((rows, unit_rows, size), low)
    vmem = pl.BlockSpec(memory_space=pltpu.VMEM)
    return pl.pallas_call(
        functools.partial(scatter_kernel, n, rows),
        out_shape=(
            jax.ShapeDtypeStruct((height, cols), jnp.float32),
            jax.ShapeDtypeStruct((rows, 2, nc, unit_rows, size), low),
        ),
        in_specs=[pl.BlockSpec(memory_space=pltpu.HBM)] + [vmem] * 4,
        out_specs=(vmem,) * 2,
        scratch_shapes=[buf] * 4 + [small] * 2 + [dma((nc,))] + [dma((nc, 4))] * 6
        + [dma((rows,))] * 2 + [dma((nc,))] * 2 + [dma((rows,))] * 4,
        compiler_params=pltpu.CompilerParams(
            collective_id=collective_id, has_side_effects=True, vmem_limit_bytes=32 << 20
        ),
        cost_estimate=pl.CostEstimate(flops=0, transcendentals=0, bytes_accessed=1 << 20),
        name="scatter_seq",
    )(*in_hbm(x), *own_units)


def reduce_kernel(n, rows, ga_qkv, ga_o, gb_qkv, gb_o, ga_gu, gb_d, gm_qkv, gm_o, gm_d,
                  whole, part, from_sib, mid, from_rows, from_line, line_out,
                  sib_out, sib_in, row_out, row_in, line_send, line_in, back_send, back_in, wide_send, wide_in,
                  pass_send, pass_in):
    nc = n // 2
    f32, low = jnp.float32, jnp.bfloat16
    s, q, c = place_in_seq()
    sibling = s + 1 - 2 * c
    r = lax.axis_index("rows")
    width = ga_o.shape[1]
    cols = width // (2 * rows)
    kv = (gb_qkv.shape[1] - width) // 2
    height = part.shape[2]
    piece = height // nc

    greet_cross(n, rows, wait=False)
    gb_k, gb_v = gb_qkv[:, width : width + kv], gb_qkv[:, width + kv :]
    small = jnp.concatenate(
        [
            jnp.concatenate([gb_k[:8], gb_k[8:], gb_v[:8], gb_v[8:]], axis=1),
            gm_qkv[:, :width],
            gm_o[...],
            gm_d[...],
            jnp.concatenate([gm_qkv[:, width:], jnp.zeros((1, width - 2 * kv), f32)], axis=1),
            jnp.zeros((4, width), f32),
        ],
        axis=0,
    )
    groups = [ga_qkv[0], ga_qkv[1], ga_qkv[2], ga_o[...], gb_qkv[:, :width], gb_o[...], ga_gu[0], ga_gu[1], gb_d[...], small]
    for j in range(2 * rows):
        for g, value in enumerate(groups):
            part[j % 2, j // 2, 16 * g : 16 * g + 16] = value[:, cols * j : cols * (j + 1)].astype(low)
        if height > 160:
            part[j % 2, j // 2, 160:] = jnp.zeros((height - 160, cols), low)
    pl.semaphore_wait(pltpu.get_barrier_semaphore(), n + rows - 2)

    def to_sibling():
        return remote(part.at[1 - c], from_sib, sib_out.at[0], sib_in.at[0], r, sibling)

    def member(t):
        return lax.rem(r + t + rows, rows)

    def row_send(t):
        return remote(mid.at[member(t)], from_rows.at[t], row_out.at[t], row_in.at[t], member(t), s)

    def chip(t):
        return lax.rem(q + t + nc, nc)

    def line_part(t):
        return remote(line_out.at[chip(t)], from_line.at[t], line_send.at[t], line_in.at[t], r, 2 * chip(t) + c)

    def back(t, slot):
        return remote(whole.at[r, c, slot], whole.at[r, c, slot], back_send.at[t], back_in.at[t], r, 2 * chip(t) + c)

    def wide(t, row):
        return remote(whole.at[row, c], whole.at[row, c], wide_send.at[t], wide_in.at[t], member(t), s)

    def hand(t, row, core):
        return remote(whole.at[row, core], whole.at[row, core], pass_send.at[t], pass_in.at[t], r, sibling)

    to_sibling().start()
    to_sibling().wait_recv()
    for t in range(rows):
        mid[member(t)] = (part[c, member(t)].astype(f32) + from_sib[member(t)].astype(f32)).astype(low)
        if t:
            row_send(t).start()
    total = mid[r].astype(f32)
    for t in range(1, rows):
        row_send(t).wait_recv()
        total = total + from_rows[t].astype(f32)
    for p in range(nc):
        line_out[p] = total[piece * p : piece * (p + 1)].astype(low)
    for t in range(1, nc):
        line_part(t).start()
    own = line_out[q].astype(f32)
    for t in range(1, nc):
        line_part(t).wait_recv()
        own = own + from_line[t].astype(f32)
    whole[r, c, q] = own.astype(low)
    for t in range(1, nc):
        back(t, q).start()
    for t in range(1, nc):
        back(t, chip(-t)).wait_recv()
    for t in range(1, rows):
        wide(t, r).start()
    hand(0, r, c).start()
    for t in range(1, rows):
        wide(t, member(-t)).wait_recv()
        hand(t, member(-t), c).start()
    for t in range(rows):
        hand(t, member(-t), 1 - c).wait_recv()

    to_sibling().wait_send()
    for t in range(1, rows):
        row_send(t).wait_send()
        wide(t, r).wait_send()
    for t in range(1, nc):
        line_part(t).wait_send()
        back(t, q).wait_send()
    for t in range(rows):
        hand(t, member(-t), c).wait_send()


def sum_gradients(n, rows, full, collective_id):
    nc = n // 2
    width = full[1].shape[1]
    cols = width // (2 * rows)
    height = -(-160 // (8 * nc)) * 8 * nc
    low = jnp.bfloat16
    vmem = pl.BlockSpec(memory_space=pltpu.VMEM)
    dma = pltpu.SemaphoreType.DMA
    block = (rows, height, cols)
    return pl.pallas_call(
        functools.partial(reduce_kernel, n, rows),
        out_shape=jax.ShapeDtypeStruct((rows, 2, nc, height // nc, cols), low),
        in_specs=[vmem] * 9,
        out_specs=vmem,
        scratch_shapes=[
            pltpu.VMEM((2, *block), low),
            pltpu.VMEM(block, low),
            pltpu.VMEM(block, low),
            pltpu.VMEM(block, low),
            pltpu.VMEM((nc, height // nc, cols), low),
            pltpu.VMEM((nc, height // nc, cols), low),
            dma((1,)), dma((1,)), dma((rows,)), dma((rows,)), dma((nc,)), dma((nc,)),
            dma((nc,)), dma((nc,)), dma((rows,)), dma((rows,)), dma((rows,)), dma((rows,)),
        ],
        compiler_params=pltpu.CompilerParams(
            collective_id=collective_id, has_side_effects=True, vmem_limit_bytes=48 << 20
        ),
        cost_estimate=pl.CostEstimate(flops=0, transcendentals=0, bytes_accessed=1 << 20),
        name="sum_gradients",
    )(*full)


def finish_kernel(n, rows, whole, units_all, x1, before_0, before_1, m_attn, n_attn, m_d, n_d, m_gu,
                  o_out, o_ga, o_gb_qo, o_gb_kv, o_gm_q, o_gm_kv, o_gm_o, o_ga_gu, o_gb_gu, o_gm_gu, o_ga_d, o_gb_d,
                  o_gm_d, o_stats, n_gu):
    f32 = jnp.float32
    nc = n // 2
    width = o_gb_d.shape[1]
    kv = o_gb_kv.shape[2]
    cols = width // (2 * rows)
    size = units_all.shape[4]
    per = units_all.shape[3] // 8
    half = x1.shape[0] // 2
    for k, before in enumerate((before_0, before_1)):
        own = slice(half * k, half * (k + 1))
        o_out[own] = (x1[own] + before[...].astype(f32) * (m_d[...] / n_d[...])).astype(o_out.dtype)
    for j in range(2 * rows):
        block = jnp.concatenate([whole[j // 2, j % 2, p].astype(f32) for p in range(nc)], axis=0)
        at = slice(cols * j, cols * (j + 1))
        for g in range(4):
            o_ga[g, :, at] = block[16 * g : 16 * g + 16]
        o_gb_qo[0, :, at] = block[64:80]
        o_gb_qo[1, :, at] = block[80:96]
        o_ga_gu[0, :, at] = block[96:112]
        o_ga_gu[1, :, at] = block[112:128]
        o_gb_d[:, at] = block[128:144]
        which, start = divmod(cols * j, kv)
        o_gb_kv[which // 2, 8 * (which % 2) : 8 * (which % 2) + 8, start : start + cols] = block[144:152]
        o_gm_q[at] = block[152]
        o_gm_o[at] = block[153]
        o_gm_d[at] = block[154]
        if which < 2:
            o_gm_kv[which : which + 1, start : start + cols] = block[155:156]
    for j in range(rows):
        for dev in range(n):
            block = units_all[j, dev % 2, dev // 2].astype(f32)
            at = slice(size * dev, size * (dev + 1))
            for t in range(per):
                rows8, place = block[8 * t : 8 * t + 8], per * j + t
                half = slice(8 * (place % 2), 8 * (place % 2) + 8)
                if place < 4:
                    o_gb_gu[place // 2, half, at] = rows8
                elif place < 6:
                    o_ga_d[half, at] = rows8
                elif place == 6:
                    o_gm_gu[:, at] = rows8[:2]
                    n_gu[0:1, at] = rows8[2:3] + rows8[3:4]
                    n_gu[1:2, at] = rows8[4:5] + rows8[5:6]


    row = lax.broadcasted_iota(jnp.int32, o_stats.shape, 0)
    col = lax.broadcasted_iota(jnp.int32, o_stats.shape, 1)
    bounds = [(0, width), (width, width + kv), (width + kv, width + 2 * kv), (width + 2 * kv, 2 * width + 2 * kv)]
    both = [(m_attn[:, i:j], n_attn[:, i:j]) for i, j in bounds]
    both += [(m_gu[g : g + 1, :], n_gu[g : g + 1, :]) for g in range(2)] + [(m_d[...], n_d[...])]
    stats = jnp.zeros(o_stats.shape, f32)
    for p, (m, norm) in enumerate(both):
        drift = jnp.mean(jnp.square(m - norm), axis=1, keepdims=True)
        drift = jnp.sqrt(drift) / jnp.sqrt(jnp.mean(jnp.square(m), axis=1, keepdims=True) + 1e-06)
        stats = jnp.where((row == 0) & (col == p), drift, stats)
        stats = jnp.where((row == 1) & (col == p), jnp.mean(norm, axis=1, keepdims=True), stats)
    o_stats[...] = stats


def finish(n, rows, sums, units, x1, before_0, before_1, m_attn, n_attn, m_d, n_d, m_gu):
    tokens, width = x1.shape
    kv = (m_attn.shape[1] - 2 * width) // 2
    wide_units = m_gu.shape[1]
    shape = lambda *dims: pltpu.HBM(dims, jnp.float32)
    vmem = pl.BlockSpec(memory_space=pltpu.VMEM)
    return pl.pallas_call(
        functools.partial(finish_kernel, n, rows),
        out_shape=(
            pltpu.HBM((tokens, width), jnp.bfloat16), shape(4, 16, width), shape(2, 16, width), shape(2, 16, kv),
            shape(width), shape(2, kv), shape(width), shape(2, 16, width), shape(2, 16, wide_units), shape(2, wide_units),
            shape(16, wide_units), shape(16, width), shape(width), shape(2, 7),
        ),
        in_specs=[vmem] * 2 + [pl.BlockSpec()] * 8,
        scratch_shapes=[pltpu.VMEM((2, wide_units), jnp.float32)],
        compiler_params=pltpu.CompilerParams(vmem_limit_bytes=40 << 20),
        cost_estimate=pl.CostEstimate(flops=0, transcendentals=0, bytes_accessed=8 << 20),
        name="finish",
    )(sums, units, *in_hbm(x1, before_0, before_1), m_attn, n_attn, m_d, n_d, m_gu)

def local(
    layer_input,
    output_gradient,
    norm_gain_vectors,
    query_output_frozen,
    key_value_frozen,
    gate_up_frozen,
    down_frozen_weight,
    attention_adapter_a,
    query_output_adapter_b,
    key_value_adapter_b,
    query_magnitude,
    key_value_magnitude,
    output_magnitude,
    gate_up_adapter_a,
    gate_up_adapter_b,
    gate_up_magnitude,
    down_adapter_a,
    down_adapter_b,
    down_magnitude,
    prompt_length_list,
    response_length_list,
):
    pair_rows, span_len, model_width = layer_input.shape
    token_count = pair_rows * span_len
    kv_width = KV_HEADS * HEAD_DIM
    seq_size = lax.axis_size("seq")
    rows_size = lax.axis_size("rows")
    seq_index = lax.axis_index("seq")
    f32 = jnp.float32

    x = layer_input.reshape(token_count, model_width)
    grad_out_rows = output_gradient.reshape(token_count, model_width)
    weights, gu_own, gu_near, sq_d, grams, u1, inner_1, gy_halves = gather_weights(
        seq_size, rows_size, query_output_frozen, key_value_frozen, gate_up_frozen,
        down_frozen_weight, down_adapter_a, down_adapter_b, x, norm_gain_vectors,
        attention_adapter_a, gate_up_adapter_a, grad_out_rows, 1,
    )
    shares_1, shares_2 = share_plan(rows_size)
    gy_0 = lax.all_gather(gy_halves[0], "seq", axis=0, tiled=False)

    b_attn = jnp.concatenate(
        [
            query_output_adapter_b[0],
            key_value_adapter_b[0],
            key_value_adapter_b[1],
            query_output_adapter_b[1],
        ],
        axis=1,
    )
    m_attn = jnp.concatenate(
        [query_magnitude, key_value_magnitude[0], key_value_magnitude[1], output_magnitude]
    )[None]
    m_d = down_magnitude[None]

    positions = seq_index * span_len + jnp.arange(span_len, dtype=jnp.int32)
    half_dim = HEAD_DIM // 2
    frequency = 500000.0 ** (-(jnp.arange(half_dim, dtype=f32) * 2.0) / HEAD_DIM)
    angles = positions.astype(f32)[:, None] * frequency[None, :]
    cosine = jnp.tile(jnp.cos(angles), (pair_rows, 4))
    sine = jnp.tile(jnp.sin(angles), (pair_rows, 4))
    valid_len = prompt_length_list[0] + response_length_list

    before_qkv, q, n_attn, cross_attn, kv_all, sq_all, gu_1 = project_qkv(
        seq_size, rows_size, u1, inner_1, grams, attention_adapter_a, weights, b_attn, m_attn,
        cosine, sine, sq_d, gu_own, shares_1, 2,
    )
    kv_all, half_1 = lax.optimization_barrier((kv_all, gy_halves[1]))
    gy_1 = lax.all_gather(half_1, "seq", axis=0, tiled=False)
    kv_all = kv_all.reshape(seq_size, pair_rows, span_len, 2 * kv_width)
    q = q.reshape(pair_rows, span_len, model_width)
    att, shares = attend(q, kv_all, valid_len)
    att = att.reshape(token_count, model_width)
    before_o, x1, u2, inner_2 = project_out(
        att, attention_adapter_a, weights, b_attn, m_attn, n_attn, x, norm_gain_vectors, gate_up_adapter_a
    )

    (u2_all, inner_all), gu_2 = gather_seq(
        seq_size, rows_size, [u2, inner_2], 3, (gu_own, *gu_1), shares_2
    )
    in_grad, down_0, down_1, ga_gu, gb_gu, gm_gu, n_gu, ga_d, gb_d, gm_d, n_d = feed_forward(
        seq_size, rows_size, (gu_own, gu_near, *gu_1, *gu_2), u2_all, inner_all, gy_0, gy_1,
        down_frozen_weight, gate_up_adapter_a, gate_up_adapter_b, gate_up_magnitude, down_adapter_a,
        down_adapter_b, m_d, sq_all, grams, 4,
    )
    flat = lambda v: v.reshape(-1, model_width)
    before_0 = lax.psum_scatter(flat(down_0), "seq", scatter_dimension=0, tiled=True)

    gx1, grad_att, ga_o, gb_o, gm_o = out_back(
        in_grad, x1, norm_gain_vectors, grad_out_rows, before_o, att, attention_adapter_a, b_attn, m_attn,
        n_attn, cross_attn, weights,
    )
    gq, gkv = attend_back(q, kv_all, shares, grad_att.reshape(q.shape))
    gkv, units = scatter_seq(
        seq_size, rows_size, gkv.reshape(seq_size, token_count, 2 * kv_width),
        (gb_gu, gm_gu, n_gu, ga_d), 5,
    )
    gkv, down_1, before_0 = lax.optimization_barrier((gkv, down_1, before_0))
    before_1 = lax.psum_scatter(flat(down_1), "seq", scatter_dimension=0, tiled=True)
    grad_inputs, ga_qkv, gb_qkv, gm_qkv = qkv_back(
        gq.reshape(token_count, model_width), gkv, cosine, sine, before_qkv, u1, inner_1,
        attention_adapter_a, b_attn, m_attn, n_attn, cross_attn, x, norm_gain_vectors, gx1, weights,
    )

    sums = sum_gradients(
        seq_size, rows_size,
        (ga_qkv, ga_o, gb_qkv, gb_o, ga_gu, gb_d, gm_qkv, gm_o, gm_d),
        6,
    )
    layer_result, *summed, stats = finish(
        seq_size, rows_size, sums, units, x1, before_0, before_1, m_attn, n_attn, m_d, n_d, gate_up_magnitude
    )
    shape = (pair_rows, span_len, model_width)
    return (layer_result.reshape(shape), grad_inputs.reshape(shape), *summed, stats.T)

def solution(mesh):
    return jax.shard_map(
        local,
        mesh=mesh,
        in_specs=(
            P("rows", "seq", None),
            P("rows", "seq", None),
            P(),
            P(None, "seq", None),
            P(None, "seq", None),
            P(None, "seq", None),
            P("seq", None),
            P(),
            P(),
            P(),
            P(),
            P(),
            P(),
            P(),
            P(),
            P(),
            P(),
            P(),
            P(),
            P("rows"),
            P("rows"),
        ),
        out_specs=(
            P("rows", "seq", None),
            P("rows", "seq", None),
            P(),
            P(),
            P(),
            P(),
            P(),
            P(),
            P(),
            P(),
            P(),
            P(),
            P(),
            P(),
            P(),
        ),
        check_vma=False,
    )
```
